32 devices in a mesh: dp: 8 (over y, x, core), tensor: 4 (over z).
Axes of the slice: x: 2, y: 2, z: 4, core: 2. Of those that a mesh axis runs over, the one named last changes fastest.
Arguments:
- activations: bfloat16 [8, 2048, 2048], P('dp', 'tensor'), may hold values from -6 to 6
- segment_ids: int32 [8, 2048], P('dp'), may hold values from 0 to 3, as said below
- attn_gain: float32 [2048], replicated, may hold values from 0.1 to 1.9
- w_query: bfloat16 [2048, 2048], P('dp', 'tensor'), may hold values from -0.125 to 0.125
- w_key: bfloat16 [2048, 512], P('dp', 'tensor'), may hold values from -0.125 to 0.125
- w_value: bfloat16 [2048, 512], P('dp', 'tensor'), may hold values from -0.125 to 0.125
- w_out: bfloat16 [2048, 2048], P('dp', 'tensor'), may hold values from -0.375 to 0.375
- mlp_gain: float32 [2048], replicated, may hold values from 0.1 to 1.9
- w_gate: bfloat16 [2048, 8192], P('dp', 'tensor'), may hold values from -0.125 to 0.125
- w_up: bfloat16 [2048, 8192], P('dp', 'tensor'), may hold values from -0.125 to 0.125
- w_down: bfloat16 [2048, 8192], P('dp', 'tensor'), may hold values from -0.09375 to 0.09375
- cotangent: bfloat16 [8, 2048, 2048], P('dp', 'tensor'), may hold values from -6 to 6
Outputs:
- output: bfloat16 [8, 2048, 2048], P('dp', 'tensor')
- input_grad: bfloat16 [8, 2048, 2048], P('dp', 'tensor')
- attn_gain_grad: float32 [2048], replicated
- w_query_grad: float32 [2048, 2048], P('dp', 'tensor')
- w_key_grad: float32 [2048, 512], P('dp', 'tensor')
- w_value_grad: float32 [2048, 512], P('dp', 'tensor')
- w_out_grad: float32 [2048, 2048], P('dp', 'tensor')
- mlp_gain_grad: float32 [2048], replicated
- w_gate_grad: float32 [2048, 8192], P('dp', 'tensor')
- w_up_grad: float32 [2048, 8192], P('dp', 'tensor')
- w_down_grad: float32 [2048, 8192], P('dp', 'tensor')
The draws below stay inside these ranges and needn't reach their ends.
Inputs may be any that keep to these rules, and one draw needn't show every extreme that they name: `segment_ids`: along each sequence the ids never fall; each of the 4 documents has 204 to 1024 tokens, and exactly one document of each sequence has 1024.
All inputs are finite; a program needn't handle non-finite values.
Results may differ from the reference program's by a relative error of at most 0.018.
Values may be sent and summed in bfloat16 or wider, within the bound.
A program may use at most 320 MiB of HBM per device.

```python
import math
import jax
import jax.numpy as jnp
from jax import lax

D = 2048
FF = 8192
HEADS = 32
KV_HEADS = 8
HEAD_DIM = 64
SEQ_LEN = 2048
DOCS = 4
MOST_DOC = 1024
MIN_DOC = 204
QBLOCK = 512
SEQUENCES = 8


def draw_segment_ids(key, part):
    spare_room = SEQ_LEN - MOST_DOC - (DOCS - 1) * MIN_DOC

    def draw_row(row_key):
        cut_key, place_key = jax.random.split(row_key)
        cut_points = jnp.sort(jax.random.randint(cut_key, (DOCS - 2,), 0, spare_room + 1).astype(jnp.int32))
        edge_list = jnp.concatenate([jnp.zeros((1,), jnp.int32), cut_points, jnp.full((1,), spare_room, jnp.int32)])
        others = MIN_DOC + edge_list[1:] - edge_list[:-1]
        long_place = jax.random.randint(place_key, (), 0, DOCS).astype(jnp.int32)
        doc_index = jnp.arange(DOCS, dtype=jnp.int32)
        direct = jnp.take(others, jnp.clip(doc_index, 0, DOCS - 2))
        shifted = jnp.take(others, jnp.clip(doc_index - 1, 0, DOCS - 2))
        doc_sizes = jnp.where(doc_index < long_place, direct, jnp.where(doc_index == long_place, MOST_DOC, shifted)).astype(jnp.int32)
        doc_ends = jnp.cumsum(doc_sizes).astype(jnp.int32)
        token_pos = jnp.arange(SEQ_LEN, dtype=jnp.int32)
        return jnp.sum((token_pos[:, None] >= doc_ends[None, :DOCS - 1]).astype(jnp.int32), axis=1).astype(jnp.int32)
    return jax.vmap(draw_row)(jax.random.split(key, SEQUENCES))


def with_spikes(values, stream_key, source, target, parts, factor):
    def block_of(dim):
        return (jnp.arange(values.shape[dim]) // (values.shape[dim] // parts)).reshape((-1,) + (1,) * (values.ndim - 1 - dim))

    first = jax.random.permutation(stream_key, parts)[block_of(target)]
    far = (block_of(target) + parts // 2) % parts
    return jnp.where((block_of(source) == first) | (block_of(source) == far), factor * values, values)


def block_levels(own_key, dims, pieces, low, top_value):
    level = 1.0
    for axis_at, blocks in pieces:
        draws = jax.random.uniform(jax.random.fold_in(jax.random.fold_in(own_key, 6), axis_at), (blocks,), jnp.float32, low / len(pieces), top_value / len(pieces))
        level = level * jnp.repeat(jnp.exp(draws), dims[axis_at] // blocks).reshape((-1,) + (1,) * (len(dims) - 1 - axis_at))
    return level


def scatter_about(own_key, extent, width, reach, shards=(), kind=jnp.bfloat16):
    array = width * jax.random.normal(own_key, extent, jnp.float32)
    if shards:
        array = array * block_levels(own_key, extent, shards, -0.22, 0.18)
    return jnp.clip(array, -reach, reach).astype(kind)


def bell_draw_with(key, dims, spread, reach, pieces, heavy, held_as=jnp.bfloat16):
    values = spread * jax.random.normal(key, dims, jnp.float32)
    if pieces:
        values = values * block_levels(key, dims, pieces, -0.22, 0.18)
    return jnp.clip(with_spikes(values, jax.random.fold_in(key, 3), *heavy), -reach, reach).astype(held_as)


def setup_inputs(seed: int = 0) -> dict:
    seeds = jax.random.split(jax.random.key(seed), 13)
    activations = bell_draw_with(seeds[0], (SEQUENCES, SEQ_LEN, D), 1.0, 6.0, ((0, 8), (1, 4)), (0, 2, 8, 2.0))
    segment_ids = draw_segment_ids(jax.random.fold_in(seeds[12], 71), 0)
    attn_gain = jnp.clip(1.0 + 0.18 * jax.random.normal(seeds[2], (D,), jnp.float32), 0.1, 1.9)
    w_query = scatter_about(seeds[3], (D, HEADS * HEAD_DIM), D ** -0.5, 0.125, ((0, 8), (1, 4)))
    w_key = scatter_about(seeds[4], (D, KV_HEADS * HEAD_DIM), D ** -0.5, 0.125, ((0, 8), (1, 4)))
    w_value = scatter_about(seeds[5], (D, KV_HEADS * HEAD_DIM), D ** -0.5, 0.125, ((0, 8), (1, 4)))
    w_out = scatter_about(seeds[6], (D, HEADS * HEAD_DIM), (HEADS * HEAD_DIM // 8) ** -0.5, 0.375, ((0, 8), (1, 4)))
    mlp_gain = jnp.clip(1.0 + 0.18 * jax.random.normal(seeds[7], (D,), jnp.float32), 0.1, 1.9)
    w_gate = scatter_about(seeds[8], (D, FF), D ** -0.5, 0.125, ((0, 8), (1, 4)))
    w_up = scatter_about(seeds[9], (D, FF), D ** -0.5, 0.125, ((0, 8), (1, 4)))
    w_down = scatter_about(seeds[10], (D, FF), (FF // 2) ** -0.5, 0.09375, ((0, 8), (1, 4)))
    cotangent = bell_draw_with(seeds[11], (SEQUENCES, SEQ_LEN, D), 1.0, 6.0, ((0, 8), (1, 4)), (0, 2, 8, 2.0))
    return dict(activations=activations, segment_ids=segment_ids, attn_gain=attn_gain, w_query=w_query, w_key=w_key, w_value=w_value, w_out=w_out, mlp_gain=mlp_gain, w_gate=w_gate, w_up=w_up, w_down=w_down, cotangent=cotangent)


NORM_EPS = 1e-05
ROPE_THETA = 500000.0
HIGHEST = lax.Precision.HIGHEST

@jax.custom_vjp
def low(v):
    return lax.optimization_barrier(v.astype(jnp.bfloat16)).astype(jnp.float32)

@jax.custom_vjp
def low_back(v):
    return v

def low_keep(v):
    return (low(v), None)

def low_pass(kept, grad):
    return (grad,)

def back_keep(v):
    return (v, None)

def back_low(kept, grad):
    return (low(grad),)
low.defvjp(low_keep, low_pass)
low_back.defvjp(back_keep, back_low)

def matmul(left, right):
    return jnp.dot(left, right, precision=HIGHEST, preferred_element_type=jnp.float32)

def rope_tables(segments):
    length = segments.shape[-1]
    doc_ids = jnp.arange(DOCS, dtype=jnp.int32)
    member = (segments[..., :, None] == doc_ids).astype(jnp.int32)
    counts = lax.optimization_barrier(jnp.sum(member, axis=-2))
    before = (doc_ids < segments[..., :, None]).astype(jnp.int32)
    first = lax.optimization_barrier(jnp.sum(before * counts[..., None, :], axis=-1))
    position = (jnp.arange(length, dtype=jnp.int32) - first).astype(jnp.float32)
    frequency = jnp.exp(jnp.arange(HEAD_DIM // 2, dtype=jnp.float32) * (-2.0 * math.log(ROPE_THETA) / HEAD_DIM))
    angles = position[..., None] * frequency
    return (jnp.cos(angles), jnp.sin(angles))

def rotate(values_in, cosine, sine_tab):
    half_dim = HEAD_DIM // 2
    first_half = values_in[..., :half_dim]
    second_half = values_in[..., half_dim:]
    cos_wide = cosine[..., None, :]
    sin_wide = sine_tab[..., None, :]
    return jnp.concatenate([first_half * cos_wide - second_half * sin_wide, second_half * cos_wide + first_half * sin_wide], axis=-1)

def rms_scale(values_in):
    return lax.rsqrt(lax.optimization_barrier(jnp.mean(values_in * values_in, axis=-1, keepdims=True)) + NORM_EPS)

def attention(query_rot, key_rot, value_rows, segments):
    length = segments.shape[0]
    group_size = HEADS // KV_HEADS
    scaling = HEAD_DIM ** (-0.5)
    grouped = query_rot.reshape(length, KV_HEADS, group_size, HEAD_DIM)
    key_pos = jnp.arange(length, dtype=jnp.int32)

    def block(block_id):
        offset = block_id * QBLOCK
        query_block = lax.dynamic_slice_in_dim(grouped, offset, QBLOCK, 0)
        query_seg = lax.dynamic_slice_in_dim(segments, offset, QBLOCK, 0)
        query_pos = offset + jnp.arange(QBLOCK, dtype=jnp.int32)
        allowed = (query_seg[:, None] == segments[None, :]) & (key_pos[None, :] <= query_pos[:, None])
        score = low_back(jnp.einsum('qkgd,skd->kgqs', query_block, key_rot, precision=HIGHEST) * scaling)
        score = jnp.where(allowed, score, -1e+30)
        weights = low(jax.nn.softmax(score, axis=-1))
        result = jnp.einsum('kgqs,skd->qkgd', weights, value_rows, precision=HIGHEST)
        return result.reshape(QBLOCK, HEADS * HEAD_DIM)
    blocks_out = lax.map(jax.checkpoint(block), jnp.arange(length // QBLOCK, dtype=jnp.int32))
    return blocks_out.reshape(length, HEADS * HEAD_DIM)

def layer(inputs, segments, attn_gain, w_query, w_key, w_value, w_out, mlp_gain, w_gate, w_up, w_down):
    length = inputs.shape[0]
    cosine, sine_tab = rope_tables(segments)
    normed = low(inputs * rms_scale(inputs) * attn_gain)
    query_rot = low(rotate(low_back(matmul(normed, w_query).reshape(length, HEADS, HEAD_DIM)), cosine, sine_tab))
    key_rot = low(rotate(low_back(matmul(normed, w_key).reshape(length, KV_HEADS, HEAD_DIM)), cosine, sine_tab))
    value_rows = low(low_back(matmul(normed, w_value))).reshape(length, KV_HEADS, HEAD_DIM)
    attended = low(low_back(attention(query_rot, key_rot, value_rows, segments)))
    resid = inputs + low_back(matmul(attended, w_out.T))
    normed_mlp = low(resid * rms_scale(resid) * mlp_gain)
    gate_pre = low_back(matmul(normed_mlp, w_gate))
    up_proj = low_back(matmul(normed_mlp, w_up))
    hidden = low(jax.nn.silu(gate_pre) * up_proj)
    return resid + low_back(matmul(hidden, w_down.T))

def reference(activations, segment_ids, attn_gain, w_query, w_key, w_value, w_out, mlp_gain, w_gate, w_up, w_down, cotangent):
    params = tuple((weight.astype(jnp.float32) for weight in (attn_gain, w_query, w_key, w_value, w_out, mlp_gain, w_gate, w_up, w_down)))
    grad_init = tuple((jnp.zeros_like(weight) for weight in params))

    def step(carry, item):
        seq_input, seq_segments, seq_cotan = item

        def apply(seq_in, *weights):
            return layer(seq_in, seq_segments, *weights)
        result, pullback = jax.vjp(apply, seq_input.astype(jnp.float32), *params)
        grads = pullback(seq_cotan.astype(jnp.float32))
        summed = tuple((total_grad + grad_part for total_grad, grad_part in zip(carry, grads[1:])))
        return (summed, (result.astype(jnp.bfloat16), grads[0].astype(jnp.bfloat16)))
    totals, (outputs, input_grads) = lax.scan(step, grad_init, (activations, segment_ids, cotangent))
    return (outputs, input_grads, totals[0], totals[1], totals[2], totals[3], totals[4], totals[5], totals[6], totals[7], totals[8])
```

```python
import functools
import math

import jax
import jax.numpy as jnp
from jax import lax
from jax.experimental import pallas as pl
from jax.experimental.pallas import tpu as pltpu
from jax.sharding import PartitionSpec as P

HEAD_DIM = 64
DOCS = 4
MOST_DOC = 1024
NORM_EPS = 1e-05
ROPE_THETA = 500000.0
GROUP = 8
LANES = 128
QTILE = 256
SCALE = HEAD_DIM ** (-0.5)
LOG2E = 1.4426950408889634
FAR = -1e30
NTILE = 512

F32 = jnp.float32
BF16 = jnp.bfloat16


def dot_nn(left, right):
    return lax.dot_general(left, right, (((1,), (0,)), ((), ())), preferred_element_type=F32)


def dot_nt(left, right):
    return lax.dot_general(left, right, (((1,), (1,)), ((), ())), preferred_element_type=F32)


def dot_tn(left, right):
    return lax.dot_general(left, right, (((0,), (0,)), ((), ())), preferred_element_type=F32)


def document_starts(segments):
    doc_ids = jnp.arange(DOCS, dtype=jnp.int32)
    counts = jnp.sum((segments[:, None] == doc_ids).astype(jnp.int32), axis=0)
    before = (doc_ids < segments[:, None]).astype(jnp.int32)
    return jnp.sum(before * counts[None, :], axis=-1)


def rope_tables(positions):
    half = HEAD_DIM // 2
    frequency = jnp.exp(
        jnp.arange(half, dtype=F32) * (-2.0 * math.log(ROPE_THETA) / HEAD_DIM)
    )
    angles = positions.astype(F32)[:, None] * frequency
    cosine, sine = jnp.cos(angles), jnp.sin(angles)
    wide_cos = jnp.concatenate([cosine] * 4, axis=1)
    wide_sin = jnp.concatenate([-sine, sine, -sine, sine], axis=1)
    return wide_cos, wide_sin


def swap_halves(values):
    lane = lax.broadcasted_iota(jnp.int32, values.shape, 1)
    ahead = pltpu.roll(values, LANES - 32, 1)
    behind = pltpu.roll(values, 32, 1)
    return jnp.where((lane % 64) < 32, ahead, behind)


def qkv_kernel(x_ref, wq_ref, wkv_ref, cos_ref, sin_ref, q_ref, kv_ref):
    x = x_ref[...]
    cosine, sine = cos_ref[...], sin_ref[...]
    for at in range(wq_ref.shape[1] // LANES):
        part = pl.ds(at * LANES, LANES)
        value = dot_nn(x, wq_ref[:, part])
        q_ref[:, part] = (value * cosine + swap_halves(value) * sine).astype(BF16)
    value = dot_nn(x, wkv_ref[...])
    key = value[:, :LANES]
    kv_ref[:, :LANES] = (key * cosine + swap_halves(key) * sine).astype(BF16)
    kv_ref[:, LANES:] = value[:, LANES:].astype(BF16)


def project_qkv(x, wq, wkv, cosine, sine):
    rows, width = x.shape
    blocks = wkv.shape[1] // (2 * LANES)
    qcols = wq.shape[1] // blocks
    return pl.pallas_call(
        qkv_kernel,
        grid=(blocks,),
        in_specs=[
            pl.BlockSpec((rows, width), lambda g: (0, 0)),
            pl.BlockSpec((width, qcols), lambda g: (0, g)),
            pl.BlockSpec((width, 2 * LANES), lambda g: (0, g)),
            pl.BlockSpec((rows, LANES), lambda g: (0, 0)),
            pl.BlockSpec((rows, LANES), lambda g: (0, 0)),
        ],
        out_specs=[
            pl.BlockSpec((rows, qcols), lambda g: (0, g)),
            pl.BlockSpec((rows, 2 * LANES), lambda g: (0, g)),
        ],
        out_shape=[
            jax.ShapeDtypeStruct((rows, wq.shape[1]), BF16),
            jax.ShapeDtypeStruct((rows, wkv.shape[1]), BF16),
        ],
        compiler_params=pltpu.CompilerParams(vmem_limit_bytes=40 << 20),
        cost_estimate=pl.CostEstimate(
            flops=2 * rows * width * (wq.shape[1] + wkv.shape[1]),
            bytes_accessed=2 * width * (wq.shape[1] + wkv.shape[1]),
            transcendentals=0,
        ),
    )(x, wq, wkv, cosine, sine)


def fill_bias(bias_ref, low_ref, reach):
    span = bias_ref.shape[1]
    for tile in range(bias_ref.shape[0]):
        row = lax.broadcasted_iota(jnp.int32, (span, QTILE), 0)
        col = lax.broadcasted_iota(jnp.int32, (span, QTILE), 1)
        low = low_ref[0:1, tile * QTILE : (tile + 1) * QTILE]
        allowed = (row <= reach + col) & (row + tile * QTILE >= low)
        bias_ref[tile] = jnp.where(allowed, 0.0, FAR)


def spread_pair(pair, half):
    wide = pair.astype(F32)
    turned = pltpu.roll(wide, 64, 1)
    lane = lax.broadcasted_iota(jnp.int32, wide.shape, 1)
    mine = (lane // 64) == half
    even = half == 0
    first = jnp.where(mine, jnp.where(even, wide, turned), 0.0)
    second = jnp.where(mine, jnp.where(even, turned, wide), 0.0)
    return jnp.concatenate([first, second], axis=0).astype(BF16)


def gather_pair(transposed, half):
    count = transposed.shape[1] // 2
    mine = jnp.where(half == 0, transposed[:64], transposed[64:])
    return jnp.concatenate([mine[:, :count], mine[:, count:]], axis=0).T


def attend_kernel(reach, q_ref, k_ref, v_ref, low_ref, att_ref, lse_ref, bias_ref):
    head, tile, pair = pl.program_id(0), pl.program_id(1), pl.program_id(2)
    half = head % 2

    @pl.when((head == 0) & (tile == 0) & (pair == 0))
    def _():
        fill_bias(bias_ref, low_ref, reach)

    keys = pl.ds(pl.multiple_of(tile * QTILE, QTILE), bias_ref.shape[1])
    queries = spread_pair(q_ref[...], half)
    bias = bias_ref[tile]
    score = dot_nt(k_ref[keys, :], queries)
    score = score + jnp.concatenate([bias, bias], axis=1)
    top = jnp.max(score, axis=0, keepdims=True) * (SCALE * LOG2E)
    weight = jnp.exp2(score * (SCALE * LOG2E) - top)
    total = jnp.sum(weight, axis=0, keepdims=True)
    result = dot_tn(v_ref[keys, :], weight.astype(BF16)) / total
    att_ref[...] = gather_pair(result, half).astype(BF16)
    lse_ref[0] = top + jnp.log2(total)


def attend(q, kv, low):
    rows, width = q.shape
    keys = kv.shape[0]
    reach = keys - rows
    tiles = rows // QTILE
    pairs = width // LANES
    heads = kv.shape[1] // LANES
    per_head = pairs // heads
    span = reach + QTILE
    return pl.pallas_call(
        functools.partial(attend_kernel, reach),
        grid=(heads, tiles, per_head),
        in_specs=[
            pl.BlockSpec((QTILE, LANES), lambda a, t, p: (t, a * per_head + p)),
            pl.BlockSpec((keys, LANES), lambda a, t, p: (0, 2 * (a // 2))),
            pl.BlockSpec((keys, LANES), lambda a, t, p: (0, 2 * (a // 2) + 1)),
            pl.BlockSpec((1, rows), lambda a, t, p: (0, 0)),
        ],
        out_specs=[
            pl.BlockSpec((QTILE, LANES), lambda a, t, p: (t, a * per_head + p)),
            pl.BlockSpec((1, 1, 2 * QTILE), lambda a, t, p: ((a * tiles + t) * per_head + p, 0, 0)),
        ],
        out_shape=[
            jax.ShapeDtypeStruct((rows, width), BF16),
            jax.ShapeDtypeStruct((pairs * tiles, 1, 2 * QTILE), F32),
        ],
        scratch_shapes=[pltpu.VMEM((tiles, span, QTILE), F32)],
        compiler_params=pltpu.CompilerParams(vmem_limit_bytes=48 << 20),
        cost_estimate=pl.CostEstimate(
            flops=16 * rows * span * LANES * pairs,
            bytes_accessed=4 * rows * width + 2 * keys * kv.shape[1],
            transcendentals=2 * rows * span * pairs,
        ),
    )(q, kv, kv, low)


def attend_back_kernel(
    reach, q_ref, do_ref, o_ref, k_ref, v_ref, lse_ref, low_ref, cos_ref, sin_ref,
    dq_ref, dkv_ref, bias_ref, dk_acc, dv_acc,
):
    block, half, tile, pair = (pl.program_id(at) for at in range(4))
    inner = (half * pl.num_programs(2) + tile) * pl.num_programs(3) + pair

    @pl.when((block == 0) & (inner == 0))
    def _():
        fill_bias(bias_ref, low_ref, reach)

    @pl.when(inner == 0)
    def _():
        dk_acc[...] = jnp.zeros_like(dk_acc)
        dv_acc[...] = jnp.zeros_like(dv_acc)

    keys = pl.ds(pl.multiple_of(tile * QTILE, QTILE), bias_ref.shape[1])
    queries = spread_pair(q_ref[...], half)
    grads = spread_pair(do_ref[...], half)
    product = (do_ref[...].astype(F32) * o_ref[...].astype(F32)).T
    row_dot = jnp.concatenate(
        [
            jnp.sum(product[:64], axis=0, keepdims=True),
            jnp.sum(product[64:], axis=0, keepdims=True),
        ],
        axis=1,
    )
    bias = bias_ref[tile]
    key, value = k_ref[keys, :], v_ref[keys, :]
    score = dot_nt(key, queries) + jnp.concatenate([bias, bias], axis=1)
    weight = jnp.exp2(score * (SCALE * LOG2E) - lse_ref[0])
    dv_acc[keys, :] += dot_nn(weight.astype(BF16), grads)
    dscore = (weight * (dot_nt(value, grads) - row_dot)).astype(BF16)
    dk_acc[keys, :] += dot_nn(dscore, queries)
    dq = gather_pair(dot_tn(key, dscore), half) * SCALE
    dq_ref[...] = (dq * cos_ref[...] - swap_halves(dq) * sin_ref[...]).astype(BF16)

    @pl.when(inner == pl.num_programs(1) * pl.num_programs(2) * pl.num_programs(3) - 1)
    def _():
        dkv_ref[:, :LANES] = (dk_acc[...] * SCALE).astype(BF16)
        dkv_ref[:, LANES:] = dv_acc[...].astype(BF16)


def attend_back(q, do, att, kv, lse, low, cosine, sine):
    rows, width = q.shape
    keys = kv.shape[0]
    reach = keys - rows
    tiles = rows // QTILE
    pairs = width // LANES
    heads = kv.shape[1] // LANES
    per_head = pairs // heads
    span = reach + QTILE

    def pair_at(g, h, t, p):
        return (t, (2 * g + h) * per_head + p)

    return pl.pallas_call(
        functools.partial(attend_back_kernel, reach),
        grid=(heads // 2, 2, tiles, per_head),
        in_specs=[
            pl.BlockSpec((QTILE, LANES), pair_at),
            pl.BlockSpec((QTILE, LANES), pair_at),
            pl.BlockSpec((QTILE, LANES), pair_at),
            pl.BlockSpec((keys, LANES), lambda g, h, t, p: (0, 2 * g)),
            pl.BlockSpec((keys, LANES), lambda g, h, t, p: (0, 2 * g + 1)),
            pl.BlockSpec(
                (1, 1, 2 * QTILE),
                lambda g, h, t, p: (((2 * g + h) * tiles + t) * per_head + p, 0, 0),
            ),
            pl.BlockSpec((1, rows), lambda g, h, t, p: (0, 0)),
            pl.BlockSpec((QTILE, LANES), lambda g, h, t, p: (t, 0)),
            pl.BlockSpec((QTILE, LANES), lambda g, h, t, p: (t, 0)),
        ],
        out_specs=[
            pl.BlockSpec((QTILE, LANES), pair_at),
            pl.BlockSpec((keys, 2 * LANES), lambda g, h, t, p: (0, g)),
        ],
        out_shape=[
            jax.ShapeDtypeStruct((rows, width), BF16),
            jax.ShapeDtypeStruct(kv.shape, BF16),
        ],
        scratch_shapes=[
            pltpu.VMEM((tiles, span, QTILE), F32),
            pltpu.VMEM((keys, LANES), F32),
            pltpu.VMEM((keys, LANES), F32),
        ],
        compiler_params=pltpu.CompilerParams(vmem_limit_bytes=56 << 20),
        cost_estimate=pl.CostEstimate(
            flops=40 * rows * span * LANES * pairs,
            bytes_accessed=8 * rows * width + 4 * keys * kv.shape[1],
            transcendentals=2 * rows * span * pairs,
        ),
    )(q, do, att, kv, kv, lse, low, cosine, sine)


def finish_dkv_kernel(own_ref, recv_ref, cos_ref, sin_ref, out_ref):
    total = own_ref[...].astype(F32) + recv_ref[...].astype(F32)
    key = total[:, :LANES]
    out_ref[:, :LANES] = (key * cos_ref[...] - swap_halves(key) * sin_ref[...]).astype(BF16)
    out_ref[:, LANES:] = total[:, LANES:].astype(BF16)


def finish_dkv(own, recv, cosine, sine):
    rows, width = own.shape
    spec = pl.BlockSpec((rows, 2 * LANES), lambda g: (0, g))
    table = pl.BlockSpec((rows, LANES), lambda g: (0, 0))
    return pl.pallas_call(
        finish_dkv_kernel,
        grid=(width // (2 * LANES),),
        in_specs=[spec, spec, table, table],
        out_specs=spec,
        out_shape=jax.ShapeDtypeStruct((rows, width), BF16),
    )(own, recv, cosine, sine)


MESH = pl.DeviceIdType.MESH


def neighbours(wide):
    dp = lax.axis_index("dp")
    core, col, row = dp % 2, (dp // 2) % 2, (dp // (2 * wide)) % 2
    sibling = dp + 1 - 2 * core
    beside = dp + 2 - 4 * col
    above = dp + 2 * wide - 4 * wide * row
    return (row, col, core), (sibling, beside, above)


def meet(peers):
    barrier = pltpu.get_barrier_semaphore()
    for peer in peers:
        pl.semaphore_signal(barrier, inc=1, device_id={"dp": peer}, device_id_type=MESH)
    pl.semaphore_wait(barrier, len(peers))


SIB, XN, YN = 0, 1, 2


def spread_kernel(wide, z_size, mlp_count, *refs):
    attn_count = (len(refs) - 3) // 2 - mlp_count
    count = mlp_count + attn_count
    ins, outs = refs[:count], refs[count : 2 * count]
    own_sem, send_sem, recv_sem = refs[2 * count :]
    (row, col, core), _ = neighbours(wide)
    dp, place = lax.axis_index("dp"), lax.axis_index("tensor")
    mine = 4 * row + 2 * col + core
    base = dp - (2 * wide * row + 2 * col + core)

    def peer(dy, dx, dc):
        y, x, c = (row + dy) % 2, (col + dx) % 2, (core + dc) % 2
        return base + 2 * wide * y + 2 * x + c, 4 * y + 2 * x + c

    flips = [(dy, dx, dc) for dy in range(2) for dx in range(2) for dc in range(2)][1:]
    barrier = pltpu.get_barrier_semaphore()
    for flip in flips:
        pl.semaphore_signal(
            barrier, inc=1, device_id={"dp": peer(*flip)[0]}, device_id_type=MESH
        )
    for step in range(1, z_size):
        pl.semaphore_signal(
            barrier, inc=1, device_id={"tensor": (place + step) % z_size}, device_id_type=MESH
        )
    pl.semaphore_wait(barrier, len(flips) + z_size - 1)

    copies, local = [], []
    slot = 0
    for at in range(mlp_count, count):
        src, dst = ins[at], outs[at]
        cols = src.shape[1]
        part = pl.ds(pl.multiple_of(place * cols, LANES), cols)
        for step in range(1, z_size):
            copies.append(
                pltpu.make_async_remote_copy(
                    src_ref=src, dst_ref=dst.at[:, part],
                    send_sem=send_sem.at[slot], recv_sem=recv_sem.at[slot],
                    device_id={"tensor": (place + step) % z_size}, device_id_type=MESH,
                )
            )
            slot += 1
        local.append(pltpu.make_async_copy(src, dst.at[:, part], own_sem.at[at]))
    for at in range(mlp_count):
        src, dst = ins[at], outs[at]
        rows, cols = src.shape[0], dst.shape[1]
        here = pl.ds(pl.multiple_of(mine * rows, rows), rows)
        for flip in flips:
            device, other = peer(*flip)
            copies.append(
                pltpu.make_async_remote_copy(
                    src_ref=src.at[:, pl.ds(pl.multiple_of(other * cols, LANES), cols)],
                    dst_ref=dst.at[here],
                    send_sem=send_sem.at[slot], recv_sem=recv_sem.at[slot],
                    device_id={"dp": device}, device_id_type=MESH,
                )
            )
            slot += 1
        own = src.at[:, pl.ds(pl.multiple_of(mine * cols, LANES), cols)]
        local.append(pltpu.make_async_copy(own, dst.at[here], own_sem.at[at]))
    for copy in copies:
        copy.start()
    for copy in local:
        copy.start()
    for copy in local:
        copy.wait()
    for copy in copies:
        copy.wait()


def spread_weights(mlp, attn, dp_size, z_size):
    count = len(mlp) + len(attn)
    slots = (z_size - 1) * len(attn) + (GROUP - 1) * len(mlp)
    spec = pl.BlockSpec(memory_space=pl.ANY)
    out = [jax.ShapeDtypeStruct((GROUP * w.shape[0], w.shape[1] // GROUP), BF16) for w in mlp]
    out += [jax.ShapeDtypeStruct((w.shape[0], z_size * w.shape[1]), BF16) for w in attn]
    return pl.pallas_call(
        functools.partial(spread_kernel, 2 * math.isqrt(dp_size // GROUP), z_size, len(mlp)),
        in_specs=[spec] * count,
        out_specs=[spec] * count,
        out_shape=out,
        scratch_shapes=[
            pltpu.SemaphoreType.DMA((count,)),
            pltpu.SemaphoreType.DMA((slots,)),
            pltpu.SemaphoreType.DMA((slots,)),
        ],
        compiler_params=pltpu.CompilerParams(collective_id=2, has_side_effects=True),
    )(*mlp, *attn)


class Ring:
    FLIP = {SIB: (0, 0, 1), XN: (0, 1, 0), YN: (1, 0, 0)}
    COPIES = 14

    def __init__(self, wide, ref, rows, send_sem, recv_sem):
        (self.row, self.col, self.core), self.peers = neighbours(wide)
        self.ref, self.rows, self.part = ref, rows, rows // 2
        self.send_sem, self.recv_sem = send_sem, recv_sem
        self.sends = {}
        for half in range(2):
            self.sends["own", XN, half] = (2 + half, 0, 0, 0, half)
            self.sends["own", YN, half] = (4 + half, 0, 0, 0, half)
            self.sends["own", SIB, half] = (0 + half, 0, 0, 0, half)
        for half in range(2):
            self.sends["x", SIB, half] = (6 + half, 0, 1, 0, half)
            self.sends["y", SIB, half] = (8 + half, 1, 0, 0, half)
            self.sends["d", SIB, half] = (10 + half, 1, 1, 0, half)
        self.sends["x", YN, 0] = (12, 0, 1, 0, 0)
        self.sends["y", XN, 1] = (13, 1, 0, 0, 1)

    def place(self, dy, dx, dc, half):
        p = 4 * ((self.row + dy) % 2) + 2 * ((self.col + dx) % 2) + (self.core + dc) % 2
        return pl.ds(pl.multiple_of(p * self.rows + half * self.part, self.part), self.part)

    def mine(self):
        p = 4 * self.row + 2 * self.col + self.core
        return pl.ds(pl.multiple_of(p * self.rows, self.rows), self.rows)

    def copy(self, slot, dy, dx, dc, half, peer):
        where = self.place(dy, dx, dc, half)
        return pltpu.make_async_remote_copy(
            src_ref=self.ref.at[where], dst_ref=self.ref.at[where],
            send_sem=self.send_sem.at[slot], recv_sem=self.recv_sem.at[slot],
            device_id={"dp": self.peers[peer]}, device_id_type=MESH,
        )

    def start(self, name, peer, half):
        self.copy(*self.sends[name, peer, half], peer).start()

    def arrived(self, name, peer, half):
        slot, dy, dx, dc, half = self.sends[name, peer, half]
        fy, fx, fc = self.FLIP[peer]
        self.copy(slot, (dy + fy) % 2, (dx + fx) % 2, (dc + fc) % 2, half, peer).wait_recv()

    def start_own(self):
        for half in range(2):
            for peer in (XN, YN, SIB):
                self.start("own", peer, half)

    def first_halves(self):
        self.arrived("own", XN, 0)
        self.start("x", YN, 0)
        self.start("x", SIB, 0)
        self.arrived("own", YN, 0)
        self.start("y", SIB, 0)

    def second_halves(self):
        self.arrived("own", YN, 1)
        self.start("y", XN, 1)
        self.start("y", SIB, 1)
        self.arrived("own", XN, 1)
        self.start("x", SIB, 1)

    def far_halves(self):
        self.arrived("x", YN, 0)
        self.start("d", SIB, 0)
        self.arrived("y", XN, 1)
        self.start("d", SIB, 1)

    def from_sibling(self, name, *halves):
        for half in halves:
            self.arrived(name, SIB, half)

    def sent(self):
        for (name, peer, half), entry in self.sends.items():
            self.copy(*entry, peer).wait_send()


def gather_kernel(wide, count, *refs):
    ins, outs = refs[:count], refs[count : 2 * count]
    own_sem, send_sem, recv_sem = refs[2 * count :]
    rings = [
        Ring(wide, outs[at], ins[at].shape[0], send_sem.at[at], recv_sem.at[at])
        for at in range(count)
    ]
    local = [
        pltpu.make_async_copy(ins[at], outs[at].at[rings[at].mine()], own_sem.at[at])
        for at in range(count)
    ]
    for copy in local:
        copy.start()
    meet(rings[0].peers)
    for copy, ring in zip(local, rings):
        copy.wait()
        ring.start_own()
    for ring in rings:
        ring.first_halves()
        ring.second_halves()
    for ring in rings:
        ring.far_halves()
        for name in ("own", "x", "y", "d"):
            ring.from_sibling(name, 0, 1)
    for ring in rings:
        ring.sent()


def gather_rows(arrays, dp_size):
    count = len(arrays)
    spec = pl.BlockSpec(memory_space=pl.ANY)
    return pl.pallas_call(
        functools.partial(gather_kernel, 2 * math.isqrt(dp_size // GROUP), count),
        in_specs=[spec] * count,
        out_specs=[spec] * count,
        out_shape=[jax.ShapeDtypeStruct((GROUP * a.shape[0], a.shape[1]), a.dtype) for a in arrays],
        scratch_shapes=[
            pltpu.SemaphoreType.DMA((count,)),
            pltpu.SemaphoreType.DMA((count, Ring.COPIES)),
            pltpu.SemaphoreType.DMA((count, Ring.COPIES)),
        ],
        compiler_params=pltpu.CompilerParams(collective_id=3, has_side_effects=True),
    )(*arrays)


def gate_up_kernel(
    wide, own_ref, wg_ref, wu_ref, all_ref, gate_ref, up_ref, hid_ref,
    full, stage, own_sem, send_sem, recv_sem, out_sem, all_sem,
):
    rows = own_ref.shape[0]
    cols = gate_ref.shape[1]
    ring = Ring(wide, full, rows, send_sem, recv_sem)
    local = pltpu.make_async_copy(own_ref, full.at[ring.mine()], own_sem)
    local.start()
    meet(ring.peers)
    local.wait()
    ring.start_own()

    def out_copies(slot, where):
        return [
            pltpu.make_async_copy(stage.at[slot, i], ref.at[where], out_sem.at[slot, i])
            for i, ref in enumerate((gate_ref, up_ref, hid_ref))
        ] + [pltpu.make_async_copy(full.at[where], all_ref.at[where], all_sem.at[slot])]

    def step_place(step):
        phase, i = step // 4, step % 4
        high, low = phase // 2, phase % 2
        first, last = (1 - high) * (1 - low), high * low
        middle = high + low - 2 * last
        half = (first + last) * (i % 2) + high * (1 - low)
        dx = middle * (1 - i % 2) + last
        dy = middle * (i % 2) + last
        return ring.place(dy, dx, i // 2, half)

    @pl.loop(0, 16)
    def _(step):
        pl.when(step == 2)(lambda: ring.from_sibling("own", 0, 1))
        pl.when(step == 4)(ring.first_halves)

        @pl.when(step == 6)
        def _():
            ring.from_sibling("x", 0)
            ring.from_sibling("y", 0)

        pl.when(step == 8)(ring.second_halves)

        @pl.when(step == 10)
        def _():
            ring.from_sibling("x", 1)
            ring.from_sibling("y", 1)

        pl.when(step == 12)(ring.far_halves)
        pl.when(step == 14)(lambda: ring.from_sibling("d", 0, 1))

        slot = step % 2
        where = step_place(step)

        @pl.when(step >= 2)
        def _():
            for copy in out_copies(slot, step_place(step - 2)):
                copy.wait()

        x = full[where, :]

        @pl.loop(0, cols // NTILE)
        def _(at):
            n = pl.ds(pl.multiple_of(at * NTILE, NTILE), NTILE)
            gate = dot_nn(x, wg_ref[:, n])
            up = dot_nn(x, wu_ref[:, n])
            stage[slot, 0, :, n] = gate.astype(BF16)
            stage[slot, 1, :, n] = up.astype(BF16)
            stage[slot, 2, :, n] = (gate * up / (1.0 + jnp.exp(-gate))).astype(BF16)

        for copy in out_copies(slot, where):
            copy.start()

    for step in (14, 15):
        for copy in out_copies(step % 2, step_place(step)):
            copy.wait()
    ring.sent()


def gate_up(hn, wg, wu, dp_size):
    rows, width = hn.shape
    cols = wg.shape[1]
    tokens = GROUP * rows
    far = pl.BlockSpec(memory_space=pl.ANY)
    near = pl.BlockSpec(memory_space=pltpu.VMEM)
    return pl.pallas_call(
        functools.partial(gate_up_kernel, 2 * math.isqrt(dp_size // GROUP)),
        in_specs=[far, near, near],
        out_specs=[far] * 4,
        out_shape=[jax.ShapeDtypeStruct((tokens, width), BF16)]
        + [jax.ShapeDtypeStruct((tokens, cols), BF16)] * 3,
        scratch_shapes=[
            pltpu.VMEM((tokens, width), BF16),
            pltpu.VMEM((2, 3, rows // 2, cols), BF16),
            pltpu.SemaphoreType.DMA,
            pltpu.SemaphoreType.DMA((Ring.COPIES,)),
            pltpu.SemaphoreType.DMA((Ring.COPIES,)),
            pltpu.SemaphoreType.DMA((2, 3)),
            pltpu.SemaphoreType.DMA((2,)),
        ],
        compiler_params=pltpu.CompilerParams(
            collective_id=1, has_side_effects=True, vmem_limit_bytes=56 << 20
        ),
        cost_estimate=pl.CostEstimate(
            flops=4 * tokens * width * cols,
            bytes_accessed=tokens * (2 * width + 6 * cols) + 4 * width * cols,
            transcendentals=tokens * cols,
        ),
    )(hn, wg, wu)


class Layout:
    def __init__(self, dp_size):
        self.blocks = dp_size // GROUP
        side = math.isqrt(self.blocks)
        self.rows, self.cols = side, self.blocks // side
        wide = 2 * self.cols

        def index(by, bx, y, x, core):
            return ((2 * by + y) * wide + 2 * bx + x) * 2 + core

        places = [(y, x, c) for y in range(2) for x in range(2) for c in range(2)]
        spots = [(by, bx) for by in range(self.rows) for bx in range(self.cols)]
        self.inner = [[index(*s, *p) for p in places] for s in spots]
        self.outer = [[index(*s, *p) for s in spots] for p in places]

    def groups(self):
        return None if self.blocks == 1 else self.inner

    def to_rows(self, array):
        if self.blocks == 1:
            return array
        rest = array.shape[1:]
        split = array.reshape(2, 2, 2, self.rows, self.cols, -1, *rest)
        order = (3, 0, 4, 1, 2, 5) + tuple(range(6, 6 + len(rest)))
        return split.transpose(order).reshape(array.shape)

    def from_rows(self, array):
        if self.blocks == 1:
            return array
        rest = array.shape[1:]
        split = array.reshape(self.rows, 2, self.cols, 2, 2, -1, *rest)
        order = (1, 3, 4, 0, 2, 5) + tuple(range(6, 6 + len(rest)))
        return split.transpose(order).reshape(array.shape)

    def gather_outer(self, array):
        if self.blocks == 1:
            return array
        return lax.all_gather(array, "dp", axis_index_groups=self.outer, axis=0, tiled=True)

    def scatter_outer(self, array):
        if self.blocks == 1:
            return array
        return lax.psum_scatter(
            array, "dp", scatter_dimension=0, axis_index_groups=self.outer, tiled=True
        )

    def gather(self, array):
        return lax.all_gather(array, "dp", axis_index_groups=self.groups(), axis=0, tiled=True)

    def scatter(self, array):
        return lax.psum_scatter(
            array, "dp", scatter_dimension=0, axis_index_groups=self.groups(), tiled=True
        )

    def spread(self, array):
        return lax.all_to_all(
            array, "dp", 1, 0, axis_index_groups=self.groups(), tiled=True
        )

    def unspread(self, array):
        return lax.all_to_all(
            array, "dp", 0, 1, axis_index_groups=self.groups(), tiled=True
        )


def rms_scale(values):
    return lax.rsqrt(jnp.mean(values * values, axis=-1, keepdims=True) + NORM_EPS)


def norm_back(values, scaling, gain, grad):
    gained = grad * gain
    gain_part = jnp.sum(grad * values * scaling, axis=0)
    inner = jnp.mean(gained * values, axis=-1, keepdims=True)
    return gain_part, scaling * gained - values * scaling * scaling * scaling * inner


def gather_all(array):
    return lax.all_gather(
        lax.all_gather(array, "tensor", axis=1, tiled=True), "dp", axis=0, tiled=True
    )


def scatter_all(array):
    part = lax.psum_scatter(array.astype(BF16), "dp", scatter_dimension=0, tiled=True)
    return lax.psum_scatter(part, "tensor", scatter_dimension=1, tiled=True).astype(F32)


def per_device(
    dp_size, z_size, activations, segment_ids, attn_gain, w_query, w_key, w_value, w_out,
    mlp_gain, w_gate, w_up, w_down, cotangent,
):
    layout = Layout(dp_size)
    rows, width = activations.shape[1:]
    x = activations[0].astype(F32)
    place = lax.axis_index("tensor")
    reach = -(-(MOST_DOC - 1) // rows) * rows

    def shift(array, step):
        pairs = [(at, at + step) for at in range(z_size) if 0 <= at + step < z_size]
        return lax.ppermute(array, "tensor", pairs)

    starts = document_starts(segment_ids[0])
    own_starts = lax.dynamic_slice_in_dim(starts, place * rows, rows)
    own_tokens = place * rows + jnp.arange(rows, dtype=jnp.int32)
    cosine, sine = rope_tables(own_tokens - own_starts)
    low = (own_starts - place * rows + reach)[None, :]

    shards = [
        layout.gather_outer(w)
        for w in (w_gate, w_up, w_down, jnp.concatenate([w_key, w_value], axis=1), w_query, w_out)
    ]
    spread = spread_weights(shards[:3], shards[3:], dp_size, z_size)
    wg, wu, wd = (
        layout.to_rows(lax.all_gather(w, "tensor", axis=1, tiled=True)) for w in spread[:3]
    )
    wkv, wq, wo = (layout.to_rows(w) for w in gather_rows(spread[3:], dp_size))

    r1 = rms_scale(x)
    xn = (x * r1 * attn_gain).astype(BF16)
    q, kv = project_qkv(xn, wq, wkv, cosine, sine)
    pieces, moved = [kv], kv
    for _ in range(reach // rows):
        moved = shift(moved, 1)
        pieces.insert(0, moved)
    kv_all = jnp.concatenate(pieces, axis=0)
    att, lse = attend(q, kv_all, low)
    h = x + dot_nt(att, wo)

    r2 = rms_scale(h)
    hn, gate, up, hidden = gate_up((h * r2 * mlp_gain).astype(BF16), wg, wu, dp_size)
    grad, wd = lax.optimization_barrier((cotangent[0], wd))
    dy = layout.gather(grad)
    gate, up = gate.astype(F32), up.astype(F32)
    sigma = jax.nn.sigmoid(gate)
    output = h + layout.scatter(dot_nt(hidden, wd).astype(BF16)).astype(F32)
    dhid = dot_nn(dy, wd)
    dgate = (dhid * up * sigma * (1.0 + gate * (1.0 - sigma))).astype(BF16)
    dup = (dhid * gate * sigma).astype(BF16)
    dhn = layout.scatter((dot_nt(dgate, wg) + dot_nt(dup, wu)).astype(BF16)).astype(F32)

    def mlp_grad(left, right):
        total = layout.from_rows(dot_tn(left, right).astype(BF16))
        part = lax.psum_scatter(total, "tensor", scatter_dimension=1, tiled=True)
        return layout.scatter_outer(layout.unspread(part)).astype(F32)

    wd_grad = mlp_grad(dy, hidden)
    wg_grad = mlp_grad(hn, dgate)
    wu_grad = mlp_grad(hn, dup)
    gain_two, dh_norm = norm_back(h, r2, mlp_gain, dhn)
    dh = cotangent[0].astype(F32) + dh_norm

    dhb = dh.astype(BF16)
    wo_grad = scatter_all(dot_tn(dhb, att))
    datt = dot_nn(dhb, wo).astype(BF16)
    dq, dkv_all = attend_back(q, datt, att, kv_all, lse, low, cosine, sine)
    count = reach // rows
    moved = dkv_all[:rows]
    for at in range(1, count + 1):
        moved = shift(moved, -1)
        if at < count:
            here = dkv_all[at * rows : (at + 1) * rows]
            moved = (moved.astype(F32) + here.astype(F32)).astype(BF16)
    dkv = finish_dkv(dkv_all[count * rows :], moved, cosine, sine)
    wq_grad = scatter_all(dot_tn(xn, dq))
    wkv_grad = scatter_all(dot_tn(xn, dkv))
    key_cols = w_key.shape[1]
    dxn = dot_nt(dq, wq) + dot_nt(dkv, wkv)
    gain_one, dx_norm = norm_back(x, r1, attn_gain, dxn)
    input_grad = (dh + dx_norm).astype(BF16)
    gain_one, gain_two = lax.psum((gain_one, gain_two), ("dp", "tensor"))
    return (
        output.astype(BF16)[None],
        input_grad[None],
        gain_one,
        wq_grad,
        wkv_grad[:, :key_cols],
        wkv_grad[:, key_cols:],
        wo_grad,
        gain_two,
        wg_grad,
        wu_grad,
        wd_grad,
    )


def solution(mesh):
    split = P("dp", "tensor")
    tokens = P("dp", "tensor", None)
    in_specs = (
        tokens, P("dp", None), P(), split, split, split, split, P(), split, split, split, tokens,
    )
    out_specs = (tokens, tokens, P(), split, split, split, split, P(), split, split, split)
    return jax.shard_map(
        functools.partial(per_device, mesh.shape["dp"], mesh.shape["tensor"]),
        mesh=mesh, in_specs=in_specs, out_specs=out_specs, check_vma=False,
    )
```

```python
import functools
import math

import jax
import jax.numpy as jnp
from jax import lax
from jax.experimental import pallas as pl
from jax.experimental.pallas import tpu as pltpu
from jax.sharding import PartitionSpec as P

HEAD_DIM = 64
DOCS = 4
MOST_DOC = 1024
NORM_EPS = 1e-05
ROPE_THETA = 500000.0
GROUP = 8
LANES = 128
QTILE = 256
SCALE = HEAD_DIM ** (-0.5)
LOG2E = 1.4426950408889634
FAR = -1e30
NTILE = 512
STRIP = 16
LONG = 60_000_000_000

F32 = jnp.float32
BF16 = jnp.bfloat16


def dot_nn(left, right):
    return lax.dot_general(left, right, (((1,), (0,)), ((), ())), preferred_element_type=F32)


def dot_nt(left, right):
    return lax.dot_general(left, right, (((1,), (1,)), ((), ())), preferred_element_type=F32)


def dot_tn(left, right):
    return lax.dot_general(left, right, (((0,), (0,)), ((), ())), preferred_element_type=F32)


def document_starts(segments):
    doc_ids = jnp.arange(DOCS, dtype=jnp.int32)
    counts = jnp.sum((segments[:, None] == doc_ids).astype(jnp.int32), axis=0)
    before = (doc_ids < segments[:, None]).astype(jnp.int32)
    return jnp.sum(before * counts[None, :], axis=-1)


def rope_tables(positions):
    half = HEAD_DIM // 2
    frequency = jnp.exp(
        jnp.arange(half, dtype=F32) * (-2.0 * math.log(ROPE_THETA) / HEAD_DIM)
    )
    angles = positions.astype(F32)[:, None] * frequency
    cosine, sine = jnp.cos(angles), jnp.sin(angles)
    wide_cos = jnp.concatenate([cosine] * 4, axis=1)
    wide_sin = jnp.concatenate([-sine, sine, -sine, sine], axis=1)
    return wide_cos, wide_sin


def swap_halves(values):
    lane = lax.broadcasted_iota(jnp.int32, values.shape, 1)
    ahead = pltpu.roll(values, LANES - 32, 1)
    behind = pltpu.roll(values, 32, 1)
    return jnp.where((lane % 64) < 32, ahead, behind)


def qkv_kernel(x_ref, wq_ref, wkv_ref, cos_ref, sin_ref, q_ref, kv_ref):
    x = x_ref[...]
    cosine, sine = cos_ref[...], sin_ref[...]
    for at in range(wq_ref.shape[1] // LANES):
        part = pl.ds(at * LANES, LANES)
        value = dot_nn(x, wq_ref[:, part])
        q_ref[:, part] = (value * cosine + swap_halves(value) * sine).astype(BF16)
    value = dot_nn(x, wkv_ref[...])
    key = value[:, :LANES]
    kv_ref[:, :LANES] = (key * cosine + swap_halves(key) * sine).astype(BF16)
    kv_ref[:, LANES:] = value[:, LANES:].astype(BF16)


def project_qkv(x, wq, wkv, cosine, sine):
    rows, width = x.shape
    blocks = wkv.shape[1] // (2 * LANES)
    qcols = wq.shape[1] // blocks
    return pl.pallas_call(
        qkv_kernel,
        grid=(blocks,),
        in_specs=[
            pl.BlockSpec((rows, width), lambda g: (0, 0)),
            pl.BlockSpec((width, qcols), lambda g: (0, g)),
            pl.BlockSpec((width, 2 * LANES), lambda g: (0, g)),
            pl.BlockSpec((rows, LANES), lambda g: (0, 0)),
            pl.BlockSpec((rows, LANES), lambda g: (0, 0)),
        ],
        out_specs=[
            pl.BlockSpec((rows, qcols), lambda g: (0, g)),
            pl.BlockSpec((rows, 2 * LANES), lambda g: (0, g)),
        ],
        out_shape=[
            jax.ShapeDtypeStruct((rows, wq.shape[1]), BF16),
            jax.ShapeDtypeStruct((rows, wkv.shape[1]), BF16),
        ],
        compiler_params=pltpu.CompilerParams(vmem_limit_bytes=40 << 20),
        cost_estimate=pl.CostEstimate(
            flops=2 * rows * width * (wq.shape[1] + wkv.shape[1]),
            bytes_accessed=2 * width * (wq.shape[1] + wkv.shape[1]),
            transcendentals=0,
        ),
    )(x, wq, wkv, cosine, sine)


def fill_bias(bias_ref, low_ref, reach):
    span = bias_ref.shape[1]
    for tile in range(bias_ref.shape[0]):
        row = lax.broadcasted_iota(jnp.int32, (span, QTILE), 0)
        col = lax.broadcasted_iota(jnp.int32, (span, QTILE), 1)
        low = low_ref[0:1, tile * QTILE : (tile + 1) * QTILE]
        allowed = (row <= reach + col) & (row + tile * QTILE >= low)
        bias_ref[tile] = jnp.where(allowed, 0.0, FAR)


def spread_pair(pair, half):
    wide = pair.astype(F32)
    turned = pltpu.roll(wide, 64, 1)
    lane = lax.broadcasted_iota(jnp.int32, wide.shape, 1)
    mine = (lane // 64) == half
    even = half == 0
    first = jnp.where(mine, jnp.where(even, wide, turned), 0.0)
    second = jnp.where(mine, jnp.where(even, turned, wide), 0.0)
    return jnp.concatenate([first, second], axis=0).astype(BF16)


def gather_pair(transposed, half):
    count = transposed.shape[1] // 2
    mine = jnp.where(half == 0, transposed[:64], transposed[64:])
    return jnp.concatenate([mine[:, :count], mine[:, count:]], axis=0).T


def attend_kernel(reach, q_ref, k_ref, v_ref, low_ref, att_ref, lse_ref, bias_ref):
    head, tile, pair = pl.program_id(0), pl.program_id(1), pl.program_id(2)
    half = head % 2

    @pl.when((head == 0) & (tile == 0) & (pair == 0))
    def _():
        fill_bias(bias_ref, low_ref, reach)

    keys = pl.ds(pl.multiple_of(tile * QTILE, QTILE), bias_ref.shape[1])
    queries = spread_pair(q_ref[...], half)
    bias = bias_ref[tile]
    score = dot_nt(k_ref[keys, :], queries)
    score = score + jnp.concatenate([bias, bias], axis=1)
    top = jnp.max(score, axis=0, keepdims=True) * (SCALE * LOG2E)
    weight = jnp.exp2(score * (SCALE * LOG2E) - top)
    total = jnp.sum(weight, axis=0, keepdims=True)
    result = dot_tn(v_ref[keys, :], weight.astype(BF16)) / total
    att_ref[...] = gather_pair(result, half).astype(BF16)
    lse_ref[0] = top + jnp.log2(total)


def attend(q, kv, low):
    rows, width = q.shape
    keys = kv.shape[0]
    reach = keys - rows
    tiles = rows // QTILE
    pairs = width // LANES
    heads = kv.shape[1] // LANES
    per_head = pairs // heads
    span = reach + QTILE
    return pl.pallas_call(
        functools.partial(attend_kernel, reach),
        grid=(heads, tiles, per_head),
        in_specs=[
            pl.BlockSpec((QTILE, LANES), lambda a, t, p: (t, a * per_head + p)),
            pl.BlockSpec((keys, LANES), lambda a, t, p: (0, 2 * (a // 2))),
            pl.BlockSpec((keys, LANES), lambda a, t, p: (0, 2 * (a // 2) + 1)),
            pl.BlockSpec((1, rows), lambda a, t, p: (0, 0)),
        ],
        out_specs=[
            pl.BlockSpec((QTILE, LANES), lambda a, t, p: (t, a * per_head + p)),
            pl.BlockSpec((1, 1, 2 * QTILE), lambda a, t, p: ((a * tiles + t) * per_head + p, 0, 0)),
        ],
        out_shape=[
            jax.ShapeDtypeStruct((rows, width), BF16),
            jax.ShapeDtypeStruct((pairs * tiles, 1, 2 * QTILE), F32),
        ],
        scratch_shapes=[pltpu.VMEM((tiles, span, QTILE), F32)],
        compiler_params=pltpu.CompilerParams(vmem_limit_bytes=48 << 20),
        cost_estimate=pl.CostEstimate(
            flops=16 * rows * span * LANES * pairs,
            bytes_accessed=4 * rows * width + 2 * keys * kv.shape[1],
            transcendentals=2 * rows * span * pairs,
        ),
    )(q, kv, kv, low)


def attend_back_kernel(
    reach, q_ref, do_ref, o_ref, k_ref, v_ref, lse_ref, low_ref, cos_ref, sin_ref,
    dq_ref, dkv_ref, bias_ref, dk_acc, dv_acc,
):
    block, half, tile, pair = (pl.program_id(at) for at in range(4))
    inner = (half * pl.num_programs(2) + tile) * pl.num_programs(3) + pair

    @pl.when((block == 0) & (inner == 0))
    def _():
        fill_bias(bias_ref, low_ref, reach)

    @pl.when(inner == 0)
    def _():
        dk_acc[...] = jnp.zeros_like(dk_acc)
        dv_acc[...] = jnp.zeros_like(dv_acc)

    keys = pl.ds(pl.multiple_of(tile * QTILE, QTILE), bias_ref.shape[1])
    queries = spread_pair(q_ref[...], half)
    grads = spread_pair(do_ref[...], half)
    product = (do_ref[...].astype(F32) * o_ref[...].astype(F32)).T
    row_dot = jnp.concatenate(
        [
            jnp.sum(product[:64], axis=0, keepdims=True),
            jnp.sum(product[64:], axis=0, keepdims=True),
        ],
        axis=1,
    )
    bias = bias_ref[tile]
    key, value = k_ref[keys, :], v_ref[keys, :]
    score = dot_nt(key, queries) + jnp.concatenate([bias, bias], axis=1)
    weight = jnp.exp2(score * (SCALE * LOG2E) - lse_ref[0])
    dv_acc[keys, :] += dot_nn(weight.astype(BF16), grads)
    dscore = (weight * (dot_nt(value, grads) - row_dot)).astype(BF16)
    dk_acc[keys, :] += dot_nn(dscore, queries)
    dq = gather_pair(dot_tn(key, dscore), half) * SCALE
    dq_ref[...] = (dq * cos_ref[...] - swap_halves(dq) * sin_ref[...]).astype(BF16)

    @pl.when(inner == pl.num_programs(1) * pl.num_programs(2) * pl.num_programs(3) - 1)
    def _():
        dkv_ref[:, :LANES] = (dk_acc[...] * SCALE).astype(BF16)
        dkv_ref[:, LANES:] = dv_acc[...].astype(BF16)


def attend_back(q, do, att, kv, lse, low, cosine, sine):
    rows, width = q.shape
    keys = kv.shape[0]
    reach = keys - rows
    tiles = rows // QTILE
    pairs = width // LANES
    heads = kv.shape[1] // LANES
    per_head = pairs // heads
    span = reach + QTILE

    def pair_at(g, h, t, p):
        return (t, (2 * g + h) * per_head + p)

    return pl.pallas_call(
        functools.partial(attend_back_kernel, reach),
        grid=(heads // 2, 2, tiles, per_head),
        in_specs=[
            pl.BlockSpec((QTILE, LANES), pair_at),
            pl.BlockSpec((QTILE, LANES), pair_at),
            pl.BlockSpec((QTILE, LANES), pair_at),
            pl.BlockSpec((keys, LANES), lambda g, h, t, p: (0, 2 * g)),
            pl.BlockSpec((keys, LANES), lambda g, h, t, p: (0, 2 * g + 1)),
            pl.BlockSpec(
                (1, 1, 2 * QTILE),
                lambda g, h, t, p: (((2 * g + h) * tiles + t) * per_head + p, 0, 0),
            ),
            pl.BlockSpec((1, rows), lambda g, h, t, p: (0, 0)),
            pl.BlockSpec((QTILE, LANES), lambda g, h, t, p: (t, 0)),
            pl.BlockSpec((QTILE, LANES), lambda g, h, t, p: (t, 0)),
        ],
        out_specs=[
            pl.BlockSpec((QTILE, LANES), pair_at),
            pl.BlockSpec((keys, 2 * LANES), lambda g, h, t, p: (0, g)),
        ],
        out_shape=[
            jax.ShapeDtypeStruct((rows, width), BF16),
            jax.ShapeDtypeStruct(kv.shape, BF16),
        ],
        scratch_shapes=[
            pltpu.VMEM((tiles, span, QTILE), F32),
            pltpu.VMEM((keys, LANES), F32),
            pltpu.VMEM((keys, LANES), F32),
        ],
        compiler_params=pltpu.CompilerParams(vmem_limit_bytes=56 << 20),
        cost_estimate=pl.CostEstimate(
            flops=40 * rows * span * LANES * pairs,
            bytes_accessed=8 * rows * width + 4 * keys * kv.shape[1],
            transcendentals=2 * rows * span * pairs,
        ),
    )(q, do, att, kv, kv, lse, low, cosine, sine)


def finish_dkv_kernel(own_ref, recv_ref, cos_ref, sin_ref, out_ref):
    total = own_ref[...].astype(F32) + recv_ref[...].astype(F32)
    key = total[:, :LANES]
    out_ref[:, :LANES] = (key * cos_ref[...] - swap_halves(key) * sin_ref[...]).astype(BF16)
    out_ref[:, LANES:] = total[:, LANES:].astype(BF16)


def finish_dkv(own, recv, cosine, sine):
    rows, width = own.shape
    spec = pl.BlockSpec((rows, 2 * LANES), lambda g: (0, g))
    table = pl.BlockSpec((rows, LANES), lambda g: (0, 0))
    return pl.pallas_call(
        finish_dkv_kernel,
        grid=(width // (2 * LANES),),
        in_specs=[spec, spec, table, table],
        out_specs=spec,
        out_shape=jax.ShapeDtypeStruct((rows, width), BF16),
    )(own, recv, cosine, sine)


MESH = pl.DeviceIdType.MESH


def neighbours(wide):
    dp = lax.axis_index("dp")
    core, col, row = dp % 2, (dp // 2) % 2, (dp // (2 * wide)) % 2
    sibling = dp + 1 - 2 * core
    beside = dp + 2 - 4 * col
    above = dp + 2 * wide - 4 * wide * row
    return (row, col, core), (sibling, beside, above)


def meet(peers):
    barrier = pltpu.get_barrier_semaphore()
    for peer in peers:
        pl.semaphore_signal(barrier, inc=1, device_id={"dp": peer}, device_id_type=MESH)
    pl.semaphore_wait(barrier, len(peers))


SIB, XN, YN = 0, 1, 2


def spread_kernel(wide, z_size, mlp_count, *refs):
    attn_count = (len(refs) - 3) // 2 - mlp_count
    count = mlp_count + attn_count
    ins, outs = refs[:count], refs[count : 2 * count]
    own_sem, send_sem, recv_sem = refs[2 * count :]
    (row, col, core), _ = neighbours(wide)
    dp, place = lax.axis_index("dp"), lax.axis_index("tensor")
    mine = 4 * row + 2 * col + core
    base = dp - (2 * wide * row + 2 * col + core)

    def peer(dy, dx, dc):
        y, x, c = (row + dy) % 2, (col + dx) % 2, (core + dc) % 2
        return base + 2 * wide * y + 2 * x + c, 4 * y + 2 * x + c

    flips = [(dy, dx, dc) for dy in range(2) for dx in range(2) for dc in range(2)][1:]
    barrier = pltpu.get_barrier_semaphore()
    for flip in flips:
        pl.semaphore_signal(
            barrier, inc=1, device_id={"dp": peer(*flip)[0]}, device_id_type=MESH
        )
    for step in range(1, z_size):
        pl.semaphore_signal(
            barrier, inc=1, device_id={"tensor": (place + step) % z_size}, device_id_type=MESH
        )
    pl.semaphore_wait(barrier, len(flips) + z_size - 1)

    copies, local = [], []
    slot = 0
    for at in range(mlp_count, count):
        src, dst = ins[at], outs[at]
        cols = src.shape[1]
        part = pl.ds(pl.multiple_of(place * cols, LANES), cols)
        for step in range(1, z_size):
            copies.append(
                pltpu.make_async_remote_copy(
                    src_ref=src, dst_ref=dst.at[:, part],
                    send_sem=send_sem.at[slot], recv_sem=recv_sem.at[slot],
                    device_id={"tensor": (place + step) % z_size}, device_id_type=MESH,
                )
            )
            slot += 1
        local.append(pltpu.make_async_copy(src, dst.at[:, part], own_sem.at[at]))
    for at in range(mlp_count):
        src, dst = ins[at], outs[at]
        rows, cols = src.shape[0], dst.shape[1]
        here = pl.ds(pl.multiple_of(mine * rows, rows), rows)
        for flip in flips:
            device, other = peer(*flip)
            copies.append(
                pltpu.make_async_remote_copy(
                    src_ref=src.at[:, pl.ds(pl.multiple_of(other * cols, LANES), cols)],
                    dst_ref=dst.at[here],
                    send_sem=send_sem.at[slot], recv_sem=recv_sem.at[slot],
                    device_id={"dp": device}, device_id_type=MESH,
                )
            )
            slot += 1
        own = src.at[:, pl.ds(pl.multiple_of(mine * cols, LANES), cols)]
        local.append(pltpu.make_async_copy(own, dst.at[here], own_sem.at[at]))
    for copy in copies:
        copy.start()
    for copy in local:
        copy.start()
    for copy in local:
        copy.wait()
    for copy in copies:
        copy.wait()


def spread_weights(mlp, attn, dp_size, z_size):
    count = len(mlp) + len(attn)
    slots = (z_size - 1) * len(attn) + (GROUP - 1) * len(mlp)
    spec = pl.BlockSpec(memory_space=pl.ANY)
    out = [jax.ShapeDtypeStruct((GROUP * w.shape[0], w.shape[1] // GROUP), BF16) for w in mlp]
    out += [jax.ShapeDtypeStruct((w.shape[0], z_size * w.shape[1]), BF16) for w in attn]
    return pl.pallas_call(
        functools.partial(spread_kernel, 2 * math.isqrt(dp_size // GROUP), z_size, len(mlp)),
        in_specs=[spec] * count,
        out_specs=[spec] * count,
        out_shape=out,
        scratch_shapes=[
            pltpu.SemaphoreType.DMA((count,)),
            pltpu.SemaphoreType.DMA((slots,)),
            pltpu.SemaphoreType.DMA((slots,)),
        ],
        compiler_params=pltpu.CompilerParams(collective_id=2, has_side_effects=True),
        cost_estimate=pl.CostEstimate(flops=LONG, bytes_accessed=0, transcendentals=0),
    )(*mlp, *attn)


class Ring:
    FLIP = {SIB: (0, 0, 1), XN: (0, 1, 0), YN: (1, 0, 0)}
    COPIES = 14

    def __init__(self, wide, ref, rows, send_sem, recv_sem):
        (self.row, self.col, self.core), self.peers = neighbours(wide)
        self.ref, self.rows, self.part = ref, rows, rows // 2
        self.send_sem, self.recv_sem = send_sem, recv_sem
        self.sends = {}
        for half in range(2):
            self.sends["own", XN, half] = (2 + half, 0, 0, 0, half)
            self.sends["own", YN, half] = (4 + half, 0, 0, 0, half)
            self.sends["own", SIB, half] = (0 + half, 0, 0, 0, half)
        for half in range(2):
            self.sends["x", SIB, half] = (6 + half, 0, 1, 0, half)
            self.sends["y", SIB, half] = (8 + half, 1, 0, 0, half)
            self.sends["d", SIB, half] = (10 + half, 1, 1, 0, half)
        self.sends["x", YN, 0] = (12, 0, 1, 0, 0)
        self.sends["y", XN, 1] = (13, 1, 0, 0, 1)

    def place(self, dy, dx, dc, half):
        p = 4 * ((self.row + dy) % 2) + 2 * ((self.col + dx) % 2) + (self.core + dc) % 2
        return pl.ds(pl.multiple_of(p * self.rows + half * self.part, self.part), self.part)

    def mine(self):
        p = 4 * self.row + 2 * self.col + self.core
        return pl.ds(pl.multiple_of(p * self.rows, self.rows), self.rows)

    def copy(self, slot, dy, dx, dc, half, peer):
        where = self.place(dy, dx, dc, half)
        return pltpu.make_async_remote_copy(
            src_ref=self.ref.at[where], dst_ref=self.ref.at[where],
            send_sem=self.send_sem.at[slot], recv_sem=self.recv_sem.at[slot],
            device_id={"dp": self.peers[peer]}, device_id_type=MESH,
        )

    def start(self, name, peer, half):
        self.copy(*self.sends[name, peer, half], peer).start()

    def arrived(self, name, peer, half):
        slot, dy, dx, dc, half = self.sends[name, peer, half]
        fy, fx, fc = self.FLIP[peer]
        self.copy(slot, (dy + fy) % 2, (dx + fx) % 2, (dc + fc) % 2, half, peer).wait_recv()

    def start_own(self):
        for half in range(2):
            for peer in (XN, YN, SIB):
                self.start("own", peer, half)

    def first_halves(self):
        self.arrived("own", XN, 0)
        self.start("x", YN, 0)
        self.start("x", SIB, 0)
        self.arrived("own", YN, 0)
        self.start("y", SIB, 0)

    def second_halves(self):
        self.arrived("own", YN, 1)
        self.start("y", XN, 1)
        self.start("y", SIB, 1)
        self.arrived("own", XN, 1)
        self.start("x", SIB, 1)

    def far_halves(self):
        self.arrived("x", YN, 0)
        self.start("d", SIB, 0)
        self.arrived("y", XN, 1)
        self.start("d", SIB, 1)

    def from_sibling(self, name, *halves):
        for half in halves:
            self.arrived(name, SIB, half)

    def sent(self):
        for (name, peer, half), entry in self.sends.items():
            self.copy(*entry, peer).wait_send()


def gather_kernel(wide, count, *refs):
    ins, outs = refs[:count], refs[count : 2 * count]
    own_sem, send_sem, recv_sem = refs[2 * count :]
    rings = [
        Ring(wide, outs[at], ins[at].shape[0], send_sem.at[at], recv_sem.at[at])
        for at in range(count)
    ]
    local = [
        pltpu.make_async_copy(ins[at], outs[at].at[rings[at].mine()], own_sem.at[at])
        for at in range(count)
    ]
    for copy in local:
        copy.start()
    meet(rings[0].peers)
    for copy, ring in zip(local, rings):
        copy.wait()
        ring.start_own()
    for ring in rings:
        ring.first_halves()
        ring.second_halves()
    for ring in rings:
        ring.far_halves()
        for name in ("own", "x", "y", "d"):
            ring.from_sibling(name, 0, 1)
    for ring in rings:
        ring.sent()


def gather_rows(arrays, dp_size):
    count = len(arrays)
    spec = pl.BlockSpec(memory_space=pl.ANY)
    return pl.pallas_call(
        functools.partial(gather_kernel, 2 * math.isqrt(dp_size // GROUP), count),
        in_specs=[spec] * count,
        out_specs=[spec] * count,
        out_shape=[jax.ShapeDtypeStruct((GROUP * a.shape[0], a.shape[1]), a.dtype) for a in arrays],
        scratch_shapes=[
            pltpu.SemaphoreType.DMA((count,)),
            pltpu.SemaphoreType.DMA((count, Ring.COPIES)),
            pltpu.SemaphoreType.DMA((count, Ring.COPIES)),
        ],
        compiler_params=pltpu.CompilerParams(collective_id=3, has_side_effects=True),
        cost_estimate=pl.CostEstimate(flops=2 * LONG, bytes_accessed=0, transcendentals=0),
    )(*arrays)


def gate_up_kernel(
    wide, own_ref, wg_ref, wu_ref, all_ref, gate_ref, up_ref, hid_ref,
    full, stage, own_sem, send_sem, recv_sem, out_sem, all_sem,
):
    rows = own_ref.shape[0]
    cols = gate_ref.shape[1]
    ring = Ring(wide, full, rows, send_sem, recv_sem)
    local = pltpu.make_async_copy(own_ref, full.at[ring.mine()], own_sem)
    local.start()
    meet(ring.peers)
    local.wait()
    ring.start_own()

    def out_copies(slot, where):
        return [
            pltpu.make_async_copy(stage.at[slot, i], ref.at[where], out_sem.at[slot, i])
            for i, ref in enumerate((gate_ref, up_ref, hid_ref))
        ] + [pltpu.make_async_copy(full.at[where], all_ref.at[where], all_sem.at[slot])]

    def step_place(step):
        phase, i = step // 4, step % 4
        high, low = phase // 2, phase % 2
        first, last = (1 - high) * (1 - low), high * low
        middle = high + low - 2 * last
        half = (first + last) * (i % 2) + high * (1 - low)
        dx = middle * (1 - i % 2) + last
        dy = middle * (i % 2) + last
        return ring.place(dy, dx, i // 2, half)

    @pl.loop(0, 16)
    def _(step):
        pl.when(step == 2)(lambda: ring.from_sibling("own", 0, 1))
        pl.when(step == 4)(ring.first_halves)

        @pl.when(step == 6)
        def _():
            ring.from_sibling("x", 0)
            ring.from_sibling("y", 0)

        pl.when(step == 8)(ring.second_halves)

        @pl.when(step == 10)
        def _():
            ring.from_sibling("x", 1)
            ring.from_sibling("y", 1)

        pl.when(step == 12)(ring.far_halves)
        pl.when(step == 14)(lambda: ring.from_sibling("d", 0, 1))

        slot = step % 2
        where = step_place(step)

        @pl.when(step >= 2)
        def _():
            for copy in out_copies(slot, step_place(step - 2)):
                copy.wait()

        x = full[where, :]

        @pl.loop(0, cols // NTILE)
        def _(at):
            n = pl.ds(pl.multiple_of(at * NTILE, NTILE), NTILE)
            gate = dot_nn(x, wg_ref[:, n])
            up = dot_nn(x, wu_ref[:, n])
            stage[slot, 0, :, n] = gate.astype(BF16)
            stage[slot, 1, :, n] = up.astype(BF16)
            stage[slot, 2, :, n] = (gate * up / (1.0 + jnp.exp(-gate))).astype(BF16)

        for copy in out_copies(slot, where):
            copy.start()

    for step in (14, 15):
        for copy in out_copies(step % 2, step_place(step)):
            copy.wait()
    ring.sent()


def gate_up(hn, wg, wu, dp_size):
    rows, width = hn.shape
    cols = wg.shape[1]
    tokens = GROUP * rows
    far = pl.BlockSpec(memory_space=pl.ANY)
    near = pl.BlockSpec(memory_space=pltpu.VMEM)
    return pl.pallas_call(
        functools.partial(gate_up_kernel, 2 * math.isqrt(dp_size // GROUP)),
        in_specs=[far, near, near],
        out_specs=[far] * 4,
        out_shape=[jax.ShapeDtypeStruct((tokens, width), BF16)]
        + [jax.ShapeDtypeStruct((tokens, cols), BF16)] * 3,
        scratch_shapes=[
            pltpu.VMEM((tokens, width), BF16),
            pltpu.VMEM((2, 3, rows // 2, cols), BF16),
            pltpu.SemaphoreType.DMA,
            pltpu.SemaphoreType.DMA((Ring.COPIES,)),
            pltpu.SemaphoreType.DMA((Ring.COPIES,)),
            pltpu.SemaphoreType.DMA((2, 3)),
            pltpu.SemaphoreType.DMA((2,)),
        ],
        compiler_params=pltpu.CompilerParams(
            collective_id=1, has_side_effects=True, vmem_limit_bytes=56 << 20
        ),
        cost_estimate=pl.CostEstimate(
            flops=4 * tokens * width * cols,
            bytes_accessed=tokens * (2 * width + 6 * cols) + 4 * width * cols,
            transcendentals=tokens * cols,
        ),
    )(hn, wg, wu)


FAR_CHUNK, X_CHUNK, Y_CHUNK, OWN_CHUNK = range(4)


class Reduce:
    COPIES = 10

    def __init__(self, wide, parts, cores, far, near, send_sem, recv_sem):
        self.at, self.peers = neighbours(wide)
        self.parts, self.cores, self.far, self.near = parts, cores, far, near
        self.send_sem, self.recv_sem = send_sem, recv_sem
        self.half = parts.shape[2] // 2

    @staticmethod
    def scratch(rows, cols):
        return [
            pltpu.VMEM((2, 4, rows, cols), BF16),
            pltpu.VMEM((4, rows, cols), BF16),
            pltpu.VMEM((2, rows // 2, cols), BF16),
            pltpu.VMEM((2, rows, cols), BF16),
            pltpu.SemaphoreType.DMA((Reduce.COPIES,)),
            pltpu.SemaphoreType.DMA((Reduce.COPIES,)),
        ]

    def chunk(self, step):
        slot, other = step // 2, 1 - step % 2
        row, col, core = self.at
        dy, dx = 1 - slot % 2, 1 - slot // 2
        place = 4 * ((row + dy) % 2) + 2 * ((col + dx) % 2) + (core + other) % 2
        return place, self.parts.at[other, slot]

    def copy(self, name):
        upper, lower = pl.ds(0, self.half), pl.ds(self.half, self.half)
        mine = self.parts.at[0]
        table = {
            "far0": (self.parts.at[1, FAR_CHUNK], self.cores.at[FAR_CHUNK], SIB),
            "x": (self.parts.at[1, X_CHUNK], self.cores.at[X_CHUNK], SIB),
            "y": (self.parts.at[1, Y_CHUNK], self.cores.at[Y_CHUNK], SIB),
            "own": (self.parts.at[1, OWN_CHUNK], self.cores.at[OWN_CHUNK], SIB),
            "far_x": (mine.at[FAR_CHUNK, lower], self.far.at[0], XN),
            "far_y": (mine.at[FAR_CHUNK, upper], self.far.at[1], YN),
            "x_upper": (mine.at[X_CHUNK, upper], self.near.at[0, upper], XN),
            "x_lower": (mine.at[X_CHUNK, lower], self.near.at[0, lower], XN),
            "y_upper": (mine.at[Y_CHUNK, upper], self.near.at[1, upper], YN),
            "y_lower": (mine.at[Y_CHUNK, lower], self.near.at[1, lower], YN),
        }
        src, dst, peer = table[name]
        at = list(table).index(name)
        return pltpu.make_async_remote_copy(
            src_ref=src, dst_ref=dst, send_sem=self.send_sem.at[at],
            recv_sem=self.recv_sem.at[at], device_id={"dp": self.peers[peer]},
            device_id_type=MESH,
        )

    def start(self, *names):
        for name in names:
            self.copy(name).start()

    def add(self, slot, start, other):
        count = other.shape[0] // STRIP

        @pl.loop(0, count)
        def _(at):
            here = pl.ds(pl.multiple_of(start + at * STRIP, STRIP), STRIP)
            there = pl.ds(pl.multiple_of(at * STRIP, STRIP), STRIP)
            value = self.parts[0, slot, here, :].astype(F32) + other[there, :].astype(F32)
            self.parts[0, slot, here, :] = value.astype(BF16)

    def merge_core(self, slot, name):
        self.copy(name).wait_recv()
        self.add(slot, 0, self.cores.at[slot])

    def after(self, step):
        names = ("far0", "x", "y", "own")
        for slot in range(4):
            pl.when(step == 2 * slot)(functools.partial(self.start, names[slot]))

        @pl.when(step == 1)
        def _():
            self.merge_core(FAR_CHUNK, "far0")
            self.start("far_x", "far_y")

        @pl.when(step == 3)
        def _():
            self.merge_core(X_CHUNK, "x")
            self.start("x_lower")

        @pl.when(step == 5)
        def _():
            self.merge_core(Y_CHUNK, "y")
            self.start("y_upper")

    def pass_on(self):
        self.copy("far_y").wait_recv()
        self.add(X_CHUNK, 0, self.far.at[1])
        self.start("x_upper")
        self.copy("far_x").wait_recv()
        self.add(Y_CHUNK, self.half, self.far.at[0])
        self.start("y_lower")

    def finish(self, store):
        for name in ("own", "x_upper", "x_lower", "y_upper", "y_lower"):
            self.copy(name).wait_recv()

        @pl.loop(0, 2 * self.half // STRIP)
        def _(at):
            here = pl.ds(pl.multiple_of(at * STRIP, STRIP), STRIP)
            value = self.parts[0, OWN_CHUNK, here, :].astype(F32)
            value += self.cores[OWN_CHUNK, here, :].astype(F32)
            value += self.near[0, here, :].astype(F32)
            value += self.near[1, here, :].astype(F32)
            store(here, value)

    def sent(self):
        for name in (
            "far0", "x", "y", "own", "far_x", "far_y", "x_upper", "x_lower", "y_upper", "y_lower",
        ):
            self.copy(name).wait_send()


def tail_kernel(
    wide, z_size, x_ref, h_ref, dq_ref, dkv_ref, att_ref, gain_ref,
    wo_out, wq_out, wkv_out, gain_out,
    *scratch,
):
    own_scratch, (sums, zrecv, gain_z, gain_p, z_send, z_recv, g_send, g_recv) = (
        scratch[:18], scratch[18:],
    )
    rings = [Reduce(wide, *own_scratch[6 * at : 6 * at + 6]) for at in range(3)]
    place = lax.axis_index("tensor")
    dp = lax.axis_index("dp")
    row, col, core = rings[0].at
    mine = 4 * row + 2 * col + core
    base = dp - (2 * wide * row + 2 * col + core)
    flips = [(y, x, c) for y in range(2) for x in range(2) for c in range(2)][1:]

    def device(flip):
        y, x, c = (row + flip[0]) % 2, (col + flip[1]) % 2, (core + flip[2]) % 2
        return {"dp": base + 2 * wide * y + 2 * x + c}

    along = [{"tensor": (place + step) % z_size} for step in range(1, z_size)]
    around = [device(flip) for flip in flips]
    barrier = pltpu.get_barrier_semaphore()
    for peer in along + around:
        pl.semaphore_signal(barrier, inc=1, device_id=peer, device_id_type=MESH)
    pl.semaphore_wait(barrier, len(along) + len(around))

    gain_z[place] = gain_ref[...]
    gain_copies = [
        pltpu.make_async_remote_copy(
            src_ref=gain_ref, dst_ref=gain_z.at[place], send_sem=g_send.at[at],
            recv_sem=g_recv.at[at], device_id=peer, device_id_type=MESH,
        )
        for at, peer in enumerate(along)
    ]
    for copy in gain_copies:
        copy.start()

    lefts = (h_ref, x_ref, x_ref)
    rights = (att_ref, dq_ref, dkv_ref)
    rows = sums.shape[0]
    outs = (wo_out, wq_out, wkv_out)
    z_copies = []
    for index, ring in enumerate(rings):
        left, right = lefts[index], rights[index]
        cols = right.shape[1]

        @pl.loop(0, 8)
        def _(step):
            chunk, target = ring.chunk(step)
            x = left[:, pl.ds(pl.multiple_of(chunk * rows, rows), rows)].T

            @pl.loop(0, cols // NTILE)
            def _(at):
                n = pl.ds(pl.multiple_of(at * NTILE, NTILE), NTILE)
                target[:, n] = dot_nn(x, right[:, n]).astype(BF16)

            ring.after(step)

        if index == 0:
            for copy in gain_copies:
                copy.wait_recv()
            total = gain_z[0]
            for at in range(1, z_size):
                total = total + gain_z[at]
            gain_p[mine] = total
            for at, peer in enumerate(around):
                copy = pltpu.make_async_remote_copy(
                    src_ref=gain_p.at[mine], dst_ref=gain_p.at[mine],
                    send_sem=g_send.at[z_size - 1 + at], recv_sem=g_recv.at[z_size - 1 + at],
                    device_id=peer, device_id_type=MESH,
                )
                gain_copies.append(copy)
                copy.start()

    def send_along(index, ring, start):
        cols = rights[index].shape[1]
        part = cols // z_size

        def store(here, value):
            sums[here, pl.ds(start, cols)] = value.astype(BF16)

        ring.finish(store)
        for at, peer in enumerate(along):
            other = (place + at + 1) % z_size
            copy = pltpu.make_async_remote_copy(
                src_ref=sums.at[:, pl.ds(pl.multiple_of(start + other * part, LANES), part)],
                dst_ref=zrecv.at[at, :, pl.ds(start // z_size, part)],
                send_sem=z_send.at[index, at], recv_sem=z_recv.at[index, at],
                device_id=peer, device_id_type=MESH,
            )
            z_copies.append(copy)
            copy.start()

    starts = [0, rights[0].shape[1], rights[0].shape[1] + rights[1].shape[1]]
    for index, ring in enumerate(rings):
        ring.pass_on()
        if index:
            send_along(index - 1, rings[index - 1], starts[index - 1])
    send_along(2, rings[2], starts[2])

    for copy in gain_copies[z_size - 1 :]:
        copy.wait_recv()
    total = gain_p[0]
    for at in range(1, GROUP):
        total = total + gain_p[at]
    gain_out[...] = total

    for copy in z_copies:
        copy.wait_recv()
    for index in range(3):
        part = rights[index].shape[1] // z_size
        own = pl.ds(pl.multiple_of(starts[index] + place * part, LANES), part)
        value = sums[:, own].astype(F32)
        for at in range(z_size - 1):
            value += zrecv[at, :, pl.ds(starts[index] // z_size, part)].astype(F32)
        outs[index][...] = value
    for copy in z_copies + gain_copies:
        copy.wait_send()
    for ring in rings:
        ring.sent()


def attention_grads(x, h, dq, dkv, att, gains, dp_size, z_size):
    tokens, width = x.shape
    rows = width // GROUP
    near = pl.BlockSpec(memory_space=pltpu.VMEM)
    sizes = [att.shape[1], dq.shape[1], dkv.shape[1]]
    scratch = []
    for cols in sizes:
        scratch += Reduce.scratch(rows, cols)
    total = sum(sizes)
    return pl.pallas_call(
        functools.partial(tail_kernel, 2 * math.isqrt(dp_size // GROUP), z_size),
        in_specs=[near] * 6,
        out_specs=[near] * 4,
        out_shape=[jax.ShapeDtypeStruct((rows, cols // z_size), F32) for cols in sizes]
        + [jax.ShapeDtypeStruct(gains.shape, F32)],
        scratch_shapes=scratch
        + [
            pltpu.VMEM((rows, total), BF16),
            pltpu.VMEM((z_size - 1, rows, total // z_size), BF16),
            pltpu.VMEM((z_size, *gains.shape), F32),
            pltpu.VMEM((GROUP, *gains.shape), F32),
            pltpu.SemaphoreType.DMA((3, z_size - 1)),
            pltpu.SemaphoreType.DMA((3, z_size - 1)),
            pltpu.SemaphoreType.DMA((z_size - 1 + GROUP - 1,)),
            pltpu.SemaphoreType.DMA((z_size - 1 + GROUP - 1,)),
        ],
        compiler_params=pltpu.CompilerParams(
            collective_id=4, has_side_effects=True, vmem_limit_bytes=60 << 20
        ),
        cost_estimate=pl.CostEstimate(
            flops=2 * LONG, bytes_accessed=4 * tokens * total, transcendentals=0
        ),
    )(x, h, dq, dkv, att, gains)


class Layout:
    def __init__(self, dp_size):
        self.blocks = dp_size // GROUP
        side = math.isqrt(self.blocks)
        self.rows, self.cols = side, self.blocks // side
        wide = 2 * self.cols

        def index(by, bx, y, x, core):
            return ((2 * by + y) * wide + 2 * bx + x) * 2 + core

        places = [(y, x, c) for y in range(2) for x in range(2) for c in range(2)]
        spots = [(by, bx) for by in range(self.rows) for bx in range(self.cols)]
        self.inner = [[index(*s, *p) for p in places] for s in spots]
        self.outer = [[index(*s, *p) for s in spots] for p in places]

    def groups(self):
        return None if self.blocks == 1 else self.inner

    def to_rows(self, array):
        if self.blocks == 1:
            return array
        rest = array.shape[1:]
        split = array.reshape(2, 2, 2, self.rows, self.cols, -1, *rest)
        order = (3, 0, 4, 1, 2, 5) + tuple(range(6, 6 + len(rest)))
        return split.transpose(order).reshape(array.shape)

    def from_rows(self, array):
        if self.blocks == 1:
            return array
        rest = array.shape[1:]
        split = array.reshape(self.rows, 2, self.cols, 2, 2, -1, *rest)
        order = (1, 3, 4, 0, 2, 5) + tuple(range(6, 6 + len(rest)))
        return split.transpose(order).reshape(array.shape)

    def from_cols(self, array):
        return array if self.blocks == 1 else self.from_rows(array.T).T

    def gather_outer(self, array):
        if self.blocks == 1:
            return array
        return lax.all_gather(array, "dp", axis_index_groups=self.outer, axis=0, tiled=True)

    def scatter_outer(self, array):
        if self.blocks == 1:
            return array
        return lax.psum_scatter(
            array, "dp", scatter_dimension=0, axis_index_groups=self.outer, tiled=True
        )

    def sum_outer(self, array):
        if self.blocks == 1:
            return array
        return lax.psum(array, "dp", axis_index_groups=self.outer)

    def gather(self, array):
        return lax.all_gather(array, "dp", axis_index_groups=self.groups(), axis=0, tiled=True)

    def scatter(self, array):
        return lax.psum_scatter(
            array, "dp", scatter_dimension=0, axis_index_groups=self.groups(), tiled=True
        )

    def spread(self, array):
        return lax.all_to_all(
            array, "dp", 1, 0, axis_index_groups=self.groups(), tiled=True
        )

    def unspread(self, array):
        return lax.all_to_all(
            array, "dp", 0, 1, axis_index_groups=self.groups(), tiled=True
        )


def rms_scale(values):
    return lax.rsqrt(jnp.mean(values * values, axis=-1, keepdims=True) + NORM_EPS)


def norm_back(values, scaling, gain, grad):
    gained = grad * gain
    gain_part = jnp.sum(grad * values * scaling, axis=0)
    inner = jnp.mean(gained * values, axis=-1, keepdims=True)
    return gain_part, scaling * gained - values * scaling * scaling * scaling * inner


def per_device(
    dp_size, z_size, activations, segment_ids, attn_gain, w_query, w_key, w_value, w_out,
    mlp_gain, w_gate, w_up, w_down, cotangent,
):
    layout = Layout(dp_size)
    rows, width = activations.shape[1:]
    x = activations[0].astype(F32)
    place = lax.axis_index("tensor")
    reach = -(-(MOST_DOC - 1) // rows) * rows

    def shift(array, step):
        pairs = [(at, at + step) for at in range(z_size) if 0 <= at + step < z_size]
        return lax.ppermute(array, "tensor", pairs)

    starts = document_starts(segment_ids[0])
    own_starts = lax.dynamic_slice_in_dim(starts, place * rows, rows)
    own_tokens = place * rows + jnp.arange(rows, dtype=jnp.int32)
    cosine, sine = rope_tables(own_tokens - own_starts)
    low = (own_starts - place * rows + reach)[None, :]

    shards = [
        layout.gather_outer(w)
        for w in (w_gate, w_up, w_down, jnp.concatenate([w_key, w_value], axis=1), w_query, w_out)
    ]
    spread = spread_weights(shards[:3], shards[3:], dp_size, z_size)
    wg, wu, wd = (
        layout.to_rows(lax.all_gather(w, "tensor", axis=1, tiled=True)) for w in spread[:3]
    )
    wkv, wq, wo = (layout.to_rows(w) for w in gather_rows(spread[3:], dp_size))

    def along_z(total):
        return lax.psum_scatter(
            layout.from_rows(total), "tensor", scatter_dimension=1, tiled=True
        )

    r1 = rms_scale(x)
    xn = (x * r1 * attn_gain).astype(BF16)
    q, kv = project_qkv(xn, wq, wkv, cosine, sine)
    pieces, moved = [kv], kv
    for _ in range(reach // rows):
        moved = shift(moved, 1)
        pieces.insert(0, moved)
    kv_all = jnp.concatenate(pieces, axis=0)
    att, lse = attend(q, kv_all, low)
    h = x + dot_nt(att, wo)

    r2 = rms_scale(h)
    hn, gate, up, hidden = gate_up((h * r2 * mlp_gain).astype(BF16), wg, wu, dp_size)
    grad, wd = lax.optimization_barrier((cotangent[0], wd))
    dy = layout.gather(grad)
    total_wd = dot_tn(dy, hidden).astype(BF16)
    dy, total_wd = lax.optimization_barrier((dy, total_wd))
    part_wd = along_z(total_wd)
    gate, up = gate.astype(F32), up.astype(F32)
    sigma = jax.nn.sigmoid(gate)
    dhid = dot_nn(dy, wd)
    dgate = (dhid * up * sigma * (1.0 + gate * (1.0 - sigma))).astype(BF16)
    dup = (dhid * gate * sigma).astype(BF16)
    half = width // 2
    left_dhn = (dot_nt(dgate, wg[:half]) + dot_nt(dup, wu[:half])).astype(BF16)
    dgate, dup, left_dhn, part_wd = lax.optimization_barrier((dgate, dup, left_dhn, part_wd))
    dhn_left = layout.scatter(left_dhn)
    right_dhn = (dot_nt(dgate, wg[half:]) + dot_nt(dup, wu[half:])).astype(BF16)
    hn, hidden, right_dhn = lax.optimization_barrier((hn, hidden, right_dhn))
    dhn_right = layout.scatter(right_dhn)
    total_wg = dot_tn(hn, dgate).astype(BF16)
    total_wu = dot_tn(hn, dup).astype(BF16)
    partial_out = dot_nt(hidden, wd).astype(BF16)
    dhn_left, dhn_right, total_wg, total_wu, partial_out = lax.optimization_barrier(
        (dhn_left, dhn_right, total_wg, total_wu, partial_out)
    )
    dhn = jnp.concatenate([dhn_left, dhn_right], axis=1).astype(F32)
    gain_two, dh_norm = norm_back(h, r2, mlp_gain, dhn)
    dh = cotangent[0].astype(F32) + dh_norm

    dhb = dh.astype(BF16)
    datt = dot_nn(dhb, wo).astype(BF16)
    dq, dkv_all = attend_back(q, datt, att, kv_all, lse, low, cosine, sine)
    out_sum = layout.scatter(partial_out)
    out_sum, dkv_all = lax.optimization_barrier((out_sum, dkv_all))
    output = h + out_sum.astype(F32)
    count = reach // rows
    moved = dkv_all[:rows]
    for at in range(1, count + 1):
        moved = shift(moved, -1)
        if at < count:
            here = dkv_all[at * rows : (at + 1) * rows]
            moved = (moved.astype(F32) + here.astype(F32)).astype(BF16)
    dkv = finish_dkv(dkv_all[count * rows :], moved, cosine, sine)
    dxn = dot_nt(dq, wq) + dot_nt(dkv, wkv)
    gain_one, dx_norm = norm_back(x, r1, attn_gain, dxn)
    input_grad = (dh + dx_norm).astype(BF16)
    out_sum, total_wg, total_wu = lax.optimization_barrier((out_sum, total_wg, total_wu))
    part_wg, part_wu = along_z(total_wg), along_z(total_wu)
    gains = layout.sum_outer(jnp.stack([gain_one, gain_two]))
    wo_grad, wq_grad, wkv_grad, gains = attention_grads(
        layout.from_cols(xn), layout.from_cols(dhb), dq, dkv, att, gains, dp_size, z_size
    )
    wo_grad, wq_grad, wkv_grad = (
        layout.scatter_outer(grad) for grad in (wo_grad, wq_grad, wkv_grad)
    )
    wd_grad, wg_grad, wu_grad = (
        layout.scatter_outer(layout.unspread(part)).astype(F32)
        for part in (part_wd, part_wg, part_wu)
    )
    key_cols = w_key.shape[1]
    return (
        output.astype(BF16)[None],
        input_grad[None],
        gains[0],
        wq_grad,
        wkv_grad[:, :key_cols],
        wkv_grad[:, key_cols:],
        wo_grad,
        gains[1],
        wg_grad,
        wu_grad,
        wd_grad,
    )


def solution(mesh):
    split = P("dp", "tensor")
    tokens = P("dp", "tensor", None)
    in_specs = (
        tokens, P("dp", None), P(), split, split, split, split, P(), split, split, split, tokens,
    )
    out_specs = (tokens, tokens, P(), split, split, split, split, P(), split, split, split)
    return jax.shard_map(
        functools.partial(per_device, mesh.shape["dp"], mesh.shape["tensor"]),
        mesh=mesh, in_specs=in_specs, out_specs=out_specs, check_vma=False,
    )
```

```python
import functools
import math

import jax
import jax.numpy as jnp
from jax import lax
from jax.experimental import pallas as pl
from jax.experimental.pallas import tpu as pltpu
from jax.sharding import PartitionSpec as P

HEAD_DIM = 64
DOCS = 4
MOST_DOC = 1024
NORM_EPS = 1e-05
ROPE_THETA = 500000.0
GROUP = 8
LANES = 128
QTILE = 256
SCALE = HEAD_DIM ** (-0.5)
LOG2E = 1.4426950408889634
FAR = -1e30
NTILE = 512
STRIP = 16
LONG = 60_000_000_000

F32 = jnp.float32
BF16 = jnp.bfloat16


def dot_nn(left, right):
    return lax.dot_general(left, right, (((1,), (0,)), ((), ())), preferred_element_type=F32)


def dot_nt(left, right):
    return lax.dot_general(left, right, (((1,), (1,)), ((), ())), preferred_element_type=F32)


def dot_tn(left, right):
    return lax.dot_general(left, right, (((0,), (0,)), ((), ())), preferred_element_type=F32)


def document_starts(segments):
    doc_ids = jnp.arange(DOCS, dtype=jnp.int32)
    counts = jnp.sum((segments[:, None] == doc_ids).astype(jnp.int32), axis=0)
    before = (doc_ids < segments[:, None]).astype(jnp.int32)
    return jnp.sum(before * counts[None, :], axis=-1)


def rope_tables(positions):
    half = HEAD_DIM // 2
    frequency = jnp.exp(
        jnp.arange(half, dtype=F32) * (-2.0 * math.log(ROPE_THETA) / HEAD_DIM)
    )
    angles = positions.astype(F32)[:, None] * frequency
    cosine, sine = jnp.cos(angles), jnp.sin(angles)
    wide_cos = jnp.concatenate([cosine] * 4, axis=1)
    wide_sin = jnp.concatenate([-sine, sine, -sine, sine], axis=1)
    return wide_cos, wide_sin


def swap_halves(values):
    lane = lax.broadcasted_iota(jnp.int32, values.shape, 1)
    ahead = pltpu.roll(values, LANES - 32, 1)
    behind = pltpu.roll(values, 32, 1)
    return jnp.where((lane % 64) < 32, ahead, behind)


def qkv_kernel(x_ref, wq_ref, wkv_ref, cos_ref, sin_ref, q_ref, kv_ref):
    x = x_ref[...]
    cosine, sine = cos_ref[...], sin_ref[...]
    for at in range(wq_ref.shape[1] // LANES):
        part = pl.ds(at * LANES, LANES)
        value = dot_nn(x, wq_ref[:, part])
        q_ref[:, part] = (value * cosine + swap_halves(value) * sine).astype(BF16)
    value = dot_nn(x, wkv_ref[...])
    key = value[:, :LANES]
    kv_ref[:, :LANES] = (key * cosine + swap_halves(key) * sine).astype(BF16)
    kv_ref[:, LANES:] = value[:, LANES:].astype(BF16)


def project_qkv(x, wq, wkv, cosine, sine):
    rows, width = x.shape
    blocks = wkv.shape[1] // (2 * LANES)
    qcols = wq.shape[1] // blocks
    return pl.pallas_call(
        qkv_kernel,
        grid=(blocks,),
        in_specs=[
            pl.BlockSpec((rows, width), lambda g: (0, 0)),
            pl.BlockSpec((width, qcols), lambda g: (0, g)),
            pl.BlockSpec((width, 2 * LANES), lambda g: (0, g)),
            pl.BlockSpec((rows, LANES), lambda g: (0, 0)),
            pl.BlockSpec((rows, LANES), lambda g: (0, 0)),
        ],
        out_specs=[
            pl.BlockSpec((rows, qcols), lambda g: (0, g)),
            pl.BlockSpec((rows, 2 * LANES), lambda g: (0, g)),
        ],
        out_shape=[
            jax.ShapeDtypeStruct((rows, wq.shape[1]), BF16),
            jax.ShapeDtypeStruct((rows, wkv.shape[1]), BF16),
        ],
        compiler_params=pltpu.CompilerParams(vmem_limit_bytes=40 << 20),
        cost_estimate=pl.CostEstimate(
            flops=2 * rows * width * (wq.shape[1] + wkv.shape[1]),
            bytes_accessed=2 * width * (wq.shape[1] + wkv.shape[1]),
            transcendentals=0,
        ),
    )(x, wq, wkv, cosine, sine)


def fill_bias(bias_ref, low_ref, reach):
    span = bias_ref.shape[1]
    for tile in range(bias_ref.shape[0]):
        row = lax.broadcasted_iota(jnp.int32, (span, QTILE), 0)
        col = lax.broadcasted_iota(jnp.int32, (span, QTILE), 1)
        low = low_ref[0:1, tile * QTILE : (tile + 1) * QTILE]
        allowed = (row <= reach + col) & (row + tile * QTILE >= low)
        bias_ref[tile] = jnp.where(allowed, 0.0, FAR)


def spread_pair(pair, half):
    wide = pair.astype(F32)
    turned = pltpu.roll(wide, 64, 1)
    lane = lax.broadcasted_iota(jnp.int32, wide.shape, 1)
    mine = (lane // 64) == half
    even = half == 0
    first = jnp.where(mine, jnp.where(even, wide, turned), 0.0)
    second = jnp.where(mine, jnp.where(even, turned, wide), 0.0)
    return jnp.concatenate([first, second], axis=0).astype(BF16)


def gather_pair(transposed, half):
    count = transposed.shape[1] // 2
    mine = jnp.where(half == 0, transposed[:64], transposed[64:])
    return jnp.concatenate([mine[:, :count], mine[:, count:]], axis=0).T


def attend_kernel(reach, q_ref, k_ref, v_ref, low_ref, att_ref, lse_ref, bias_ref):
    head, tile, pair = pl.program_id(0), pl.program_id(1), pl.program_id(2)
    half = head % 2

    @pl.when((head == 0) & (tile == 0) & (pair == 0))
    def _():
        fill_bias(bias_ref, low_ref, reach)

    keys = pl.ds(pl.multiple_of(tile * QTILE, QTILE), bias_ref.shape[1])
    queries = spread_pair(q_ref[...], half)
    bias = bias_ref[tile]
    score = dot_nt(k_ref[keys, :], queries)
    score = score + jnp.concatenate([bias, bias], axis=1)
    top = jnp.max(score, axis=0, keepdims=True) * (SCALE * LOG2E)
    weight = jnp.exp2(score * (SCALE * LOG2E) - top)
    total = jnp.sum(weight, axis=0, keepdims=True)
    result = dot_tn(v_ref[keys, :], weight.astype(BF16)) / total
    att_ref[...] = gather_pair(result, half).astype(BF16)
    lse_ref[0] = top + jnp.log2(total)


def attend(q, kv, low):
    rows, width = q.shape
    keys = kv.shape[0]
    reach = keys - rows
    tiles = rows // QTILE
    pairs = width // LANES
    heads = kv.shape[1] // LANES
    per_head = pairs // heads
    span = reach + QTILE
    return pl.pallas_call(
        functools.partial(attend_kernel, reach),
        grid=(heads, tiles, per_head),
        in_specs=[
            pl.BlockSpec((QTILE, LANES), lambda a, t, p: (t, a * per_head + p)),
            pl.BlockSpec((keys, LANES), lambda a, t, p: (0, 2 * (a // 2))),
            pl.BlockSpec((keys, LANES), lambda a, t, p: (0, 2 * (a // 2) + 1)),
            pl.BlockSpec((1, rows), lambda a, t, p: (0, 0)),
        ],
        out_specs=[
            pl.BlockSpec((QTILE, LANES), lambda a, t, p: (t, a * per_head + p)),
            pl.BlockSpec((1, 1, 2 * QTILE), lambda a, t, p: ((a * tiles + t) * per_head + p, 0, 0)),
        ],
        out_shape=[
            jax.ShapeDtypeStruct((rows, width), BF16),
            jax.ShapeDtypeStruct((pairs * tiles, 1, 2 * QTILE), F32),
        ],
        scratch_shapes=[pltpu.VMEM((tiles, span, QTILE), F32)],
        compiler_params=pltpu.CompilerParams(vmem_limit_bytes=48 << 20),
        cost_estimate=pl.CostEstimate(
            flops=16 * rows * span * LANES * pairs,
            bytes_accessed=4 * rows * width + 2 * keys * kv.shape[1],
            transcendentals=2 * rows * span * pairs,
        ),
    )(q, kv, kv, low)


def attend_back_kernel(
    reach, wide, z_size,
    q_ref, do_ref, o_ref, k_ref, v_ref, lse_ref, low_ref, cos_ref, sin_ref, cos_all, sin_all,
    h_ref, att_ref,
    dq_ref, dkv_ref, wo_out,
    bias_ref, dk_acc, dv_acc, own_part, send_part, recv_part, kv_send, kv_recv,
    *scratch,
):
    ring = Reduce(wide, *scratch[:6])
    sums, zrecv, z_send, z_recv = scratch[6:]
    block, half, tile, pair = (pl.program_id(at) for at in range(4))
    steps = pl.num_programs(1) * pl.num_programs(2) * pl.num_programs(3)
    inner = (half * pl.num_programs(2) + tile) * pl.num_programs(3) + pair
    step = block * steps + inner
    blocks = own_part.shape[0]
    rows = own_part.shape[1]
    count = reach // rows
    place = lax.axis_index("tensor")

    def exchange(at, distance):
        return pltpu.make_async_remote_copy(
            src_ref=send_part.at[at, pl.ds((count - distance) * rows, rows)],
            dst_ref=recv_part.at[at, distance - 1],
            send_sem=kv_send.at[at, distance - 1], recv_sem=kv_recv.at[at, distance - 1],
            device_id={"tensor": (place + z_size - distance) % z_size}, device_id_type=MESH,
        )

    def each_exchange(at, condition, action):
        for distance in range(1, count + 1):
            pl.when(condition(distance))(
                functools.partial(action, exchange(at, distance), at, distance)
            )

    def along(at):
        cols = wo_out.shape[1]
        other = (place + at + 1) % z_size
        return pltpu.make_async_remote_copy(
            src_ref=sums.at[:, pl.ds(pl.multiple_of(other * cols, LANES), cols)],
            dst_ref=zrecv.at[at], send_sem=z_send.at[at], recv_sem=z_recv.at[at],
            device_id={"tensor": other}, device_id_type=MESH,
        )

    @pl.when(step == 0)
    def _():
        barrier = pltpu.get_barrier_semaphore()
        peers = [{"dp": peer} for peer in ring.peers]
        peers += [{"tensor": (place + at) % z_size} for at in range(1, z_size)]
        for peer in peers:
            pl.semaphore_signal(barrier, inc=1, device_id=peer, device_id_type=MESH)
        pl.semaphore_wait(barrier, len(peers))
        fill_bias(bias_ref, low_ref, reach)

    @pl.when((step % 2 == 0) & (step < 16))
    def _():
        chunk, target = ring.chunk(step // 2)
        part = target.shape[0]
        x = h_ref[:, pl.ds(pl.multiple_of(chunk * part, part), part)].T

        @pl.loop(0, att_ref.shape[1] // NTILE)
        def _(at):
            n = pl.ds(pl.multiple_of(at * NTILE, NTILE), NTILE)
            target[:, n] = dot_nn(x, att_ref[:, n]).astype(BF16)

        ring.after(step // 2)

    pl.when(step == 19)(ring.pass_on)

    @pl.when(step == 27)
    def _():
        def store(here, value):
            sums[here, :] = value.astype(BF16)

        ring.finish(store)
        for at in range(z_size - 1):
            along(at).start()

    @pl.when(inner == 0)
    def _():
        dk_acc[...] = jnp.zeros_like(dk_acc)
        dv_acc[...] = jnp.zeros_like(dv_acc)

    keys = pl.ds(pl.multiple_of(tile * QTILE, QTILE), bias_ref.shape[1])
    queries = spread_pair(q_ref[...], half)
    grads = spread_pair(do_ref[...], half)
    product = (do_ref[...].astype(F32) * o_ref[...].astype(F32)).T
    row_dot = jnp.concatenate(
        [
            jnp.sum(product[:64], axis=0, keepdims=True),
            jnp.sum(product[64:], axis=0, keepdims=True),
        ],
        axis=1,
    )
    bias = bias_ref[tile]
    key, value = k_ref[keys, :], v_ref[keys, :]
    score = dot_nt(key, queries) + jnp.concatenate([bias, bias], axis=1)
    weight = jnp.exp2(score * (SCALE * LOG2E) - lse_ref[0])
    dv_acc[keys, :] += dot_nn(weight.astype(BF16), grads)
    dscore = (weight * (dot_nt(value, grads) - row_dot)).astype(BF16)
    dk_acc[keys, :] += dot_nn(dscore, queries)
    dq = gather_pair(dot_tn(key, dscore), half) * SCALE
    dq_ref[...] = (dq * cos_ref[...] - swap_halves(dq) * sin_ref[...]).astype(BF16)

    @pl.when(inner == steps - 1)
    def _():
        send_part[block, :, :LANES] = (dk_acc[:reach] * SCALE).astype(BF16)
        send_part[block, :, LANES:] = dv_acc[:reach].astype(BF16)
        own_part[block, :, :LANES] = dk_acc[reach:] * SCALE
        own_part[block, :, LANES:] = dv_acc[reach:]
        each_exchange(block, lambda distance: place >= distance, lambda copy, *_: copy.start())

    @pl.when(step == blocks * steps - 1)
    def _():
        def collect(copy, at, distance):
            copy.wait_recv()
            own_part[at] += recv_part[at, distance - 1].astype(F32)

        for at in range(blocks):
            each_exchange(at, lambda distance: place + distance < z_size, collect)
            dkey = own_part[at, :, :LANES]
            dkey = dkey * cos_all[...] - swap_halves(dkey) * sin_all[...]
            dkv_ref[:, 2 * at * LANES : (2 * at + 1) * LANES] = dkey.astype(BF16)
            dkv_ref[:, (2 * at + 1) * LANES : (2 * at + 2) * LANES] = own_part[
                at, :, LANES:
            ].astype(BF16)
        total = sums[:, pl.ds(pl.multiple_of(place * wo_out.shape[1], LANES), wo_out.shape[1])]
        total = total.astype(F32)
        for at in range(z_size - 1):
            along(at).wait_recv()
            total += zrecv[at].astype(F32)
        wo_out[...] = total
        for at in range(z_size - 1):
            along(at).wait_send()
        for at in range(blocks):
            each_exchange(
                at, lambda distance: place >= distance, lambda copy, *_: copy.wait_send()
            )
        ring.sent()


def attend_back(q, do, att, kv, lse, low, cosine, sine, h, dp_size, z_size):
    rows, width = q.shape
    keys = kv.shape[0]
    reach = keys - rows
    tiles = rows // QTILE
    pairs = width // LANES
    heads = kv.shape[1] // LANES
    per_head = pairs // heads
    span = reach + QTILE
    blocks = heads // 2
    part = h.shape[1] // GROUP
    cols = width // z_size

    def pair_at(g, h, t, p):
        return (t, (2 * g + h) * per_head + p)

    def whole(shape):
        return pl.BlockSpec(shape, lambda g, h, t, p: (0, 0), pipeline_mode=pl.Buffered(1))

    table = pl.BlockSpec((QTILE, LANES), lambda g, h, t, p: (t, 0))
    return pl.pallas_call(
        functools.partial(
            attend_back_kernel, reach, 2 * math.isqrt(dp_size // GROUP), z_size
        ),
        grid=(blocks, 2, tiles, per_head),
        in_specs=[
            pl.BlockSpec((QTILE, LANES), pair_at),
            pl.BlockSpec((QTILE, LANES), pair_at),
            pl.BlockSpec((QTILE, LANES), pair_at),
            pl.BlockSpec((keys, LANES), lambda g, h, t, p: (0, 2 * g)),
            pl.BlockSpec((keys, LANES), lambda g, h, t, p: (0, 2 * g + 1)),
            pl.BlockSpec(
                (1, 1, 2 * QTILE),
                lambda g, h, t, p: (((2 * g + h) * tiles + t) * per_head + p, 0, 0),
            ),
            whole((1, rows)),
            table,
            table,
            whole((rows, LANES)),
            whole((rows, LANES)),
            whole(h.shape),
            whole(att.shape),
        ],
        out_specs=[
            pl.BlockSpec((QTILE, LANES), pair_at),
            pl.BlockSpec((rows, kv.shape[1]), lambda g, h, t, p: (0, 0)),
            pl.BlockSpec((part, cols), lambda g, h, t, p: (0, 0)),
        ],
        out_shape=[
            jax.ShapeDtypeStruct((rows, width), BF16),
            jax.ShapeDtypeStruct((rows, kv.shape[1]), BF16),
            jax.ShapeDtypeStruct((part, cols), F32),
        ],
        scratch_shapes=[
            pltpu.VMEM((tiles, span, QTILE), F32),
            pltpu.VMEM((keys, LANES), F32),
            pltpu.VMEM((keys, LANES), F32),
            pltpu.VMEM((blocks, rows, 2 * LANES), F32),
            pltpu.VMEM((blocks, reach, 2 * LANES), BF16),
            pltpu.VMEM((blocks, reach // rows, rows, 2 * LANES), BF16),
            pltpu.SemaphoreType.DMA((blocks, reach // rows)),
            pltpu.SemaphoreType.DMA((blocks, reach // rows)),
        ]
        + Reduce.scratch(part, width)
        + [
            pltpu.VMEM((part, width), BF16),
            pltpu.VMEM((z_size - 1, part, cols), BF16),
            pltpu.SemaphoreType.DMA((z_size - 1,)),
            pltpu.SemaphoreType.DMA((z_size - 1,)),
        ],
        compiler_params=pltpu.CompilerParams(
            collective_id=5, has_side_effects=True, vmem_limit_bytes=60 << 20
        ),
        cost_estimate=pl.CostEstimate(
            flops=40 * rows * span * LANES * pairs,
            bytes_accessed=8 * rows * width + 4 * keys * kv.shape[1],
            transcendentals=2 * rows * span * pairs,
        ),
    )(q, do, att, kv, kv, lse, low, cosine, sine, cosine, sine, h, att)


MESH = pl.DeviceIdType.MESH


def neighbours(wide):
    dp = lax.axis_index("dp")
    core, col, row = dp % 2, (dp // 2) % 2, (dp // (2 * wide)) % 2
    sibling = dp + 1 - 2 * core
    beside = dp + 2 - 4 * col
    above = dp + 2 * wide - 4 * wide * row
    return (row, col, core), (sibling, beside, above)


def meet(peers):
    barrier = pltpu.get_barrier_semaphore()
    for peer in peers:
        pl.semaphore_signal(barrier, inc=1, device_id={"dp": peer}, device_id_type=MESH)
    pl.semaphore_wait(barrier, len(peers))


SIB, XN, YN = 0, 1, 2


def spread_kernel(wide, z_size, mlp_count, *refs):
    attn_count = (len(refs) - 3) // 2 - mlp_count
    count = mlp_count + attn_count
    ins, outs = refs[:count], refs[count : 2 * count]
    own_sem, send_sem, recv_sem = refs[2 * count :]
    (row, col, core), _ = neighbours(wide)
    dp, place = lax.axis_index("dp"), lax.axis_index("tensor")
    mine = 4 * row + 2 * col + core
    base = dp - (2 * wide * row + 2 * col + core)

    def peer(dy, dx, dc):
        y, x, c = (row + dy) % 2, (col + dx) % 2, (core + dc) % 2
        return base + 2 * wide * y + 2 * x + c, 4 * y + 2 * x + c

    flips = [(dy, dx, dc) for dy in range(2) for dx in range(2) for dc in range(2)][1:]
    barrier = pltpu.get_barrier_semaphore()
    for flip in flips:
        pl.semaphore_signal(
            barrier, inc=1, device_id={"dp": peer(*flip)[0]}, device_id_type=MESH
        )
    for step in range(1, z_size):
        pl.semaphore_signal(
            barrier, inc=1, device_id={"tensor": (place + step) % z_size}, device_id_type=MESH
        )
    pl.semaphore_wait(barrier, len(flips) + z_size - 1)

    copies, local = [], []
    slot = 0
    for at in range(mlp_count, count):
        src, dst = ins[at], outs[at]
        cols = src.shape[1]
        part = pl.ds(pl.multiple_of(place * cols, LANES), cols)
        for step in range(1, z_size):
            copies.append(
                pltpu.make_async_remote_copy(
                    src_ref=src, dst_ref=dst.at[:, part],
                    send_sem=send_sem.at[slot], recv_sem=recv_sem.at[slot],
                    device_id={"tensor": (place + step) % z_size}, device_id_type=MESH,
                )
            )
            slot += 1
        local.append(pltpu.make_async_copy(src, dst.at[:, part], own_sem.at[at]))
    for at in range(mlp_count):
        src, dst = ins[at], outs[at]
        rows, cols = src.shape[0], dst.shape[1]
        here = pl.ds(pl.multiple_of(mine * rows, rows), rows)
        for flip in flips:
            device, other = peer(*flip)
            copies.append(
                pltpu.make_async_remote_copy(
                    src_ref=src.at[:, pl.ds(pl.multiple_of(other * cols, LANES), cols)],
                    dst_ref=dst.at[here],
                    send_sem=send_sem.at[slot], recv_sem=recv_sem.at[slot],
                    device_id={"dp": device}, device_id_type=MESH,
                )
            )
            slot += 1
        own = src.at[:, pl.ds(pl.multiple_of(mine * cols, LANES), cols)]
        local.append(pltpu.make_async_copy(own, dst.at[here], own_sem.at[at]))
    for copy in copies:
        copy.start()
    for copy in local:
        copy.start()
    for copy in local:
        copy.wait()
    for copy in copies:
        copy.wait()


def spread_weights(mlp, attn, dp_size, z_size):
    count = len(mlp) + len(attn)
    slots = (z_size - 1) * len(attn) + (GROUP - 1) * len(mlp)
    spec = pl.BlockSpec(memory_space=pl.ANY)
    out = [jax.ShapeDtypeStruct((GROUP * w.shape[0], w.shape[1] // GROUP), BF16) for w in mlp]
    out += [jax.ShapeDtypeStruct((w.shape[0], z_size * w.shape[1]), BF16) for w in attn]
    return pl.pallas_call(
        functools.partial(spread_kernel, 2 * math.isqrt(dp_size // GROUP), z_size, len(mlp)),
        in_specs=[spec] * count,
        out_specs=[spec] * count,
        out_shape=out,
        scratch_shapes=[
            pltpu.SemaphoreType.DMA((count,)),
            pltpu.SemaphoreType.DMA((slots,)),
            pltpu.SemaphoreType.DMA((slots,)),
        ],
        compiler_params=pltpu.CompilerParams(collective_id=2, has_side_effects=True),
        cost_estimate=pl.CostEstimate(flops=LONG, bytes_accessed=0, transcendentals=0),
    )(*mlp, *attn)


class Ring:
    FLIP = {SIB: (0, 0, 1), XN: (0, 1, 0), YN: (1, 0, 0)}
    COPIES = 14

    def __init__(self, wide, ref, rows, send_sem, recv_sem):
        (self.row, self.col, self.core), self.peers = neighbours(wide)
        self.ref, self.rows, self.part = ref, rows, rows // 2
        self.send_sem, self.recv_sem = send_sem, recv_sem
        self.sends = {}
        for half in range(2):
            self.sends["own", XN, half] = (2 + half, 0, 0, 0, half)
            self.sends["own", YN, half] = (4 + half, 0, 0, 0, half)
            self.sends["own", SIB, half] = (0 + half, 0, 0, 0, half)
        for half in range(2):
            self.sends["x", SIB, half] = (6 + half, 0, 1, 0, half)
            self.sends["y", SIB, half] = (8 + half, 1, 0, 0, half)
            self.sends["d", SIB, half] = (10 + half, 1, 1, 0, half)
        self.sends["x", YN, 0] = (12, 0, 1, 0, 0)
        self.sends["y", XN, 1] = (13, 1, 0, 0, 1)

    def place(self, dy, dx, dc, half):
        p = 4 * ((self.row + dy) % 2) + 2 * ((self.col + dx) % 2) + (self.core + dc) % 2
        return pl.ds(pl.multiple_of(p * self.rows + half * self.part, self.part), self.part)

    def mine(self):
        p = 4 * self.row + 2 * self.col + self.core
        return pl.ds(pl.multiple_of(p * self.rows, self.rows), self.rows)

    def copy(self, slot, dy, dx, dc, half, peer):
        where = self.place(dy, dx, dc, half)
        return pltpu.make_async_remote_copy(
            src_ref=self.ref.at[where], dst_ref=self.ref.at[where],
            send_sem=self.send_sem.at[slot], recv_sem=self.recv_sem.at[slot],
            device_id={"dp": self.peers[peer]}, device_id_type=MESH,
        )

    def start(self, name, peer, half):
        self.copy(*self.sends[name, peer, half], peer).start()

    def arrived(self, name, peer, half):
        slot, dy, dx, dc, half = self.sends[name, peer, half]
        fy, fx, fc = self.FLIP[peer]
        self.copy(slot, (dy + fy) % 2, (dx + fx) % 2, (dc + fc) % 2, half, peer).wait_recv()

    def start_own(self):
        for half in range(2):
            for peer in (XN, YN, SIB):
                self.start("own", peer, half)

    def first_halves(self):
        self.arrived("own", XN, 0)
        self.start("x", YN, 0)
        self.start("x", SIB, 0)
        self.arrived("own", YN, 0)
        self.start("y", SIB, 0)

    def second_halves(self):
        self.arrived("own", YN, 1)
        self.start("y", XN, 1)
        self.start("y", SIB, 1)
        self.arrived("own", XN, 1)
        self.start("x", SIB, 1)

    def far_halves(self):
        self.arrived("x", YN, 0)
        self.start("d", SIB, 0)
        self.arrived("y", XN, 1)
        self.start("d", SIB, 1)

    def from_sibling(self, name, *halves):
        for half in halves:
            self.arrived(name, SIB, half)

    def sent(self):
        for (name, peer, half), entry in self.sends.items():
            self.copy(*entry, peer).wait_send()


def gather_kernel(wide, count, *refs):
    ins, outs = refs[:count], refs[count : 2 * count]
    own_sem, send_sem, recv_sem = refs[2 * count :]
    rings = [
        Ring(wide, outs[at], ins[at].shape[0], send_sem.at[at], recv_sem.at[at])
        for at in range(count)
    ]
    local = [
        pltpu.make_async_copy(ins[at], outs[at].at[rings[at].mine()], own_sem.at[at])
        for at in range(count)
    ]
    for copy in local:
        copy.start()
    meet(rings[0].peers)
    for copy, ring in zip(local, rings):
        copy.wait()
        ring.start_own()
    for ring in rings:
        ring.first_halves()
        ring.second_halves()
    for ring in rings:
        ring.far_halves()
        for name in ("own", "x", "y", "d"):
            ring.from_sibling(name, 0, 1)
    for ring in rings:
        ring.sent()


def gather_rows(arrays, dp_size):
    count = len(arrays)
    spec = pl.BlockSpec(memory_space=pl.ANY)
    return pl.pallas_call(
        functools.partial(gather_kernel, 2 * math.isqrt(dp_size // GROUP), count),
        in_specs=[spec] * count,
        out_specs=[spec] * count,
        out_shape=[jax.ShapeDtypeStruct((GROUP * a.shape[0], a.shape[1]), a.dtype) for a in arrays],
        scratch_shapes=[
            pltpu.SemaphoreType.DMA((count,)),
            pltpu.SemaphoreType.DMA((count, Ring.COPIES)),
            pltpu.SemaphoreType.DMA((count, Ring.COPIES)),
        ],
        compiler_params=pltpu.CompilerParams(collective_id=3, has_side_effects=True),
        cost_estimate=pl.CostEstimate(flops=2 * LONG, bytes_accessed=0, transcendentals=0),
    )(*arrays)


def gate_up_kernel(
    wide, own_ref, wg_ref, wu_ref, all_ref, gate_ref, up_ref, hid_ref,
    full, stage, own_sem, send_sem, recv_sem, out_sem, all_sem,
):
    rows = own_ref.shape[0]
    cols = gate_ref.shape[1]
    ring = Ring(wide, full, rows, send_sem, recv_sem)
    local = pltpu.make_async_copy(own_ref, full.at[ring.mine()], own_sem)
    local.start()
    meet(ring.peers)
    local.wait()
    ring.start_own()

    def out_copies(slot, where):
        return [
            pltpu.make_async_copy(stage.at[slot, i], ref.at[where], out_sem.at[slot, i])
            for i, ref in enumerate((gate_ref, up_ref, hid_ref))
        ] + [pltpu.make_async_copy(full.at[where], all_ref.at[where], all_sem.at[slot])]

    def step_place(step):
        phase, i = step // 4, step % 4
        high, low = phase // 2, phase % 2
        first, last = (1 - high) * (1 - low), high * low
        middle = high + low - 2 * last
        half = (first + last) * (i % 2) + high * (1 - low)
        dx = middle * (1 - i % 2) + last
        dy = middle * (i % 2) + last
        return ring.place(dy, dx, i // 2, half)

    @pl.loop(0, 16)
    def _(step):
        pl.when(step == 2)(lambda: ring.from_sibling("own", 0, 1))
        pl.when(step == 4)(ring.first_halves)

        @pl.when(step == 6)
        def _():
            ring.from_sibling("x", 0)
            ring.from_sibling("y", 0)

        pl.when(step == 8)(ring.second_halves)

        @pl.when(step == 10)
        def _():
            ring.from_sibling("x", 1)
            ring.from_sibling("y", 1)

        pl.when(step == 12)(ring.far_halves)
        pl.when(step == 14)(lambda: ring.from_sibling("d", 0, 1))

        slot = step % 2
        where = step_place(step)

        @pl.when(step >= 2)
        def _():
            for copy in out_copies(slot, step_place(step - 2)):
                copy.wait()

        x = full[where, :]

        @pl.loop(0, cols // NTILE)
        def _(at):
            n = pl.ds(pl.multiple_of(at * NTILE, NTILE), NTILE)
            gate = dot_nn(x, wg_ref[:, n])
            up = dot_nn(x, wu_ref[:, n])
            stage[slot, 0, :, n] = gate.astype(BF16)
            stage[slot, 1, :, n] = up.astype(BF16)
            stage[slot, 2, :, n] = (gate * up / (1.0 + jnp.exp(-gate))).astype(BF16)

        for copy in out_copies(slot, where):
            copy.start()

    for step in (14, 15):
        for copy in out_copies(step % 2, step_place(step)):
            copy.wait()
    ring.sent()


def gate_up(hn, wg, wu, dp_size):
    rows, width = hn.shape
    cols = wg.shape[1]
    tokens = GROUP * rows
    far = pl.BlockSpec(memory_space=pl.ANY)
    near = pl.BlockSpec(memory_space=pltpu.VMEM)
    return pl.pallas_call(
        functools.partial(gate_up_kernel, 2 * math.isqrt(dp_size // GROUP)),
        in_specs=[far, near, near],
        out_specs=[far] * 4,
        out_shape=[jax.ShapeDtypeStruct((tokens, width), BF16)]
        + [jax.ShapeDtypeStruct((tokens, cols), BF16)] * 3,
        scratch_shapes=[
            pltpu.VMEM((tokens, width), BF16),
            pltpu.VMEM((2, 3, rows // 2, cols), BF16),
            pltpu.SemaphoreType.DMA,
            pltpu.SemaphoreType.DMA((Ring.COPIES,)),
            pltpu.SemaphoreType.DMA((Ring.COPIES,)),
            pltpu.SemaphoreType.DMA((2, 3)),
            pltpu.SemaphoreType.DMA((2,)),
        ],
        compiler_params=pltpu.CompilerParams(
            collective_id=1, has_side_effects=True, vmem_limit_bytes=56 << 20
        ),
        cost_estimate=pl.CostEstimate(
            flops=4 * tokens * width * cols,
            bytes_accessed=tokens * (2 * width + 6 * cols) + 4 * width * cols,
            transcendentals=tokens * cols,
        ),
    )(hn, wg, wu)


FAR_CHUNK, X_CHUNK, Y_CHUNK, OWN_CHUNK = range(4)


class Reduce:
    COPIES = 10

    def __init__(self, wide, parts, cores, far, near, send_sem, recv_sem):
        self.at, self.peers = neighbours(wide)
        self.parts, self.cores, self.far, self.near = parts, cores, far, near
        self.send_sem, self.recv_sem = send_sem, recv_sem
        self.half = parts.shape[2] // 2

    @staticmethod
    def scratch(rows, cols):
        return [
            pltpu.VMEM((2, 4, rows, cols), BF16),
            pltpu.VMEM((4, rows, cols), BF16),
            pltpu.VMEM((2, rows // 2, cols), BF16),
            pltpu.VMEM((2, rows, cols), BF16),
            pltpu.SemaphoreType.DMA((Reduce.COPIES,)),
            pltpu.SemaphoreType.DMA((Reduce.COPIES,)),
        ]

    def chunk(self, step):
        slot, other = step // 2, 1 - step % 2
        row, col, core = self.at
        dy, dx = 1 - slot % 2, 1 - slot // 2
        place = 4 * ((row + dy) % 2) + 2 * ((col + dx) % 2) + (core + other) % 2
        return place, self.parts.at[other, slot]

    def copy(self, name):
        upper, lower = pl.ds(0, self.half), pl.ds(self.half, self.half)
        mine = self.parts.at[0]
        table = {
            "far0": (self.parts.at[1, FAR_CHUNK], self.cores.at[FAR_CHUNK], SIB),
            "x": (self.parts.at[1, X_CHUNK], self.cores.at[X_CHUNK], SIB),
            "y": (self.parts.at[1, Y_CHUNK], self.cores.at[Y_CHUNK], SIB),
            "own": (self.parts.at[1, OWN_CHUNK], self.cores.at[OWN_CHUNK], SIB),
            "far_x": (mine.at[FAR_CHUNK, lower], self.far.at[0], XN),
            "far_y": (mine.at[FAR_CHUNK, upper], self.far.at[1], YN),
            "x_upper": (mine.at[X_CHUNK, upper], self.near.at[0, upper], XN),
            "x_lower": (mine.at[X_CHUNK, lower], self.near.at[0, lower], XN),
            "y_upper": (mine.at[Y_CHUNK, upper], self.near.at[1, upper], YN),
            "y_lower": (mine.at[Y_CHUNK, lower], self.near.at[1, lower], YN),
        }
        src, dst, peer = table[name]
        at = list(table).index(name)
        return pltpu.make_async_remote_copy(
            src_ref=src, dst_ref=dst, send_sem=self.send_sem.at[at],
            recv_sem=self.recv_sem.at[at], device_id={"dp": self.peers[peer]},
            device_id_type=MESH,
        )

    def start(self, *names):
        for name in names:
            self.copy(name).start()

    def add(self, slot, start, other):
        count = other.shape[0] // STRIP

        @pl.loop(0, count)
        def _(at):
            here = pl.ds(pl.multiple_of(start + at * STRIP, STRIP), STRIP)
            there = pl.ds(pl.multiple_of(at * STRIP, STRIP), STRIP)
            value = self.parts[0, slot, here, :].astype(F32) + other[there, :].astype(F32)
            self.parts[0, slot, here, :] = value.astype(BF16)

    def merge_core(self, slot, name):
        self.copy(name).wait_recv()
        self.add(slot, 0, self.cores.at[slot])

    def after(self, step):
        names = ("far0", "x", "y", "own")
        for slot in range(4):
            pl.when(step == 2 * slot)(functools.partial(self.start, names[slot]))

        @pl.when(step == 1)
        def _():
            self.merge_core(FAR_CHUNK, "far0")
            self.start("far_x", "far_y")

        @pl.when(step == 3)
        def _():
            self.merge_core(X_CHUNK, "x")
            self.start("x_lower")

        @pl.when(step == 5)
        def _():
            self.merge_core(Y_CHUNK, "y")
            self.start("y_upper")

    def pass_on(self):
        self.copy("far_y").wait_recv()
        self.add(X_CHUNK, 0, self.far.at[1])
        self.start("x_upper")
        self.copy("far_x").wait_recv()
        self.add(Y_CHUNK, self.half, self.far.at[0])
        self.start("y_lower")

    def finish(self, store):
        for name in ("own", "x_upper", "x_lower", "y_upper", "y_lower"):
            self.copy(name).wait_recv()

        @pl.loop(0, 2 * self.half // STRIP)
        def _(at):
            here = pl.ds(pl.multiple_of(at * STRIP, STRIP), STRIP)
            value = self.parts[0, OWN_CHUNK, here, :].astype(F32)
            value += self.cores[OWN_CHUNK, here, :].astype(F32)
            value += self.near[0, here, :].astype(F32)
            value += self.near[1, here, :].astype(F32)
            store(here, value)

    def sent(self):
        for name in (
            "far0", "x", "y", "own", "far_x", "far_y", "x_upper", "x_lower", "y_upper", "y_lower",
        ):
            self.copy(name).wait_send()


def hidden_back_kernel(
    wide, dgate_ref, dup_ref, wg_ref, wu_ref, out_ref, loaded, load_sem, *scratch
):
    ring = Reduce(wide, *scratch)
    rows = out_ref.shape[0]

    def loads(step):
        chunk, _ = ring.chunk(step)
        here = pl.ds(pl.multiple_of(chunk * rows, rows), rows)
        return [
            pltpu.make_async_copy(
                ref.at[here], loaded.at[step % 2, at], load_sem.at[step % 2, at]
            )
            for at, ref in enumerate((dgate_ref, dup_ref))
        ]

    for copy in loads(0):
        copy.start()
    meet(ring.peers)

    @pl.loop(0, 8)
    def _(step):
        @pl.when(step < 7)
        def _():
            for copy in loads(step + 1):
                copy.start()

        for copy in loads(step):
            copy.wait()
        _, target = ring.chunk(step)
        dgate, dup = loaded[step % 2, 0], loaded[step % 2, 1]

        @pl.loop(0, out_ref.shape[1] // NTILE)
        def _(at):
            n = pl.ds(pl.multiple_of(at * NTILE, NTILE), NTILE)
            value = dot_nt(dgate, wg_ref[n, :]) + dot_nt(dup, wu_ref[n, :])
            target[:, n] = value.astype(BF16)

        ring.after(step)

    ring.pass_on()

    def store(here, value):
        out_ref[here, :] = value

    ring.finish(store)
    ring.sent()


def hidden_back(dgate, dup, wg, wu, dp_size):
    tokens, cols = dgate.shape
    width = wg.shape[0]
    rows = tokens // GROUP
    far = pl.BlockSpec(memory_space=pl.ANY)
    near = pl.BlockSpec(memory_space=pltpu.VMEM)
    return pl.pallas_call(
        functools.partial(hidden_back_kernel, 2 * math.isqrt(dp_size // GROUP)),
        in_specs=[far, far, near, near],
        out_specs=near,
        out_shape=jax.ShapeDtypeStruct((rows, width), F32),
        scratch_shapes=[
            pltpu.VMEM((2, 2, rows, cols), BF16),
            pltpu.SemaphoreType.DMA((2, 2)),
        ]
        + Reduce.scratch(rows, width),
        compiler_params=pltpu.CompilerParams(
            collective_id=6, has_side_effects=True, vmem_limit_bytes=60 << 20
        ),
        cost_estimate=pl.CostEstimate(
            flops=4 * tokens * width * cols,
            bytes_accessed=4 * tokens * cols + 4 * width * cols + 4 * rows * width,
            transcendentals=0,
        ),
    )(dgate, dup, wg, wu)


def tail_kernel(wide, z_size, mlp_count, x_ref, dq_ref, dkv_ref, gain_ref, *refs):
    mlp_ins, refs = refs[:mlp_count], refs[mlp_count:]
    wq_out, wkv_out, gain_out = refs[:3]
    mlp_outs, scratch = refs[3 : 3 + mlp_count], refs[3 + mlp_count :]
    own_scratch = scratch[:12]
    sums, zrecv, gain_z, gain_p, z_send, z_recv, g_send, g_recv, m_own, m_send, m_recv = scratch[12:]
    rings = [Reduce(wide, *own_scratch[6 * at : 6 * at + 6]) for at in range(2)]
    place = lax.axis_index("tensor")
    dp = lax.axis_index("dp")
    row, col, core = rings[0].at
    mine = 4 * row + 2 * col + core
    base = dp - (2 * wide * row + 2 * col + core)
    flips = [(y, x, c) for y in range(2) for x in range(2) for c in range(2)][1:]

    def device(flip):
        y, x, c = (row + flip[0]) % 2, (col + flip[1]) % 2, (core + flip[2]) % 2
        return {"dp": base + 2 * wide * y + 2 * x + c}

    along = [{"tensor": (place + step) % z_size} for step in range(1, z_size)]
    around = [device(flip) for flip in flips]
    barrier = pltpu.get_barrier_semaphore()
    for peer in along + around:
        pl.semaphore_signal(barrier, inc=1, device_id=peer, device_id_type=MESH)
    pl.semaphore_wait(barrier, len(along) + len(around))

    mlp_copies = []
    for at in range(mlp_count):
        src, dst = mlp_ins[at], mlp_outs[at]
        part, cols = dst.shape[0], src.shape[1]
        here = pl.ds(pl.multiple_of(mine * cols, LANES), cols)
        for index, flip in enumerate(flips):
            y, x, c = (row + flip[0]) % 2, (col + flip[1]) % 2, (core + flip[2]) % 2
            other = 4 * y + 2 * x + c
            mlp_copies.append(
                pltpu.make_async_remote_copy(
                    src_ref=src.at[pl.ds(pl.multiple_of(other * part, part), part)],
                    dst_ref=dst.at[:, here],
                    send_sem=m_send.at[at, index], recv_sem=m_recv.at[at, index],
                    device_id=device(flip), device_id_type=MESH,
                )
            )
        mlp_copies.append(
            pltpu.make_async_copy(
                src.at[pl.ds(pl.multiple_of(mine * part, part), part)],
                dst.at[:, here], m_own.at[at],
            )
        )
    for copy in mlp_copies:
        copy.start()

    gain_z[place] = gain_ref[...]
    gain_copies = [
        pltpu.make_async_remote_copy(
            src_ref=gain_ref, dst_ref=gain_z.at[place], send_sem=g_send.at[at],
            recv_sem=g_recv.at[at], device_id=peer, device_id_type=MESH,
        )
        for at, peer in enumerate(along)
    ]
    for copy in gain_copies:
        copy.start()

    rights = (dkv_ref, dq_ref)
    rows = sums.shape[0]
    outs = (wkv_out, wq_out)
    z_copies = []
    for index, ring in enumerate(rings):
        right = rights[index]
        cols = right.shape[1]

        @pl.loop(0, 8)
        def _(step):
            chunk, target = ring.chunk(step)
            x = x_ref[:, pl.ds(pl.multiple_of(chunk * rows, rows), rows)].T

            @pl.loop(0, cols // NTILE)
            def _(at):
                n = pl.ds(pl.multiple_of(at * NTILE, NTILE), NTILE)
                target[:, n] = dot_nn(x, right[:, n]).astype(BF16)

            ring.after(step)

        if index == 0:
            for copy in gain_copies:
                copy.wait_recv()
            total = gain_z[0]
            for at in range(1, z_size):
                total = total + gain_z[at]
            gain_p[mine] = total
            for at, peer in enumerate(around):
                copy = pltpu.make_async_remote_copy(
                    src_ref=gain_p.at[mine], dst_ref=gain_p.at[mine],
                    send_sem=g_send.at[z_size - 1 + at], recv_sem=g_recv.at[z_size - 1 + at],
                    device_id=peer, device_id_type=MESH,
                )
                gain_copies.append(copy)
                copy.start()

    def send_along(index, ring, start):
        cols = rights[index].shape[1]
        part = cols // z_size

        def store(here, value):
            sums[here, pl.ds(start, cols)] = value.astype(BF16)

        ring.finish(store)
        for at, peer in enumerate(along):
            other = (place + at + 1) % z_size
            copy = pltpu.make_async_remote_copy(
                src_ref=sums.at[:, pl.ds(pl.multiple_of(start + other * part, LANES), part)],
                dst_ref=zrecv.at[at, :, pl.ds(start // z_size, part)],
                send_sem=z_send.at[index, at], recv_sem=z_recv.at[index, at],
                device_id=peer, device_id_type=MESH,
            )
            z_copies.append(copy)
            copy.start()

    starts = [0, rights[0].shape[1]]
    for index, ring in enumerate(rings):
        ring.pass_on()
        if index:
            send_along(index - 1, rings[index - 1], starts[index - 1])
    send_along(1, rings[1], starts[1])

    for copy in gain_copies[z_size - 1 :]:
        copy.wait_recv()
    total = gain_p[0]
    for at in range(1, GROUP):
        total = total + gain_p[at]
    gain_out[...] = total

    for copy in z_copies:
        copy.wait_recv()
    for index in range(2):
        part = rights[index].shape[1] // z_size
        own = pl.ds(pl.multiple_of(starts[index] + place * part, LANES), part)
        value = sums[:, own].astype(F32)
        for at in range(z_size - 1):
            value += zrecv[at, :, pl.ds(starts[index] // z_size, part)].astype(F32)
        outs[index][...] = value
    for copy in z_copies + gain_copies:
        copy.wait_send()
    for ring in rings:
        ring.sent()
    for copy in mlp_copies:
        copy.wait()


def last_grads(x, dq, dkv, gains, mlp, dp_size, z_size):
    tokens, width = x.shape
    rows = width // GROUP
    near = pl.BlockSpec(memory_space=pltpu.VMEM)
    far = pl.BlockSpec(memory_space=pl.ANY)
    sizes = [dkv.shape[1], dq.shape[1]]
    scratch = []
    for cols in sizes:
        scratch += Reduce.scratch(rows, cols)
    total = sum(sizes)
    return pl.pallas_call(
        functools.partial(tail_kernel, 2 * math.isqrt(dp_size // GROUP), z_size, len(mlp)),
        in_specs=[near] * 4 + [far] * len(mlp),
        out_specs=[near] * 3 + [far] * len(mlp),
        out_shape=[jax.ShapeDtypeStruct((rows, cols // z_size), F32) for cols in sizes[::-1]]
        + [jax.ShapeDtypeStruct(gains.shape, F32)]
        + [
            jax.ShapeDtypeStruct((m.shape[0] // GROUP, GROUP * m.shape[1]), BF16) for m in mlp
        ],
        scratch_shapes=scratch
        + [
            pltpu.VMEM((rows, total), BF16),
            pltpu.VMEM((z_size - 1, rows, total // z_size), BF16),
            pltpu.VMEM((z_size, *gains.shape), F32),
            pltpu.VMEM((GROUP, *gains.shape), F32),
            pltpu.SemaphoreType.DMA((2, z_size - 1)),
            pltpu.SemaphoreType.DMA((2, z_size - 1)),
            pltpu.SemaphoreType.DMA((z_size - 1 + GROUP - 1,)),
            pltpu.SemaphoreType.DMA((z_size - 1 + GROUP - 1,)),
            pltpu.SemaphoreType.DMA((len(mlp),)),
            pltpu.SemaphoreType.DMA((len(mlp), GROUP - 1)),
            pltpu.SemaphoreType.DMA((len(mlp), GROUP - 1)),
        ],
        compiler_params=pltpu.CompilerParams(
            collective_id=4, has_side_effects=True, vmem_limit_bytes=60 << 20
        ),
        cost_estimate=pl.CostEstimate(
            flops=2 * LONG, bytes_accessed=4 * tokens * total, transcendentals=0
        ),
    )(x, dq, dkv, gains, *mlp)


class Layout:
    def __init__(self, dp_size):
        self.blocks = dp_size // GROUP
        side = math.isqrt(self.blocks)
        self.rows, self.cols = side, self.blocks // side
        wide = 2 * self.cols

        def index(by, bx, y, x, core):
            return ((2 * by + y) * wide + 2 * bx + x) * 2 + core

        places = [(y, x, c) for y in range(2) for x in range(2) for c in range(2)]
        spots = [(by, bx) for by in range(self.rows) for bx in range(self.cols)]
        self.inner = [[index(*s, *p) for p in places] for s in spots]
        self.outer = [[index(*s, *p) for s in spots] for p in places]

    def groups(self):
        return None if self.blocks == 1 else self.inner

    def to_rows(self, array):
        if self.blocks == 1:
            return array
        rest = array.shape[1:]
        split = array.reshape(2, 2, 2, self.rows, self.cols, -1, *rest)
        order = (3, 0, 4, 1, 2, 5) + tuple(range(6, 6 + len(rest)))
        return split.transpose(order).reshape(array.shape)

    def from_rows(self, array):
        if self.blocks == 1:
            return array
        rest = array.shape[1:]
        split = array.reshape(self.rows, 2, self.cols, 2, 2, -1, *rest)
        order = (1, 3, 4, 0, 2, 5) + tuple(range(6, 6 + len(rest)))
        return split.transpose(order).reshape(array.shape)

    def from_cols(self, array):
        return array if self.blocks == 1 else self.from_rows(array.T).T

    def gather_outer(self, array):
        if self.blocks == 1:
            return array
        return lax.all_gather(array, "dp", axis_index_groups=self.outer, axis=0, tiled=True)

    def scatter_outer(self, array):
        if self.blocks == 1:
            return array
        return lax.psum_scatter(
            array, "dp", scatter_dimension=0, axis_index_groups=self.outer, tiled=True
        )

    def sum_outer(self, array):
        if self.blocks == 1:
            return array
        return lax.psum(array, "dp", axis_index_groups=self.outer)

    def gather(self, array):
        return lax.all_gather(array, "dp", axis_index_groups=self.groups(), axis=0, tiled=True)

    def scatter(self, array):
        return lax.psum_scatter(
            array, "dp", scatter_dimension=0, axis_index_groups=self.groups(), tiled=True
        )


def rms_scale(values):
    return lax.rsqrt(jnp.mean(values * values, axis=-1, keepdims=True) + NORM_EPS)


def norm_back(values, scaling, gain, grad):
    gained = grad * gain
    gain_part = jnp.sum(grad * values * scaling, axis=0)
    inner = jnp.mean(gained * values, axis=-1, keepdims=True)
    return gain_part, scaling * gained - values * scaling * scaling * scaling * inner


def per_device(
    dp_size, z_size, activations, segment_ids, attn_gain, w_query, w_key, w_value, w_out,
    mlp_gain, w_gate, w_up, w_down, cotangent,
):
    layout = Layout(dp_size)
    rows, width = activations.shape[1:]
    x = activations[0].astype(F32)
    place = lax.axis_index("tensor")
    reach = -(-(MOST_DOC - 1) // rows) * rows

    def shift(array, step):
        pairs = [(at, at + step) for at in range(z_size) if 0 <= at + step < z_size]
        return lax.ppermute(array, "tensor", pairs)

    starts = document_starts(segment_ids[0])
    own_starts = lax.dynamic_slice_in_dim(starts, place * rows, rows)
    own_tokens = place * rows + jnp.arange(rows, dtype=jnp.int32)
    cosine, sine = rope_tables(own_tokens - own_starts)
    low = (own_starts - place * rows + reach)[None, :]

    shards = [
        layout.gather_outer(w)
        for w in (w_gate, w_up, w_down, jnp.concatenate([w_key, w_value], axis=1), w_query, w_out)
    ]
    spread = spread_weights(shards[:3], shards[3:], dp_size, z_size)
    wg, wu, wd = (
        layout.to_rows(lax.all_gather(w, "tensor", axis=1, tiled=True)) for w in spread[:3]
    )
    wkv, wq, wo = (layout.to_rows(w) for w in gather_rows(spread[3:], dp_size))

    def along_z(total):
        return lax.psum_scatter(
            layout.from_rows(total), "tensor", scatter_dimension=1, tiled=True
        )

    r1 = rms_scale(x)
    xn = (x * r1 * attn_gain).astype(BF16)
    q, kv = project_qkv(xn, wq, wkv, cosine, sine)
    grad, kv = lax.optimization_barrier((cotangent[0], kv))
    pieces, moved = [kv], kv
    for _ in range(reach // rows):
        moved = shift(moved, 1)
        pieces.insert(0, moved)
    kv_all = jnp.concatenate(pieces, axis=0)
    att, lse = attend(q, kv_all, low)
    h = x + dot_nt(att, wo)

    r2 = rms_scale(h)
    hn, gate, up, hidden = gate_up((h * r2 * mlp_gain).astype(BF16), wg, wu, dp_size)
    dy = layout.gather(grad)
    total_wd = dot_tn(dy, hidden).astype(BF16)
    dy, total_wd = lax.optimization_barrier((dy, total_wd))
    part_wd = along_z(total_wd)
    gate, up = gate.astype(F32), up.astype(F32)
    sigma = jax.nn.sigmoid(gate)
    dhid = dot_nn(dy, wd)
    dgate = (dhid * up * sigma * (1.0 + gate * (1.0 - sigma))).astype(BF16)
    dup = (dhid * gate * sigma).astype(BF16)
    total_wg = dot_tn(hn, dgate).astype(BF16)
    dgate, total_wg = lax.optimization_barrier((dgate, total_wg))
    part_wg = along_z(total_wg)
    dhn = hidden_back(dgate, dup, wg, wu, dp_size)
    hn, hidden, dhn, part_wd = lax.optimization_barrier((hn, hidden, dhn, part_wd))
    total_wu = dot_tn(hn, dup).astype(BF16)
    partial_out = dot_nt(hidden, wd).astype(BF16)
    dhn, total_wu, partial_out, part_wg = lax.optimization_barrier(
        (dhn, total_wu, partial_out, part_wg)
    )
    part_wu = along_z(total_wu)
    gain_two, dh_norm = norm_back(h, r2, mlp_gain, dhn)
    dh = cotangent[0].astype(F32) + dh_norm

    dhb = dh.astype(BF16)
    datt = dot_nn(dhb, wo).astype(BF16)
    datt, partial_out = lax.optimization_barrier((datt, partial_out))
    out_sum = layout.scatter(partial_out)
    dq, dkv, wo_grad = attend_back(
        q, datt, att, kv_all, lse, low, cosine, sine, layout.from_cols(dhb), dp_size, z_size
    )
    dq, part_wu = lax.optimization_barrier((dq, part_wu))
    dxn = dot_nt(dq, wq) + dot_nt(dkv, wkv)
    gain_one, dx_norm = norm_back(x, r1, attn_gain, dxn)
    input_grad = (dh + dx_norm).astype(BF16)
    gains = layout.sum_outer(jnp.stack([gain_one, gain_two]))
    wq_grad, wkv_grad, gains, wd_grad, wg_grad, wu_grad = last_grads(
        layout.from_cols(xn), dq, dkv, gains, (part_wd, part_wg, part_wu), dp_size, z_size
    )
    wo_grad, wq_grad, wkv_grad, wd_grad, wg_grad, wu_grad = (
        layout.scatter_outer(grad).astype(F32)
        for grad in (wo_grad, wq_grad, wkv_grad, wd_grad, wg_grad, wu_grad)
    )
    gains, out_sum = lax.optimization_barrier((gains, out_sum))
    output = h + out_sum.astype(F32)
    key_cols = w_key.shape[1]
    return (
        output.astype(BF16)[None],
        input_grad[None],
        gains[0],
        wq_grad,
        wkv_grad[:, :key_cols],
        wkv_grad[:, key_cols:],
        wo_grad,
        gains[1],
        wg_grad,
        wu_grad,
        wd_grad,
    )


def solution(mesh):
    split = P("dp", "tensor")
    tokens = P("dp", "tensor", None)
    in_specs = (
        tokens, P("dp", None), P(), split, split, split, split, P(), split, split, split, tokens,
    )
    out_specs = (tokens, tokens, P(), split, split, split, split, P(), split, split, split)
    return jax.shard_map(
        functools.partial(per_device, mesh.shape["dp"], mesh.shape["tensor"]),
        mesh=mesh, in_specs=in_specs, out_specs=out_specs, check_vma=False,
    )
```

```python
import functools
import math

import jax
import jax.numpy as jnp
from jax import lax
from jax.experimental import pallas as pl
from jax.experimental.pallas import tpu as pltpu
from jax.sharding import PartitionSpec as P

HEAD_DIM = 64
DOCS = 4
MOST_DOC = 1024
NORM_EPS = 1e-05
ROPE_THETA = 500000.0
GROUP = 8
LANES = 128
QTILE = 256
SCALE = HEAD_DIM ** (-0.5)
LOG2E = 1.4426950408889634
FAR = -1e30
NTILE = 512
STRIP = 16
LONG = 60_000_000_000

F32 = jnp.float32
BF16 = jnp.bfloat16


def dot_nn(left, right):
    return lax.dot_general(left, right, (((1,), (0,)), ((), ())), preferred_element_type=F32)


def dot_nt(left, right):
    return lax.dot_general(left, right, (((1,), (1,)), ((), ())), preferred_element_type=F32)


def dot_tn(left, right):
    return lax.dot_general(left, right, (((0,), (0,)), ((), ())), preferred_element_type=F32)


def document_starts(segments):
    doc_ids = jnp.arange(DOCS, dtype=jnp.int32)
    counts = jnp.sum((segments[:, None] == doc_ids).astype(jnp.int32), axis=0)
    before = (doc_ids < segments[:, None]).astype(jnp.int32)
    return jnp.sum(before * counts[None, :], axis=-1)


def rope_tables(positions):
    half = HEAD_DIM // 2
    frequency = jnp.exp(
        jnp.arange(half, dtype=F32) * (-2.0 * math.log(ROPE_THETA) / HEAD_DIM)
    )
    angles = positions.astype(F32)[:, None] * frequency
    cosine, sine = jnp.cos(angles), jnp.sin(angles)
    wide_cos = jnp.concatenate([cosine] * 4, axis=1)
    wide_sin = jnp.concatenate([-sine, sine, -sine, sine], axis=1)
    return wide_cos, wide_sin


def swap_halves(values):
    lane = lax.broadcasted_iota(jnp.int32, values.shape, 1)
    ahead = pltpu.roll(values, LANES - 32, 1)
    behind = pltpu.roll(values, 32, 1)
    return jnp.where((lane % 64) < 32, ahead, behind)


def qkv_kernel(x_ref, wq_ref, wkv_ref, cos_ref, sin_ref, q_ref, kv_ref):
    x = x_ref[...]
    cosine, sine = cos_ref[...], sin_ref[...]
    for at in range(wq_ref.shape[1] // LANES):
        part = pl.ds(at * LANES, LANES)
        value = dot_nn(x, wq_ref[:, part])
        q_ref[:, part] = (value * cosine + swap_halves(value) * sine).astype(BF16)
    value = dot_nn(x, wkv_ref[...])
    key = value[:, :LANES]
    kv_ref[:, :LANES] = (key * cosine + swap_halves(key) * sine).astype(BF16)
    kv_ref[:, LANES:] = value[:, LANES:].astype(BF16)


def project_qkv(x, wq, wkv, cosine, sine):
    rows, width = x.shape
    blocks = wkv.shape[1] // (2 * LANES)
    qcols = wq.shape[1] // blocks
    return pl.pallas_call(
        qkv_kernel,
        grid=(blocks,),
        in_specs=[
            pl.BlockSpec((rows, width), lambda g: (0, 0)),
            pl.BlockSpec((width, qcols), lambda g: (0, g)),
            pl.BlockSpec((width, 2 * LANES), lambda g: (0, g)),
            pl.BlockSpec((rows, LANES), lambda g: (0, 0)),
            pl.BlockSpec((rows, LANES), lambda g: (0, 0)),
        ],
        out_specs=[
            pl.BlockSpec((rows, qcols), lambda g: (0, g)),
            pl.BlockSpec((rows, 2 * LANES), lambda g: (0, g)),
        ],
        out_shape=[
            jax.ShapeDtypeStruct((rows, wq.shape[1]), BF16),
            jax.ShapeDtypeStruct((rows, wkv.shape[1]), BF16),
        ],
        compiler_params=pltpu.CompilerParams(vmem_limit_bytes=40 << 20),
        cost_estimate=pl.CostEstimate(
            flops=2 * rows * width * (wq.shape[1] + wkv.shape[1]),
            bytes_accessed=2 * width * (wq.shape[1] + wkv.shape[1]),
            transcendentals=0,
        ),
    )(x, wq, wkv, cosine, sine)


def fill_bias(bias_ref, low_ref, reach):
    span = bias_ref.shape[1]
    for tile in range(bias_ref.shape[0]):
        row = lax.broadcasted_iota(jnp.int32, (span, QTILE), 0)
        col = lax.broadcasted_iota(jnp.int32, (span, QTILE), 1)
        low = low_ref[0:1, tile * QTILE : (tile + 1) * QTILE]
        allowed = (row <= reach + col) & (row + tile * QTILE >= low)
        bias_ref[tile] = jnp.where(allowed, 0.0, FAR)


def spread_pair(pair, half):
    wide = pair.astype(F32)
    turned = pltpu.roll(wide, 64, 1)
    lane = lax.broadcasted_iota(jnp.int32, wide.shape, 1)
    mine = (lane // 64) == half
    even = half == 0
    first = jnp.where(mine, jnp.where(even, wide, turned), 0.0)
    second = jnp.where(mine, jnp.where(even, turned, wide), 0.0)
    return jnp.concatenate([first, second], axis=0).astype(BF16)


def gather_pair(transposed, half):
    count = transposed.shape[1] // 2
    mine = jnp.where(half == 0, transposed[:64], transposed[64:])
    return jnp.concatenate([mine[:, :count], mine[:, count:]], axis=0).T


def attend_kernel(reach, q_ref, k_ref, v_ref, low_ref, att_ref, lse_ref, bias_ref):
    head, tile, pair = pl.program_id(0), pl.program_id(1), pl.program_id(2)
    half = head % 2

    @pl.when((head == 0) & (tile == 0) & (pair == 0))
    def _():
        fill_bias(bias_ref, low_ref, reach)

    keys = pl.ds(pl.multiple_of(tile * QTILE, QTILE), bias_ref.shape[1])
    queries = spread_pair(q_ref[...], half)
    bias = bias_ref[tile]
    score = dot_nt(k_ref[keys, :], queries)
    score = score + jnp.concatenate([bias, bias], axis=1)
    top = jnp.max(score, axis=0, keepdims=True) * (SCALE * LOG2E)
    weight = jnp.exp2(score * (SCALE * LOG2E) - top)
    total = jnp.sum(weight, axis=0, keepdims=True)
    result = dot_tn(v_ref[keys, :], weight.astype(BF16)) / total
    att_ref[...] = gather_pair(result, half).astype(BF16)
    lse_ref[0] = top + jnp.log2(total)


def attend(q, kv, low):
    rows, width = q.shape
    keys = kv.shape[0]
    reach = keys - rows
    tiles = rows // QTILE
    pairs = width // LANES
    heads = kv.shape[1] // LANES
    per_head = pairs // heads
    span = reach + QTILE
    return pl.pallas_call(
        functools.partial(attend_kernel, reach),
        grid=(heads, tiles, per_head),
        in_specs=[
            pl.BlockSpec((QTILE, LANES), lambda a, t, p: (t, a * per_head + p)),
            pl.BlockSpec((keys, LANES), lambda a, t, p: (0, 2 * (a // 2))),
            pl.BlockSpec((keys, LANES), lambda a, t, p: (0, 2 * (a // 2) + 1)),
            pl.BlockSpec((1, rows), lambda a, t, p: (0, 0)),
        ],
        out_specs=[
            pl.BlockSpec((QTILE, LANES), lambda a, t, p: (t, a * per_head + p)),
            pl.BlockSpec((1, 1, 2 * QTILE), lambda a, t, p: ((a * tiles + t) * per_head + p, 0, 0)),
        ],
        out_shape=[
            jax.ShapeDtypeStruct((rows, width), BF16),
            jax.ShapeDtypeStruct((pairs * tiles, 1, 2 * QTILE), F32),
        ],
        scratch_shapes=[pltpu.VMEM((tiles, span, QTILE), F32)],
        compiler_params=pltpu.CompilerParams(vmem_limit_bytes=48 << 20),
        cost_estimate=pl.CostEstimate(
            flops=16 * rows * span * LANES * pairs,
            bytes_accessed=4 * rows * width + 2 * keys * kv.shape[1],
            transcendentals=2 * rows * span * pairs,
        ),
    )(q, kv, kv, low)


def attend_back_kernel(
    reach, wide, z_size, mlp_count,
    q_ref, do_ref, o_ref, k_ref, v_ref, lse_ref, low_ref, cos_ref, sin_ref, cos_all, sin_all,
    h_ref, att_ref, *refs,
):
    mlp_ins, refs = refs[:mlp_count], refs[mlp_count:]
    dq_ref, dkv_ref, wo_out = refs[:3]
    mlp_outs, refs = refs[3 : 3 + mlp_count], refs[3 + mlp_count :]
    bias_ref, dk_acc, dv_acc, own_part, send_part, recv_part, kv_send, kv_recv = refs[:8]
    ring = Reduce(wide, *refs[8:14])
    sums, zrecv, z_send, z_recv = refs[14:18]
    home = refs[18:]
    block, half, tile, pair = (pl.program_id(at) for at in range(4))
    steps = pl.num_programs(1) * pl.num_programs(2) * pl.num_programs(3)
    inner = (half * pl.num_programs(2) + tile) * pl.num_programs(3) + pair
    step = block * steps + inner
    blocks = own_part.shape[0]
    rows = own_part.shape[1]
    count = reach // rows
    place = lax.axis_index("tensor")

    def exchange(at, distance):
        return pltpu.make_async_remote_copy(
            src_ref=send_part.at[at, pl.ds((count - distance) * rows, rows)],
            dst_ref=recv_part.at[at, distance - 1],
            send_sem=kv_send.at[at, distance - 1], recv_sem=kv_recv.at[at, distance - 1],
            device_id={"tensor": (place + z_size - distance) % z_size}, device_id_type=MESH,
        )

    def each_exchange(at, condition, action):
        for distance in range(1, count + 1):
            pl.when(condition(distance))(
                functools.partial(action, exchange(at, distance), at, distance)
            )

    def along(at):
        cols = wo_out.shape[1]
        other = (place + at + 1) % z_size
        return pltpu.make_async_remote_copy(
            src_ref=sums.at[:, pl.ds(pl.multiple_of(other * cols, LANES), cols)],
            dst_ref=zrecv.at[at], send_sem=z_send.at[at], recv_sem=z_recv.at[at],
            device_id={"tensor": other}, device_id_type=MESH,
        )

    @pl.when(step == 0)
    def _():
        greet(along_peers(place, z_size) + [device for _, device in others(wide)[1]])
        for copy in send_home(wide, mlp_ins, mlp_outs, *home):
            copy.start()
        fill_bias(bias_ref, low_ref, reach)

    @pl.when((step % 2 == 0) & (step < 16))
    def _():
        chunk, target = ring.chunk(step // 2)
        part = target.shape[0]
        x = h_ref[:, pl.ds(pl.multiple_of(chunk * part, part), part)].T

        @pl.loop(0, att_ref.shape[1] // NTILE)
        def _(at):
            n = pl.ds(pl.multiple_of(at * NTILE, NTILE), NTILE)
            target[:, n] = dot_nn(x, att_ref[:, n]).astype(BF16)

        ring.after(step // 2)

    pl.when(step == 19)(ring.pass_on)

    @pl.when(step == 27)
    def _():
        def store(here, value):
            sums[here, :] = value.astype(BF16)

        ring.finish(store)
        for at in range(z_size - 1):
            along(at).start()

    @pl.when(inner == 0)
    def _():
        dk_acc[...] = jnp.zeros_like(dk_acc)
        dv_acc[...] = jnp.zeros_like(dv_acc)

    keys = pl.ds(pl.multiple_of(tile * QTILE, QTILE), bias_ref.shape[1])
    queries = spread_pair(q_ref[...], half)
    grads = spread_pair(do_ref[...], half)
    product = (do_ref[...].astype(F32) * o_ref[...].astype(F32)).T
    row_dot = jnp.concatenate(
        [
            jnp.sum(product[:64], axis=0, keepdims=True),
            jnp.sum(product[64:], axis=0, keepdims=True),
        ],
        axis=1,
    )
    bias = bias_ref[tile]
    key, value = k_ref[keys, :], v_ref[keys, :]
    score = dot_nt(key, queries) + jnp.concatenate([bias, bias], axis=1)
    weight = jnp.exp2(score * (SCALE * LOG2E) - lse_ref[0])
    dv_acc[keys, :] += dot_nn(weight.astype(BF16), grads)
    dscore = (weight * (dot_nt(value, grads) - row_dot)).astype(BF16)
    dk_acc[keys, :] += dot_nn(dscore, queries)
    dq = gather_pair(dot_tn(key, dscore), half) * SCALE
    dq_ref[...] = (dq * cos_ref[...] - swap_halves(dq) * sin_ref[...]).astype(BF16)

    @pl.when(inner == steps - 1)
    def _():
        send_part[block, :, :LANES] = (dk_acc[:reach] * SCALE).astype(BF16)
        send_part[block, :, LANES:] = dv_acc[:reach].astype(BF16)
        own_part[block, :, :LANES] = dk_acc[reach:] * SCALE
        own_part[block, :, LANES:] = dv_acc[reach:]
        each_exchange(block, lambda distance: place >= distance, lambda copy, *_: copy.start())

    @pl.when(step == blocks * steps - 1)
    def _():
        def collect(copy, at, distance):
            copy.wait_recv()
            own_part[at] += recv_part[at, distance - 1].astype(F32)

        for at in range(blocks):
            each_exchange(at, lambda distance: place + distance < z_size, collect)
            dkey = own_part[at, :, :LANES]
            dkey = dkey * cos_all[...] - swap_halves(dkey) * sin_all[...]
            dkv_ref[:, 2 * at * LANES : (2 * at + 1) * LANES] = dkey.astype(BF16)
            dkv_ref[:, (2 * at + 1) * LANES : (2 * at + 2) * LANES] = own_part[
                at, :, LANES:
            ].astype(BF16)
        total = sums[:, pl.ds(pl.multiple_of(place * wo_out.shape[1], LANES), wo_out.shape[1])]
        total = total.astype(F32)
        for at in range(z_size - 1):
            along(at).wait_recv()
            total += zrecv[at].astype(F32)
        wo_out[...] = total
        for at in range(z_size - 1):
            along(at).wait_send()
        for at in range(blocks):
            each_exchange(
                at, lambda distance: place >= distance, lambda copy, *_: copy.wait_send()
            )
        ring.sent()
        for copy in send_home(wide, mlp_ins, mlp_outs, *home):
            copy.wait()


def attend_back(q, do, att, kv, lse, low, cosine, sine, h, mlp, dp_size, z_size):
    rows, width = q.shape
    keys = kv.shape[0]
    reach = keys - rows
    tiles = rows // QTILE
    pairs = width // LANES
    heads = kv.shape[1] // LANES
    per_head = pairs // heads
    span = reach + QTILE
    blocks = heads // 2
    part = h.shape[1] // GROUP
    cols = width // z_size

    def pair_at(g, h, t, p):
        return (t, (2 * g + h) * per_head + p)

    def whole(shape):
        return pl.BlockSpec(shape, lambda g, h, t, p: (0, 0), pipeline_mode=pl.Buffered(1))

    table = pl.BlockSpec((QTILE, LANES), lambda g, h, t, p: (t, 0))
    return pl.pallas_call(
        functools.partial(
            attend_back_kernel, reach, 2 * math.isqrt(dp_size // GROUP), z_size, len(mlp)
        ),
        grid=(blocks, 2, tiles, per_head),
        in_specs=[
            pl.BlockSpec((QTILE, LANES), pair_at),
            pl.BlockSpec((QTILE, LANES), pair_at),
            pl.BlockSpec((QTILE, LANES), pair_at),
            pl.BlockSpec((keys, LANES), lambda g, h, t, p: (0, 2 * g)),
            pl.BlockSpec((keys, LANES), lambda g, h, t, p: (0, 2 * g + 1)),
            pl.BlockSpec(
                (1, 1, 2 * QTILE),
                lambda g, h, t, p: (((2 * g + h) * tiles + t) * per_head + p, 0, 0),
            ),
            whole((1, rows)),
            table,
            table,
            whole((rows, LANES)),
            whole((rows, LANES)),
            whole(h.shape),
            whole(att.shape),
        ]
        + [pl.BlockSpec(memory_space=pl.ANY)] * len(mlp),
        out_specs=[
            pl.BlockSpec((QTILE, LANES), pair_at),
            pl.BlockSpec((rows, kv.shape[1]), lambda g, h, t, p: (0, 0)),
            pl.BlockSpec((part, cols), lambda g, h, t, p: (0, 0)),
        ]
        + [pl.BlockSpec(memory_space=pl.ANY)] * len(mlp),
        out_shape=[
            jax.ShapeDtypeStruct((rows, width), BF16),
            jax.ShapeDtypeStruct((rows, kv.shape[1]), BF16),
            jax.ShapeDtypeStruct((part, cols), F32),
        ]
        + home_shapes(mlp),
        scratch_shapes=[
            pltpu.VMEM((tiles, span, QTILE), F32),
            pltpu.VMEM((keys, LANES), F32),
            pltpu.VMEM((keys, LANES), F32),
            pltpu.VMEM((blocks, rows, 2 * LANES), F32),
            pltpu.VMEM((blocks, reach, 2 * LANES), BF16),
            pltpu.VMEM((blocks, reach // rows, rows, 2 * LANES), BF16),
            pltpu.SemaphoreType.DMA((blocks, reach // rows)),
            pltpu.SemaphoreType.DMA((blocks, reach // rows)),
        ]
        + Reduce.scratch(part, width)
        + [
            pltpu.VMEM((part, width), BF16),
            pltpu.VMEM((z_size - 1, part, cols), BF16),
            pltpu.SemaphoreType.DMA((z_size - 1,)),
            pltpu.SemaphoreType.DMA((z_size - 1,)),
        ]
        + home_scratch(mlp),
        compiler_params=pltpu.CompilerParams(
            collective_id=5, has_side_effects=True, vmem_limit_bytes=60 << 20
        ),
        cost_estimate=pl.CostEstimate(
            flops=40 * rows * span * LANES * pairs,
            bytes_accessed=8 * rows * width + 4 * keys * kv.shape[1],
            transcendentals=2 * rows * span * pairs,
        ),
    )(q, do, att, kv, kv, lse, low, cosine, sine, cosine, sine, h, att, *mlp)


MESH = pl.DeviceIdType.MESH


def neighbours(wide):
    dp = lax.axis_index("dp")
    core, col, row = dp % 2, (dp // 2) % 2, (dp // (2 * wide)) % 2
    sibling = dp + 1 - 2 * core
    beside = dp + 2 - 4 * col
    above = dp + 2 * wide - 4 * wide * row
    return (row, col, core), (sibling, beside, above)


def meet(peers):
    barrier = pltpu.get_barrier_semaphore()
    for peer in peers:
        pl.semaphore_signal(barrier, inc=1, device_id={"dp": peer}, device_id_type=MESH)
    pl.semaphore_wait(barrier, len(peers))


def others(wide):
    (row, col, core), _ = neighbours(wide)
    base = lax.axis_index("dp") - (2 * wide * row + 2 * col + core)
    found = []
    for flip in range(1, GROUP):
        y, x, c = (row + flip // 4) % 2, (col + flip // 2) % 2, (core + flip) % 2
        found.append((4 * y + 2 * x + c, {"dp": base + 2 * wide * y + 2 * x + c}))
    return 4 * row + 2 * col + core, found


def along_peers(place, z_size):
    return [{"tensor": (place + step) % z_size} for step in range(1, z_size)]


def greet(peers):
    barrier = pltpu.get_barrier_semaphore()
    for peer in peers:
        pl.semaphore_signal(barrier, inc=1, device_id=peer, device_id_type=MESH)
    pl.semaphore_wait(barrier, len(peers))


def send_home(wide, ins, outs, own_sem, send_sem, recv_sem):
    mine, found = others(wide)
    copies = []
    for at, (src, dst) in enumerate(zip(ins, outs)):
        part, cols = dst.shape[0], src.shape[1]
        here = pl.ds(pl.multiple_of(mine * cols, LANES), cols)
        for index, (other, device) in enumerate(found):
            copies.append(
                pltpu.make_async_remote_copy(
                    src_ref=src.at[pl.ds(pl.multiple_of(other * part, part), part)],
                    dst_ref=dst.at[:, here],
                    send_sem=send_sem.at[at, index], recv_sem=recv_sem.at[at, index],
                    device_id=device, device_id_type=MESH,
                )
            )
        own = src.at[pl.ds(pl.multiple_of(mine * part, part), part)]
        copies.append(pltpu.make_async_copy(own, dst.at[:, here], own_sem.at[at]))
    return copies


def home_shapes(arrays):
    return [jax.ShapeDtypeStruct((a.shape[0] // GROUP, GROUP * a.shape[1]), BF16) for a in arrays]


def home_scratch(arrays):
    count = len(arrays)
    return [
        pltpu.SemaphoreType.DMA((count,)),
        pltpu.SemaphoreType.DMA((count, GROUP - 1)),
        pltpu.SemaphoreType.DMA((count, GROUP - 1)),
    ]


SIB, XN, YN = 0, 1, 2


def spread_kernel(wide, z_size, mlp_count, *refs):
    attn_count = (len(refs) - 3) // 2 - mlp_count
    count = mlp_count + attn_count
    ins, outs = refs[:count], refs[count : 2 * count]
    own_sem, send_sem, recv_sem = refs[2 * count :]
    (row, col, core), _ = neighbours(wide)
    dp, place = lax.axis_index("dp"), lax.axis_index("tensor")
    mine = 4 * row + 2 * col + core
    base = dp - (2 * wide * row + 2 * col + core)

    def peer(dy, dx, dc):
        y, x, c = (row + dy) % 2, (col + dx) % 2, (core + dc) % 2
        return base + 2 * wide * y + 2 * x + c, 4 * y + 2 * x + c

    flips = [(dy, dx, dc) for dy in range(2) for dx in range(2) for dc in range(2)][1:]
    barrier = pltpu.get_barrier_semaphore()
    for flip in flips:
        pl.semaphore_signal(
            barrier, inc=1, device_id={"dp": peer(*flip)[0]}, device_id_type=MESH
        )
    for step in range(1, z_size):
        pl.semaphore_signal(
            barrier, inc=1, device_id={"tensor": (place + step) % z_size}, device_id_type=MESH
        )
    pl.semaphore_wait(barrier, len(flips) + z_size - 1)

    copies, local = [], []
    slot = 0
    for at in range(mlp_count, count):
        src, dst = ins[at], outs[at]
        cols = src.shape[1]
        part = pl.ds(pl.multiple_of(place * cols, LANES), cols)
        for step in range(1, z_size):
            copies.append(
                pltpu.make_async_remote_copy(
                    src_ref=src, dst_ref=dst.at[:, part],
                    send_sem=send_sem.at[slot], recv_sem=recv_sem.at[slot],
                    device_id={"tensor": (place + step) % z_size}, device_id_type=MESH,
                )
            )
            slot += 1
        local.append(pltpu.make_async_copy(src, dst.at[:, part], own_sem.at[at]))
    for at in range(mlp_count):
        src, dst = ins[at], outs[at]
        rows, cols = src.shape[0], dst.shape[1]
        here = pl.ds(pl.multiple_of(mine * rows, rows), rows)
        for flip in flips:
            device, other = peer(*flip)
            copies.append(
                pltpu.make_async_remote_copy(
                    src_ref=src.at[:, pl.ds(pl.multiple_of(other * cols, LANES), cols)],
                    dst_ref=dst.at[here],
                    send_sem=send_sem.at[slot], recv_sem=recv_sem.at[slot],
                    device_id={"dp": device}, device_id_type=MESH,
                )
            )
            slot += 1
        own = src.at[:, pl.ds(pl.multiple_of(mine * cols, LANES), cols)]
        local.append(pltpu.make_async_copy(own, dst.at[here], own_sem.at[at]))
    for copy in copies:
        copy.start()
    for copy in local:
        copy.start()
    for copy in local:
        copy.wait()
    for copy in copies:
        copy.wait()


def spread_weights(mlp, attn, dp_size, z_size):
    count = len(mlp) + len(attn)
    slots = (z_size - 1) * len(attn) + (GROUP - 1) * len(mlp)
    spec = pl.BlockSpec(memory_space=pl.ANY)
    out = [jax.ShapeDtypeStruct((GROUP * w.shape[0], w.shape[1] // GROUP), BF16) for w in mlp]
    out += [jax.ShapeDtypeStruct((w.shape[0], z_size * w.shape[1]), BF16) for w in attn]
    return pl.pallas_call(
        functools.partial(spread_kernel, 2 * math.isqrt(dp_size // GROUP), z_size, len(mlp)),
        in_specs=[spec] * count,
        out_specs=[spec] * count,
        out_shape=out,
        scratch_shapes=[
            pltpu.SemaphoreType.DMA((count,)),
            pltpu.SemaphoreType.DMA((slots,)),
            pltpu.SemaphoreType.DMA((slots,)),
        ],
        compiler_params=pltpu.CompilerParams(collective_id=2, has_side_effects=True),
        cost_estimate=pl.CostEstimate(flops=LONG, bytes_accessed=0, transcendentals=0),
    )(*mlp, *attn)


class Ring:
    FLIP = {SIB: (0, 0, 1), XN: (0, 1, 0), YN: (1, 0, 0)}
    COPIES = 14

    def __init__(self, wide, ref, rows, send_sem, recv_sem):
        (self.row, self.col, self.core), self.peers = neighbours(wide)
        self.ref, self.rows, self.part = ref, rows, rows // 2
        self.send_sem, self.recv_sem = send_sem, recv_sem
        self.sends = {}
        for half in range(2):
            self.sends["own", XN, half] = (2 + half, 0, 0, 0, half)
            self.sends["own", YN, half] = (4 + half, 0, 0, 0, half)
            self.sends["own", SIB, half] = (0 + half, 0, 0, 0, half)
        for half in range(2):
            self.sends["x", SIB, half] = (6 + half, 0, 1, 0, half)
            self.sends["y", SIB, half] = (8 + half, 1, 0, 0, half)
            self.sends["d", SIB, half] = (10 + half, 1, 1, 0, half)
        self.sends["x", YN, 0] = (12, 0, 1, 0, 0)
        self.sends["y", XN, 1] = (13, 1, 0, 0, 1)

    def place(self, dy, dx, dc, half):
        p = 4 * ((self.row + dy) % 2) + 2 * ((self.col + dx) % 2) + (self.core + dc) % 2
        return pl.ds(pl.multiple_of(p * self.rows + half * self.part, self.part), self.part)

    def mine(self):
        p = 4 * self.row + 2 * self.col + self.core
        return pl.ds(pl.multiple_of(p * self.rows, self.rows), self.rows)

    def copy(self, slot, dy, dx, dc, half, peer):
        where = self.place(dy, dx, dc, half)
        return pltpu.make_async_remote_copy(
            src_ref=self.ref.at[where], dst_ref=self.ref.at[where],
            send_sem=self.send_sem.at[slot], recv_sem=self.recv_sem.at[slot],
            device_id={"dp": self.peers[peer]}, device_id_type=MESH,
        )

    def start(self, name, peer, half):
        self.copy(*self.sends[name, peer, half], peer).start()

    def arrived(self, name, peer, half):
        slot, dy, dx, dc, half = self.sends[name, peer, half]
        fy, fx, fc = self.FLIP[peer]
        self.copy(slot, (dy + fy) % 2, (dx + fx) % 2, (dc + fc) % 2, half, peer).wait_recv()

    def start_own(self):
        for half in range(2):
            for peer in (XN, YN, SIB):
                self.start("own", peer, half)

    def first_halves(self):
        self.arrived("own", XN, 0)
        self.start("x", YN, 0)
        self.start("x", SIB, 0)
        self.arrived("own", YN, 0)
        self.start("y", SIB, 0)

    def second_halves(self):
        self.arrived("own", YN, 1)
        self.start("y", XN, 1)
        self.start("y", SIB, 1)
        self.arrived("own", XN, 1)
        self.start("x", SIB, 1)

    def far_halves(self):
        self.arrived("x", YN, 0)
        self.start("d", SIB, 0)
        self.arrived("y", XN, 1)
        self.start("d", SIB, 1)

    def from_sibling(self, name, *halves):
        for half in halves:
            self.arrived(name, SIB, half)

    def sent(self):
        for (name, peer, half), entry in self.sends.items():
            self.copy(*entry, peer).wait_send()


def gather_kernel(wide, count, *refs):
    ins, outs = refs[:count], refs[count : 2 * count]
    own_sem, send_sem, recv_sem = refs[2 * count :]
    rings = [
        Ring(wide, outs[at], ins[at].shape[0], send_sem.at[at], recv_sem.at[at])
        for at in range(count)
    ]
    local = [
        pltpu.make_async_copy(ins[at], outs[at].at[rings[at].mine()], own_sem.at[at])
        for at in range(count)
    ]
    for copy in local:
        copy.start()
    meet(rings[0].peers)
    for copy, ring in zip(local, rings):
        copy.wait()
        ring.start_own()
    for ring in rings:
        ring.first_halves()
        ring.second_halves()
    for ring in rings:
        ring.far_halves()
        for name in ("own", "x", "y", "d"):
            ring.from_sibling(name, 0, 1)
    for ring in rings:
        ring.sent()


def gather_rows(arrays, dp_size):
    count = len(arrays)
    spec = pl.BlockSpec(memory_space=pl.ANY)
    return pl.pallas_call(
        functools.partial(gather_kernel, 2 * math.isqrt(dp_size // GROUP), count),
        in_specs=[spec] * count,
        out_specs=[spec] * count,
        out_shape=[jax.ShapeDtypeStruct((GROUP * a.shape[0], a.shape[1]), a.dtype) for a in arrays],
        scratch_shapes=[
            pltpu.SemaphoreType.DMA((count,)),
            pltpu.SemaphoreType.DMA((count, Ring.COPIES)),
            pltpu.SemaphoreType.DMA((count, Ring.COPIES)),
        ],
        compiler_params=pltpu.CompilerParams(collective_id=3, has_side_effects=True),
        cost_estimate=pl.CostEstimate(flops=2 * LONG, bytes_accessed=0, transcendentals=0),
    )(*arrays)


def gate_up_kernel(
    wide, own_ref, wg_ref, wu_ref, all_ref, gate_ref, up_ref, hid_ref,
    full, stage, own_sem, send_sem, recv_sem, out_sem, all_sem,
):
    rows = own_ref.shape[0]
    cols = gate_ref.shape[1]
    ring = Ring(wide, full, rows, send_sem, recv_sem)
    local = pltpu.make_async_copy(own_ref, full.at[ring.mine()], own_sem)
    local.start()
    meet(ring.peers)
    local.wait()
    ring.start_own()

    def out_copies(slot, where):
        return [
            pltpu.make_async_copy(stage.at[slot, i], ref.at[where], out_sem.at[slot, i])
            for i, ref in enumerate((gate_ref, up_ref, hid_ref))
        ] + [pltpu.make_async_copy(full.at[where], all_ref.at[where], all_sem.at[slot])]

    def step_place(step):
        phase, i = step // 4, step % 4
        high, low = phase // 2, phase % 2
        first, last = (1 - high) * (1 - low), high * low
        middle = high + low - 2 * last
        half = (first + last) * (i % 2) + high * (1 - low)
        dx = middle * (1 - i % 2) + last
        dy = middle * (i % 2) + last
        return ring.place(dy, dx, i // 2, half)

    @pl.loop(0, 16)
    def _(step):
        pl.when(step == 2)(lambda: ring.from_sibling("own", 0, 1))
        pl.when(step == 4)(ring.first_halves)

        @pl.when(step == 6)
        def _():
            ring.from_sibling("x", 0)
            ring.from_sibling("y", 0)

        pl.when(step == 8)(ring.second_halves)

        @pl.when(step == 10)
        def _():
            ring.from_sibling("x", 1)
            ring.from_sibling("y", 1)

        pl.when(step == 12)(ring.far_halves)
        pl.when(step == 14)(lambda: ring.from_sibling("d", 0, 1))

        slot = step % 2
        where = step_place(step)

        @pl.when(step >= 2)
        def _():
            for copy in out_copies(slot, step_place(step - 2)):
                copy.wait()

        x = full[where, :]

        @pl.loop(0, cols // NTILE)
        def _(at):
            n = pl.ds(pl.multiple_of(at * NTILE, NTILE), NTILE)
            gate = dot_nn(x, wg_ref[:, n])
            up = dot_nn(x, wu_ref[:, n])
            stage[slot, 0, :, n] = gate.astype(BF16)
            stage[slot, 1, :, n] = up.astype(BF16)
            stage[slot, 2, :, n] = (gate * up / (1.0 + jnp.exp(-gate))).astype(BF16)

        for copy in out_copies(slot, where):
            copy.start()

    for step in (14, 15):
        for copy in out_copies(step % 2, step_place(step)):
            copy.wait()
    ring.sent()


def gate_up(hn, wg, wu, dp_size):
    rows, width = hn.shape
    cols = wg.shape[1]
    tokens = GROUP * rows
    far = pl.BlockSpec(memory_space=pl.ANY)
    near = pl.BlockSpec(memory_space=pltpu.VMEM)
    return pl.pallas_call(
        functools.partial(gate_up_kernel, 2 * math.isqrt(dp_size // GROUP)),
        in_specs=[far, near, near],
        out_specs=[far] * 4,
        out_shape=[jax.ShapeDtypeStruct((tokens, width), BF16)]
        + [jax.ShapeDtypeStruct((tokens, cols), BF16)] * 3,
        scratch_shapes=[
            pltpu.VMEM((tokens, width), BF16),
            pltpu.VMEM((2, 3, rows // 2, cols), BF16),
            pltpu.SemaphoreType.DMA,
            pltpu.SemaphoreType.DMA((Ring.COPIES,)),
            pltpu.SemaphoreType.DMA((Ring.COPIES,)),
            pltpu.SemaphoreType.DMA((2, 3)),
            pltpu.SemaphoreType.DMA((2,)),
        ],
        compiler_params=pltpu.CompilerParams(
            collective_id=1, has_side_effects=True, vmem_limit_bytes=56 << 20
        ),
        cost_estimate=pl.CostEstimate(
            flops=4 * tokens * width * cols,
            bytes_accessed=tokens * (2 * width + 6 * cols) + 4 * width * cols,
            transcendentals=tokens * cols,
        ),
    )(hn, wg, wu)


FAR_CHUNK, X_CHUNK, Y_CHUNK, OWN_CHUNK = range(4)


class Reduce:
    COPIES = 10

    def __init__(self, wide, parts, cores, far, near, send_sem, recv_sem):
        self.at, self.peers = neighbours(wide)
        self.parts, self.cores, self.far, self.near = parts, cores, far, near
        self.send_sem, self.recv_sem = send_sem, recv_sem
        self.half = parts.shape[2] // 2

    @staticmethod
    def scratch(rows, cols):
        return [
            pltpu.VMEM((2, 4, rows, cols), BF16),
            pltpu.VMEM((4, rows, cols), BF16),
            pltpu.VMEM((2, rows // 2, cols), BF16),
            pltpu.VMEM((2, rows, cols), BF16),
            pltpu.SemaphoreType.DMA((Reduce.COPIES,)),
            pltpu.SemaphoreType.DMA((Reduce.COPIES,)),
        ]

    def chunk(self, step):
        slot, other = step // 2, 1 - step % 2
        row, col, core = self.at
        dy, dx = 1 - slot % 2, 1 - slot // 2
        place = 4 * ((row + dy) % 2) + 2 * ((col + dx) % 2) + (core + other) % 2
        return place, self.parts.at[other, slot]

    def copy(self, name):
        upper, lower = pl.ds(0, self.half), pl.ds(self.half, self.half)
        mine = self.parts.at[0]
        table = {
            "far0": (self.parts.at[1, FAR_CHUNK], self.cores.at[FAR_CHUNK], SIB),
            "x": (self.parts.at[1, X_CHUNK], self.cores.at[X_CHUNK], SIB),
            "y": (self.parts.at[1, Y_CHUNK], self.cores.at[Y_CHUNK], SIB),
            "own": (self.parts.at[1, OWN_CHUNK], self.cores.at[OWN_CHUNK], SIB),
            "far_x": (mine.at[FAR_CHUNK, lower], self.far.at[0], XN),
            "far_y": (mine.at[FAR_CHUNK, upper], self.far.at[1], YN),
            "x_upper": (mine.at[X_CHUNK, upper], self.near.at[0, upper], XN),
            "x_lower": (mine.at[X_CHUNK, lower], self.near.at[0, lower], XN),
            "y_upper": (mine.at[Y_CHUNK, upper], self.near.at[1, upper], YN),
            "y_lower": (mine.at[Y_CHUNK, lower], self.near.at[1, lower], YN),
        }
        src, dst, peer = table[name]
        at = list(table).index(name)
        return pltpu.make_async_remote_copy(
            src_ref=src, dst_ref=dst, send_sem=self.send_sem.at[at],
            recv_sem=self.recv_sem.at[at], device_id={"dp": self.peers[peer]},
            device_id_type=MESH,
        )

    def start(self, *names):
        for name in names:
            self.copy(name).start()

    def add(self, slot, start, other):
        count = other.shape[0] // STRIP

        @pl.loop(0, count)
        def _(at):
            here = pl.ds(pl.multiple_of(start + at * STRIP, STRIP), STRIP)
            there = pl.ds(pl.multiple_of(at * STRIP, STRIP), STRIP)
            value = self.parts[0, slot, here, :].astype(F32) + other[there, :].astype(F32)
            self.parts[0, slot, here, :] = value.astype(BF16)

    def merge_core(self, slot, name):
        self.copy(name).wait_recv()
        self.add(slot, 0, self.cores.at[slot])

    def after(self, step):
        names = ("far0", "x", "y", "own")
        for slot in range(4):
            pl.when(step == 2 * slot)(functools.partial(self.start, names[slot]))

        @pl.when(step == 1)
        def _():
            self.merge_core(FAR_CHUNK, "far0")
            self.start("far_x", "far_y")

        @pl.when(step == 3)
        def _():
            self.merge_core(X_CHUNK, "x")
            self.start("x_lower")

        @pl.when(step == 5)
        def _():
            self.merge_core(Y_CHUNK, "y")
            self.start("y_upper")

    def pass_on(self):
        self.copy("far_y").wait_recv()
        self.add(X_CHUNK, 0, self.far.at[1])
        self.start("x_upper")
        self.copy("far_x").wait_recv()
        self.add(Y_CHUNK, self.half, self.far.at[0])
        self.start("y_lower")

    def finish(self, store):
        for name in ("own", "x_upper", "x_lower", "y_upper", "y_lower"):
            self.copy(name).wait_recv()

        @pl.loop(0, 2 * self.half // STRIP)
        def _(at):
            here = pl.ds(pl.multiple_of(at * STRIP, STRIP), STRIP)
            value = self.parts[0, OWN_CHUNK, here, :].astype(F32)
            value += self.cores[OWN_CHUNK, here, :].astype(F32)
            value += self.near[0, here, :].astype(F32)
            value += self.near[1, here, :].astype(F32)
            store(here, value)

    def sent(self):
        for name in (
            "far0", "x", "y", "own", "far_x", "far_y", "x_upper", "x_lower", "y_upper", "y_lower",
        ):
            self.copy(name).wait_send()


def hidden_back_kernel(
    wide, dgate_ref, dup_ref, wg_ref, wu_ref, out_ref, loaded, load_sem, *scratch
):
    ring = Reduce(wide, *scratch)
    rows = out_ref.shape[0]

    def loads(step):
        chunk, _ = ring.chunk(step)
        here = pl.ds(pl.multiple_of(chunk * rows, rows), rows)
        return [
            pltpu.make_async_copy(
                ref.at[here], loaded.at[step % 2, at], load_sem.at[step % 2, at]
            )
            for at, ref in enumerate((dgate_ref, dup_ref))
        ]

    for copy in loads(0):
        copy.start()
    meet(ring.peers)

    @pl.loop(0, 8)
    def _(step):
        @pl.when(step < 7)
        def _():
            for copy in loads(step + 1):
                copy.start()

        for copy in loads(step):
            copy.wait()
        _, target = ring.chunk(step)
        dgate, dup = loaded[step % 2, 0], loaded[step % 2, 1]

        @pl.loop(0, out_ref.shape[1] // NTILE)
        def _(at):
            n = pl.ds(pl.multiple_of(at * NTILE, NTILE), NTILE)
            value = dot_nt(dgate, wg_ref[n, :]) + dot_nt(dup, wu_ref[n, :])
            target[:, n] = value.astype(BF16)

        ring.after(step)

    ring.pass_on()

    def store(here, value):
        out_ref[here, :] = value

    ring.finish(store)
    ring.sent()


def hidden_back(dgate, dup, wg, wu, dp_size):
    tokens, cols = dgate.shape
    width = wg.shape[0]
    rows = tokens // GROUP
    far = pl.BlockSpec(memory_space=pl.ANY)
    near = pl.BlockSpec(memory_space=pltpu.VMEM)
    return pl.pallas_call(
        functools.partial(hidden_back_kernel, 2 * math.isqrt(dp_size // GROUP)),
        in_specs=[far, far, near, near],
        out_specs=near,
        out_shape=jax.ShapeDtypeStruct((rows, width), F32),
        scratch_shapes=[
            pltpu.VMEM((2, 2, rows, cols), BF16),
            pltpu.SemaphoreType.DMA((2, 2)),
        ]
        + Reduce.scratch(rows, width),
        compiler_params=pltpu.CompilerParams(
            collective_id=6, has_side_effects=True, vmem_limit_bytes=60 << 20
        ),
        cost_estimate=pl.CostEstimate(
            flops=4 * tokens * width * cols,
            bytes_accessed=4 * tokens * cols + 4 * width * cols + 4 * rows * width,
            transcendentals=0,
        ),
    )(dgate, dup, wg, wu)


def tail_kernel(wide, z_size, mlp_count, x_ref, dq_ref, dkv_ref, gain_ref, *refs):
    mlp_ins, refs = refs[:mlp_count], refs[mlp_count:]
    wq_out, wkv_out, gain_out = refs[:3]
    mlp_outs, scratch = refs[3 : 3 + mlp_count], refs[3 + mlp_count :]
    own_scratch = scratch[:12]
    sums, zrecv, gain_z, gain_p, z_send, z_recv, g_send, g_recv, m_own, m_send, m_recv = scratch[12:]
    rings = [Reduce(wide, *own_scratch[6 * at : 6 * at + 6]) for at in range(2)]
    place = lax.axis_index("tensor")
    mine, found = others(wide)
    along = along_peers(place, z_size)
    around = [device for _, device in found]
    greet(along + around)

    mlp_copies = send_home(wide, mlp_ins, mlp_outs, m_own, m_send, m_recv)
    for copy in mlp_copies:
        copy.start()

    gain_z[place] = gain_ref[...]
    gain_copies = [
        pltpu.make_async_remote_copy(
            src_ref=gain_ref, dst_ref=gain_z.at[place], send_sem=g_send.at[at],
            recv_sem=g_recv.at[at], device_id=peer, device_id_type=MESH,
        )
        for at, peer in enumerate(along)
    ]
    for copy in gain_copies:
        copy.start()

    rights = (dkv_ref, dq_ref)
    rows = sums.shape[0]
    outs = (wkv_out, wq_out)
    z_copies = []
    for index, ring in enumerate(rings):
        right = rights[index]
        cols = right.shape[1]

        @pl.loop(0, 8)
        def _(step):
            chunk, target = ring.chunk(step)
            x = x_ref[:, pl.ds(pl.multiple_of(chunk * rows, rows), rows)].T

            @pl.loop(0, cols // NTILE)
            def _(at):
                n = pl.ds(pl.multiple_of(at * NTILE, NTILE), NTILE)
                target[:, n] = dot_nn(x, right[:, n]).astype(BF16)

            ring.after(step)

        if index == 0:
            for copy in gain_copies:
                copy.wait_recv()
            total = gain_z[0]
            for at in range(1, z_size):
                total = total + gain_z[at]
            gain_p[mine] = total
            for at, peer in enumerate(around):
                copy = pltpu.make_async_remote_copy(
                    src_ref=gain_p.at[mine], dst_ref=gain_p.at[mine],
                    send_sem=g_send.at[z_size - 1 + at], recv_sem=g_recv.at[z_size - 1 + at],
                    device_id=peer, device_id_type=MESH,
                )
                gain_copies.append(copy)
                copy.start()

    def send_along(index, ring, start):
        cols = rights[index].shape[1]
        part = cols // z_size

        def store(here, value):
            sums[here, pl.ds(start, cols)] = value.astype(BF16)

        ring.finish(store)
        for at, peer in enumerate(along):
            other = (place + at + 1) % z_size
            copy = pltpu.make_async_remote_copy(
                src_ref=sums.at[:, pl.ds(pl.multiple_of(start + other * part, LANES), part)],
                dst_ref=zrecv.at[at, :, pl.ds(start // z_size, part)],
                send_sem=z_send.at[index, at], recv_sem=z_recv.at[index, at],
                device_id=peer, device_id_type=MESH,
            )
            z_copies.append(copy)
            copy.start()

    starts = [0, rights[0].shape[1]]
    for index, ring in enumerate(rings):
        ring.pass_on()
        if index:
            send_along(index - 1, rings[index - 1], starts[index - 1])
    send_along(1, rings[1], starts[1])

    for copy in gain_copies[z_size - 1 :]:
        copy.wait_recv()
    total = gain_p[0]
    for at in range(1, GROUP):
        total = total + gain_p[at]
    gain_out[...] = total

    for copy in z_copies:
        copy.wait_recv()
    for index in range(2):
        part = rights[index].shape[1] // z_size
        own = pl.ds(pl.multiple_of(starts[index] + place * part, LANES), part)
        value = sums[:, own].astype(F32)
        for at in range(z_size - 1):
            value += zrecv[at, :, pl.ds(starts[index] // z_size, part)].astype(F32)
        outs[index][...] = value
    for copy in z_copies + gain_copies:
        copy.wait_send()
    for ring in rings:
        ring.sent()
    for copy in mlp_copies:
        copy.wait()


def last_grads(x, dq, dkv, gains, mlp, dp_size, z_size):
    tokens, width = x.shape
    rows = width // GROUP
    near = pl.BlockSpec(memory_space=pltpu.VMEM)
    far = pl.BlockSpec(memory_space=pl.ANY)
    sizes = [dkv.shape[1], dq.shape[1]]
    scratch = []
    for cols in sizes:
        scratch += Reduce.scratch(rows, cols)
    total = sum(sizes)
    return pl.pallas_call(
        functools.partial(tail_kernel, 2 * math.isqrt(dp_size // GROUP), z_size, len(mlp)),
        in_specs=[near] * 4 + [far] * len(mlp),
        out_specs=[near] * 3 + [far] * len(mlp),
        out_shape=[jax.ShapeDtypeStruct((rows, cols // z_size), F32) for cols in sizes[::-1]]
        + [jax.ShapeDtypeStruct(gains.shape, F32)]
        + home_shapes(mlp),
        scratch_shapes=scratch
        + [
            pltpu.VMEM((rows, total), BF16),
            pltpu.VMEM((z_size - 1, rows, total // z_size), BF16),
            pltpu.VMEM((z_size, *gains.shape), F32),
            pltpu.VMEM((GROUP, *gains.shape), F32),
            pltpu.SemaphoreType.DMA((2, z_size - 1)),
            pltpu.SemaphoreType.DMA((2, z_size - 1)),
            pltpu.SemaphoreType.DMA((z_size - 1 + GROUP - 1,)),
            pltpu.SemaphoreType.DMA((z_size - 1 + GROUP - 1,)),
        ]
        + home_scratch(mlp),
        compiler_params=pltpu.CompilerParams(
            collective_id=4, has_side_effects=True, vmem_limit_bytes=60 << 20
        ),
        cost_estimate=pl.CostEstimate(
            flops=2 * LONG, bytes_accessed=4 * tokens * total, transcendentals=0
        ),
    )(x, dq, dkv, gains, *mlp)


class Layout:
    def __init__(self, dp_size):
        self.blocks = dp_size // GROUP
        side = math.isqrt(self.blocks)
        self.rows, self.cols = side, self.blocks // side
        wide = 2 * self.cols

        def index(by, bx, y, x, core):
            return ((2 * by + y) * wide + 2 * bx + x) * 2 + core

        places = [(y, x, c) for y in range(2) for x in range(2) for c in range(2)]
        spots = [(by, bx) for by in range(self.rows) for bx in range(self.cols)]
        self.inner = [[index(*s, *p) for p in places] for s in spots]
        self.outer = [[index(*s, *p) for s in spots] for p in places]

    def groups(self):
        return None if self.blocks == 1 else self.inner

    def to_rows(self, array):
        if self.blocks == 1:
            return array
        rest = array.shape[1:]
        split = array.reshape(2, 2, 2, self.rows, self.cols, -1, *rest)
        order = (3, 0, 4, 1, 2, 5) + tuple(range(6, 6 + len(rest)))
        return split.transpose(order).reshape(array.shape)

    def from_rows(self, array):
        if self.blocks == 1:
            return array
        rest = array.shape[1:]
        split = array.reshape(self.rows, 2, self.cols, 2, 2, -1, *rest)
        order = (1, 3, 4, 0, 2, 5) + tuple(range(6, 6 + len(rest)))
        return split.transpose(order).reshape(array.shape)

    def from_cols(self, array):
        return array if self.blocks == 1 else self.from_rows(array.T).T

    def gather_outer(self, array):
        if self.blocks == 1:
            return array
        return lax.all_gather(array, "dp", axis_index_groups=self.outer, axis=0, tiled=True)

    def scatter_outer(self, array):
        if self.blocks == 1:
            return array
        return lax.psum_scatter(
            array, "dp", scatter_dimension=0, axis_index_groups=self.outer, tiled=True
        )

    def swap(self, array, flip):
        pairs = [
            (block[at], block[at ^ flip]) for block in self.inner for at in range(GROUP)
        ]
        return lax.ppermute(array, "dp", pairs)

    def sum_outer(self, array):
        if self.blocks == 1:
            return array
        return lax.psum(array, "dp", axis_index_groups=self.outer)

    def gather(self, array):
        return lax.all_gather(array, "dp", axis_index_groups=self.groups(), axis=0, tiled=True)

    def scatter(self, array):
        return lax.psum_scatter(
            array, "dp", scatter_dimension=0, axis_index_groups=self.groups(), tiled=True
        )


def rms_scale(values):
    return lax.rsqrt(jnp.mean(values * values, axis=-1, keepdims=True) + NORM_EPS)


def norm_back(values, scaling, gain, grad):
    gained = grad * gain
    gain_part = jnp.sum(grad * values * scaling, axis=0)
    inner = jnp.mean(gained * values, axis=-1, keepdims=True)
    return gain_part, scaling * gained - values * scaling * scaling * scaling * inner


def per_device(
    dp_size, z_size, activations, segment_ids, attn_gain, w_query, w_key, w_value, w_out,
    mlp_gain, w_gate, w_up, w_down, cotangent,
):
    layout = Layout(dp_size)
    rows, width = activations.shape[1:]
    x = activations[0].astype(F32)
    place = lax.axis_index("tensor")
    reach = -(-(MOST_DOC - 1) // rows) * rows

    def shift(array, step):
        pairs = [(at, at + step) for at in range(z_size) if 0 <= at + step < z_size]
        return lax.ppermute(array, "tensor", pairs)

    starts = document_starts(segment_ids[0])
    own_starts = lax.dynamic_slice_in_dim(starts, place * rows, rows)
    own_tokens = place * rows + jnp.arange(rows, dtype=jnp.int32)
    cosine, sine = rope_tables(own_tokens - own_starts)
    low = (own_starts - place * rows + reach)[None, :]

    shards = [
        layout.gather_outer(w)
        for w in (w_gate, w_up, w_down, jnp.concatenate([w_key, w_value], axis=1), w_query, w_out)
    ]
    spread = spread_weights(shards[:3], shards[3:], dp_size, z_size)
    wg, wu, wd = (
        layout.to_rows(lax.all_gather(w, "tensor", axis=1, tiled=True)) for w in spread[:3]
    )
    wkv, wq, wo = (layout.to_rows(w) for w in gather_rows(spread[3:], dp_size))

    def along_z(total):
        return lax.psum_scatter(
            layout.from_rows(total), "tensor", scatter_dimension=1, tiled=True
        )

    r1 = rms_scale(x)
    xn = (x * r1 * attn_gain).astype(BF16)
    q, kv = project_qkv(xn, wq, wkv, cosine, sine)
    grad, kv = lax.optimization_barrier((cotangent[0], kv))
    pieces, moved = [kv], kv
    for _ in range(reach // rows):
        moved = shift(moved, 1)
        pieces.insert(0, moved)
    kv_all = jnp.concatenate(pieces, axis=0)
    att, lse = attend(q, kv_all, low)
    h = x + dot_nt(att, wo)

    r2 = rms_scale(h)
    hn, gate, up, hidden = gate_up((h * r2 * mlp_gain).astype(BF16), wg, wu, dp_size)
    dy = layout.gather(grad)
    row, col, core = neighbours(2 * layout.cols)[0]
    by_core = hidden.reshape(GROUP // 2, 2, rows, -1)

    def out_part(of_core):
        some = lax.dynamic_index_in_dim(by_core, of_core, 1, False)
        return dot_nt(some.reshape(GROUP * rows // 2, -1), wd)

    def chunk(array, y, x):
        return lax.dynamic_index_in_dim(array, 2 * y + x, 0, False)

    away = out_part(1 - core).astype(BF16)
    dy, away = lax.optimization_barrier((dy, away))
    total_wd = dot_tn(dy, hidden).astype(BF16)
    near_sum = out_part(core) + layout.swap(away, 1).astype(F32)
    near_sum = near_sum.astype(BF16)
    dy, total_wd, near_sum = lax.optimization_barrier((dy, total_wd, near_sum))
    part_wd = along_z(total_wd)
    near_sum = near_sum.reshape(GROUP // 2, rows, width)
    far_chunk = chunk(near_sum, 1 - row, 1 - col)
    from_x = layout.swap(far_chunk[rows // 2 :], 2)
    from_y = layout.swap(far_chunk[: rows // 2], 4)
    gate, up = gate.astype(F32), up.astype(F32)
    sigma = jax.nn.sigmoid(gate)
    dhid = dot_nn(dy, wd)
    dgate = (dhid * up * sigma * (1.0 + gate * (1.0 - sigma))).astype(BF16)
    dup = (dhid * gate * sigma).astype(BF16)
    x_chunk = chunk(near_sum, row, 1 - col)
    y_chunk = chunk(near_sum, 1 - row, col)
    x_upper = (x_chunk[: rows // 2].astype(F32) + from_y.astype(F32)).astype(BF16)
    y_lower = (y_chunk[rows // 2 :].astype(F32) + from_x.astype(F32)).astype(BF16)
    x_chunk = jnp.concatenate([x_upper, x_chunk[rows // 2 :]], axis=0)
    y_chunk = jnp.concatenate([y_chunk[: rows // 2], y_lower], axis=0)
    dgate, dup, x_chunk, y_chunk = lax.optimization_barrier((dgate, dup, x_chunk, y_chunk))
    from_x, from_y = layout.swap(x_chunk, 2), layout.swap(y_chunk, 4)
    total_wg = dot_tn(hn, dgate).astype(BF16)
    dup, total_wg = lax.optimization_barrier((dup, total_wg))
    part_wg = along_z(total_wg)
    total_wu = dot_tn(hn, dup).astype(BF16)
    dup, total_wu = lax.optimization_barrier((dup, total_wu))
    part_wu = along_z(total_wu)
    dup, from_x, from_y = lax.optimization_barrier((dup, from_x, from_y))
    dhn = hidden_back(dgate, dup, wg, wu, dp_size)
    dhn, part_wd = lax.optimization_barrier((dhn, part_wd))
    gain_two, dh_norm = norm_back(h, r2, mlp_gain, dhn)
    dh = cotangent[0].astype(F32) + dh_norm
    output = h + chunk(near_sum, row, col).astype(F32)
    output = output + from_x.astype(F32) + from_y.astype(F32)

    dhb = dh.astype(BF16)
    datt = dot_nn(dhb, wo).astype(BF16)
    datt, part_wg = lax.optimization_barrier((datt, part_wg))
    dq, dkv, wo_grad, wd_grad, wg_grad = attend_back(
        q, datt, att, kv_all, lse, low, cosine, sine, layout.from_cols(dhb),
        (part_wd, part_wg), dp_size, z_size,
    )
    dq, part_wu = lax.optimization_barrier((dq, part_wu))
    dxn = dot_nt(dq, wq) + dot_nt(dkv, wkv)
    gain_one, dx_norm = norm_back(x, r1, attn_gain, dxn)
    input_grad = (dh + dx_norm).astype(BF16)
    gains = layout.sum_outer(jnp.stack([gain_one, gain_two]))
    wq_grad, wkv_grad, gains, wu_grad = last_grads(
        layout.from_cols(xn), dq, dkv, gains, (part_wu,), dp_size, z_size
    )
    wo_grad, wq_grad, wkv_grad, wd_grad, wg_grad, wu_grad = (
        layout.scatter_outer(grad).astype(F32)
        for grad in (wo_grad, wq_grad, wkv_grad, wd_grad, wg_grad, wu_grad)
    )
    key_cols = w_key.shape[1]
    return (
        output.astype(BF16)[None],
        input_grad[None],
        gains[0],
        wq_grad,
        wkv_grad[:, :key_cols],
        wkv_grad[:, key_cols:],
        wo_grad,
        gains[1],
        wg_grad,
        wu_grad,
        wd_grad,
    )


def solution(mesh):
    split = P("dp", "tensor")
    tokens = P("dp", "tensor", None)
    in_specs = (
        tokens, P("dp", None), P(), split, split, split, split, P(), split, split, split, tokens,
    )
    out_specs = (tokens, tokens, P(), split, split, split, split, P(), split, split, split)
    return jax.shard_map(
        functools.partial(per_device, mesh.shape["dp"], mesh.shape["tensor"]),
        mesh=mesh, in_specs=in_specs, out_specs=out_specs, check_vma=False,
    )
```

```python
import functools
import math

import jax
import jax.numpy as jnp
from jax import lax
from jax.experimental import pallas as pl
from jax.experimental.pallas import tpu as pltpu
from jax.sharding import PartitionSpec as P

HEAD_DIM = 64
DOCS = 4
MOST_DOC = 1024
NORM_EPS = 1e-05
ROPE_THETA = 500000.0
GROUP = 8
LANES = 128
QTILE = 256
SCALE = HEAD_DIM ** (-0.5)
LOG2E = 1.4426950408889634
FAR = -1e30
NTILE = 512
STRIP = 16
LONG = 60_000_000_000
SHORT = 1_000_000

F32 = jnp.float32
BF16 = jnp.bfloat16


def dot_nn(left, right):
    return lax.dot_general(left, right, (((1,), (0,)), ((), ())), preferred_element_type=F32)


def dot_nt(left, right):
    return lax.dot_general(left, right, (((1,), (1,)), ((), ())), preferred_element_type=F32)


def dot_tn(left, right):
    return lax.dot_general(left, right, (((0,), (0,)), ((), ())), preferred_element_type=F32)


def document_starts(segments):
    doc_ids = jnp.arange(DOCS, dtype=jnp.int32)
    counts = jnp.sum((segments[:, None] == doc_ids).astype(jnp.int32), axis=0)
    before = (doc_ids < segments[:, None]).astype(jnp.int32)
    return jnp.sum(before * counts[None, :], axis=-1)


def rope_tables(positions):
    half = HEAD_DIM // 2
    frequency = jnp.exp(
        jnp.arange(half, dtype=F32) * (-2.0 * math.log(ROPE_THETA) / HEAD_DIM)
    )
    angles = positions.astype(F32)[:, None] * frequency
    cosine, sine = jnp.cos(angles), jnp.sin(angles)
    wide_cos = jnp.concatenate([cosine] * 4, axis=1)
    wide_sin = jnp.concatenate([-sine, sine, -sine, sine], axis=1)
    return wide_cos, wide_sin


def swap_halves(values):
    lane = lax.broadcasted_iota(jnp.int32, values.shape, 1)
    ahead = pltpu.roll(values, LANES - 32, 1)
    behind = pltpu.roll(values, 32, 1)
    return jnp.where((lane % 64) < 32, ahead, behind)


def fill_bias(bias_ref, low_ref, reach):
    span = bias_ref.shape[1]
    for tile in range(bias_ref.shape[0]):
        row = lax.broadcasted_iota(jnp.int32, (span, QTILE), 0)
        col = lax.broadcasted_iota(jnp.int32, (span, QTILE), 1)
        low = low_ref[0:1, tile * QTILE : (tile + 1) * QTILE]
        allowed = (row <= reach + col) & (row + tile * QTILE >= low)
        bias_ref[tile] = jnp.where(allowed, 0.0, FAR)


def spread_pair(pair, half):
    wide = pair.astype(F32)
    turned = pltpu.roll(wide, 64, 1)
    lane = lax.broadcasted_iota(jnp.int32, wide.shape, 1)
    mine = (lane // 64) == half
    even = half == 0
    first = jnp.where(mine, jnp.where(even, wide, turned), 0.0)
    second = jnp.where(mine, jnp.where(even, turned, wide), 0.0)
    return jnp.concatenate([first, second], axis=0).astype(BF16)


def gather_pair(transposed, half):
    count = transposed.shape[1] // 2
    mine = jnp.where(half == 0, transposed[:64], transposed[64:])
    return jnp.concatenate([mine[:, :count], mine[:, count:]], axis=0).T


def attend_kernel(reach, q_ref, k_ref, v_ref, low_ref, att_ref, lse_ref, bias_ref):
    head, tile, pair = pl.program_id(0), pl.program_id(1), pl.program_id(2)
    half = head % 2

    @pl.when((head == 0) & (tile == 0) & (pair == 0))
    def _():
        fill_bias(bias_ref, low_ref, reach)

    keys = pl.ds(pl.multiple_of(tile * QTILE, QTILE), bias_ref.shape[1])
    queries = spread_pair(q_ref[...], half)
    bias = bias_ref[tile]
    score = dot_nt(k_ref[keys, :], queries)
    score = score + jnp.concatenate([bias, bias], axis=1)
    top = jnp.max(score, axis=0, keepdims=True) * (SCALE * LOG2E)
    weight = jnp.exp2(score * (SCALE * LOG2E) - top)
    total = jnp.sum(weight, axis=0, keepdims=True)
    result = dot_tn(v_ref[keys, :], weight.astype(BF16)) / total
    att_ref[...] = gather_pair(result, half).astype(BF16)
    lse_ref[0] = top + jnp.log2(total)


def attend(q, kv, low):
    rows, width = q.shape
    keys = kv.shape[0]
    reach = keys - rows
    tiles = rows // QTILE
    pairs = width // LANES
    heads = kv.shape[1] // LANES
    per_head = pairs // heads
    span = reach + QTILE
    return pl.pallas_call(
        functools.partial(attend_kernel, reach),
        grid=(heads, tiles, per_head),
        in_specs=[
            pl.BlockSpec((QTILE, LANES), lambda a, t, p: (t, a * per_head + p)),
            pl.BlockSpec((keys, LANES), lambda a, t, p: (0, 2 * (a // 2))),
            pl.BlockSpec((keys, LANES), lambda a, t, p: (0, 2 * (a // 2) + 1)),
            pl.BlockSpec((1, rows), lambda a, t, p: (0, 0)),
        ],
        out_specs=[
            pl.BlockSpec((QTILE, LANES), lambda a, t, p: (t, a * per_head + p)),
            pl.BlockSpec((1, 1, 2 * QTILE), lambda a, t, p: ((a * tiles + t) * per_head + p, 0, 0)),
        ],
        out_shape=[
            jax.ShapeDtypeStruct((rows, width), BF16),
            jax.ShapeDtypeStruct((pairs * tiles, 1, 2 * QTILE), F32),
        ],
        scratch_shapes=[pltpu.VMEM((tiles, span, QTILE), F32)],
        compiler_params=pltpu.CompilerParams(vmem_limit_bytes=48 << 20),
        cost_estimate=pl.CostEstimate(
            flops=16 * rows * span * LANES * pairs,
            bytes_accessed=4 * rows * width + 2 * keys * kv.shape[1],
            transcendentals=2 * rows * span * pairs,
        ),
    )(q, kv, kv, low)


def attend_back_kernel(
    reach, wide, z_size, mlp_count,
    q_ref, do_ref, o_ref, k_ref, v_ref, lse_ref, low_ref, cos_ref, sin_ref, cos_all, sin_all,
    h_ref, att_ref, *refs,
):
    mlp_ins, refs = refs[:mlp_count], refs[mlp_count:]
    dq_ref, dkv_ref, wo_out = refs[:3]
    mlp_outs, refs = refs[3 : 3 + mlp_count], refs[3 + mlp_count :]
    bias_ref, dk_acc, dv_acc, own_part, send_part, recv_part, kv_send, kv_recv = refs[:8]
    ring = Reduce(wide, *refs[8:14])
    sums, zrecv, z_send, z_recv = refs[14:18]
    home = refs[18:]
    block, half, tile, pair = (pl.program_id(at) for at in range(4))
    steps = pl.num_programs(1) * pl.num_programs(2) * pl.num_programs(3)
    inner = (half * pl.num_programs(2) + tile) * pl.num_programs(3) + pair
    step = block * steps + inner
    blocks = own_part.shape[0]
    rows = own_part.shape[1]
    count = reach // rows
    place = lax.axis_index("tensor")

    def exchange(at, distance):
        return pltpu.make_async_remote_copy(
            src_ref=send_part.at[at, pl.ds((count - distance) * rows, rows)],
            dst_ref=recv_part.at[at, distance - 1],
            send_sem=kv_send.at[at, distance - 1], recv_sem=kv_recv.at[at, distance - 1],
            device_id={"tensor": (place + z_size - distance) % z_size}, device_id_type=MESH,
        )

    def each_exchange(at, condition, action):
        for distance in range(1, count + 1):
            pl.when(condition(distance))(
                functools.partial(action, exchange(at, distance), at, distance)
            )

    def along(at):
        cols = wo_out.shape[1]
        other = (place + at + 1) % z_size
        return pltpu.make_async_remote_copy(
            src_ref=sums.at[:, pl.ds(pl.multiple_of(other * cols, LANES), cols)],
            dst_ref=zrecv.at[at], send_sem=z_send.at[at], recv_sem=z_recv.at[at],
            device_id={"tensor": other}, device_id_type=MESH,
        )

    @pl.when(step == 0)
    def _():
        greet(along_peers(place, z_size) + [device for _, device in others(wide)[1]])
        for copy in send_home(wide, mlp_ins, mlp_outs, *home):
            copy.start()
        fill_bias(bias_ref, low_ref, reach)

    @pl.when((step % 2 == 0) & (step < 16))
    def _():
        chunk, target = ring.chunk(step // 2)
        part = target.shape[0]
        x = h_ref[:, pl.ds(pl.multiple_of(chunk * part, part), part)].T

        @pl.loop(0, att_ref.shape[1] // NTILE)
        def _(at):
            n = pl.ds(pl.multiple_of(at * NTILE, NTILE), NTILE)
            target[:, n] = dot_nn(x, att_ref[:, n]).astype(BF16)

        ring.after(step // 2)

    pl.when(step == 19)(ring.pass_on)

    @pl.when(step == 27)
    def _():
        def store(here, value):
            sums[here, :] = value.astype(BF16)

        ring.finish(store)
        for at in range(z_size - 1):
            along(at).start()

    @pl.when(inner == 0)
    def _():
        dk_acc[...] = jnp.zeros_like(dk_acc)
        dv_acc[...] = jnp.zeros_like(dv_acc)

    keys = pl.ds(pl.multiple_of(tile * QTILE, QTILE), bias_ref.shape[1])
    queries = spread_pair(q_ref[...], half)
    grads = spread_pair(do_ref[...], half)
    product = (do_ref[...].astype(F32) * o_ref[...].astype(F32)).T
    row_dot = jnp.concatenate(
        [
            jnp.sum(product[:64], axis=0, keepdims=True),
            jnp.sum(product[64:], axis=0, keepdims=True),
        ],
        axis=1,
    )
    bias = bias_ref[tile]
    key, value = k_ref[keys, :], v_ref[keys, :]
    score = dot_nt(key, queries) + jnp.concatenate([bias, bias], axis=1)
    weight = jnp.exp2(score * (SCALE * LOG2E) - lse_ref[0])
    dv_acc[keys, :] += dot_nn(weight.astype(BF16), grads)
    dscore = (weight * (dot_nt(value, grads) - row_dot)).astype(BF16)
    dk_acc[keys, :] += dot_nn(dscore, queries)
    dq = gather_pair(dot_tn(key, dscore), half) * SCALE
    dq_ref[...] = (dq * cos_ref[...] - swap_halves(dq) * sin_ref[...]).astype(BF16)

    @pl.when(inner == steps - 1)
    def _():
        send_part[block, :, :LANES] = (dk_acc[:reach] * SCALE).astype(BF16)
        send_part[block, :, LANES:] = dv_acc[:reach].astype(BF16)
        own_part[block, :, :LANES] = dk_acc[reach:] * SCALE
        own_part[block, :, LANES:] = dv_acc[reach:]
        each_exchange(block, lambda distance: place >= distance, lambda copy, *_: copy.start())

    @pl.when(step == blocks * steps - 1)
    def _():
        def collect(copy, at, distance):
            copy.wait_recv()
            own_part[at] += recv_part[at, distance - 1].astype(F32)

        for at in range(blocks):
            each_exchange(at, lambda distance: place + distance < z_size, collect)
            dkey = own_part[at, :, :LANES]
            dkey = dkey * cos_all[...] - swap_halves(dkey) * sin_all[...]
            dkv_ref[:, 2 * at * LANES : (2 * at + 1) * LANES] = dkey.astype(BF16)
            dkv_ref[:, (2 * at + 1) * LANES : (2 * at + 2) * LANES] = own_part[
                at, :, LANES:
            ].astype(BF16)
        total = sums[:, pl.ds(pl.multiple_of(place * wo_out.shape[1], LANES), wo_out.shape[1])]
        total = total.astype(F32)
        for at in range(z_size - 1):
            along(at).wait_recv()
            total += zrecv[at].astype(F32)
        wo_out[...] = total
        for at in range(z_size - 1):
            along(at).wait_send()
        for at in range(blocks):
            each_exchange(
                at, lambda distance: place >= distance, lambda copy, *_: copy.wait_send()
            )
        ring.sent()
        for copy in send_home(wide, mlp_ins, mlp_outs, *home):
            copy.wait()


def attend_back(q, do, att, kv, lse, low, cosine, sine, h, mlp, dp_size, z_size):
    rows, width = q.shape
    keys = kv.shape[0]
    reach = keys - rows
    tiles = rows // QTILE
    pairs = width // LANES
    heads = kv.shape[1] // LANES
    per_head = pairs // heads
    span = reach + QTILE
    blocks = heads // 2
    part = h.shape[1] // GROUP
    cols = width // z_size

    def pair_at(g, h, t, p):
        return (t, (2 * g + h) * per_head + p)

    def whole(shape):
        return pl.BlockSpec(shape, lambda g, h, t, p: (0, 0), pipeline_mode=pl.Buffered(1))

    table = pl.BlockSpec((QTILE, LANES), lambda g, h, t, p: (t, 0))
    return pl.pallas_call(
        functools.partial(
            attend_back_kernel, reach, 2 * math.isqrt(dp_size // GROUP), z_size, len(mlp)
        ),
        grid=(blocks, 2, tiles, per_head),
        in_specs=[
            pl.BlockSpec((QTILE, LANES), pair_at),
            pl.BlockSpec((QTILE, LANES), pair_at),
            pl.BlockSpec((QTILE, LANES), pair_at),
            pl.BlockSpec((keys, LANES), lambda g, h, t, p: (0, 2 * g)),
            pl.BlockSpec((keys, LANES), lambda g, h, t, p: (0, 2 * g + 1)),
            pl.BlockSpec(
                (1, 1, 2 * QTILE),
                lambda g, h, t, p: (((2 * g + h) * tiles + t) * per_head + p, 0, 0),
            ),
            whole((1, rows)),
            table,
            table,
            whole((rows, LANES)),
            whole((rows, LANES)),
            whole(h.shape),
            whole(att.shape),
        ]
        + [pl.BlockSpec(memory_space=pl.ANY)] * len(mlp),
        out_specs=[
            pl.BlockSpec((QTILE, LANES), pair_at),
            pl.BlockSpec((rows, kv.shape[1]), lambda g, h, t, p: (0, 0)),
            pl.BlockSpec((part, cols), lambda g, h, t, p: (0, 0)),
        ]
        + [pl.BlockSpec(memory_space=pl.ANY)] * len(mlp),
        out_shape=[
            jax.ShapeDtypeStruct((rows, width), BF16),
            jax.ShapeDtypeStruct((rows, kv.shape[1]), BF16),
            jax.ShapeDtypeStruct((part, cols), F32),
        ]
        + home_shapes(mlp),
        scratch_shapes=[
            pltpu.VMEM((tiles, span, QTILE), F32),
            pltpu.VMEM((keys, LANES), F32),
            pltpu.VMEM((keys, LANES), F32),
            pltpu.VMEM((blocks, rows, 2 * LANES), F32),
            pltpu.VMEM((blocks, reach, 2 * LANES), BF16),
            pltpu.VMEM((blocks, reach // rows, rows, 2 * LANES), BF16),
            pltpu.SemaphoreType.DMA((blocks, reach // rows)),
            pltpu.SemaphoreType.DMA((blocks, reach // rows)),
        ]
        + Reduce.scratch(part, width)
        + [
            pltpu.VMEM((part, width), BF16),
            pltpu.VMEM((z_size - 1, part, cols), BF16),
            pltpu.SemaphoreType.DMA((z_size - 1,)),
            pltpu.SemaphoreType.DMA((z_size - 1,)),
        ]
        + home_scratch(mlp),
        compiler_params=pltpu.CompilerParams(
            collective_id=5, has_side_effects=True, vmem_limit_bytes=60 << 20
        ),
        cost_estimate=pl.CostEstimate(
            flops=40 * rows * span * LANES * pairs,
            bytes_accessed=8 * rows * width + 4 * keys * kv.shape[1],
            transcendentals=2 * rows * span * pairs,
        ),
    )(q, do, att, kv, kv, lse, low, cosine, sine, cosine, sine, h, att, *mlp)


MESH = pl.DeviceIdType.MESH


def neighbours(wide):
    dp = lax.axis_index("dp")
    core, col, row = dp % 2, (dp // 2) % 2, (dp // (2 * wide)) % 2
    sibling = dp + 1 - 2 * core
    beside = dp + 2 - 4 * col
    above = dp + 2 * wide - 4 * wide * row
    return (row, col, core), (sibling, beside, above)


def meet(peers):
    barrier = pltpu.get_barrier_semaphore()
    for peer in peers:
        pl.semaphore_signal(barrier, inc=1, device_id={"dp": peer}, device_id_type=MESH)
    pl.semaphore_wait(barrier, len(peers))


def others(wide):
    (row, col, core), _ = neighbours(wide)
    base = lax.axis_index("dp") - (2 * wide * row + 2 * col + core)
    found = []
    for flip in range(1, GROUP):
        y, x, c = (row + flip // 4) % 2, (col + flip // 2) % 2, (core + flip) % 2
        found.append((4 * y + 2 * x + c, {"dp": base + 2 * wide * y + 2 * x + c}))
    return 4 * row + 2 * col + core, found


def along_peers(place, z_size):
    return [{"tensor": (place + step) % z_size} for step in range(1, z_size)]


def greet(peers):
    barrier = pltpu.get_barrier_semaphore()
    for peer in peers:
        pl.semaphore_signal(barrier, inc=1, device_id=peer, device_id_type=MESH)
    pl.semaphore_wait(barrier, len(peers))


def send_home(wide, ins, outs, own_sem, send_sem, recv_sem):
    mine, found = others(wide)
    copies = []
    for at, (src, dst) in enumerate(zip(ins, outs)):
        part, cols = dst.shape[0], src.shape[1]
        here = pl.ds(pl.multiple_of(mine * cols, LANES), cols)
        for index, (other, device) in enumerate(found):
            copies.append(
                pltpu.make_async_remote_copy(
                    src_ref=src.at[pl.ds(pl.multiple_of(other * part, part), part)],
                    dst_ref=dst.at[:, here],
                    send_sem=send_sem.at[at, index], recv_sem=recv_sem.at[at, index],
                    device_id=device, device_id_type=MESH,
                )
            )
        own = src.at[pl.ds(pl.multiple_of(mine * part, part), part)]
        copies.append(pltpu.make_async_copy(own, dst.at[:, here], own_sem.at[at]))
    return copies


def home_shapes(arrays):
    return [jax.ShapeDtypeStruct((a.shape[0] // GROUP, GROUP * a.shape[1]), BF16) for a in arrays]


def home_scratch(arrays):
    count = len(arrays)
    return [
        pltpu.SemaphoreType.DMA((count,)),
        pltpu.SemaphoreType.DMA((count, GROUP - 1)),
        pltpu.SemaphoreType.DMA((count, GROUP - 1)),
    ]


SIB, XN, YN = 0, 1, 2


def spread_kernel(wide, z_size, mlp_count, *refs):
    attn_count = (len(refs) - 5) // 2 - mlp_count
    count = mlp_count + attn_count
    ins, outs = refs[:count], refs[count : 2 * count]
    own_sem, send_sem, recv_sem, z_send, z_recv = refs[2 * count :]
    place = lax.axis_index("tensor")
    mine, found = others(wide)
    greet(along_peers(place, z_size) + [device for _, device in found])

    local, copies = [], []
    for at in range(mlp_count):
        src, dst = ins[at], outs[at]
        rows, cols = src.shape[0], dst.shape[1]
        here = pl.ds(pl.multiple_of(mine * rows, rows), rows)
        for index, (other, device) in enumerate(found):
            copies.append(
                pltpu.make_async_remote_copy(
                    src_ref=src.at[:, pl.ds(pl.multiple_of(other * cols, LANES), cols)],
                    dst_ref=dst.at[here],
                    send_sem=send_sem.at[at, index], recv_sem=recv_sem.at[at, index],
                    device_id=device, device_id_type=MESH,
                )
            )
        own = src.at[:, pl.ds(pl.multiple_of(mine * cols, LANES), cols)]
        local.append(pltpu.make_async_copy(own, dst.at[here], own_sem.at[at]))

    def block(at, origin):
        cols = ins[at].shape[1]
        return outs[at].at[:, pl.ds(pl.multiple_of(origin * cols, LANES), cols)]

    def hop(at, way, step, receive=False):
        sign = 1 - 2 * way
        origin = place - sign * (step if receive else step - 1)
        slot = 2 * (step - 1) + way
        src = block(at, origin) if receive or step > 1 else ins[at]
        return pltpu.make_async_remote_copy(
            src_ref=src, dst_ref=block(at, origin),
            send_sem=z_send.at[at - mlp_count, slot], recv_sem=z_recv.at[at - mlp_count, slot],
            device_id={"tensor": (place + z_size + sign) % z_size}, device_id_type=MESH,
        )

    def sends(way, step):
        if way == 0:
            return (place + 1 < z_size) & (place >= step - 1)
        return (place >= 1) & (place + step - 1 < z_size)

    def receives(way, step):
        return place >= step if way == 0 else place + step < z_size

    for at in range(mlp_count, count):
        local.append(pltpu.make_async_copy(ins[at], block(at, place), own_sem.at[at]))
        for way in range(2):
            pl.when(sends(way, 1))(lambda: hop(at, way, 1).start())
    for copy in copies + local:
        copy.start()
    for step in range(1, z_size):
        for at in range(mlp_count, count):
            for way in range(2):

                @pl.when(receives(way, step))
                def _():
                    hop(at, way, step, True).wait_recv()

                if step + 1 < z_size:
                    pl.when(sends(way, step + 1))(lambda: hop(at, way, step + 1).start())
    for step in range(1, z_size):
        for at in range(mlp_count, count):
            for way in range(2):
                pl.when(sends(way, step))(lambda: hop(at, way, step).wait_send())
    for copy in local + copies:
        copy.wait()


def spread_weights(mlp, attn, dp_size, z_size):
    count = len(mlp) + len(attn)
    spec = pl.BlockSpec(memory_space=pl.ANY)
    out = [jax.ShapeDtypeStruct((GROUP * w.shape[0], w.shape[1] // GROUP), BF16) for w in mlp]
    out += [jax.ShapeDtypeStruct((w.shape[0], z_size * w.shape[1]), BF16) for w in attn]
    return pl.pallas_call(
        functools.partial(spread_kernel, 2 * math.isqrt(dp_size // GROUP), z_size, len(mlp)),
        in_specs=[spec] * count,
        out_specs=[spec] * count,
        out_shape=out,
        scratch_shapes=[
            pltpu.SemaphoreType.DMA((count,)),
            pltpu.SemaphoreType.DMA((len(mlp), GROUP - 1)),
            pltpu.SemaphoreType.DMA((len(mlp), GROUP - 1)),
            pltpu.SemaphoreType.DMA((len(attn), 2 * (z_size - 1))),
            pltpu.SemaphoreType.DMA((len(attn), 2 * (z_size - 1))),
        ],
        compiler_params=pltpu.CompilerParams(collective_id=2, has_side_effects=True),
        cost_estimate=pl.CostEstimate(flops=LONG, bytes_accessed=0, transcendentals=0),
    )(*mlp, *attn)


class Ring:
    FLIP = {SIB: (0, 0, 1), XN: (0, 1, 0), YN: (1, 0, 0)}
    COPIES = 14

    def __init__(self, wide, ref, rows, send_sem, recv_sem):
        (self.row, self.col, self.core), self.peers = neighbours(wide)
        self.ref, self.rows, self.part = ref, rows, rows // 2
        self.send_sem, self.recv_sem = send_sem, recv_sem
        self.sends = {}
        for half in range(2):
            self.sends["own", XN, half] = (2 + half, 0, 0, 0, half)
            self.sends["own", YN, half] = (4 + half, 0, 0, 0, half)
            self.sends["own", SIB, half] = (0 + half, 0, 0, 0, half)
        for half in range(2):
            self.sends["x", SIB, half] = (6 + half, 0, 1, 0, half)
            self.sends["y", SIB, half] = (8 + half, 1, 0, 0, half)
            self.sends["d", SIB, half] = (10 + half, 1, 1, 0, half)
        self.sends["x", YN, 0] = (12, 0, 1, 0, 0)
        self.sends["y", XN, 1] = (13, 1, 0, 0, 1)

    def place(self, dy, dx, dc, half):
        p = 4 * ((self.row + dy) % 2) + 2 * ((self.col + dx) % 2) + (self.core + dc) % 2
        return pl.ds(pl.multiple_of(p * self.rows + half * self.part, self.part), self.part)

    def mine(self):
        p = 4 * self.row + 2 * self.col + self.core
        return pl.ds(pl.multiple_of(p * self.rows, self.rows), self.rows)

    def copy(self, slot, dy, dx, dc, half, peer):
        where = self.place(dy, dx, dc, half)
        return pltpu.make_async_remote_copy(
            src_ref=self.ref.at[where], dst_ref=self.ref.at[where],
            send_sem=self.send_sem.at[slot], recv_sem=self.recv_sem.at[slot],
            device_id={"dp": self.peers[peer]}, device_id_type=MESH,
        )

    def start(self, name, peer, half):
        self.copy(*self.sends[name, peer, half], peer).start()

    def arrived(self, name, peer, half):
        slot, dy, dx, dc, half = self.sends[name, peer, half]
        fy, fx, fc = self.FLIP[peer]
        self.copy(slot, (dy + fy) % 2, (dx + fx) % 2, (dc + fc) % 2, half, peer).wait_recv()

    def start_own(self):
        for half in range(2):
            for peer in (XN, YN, SIB):
                self.start("own", peer, half)

    def first_halves(self):
        self.arrived("own", XN, 0)
        self.start("x", YN, 0)
        self.start("x", SIB, 0)
        self.arrived("own", YN, 0)
        self.start("y", SIB, 0)

    def second_halves(self):
        self.arrived("own", YN, 1)
        self.start("y", XN, 1)
        self.start("y", SIB, 1)
        self.arrived("own", XN, 1)
        self.start("x", SIB, 1)

    def far_halves(self):
        self.arrived("x", YN, 0)
        self.start("d", SIB, 0)
        self.arrived("y", XN, 1)
        self.start("d", SIB, 1)

    def from_sibling(self, name, *halves):
        for half in halves:
            self.arrived(name, SIB, half)

    def sent(self):
        for (name, peer, half), entry in self.sends.items():
            self.copy(*entry, peer).wait_send()


def project_kernel(
    wide, z_size, x_ref, cos_ref, sin_ref, wkv_ref, wq_ref, wo_ref,
    q_ref, kv_ref, wkv_out, wq_out, wo_out,
    wkv_all, wq_all, wo_all, keys, own_sem, send_sem, recv_sem, kv_send, kv_recv, out_sem,
):
    place = lax.axis_index("tensor")
    rows = x_ref.shape[0]
    count = keys.shape[0] // rows - 1
    parts = ((wkv_ref, wkv_all, wkv_out), (wq_ref, wq_all, wq_out), (wo_ref, wo_all, wo_out))
    rings = [
        Ring(wide, full, part.shape[0], send_sem.at[at], recv_sem.at[at])
        for at, (part, full, _) in enumerate(parts)
    ]
    local = [
        pltpu.make_async_copy(part, full.at[ring.mine()], own_sem.at[at])
        for at, ((part, full, _), ring) in enumerate(zip(parts, rings))
    ]
    outward = [
        pltpu.make_async_copy(full, out, out_sem.at[at])
        for at, (_, full, out) in enumerate(parts)
    ]
    for copy in local:
        copy.start()
    keys[: count * rows, :] = jnp.zeros((count * rows, keys.shape[1]), BF16)
    greet([{"dp": peer} for peer in rings[0].peers] + along_peers(place, z_size))
    for copy in local:
        copy.wait()

    def rotated(value):
        return (value * cos_ref[...] + swap_halves(value) * sin_ref[...]).astype(BF16)

    def hop(step):
        return pltpu.make_async_remote_copy(
            src_ref=keys.at[pl.ds((count - step + 1) * rows, rows)],
            dst_ref=keys.at[pl.ds((count - step) * rows, rows)],
            send_sem=kv_send.at[step - 1], recv_sem=kv_recv.at[step - 1],
            device_id={"tensor": (place + 1) % z_size}, device_id_type=MESH,
        )

    def pass_keys(step):
        if step > 1:
            pl.when(place >= step - 1)(lambda: hop(step - 1).wait_recv())
        if step <= count:
            sends = (place + 1 < z_size) & (place >= step - 1)
            pl.when(sends)(lambda: hop(step).start())

    def finish(ring):
        ring.far_halves()
        for name in ("own", "x", "y", "d"):
            ring.from_sibling(name, 0, 1)

    rings[0].start_own()
    rings[0].first_halves()
    rings[0].second_halves()
    rings[1].start_own()
    finish(rings[0])
    outward[0].start()

    @pl.loop(0, wkv_all.shape[1] // (2 * LANES))
    def _(at):
        n = pl.ds(pl.multiple_of(at * 2 * LANES, LANES), 2 * LANES)
        value = dot_nn(x_ref[...], wkv_all[:, n])
        both = jnp.concatenate([rotated(value[:, :LANES]), value[:, LANES:].astype(BF16)], axis=1)
        keys[pl.ds(count * rows, rows), n] = both

    pass_keys(1)
    rings[1].first_halves()
    rings[1].second_halves()
    rings[2].start_own()
    finish(rings[1])
    outward[1].start()

    @pl.loop(0, wq_all.shape[1] // (2 * LANES))
    def _(at):
        n = pl.ds(pl.multiple_of(at * 2 * LANES, LANES), 2 * LANES)
        value = dot_nn(x_ref[...], wq_all[:, n])
        both = [rotated(value[:, :LANES]), rotated(value[:, LANES:])]
        q_ref[:, n] = jnp.concatenate(both, axis=1)

    rings[2].first_halves()
    rings[2].second_halves()
    for step in range(2, count + 2):
        pass_keys(step)
    keys_out = pltpu.make_async_copy(keys, kv_ref, out_sem.at[3])
    keys_out.start()
    finish(rings[2])
    outward[2].start()
    for step in range(1, count + 1):
        sends = (place + 1 < z_size) & (place >= step - 1)
        pl.when(sends)(lambda: hop(step).wait_send())
    for ring in rings:
        ring.sent()
    for copy in outward + [keys_out]:
        copy.wait()


def project(x, cosine, sine, wkv, wq, wo, reach, dp_size, z_size):
    rows, width = x.shape
    far = pl.BlockSpec(memory_space=pl.ANY)
    near = pl.BlockSpec(memory_space=pltpu.VMEM)
    weights = (wkv, wq, wo)
    whole = [(GROUP * w.shape[0], w.shape[1]) for w in weights]
    keys = (reach + rows, wkv.shape[1])
    return pl.pallas_call(
        functools.partial(project_kernel, 2 * math.isqrt(dp_size // GROUP), z_size),
        in_specs=[near] * 3 + [far] * 3,
        out_specs=[near] + [far] * 4,
        out_shape=[jax.ShapeDtypeStruct((rows, wq.shape[1]), BF16)]
        + [jax.ShapeDtypeStruct(shape, BF16) for shape in [keys] + whole],
        scratch_shapes=[pltpu.VMEM(shape, BF16) for shape in whole + [keys]]
        + [
            pltpu.SemaphoreType.DMA((3,)),
            pltpu.SemaphoreType.DMA((3, Ring.COPIES)),
            pltpu.SemaphoreType.DMA((3, Ring.COPIES)),
            pltpu.SemaphoreType.DMA((reach // rows,)),
            pltpu.SemaphoreType.DMA((reach // rows,)),
            pltpu.SemaphoreType.DMA((4,)),
        ],
        compiler_params=pltpu.CompilerParams(
            collective_id=3, has_side_effects=True, vmem_limit_bytes=56 << 20
        ),
        cost_estimate=pl.CostEstimate(
            flops=2 * LONG, bytes_accessed=4 * width * sum(w.shape[1] for w in weights),
            transcendentals=0,
        ),
    )(x, cosine, sine, wkv, wq, wo)


def gate_up_kernel(
    wide, own_ref, wg_ref, wu_ref, all_ref, gate_ref, up_ref, hid_ref, core_ref,
    full, stage, own_sem, send_sem, recv_sem, out_sem, all_sem,
):
    rows = own_ref.shape[0]
    cols = gate_ref.shape[1]
    ring = Ring(wide, full, rows, send_sem, recv_sem)
    local = pltpu.make_async_copy(own_ref, full.at[ring.mine()], own_sem)
    local.start()
    meet(ring.peers)
    local.wait()
    ring.start_own()

    def out_copies(slot, places):
        where, core, chip = places
        return [
            pltpu.make_async_copy(stage.at[slot, i], ref.at[where], out_sem.at[slot, i])
            for i, ref in enumerate((gate_ref, up_ref, hid_ref))
        ] + [
            pltpu.make_async_copy(stage.at[slot, 2], core_ref.at[core, chip], out_sem.at[slot, 3]),
            pltpu.make_async_copy(full.at[where], all_ref.at[where], all_sem.at[slot]),
        ]

    def step_place(step):
        phase, i = step // 4, step % 4
        high, low = phase // 2, phase % 2
        first, last = (1 - high) * (1 - low), high * low
        middle = high + low - 2 * last
        half = (first + last) * (i % 2) + high * (1 - low)
        dx = middle * (1 - i % 2) + last
        dy = middle * (i % 2) + last
        chip = 2 * ((ring.row + dy) % 2) + (ring.col + dx) % 2
        part = rows // 2
        chip_rows = pl.ds(pl.multiple_of(chip * rows + half * part, part), part)
        return ring.place(dy, dx, i // 2, half), i // 2, chip_rows

    @pl.loop(0, 16)
    def _(step):
        pl.when(step == 2)(lambda: ring.from_sibling("own", 0, 1))
        pl.when(step == 4)(ring.first_halves)

        @pl.when(step == 6)
        def _():
            ring.from_sibling("x", 0)
            ring.from_sibling("y", 0)

        pl.when(step == 8)(ring.second_halves)

        @pl.when(step == 10)
        def _():
            ring.from_sibling("x", 1)
            ring.from_sibling("y", 1)

        pl.when(step == 12)(ring.far_halves)
        pl.when(step == 14)(lambda: ring.from_sibling("d", 0, 1))

        slot = step % 2
        places = step_place(step)

        @pl.when(step >= 2)
        def _():
            for copy in out_copies(slot, step_place(step - 2)):
                copy.wait()

        x = full[places[0], :]

        @pl.loop(0, cols // NTILE)
        def _(at):
            n = pl.ds(pl.multiple_of(at * NTILE, NTILE), NTILE)
            gate = dot_nn(x, wg_ref[:, n])
            up = dot_nn(x, wu_ref[:, n])
            stage[slot, 0, :, n] = gate.astype(BF16)
            stage[slot, 1, :, n] = up.astype(BF16)
            stage[slot, 2, :, n] = (gate * up / (1.0 + jnp.exp(-gate))).astype(BF16)

        for copy in out_copies(slot, places):
            copy.start()

    for step in (14, 15):
        for copy in out_copies(step % 2, step_place(step)):
            copy.wait()
    ring.sent()


def gate_up(hn, wg, wu, dp_size):
    rows, width = hn.shape
    cols = wg.shape[1]
    tokens = GROUP * rows
    far = pl.BlockSpec(memory_space=pl.ANY)
    near = pl.BlockSpec(memory_space=pltpu.VMEM)
    return pl.pallas_call(
        functools.partial(gate_up_kernel, 2 * math.isqrt(dp_size // GROUP)),
        in_specs=[far, near, near],
        out_specs=[far] * 5,
        out_shape=[jax.ShapeDtypeStruct((tokens, width), BF16)]
        + [jax.ShapeDtypeStruct((tokens, cols), BF16)] * 3
        + [jax.ShapeDtypeStruct((2, tokens // 2, cols), BF16)],
        scratch_shapes=[
            pltpu.VMEM((tokens, width), BF16),
            pltpu.VMEM((2, 3, rows // 2, cols), BF16),
            pltpu.SemaphoreType.DMA,
            pltpu.SemaphoreType.DMA((Ring.COPIES,)),
            pltpu.SemaphoreType.DMA((Ring.COPIES,)),
            pltpu.SemaphoreType.DMA((2, 4)),
            pltpu.SemaphoreType.DMA((2,)),
        ],
        compiler_params=pltpu.CompilerParams(
            collective_id=1, has_side_effects=True, vmem_limit_bytes=56 << 20
        ),
        cost_estimate=pl.CostEstimate(
            flops=SHORT, bytes_accessed=0, transcendentals=0
        ),
    )(hn, wg, wu)


FAR_CHUNK, X_CHUNK, Y_CHUNK, OWN_CHUNK = range(4)


class Reduce:
    COPIES = 10

    def __init__(self, wide, parts, cores, far, near, send_sem, recv_sem):
        self.at, self.peers = neighbours(wide)
        self.parts, self.cores, self.far, self.near = parts, cores, far, near
        self.send_sem, self.recv_sem = send_sem, recv_sem
        self.half = parts.shape[2] // 2

    @staticmethod
    def scratch(rows, cols):
        return [
            pltpu.VMEM((2, 4, rows, cols), BF16),
            pltpu.VMEM((4, rows, cols), BF16),
            pltpu.VMEM((2, rows // 2, cols), BF16),
            pltpu.VMEM((2, rows, cols), BF16),
            pltpu.SemaphoreType.DMA((Reduce.COPIES,)),
            pltpu.SemaphoreType.DMA((Reduce.COPIES,)),
        ]

    def chunk(self, step):
        slot, other = step // 2, 1 - step % 2
        row, col, core = self.at
        dy, dx = 1 - slot % 2, 1 - slot // 2
        place = 4 * ((row + dy) % 2) + 2 * ((col + dx) % 2) + (core + other) % 2
        return place, self.parts.at[other, slot]

    def copy(self, name):
        upper, lower = pl.ds(0, self.half), pl.ds(self.half, self.half)
        mine = self.parts.at[0]
        table = {
            "far0": (self.parts.at[1, FAR_CHUNK], self.cores.at[FAR_CHUNK], SIB),
            "x": (self.parts.at[1, X_CHUNK], self.cores.at[X_CHUNK], SIB),
            "y": (self.parts.at[1, Y_CHUNK], self.cores.at[Y_CHUNK], SIB),
            "own": (self.parts.at[1, OWN_CHUNK], self.cores.at[OWN_CHUNK], SIB),
            "far_x": (mine.at[FAR_CHUNK, lower], self.far.at[0], XN),
            "far_y": (mine.at[FAR_CHUNK, upper], self.far.at[1], YN),
            "x_upper": (mine.at[X_CHUNK, upper], self.near.at[0, upper], XN),
            "x_lower": (mine.at[X_CHUNK, lower], self.near.at[0, lower], XN),
            "y_upper": (mine.at[Y_CHUNK, upper], self.near.at[1, upper], YN),
            "y_lower": (mine.at[Y_CHUNK, lower], self.near.at[1, lower], YN),
        }
        src, dst, peer = table[name]
        at = list(table).index(name)
        return pltpu.make_async_remote_copy(
            src_ref=src, dst_ref=dst, send_sem=self.send_sem.at[at],
            recv_sem=self.recv_sem.at[at], device_id={"dp": self.peers[peer]},
            device_id_type=MESH,
        )

    def start(self, *names):
        for name in names:
            self.copy(name).start()

    def add(self, slot, start, other):
        count = other.shape[0] // STRIP

        @pl.loop(0, count)
        def _(at):
            here = pl.ds(pl.multiple_of(start + at * STRIP, STRIP), STRIP)
            there = pl.ds(pl.multiple_of(at * STRIP, STRIP), STRIP)
            value = self.parts[0, slot, here, :].astype(F32) + other[there, :].astype(F32)
            self.parts[0, slot, here, :] = value.astype(BF16)

    def merge_core(self, slot, name):
        self.copy(name).wait_recv()
        self.add(slot, 0, self.cores.at[slot])

    def after(self, step):
        names = ("far0", "x", "y", "own")
        for slot in range(4):
            pl.when(step == 2 * slot)(functools.partial(self.start, names[slot]))

        @pl.when(step == 1)
        def _():
            self.merge_core(FAR_CHUNK, "far0")
            self.start("far_x", "far_y")

        @pl.when(step == 3)
        def _():
            self.merge_core(X_CHUNK, "x")
            self.start("x_lower")

        @pl.when(step == 5)
        def _():
            self.merge_core(Y_CHUNK, "y")
            self.start("y_upper")

    def pass_on(self):
        self.copy("far_y").wait_recv()
        self.add(X_CHUNK, 0, self.far.at[1])
        self.start("x_upper")
        self.copy("far_x").wait_recv()
        self.add(Y_CHUNK, self.half, self.far.at[0])
        self.start("y_lower")

    def finish(self, store):
        for name in ("own", "x_upper", "x_lower", "y_upper", "y_lower"):
            self.copy(name).wait_recv()

        @pl.loop(0, 2 * self.half // STRIP)
        def _(at):
            here = pl.ds(pl.multiple_of(at * STRIP, STRIP), STRIP)
            value = self.parts[0, OWN_CHUNK, here, :].astype(F32)
            value += self.cores[OWN_CHUNK, here, :].astype(F32)
            value += self.near[0, here, :].astype(F32)
            value += self.near[1, here, :].astype(F32)
            store(here, value)

    def sent(self):
        for name in (
            "far0", "x", "y", "own", "far_x", "far_y", "x_upper", "x_lower", "y_upper", "y_lower",
        ):
            self.copy(name).wait_send()


def hidden_back_kernel(
    wide, dgate_ref, dup_ref, wg_ref, wu_ref, out_ref, loaded, load_sem, *scratch
):
    ring = Reduce(wide, *scratch)
    rows = out_ref.shape[0]

    def loads(step):
        chunk, _ = ring.chunk(step)
        here = pl.ds(pl.multiple_of(chunk * rows, rows), rows)
        return [
            pltpu.make_async_copy(
                ref.at[here], loaded.at[step % 2, at], load_sem.at[step % 2, at]
            )
            for at, ref in enumerate((dgate_ref, dup_ref))
        ]

    for copy in loads(0):
        copy.start()
    meet(ring.peers)

    @pl.loop(0, 8)
    def _(step):
        @pl.when(step < 7)
        def _():
            for copy in loads(step + 1):
                copy.start()

        for copy in loads(step):
            copy.wait()
        _, target = ring.chunk(step)
        dgate, dup = loaded[step % 2, 0], loaded[step % 2, 1]

        @pl.loop(0, out_ref.shape[1] // NTILE)
        def _(at):
            n = pl.ds(pl.multiple_of(at * NTILE, NTILE), NTILE)
            value = dot_nt(dgate, wg_ref[n, :]) + dot_nt(dup, wu_ref[n, :])
            target[:, n] = value.astype(BF16)

        ring.after(step)

    ring.pass_on()

    def store(here, value):
        out_ref[here, :] = value

    ring.finish(store)
    ring.sent()


def hidden_back(dgate, dup, wg, wu, dp_size):
    tokens, cols = dgate.shape
    width = wg.shape[0]
    rows = tokens // GROUP
    far = pl.BlockSpec(memory_space=pl.ANY)
    near = pl.BlockSpec(memory_space=pltpu.VMEM)
    return pl.pallas_call(
        functools.partial(hidden_back_kernel, 2 * math.isqrt(dp_size // GROUP)),
        in_specs=[far, far, near, near],
        out_specs=near,
        out_shape=jax.ShapeDtypeStruct((rows, width), F32),
        scratch_shapes=[
            pltpu.VMEM((2, 2, rows, cols), BF16),
            pltpu.SemaphoreType.DMA((2, 2)),
        ]
        + Reduce.scratch(rows, width),
        compiler_params=pltpu.CompilerParams(
            collective_id=6, has_side_effects=True, vmem_limit_bytes=60 << 20
        ),
        cost_estimate=pl.CostEstimate(
            flops=4 * tokens * width * cols,
            bytes_accessed=4 * tokens * cols + 4 * width * cols + 4 * rows * width,
            transcendentals=0,
        ),
    )(dgate, dup, wg, wu)


def tail_kernel(wide, z_size, mlp_count, x_ref, dq_ref, dkv_ref, gain_ref, *refs):
    mlp_ins, refs = refs[:mlp_count], refs[mlp_count:]
    wq_out, wkv_out, gain_out = refs[:3]
    mlp_outs, scratch = refs[3 : 3 + mlp_count], refs[3 + mlp_count :]
    own_scratch = scratch[:12]
    sums, zrecv, gain_z, gain_p, z_send, z_recv, g_send, g_recv, m_own, m_send, m_recv = scratch[12:]
    rings = [Reduce(wide, *own_scratch[6 * at : 6 * at + 6]) for at in range(2)]
    place = lax.axis_index("tensor")
    mine, found = others(wide)
    along = along_peers(place, z_size)
    around = [device for _, device in found]
    greet(along + around)

    mlp_copies = send_home(wide, mlp_ins, mlp_outs, m_own, m_send, m_recv)
    for copy in mlp_copies:
        copy.start()

    gain_z[place] = gain_ref[...]
    gain_copies = [
        pltpu.make_async_remote_copy(
            src_ref=gain_ref, dst_ref=gain_z.at[place], send_sem=g_send.at[at],
            recv_sem=g_recv.at[at], device_id=peer, device_id_type=MESH,
        )
        for at, peer in enumerate(along)
    ]
    for copy in gain_copies:
        copy.start()

    rights = (dkv_ref, dq_ref)
    rows = sums.shape[0]
    outs = (wkv_out, wq_out)
    z_copies = []
    for index, ring in enumerate(rings):
        right = rights[index]
        cols = right.shape[1]

        @pl.loop(0, 8)
        def _(step):
            chunk, target = ring.chunk(step)
            x = x_ref[:, pl.ds(pl.multiple_of(chunk * rows, rows), rows)].T

            @pl.loop(0, cols // NTILE)
            def _(at):
                n = pl.ds(pl.multiple_of(at * NTILE, NTILE), NTILE)
                target[:, n] = dot_nn(x, right[:, n]).astype(BF16)

            ring.after(step)

        if index == 0:
            for copy in gain_copies:
                copy.wait_recv()
            total = gain_z[0]
            for at in range(1, z_size):
                total = total + gain_z[at]
            gain_p[mine] = total
            for at, peer in enumerate(around):
                copy = pltpu.make_async_remote_copy(
                    src_ref=gain_p.at[mine], dst_ref=gain_p.at[mine],
                    send_sem=g_send.at[z_size - 1 + at], recv_sem=g_recv.at[z_size - 1 + at],
                    device_id=peer, device_id_type=MESH,
                )
                gain_copies.append(copy)
                copy.start()

    def send_along(index, ring, start):
        cols = rights[index].shape[1]
        part = cols // z_size

        def store(here, value):
            sums[here, pl.ds(start, cols)] = value.astype(BF16)

        ring.finish(store)
        for at, peer in enumerate(along):
            other = (place + at + 1) % z_size
            copy = pltpu.make_async_remote_copy(
                src_ref=sums.at[:, pl.ds(pl.multiple_of(start + other * part, LANES), part)],
                dst_ref=zrecv.at[at, :, pl.ds(start // z_size, part)],
                send_sem=z_send.at[index, at], recv_sem=z_recv.at[index, at],
                device_id=peer, device_id_type=MESH,
            )
            z_copies.append(copy)
            copy.start()

    starts = [0, rights[0].shape[1]]
    for index, ring in enumerate(rings):
        ring.pass_on()
        if index:
            send_along(index - 1, rings[index - 1], starts[index - 1])
    send_along(1, rings[1], starts[1])

    for copy in gain_copies[z_size - 1 :]:
        copy.wait_recv()
    total = gain_p[0]
    for at in range(1, GROUP):
        total = total + gain_p[at]
    gain_out[...] = total

    for copy in z_copies:
        copy.wait_recv()
    for index in range(2):
        part = rights[index].shape[1] // z_size
        own = pl.ds(pl.multiple_of(starts[index] + place * part, LANES), part)
        value = sums[:, own].astype(F32)
        for at in range(z_size - 1):
            value += zrecv[at, :, pl.ds(starts[index] // z_size, part)].astype(F32)
        outs[index][...] = value
    for copy in z_copies + gain_copies:
        copy.wait_send()
    for ring in rings:
        ring.sent()
    for copy in mlp_copies:
        copy.wait()


def last_grads(x, dq, dkv, gains, mlp, dp_size, z_size):
    tokens, width = x.shape
    rows = width // GROUP
    near = pl.BlockSpec(memory_space=pltpu.VMEM)
    far = pl.BlockSpec(memory_space=pl.ANY)
    sizes = [dkv.shape[1], dq.shape[1]]
    scratch = []
    for cols in sizes:
        scratch += Reduce.scratch(rows, cols)
    total = sum(sizes)
    return pl.pallas_call(
        functools.partial(tail_kernel, 2 * math.isqrt(dp_size // GROUP), z_size, len(mlp)),
        in_specs=[near] * 4 + [far] * len(mlp),
        out_specs=[near] * 3 + [far] * len(mlp),
        out_shape=[jax.ShapeDtypeStruct((rows, cols // z_size), F32) for cols in sizes[::-1]]
        + [jax.ShapeDtypeStruct(gains.shape, F32)]
        + home_shapes(mlp),
        scratch_shapes=scratch
        + [
            pltpu.VMEM((rows, total), BF16),
            pltpu.VMEM((z_size - 1, rows, total // z_size), BF16),
            pltpu.VMEM((z_size, *gains.shape), F32),
            pltpu.VMEM((GROUP, *gains.shape), F32),
            pltpu.SemaphoreType.DMA((2, z_size - 1)),
            pltpu.SemaphoreType.DMA((2, z_size - 1)),
            pltpu.SemaphoreType.DMA((z_size - 1 + GROUP - 1,)),
            pltpu.SemaphoreType.DMA((z_size - 1 + GROUP - 1,)),
        ]
        + home_scratch(mlp),
        compiler_params=pltpu.CompilerParams(
            collective_id=4, has_side_effects=True, vmem_limit_bytes=60 << 20
        ),
        cost_estimate=pl.CostEstimate(
            flops=2 * LONG, bytes_accessed=4 * tokens * total, transcendentals=0
        ),
    )(x, dq, dkv, gains, *mlp)


class Layout:
    def __init__(self, dp_size):
        self.blocks = dp_size // GROUP
        side = math.isqrt(self.blocks)
        self.rows, self.cols = side, self.blocks // side
        wide = 2 * self.cols

        def index(by, bx, y, x, core):
            return ((2 * by + y) * wide + 2 * bx + x) * 2 + core

        places = [(y, x, c) for y in range(2) for x in range(2) for c in range(2)]
        spots = [(by, bx) for by in range(self.rows) for bx in range(self.cols)]
        self.inner = [[index(*s, *p) for p in places] for s in spots]
        self.outer = [[index(*s, *p) for s in spots] for p in places]

    def groups(self):
        return None if self.blocks == 1 else self.inner

    def to_rows(self, array):
        if self.blocks == 1:
            return array
        rest = array.shape[1:]
        split = array.reshape(2, 2, 2, self.rows, self.cols, -1, *rest)
        order = (3, 0, 4, 1, 2, 5) + tuple(range(6, 6 + len(rest)))
        return split.transpose(order).reshape(array.shape)

    def from_rows(self, array):
        if self.blocks == 1:
            return array
        rest = array.shape[1:]
        split = array.reshape(self.rows, 2, self.cols, 2, 2, -1, *rest)
        order = (1, 3, 4, 0, 2, 5) + tuple(range(6, 6 + len(rest)))
        return split.transpose(order).reshape(array.shape)

    def from_cols(self, array):
        return array if self.blocks == 1 else self.from_rows(array.T).T

    def gather_outer(self, array):
        if self.blocks == 1:
            return array
        return lax.all_gather(array, "dp", axis_index_groups=self.outer, axis=0, tiled=True)

    def scatter_outer(self, array):
        if self.blocks == 1:
            return array
        return lax.psum_scatter(
            array, "dp", scatter_dimension=0, axis_index_groups=self.outer, tiled=True
        )

    def swap(self, array, flip):
        pairs = [
            (block[at], block[at ^ flip]) for block in self.inner for at in range(GROUP)
        ]
        return lax.ppermute(array, "dp", pairs)

    def sum_outer(self, array):
        if self.blocks == 1:
            return array
        return lax.psum(array, "dp", axis_index_groups=self.outer)

    def gather(self, array):
        return lax.all_gather(array, "dp", axis_index_groups=self.groups(), axis=0, tiled=True)

    def scatter(self, array):
        return lax.psum_scatter(
            array, "dp", scatter_dimension=0, axis_index_groups=self.groups(), tiled=True
        )


def rms_scale(values):
    return lax.rsqrt(jnp.mean(values * values, axis=-1, keepdims=True) + NORM_EPS)


def norm_back(values, scaling, gain, grad):
    gained = grad * gain
    gain_part = jnp.sum(grad * values * scaling, axis=0)
    inner = jnp.mean(gained * values, axis=-1, keepdims=True)
    return gain_part, scaling * gained - values * scaling * scaling * scaling * inner


def per_device(
    dp_size, z_size, activations, segment_ids, attn_gain, w_query, w_key, w_value, w_out,
    mlp_gain, w_gate, w_up, w_down, cotangent,
):
    layout = Layout(dp_size)
    rows, width = activations.shape[1:]
    x = activations[0].astype(F32)
    place = lax.axis_index("tensor")
    reach = -(-(MOST_DOC - 1) // rows) * rows

    def shift(array, step):
        pairs = [(at, at + step) for at in range(z_size) if 0 <= at + step < z_size]
        return lax.ppermute(array, "tensor", pairs)

    starts = document_starts(segment_ids[0])
    own_starts = lax.dynamic_slice_in_dim(starts, place * rows, rows)
    own_tokens = place * rows + jnp.arange(rows, dtype=jnp.int32)
    cosine, sine = rope_tables(own_tokens - own_starts)
    low = (own_starts - place * rows + reach)[None, :]

    shards = [
        layout.gather_outer(w)
        for w in (w_gate, w_up, w_down, jnp.concatenate([w_key, w_value], axis=1), w_query, w_out)
    ]
    spread = spread_weights(shards[:3], shards[3:], dp_size, z_size)
    def gather_z(array):
        return layout.to_rows(lax.all_gather(array, "tensor", axis=1, tiled=True))

    wg, wu = gather_z(spread[0]), gather_z(spread[1])

    def along_z(total):
        return lax.psum_scatter(
            layout.from_rows(total), "tensor", scatter_dimension=1, tiled=True
        )

    r1 = rms_scale(x)
    xn = (x * r1 * attn_gain).astype(BF16)
    q, kv_all, wkv, wq, wo = project(
        layout.from_cols(xn), cosine, sine, *spread[3:], reach, dp_size, z_size
    )
    grad, q, spread_wd = lax.optimization_barrier((cotangent[0], q, spread[2]))
    wkv, wq, wo = layout.to_rows(wkv), layout.to_rows(wq), layout.to_rows(wo)
    dy = layout.gather(grad)
    att, lse = attend(q, kv_all, low)
    wd = gather_z(spread_wd)
    h = x + dot_nt(att, wo)

    r2 = rms_scale(h)
    hn, gate, up, hidden, by_core = gate_up((h * r2 * mlp_gain).astype(BF16), wg, wu, dp_size)
    row, col, core = neighbours(2 * layout.cols)[0]
    def chunk(array, y, x):
        return lax.dynamic_index_in_dim(array, 2 * y + x, 0, False)

    by_core, dy = lax.optimization_barrier((by_core, dy))
    away = dot_nt(by_core[1], wd).astype(BF16)
    dy, away = lax.optimization_barrier((dy, away))
    total_wd = dot_tn(dy, hidden).astype(BF16)
    near_sum = dot_nt(by_core[0], wd) + layout.swap(away, 1).astype(F32)
    near_sum = near_sum.astype(BF16)
    dy, total_wd, near_sum = lax.optimization_barrier((dy, total_wd, near_sum))
    part_wd = along_z(total_wd)
    near_sum = near_sum.reshape(GROUP // 2, rows, width)
    far_chunk = chunk(near_sum, 1 - row, 1 - col)
    from_x = layout.swap(far_chunk[rows // 2 :], 2)
    from_y = layout.swap(far_chunk[: rows // 2], 4)
    gate, up = gate.astype(F32), up.astype(F32)
    sigma = jax.nn.sigmoid(gate)
    dhid = dot_nn(dy, wd)
    dgate = (dhid * up * sigma * (1.0 + gate * (1.0 - sigma))).astype(BF16)
    dup = (dhid * gate * sigma).astype(BF16)
    x_chunk = chunk(near_sum, row, 1 - col)
    y_chunk = chunk(near_sum, 1 - row, col)
    x_upper = (x_chunk[: rows // 2].astype(F32) + from_y.astype(F32)).astype(BF16)
    y_lower = (y_chunk[rows // 2 :].astype(F32) + from_x.astype(F32)).astype(BF16)
    x_chunk = jnp.concatenate([x_upper, x_chunk[rows // 2 :]], axis=0)
    y_chunk = jnp.concatenate([y_chunk[: rows // 2], y_lower], axis=0)
    dgate, dup, x_chunk, y_chunk = lax.optimization_barrier((dgate, dup, x_chunk, y_chunk))
    from_x, from_y = layout.swap(x_chunk, 2), layout.swap(y_chunk, 4)
    total_wg = dot_tn(hn, dgate).astype(BF16)
    dup, total_wg = lax.optimization_barrier((dup, total_wg))
    part_wg = along_z(total_wg)
    total_wu = dot_tn(hn, dup).astype(BF16)
    dup, total_wu = lax.optimization_barrier((dup, total_wu))
    part_wu = along_z(total_wu)
    dup, from_x, from_y = lax.optimization_barrier((dup, from_x, from_y))
    dhn = hidden_back(dgate, dup, wg, wu, dp_size)
    dhn, part_wd = lax.optimization_barrier((dhn, part_wd))
    gain_two, dh_norm = norm_back(h, r2, mlp_gain, dhn)
    dh = cotangent[0].astype(F32) + dh_norm
    output = h + chunk(near_sum, row, col).astype(F32)
    output = output + from_x.astype(F32) + from_y.astype(F32)

    dhb = dh.astype(BF16)
    datt = dot_nn(dhb, wo).astype(BF16)
    datt, part_wg = lax.optimization_barrier((datt, part_wg))
    dq, dkv, wo_grad, wd_grad, wg_grad = attend_back(
        q, datt, att, kv_all, lse, low, cosine, sine, layout.from_cols(dhb),
        (part_wd, part_wg), dp_size, z_size,
    )
    dq, part_wu = lax.optimization_barrier((dq, part_wu))
    dxn = dot_nt(dq, wq) + dot_nt(dkv, wkv)
    gain_one, dx_norm = norm_back(x, r1, attn_gain, dxn)
    input_grad = (dh + dx_norm).astype(BF16)
    gains = layout.sum_outer(jnp.stack([gain_one, gain_two]))
    wq_grad, wkv_grad, gains, wu_grad = last_grads(
        layout.from_cols(xn), dq, dkv, gains, (part_wu,), dp_size, z_size
    )
    wo_grad, wq_grad, wkv_grad, wd_grad, wg_grad, wu_grad = (
        layout.scatter_outer(grad).astype(F32)
        for grad in (wo_grad, wq_grad, wkv_grad, wd_grad, wg_grad, wu_grad)
    )
    key_cols = w_key.shape[1]
    return (
        output.astype(BF16)[None],
        input_grad[None],
        gains[0],
        wq_grad,
        wkv_grad[:, :key_cols],
        wkv_grad[:, key_cols:],
        wo_grad,
        gains[1],
        wg_grad,
        wu_grad,
        wd_grad,
    )


def solution(mesh):
    split = P("dp", "tensor")
    tokens = P("dp", "tensor", None)
    in_specs = (
        tokens, P("dp", None), P(), split, split, split, split, P(), split, split, split, tokens,
    )
    out_specs = (tokens, tokens, P(), split, split, split, split, P(), split, split, split)
    return jax.shard_map(
        functools.partial(per_device, mesh.shape["dp"], mesh.shape["tensor"]),
        mesh=mesh, in_specs=in_specs, out_specs=out_specs, check_vma=False,
    )
```

```python
import functools
import math

import jax
import jax.numpy as jnp
from jax import lax
from jax.experimental import pallas as pl
from jax.experimental.pallas import tpu as pltpu
from jax.sharding import PartitionSpec as P

HEAD_DIM = 64
DOCS = 4
MOST_DOC = 1024
NORM_EPS = 1e-05
ROPE_THETA = 500000.0
GROUP = 8
LANES = 128
QTILE = 256
SCALE = HEAD_DIM ** (-0.5)
LOG2E = 1.4426950408889634
FAR = -1e30
NTILE = 512
STRIP = 16
LONG = 60_000_000_000
SHORT = 1_000_000

F32 = jnp.float32
BF16 = jnp.bfloat16


def dot_nn(left, right):
    return lax.dot_general(left, right, (((1,), (0,)), ((), ())), preferred_element_type=F32)


def dot_nt(left, right):
    return lax.dot_general(left, right, (((1,), (1,)), ((), ())), preferred_element_type=F32)


def dot_tn(left, right):
    return lax.dot_general(left, right, (((0,), (0,)), ((), ())), preferred_element_type=F32)


def document_starts(segments):
    doc_ids = jnp.arange(DOCS, dtype=jnp.int32)
    counts = jnp.sum((segments[:, None] == doc_ids).astype(jnp.int32), axis=0)
    before = (doc_ids < segments[:, None]).astype(jnp.int32)
    return jnp.sum(before * counts[None, :], axis=-1)


def rope_tables(positions):
    half = HEAD_DIM // 2
    frequency = jnp.exp(
        jnp.arange(half, dtype=F32) * (-2.0 * math.log(ROPE_THETA) / HEAD_DIM)
    )
    angles = positions.astype(F32)[:, None] * frequency
    cosine, sine = jnp.cos(angles), jnp.sin(angles)
    wide_cos = jnp.concatenate([cosine] * 4, axis=1)
    wide_sin = jnp.concatenate([-sine, sine, -sine, sine], axis=1)
    return wide_cos, wide_sin


def swap_halves(values):
    lane = lax.broadcasted_iota(jnp.int32, values.shape, 1)
    ahead = pltpu.roll(values, LANES - 32, 1)
    behind = pltpu.roll(values, 32, 1)
    return jnp.where((lane % 64) < 32, ahead, behind)


def fill_bias(bias_ref, low_ref, reach):
    span = bias_ref.shape[1]
    for tile in range(bias_ref.shape[0]):
        row = lax.broadcasted_iota(jnp.int32, (span, QTILE), 0)
        col = lax.broadcasted_iota(jnp.int32, (span, QTILE), 1)
        low = low_ref[0:1, tile * QTILE : (tile + 1) * QTILE]
        allowed = (row <= reach + col) & (row + tile * QTILE >= low)
        bias_ref[tile] = jnp.where(allowed, 0.0, FAR)


def spread_pair(pair, half):
    wide = pair.astype(F32)
    turned = pltpu.roll(wide, 64, 1)
    lane = lax.broadcasted_iota(jnp.int32, wide.shape, 1)
    mine = (lane // 64) == half
    even = half == 0
    first = jnp.where(mine, jnp.where(even, wide, turned), 0.0)
    second = jnp.where(mine, jnp.where(even, turned, wide), 0.0)
    return jnp.concatenate([first, second], axis=0).astype(BF16)


def gather_pair(transposed, half):
    count = transposed.shape[1] // 2
    mine = jnp.where(half == 0, transposed[:64], transposed[64:])
    return jnp.concatenate([mine[:, :count], mine[:, count:]], axis=0).T


def attend_kernel(
    reach, wide, q_ref, k_ref, v_ref, low_ref, own_ref, att_ref, lse_ref, all_ref,
    bias_ref, full, own_sem, send_sem, recv_sem, out_sem,
):
    head, tile, pair = pl.program_id(0), pl.program_id(1), pl.program_id(2)
    half = head % 2
    inner = pl.num_programs(1) * pl.num_programs(2)
    step = head * inner + tile * pl.num_programs(2) + pair
    ring = Ring(wide, full, own_ref.shape[0], send_sem, recv_sem)

    def outward(slot, *flips):
        where = ring.whole(*flips)
        return pltpu.make_async_copy(full.at[where], all_ref.at[where], out_sem.at[slot])

    near = [(0, 0, 0), (0, 0, 1), (0, 1, 0), (1, 0, 0)]
    rest = [(0, 1, 1), (1, 0, 1), (1, 1, 0), (1, 1, 1)]

    @pl.when(step == 0)
    def _():
        local = pltpu.make_async_copy(own_ref, full.at[ring.mine()], own_sem)
        local.start()
        meet(ring.peers)
        local.wait()
        ring.start_own()
        fill_bias(bias_ref, low_ref, reach)

    pl.when(step == 4 * inner)(ring.first_halves)

    keys = pl.ds(pl.multiple_of(tile * QTILE, QTILE), bias_ref.shape[1])
    queries = spread_pair(q_ref[...], half)
    bias = bias_ref[tile]
    score = dot_nt(k_ref[keys, :], queries)
    score = score + jnp.concatenate([bias, bias], axis=1)
    top = jnp.max(score, axis=0, keepdims=True) * (SCALE * LOG2E)
    weight = jnp.exp2(score * (SCALE * LOG2E) - top)
    total = jnp.sum(weight, axis=0, keepdims=True)
    result = dot_tn(v_ref[keys, :], weight.astype(BF16)) / total
    att_ref[...] = gather_pair(result, half).astype(BF16)
    lse_ref[0] = top + jnp.log2(total)

    @pl.when(step == pl.num_programs(0) * inner - 1)
    def _():
        ring.second_halves()
        ring.from_sibling("own", 0, 1)
        for slot, flips in enumerate(near):
            outward(slot, *flips).start()
        ring.far_halves()
        for name in ("x", "y", "d"):
            ring.from_sibling(name, 0, 1)
        for slot, flips in enumerate(rest):
            outward(4 + slot, *flips).start()
        for slot, flips in enumerate(near + rest):
            outward(slot, *flips).wait()
        ring.sent()


def attend(q, kv, low, grad, dp_size):
    rows, width = q.shape
    keys = kv.shape[0]
    reach = keys - rows
    tiles = rows // QTILE
    pairs = width // LANES
    heads = kv.shape[1] // LANES
    per_head = pairs // heads
    span = reach + QTILE
    whole = (GROUP * grad.shape[0], grad.shape[1])
    far = pl.BlockSpec(memory_space=pl.ANY)
    return pl.pallas_call(
        functools.partial(attend_kernel, reach, 2 * math.isqrt(dp_size // GROUP)),
        grid=(heads, tiles, per_head),
        in_specs=[
            pl.BlockSpec((QTILE, LANES), lambda a, t, p: (t, a * per_head + p)),
            pl.BlockSpec((keys, LANES), lambda a, t, p: (0, 2 * (a // 2))),
            pl.BlockSpec((keys, LANES), lambda a, t, p: (0, 2 * (a // 2) + 1)),
            pl.BlockSpec((1, rows), lambda a, t, p: (0, 0)),
            far,
        ],
        out_specs=[
            pl.BlockSpec((QTILE, LANES), lambda a, t, p: (t, a * per_head + p)),
            pl.BlockSpec((1, 1, 2 * QTILE), lambda a, t, p: ((a * tiles + t) * per_head + p, 0, 0)),
            far,
        ],
        out_shape=[
            jax.ShapeDtypeStruct((rows, width), BF16),
            jax.ShapeDtypeStruct((pairs * tiles, 1, 2 * QTILE), F32),
            jax.ShapeDtypeStruct(whole, BF16),
        ],
        scratch_shapes=[
            pltpu.VMEM((tiles, span, QTILE), F32),
            pltpu.VMEM(whole, BF16),
            pltpu.SemaphoreType.DMA,
            pltpu.SemaphoreType.DMA((Ring.COPIES,)),
            pltpu.SemaphoreType.DMA((Ring.COPIES,)),
            pltpu.SemaphoreType.DMA((8,)),
        ],
        compiler_params=pltpu.CompilerParams(
            collective_id=7, has_side_effects=True, vmem_limit_bytes=56 << 20
        ),
        cost_estimate=pl.CostEstimate(
            flops=16 * rows * span * LANES * pairs,
            bytes_accessed=4 * rows * width + 2 * keys * kv.shape[1],
            transcendentals=2 * rows * span * pairs,
        ),
    )(q, kv, kv, low, grad)


def attend_back_kernel(
    reach, wide, z_size, mlp_count,
    q_ref, do_ref, o_ref, k_ref, v_ref, lse_ref, low_ref, cos_ref, sin_ref, cos_all, sin_all,
    *refs,
):
    mlp_ins, refs = refs[:mlp_count], refs[mlp_count:]
    dq_ref, dkv_ref = refs[:2]
    mlp_outs, refs = refs[2 : 2 + mlp_count], refs[2 + mlp_count :]
    bias_ref, dk_acc, dv_acc, own_part, send_part, recv_part, kv_send, kv_recv = refs[:8]
    home = refs[8:]
    block, half, tile, pair = (pl.program_id(at) for at in range(4))
    steps = pl.num_programs(1) * pl.num_programs(2) * pl.num_programs(3)
    inner = (half * pl.num_programs(2) + tile) * pl.num_programs(3) + pair
    step = block * steps + inner
    blocks = own_part.shape[0]
    rows = own_part.shape[1]
    count = reach // rows
    place = lax.axis_index("tensor")

    def exchange(at, distance):
        return pltpu.make_async_remote_copy(
            src_ref=send_part.at[at, pl.ds((count - distance) * rows, rows)],
            dst_ref=recv_part.at[at, distance - 1],
            send_sem=kv_send.at[at, distance - 1], recv_sem=kv_recv.at[at, distance - 1],
            device_id={"tensor": (place + z_size - distance) % z_size}, device_id_type=MESH,
        )

    def each_exchange(at, condition, action):
        for distance in range(1, count + 1):
            pl.when(condition(distance))(
                functools.partial(action, exchange(at, distance), at, distance)
            )

    @pl.when(step == 0)
    def _():
        greet(along_peers(place, z_size) + [device for _, device in others(wide)[1]])
        for copy in send_home(wide, mlp_ins, mlp_outs, *home):
            copy.start()
        fill_bias(bias_ref, low_ref, reach)

    @pl.when(inner == 0)
    def _():
        dk_acc[...] = jnp.zeros_like(dk_acc)
        dv_acc[...] = jnp.zeros_like(dv_acc)

    keys = pl.ds(pl.multiple_of(tile * QTILE, QTILE), bias_ref.shape[1])
    queries = spread_pair(q_ref[...], half)
    grads = spread_pair(do_ref[...], half)
    product = (do_ref[...].astype(F32) * o_ref[...].astype(F32)).T
    row_dot = jnp.concatenate(
        [
            jnp.sum(product[:64], axis=0, keepdims=True),
            jnp.sum(product[64:], axis=0, keepdims=True),
        ],
        axis=1,
    )
    bias = bias_ref[tile]
    key, value = k_ref[keys, :], v_ref[keys, :]
    score = dot_nt(key, queries) + jnp.concatenate([bias, bias], axis=1)
    weight = jnp.exp2(score * (SCALE * LOG2E) - lse_ref[0])
    dv_acc[keys, :] += dot_nn(weight.astype(BF16), grads)
    dscore = (weight * (dot_nt(value, grads) - row_dot)).astype(BF16)
    dk_acc[keys, :] += dot_nn(dscore, queries)
    dq = gather_pair(dot_tn(key, dscore), half) * SCALE
    dq_ref[...] = (dq * cos_ref[...] - swap_halves(dq) * sin_ref[...]).astype(BF16)

    @pl.when(inner == steps - 1)
    def _():
        send_part[block, :, :LANES] = (dk_acc[:reach] * SCALE).astype(BF16)
        send_part[block, :, LANES:] = dv_acc[:reach].astype(BF16)
        own_part[block, :, :LANES] = dk_acc[reach:] * SCALE
        own_part[block, :, LANES:] = dv_acc[reach:]
        each_exchange(block, lambda distance: place >= distance, lambda copy, *_: copy.start())

    @pl.when(step == blocks * steps - 1)
    def _():
        def collect(copy, at, distance):
            copy.wait_recv()
            own_part[at] += recv_part[at, distance - 1].astype(F32)

        for at in range(blocks):
            each_exchange(at, lambda distance: place + distance < z_size, collect)
            dkey = own_part[at, :, :LANES]
            dkey = dkey * cos_all[...] - swap_halves(dkey) * sin_all[...]
            dkv_ref[:, 2 * at * LANES : (2 * at + 1) * LANES] = dkey.astype(BF16)
            dkv_ref[:, (2 * at + 1) * LANES : (2 * at + 2) * LANES] = own_part[
                at, :, LANES:
            ].astype(BF16)
        for at in range(blocks):
            each_exchange(
                at, lambda distance: place >= distance, lambda copy, *_: copy.wait_send()
            )
        for copy in send_home(wide, mlp_ins, mlp_outs, *home):
            copy.wait()


def attend_back(q, do, att, kv, lse, low, cosine, sine, mlp, dp_size, z_size):
    rows, width = q.shape
    keys = kv.shape[0]
    reach = keys - rows
    tiles = rows // QTILE
    pairs = width // LANES
    heads = kv.shape[1] // LANES
    per_head = pairs // heads
    span = reach + QTILE
    blocks = heads // 2

    def pair_at(g, h, t, p):
        return (t, (2 * g + h) * per_head + p)

    def whole(shape):
        return pl.BlockSpec(shape, lambda g, h, t, p: (0, 0), pipeline_mode=pl.Buffered(1))

    table = pl.BlockSpec((QTILE, LANES), lambda g, h, t, p: (t, 0))
    return pl.pallas_call(
        functools.partial(
            attend_back_kernel, reach, 2 * math.isqrt(dp_size // GROUP), z_size, len(mlp)
        ),
        grid=(blocks, 2, tiles, per_head),
        in_specs=[
            pl.BlockSpec((QTILE, LANES), pair_at),
            pl.BlockSpec((QTILE, LANES), pair_at),
            pl.BlockSpec((QTILE, LANES), pair_at),
            pl.BlockSpec((keys, LANES), lambda g, h, t, p: (0, 2 * g)),
            pl.BlockSpec((keys, LANES), lambda g, h, t, p: (0, 2 * g + 1)),
            pl.BlockSpec(
                (1, 1, 2 * QTILE),
                lambda g, h, t, p: (((2 * g + h) * tiles + t) * per_head + p, 0, 0),
            ),
            whole((1, rows)),
            table,
            table,
            whole((rows, LANES)),
            whole((rows, LANES)),
        ]
        + [pl.BlockSpec(memory_space=pl.ANY)] * len(mlp),
        out_specs=[
            pl.BlockSpec((QTILE, LANES), pair_at),
            pl.BlockSpec((rows, kv.shape[1]), lambda g, h, t, p: (0, 0)),
        ]
        + [pl.BlockSpec(memory_space=pl.ANY)] * len(mlp),
        out_shape=[
            jax.ShapeDtypeStruct((rows, width), BF16),
            jax.ShapeDtypeStruct((rows, kv.shape[1]), BF16),
        ]
        + home_shapes(mlp),
        scratch_shapes=[
            pltpu.VMEM((tiles, span, QTILE), F32),
            pltpu.VMEM((keys, LANES), F32),
            pltpu.VMEM((keys, LANES), F32),
            pltpu.VMEM((blocks, rows, 2 * LANES), F32),
            pltpu.VMEM((blocks, reach, 2 * LANES), BF16),
            pltpu.VMEM((blocks, reach // rows, rows, 2 * LANES), BF16),
            pltpu.SemaphoreType.DMA((blocks, reach // rows)),
            pltpu.SemaphoreType.DMA((blocks, reach // rows)),
        ]
        + home_scratch(mlp),
        compiler_params=pltpu.CompilerParams(
            collective_id=5, has_side_effects=True, vmem_limit_bytes=60 << 20
        ),
        cost_estimate=pl.CostEstimate(
            flops=40 * rows * span * LANES * pairs,
            bytes_accessed=8 * rows * width + 4 * keys * kv.shape[1],
            transcendentals=2 * rows * span * pairs,
        ),
    )(q, do, att, kv, kv, lse, low, cosine, sine, cosine, sine, *mlp)


MESH = pl.DeviceIdType.MESH


def neighbours(wide):
    dp = lax.axis_index("dp")
    core, col, row = dp % 2, (dp // 2) % 2, (dp // (2 * wide)) % 2
    sibling = dp + 1 - 2 * core
    beside = dp + 2 - 4 * col
    above = dp + 2 * wide - 4 * wide * row
    return (row, col, core), (sibling, beside, above)


def meet(peers):
    barrier = pltpu.get_barrier_semaphore()
    for peer in peers:
        pl.semaphore_signal(barrier, inc=1, device_id={"dp": peer}, device_id_type=MESH)
    pl.semaphore_wait(barrier, len(peers))


def others(wide):
    (row, col, core), _ = neighbours(wide)
    base = lax.axis_index("dp") - (2 * wide * row + 2 * col + core)
    found = []
    for flip in range(1, GROUP):
        y, x, c = (row + flip // 4) % 2, (col + flip // 2) % 2, (core + flip) % 2
        found.append((4 * y + 2 * x + c, {"dp": base + 2 * wide * y + 2 * x + c}))
    return 4 * row + 2 * col + core, found


def along_peers(place, z_size):
    return [{"tensor": (place + step) % z_size} for step in range(1, z_size)]


def greet(peers):
    barrier = pltpu.get_barrier_semaphore()
    for peer in peers:
        pl.semaphore_signal(barrier, inc=1, device_id=peer, device_id_type=MESH)
    pl.semaphore_wait(barrier, len(peers))


def send_home(wide, ins, outs, own_sem, send_sem, recv_sem):
    mine, found = others(wide)
    copies = []
    for at, (src, dst) in enumerate(zip(ins, outs)):
        part, cols = dst.shape[0], src.shape[1]
        here = pl.ds(pl.multiple_of(mine * cols, LANES), cols)
        for index, (other, device) in enumerate(found):
            copies.append(
                pltpu.make_async_remote_copy(
                    src_ref=src.at[pl.ds(pl.multiple_of(other * part, part), part)],
                    dst_ref=dst.at[:, here],
                    send_sem=send_sem.at[at, index], recv_sem=recv_sem.at[at, index],
                    device_id=device, device_id_type=MESH,
                )
            )
        own = src.at[pl.ds(pl.multiple_of(mine * part, part), part)]
        copies.append(pltpu.make_async_copy(own, dst.at[:, here], own_sem.at[at]))
    return copies


def home_shapes(arrays):
    return [jax.ShapeDtypeStruct((a.shape[0] // GROUP, GROUP * a.shape[1]), BF16) for a in arrays]


def home_scratch(arrays):
    count = len(arrays)
    return [
        pltpu.SemaphoreType.DMA((count,)),
        pltpu.SemaphoreType.DMA((count, GROUP - 1)),
        pltpu.SemaphoreType.DMA((count, GROUP - 1)),
    ]


SIB, XN, YN = 0, 1, 2


def spread_kernel(wide, z_size, mlp_count, *refs):
    attn_count = (len(refs) - 5) // 2 - mlp_count
    count = mlp_count + attn_count
    ins, outs = refs[:count], refs[count : 2 * count]
    own_sem, send_sem, recv_sem, z_send, z_recv = refs[2 * count :]
    place = lax.axis_index("tensor")
    mine, found = others(wide)
    greet(along_peers(place, z_size) + [device for _, device in found])

    local, copies = [], []
    for at in range(mlp_count):
        src, dst = ins[at], outs[at]
        rows, cols = src.shape[0], dst.shape[1]
        here = pl.ds(pl.multiple_of(mine * rows, rows), rows)
        for index, (other, device) in enumerate(found):
            copies.append(
                pltpu.make_async_remote_copy(
                    src_ref=src.at[:, pl.ds(pl.multiple_of(other * cols, LANES), cols)],
                    dst_ref=dst.at[here],
                    send_sem=send_sem.at[at, index], recv_sem=recv_sem.at[at, index],
                    device_id=device, device_id_type=MESH,
                )
            )
        own = src.at[:, pl.ds(pl.multiple_of(mine * cols, LANES), cols)]
        local.append(pltpu.make_async_copy(own, dst.at[here], own_sem.at[at]))

    def block(at, origin):
        cols = ins[at].shape[1]
        return outs[at].at[:, pl.ds(pl.multiple_of(origin * cols, LANES), cols)]

    def hop(at, way, step, receive=False):
        sign = 1 - 2 * way
        origin = place - sign * (step if receive else step - 1)
        slot = 2 * (step - 1) + way
        src = block(at, origin) if receive or step > 1 else ins[at]
        return pltpu.make_async_remote_copy(
            src_ref=src, dst_ref=block(at, origin),
            send_sem=z_send.at[at - mlp_count, slot], recv_sem=z_recv.at[at - mlp_count, slot],
            device_id={"tensor": (place + z_size + sign) % z_size}, device_id_type=MESH,
        )

    def sends(way, step):
        if way == 0:
            return (place + 1 < z_size) & (place >= step - 1)
        return (place >= 1) & (place + step - 1 < z_size)

    def receives(way, step):
        return place >= step if way == 0 else place + step < z_size

    for at in range(mlp_count, count):
        local.append(pltpu.make_async_copy(ins[at], block(at, place), own_sem.at[at]))
        for way in range(2):
            pl.when(sends(way, 1))(lambda: hop(at, way, 1).start())
    for copy in copies + local:
        copy.start()
    for step in range(1, z_size):
        for at in range(mlp_count, count):
            for way in range(2):

                @pl.when(receives(way, step))
                def _():
                    hop(at, way, step, True).wait_recv()

                if step + 1 < z_size:
                    pl.when(sends(way, step + 1))(lambda: hop(at, way, step + 1).start())
    for step in range(1, z_size):
        for at in range(mlp_count, count):
            for way in range(2):
                pl.when(sends(way, step))(lambda: hop(at, way, step).wait_send())
    for copy in local + copies:
        copy.wait()


def spread_weights(mlp, attn, dp_size, z_size):
    count = len(mlp) + len(attn)
    spec = pl.BlockSpec(memory_space=pl.ANY)
    out = [jax.ShapeDtypeStruct((GROUP * w.shape[0], w.shape[1] // GROUP), BF16) for w in mlp]
    out += [jax.ShapeDtypeStruct((w.shape[0], z_size * w.shape[1]), BF16) for w in attn]
    return pl.pallas_call(
        functools.partial(spread_kernel, 2 * math.isqrt(dp_size // GROUP), z_size, len(mlp)),
        in_specs=[spec] * count,
        out_specs=[spec] * count,
        out_shape=out,
        scratch_shapes=[
            pltpu.SemaphoreType.DMA((count,)),
            pltpu.SemaphoreType.DMA((len(mlp), GROUP - 1)),
            pltpu.SemaphoreType.DMA((len(mlp), GROUP - 1)),
            pltpu.SemaphoreType.DMA((len(attn), 2 * (z_size - 1))),
            pltpu.SemaphoreType.DMA((len(attn), 2 * (z_size - 1))),
        ],
        compiler_params=pltpu.CompilerParams(collective_id=2, has_side_effects=True),
        cost_estimate=pl.CostEstimate(flops=LONG, bytes_accessed=0, transcendentals=0),
    )(*mlp, *attn)


class Ring:
    FLIP = {SIB: (0, 0, 1), XN: (0, 1, 0), YN: (1, 0, 0)}
    COPIES = 14

    def __init__(self, wide, ref, rows, send_sem, recv_sem):
        (self.row, self.col, self.core), self.peers = neighbours(wide)
        self.ref, self.rows, self.part = ref, rows, rows // 2
        self.send_sem, self.recv_sem = send_sem, recv_sem
        self.sends = {}
        for half in range(2):
            self.sends["own", XN, half] = (2 + half, 0, 0, 0, half)
            self.sends["own", YN, half] = (4 + half, 0, 0, 0, half)
            self.sends["own", SIB, half] = (0 + half, 0, 0, 0, half)
        for half in range(2):
            self.sends["x", SIB, half] = (6 + half, 0, 1, 0, half)
            self.sends["y", SIB, half] = (8 + half, 1, 0, 0, half)
            self.sends["d", SIB, half] = (10 + half, 1, 1, 0, half)
        self.sends["x", YN, 0] = (12, 0, 1, 0, 0)
        self.sends["y", XN, 1] = (13, 1, 0, 0, 1)

    def place(self, dy, dx, dc, half):
        p = 4 * ((self.row + dy) % 2) + 2 * ((self.col + dx) % 2) + (self.core + dc) % 2
        return pl.ds(pl.multiple_of(p * self.rows + half * self.part, self.part), self.part)

    def mine(self):
        p = 4 * self.row + 2 * self.col + self.core
        return pl.ds(pl.multiple_of(p * self.rows, self.rows), self.rows)

    def whole(self, dy, dx, dc):
        p = 4 * ((self.row + dy) % 2) + 2 * ((self.col + dx) % 2) + (self.core + dc) % 2
        return pl.ds(pl.multiple_of(p * self.rows, self.rows), self.rows)

    def copy(self, slot, dy, dx, dc, half, peer):
        where = self.place(dy, dx, dc, half)
        return pltpu.make_async_remote_copy(
            src_ref=self.ref.at[where], dst_ref=self.ref.at[where],
            send_sem=self.send_sem.at[slot], recv_sem=self.recv_sem.at[slot],
            device_id={"dp": self.peers[peer]}, device_id_type=MESH,
        )

    def start(self, name, peer, half):
        self.copy(*self.sends[name, peer, half], peer).start()

    def arrived(self, name, peer, half):
        slot, dy, dx, dc, half = self.sends[name, peer, half]
        fy, fx, fc = self.FLIP[peer]
        self.copy(slot, (dy + fy) % 2, (dx + fx) % 2, (dc + fc) % 2, half, peer).wait_recv()

    def start_own(self):
        for half in range(2):
            for peer in (XN, YN, SIB):
                self.start("own", peer, half)

    def first_halves(self):
        self.arrived("own", XN, 0)
        self.start("x", YN, 0)
        self.start("x", SIB, 0)
        self.arrived("own", YN, 0)
        self.start("y", SIB, 0)

    def second_halves(self):
        self.arrived("own", YN, 1)
        self.start("y", XN, 1)
        self.start("y", SIB, 1)
        self.arrived("own", XN, 1)
        self.start("x", SIB, 1)

    def far_halves(self):
        self.arrived("x", YN, 0)
        self.start("d", SIB, 0)
        self.arrived("y", XN, 1)
        self.start("d", SIB, 1)

    def from_sibling(self, name, *halves):
        for half in halves:
            self.arrived(name, SIB, half)

    def sent(self):
        for (name, peer, half), entry in self.sends.items():
            self.copy(*entry, peer).wait_send()


def project_kernel(
    wide, z_size, x_ref, cos_ref, sin_ref, wkv_ref, wq_ref, wo_ref,
    q_ref, kv_ref, wkv_out, wq_out, wo_out,
    wkv_all, wq_all, wo_all, keys, own_sem, send_sem, recv_sem, kv_send, kv_recv, out_sem,
):
    place = lax.axis_index("tensor")
    rows = x_ref.shape[0]
    count = keys.shape[0] // rows - 1
    parts = ((wkv_ref, wkv_all, wkv_out), (wq_ref, wq_all, wq_out), (wo_ref, wo_all, wo_out))
    rings = [
        Ring(wide, full, part.shape[0], send_sem.at[at], recv_sem.at[at])
        for at, (part, full, _) in enumerate(parts)
    ]
    local = [
        pltpu.make_async_copy(part, full.at[ring.mine()], own_sem.at[at])
        for at, ((part, full, _), ring) in enumerate(zip(parts, rings))
    ]
    outward = [
        pltpu.make_async_copy(full, out, out_sem.at[at])
        for at, (_, full, out) in enumerate(parts)
    ]
    for copy in local:
        copy.start()
    keys[: count * rows, :] = jnp.zeros((count * rows, keys.shape[1]), BF16)
    greet([{"dp": peer} for peer in rings[0].peers] + along_peers(place, z_size))
    for copy in local:
        copy.wait()

    def rotated(value):
        return (value * cos_ref[...] + swap_halves(value) * sin_ref[...]).astype(BF16)

    def hop(step):
        return pltpu.make_async_remote_copy(
            src_ref=keys.at[pl.ds((count - step + 1) * rows, rows)],
            dst_ref=keys.at[pl.ds((count - step) * rows, rows)],
            send_sem=kv_send.at[step - 1], recv_sem=kv_recv.at[step - 1],
            device_id={"tensor": (place + 1) % z_size}, device_id_type=MESH,
        )

    def pass_keys(step):
        if step > 1:
            pl.when(place >= step - 1)(lambda: hop(step - 1).wait_recv())
        if step <= count:
            sends = (place + 1 < z_size) & (place >= step - 1)
            pl.when(sends)(lambda: hop(step).start())

    def finish(ring):
        ring.far_halves()
        for name in ("own", "x", "y", "d"):
            ring.from_sibling(name, 0, 1)

    rings[0].start_own()
    rings[0].first_halves()
    rings[0].second_halves()
    rings[1].start_own()
    finish(rings[0])
    outward[0].start()

    @pl.loop(0, wkv_all.shape[1] // (2 * LANES))
    def _(at):
        n = pl.ds(pl.multiple_of(at * 2 * LANES, LANES), 2 * LANES)
        value = dot_nn(x_ref[...], wkv_all[:, n])
        both = jnp.concatenate([rotated(value[:, :LANES]), value[:, LANES:].astype(BF16)], axis=1)
        keys[pl.ds(count * rows, rows), n] = both

    pass_keys(1)
    rings[1].first_halves()
    rings[1].second_halves()
    rings[2].start_own()
    finish(rings[1])
    outward[1].start()

    @pl.loop(0, wq_all.shape[1] // (2 * LANES))
    def _(at):
        n = pl.ds(pl.multiple_of(at * 2 * LANES, LANES), 2 * LANES)
        value = dot_nn(x_ref[...], wq_all[:, n])
        both = [rotated(value[:, :LANES]), rotated(value[:, LANES:])]
        q_ref[:, n] = jnp.concatenate(both, axis=1)

    rings[2].first_halves()
    rings[2].second_halves()
    for step in range(2, count + 2):
        pass_keys(step)
    keys_out = pltpu.make_async_copy(keys, kv_ref, out_sem.at[3])
    keys_out.start()
    finish(rings[2])
    outward[2].start()
    for step in range(1, count + 1):
        sends = (place + 1 < z_size) & (place >= step - 1)
        pl.when(sends)(lambda: hop(step).wait_send())
    for ring in rings:
        ring.sent()
    for copy in outward + [keys_out]:
        copy.wait()


def project(x, cosine, sine, wkv, wq, wo, reach, dp_size, z_size):
    rows, width = x.shape
    far = pl.BlockSpec(memory_space=pl.ANY)
    near = pl.BlockSpec(memory_space=pltpu.VMEM)
    weights = (wkv, wq, wo)
    whole = [(GROUP * w.shape[0], w.shape[1]) for w in weights]
    keys = (reach + rows, wkv.shape[1])
    return pl.pallas_call(
        functools.partial(project_kernel, 2 * math.isqrt(dp_size // GROUP), z_size),
        in_specs=[near] * 3 + [far] * 3,
        out_specs=[near] + [far] * 4,
        out_shape=[jax.ShapeDtypeStruct((rows, wq.shape[1]), BF16)]
        + [jax.ShapeDtypeStruct(shape, BF16) for shape in [keys] + whole],
        scratch_shapes=[pltpu.VMEM(shape, BF16) for shape in whole + [keys]]
        + [
            pltpu.SemaphoreType.DMA((3,)),
            pltpu.SemaphoreType.DMA((3, Ring.COPIES)),
            pltpu.SemaphoreType.DMA((3, Ring.COPIES)),
            pltpu.SemaphoreType.DMA((reach // rows,)),
            pltpu.SemaphoreType.DMA((reach // rows,)),
            pltpu.SemaphoreType.DMA((4,)),
        ],
        compiler_params=pltpu.CompilerParams(
            collective_id=3, has_side_effects=True, vmem_limit_bytes=56 << 20
        ),
        cost_estimate=pl.CostEstimate(
            flops=2 * LONG, bytes_accessed=4 * width * sum(w.shape[1] for w in weights),
            transcendentals=0,
        ),
    )(x, cosine, sine, wkv, wq, wo)


def gate_up_kernel(
    wide, own_ref, wg_ref, wu_ref, all_ref, gate_ref, up_ref, hid_ref, core_ref,
    full, stage, own_sem, send_sem, recv_sem, out_sem, all_sem,
):
    rows = own_ref.shape[0]
    cols = gate_ref.shape[1]
    ring = Ring(wide, full, rows, send_sem, recv_sem)
    local = pltpu.make_async_copy(own_ref, full.at[ring.mine()], own_sem)
    local.start()
    meet(ring.peers)
    local.wait()
    ring.start_own()

    def out_copies(slot, places):
        where, core, chip = places
        return [
            pltpu.make_async_copy(stage.at[slot, i], ref.at[where], out_sem.at[slot, i])
            for i, ref in enumerate((gate_ref, up_ref, hid_ref))
        ] + [
            pltpu.make_async_copy(stage.at[slot, 2], core_ref.at[core, chip], out_sem.at[slot, 3]),
            pltpu.make_async_copy(full.at[where], all_ref.at[where], all_sem.at[slot]),
        ]

    def step_place(step):
        phase, i = step // 4, step % 4
        high, low = phase // 2, phase % 2
        first, last = (1 - high) * (1 - low), high * low
        middle = high + low - 2 * last
        half = (first + last) * (i % 2) + high * (1 - low)
        dx = middle * (1 - i % 2) + last
        dy = middle * (i % 2) + last
        chip = 2 * ((ring.row + dy) % 2) + (ring.col + dx) % 2
        part = rows // 2
        chip_rows = pl.ds(pl.multiple_of(chip * rows + half * part, part), part)
        return ring.place(dy, dx, i // 2, half), i // 2, chip_rows

    @pl.loop(0, 16)
    def _(step):
        pl.when(step == 2)(lambda: ring.from_sibling("own", 0, 1))
        pl.when(step == 4)(ring.first_halves)

        @pl.when(step == 6)
        def _():
            ring.from_sibling("x", 0)
            ring.from_sibling("y", 0)

        pl.when(step == 8)(ring.second_halves)

        @pl.when(step == 10)
        def _():
            ring.from_sibling("x", 1)
            ring.from_sibling("y", 1)

        pl.when(step == 12)(ring.far_halves)
        pl.when(step == 14)(lambda: ring.from_sibling("d", 0, 1))

        slot = step % 2
        places = step_place(step)

        @pl.when(step >= 2)
        def _():
            for copy in out_copies(slot, step_place(step - 2)):
                copy.wait()

        x = full[places[0], :]

        @pl.loop(0, cols // NTILE)
        def _(at):
            n = pl.ds(pl.multiple_of(at * NTILE, NTILE), NTILE)
            gate = dot_nn(x, wg_ref[:, n])
            up = dot_nn(x, wu_ref[:, n])
            stage[slot, 0, :, n] = gate.astype(BF16)
            stage[slot, 1, :, n] = up.astype(BF16)
            stage[slot, 2, :, n] = (gate * up / (1.0 + jnp.exp(-gate))).astype(BF16)

        for copy in out_copies(slot, places):
            copy.start()

    for step in (14, 15):
        for copy in out_copies(step % 2, step_place(step)):
            copy.wait()
    ring.sent()


def gate_up(hn, wg, wu, dp_size):
    rows, width = hn.shape
    cols = wg.shape[1]
    tokens = GROUP * rows
    far = pl.BlockSpec(memory_space=pl.ANY)
    near = pl.BlockSpec(memory_space=pltpu.VMEM)
    return pl.pallas_call(
        functools.partial(gate_up_kernel, 2 * math.isqrt(dp_size // GROUP)),
        in_specs=[far, near, near],
        out_specs=[far] * 5,
        out_shape=[jax.ShapeDtypeStruct((tokens, width), BF16)]
        + [jax.ShapeDtypeStruct((tokens, cols), BF16)] * 3
        + [jax.ShapeDtypeStruct((2, tokens // 2, cols), BF16)],
        scratch_shapes=[
            pltpu.VMEM((tokens, width), BF16),
            pltpu.VMEM((2, 3, rows // 2, cols), BF16),
            pltpu.SemaphoreType.DMA,
            pltpu.SemaphoreType.DMA((Ring.COPIES,)),
            pltpu.SemaphoreType.DMA((Ring.COPIES,)),
            pltpu.SemaphoreType.DMA((2, 4)),
            pltpu.SemaphoreType.DMA((2,)),
        ],
        compiler_params=pltpu.CompilerParams(
            collective_id=1, has_side_effects=True, vmem_limit_bytes=56 << 20
        ),
        cost_estimate=pl.CostEstimate(
            flops=SHORT, bytes_accessed=0, transcendentals=0
        ),
    )(hn, wg, wu)


FAR_CHUNK, X_CHUNK, Y_CHUNK, OWN_CHUNK = range(4)


class Reduce:
    COPIES = 10

    def __init__(self, wide, parts, cores, far, near, send_sem, recv_sem):
        self.at, self.peers = neighbours(wide)
        self.parts, self.cores, self.far, self.near = parts, cores, far, near
        self.send_sem, self.recv_sem = send_sem, recv_sem
        self.half = parts.shape[2] // 2

    @staticmethod
    def scratch(rows, cols):
        return [
            pltpu.VMEM((2, 4, rows, cols), BF16),
            pltpu.VMEM((4, rows, cols), BF16),
            pltpu.VMEM((2, rows // 2, cols), BF16),
            pltpu.VMEM((2, rows, cols), BF16),
            pltpu.SemaphoreType.DMA((Reduce.COPIES,)),
            pltpu.SemaphoreType.DMA((Reduce.COPIES,)),
        ]

    def chunk(self, step):
        slot, other = step // 2, 1 - step % 2
        row, col, core = self.at
        dy, dx = 1 - slot % 2, 1 - slot // 2
        place = 4 * ((row + dy) % 2) + 2 * ((col + dx) % 2) + (core + other) % 2
        return place, self.parts.at[other, slot]

    def copy(self, name):
        upper, lower = pl.ds(0, self.half), pl.ds(self.half, self.half)
        mine = self.parts.at[0]
        table = {
            "far0": (self.parts.at[1, FAR_CHUNK], self.cores.at[FAR_CHUNK], SIB),
            "x": (self.parts.at[1, X_CHUNK], self.cores.at[X_CHUNK], SIB),
            "y": (self.parts.at[1, Y_CHUNK], self.cores.at[Y_CHUNK], SIB),
            "own": (self.parts.at[1, OWN_CHUNK], self.cores.at[OWN_CHUNK], SIB),
            "far_x": (mine.at[FAR_CHUNK, lower], self.far.at[0], XN),
            "far_y": (mine.at[FAR_CHUNK, upper], self.far.at[1], YN),
            "x_upper": (mine.at[X_CHUNK, upper], self.near.at[0, upper], XN),
            "x_lower": (mine.at[X_CHUNK, lower], self.near.at[0, lower], XN),
            "y_upper": (mine.at[Y_CHUNK, upper], self.near.at[1, upper], YN),
            "y_lower": (mine.at[Y_CHUNK, lower], self.near.at[1, lower], YN),
        }
        src, dst, peer = table[name]
        at = list(table).index(name)
        return pltpu.make_async_remote_copy(
            src_ref=src, dst_ref=dst, send_sem=self.send_sem.at[at],
            recv_sem=self.recv_sem.at[at], device_id={"dp": self.peers[peer]},
            device_id_type=MESH,
        )

    def start(self, *names):
        for name in names:
            self.copy(name).start()

    def add(self, slot, start, other):
        count = other.shape[0] // STRIP

        @pl.loop(0, count)
        def _(at):
            here = pl.ds(pl.multiple_of(start + at * STRIP, STRIP), STRIP)
            there = pl.ds(pl.multiple_of(at * STRIP, STRIP), STRIP)
            value = self.parts[0, slot, here, :].astype(F32) + other[there, :].astype(F32)
            self.parts[0, slot, here, :] = value.astype(BF16)

    def merge_core(self, slot, name):
        self.copy(name).wait_recv()
        self.add(slot, 0, self.cores.at[slot])

    def after(self, step):
        names = ("far0", "x", "y", "own")
        for slot in range(4):
            pl.when(step == 2 * slot)(functools.partial(self.start, names[slot]))

        @pl.when(step == 1)
        def _():
            self.merge_core(FAR_CHUNK, "far0")
            self.start("far_x", "far_y")

        @pl.when(step == 3)
        def _():
            self.merge_core(X_CHUNK, "x")
            self.start("x_lower")

        @pl.when(step == 5)
        def _():
            self.merge_core(Y_CHUNK, "y")
            self.start("y_upper")

    def pass_on(self):
        self.copy("far_y").wait_recv()
        self.add(X_CHUNK, 0, self.far.at[1])
        self.start("x_upper")
        self.copy("far_x").wait_recv()
        self.add(Y_CHUNK, self.half, self.far.at[0])
        self.start("y_lower")

    def finish(self, store):
        for name in ("own", "x_upper", "x_lower", "y_upper", "y_lower"):
            self.copy(name).wait_recv()

        @pl.loop(0, 2 * self.half // STRIP)
        def _(at):
            here = pl.ds(pl.multiple_of(at * STRIP, STRIP), STRIP)
            value = self.parts[0, OWN_CHUNK, here, :].astype(F32)
            value += self.cores[OWN_CHUNK, here, :].astype(F32)
            value += self.near[0, here, :].astype(F32)
            value += self.near[1, here, :].astype(F32)
            store(here, value)

    def sent(self):
        for name in (
            "far0", "x", "y", "own", "far_x", "far_y", "x_upper", "x_lower", "y_upper", "y_lower",
        ):
            self.copy(name).wait_send()


def hidden_back_kernel(
    wide, dgate_ref, dup_ref, wg_ref, wu_ref, out_ref, loaded, load_sem, *scratch
):
    ring = Reduce(wide, *scratch)
    rows = out_ref.shape[0]

    def loads(step):
        chunk, _ = ring.chunk(step)
        here = pl.ds(pl.multiple_of(chunk * rows, rows), rows)
        return [
            pltpu.make_async_copy(
                ref.at[here], loaded.at[step % 2, at], load_sem.at[step % 2, at]
            )
            for at, ref in enumerate((dgate_ref, dup_ref))
        ]

    for copy in loads(0):
        copy.start()
    meet(ring.peers)

    @pl.loop(0, 8)
    def _(step):
        @pl.when(step < 7)
        def _():
            for copy in loads(step + 1):
                copy.start()

        for copy in loads(step):
            copy.wait()
        _, target = ring.chunk(step)
        dgate, dup = loaded[step % 2, 0], loaded[step % 2, 1]

        @pl.loop(0, out_ref.shape[1] // NTILE)
        def _(at):
            n = pl.ds(pl.multiple_of(at * NTILE, NTILE), NTILE)
            value = dot_nt(dgate, wg_ref[n, :]) + dot_nt(dup, wu_ref[n, :])
            target[:, n] = value.astype(BF16)

        ring.after(step)

    ring.pass_on()

    def store(here, value):
        out_ref[here, :] = value

    ring.finish(store)
    ring.sent()


def hidden_back(dgate, dup, wg, wu, dp_size):
    tokens, cols = dgate.shape
    width = wg.shape[0]
    rows = tokens // GROUP
    far = pl.BlockSpec(memory_space=pl.ANY)
    near = pl.BlockSpec(memory_space=pltpu.VMEM)
    return pl.pallas_call(
        functools.partial(hidden_back_kernel, 2 * math.isqrt(dp_size // GROUP)),
        in_specs=[far, far, near, near],
        out_specs=near,
        out_shape=jax.ShapeDtypeStruct((rows, width), F32),
        scratch_shapes=[
            pltpu.VMEM((2, 2, rows, cols), BF16),
            pltpu.SemaphoreType.DMA((2, 2)),
        ]
        + Reduce.scratch(rows, width),
        compiler_params=pltpu.CompilerParams(
            collective_id=6, has_side_effects=True, vmem_limit_bytes=60 << 20
        ),
        cost_estimate=pl.CostEstimate(
            flops=4 * tokens * width * cols,
            bytes_accessed=4 * tokens * cols + 4 * width * cols + 4 * rows * width,
            transcendentals=0,
        ),
    )(dgate, dup, wg, wu)


def tail_kernel(
    wide, z_size, mlp_count, x_ref, dq_ref, dkv_ref, wo_ref, gain_ref, *refs
):
    mlp_ins, refs = refs[:mlp_count], refs[mlp_count:]
    wq_out, wkv_out, wo_out, gain_out = refs[:4]
    mlp_outs, scratch = refs[4 : 4 + mlp_count], refs[4 + mlp_count :]
    own_scratch = scratch[:12]
    sums, zrecv, gain_z, gain_p, z_send, z_recv, g_send, g_recv = scratch[12:20]
    wo_recv, w_send, w_recv, m_own, m_send, m_recv = scratch[20:]
    rings = [Reduce(wide, *own_scratch[6 * at : 6 * at + 6]) for at in range(2)]
    place = lax.axis_index("tensor")
    mine, found = others(wide)
    along = along_peers(place, z_size)
    around = [device for _, device in found]
    greet(along + around)

    mlp_copies = send_home(wide, mlp_ins, mlp_outs, m_own, m_send, m_recv)
    wo_part = wo_out.shape[1]
    wo_copies = [
        pltpu.make_async_remote_copy(
            src_ref=wo_ref.at[
                :,
                pl.ds(pl.multiple_of((place + at + 1) % z_size * wo_part, LANES), wo_part),
            ],
            dst_ref=wo_recv.at[at], send_sem=w_send.at[at], recv_sem=w_recv.at[at],
            device_id=peer, device_id_type=MESH,
        )
        for at, peer in enumerate(along)
    ]
    for copy in wo_copies:
        copy.start()

    gain_z[place] = gain_ref[...]
    gain_copies = [
        pltpu.make_async_remote_copy(
            src_ref=gain_ref, dst_ref=gain_z.at[place], send_sem=g_send.at[at],
            recv_sem=g_recv.at[at], device_id=peer, device_id_type=MESH,
        )
        for at, peer in enumerate(along)
    ]
    for copy in gain_copies:
        copy.start()

    rights = (dq_ref, dkv_ref)
    rows = sums.shape[0]
    outs = (wq_out, wkv_out)
    z_copies = []
    for index, ring in enumerate(rings):
        right = rights[index]
        cols = right.shape[1]

        @pl.loop(0, 8)
        def _(step):
            chunk, target = ring.chunk(step)
            x = x_ref[:, pl.ds(pl.multiple_of(chunk * rows, rows), rows)].T

            @pl.loop(0, cols // NTILE)
            def _(at):
                n = pl.ds(pl.multiple_of(at * NTILE, NTILE), NTILE)
                target[:, n] = dot_nn(x, right[:, n]).astype(BF16)

            ring.after(step)

        if index == 0:
            for copy in mlp_copies:
                copy.start()
            for copy in gain_copies:
                copy.wait_recv()
            total = gain_z[0]
            for at in range(1, z_size):
                total = total + gain_z[at]
            gain_p[mine] = total
            for at, peer in enumerate(around):
                copy = pltpu.make_async_remote_copy(
                    src_ref=gain_p.at[mine], dst_ref=gain_p.at[mine],
                    send_sem=g_send.at[z_size - 1 + at], recv_sem=g_recv.at[z_size - 1 + at],
                    device_id=peer, device_id_type=MESH,
                )
                gain_copies.append(copy)
                copy.start()

    def send_along(index, ring, start):
        cols = rights[index].shape[1]
        part = cols // z_size

        def store(here, value):
            sums[here, pl.ds(start, cols)] = value.astype(BF16)

        ring.finish(store)
        for at, peer in enumerate(along):
            other = (place + at + 1) % z_size
            copy = pltpu.make_async_remote_copy(
                src_ref=sums.at[:, pl.ds(pl.multiple_of(start + other * part, LANES), part)],
                dst_ref=zrecv.at[at, :, pl.ds(start // z_size, part)],
                send_sem=z_send.at[index, at], recv_sem=z_recv.at[index, at],
                device_id=peer, device_id_type=MESH,
            )
            z_copies.append(copy)
            copy.start()

    starts = [0, rights[0].shape[1]]
    for index, ring in enumerate(rings):
        ring.pass_on()
        if index:
            send_along(index - 1, rings[index - 1], starts[index - 1])
    send_along(1, rings[1], starts[1])

    for copy in gain_copies[z_size - 1 :]:
        copy.wait_recv()
    total = gain_p[0]
    for at in range(1, GROUP):
        total = total + gain_p[at]
    gain_out[...] = total

    for copy in wo_copies:
        copy.wait()
    total = wo_ref[:, pl.ds(pl.multiple_of(place * wo_part, LANES), wo_part)].astype(F32)
    for at in range(z_size - 1):
        total += wo_recv[at].astype(F32)
    wo_out[...] = total

    for copy in z_copies:
        copy.wait_recv()
    for index in range(2):
        part = rights[index].shape[1] // z_size
        own = pl.ds(pl.multiple_of(starts[index] + place * part, LANES), part)
        value = sums[:, own].astype(F32)
        for at in range(z_size - 1):
            value += zrecv[at, :, pl.ds(starts[index] // z_size, part)].astype(F32)
        outs[index][...] = value
    for copy in z_copies + gain_copies:
        copy.wait_send()
    for ring in rings:
        ring.sent()
    for copy in mlp_copies:
        copy.wait()


def last_grads(x, dq, dkv, wo_sum, gains, mlp, dp_size, z_size):
    tokens, width = x.shape
    rows = width // GROUP
    near = pl.BlockSpec(memory_space=pltpu.VMEM)
    far = pl.BlockSpec(memory_space=pl.ANY)
    sizes = [dq.shape[1], dkv.shape[1]]
    scratch = []
    for cols in sizes:
        scratch += Reduce.scratch(rows, cols)
    total = sum(sizes)
    return pl.pallas_call(
        functools.partial(tail_kernel, 2 * math.isqrt(dp_size // GROUP), z_size, len(mlp)),
        in_specs=[near] * 5 + [far] * len(mlp),
        out_specs=[near] * 4 + [far] * len(mlp),
        out_shape=[jax.ShapeDtypeStruct((rows, cols // z_size), F32) for cols in sizes]
        + [jax.ShapeDtypeStruct((rows, wo_sum.shape[1] // z_size), F32)]
        + [jax.ShapeDtypeStruct(gains.shape, F32)]
        + home_shapes(mlp),
        scratch_shapes=scratch
        + [
            pltpu.VMEM((rows, total), BF16),
            pltpu.VMEM((z_size - 1, rows, total // z_size), BF16),
            pltpu.VMEM((z_size, *gains.shape), F32),
            pltpu.VMEM((GROUP, *gains.shape), F32),
            pltpu.SemaphoreType.DMA((2, z_size - 1)),
            pltpu.SemaphoreType.DMA((2, z_size - 1)),
            pltpu.SemaphoreType.DMA((z_size - 1 + GROUP - 1,)),
            pltpu.SemaphoreType.DMA((z_size - 1 + GROUP - 1,)),
            pltpu.VMEM((z_size - 1, rows, wo_sum.shape[1] // z_size), BF16),
            pltpu.SemaphoreType.DMA((z_size - 1,)),
            pltpu.SemaphoreType.DMA((z_size - 1,)),
        ]
        + home_scratch(mlp),
        compiler_params=pltpu.CompilerParams(
            collective_id=4, has_side_effects=True, vmem_limit_bytes=60 << 20
        ),
        cost_estimate=pl.CostEstimate(
            flops=2 * LONG, bytes_accessed=4 * tokens * total, transcendentals=0
        ),
    )(x, dq, dkv, wo_sum, gains, *mlp)


class Layout:
    def __init__(self, dp_size):
        self.blocks = dp_size // GROUP
        side = math.isqrt(self.blocks)
        self.rows, self.cols = side, self.blocks // side
        wide = 2 * self.cols

        def index(by, bx, y, x, core):
            return ((2 * by + y) * wide + 2 * bx + x) * 2 + core

        places = [(y, x, c) for y in range(2) for x in range(2) for c in range(2)]
        spots = [(by, bx) for by in range(self.rows) for bx in range(self.cols)]
        self.inner = [[index(*s, *p) for p in places] for s in spots]
        self.outer = [[index(*s, *p) for s in spots] for p in places]

    def groups(self):
        return None if self.blocks == 1 else self.inner

    def to_rows(self, array):
        if self.blocks == 1:
            return array
        rest = array.shape[1:]
        split = array.reshape(2, 2, 2, self.rows, self.cols, -1, *rest)
        order = (3, 0, 4, 1, 2, 5) + tuple(range(6, 6 + len(rest)))
        return split.transpose(order).reshape(array.shape)

    def from_rows(self, array):
        if self.blocks == 1:
            return array
        rest = array.shape[1:]
        split = array.reshape(self.rows, 2, self.cols, 2, 2, -1, *rest)
        order = (1, 3, 4, 0, 2, 5) + tuple(range(6, 6 + len(rest)))
        return split.transpose(order).reshape(array.shape)

    def from_cols(self, array):
        return array if self.blocks == 1 else self.from_rows(array.T).T

    def gather_outer(self, array):
        if self.blocks == 1:
            return array
        return lax.all_gather(array, "dp", axis_index_groups=self.outer, axis=0, tiled=True)

    def scatter_outer(self, array):
        if self.blocks == 1:
            return array
        return lax.psum_scatter(
            array, "dp", scatter_dimension=0, axis_index_groups=self.outer, tiled=True
        )

    def swap(self, array, flip):
        pairs = [
            (block[at], block[at ^ flip]) for block in self.inner for at in range(GROUP)
        ]
        return lax.ppermute(array, "dp", pairs)

    def sum_outer(self, array):
        if self.blocks == 1:
            return array
        return lax.psum(array, "dp", axis_index_groups=self.outer)

    def gather(self, array):
        return lax.all_gather(array, "dp", axis_index_groups=self.groups(), axis=0, tiled=True)

    def scatter(self, array):
        return lax.psum_scatter(
            array, "dp", scatter_dimension=0, axis_index_groups=self.groups(), tiled=True
        )


def rms_scale(values):
    return lax.rsqrt(jnp.mean(values * values, axis=-1, keepdims=True) + NORM_EPS)


def norm_back(values, scaling, gain, grad):
    gained = grad * gain
    gain_part = jnp.sum(grad * values * scaling, axis=0)
    inner = jnp.mean(gained * values, axis=-1, keepdims=True)
    return gain_part, scaling * gained - values * scaling * scaling * scaling * inner


def per_device(
    dp_size, z_size, activations, segment_ids, attn_gain, w_query, w_key, w_value, w_out,
    mlp_gain, w_gate, w_up, w_down, cotangent,
):
    layout = Layout(dp_size)
    rows, width = activations.shape[1:]
    x = activations[0].astype(F32)
    place = lax.axis_index("tensor")
    reach = -(-(MOST_DOC - 1) // rows) * rows

    def shift(array, step):
        pairs = [(at, at + step) for at in range(z_size) if 0 <= at + step < z_size]
        return lax.ppermute(array, "tensor", pairs)

    starts = document_starts(segment_ids[0])
    own_starts = lax.dynamic_slice_in_dim(starts, place * rows, rows)
    own_tokens = place * rows + jnp.arange(rows, dtype=jnp.int32)
    cosine, sine = rope_tables(own_tokens - own_starts)
    low = (own_starts - place * rows + reach)[None, :]

    shards = [
        layout.gather_outer(w)
        for w in (w_gate, w_up, w_down, jnp.concatenate([w_key, w_value], axis=1), w_query, w_out)
    ]
    spread = spread_weights(shards[:3], shards[3:], dp_size, z_size)
    def gather_z(array):
        return layout.to_rows(lax.all_gather(array, "tensor", axis=1, tiled=True))

    wg, wu = gather_z(spread[0]), gather_z(spread[1])

    def along_z(total):
        return lax.psum_scatter(
            layout.from_rows(total), "tensor", scatter_dimension=1, tiled=True
        )

    r1 = rms_scale(x)
    xn = (x * r1 * attn_gain).astype(BF16)
    q, kv_all, wkv, wq, wo = project(
        layout.from_cols(xn), cosine, sine, *spread[3:], reach, dp_size, z_size
    )
    wd = gather_z(spread[2])
    wkv, wq, wo = layout.to_rows(wkv), layout.to_rows(wq), layout.to_rows(wo)
    att, lse, dy = attend(q, kv_all, low, cotangent[0], dp_size)
    h = x + dot_nt(att, wo)

    r2 = rms_scale(h)
    hn, gate, up, hidden, by_core = gate_up((h * r2 * mlp_gain).astype(BF16), wg, wu, dp_size)
    row, col, core = neighbours(2 * layout.cols)[0]
    def chunk(array, y, x):
        return lax.dynamic_index_in_dim(array, 2 * y + x, 0, False)

    away = dot_nt(by_core[1], wd).astype(BF16)
    dy, away = lax.optimization_barrier((dy, away))
    total_wd = dot_tn(dy, hidden).astype(BF16)
    near_sum = dot_nt(by_core[0], wd) + layout.swap(away, 1).astype(F32)
    near_sum = near_sum.astype(BF16)
    dy, total_wd, near_sum = lax.optimization_barrier((dy, total_wd, near_sum))
    part_wd = along_z(total_wd)
    near_sum = near_sum.reshape(GROUP // 2, rows, width)
    far_chunk = chunk(near_sum, 1 - row, 1 - col)
    from_x = layout.swap(far_chunk[rows // 2 :], 2)
    from_y = layout.swap(far_chunk[: rows // 2], 4)
    gate, up = gate.astype(F32), up.astype(F32)
    sigma = jax.nn.sigmoid(gate)
    dhid = dot_nn(dy, wd)
    dgate = (dhid * up * sigma * (1.0 + gate * (1.0 - sigma))).astype(BF16)
    dup = (dhid * gate * sigma).astype(BF16)
    x_chunk = chunk(near_sum, row, 1 - col)
    y_chunk = chunk(near_sum, 1 - row, col)
    x_upper = (x_chunk[: rows // 2].astype(F32) + from_y.astype(F32)).astype(BF16)
    y_lower = (y_chunk[rows // 2 :].astype(F32) + from_x.astype(F32)).astype(BF16)
    x_chunk = jnp.concatenate([x_upper, x_chunk[rows // 2 :]], axis=0)
    y_chunk = jnp.concatenate([y_chunk[: rows // 2], y_lower], axis=0)
    total_wg = dot_tn(hn, dgate).astype(BF16)
    dup, total_wg = lax.optimization_barrier((dup, total_wg))
    part_wg = along_z(total_wg)
    total_wu = dot_tn(hn, dup).astype(BF16)
    dup, total_wu = lax.optimization_barrier((dup, total_wu))
    part_wu = along_z(total_wu)
    dup, x_chunk, y_chunk = lax.optimization_barrier((dup, x_chunk, y_chunk))
    dhn = hidden_back(dgate, dup, wg, wu, dp_size)
    dhn, part_wd, x_chunk, y_chunk = lax.optimization_barrier((dhn, part_wd, x_chunk, y_chunk))
    from_x, from_y = layout.swap(x_chunk, 2), layout.swap(y_chunk, 4)
    gain_two, dh_norm = norm_back(h, r2, mlp_gain, dhn)
    dh = cotangent[0].astype(F32) + dh_norm
    dhb = dh.astype(BF16)
    datt = dot_nn(dhb, wo).astype(BF16)
    total_wo = layout.from_rows(dot_tn(dhb, att).astype(BF16))
    datt, part_wg, total_wo = lax.optimization_barrier((datt, part_wg, total_wo))
    part_wo = layout.scatter(total_wo)
    dq, dkv, wd_grad, wg_grad = attend_back(
        q, datt, att, kv_all, lse, low, cosine, sine, (part_wd, part_wg), dp_size, z_size
    )
    dq, part_wu = lax.optimization_barrier((dq, part_wu))
    dq, part_wo = lax.optimization_barrier((dq, part_wo))
    dxn = dot_nt(dq, wq) + dot_nt(dkv, wkv)
    gain_one, dx_norm = norm_back(x, r1, attn_gain, dxn)
    input_grad = (dh + dx_norm).astype(BF16)
    gains = layout.sum_outer(jnp.stack([gain_one, gain_two]))
    gains, from_x, from_y = lax.optimization_barrier((gains, from_x, from_y))
    output = h + chunk(near_sum, row, col).astype(F32)
    output = output + from_x.astype(F32) + from_y.astype(F32)
    wq_grad, wkv_grad, wo_grad, gains, wu_grad = last_grads(
        layout.from_cols(xn), dq, dkv, part_wo, gains, (part_wu,), dp_size, z_size
    )
    wo_grad, wq_grad, wkv_grad, wd_grad, wg_grad, wu_grad = (
        layout.scatter_outer(grad).astype(F32)
        for grad in (wo_grad, wq_grad, wkv_grad, wd_grad, wg_grad, wu_grad)
    )
    key_cols = w_key.shape[1]
    return (
        output.astype(BF16)[None],
        input_grad[None],
        gains[0],
        wq_grad,
        wkv_grad[:, :key_cols],
        wkv_grad[:, key_cols:],
        wo_grad,
        gains[1],
        wg_grad,
        wu_grad,
        wd_grad,
    )


def solution(mesh):
    split = P("dp", "tensor")
    tokens = P("dp", "tensor", None)
    in_specs = (
        tokens, P("dp", None), P(), split, split, split, split, P(), split, split, split, tokens,
    )
    out_specs = (tokens, tokens, P(), split, split, split, split, P(), split, split, split)
    return jax.shard_map(
        functools.partial(per_device, mesh.shape["dp"], mesh.shape["tensor"]),
        mesh=mesh, in_specs=in_specs, out_specs=out_specs, check_vma=False,
    )
```

```python
import functools
import math

import jax
import jax.numpy as jnp
from jax import lax
from jax.experimental import pallas as pl
from jax.experimental.pallas import tpu as pltpu
from jax.sharding import PartitionSpec as P

HEAD_DIM = 64
DOCS = 4
MOST_DOC = 1024
NORM_EPS = 1e-05
ROPE_THETA = 500000.0
GROUP = 8
LANES = 128
QTILE = 256
SCALE = HEAD_DIM ** (-0.5)
LOG2E = 1.4426950408889634
FAR = -1e30
NTILE = 512
STRIP = 16
LONG = 60_000_000_000
SHORT = 1_000_000

F32 = jnp.float32
BF16 = jnp.bfloat16


def dot_nn(left, right):
    return lax.dot_general(left, right, (((1,), (0,)), ((), ())), preferred_element_type=F32)


def dot_nt(left, right):
    return lax.dot_general(left, right, (((1,), (1,)), ((), ())), preferred_element_type=F32)


def dot_tn(left, right):
    return lax.dot_general(left, right, (((0,), (0,)), ((), ())), preferred_element_type=F32)


def document_starts(segments):
    doc_ids = jnp.arange(DOCS, dtype=jnp.int32)
    counts = jnp.sum((segments[:, None] == doc_ids).astype(jnp.int32), axis=0)
    before = (doc_ids < segments[:, None]).astype(jnp.int32)
    return jnp.sum(before * counts[None, :], axis=-1)


def rope_tables(positions):
    half = HEAD_DIM // 2
    frequency = jnp.exp(
        jnp.arange(half, dtype=F32) * (-2.0 * math.log(ROPE_THETA) / HEAD_DIM)
    )
    angles = positions.astype(F32)[:, None] * frequency
    cosine, sine = jnp.cos(angles), jnp.sin(angles)
    wide_cos = jnp.concatenate([cosine] * 4, axis=1)
    wide_sin = jnp.concatenate([-sine, sine, -sine, sine], axis=1)
    return wide_cos, wide_sin


def swap_halves(values):
    lane = lax.broadcasted_iota(jnp.int32, values.shape, 1)
    ahead = pltpu.roll(values, LANES - 32, 1)
    behind = pltpu.roll(values, 32, 1)
    return jnp.where((lane % 64) < 32, ahead, behind)


def fill_bias(bias_ref, low_ref, reach):
    span = bias_ref.shape[1]
    for tile in range(bias_ref.shape[0]):
        row = lax.broadcasted_iota(jnp.int32, (span, QTILE), 0)
        col = lax.broadcasted_iota(jnp.int32, (span, QTILE), 1)
        low = low_ref[0:1, tile * QTILE : (tile + 1) * QTILE]
        allowed = (row <= reach + col) & (row + tile * QTILE >= low)
        bias_ref[tile] = jnp.where(allowed, 0.0, FAR)


def spread_pair(pair, half):
    wide = pair.astype(F32)
    turned = pltpu.roll(wide, 64, 1)
    lane = lax.broadcasted_iota(jnp.int32, wide.shape, 1)
    mine = (lane // 64) == half
    even = half == 0
    first = jnp.where(mine, jnp.where(even, wide, turned), 0.0)
    second = jnp.where(mine, jnp.where(even, turned, wide), 0.0)
    return jnp.concatenate([first, second], axis=0).astype(BF16)


def gather_pair(transposed, half):
    count = transposed.shape[1] // 2
    mine = jnp.where(half == 0, transposed[:64], transposed[64:])
    return jnp.concatenate([mine[:, :count], mine[:, count:]], axis=0).T


def attend_kernel(
    reach, wide, q_ref, k_ref, v_ref, low_ref, own_ref, _, att_ref, lse_ref, all_ref,
    bias_ref, full, own_sem, send_sem, recv_sem, out_sem,
):
    head, tile, pair = pl.program_id(0), pl.program_id(1), pl.program_id(2)
    half = head % 2
    inner = pl.num_programs(1) * pl.num_programs(2)
    step = head * inner + tile * pl.num_programs(2) + pair
    ring = Ring(wide, full, own_ref.shape[0], send_sem, recv_sem)
    right = pl.ds(own_ref.shape[1] - full.shape[1], full.shape[1])

    def outward(slot, *flips):
        where = ring.whole(*flips)
        return pltpu.make_async_copy(full.at[where], all_ref.at[where, right], out_sem.at[slot])

    near = [(0, 0, 0), (0, 0, 1), (0, 1, 0), (1, 0, 0)]
    rest = [(0, 1, 1), (1, 0, 1), (1, 1, 0), (1, 1, 1)]

    @pl.when(step == 0)
    def _():
        local = pltpu.make_async_copy(own_ref.at[:, right], full.at[ring.mine()], own_sem)
        local.start()
        meet(ring.peers)
        local.wait()
        ring.start_own()
        fill_bias(bias_ref, low_ref, reach)

    pl.when(step == 2 * inner)(ring.first_halves)
    pl.when(step == 4 * inner)(ring.second_halves)

    keys = pl.ds(pl.multiple_of(tile * QTILE, QTILE), bias_ref.shape[1])
    queries = spread_pair(q_ref[...], half)
    bias = bias_ref[tile]
    score = dot_nt(k_ref[keys, :], queries)
    score = score + jnp.concatenate([bias, bias], axis=1)
    top = jnp.max(score, axis=0, keepdims=True) * (SCALE * LOG2E)
    weight = jnp.exp2(score * (SCALE * LOG2E) - top)
    total = jnp.sum(weight, axis=0, keepdims=True)
    result = dot_tn(v_ref[keys, :], weight.astype(BF16)) / total
    att_ref[...] = gather_pair(result, half).astype(BF16)
    lse_ref[0] = top + jnp.log2(total)

    @pl.when(step == pl.num_programs(0) * inner - 1)
    def _():
        ring.from_sibling("own", 0, 1)
        for slot, flips in enumerate(near):
            outward(slot, *flips).start()
        ring.far_halves()
        for name in ("x", "y", "d"):
            ring.from_sibling(name, 0, 1)
        for slot, flips in enumerate(rest):
            outward(4 + slot, *flips).start()
        for slot, flips in enumerate(near + rest):
            outward(slot, *flips).wait()
        ring.sent()


def attend(q, kv, low, grad, grads, dp_size):
    rows, width = q.shape
    keys = kv.shape[0]
    reach = keys - rows
    tiles = rows // QTILE
    pairs = width // LANES
    heads = kv.shape[1] // LANES
    per_head = pairs // heads
    span = reach + QTILE
    right = (grads.shape[0], grads.shape[1] // 2)
    far = pl.BlockSpec(memory_space=pl.ANY)
    return pl.pallas_call(
        functools.partial(attend_kernel, reach, 2 * math.isqrt(dp_size // GROUP)),
        grid=(heads, tiles, per_head),
        in_specs=[
            pl.BlockSpec((QTILE, LANES), lambda a, t, p: (t, a * per_head + p)),
            pl.BlockSpec((keys, LANES), lambda a, t, p: (0, 2 * (a // 2))),
            pl.BlockSpec((keys, LANES), lambda a, t, p: (0, 2 * (a // 2) + 1)),
            pl.BlockSpec((1, rows), lambda a, t, p: (0, 0)),
            far,
            far,
        ],
        out_specs=[
            pl.BlockSpec((QTILE, LANES), lambda a, t, p: (t, a * per_head + p)),
            pl.BlockSpec((1, 1, 2 * QTILE), lambda a, t, p: ((a * tiles + t) * per_head + p, 0, 0)),
            far,
        ],
        out_shape=[
            jax.ShapeDtypeStruct((rows, width), BF16),
            jax.ShapeDtypeStruct((pairs * tiles, 1, 2 * QTILE), F32),
            jax.ShapeDtypeStruct(grads.shape, BF16),
        ],
        scratch_shapes=[
            pltpu.VMEM((tiles, span, QTILE), F32),
            pltpu.VMEM(right, BF16),
            pltpu.SemaphoreType.DMA,
            pltpu.SemaphoreType.DMA((Ring.COPIES,)),
            pltpu.SemaphoreType.DMA((Ring.COPIES,)),
            pltpu.SemaphoreType.DMA((8,)),
        ],
        input_output_aliases={5: 2},
        compiler_params=pltpu.CompilerParams(
            collective_id=7, has_side_effects=True, vmem_limit_bytes=56 << 20
        ),
        cost_estimate=pl.CostEstimate(
            flops=16 * rows * span * LANES * pairs,
            bytes_accessed=4 * rows * width + 2 * keys * kv.shape[1],
            transcendentals=2 * rows * span * pairs,
        ),
    )(q, kv, kv, low, grad, grads)


def attend_back_kernel(
    reach, wide, z_size, mlp_count,
    q_ref, do_ref, o_ref, k_ref, v_ref, lse_ref, low_ref, cos_ref, sin_ref, cos_all, sin_all,
    *refs,
):
    mlp_ins, refs = refs[:mlp_count], refs[mlp_count:]
    dq_ref, dkv_ref = refs[:2]
    mlp_outs, refs = refs[2 : 2 + mlp_count], refs[2 + mlp_count :]
    bias_ref, dk_acc, dv_acc, own_part, send_part, recv_part, kv_send, kv_recv = refs[:8]
    home = refs[8:]
    block, half, tile, pair = (pl.program_id(at) for at in range(4))
    steps = pl.num_programs(1) * pl.num_programs(2) * pl.num_programs(3)
    inner = (half * pl.num_programs(2) + tile) * pl.num_programs(3) + pair
    step = block * steps + inner
    blocks = own_part.shape[0]
    rows = own_part.shape[1]
    count = reach // rows
    place = lax.axis_index("tensor")

    def exchange(at, distance):
        return pltpu.make_async_remote_copy(
            src_ref=send_part.at[at, pl.ds((count - distance) * rows, rows)],
            dst_ref=recv_part.at[at, distance - 1],
            send_sem=kv_send.at[at, distance - 1], recv_sem=kv_recv.at[at, distance - 1],
            device_id={"tensor": (place + z_size - distance) % z_size}, device_id_type=MESH,
        )

    def each_exchange(at, condition, action):
        for distance in range(1, count + 1):
            pl.when(condition(distance))(
                functools.partial(action, exchange(at, distance), at, distance)
            )

    @pl.when(step == 0)
    def _():
        greet(along_peers(place, z_size) + [device for _, device in others(wide)[1]])
        for copy in send_home(wide, mlp_ins, mlp_outs, *home):
            copy.start()
        fill_bias(bias_ref, low_ref, reach)

    @pl.when(inner == 0)
    def _():
        dk_acc[...] = jnp.zeros_like(dk_acc)
        dv_acc[...] = jnp.zeros_like(dv_acc)

    keys = pl.ds(pl.multiple_of(tile * QTILE, QTILE), bias_ref.shape[1])
    queries = spread_pair(q_ref[...], half)
    grads = spread_pair(do_ref[...], half)
    product = (do_ref[...].astype(F32) * o_ref[...].astype(F32)).T
    row_dot = jnp.concatenate(
        [
            jnp.sum(product[:64], axis=0, keepdims=True),
            jnp.sum(product[64:], axis=0, keepdims=True),
        ],
        axis=1,
    )
    bias = bias_ref[tile]
    key, value = k_ref[keys, :], v_ref[keys, :]
    score = dot_nt(key, queries) + jnp.concatenate([bias, bias], axis=1)
    weight = jnp.exp2(score * (SCALE * LOG2E) - lse_ref[0])
    dv_acc[keys, :] += dot_nn(weight.astype(BF16), grads)
    dscore = (weight * (dot_nt(value, grads) - row_dot)).astype(BF16)
    dk_acc[keys, :] += dot_nn(dscore, queries)
    dq = gather_pair(dot_tn(key, dscore), half) * SCALE
    dq_ref[...] = (dq * cos_ref[...] - swap_halves(dq) * sin_ref[...]).astype(BF16)

    @pl.when(inner == steps - 1)
    def _():
        send_part[block, :, :LANES] = (dk_acc[:reach] * SCALE).astype(BF16)
        send_part[block, :, LANES:] = dv_acc[:reach].astype(BF16)
        own_part[block, :, :LANES] = dk_acc[reach:] * SCALE
        own_part[block, :, LANES:] = dv_acc[reach:]
        each_exchange(block, lambda distance: place >= distance, lambda copy, *_: copy.start())

    @pl.when(step == blocks * steps - 1)
    def _():
        def collect(copy, at, distance):
            copy.wait_recv()
            own_part[at] += recv_part[at, distance - 1].astype(F32)

        for at in range(blocks):
            each_exchange(at, lambda distance: place + distance < z_size, collect)
            dkey = own_part[at, :, :LANES]
            dkey = dkey * cos_all[...] - swap_halves(dkey) * sin_all[...]
            dkv_ref[:, 2 * at * LANES : (2 * at + 1) * LANES] = dkey.astype(BF16)
            dkv_ref[:, (2 * at + 1) * LANES : (2 * at + 2) * LANES] = own_part[
                at, :, LANES:
            ].astype(BF16)
        for at in range(blocks):
            each_exchange(
                at, lambda distance: place >= distance, lambda copy, *_: copy.wait_send()
            )
        for copy in send_home(wide, mlp_ins, mlp_outs, *home):
            copy.wait()


def attend_back(q, do, att, kv, lse, low, cosine, sine, mlp, dp_size, z_size):
    rows, width = q.shape
    keys = kv.shape[0]
    reach = keys - rows
    tiles = rows // QTILE
    pairs = width // LANES
    heads = kv.shape[1] // LANES
    per_head = pairs // heads
    span = reach + QTILE
    blocks = heads // 2

    def pair_at(g, h, t, p):
        return (t, (2 * g + h) * per_head + p)

    def whole(shape):
        return pl.BlockSpec(shape, lambda g, h, t, p: (0, 0), pipeline_mode=pl.Buffered(1))

    table = pl.BlockSpec((QTILE, LANES), lambda g, h, t, p: (t, 0))
    return pl.pallas_call(
        functools.partial(
            attend_back_kernel, reach, 2 * math.isqrt(dp_size // GROUP), z_size, len(mlp)
        ),
        grid=(blocks, 2, tiles, per_head),
        in_specs=[
            pl.BlockSpec((QTILE, LANES), pair_at),
            pl.BlockSpec((QTILE, LANES), pair_at),
            pl.BlockSpec((QTILE, LANES), pair_at),
            pl.BlockSpec((keys, LANES), lambda g, h, t, p: (0, 2 * g)),
            pl.BlockSpec((keys, LANES), lambda g, h, t, p: (0, 2 * g + 1)),
            pl.BlockSpec(
                (1, 1, 2 * QTILE),
                lambda g, h, t, p: (((2 * g + h) * tiles + t) * per_head + p, 0, 0),
            ),
            whole((1, rows)),
            table,
            table,
            whole((rows, LANES)),
            whole((rows, LANES)),
        ]
        + [pl.BlockSpec(memory_space=pl.ANY)] * len(mlp),
        out_specs=[
            pl.BlockSpec((QTILE, LANES), pair_at),
            pl.BlockSpec((rows, kv.shape[1]), lambda g, h, t, p: (0, 0)),
        ]
        + [pl.BlockSpec(memory_space=pl.ANY)] * len(mlp),
        out_shape=[
            jax.ShapeDtypeStruct((rows, width), BF16),
            jax.ShapeDtypeStruct((rows, kv.shape[1]), BF16),
        ]
        + home_shapes(mlp),
        scratch_shapes=[
            pltpu.VMEM((tiles, span, QTILE), F32),
            pltpu.VMEM((keys, LANES), F32),
            pltpu.VMEM((keys, LANES), F32),
            pltpu.VMEM((blocks, rows, 2 * LANES), F32),
            pltpu.VMEM((blocks, reach, 2 * LANES), BF16),
            pltpu.VMEM((blocks, reach // rows, rows, 2 * LANES), BF16),
            pltpu.SemaphoreType.DMA((blocks, reach // rows)),
            pltpu.SemaphoreType.DMA((blocks, reach // rows)),
        ]
        + home_scratch(mlp),
        compiler_params=pltpu.CompilerParams(
            collective_id=5, has_side_effects=True, vmem_limit_bytes=60 << 20
        ),
        cost_estimate=pl.CostEstimate(
            flops=40 * rows * span * LANES * pairs,
            bytes_accessed=8 * rows * width + 4 * keys * kv.shape[1],
            transcendentals=2 * rows * span * pairs,
        ),
    )(q, do, att, kv, kv, lse, low, cosine, sine, cosine, sine, *mlp)


MESH = pl.DeviceIdType.MESH


def neighbours(wide):
    dp = lax.axis_index("dp")
    core, col, row = dp % 2, (dp // 2) % 2, (dp // (2 * wide)) % 2
    sibling = dp + 1 - 2 * core
    beside = dp + 2 - 4 * col
    above = dp + 2 * wide - 4 * wide * row
    return (row, col, core), (sibling, beside, above)


def meet(peers):
    barrier = pltpu.get_barrier_semaphore()
    for peer in peers:
        pl.semaphore_signal(barrier, inc=1, device_id={"dp": peer}, device_id_type=MESH)
    pl.semaphore_wait(barrier, len(peers))


def others(wide):
    (row, col, core), _ = neighbours(wide)
    base = lax.axis_index("dp") - (2 * wide * row + 2 * col + core)
    found = []
    for flip in range(1, GROUP):
        y, x, c = (row + flip // 4) % 2, (col + flip // 2) % 2, (core + flip) % 2
        found.append((4 * y + 2 * x + c, {"dp": base + 2 * wide * y + 2 * x + c}))
    return 4 * row + 2 * col + core, found


def along_peers(place, z_size):
    return [{"tensor": (place + step) % z_size} for step in range(1, z_size)]


def greet(peers):
    barrier = pltpu.get_barrier_semaphore()
    for peer in peers:
        pl.semaphore_signal(barrier, inc=1, device_id=peer, device_id_type=MESH)
    pl.semaphore_wait(barrier, len(peers))


def send_home(wide, ins, outs, own_sem, send_sem, recv_sem):
    mine, found = others(wide)
    copies = []
    for at, (src, dst) in enumerate(zip(ins, outs)):
        part, cols = dst.shape[0], src.shape[1]
        here = pl.ds(pl.multiple_of(mine * cols, LANES), cols)
        for index, (other, device) in enumerate(found):
            copies.append(
                pltpu.make_async_remote_copy(
                    src_ref=src.at[pl.ds(pl.multiple_of(other * part, part), part)],
                    dst_ref=dst.at[:, here],
                    send_sem=send_sem.at[at, index], recv_sem=recv_sem.at[at, index],
                    device_id=device, device_id_type=MESH,
                )
            )
        own = src.at[pl.ds(pl.multiple_of(mine * part, part), part)]
        copies.append(pltpu.make_async_copy(own, dst.at[:, here], own_sem.at[at]))
    return copies


def home_shapes(arrays):
    return [jax.ShapeDtypeStruct((a.shape[0] // GROUP, GROUP * a.shape[1]), BF16) for a in arrays]


def home_scratch(arrays):
    count = len(arrays)
    return [
        pltpu.SemaphoreType.DMA((count,)),
        pltpu.SemaphoreType.DMA((count, GROUP - 1)),
        pltpu.SemaphoreType.DMA((count, GROUP - 1)),
    ]


SIB, XN, YN = 0, 1, 2


def spread_kernel(wide, z_size, mlp_count, *refs):
    attn_count = (len(refs) - 5) // 2 - mlp_count
    count = mlp_count + attn_count
    ins, outs = refs[:count], refs[count : 2 * count]
    own_sem, send_sem, recv_sem, z_send, z_recv = refs[2 * count :]
    place = lax.axis_index("tensor")
    mine, found = others(wide)
    greet(along_peers(place, z_size) + [device for _, device in found])

    local, copies = [], []
    for at in range(mlp_count):
        src, dst = ins[at], outs[at]
        rows, cols = src.shape[0], dst.shape[1]
        here = pl.ds(pl.multiple_of(mine * rows, rows), rows)
        for index, (other, device) in enumerate(found):
            copies.append(
                pltpu.make_async_remote_copy(
                    src_ref=src.at[:, pl.ds(pl.multiple_of(other * cols, LANES), cols)],
                    dst_ref=dst.at[here],
                    send_sem=send_sem.at[at, index], recv_sem=recv_sem.at[at, index],
                    device_id=device, device_id_type=MESH,
                )
            )
        own = src.at[:, pl.ds(pl.multiple_of(mine * cols, LANES), cols)]
        local.append(pltpu.make_async_copy(own, dst.at[here], own_sem.at[at]))

    def block(at, origin):
        cols = ins[at].shape[1]
        return outs[at].at[:, pl.ds(pl.multiple_of(origin * cols, LANES), cols)]

    def hop(at, way, step, receive=False):
        sign = 1 - 2 * way
        origin = place - sign * (step if receive else step - 1)
        slot = 2 * (step - 1) + way
        src = block(at, origin) if receive or step > 1 else ins[at]
        return pltpu.make_async_remote_copy(
            src_ref=src, dst_ref=block(at, origin),
            send_sem=z_send.at[at - mlp_count, slot], recv_sem=z_recv.at[at - mlp_count, slot],
            device_id={"tensor": (place + z_size + sign) % z_size}, device_id_type=MESH,
        )

    def sends(way, step):
        if way == 0:
            return (place + 1 < z_size) & (place >= step - 1)
        return (place >= 1) & (place + step - 1 < z_size)

    def receives(way, step):
        return place >= step if way == 0 else place + step < z_size

    for at in range(mlp_count, count):
        local.append(pltpu.make_async_copy(ins[at], block(at, place), own_sem.at[at]))
        for way in range(2):
            pl.when(sends(way, 1))(lambda: hop(at, way, 1).start())
    for copy in copies + local:
        copy.start()
    for step in range(1, z_size):
        for at in range(mlp_count, count):
            for way in range(2):

                @pl.when(receives(way, step))
                def _():
                    hop(at, way, step, True).wait_recv()

                if step + 1 < z_size:
                    pl.when(sends(way, step + 1))(lambda: hop(at, way, step + 1).start())
    for step in range(1, z_size):
        for at in range(mlp_count, count):
            for way in range(2):
                pl.when(sends(way, step))(lambda: hop(at, way, step).wait_send())
    for copy in local + copies:
        copy.wait()


def spread_weights(mlp, attn, dp_size, z_size):
    count = len(mlp) + len(attn)
    spec = pl.BlockSpec(memory_space=pl.ANY)
    out = [jax.ShapeDtypeStruct((GROUP * w.shape[0], w.shape[1] // GROUP), BF16) for w in mlp]
    out += [jax.ShapeDtypeStruct((w.shape[0], z_size * w.shape[1]), BF16) for w in attn]
    return pl.pallas_call(
        functools.partial(spread_kernel, 2 * math.isqrt(dp_size // GROUP), z_size, len(mlp)),
        in_specs=[spec] * count,
        out_specs=[spec] * count,
        out_shape=out,
        scratch_shapes=[
            pltpu.SemaphoreType.DMA((count,)),
            pltpu.SemaphoreType.DMA((len(mlp), GROUP - 1)),
            pltpu.SemaphoreType.DMA((len(mlp), GROUP - 1)),
            pltpu.SemaphoreType.DMA((len(attn), 2 * (z_size - 1))),
            pltpu.SemaphoreType.DMA((len(attn), 2 * (z_size - 1))),
        ],
        compiler_params=pltpu.CompilerParams(collective_id=2, has_side_effects=True),
        cost_estimate=pl.CostEstimate(flops=LONG, bytes_accessed=0, transcendentals=0),
    )(*mlp, *attn)


class Ring:
    FLIP = {SIB: (0, 0, 1), XN: (0, 1, 0), YN: (1, 0, 0)}
    COPIES = 14

    def __init__(self, wide, ref, rows, send_sem, recv_sem):
        (self.row, self.col, self.core), self.peers = neighbours(wide)
        self.ref, self.rows, self.part = ref, rows, rows // 2
        self.send_sem, self.recv_sem = send_sem, recv_sem
        self.sends = {}
        for half in range(2):
            self.sends["own", XN, half] = (2 + half, 0, 0, 0, half)
            self.sends["own", YN, half] = (4 + half, 0, 0, 0, half)
            self.sends["own", SIB, half] = (0 + half, 0, 0, 0, half)
        for half in range(2):
            self.sends["x", SIB, half] = (6 + half, 0, 1, 0, half)
            self.sends["y", SIB, half] = (8 + half, 1, 0, 0, half)
            self.sends["d", SIB, half] = (10 + half, 1, 1, 0, half)
        self.sends["x", YN, 0] = (12, 0, 1, 0, 0)
        self.sends["y", XN, 1] = (13, 1, 0, 0, 1)

    def place(self, dy, dx, dc, half):
        p = 4 * ((self.row + dy) % 2) + 2 * ((self.col + dx) % 2) + (self.core + dc) % 2
        return pl.ds(pl.multiple_of(p * self.rows + half * self.part, self.part), self.part)

    def mine(self):
        p = 4 * self.row + 2 * self.col + self.core
        return pl.ds(pl.multiple_of(p * self.rows, self.rows), self.rows)

    def whole(self, dy, dx, dc):
        p = 4 * ((self.row + dy) % 2) + 2 * ((self.col + dx) % 2) + (self.core + dc) % 2
        return pl.ds(pl.multiple_of(p * self.rows, self.rows), self.rows)

    def copy(self, slot, dy, dx, dc, half, peer):
        where = self.place(dy, dx, dc, half)
        return pltpu.make_async_remote_copy(
            src_ref=self.ref.at[where], dst_ref=self.ref.at[where],
            send_sem=self.send_sem.at[slot], recv_sem=self.recv_sem.at[slot],
            device_id={"dp": self.peers[peer]}, device_id_type=MESH,
        )

    def start(self, name, peer, half):
        self.copy(*self.sends[name, peer, half], peer).start()

    def arrived(self, name, peer, half):
        slot, dy, dx, dc, half = self.sends[name, peer, half]
        fy, fx, fc = self.FLIP[peer]
        self.copy(slot, (dy + fy) % 2, (dx + fx) % 2, (dc + fc) % 2, half, peer).wait_recv()

    def start_own(self):
        for half in range(2):
            for peer in (XN, YN, SIB):
                self.start("own", peer, half)

    def first_halves(self):
        self.arrived("own", XN, 0)
        self.start("x", YN, 0)
        self.start("x", SIB, 0)
        self.arrived("own", YN, 0)
        self.start("y", SIB, 0)

    def second_halves(self):
        self.arrived("own", YN, 1)
        self.start("y", XN, 1)
        self.start("y", SIB, 1)
        self.arrived("own", XN, 1)
        self.start("x", SIB, 1)

    def far_halves(self):
        self.arrived("x", YN, 0)
        self.start("d", SIB, 0)
        self.arrived("y", XN, 1)
        self.start("d", SIB, 1)

    def from_sibling(self, name, *halves):
        for half in halves:
            self.arrived(name, SIB, half)

    def sent(self):
        for (name, peer, half), entry in self.sends.items():
            self.copy(*entry, peer).wait_send()


def project_kernel(
    wide, z_size, x_ref, cos_ref, sin_ref, wkv_ref, wq_ref, wo_ref, grad_ref,
    q_ref, kv_ref, wkv_out, wq_out, wo_out, grad_out,
    wkv_all, wq_all, wo_all, grad_all, keys, own_sem, send_sem, recv_sem, kv_send, kv_recv, out_sem,
):
    place = lax.axis_index("tensor")
    rows = x_ref.shape[0]
    count = keys.shape[0] // rows - 1
    left = pl.ds(0, grad_all.shape[1])
    parts = (
        (wkv_ref, wkv_all, wkv_out), (wq_ref, wq_all, wq_out), (wo_ref, wo_all, wo_out),
        (grad_ref.at[:, left], grad_all, grad_out.at[:, left]),
    )
    rings = [
        Ring(wide, full, part.shape[0], send_sem.at[at], recv_sem.at[at])
        for at, (part, full, _) in enumerate(parts)
    ]
    local = [
        pltpu.make_async_copy(part, full.at[ring.mine()], own_sem.at[at])
        for at, ((part, full, _), ring) in enumerate(zip(parts, rings))
    ]
    outward = [
        pltpu.make_async_copy(full, out, out_sem.at[at])
        for at, (_, full, out) in enumerate(parts)
    ]
    for copy in local:
        copy.start()
    keys[: count * rows, :] = jnp.zeros((count * rows, keys.shape[1]), BF16)
    greet([{"dp": peer} for peer in rings[0].peers] + along_peers(place, z_size))
    for copy in local:
        copy.wait()

    def rotated(value):
        return (value * cos_ref[...] + swap_halves(value) * sin_ref[...]).astype(BF16)

    def hop(step):
        return pltpu.make_async_remote_copy(
            src_ref=keys.at[pl.ds((count - step + 1) * rows, rows)],
            dst_ref=keys.at[pl.ds((count - step) * rows, rows)],
            send_sem=kv_send.at[step - 1], recv_sem=kv_recv.at[step - 1],
            device_id={"tensor": (place + 1) % z_size}, device_id_type=MESH,
        )

    def pass_keys(step):
        if step > 1:
            pl.when(place >= step - 1)(lambda: hop(step - 1).wait_recv())
        if step <= count:
            sends = (place + 1 < z_size) & (place >= step - 1)
            pl.when(sends)(lambda: hop(step).start())

    def finish(ring):
        ring.far_halves()
        for name in ("own", "x", "y", "d"):
            ring.from_sibling(name, 0, 1)

    rings[0].start_own()
    rings[0].first_halves()
    rings[0].second_halves()
    rings[1].start_own()
    finish(rings[0])
    outward[0].start()

    @pl.loop(0, wkv_all.shape[1] // (2 * LANES))
    def _(at):
        n = pl.ds(pl.multiple_of(at * 2 * LANES, LANES), 2 * LANES)
        value = dot_nn(x_ref[...], wkv_all[:, n])
        both = jnp.concatenate([rotated(value[:, :LANES]), value[:, LANES:].astype(BF16)], axis=1)
        keys[pl.ds(count * rows, rows), n] = both

    pass_keys(1)
    rings[1].first_halves()
    rings[1].second_halves()
    rings[2].start_own()
    finish(rings[1])
    outward[1].start()

    @pl.loop(0, wq_all.shape[1] // (2 * LANES))
    def _(at):
        n = pl.ds(pl.multiple_of(at * 2 * LANES, LANES), 2 * LANES)
        value = dot_nn(x_ref[...], wq_all[:, n])
        both = [rotated(value[:, :LANES]), rotated(value[:, LANES:])]
        q_ref[:, n] = jnp.concatenate(both, axis=1)

    rings[2].first_halves()
    rings[2].second_halves()
    rings[3].start_own()
    for step in range(2, count + 1):
        pass_keys(step)
    finish(rings[2])
    outward[2].start()
    rings[3].first_halves()
    rings[3].second_halves()
    finish(rings[3])
    outward[3].start()
    pass_keys(count + 1)
    keys_out = pltpu.make_async_copy(keys, kv_ref, out_sem.at[4])
    keys_out.start()
    for step in range(1, count + 1):
        sends = (place + 1 < z_size) & (place >= step - 1)
        pl.when(sends)(lambda: hop(step).wait_send())
    for ring in rings:
        ring.sent()
    for copy in outward + [keys_out]:
        copy.wait()


def project(x, cosine, sine, wkv, wq, wo, grad, reach, dp_size, z_size):
    rows, width = x.shape
    far = pl.BlockSpec(memory_space=pl.ANY)
    near = pl.BlockSpec(memory_space=pltpu.VMEM)
    weights = (wkv, wq, wo)
    whole = [(GROUP * w.shape[0], w.shape[1]) for w in weights]
    keys = (reach + rows, wkv.shape[1])
    grads = (GROUP * grad.shape[0], grad.shape[1])
    left = (grads[0], grads[1] // 2)
    return pl.pallas_call(
        functools.partial(project_kernel, 2 * math.isqrt(dp_size // GROUP), z_size),
        in_specs=[near] * 3 + [far] * 4,
        out_specs=[near] + [far] * 5,
        out_shape=[jax.ShapeDtypeStruct((rows, wq.shape[1]), BF16)]
        + [jax.ShapeDtypeStruct(shape, BF16) for shape in [keys] + whole + [grads]],
        scratch_shapes=[pltpu.VMEM(shape, BF16) for shape in whole + [left, keys]]
        + [
            pltpu.SemaphoreType.DMA((4,)),
            pltpu.SemaphoreType.DMA((4, Ring.COPIES)),
            pltpu.SemaphoreType.DMA((4, Ring.COPIES)),
            pltpu.SemaphoreType.DMA((reach // rows,)),
            pltpu.SemaphoreType.DMA((reach // rows,)),
            pltpu.SemaphoreType.DMA((5,)),
        ],
        compiler_params=pltpu.CompilerParams(
            collective_id=3, has_side_effects=True, vmem_limit_bytes=56 << 20
        ),
        cost_estimate=pl.CostEstimate(
            flops=2 * LONG, bytes_accessed=4 * width * sum(w.shape[1] for w in weights),
            transcendentals=0,
        ),
    )(x, cosine, sine, wkv, wq, wo, grad)


def gate_up_kernel(
    wide, own_ref, wg_ref, wu_ref, all_ref, gate_ref, up_ref, hid_ref, core_ref,
    full, stage, own_sem, send_sem, recv_sem, out_sem, all_sem,
):
    rows = own_ref.shape[0]
    cols = gate_ref.shape[1]
    ring = Ring(wide, full, rows, send_sem, recv_sem)
    local = pltpu.make_async_copy(own_ref, full.at[ring.mine()], own_sem)
    local.start()
    meet(ring.peers)
    local.wait()
    ring.start_own()

    def out_copies(slot, places):
        where, core, chip = places
        return [
            pltpu.make_async_copy(stage.at[slot, i], ref.at[where], out_sem.at[slot, i])
            for i, ref in enumerate((gate_ref, up_ref, hid_ref))
        ] + [
            pltpu.make_async_copy(stage.at[slot, 2], core_ref.at[core, chip], out_sem.at[slot, 3]),
            pltpu.make_async_copy(full.at[where], all_ref.at[where], all_sem.at[slot]),
        ]

    def step_place(step):
        phase, i = step // 4, step % 4
        high, low = phase // 2, phase % 2
        first, last = (1 - high) * (1 - low), high * low
        middle = high + low - 2 * last
        half = (first + last) * (i % 2) + high * (1 - low)
        dx = middle * (1 - i % 2) + last
        dy = middle * (i % 2) + last
        chip = 2 * ((ring.row + dy) % 2) + (ring.col + dx) % 2
        part = rows // 2
        chip_rows = pl.ds(pl.multiple_of(chip * rows + half * part, part), part)
        return ring.place(dy, dx, i // 2, half), i // 2, chip_rows

    @pl.loop(0, 16)
    def _(step):
        pl.when(step == 2)(lambda: ring.from_sibling("own", 0, 1))
        pl.when(step == 4)(ring.first_halves)

        @pl.when(step == 6)
        def _():
            ring.from_sibling("x", 0)
            ring.from_sibling("y", 0)

        pl.when(step == 8)(ring.second_halves)

        @pl.when(step == 10)
        def _():
            ring.from_sibling("x", 1)
            ring.from_sibling("y", 1)

        pl.when(step == 12)(ring.far_halves)
        pl.when(step == 14)(lambda: ring.from_sibling("d", 0, 1))

        slot = step % 2
        places = step_place(step)

        @pl.when(step >= 2)
        def _():
            for copy in out_copies(slot, step_place(step - 2)):
                copy.wait()

        x = full[places[0], :]

        @pl.loop(0, cols // NTILE)
        def _(at):
            n = pl.ds(pl.multiple_of(at * NTILE, NTILE), NTILE)
            gate = dot_nn(x, wg_ref[:, n])
            up = dot_nn(x, wu_ref[:, n])
            stage[slot, 0, :, n] = gate.astype(BF16)
            stage[slot, 1, :, n] = up.astype(BF16)
            stage[slot, 2, :, n] = (gate * up / (1.0 + jnp.exp(-gate))).astype(BF16)

        for copy in out_copies(slot, places):
            copy.start()

    for step in (14, 15):
        for copy in out_copies(step % 2, step_place(step)):
            copy.wait()
    ring.sent()


def gate_up(hn, wg, wu, dp_size):
    rows, width = hn.shape
    cols = wg.shape[1]
    tokens = GROUP * rows
    far = pl.BlockSpec(memory_space=pl.ANY)
    near = pl.BlockSpec(memory_space=pltpu.VMEM)
    return pl.pallas_call(
        functools.partial(gate_up_kernel, 2 * math.isqrt(dp_size // GROUP)),
        in_specs=[far, near, near],
        out_specs=[far] * 5,
        out_shape=[jax.ShapeDtypeStruct((tokens, width), BF16)]
        + [jax.ShapeDtypeStruct((tokens, cols), BF16)] * 3
        + [jax.ShapeDtypeStruct((2, tokens // 2, cols), BF16)],
        scratch_shapes=[
            pltpu.VMEM((tokens, width), BF16),
            pltpu.VMEM((2, 3, rows // 2, cols), BF16),
            pltpu.SemaphoreType.DMA,
            pltpu.SemaphoreType.DMA((Ring.COPIES,)),
            pltpu.SemaphoreType.DMA((Ring.COPIES,)),
            pltpu.SemaphoreType.DMA((2, 4)),
            pltpu.SemaphoreType.DMA((2,)),
        ],
        compiler_params=pltpu.CompilerParams(
            collective_id=1, has_side_effects=True, vmem_limit_bytes=56 << 20
        ),
        cost_estimate=pl.CostEstimate(
            flops=SHORT, bytes_accessed=0, transcendentals=0
        ),
    )(hn, wg, wu)


FAR_CHUNK, X_CHUNK, Y_CHUNK, OWN_CHUNK = range(4)


class Reduce:
    COPIES = 10

    def __init__(self, wide, parts, cores, far, near, send_sem, recv_sem):
        self.at, self.peers = neighbours(wide)
        self.parts, self.cores, self.far, self.near = parts, cores, far, near
        self.send_sem, self.recv_sem = send_sem, recv_sem
        self.half = parts.shape[2] // 2

    @staticmethod
    def scratch(rows, cols):
        return [
            pltpu.VMEM((2, 4, rows, cols), BF16),
            pltpu.VMEM((4, rows, cols), BF16),
            pltpu.VMEM((2, rows // 2, cols), BF16),
            pltpu.VMEM((2, rows, cols), BF16),
            pltpu.SemaphoreType.DMA((Reduce.COPIES,)),
            pltpu.SemaphoreType.DMA((Reduce.COPIES,)),
        ]

    def chunk(self, step):
        slot, other = step // 2, 1 - step % 2
        row, col, core = self.at
        dy, dx = 1 - slot % 2, 1 - slot // 2
        place = 4 * ((row + dy) % 2) + 2 * ((col + dx) % 2) + (core + other) % 2
        return place, self.parts.at[other, slot]

    def copy(self, name):
        upper, lower = pl.ds(0, self.half), pl.ds(self.half, self.half)
        mine = self.parts.at[0]
        table = {
            "far0": (self.parts.at[1, FAR_CHUNK], self.cores.at[FAR_CHUNK], SIB),
            "x": (self.parts.at[1, X_CHUNK], self.cores.at[X_CHUNK], SIB),
            "y": (self.parts.at[1, Y_CHUNK], self.cores.at[Y_CHUNK], SIB),
            "own": (self.parts.at[1, OWN_CHUNK], self.cores.at[OWN_CHUNK], SIB),
            "far_x": (mine.at[FAR_CHUNK, lower], self.far.at[0], XN),
            "far_y": (mine.at[FAR_CHUNK, upper], self.far.at[1], YN),
            "x_upper": (mine.at[X_CHUNK, upper], self.near.at[0, upper], XN),
            "x_lower": (mine.at[X_CHUNK, lower], self.near.at[0, lower], XN),
            "y_upper": (mine.at[Y_CHUNK, upper], self.near.at[1, upper], YN),
            "y_lower": (mine.at[Y_CHUNK, lower], self.near.at[1, lower], YN),
        }
        src, dst, peer = table[name]
        at = list(table).index(name)
        return pltpu.make_async_remote_copy(
            src_ref=src, dst_ref=dst, send_sem=self.send_sem.at[at],
            recv_sem=self.recv_sem.at[at], device_id={"dp": self.peers[peer]},
            device_id_type=MESH,
        )

    def start(self, *names):
        for name in names:
            self.copy(name).start()

    def add(self, slot, start, other):
        count = other.shape[0] // STRIP

        @pl.loop(0, count)
        def _(at):
            here = pl.ds(pl.multiple_of(start + at * STRIP, STRIP), STRIP)
            there = pl.ds(pl.multiple_of(at * STRIP, STRIP), STRIP)
            value = self.parts[0, slot, here, :].astype(F32) + other[there, :].astype(F32)
            self.parts[0, slot, here, :] = value.astype(BF16)

    def merge_core(self, slot, name):
        self.copy(name).wait_recv()
        self.add(slot, 0, self.cores.at[slot])

    def after(self, step):
        names = ("far0", "x", "y", "own")
        for slot in range(4):
            pl.when(step == 2 * slot)(functools.partial(self.start, names[slot]))

        @pl.when(step == 1)
        def _():
            self.merge_core(FAR_CHUNK, "far0")
            self.start("far_x", "far_y")

        @pl.when(step == 3)
        def _():
            self.merge_core(X_CHUNK, "x")
            self.start("x_lower")

        @pl.when(step == 5)
        def _():
            self.merge_core(Y_CHUNK, "y")
            self.start("y_upper")

    def pass_on(self):
        self.copy("far_y").wait_recv()
        self.add(X_CHUNK, 0, self.far.at[1])
        self.start("x_upper")
        self.copy("far_x").wait_recv()
        self.add(Y_CHUNK, self.half, self.far.at[0])
        self.start("y_lower")

    def finish(self, store):
        for name in ("own", "x_upper", "x_lower", "y_upper", "y_lower"):
            self.copy(name).wait_recv()

        @pl.loop(0, 2 * self.half // STRIP)
        def _(at):
            here = pl.ds(pl.multiple_of(at * STRIP, STRIP), STRIP)
            value = self.parts[0, OWN_CHUNK, here, :].astype(F32)
            value += self.cores[OWN_CHUNK, here, :].astype(F32)
            value += self.near[0, here, :].astype(F32)
            value += self.near[1, here, :].astype(F32)
            store(here, value)

    def sent(self):
        for name in (
            "far0", "x", "y", "own", "far_x", "far_y", "x_upper", "x_lower", "y_upper", "y_lower",
        ):
            self.copy(name).wait_send()


def hidden_back_kernel(
    wide, dgate_ref, dup_ref, wg_ref, wu_ref, out_ref, loaded, load_sem, *scratch
):
    ring = Reduce(wide, *scratch)
    rows = out_ref.shape[0]

    def loads(step):
        chunk, _ = ring.chunk(step)
        here = pl.ds(pl.multiple_of(chunk * rows, rows), rows)
        return [
            pltpu.make_async_copy(
                ref.at[here], loaded.at[step % 2, at], load_sem.at[step % 2, at]
            )
            for at, ref in enumerate((dgate_ref, dup_ref))
        ]

    for copy in loads(0):
        copy.start()
    meet(ring.peers)

    @pl.loop(0, 8)
    def _(step):
        @pl.when(step < 7)
        def _():
            for copy in loads(step + 1):
                copy.start()

        for copy in loads(step):
            copy.wait()
        _, target = ring.chunk(step)
        dgate, dup = loaded[step % 2, 0], loaded[step % 2, 1]

        @pl.loop(0, out_ref.shape[1] // NTILE)
        def _(at):
            n = pl.ds(pl.multiple_of(at * NTILE, NTILE), NTILE)
            value = dot_nt(dgate, wg_ref[n, :]) + dot_nt(dup, wu_ref[n, :])
            target[:, n] = value.astype(BF16)

        ring.after(step)

    ring.pass_on()

    def store(here, value):
        out_ref[here, :] = value

    ring.finish(store)
    ring.sent()


def hidden_back(dgate, dup, wg, wu, dp_size):
    tokens, cols = dgate.shape
    width = wg.shape[0]
    rows = tokens // GROUP
    far = pl.BlockSpec(memory_space=pl.ANY)
    near = pl.BlockSpec(memory_space=pltpu.VMEM)
    return pl.pallas_call(
        functools.partial(hidden_back_kernel, 2 * math.isqrt(dp_size // GROUP)),
        in_specs=[far, far, near, near],
        out_specs=near,
        out_shape=jax.ShapeDtypeStruct((rows, width), F32),
        scratch_shapes=[
            pltpu.VMEM((2, 2, rows, cols), BF16),
            pltpu.SemaphoreType.DMA((2, 2)),
        ]
        + Reduce.scratch(rows, width),
        compiler_params=pltpu.CompilerParams(
            collective_id=6, has_side_effects=True, vmem_limit_bytes=60 << 20
        ),
        cost_estimate=pl.CostEstimate(
            flops=4 * tokens * width * cols,
            bytes_accessed=4 * tokens * cols + 4 * width * cols + 4 * rows * width,
            transcendentals=0,
        ),
    )(dgate, dup, wg, wu)


def tail_kernel(
    wide, z_size, mlp_count, x_ref, dq_ref, dkv_ref, wo_ref, gain_ref, *refs
):
    mlp_ins, refs = refs[:mlp_count], refs[mlp_count:]
    wq_out, wkv_out, wo_out, gain_out = refs[:4]
    mlp_outs, scratch = refs[4 : 4 + mlp_count], refs[4 + mlp_count :]
    own_scratch = scratch[:12]
    sums, zrecv, gain_z, gain_p, z_send, z_recv, g_send, g_recv = scratch[12:20]
    wo_recv, w_send, w_recv, m_own, m_send, m_recv = scratch[20:]
    rings = [Reduce(wide, *own_scratch[6 * at : 6 * at + 6]) for at in range(2)]
    place = lax.axis_index("tensor")
    mine, found = others(wide)
    along = along_peers(place, z_size)
    around = [device for _, device in found]
    greet(along + around)

    mlp_copies = send_home(wide, mlp_ins, mlp_outs, m_own, m_send, m_recv)
    wo_part = wo_out.shape[1]
    wo_copies = [
        pltpu.make_async_remote_copy(
            src_ref=wo_ref.at[
                :,
                pl.ds(pl.multiple_of((place + at + 1) % z_size * wo_part, LANES), wo_part),
            ],
            dst_ref=wo_recv.at[at], send_sem=w_send.at[at], recv_sem=w_recv.at[at],
            device_id=peer, device_id_type=MESH,
        )
        for at, peer in enumerate(along)
    ]
    for copy in wo_copies:
        copy.start()

    gain_z[place] = gain_ref[...]
    gain_copies = [
        pltpu.make_async_remote_copy(
            src_ref=gain_ref, dst_ref=gain_z.at[place], send_sem=g_send.at[at],
            recv_sem=g_recv.at[at], device_id=peer, device_id_type=MESH,
        )
        for at, peer in enumerate(along)
    ]
    for copy in gain_copies:
        copy.start()

    rights = (dq_ref, dkv_ref)
    rows = sums.shape[0]
    outs = (wq_out, wkv_out)
    z_copies = []
    for index, ring in enumerate(rings):
        right = rights[index]
        cols = right.shape[1]

        @pl.loop(0, 8)
        def _(step):
            chunk, target = ring.chunk(step)
            x = x_ref[:, pl.ds(pl.multiple_of(chunk * rows, rows), rows)].T

            @pl.loop(0, cols // NTILE)
            def _(at):
                n = pl.ds(pl.multiple_of(at * NTILE, NTILE), NTILE)
                target[:, n] = dot_nn(x, right[:, n]).astype(BF16)

            ring.after(step)

        if index == 0:
            for copy in mlp_copies:
                copy.start()
            for copy in gain_copies:
                copy.wait_recv()
            total = gain_z[0]
            for at in range(1, z_size):
                total = total + gain_z[at]
            gain_p[mine] = total
            for at, peer in enumerate(around):
                copy = pltpu.make_async_remote_copy(
                    src_ref=gain_p.at[mine], dst_ref=gain_p.at[mine],
                    send_sem=g_send.at[z_size - 1 + at], recv_sem=g_recv.at[z_size - 1 + at],
                    device_id=peer, device_id_type=MESH,
                )
                gain_copies.append(copy)
                copy.start()

    def send_along(index, ring, start):
        cols = rights[index].shape[1]
        part = cols // z_size

        def store(here, value):
            sums[here, pl.ds(start, cols)] = value.astype(BF16)

        ring.finish(store)
        for at, peer in enumerate(along):
            other = (place + at + 1) % z_size
            copy = pltpu.make_async_remote_copy(
                src_ref=sums.at[:, pl.ds(pl.multiple_of(start + other * part, LANES), part)],
                dst_ref=zrecv.at[at, :, pl.ds(start // z_size, part)],
                send_sem=z_send.at[index, at], recv_sem=z_recv.at[index, at],
                device_id=peer, device_id_type=MESH,
            )
            z_copies.append(copy)
            copy.start()

    starts = [0, rights[0].shape[1]]
    for index, ring in enumerate(rings):
        ring.pass_on()
        if index:
            send_along(index - 1, rings[index - 1], starts[index - 1])
    send_along(1, rings[1], starts[1])

    for copy in gain_copies[z_size - 1 :]:
        copy.wait_recv()
    total = gain_p[0]
    for at in range(1, GROUP):
        total = total + gain_p[at]
    gain_out[...] = total

    for copy in wo_copies:
        copy.wait()
    total = wo_ref[:, pl.ds(pl.multiple_of(place * wo_part, LANES), wo_part)].astype(F32)
    for at in range(z_size - 1):
        total += wo_recv[at].astype(F32)
    wo_out[...] = total

    for copy in z_copies:
        copy.wait_recv()
    for index in range(2):
        part = rights[index].shape[1] // z_size
        own = pl.ds(pl.multiple_of(starts[index] + place * part, LANES), part)
        value = sums[:, own].astype(F32)
        for at in range(z_size - 1):
            value += zrecv[at, :, pl.ds(starts[index] // z_size, part)].astype(F32)
        outs[index][...] = value
    for copy in z_copies + gain_copies:
        copy.wait_send()
    for ring in rings:
        ring.sent()
    for copy in mlp_copies:
        copy.wait()


def last_grads(x, dq, dkv, wo_sum, gains, mlp, dp_size, z_size):
    tokens, width = x.shape
    rows = width // GROUP
    near = pl.BlockSpec(memory_space=pltpu.VMEM)
    far = pl.BlockSpec(memory_space=pl.ANY)
    sizes = [dq.shape[1], dkv.shape[1]]
    scratch = []
    for cols in sizes:
        scratch += Reduce.scratch(rows, cols)
    total = sum(sizes)
    return pl.pallas_call(
        functools.partial(tail_kernel, 2 * math.isqrt(dp_size // GROUP), z_size, len(mlp)),
        in_specs=[near] * 5 + [far] * len(mlp),
        out_specs=[near] * 4 + [far] * len(mlp),
        out_shape=[jax.ShapeDtypeStruct((rows, cols // z_size), F32) for cols in sizes]
        + [jax.ShapeDtypeStruct((rows, wo_sum.shape[1] // z_size), F32)]
        + [jax.ShapeDtypeStruct(gains.shape, F32)]
        + home_shapes(mlp),
        scratch_shapes=scratch
        + [
            pltpu.VMEM((rows, total), BF16),
            pltpu.VMEM((z_size - 1, rows, total // z_size), BF16),
            pltpu.VMEM((z_size, *gains.shape), F32),
            pltpu.VMEM((GROUP, *gains.shape), F32),
            pltpu.SemaphoreType.DMA((2, z_size - 1)),
            pltpu.SemaphoreType.DMA((2, z_size - 1)),
            pltpu.SemaphoreType.DMA((z_size - 1 + GROUP - 1,)),
            pltpu.SemaphoreType.DMA((z_size - 1 + GROUP - 1,)),
            pltpu.VMEM((z_size - 1, rows, wo_sum.shape[1] // z_size), BF16),
            pltpu.SemaphoreType.DMA((z_size - 1,)),
            pltpu.SemaphoreType.DMA((z_size - 1,)),
        ]
        + home_scratch(mlp),
        compiler_params=pltpu.CompilerParams(
            collective_id=4, has_side_effects=True, vmem_limit_bytes=60 << 20
        ),
        cost_estimate=pl.CostEstimate(
            flops=2 * LONG, bytes_accessed=4 * tokens * total, transcendentals=0
        ),
    )(x, dq, dkv, wo_sum, gains, *mlp)


class Layout:
    def __init__(self, dp_size):
        self.blocks = dp_size // GROUP
        side = math.isqrt(self.blocks)
        self.rows, self.cols = side, self.blocks // side
        wide = 2 * self.cols

        def index(by, bx, y, x, core):
            return ((2 * by + y) * wide + 2 * bx + x) * 2 + core

        places = [(y, x, c) for y in range(2) for x in range(2) for c in range(2)]
        spots = [(by, bx) for by in range(self.rows) for bx in range(self.cols)]
        self.inner = [[index(*s, *p) for p in places] for s in spots]
        self.outer = [[index(*s, *p) for s in spots] for p in places]

    def groups(self):
        return None if self.blocks == 1 else self.inner

    def to_rows(self, array):
        if self.blocks == 1:
            return array
        rest = array.shape[1:]
        split = array.reshape(2, 2, 2, self.rows, self.cols, -1, *rest)
        order = (3, 0, 4, 1, 2, 5) + tuple(range(6, 6 + len(rest)))
        return split.transpose(order).reshape(array.shape)

    def from_rows(self, array):
        if self.blocks == 1:
            return array
        rest = array.shape[1:]
        split = array.reshape(self.rows, 2, self.cols, 2, 2, -1, *rest)
        order = (1, 3, 4, 0, 2, 5) + tuple(range(6, 6 + len(rest)))
        return split.transpose(order).reshape(array.shape)

    def from_cols(self, array):
        return array if self.blocks == 1 else self.from_rows(array.T).T

    def gather_outer(self, array):
        if self.blocks == 1:
            return array
        return lax.all_gather(array, "dp", axis_index_groups=self.outer, axis=0, tiled=True)

    def scatter_outer(self, array):
        if self.blocks == 1:
            return array
        return lax.psum_scatter(
            array, "dp", scatter_dimension=0, axis_index_groups=self.outer, tiled=True
        )

    def swap(self, array, flip):
        pairs = [
            (block[at], block[at ^ flip]) for block in self.inner for at in range(GROUP)
        ]
        return lax.ppermute(array, "dp", pairs)

    def sum_outer(self, array):
        if self.blocks == 1:
            return array
        return lax.psum(array, "dp", axis_index_groups=self.outer)

    def gather(self, array):
        return lax.all_gather(array, "dp", axis_index_groups=self.groups(), axis=0, tiled=True)

    def scatter(self, array):
        return lax.psum_scatter(
            array, "dp", scatter_dimension=0, axis_index_groups=self.groups(), tiled=True
        )


def rms_scale(values):
    return lax.rsqrt(jnp.mean(values * values, axis=-1, keepdims=True) + NORM_EPS)


def norm_back(values, scaling, gain, grad):
    gained = grad * gain
    gain_part = jnp.sum(grad * values * scaling, axis=0)
    inner = jnp.mean(gained * values, axis=-1, keepdims=True)
    return gain_part, scaling * gained - values * scaling * scaling * scaling * inner


def per_device(
    dp_size, z_size, activations, segment_ids, attn_gain, w_query, w_key, w_value, w_out,
    mlp_gain, w_gate, w_up, w_down, cotangent,
):
    layout = Layout(dp_size)
    rows, width = activations.shape[1:]
    x = activations[0].astype(F32)
    place = lax.axis_index("tensor")
    reach = -(-(MOST_DOC - 1) // rows) * rows

    def shift(array, step):
        pairs = [(at, at + step) for at in range(z_size) if 0 <= at + step < z_size]
        return lax.ppermute(array, "tensor", pairs)

    starts = document_starts(segment_ids[0])
    own_starts = lax.dynamic_slice_in_dim(starts, place * rows, rows)
    own_tokens = place * rows + jnp.arange(rows, dtype=jnp.int32)
    cosine, sine = rope_tables(own_tokens - own_starts)
    low = (own_starts - place * rows + reach)[None, :]

    shards = [
        layout.gather_outer(w)
        for w in (w_gate, w_up, w_down, jnp.concatenate([w_key, w_value], axis=1), w_query, w_out)
    ]
    spread = spread_weights(shards[:3], shards[3:], dp_size, z_size)
    def gather_z(array):
        return layout.to_rows(lax.all_gather(array, "tensor", axis=1, tiled=True))

    wg, wu = gather_z(spread[0]), gather_z(spread[1])

    def along_z(total):
        return lax.psum_scatter(
            layout.from_rows(total), "tensor", scatter_dimension=1, tiled=True
        )

    r1 = rms_scale(x)
    xn = (x * r1 * attn_gain).astype(BF16)
    q, kv_all, wkv, wq, wo, dy = project(
        layout.from_cols(xn), cosine, sine, *spread[3:], cotangent[0], reach, dp_size, z_size
    )
    wd = gather_z(spread[2])
    wkv, wq, wo = layout.to_rows(wkv), layout.to_rows(wq), layout.to_rows(wo)
    att, lse, dy = attend(q, kv_all, low, cotangent[0], dy, dp_size)
    h = x + dot_nt(att, wo)

    r2 = rms_scale(h)
    hn, gate, up, hidden, by_core = gate_up((h * r2 * mlp_gain).astype(BF16), wg, wu, dp_size)
    row, col, core = neighbours(2 * layout.cols)[0]
    def chunk(array, y, x):
        return lax.dynamic_index_in_dim(array, 2 * y + x, 0, False)

    away = dot_nt(by_core[1], wd).astype(BF16)
    dy, away = lax.optimization_barrier((dy, away))
    total_wd = dot_tn(dy, hidden).astype(BF16)
    near_sum = dot_nt(by_core[0], wd) + layout.swap(away, 1).astype(F32)
    near_sum = near_sum.astype(BF16)
    part_wd = along_z(total_wd)
    dy, near_sum = lax.optimization_barrier((dy, near_sum))
    near_sum = near_sum.reshape(GROUP // 2, rows, width)
    far_chunk = chunk(near_sum, 1 - row, 1 - col)
    from_x = layout.swap(far_chunk[rows // 2 :], 2)
    from_y = layout.swap(far_chunk[: rows // 2], 4)
    gate, up = gate.astype(F32), up.astype(F32)
    sigma = jax.nn.sigmoid(gate)
    dhid = dot_nn(dy, wd)
    dgate = (dhid * up * sigma * (1.0 + gate * (1.0 - sigma))).astype(BF16)
    dup = (dhid * gate * sigma).astype(BF16)
    x_chunk = chunk(near_sum, row, 1 - col)
    y_chunk = chunk(near_sum, 1 - row, col)
    x_upper = (x_chunk[: rows // 2].astype(F32) + from_y.astype(F32)).astype(BF16)
    y_lower = (y_chunk[rows // 2 :].astype(F32) + from_x.astype(F32)).astype(BF16)
    x_chunk = jnp.concatenate([x_upper, x_chunk[rows // 2 :]], axis=0)
    y_chunk = jnp.concatenate([y_chunk[: rows // 2], y_lower], axis=0)
    total_wg = dot_tn(hn, dgate).astype(BF16)
    dup, total_wg = lax.optimization_barrier((dup, total_wg))
    part_wg = along_z(total_wg)
    total_wu = dot_tn(hn, dup).astype(BF16)
    dup, total_wu = lax.optimization_barrier((dup, total_wu))
    part_wu = along_z(total_wu)
    dup, x_chunk, y_chunk = lax.optimization_barrier((dup, x_chunk, y_chunk))
    dhn = hidden_back(dgate, dup, wg, wu, dp_size)
    dhn, part_wd, x_chunk, y_chunk = lax.optimization_barrier((dhn, part_wd, x_chunk, y_chunk))
    from_x, from_y = layout.swap(x_chunk, 2), layout.swap(y_chunk, 4)
    gain_two, dh_norm = norm_back(h, r2, mlp_gain, dhn)
    dh = cotangent[0].astype(F32) + dh_norm
    dhb = dh.astype(BF16)
    datt = dot_nn(dhb, wo).astype(BF16)
    total_wo = layout.from_rows(dot_tn(dhb, att).astype(BF16))
    datt, part_wg, total_wo = lax.optimization_barrier((datt, part_wg, total_wo))
    part_wo = layout.scatter(total_wo)
    dq, dkv, wd_grad, wg_grad = attend_back(
        q, datt, att, kv_all, lse, low, cosine, sine, (part_wd, part_wg), dp_size, z_size
    )
    dq, part_wu = lax.optimization_barrier((dq, part_wu))
    dq, part_wo = lax.optimization_barrier((dq, part_wo))
    dxn = dot_nt(dq, wq) + dot_nt(dkv, wkv)
    gain_one, dx_norm = norm_back(x, r1, attn_gain, dxn)
    input_grad = (dh + dx_norm).astype(BF16)
    gains = layout.sum_outer(jnp.stack([gain_one, gain_two]))
    gains, from_x, from_y = lax.optimization_barrier((gains, from_x, from_y))
    output = h + chunk(near_sum, row, col).astype(F32)
    output = output + from_x.astype(F32) + from_y.astype(F32)
    wq_grad, wkv_grad, wo_grad, gains, wu_grad = last_grads(
        layout.from_cols(xn), dq, dkv, part_wo, gains, (part_wu,), dp_size, z_size
    )
    wo_grad, wq_grad, wkv_grad, wd_grad, wg_grad, wu_grad = (
        layout.scatter_outer(grad).astype(F32)
        for grad in (wo_grad, wq_grad, wkv_grad, wd_grad, wg_grad, wu_grad)
    )
    key_cols = w_key.shape[1]
    return (
        output.astype(BF16)[None],
        input_grad[None],
        gains[0],
        wq_grad,
        wkv_grad[:, :key_cols],
        wkv_grad[:, key_cols:],
        wo_grad,
        gains[1],
        wg_grad,
        wu_grad,
        wd_grad,
    )


def solution(mesh):
    split = P("dp", "tensor")
    tokens = P("dp", "tensor", None)
    in_specs = (
        tokens, P("dp", None), P(), split, split, split, split, P(), split, split, split, tokens,
    )
    out_specs = (tokens, tokens, P(), split, split, split, split, P(), split, split, split)
    return jax.shard_map(
        functools.partial(per_device, mesh.shape["dp"], mesh.shape["tensor"]),
        mesh=mesh, in_specs=in_specs, out_specs=out_specs, check_vma=False,
    )
```

```python
import functools
import math

import jax
import jax.numpy as jnp
from jax import lax
from jax.experimental import pallas as pl
from jax.experimental.pallas import tpu as pltpu
from jax.sharding import PartitionSpec as P

HEAD_DIM = 64
DOCS = 4
MOST_DOC = 1024
NORM_EPS = 1e-05
ROPE_THETA = 500000.0
GROUP = 8
LANES = 128
QTILE = 256
SCALE = HEAD_DIM ** (-0.5)
LOG2E = 1.4426950408889634
FAR = -1e30
NTILE = 512
STRIP = 16
LONG = 60_000_000_000
SHORT = 1_000_000

F32 = jnp.float32
BF16 = jnp.bfloat16


def dot_nn(left, right):
    return lax.dot_general(left, right, (((1,), (0,)), ((), ())), preferred_element_type=F32)


def dot_nt(left, right):
    return lax.dot_general(left, right, (((1,), (1,)), ((), ())), preferred_element_type=F32)


def dot_tn(left, right):
    return lax.dot_general(left, right, (((0,), (0,)), ((), ())), preferred_element_type=F32)


def document_starts(segments):
    doc_ids = jnp.arange(DOCS, dtype=jnp.int32)
    counts = jnp.sum((segments[:, None] == doc_ids).astype(jnp.int32), axis=0)
    before = (doc_ids < segments[:, None]).astype(jnp.int32)
    return jnp.sum(before * counts[None, :], axis=-1)


def rope_tables(positions):
    half = HEAD_DIM // 2
    frequency = jnp.exp(
        jnp.arange(half, dtype=F32) * (-2.0 * math.log(ROPE_THETA) / HEAD_DIM)
    )
    angles = positions.astype(F32)[:, None] * frequency
    cosine, sine = jnp.cos(angles), jnp.sin(angles)
    wide_cos = jnp.concatenate([cosine] * 4, axis=1)
    wide_sin = jnp.concatenate([-sine, sine, -sine, sine], axis=1)
    return wide_cos, wide_sin


def swap_halves(values):
    lane = lax.broadcasted_iota(jnp.int32, values.shape, 1)
    ahead = pltpu.roll(values, LANES - 32, 1)
    behind = pltpu.roll(values, 32, 1)
    return jnp.where((lane % 64) < 32, ahead, behind)


def fill_bias(bias_ref, low_ref, reach):
    span = bias_ref.shape[1]
    for tile in range(bias_ref.shape[0]):
        row = lax.broadcasted_iota(jnp.int32, (span, QTILE), 0)
        col = lax.broadcasted_iota(jnp.int32, (span, QTILE), 1)
        low = low_ref[0:1, tile * QTILE : (tile + 1) * QTILE]
        allowed = (row <= reach + col) & (row + tile * QTILE >= low)
        bias_ref[tile] = jnp.where(allowed, 0.0, FAR)


def spread_pair(pair, half):
    wide = pair.astype(F32)
    turned = pltpu.roll(wide, 64, 1)
    lane = lax.broadcasted_iota(jnp.int32, wide.shape, 1)
    mine = (lane // 64) == half
    even = half == 0
    first = jnp.where(mine, jnp.where(even, wide, turned), 0.0)
    second = jnp.where(mine, jnp.where(even, turned, wide), 0.0)
    return jnp.concatenate([first, second], axis=0).astype(BF16)


def gather_pair(transposed, half):
    count = transposed.shape[1] // 2
    mine = jnp.where(half == 0, transposed[:64], transposed[64:])
    return jnp.concatenate([mine[:, :count], mine[:, count:]], axis=0).T


def attend_kernel(
    reach, wide, q_ref, k_ref, v_ref, low_ref, own_ref, _, att_ref, lse_ref, all_ref,
    bias_ref, full, own_sem, send_sem, recv_sem, out_sem,
):
    head, tile, pair = pl.program_id(0), pl.program_id(1), pl.program_id(2)
    half = head % 2
    inner = pl.num_programs(1) * pl.num_programs(2)
    step = head * inner + tile * pl.num_programs(2) + pair
    ring = Ring(wide, full, own_ref.shape[0], send_sem, recv_sem)
    right = pl.ds(own_ref.shape[1] - full.shape[1], full.shape[1])

    def outward(slot, *flips):
        where = ring.whole(*flips)
        return pltpu.make_async_copy(full.at[where], all_ref.at[where, right], out_sem.at[slot])

    near = [(0, 0, 0), (0, 0, 1), (0, 1, 0), (1, 0, 0)]
    rest = [(0, 1, 1), (1, 0, 1), (1, 1, 0), (1, 1, 1)]

    @pl.when(step == 0)
    def _():
        local = pltpu.make_async_copy(own_ref.at[:, right], full.at[ring.mine()], own_sem)
        local.start()
        meet(ring.peers)
        local.wait()
        ring.start_own()
        fill_bias(bias_ref, low_ref, reach)

    pl.when(step == 2 * inner)(ring.first_halves)
    pl.when(step == 4 * inner)(ring.second_halves)

    keys = pl.ds(pl.multiple_of(tile * QTILE, QTILE), bias_ref.shape[1])
    queries = spread_pair(q_ref[...], half)
    bias = bias_ref[tile]
    score = dot_nt(k_ref[keys, :], queries)
    score = score + jnp.concatenate([bias, bias], axis=1)
    top = jnp.max(score, axis=0, keepdims=True) * (SCALE * LOG2E)
    weight = jnp.exp2(score * (SCALE * LOG2E) - top)
    total = jnp.sum(weight, axis=0, keepdims=True)
    result = dot_tn(v_ref[keys, :], weight.astype(BF16)) / total
    att_ref[...] = gather_pair(result, half).astype(BF16)
    lse_ref[0] = top + jnp.log2(total)

    @pl.when(step == pl.num_programs(0) * inner - 1)
    def _():
        ring.from_sibling("own", 0, 1)
        for slot, flips in enumerate(near):
            outward(slot, *flips).start()
        ring.far_halves()
        for name in ("x", "y", "d"):
            ring.from_sibling(name, 0, 1)
        for slot, flips in enumerate(rest):
            outward(4 + slot, *flips).start()
        for slot, flips in enumerate(near + rest):
            outward(slot, *flips).wait()
        ring.sent()


def attend(q, kv, low, grad, grads, dp_size):
    rows, width = q.shape
    keys = kv.shape[0]
    reach = keys - rows
    tiles = rows // QTILE
    pairs = width // LANES
    heads = kv.shape[1] // LANES
    per_head = pairs // heads
    span = reach + QTILE
    right = (grads.shape[0], grads.shape[1] * 5 // 8)
    far = pl.BlockSpec(memory_space=pl.ANY)
    return pl.pallas_call(
        functools.partial(attend_kernel, reach, 2 * math.isqrt(dp_size // GROUP)),
        grid=(heads, tiles, per_head),
        in_specs=[
            pl.BlockSpec((QTILE, LANES), lambda a, t, p: (t, a * per_head + p)),
            pl.BlockSpec((keys, LANES), lambda a, t, p: (0, 2 * (a // 2))),
            pl.BlockSpec((keys, LANES), lambda a, t, p: (0, 2 * (a // 2) + 1)),
            pl.BlockSpec((1, rows), lambda a, t, p: (0, 0)),
            far,
            far,
        ],
        out_specs=[
            pl.BlockSpec((QTILE, LANES), lambda a, t, p: (t, a * per_head + p)),
            pl.BlockSpec((1, 1, 2 * QTILE), lambda a, t, p: ((a * tiles + t) * per_head + p, 0, 0)),
            far,
        ],
        out_shape=[
            jax.ShapeDtypeStruct((rows, width), BF16),
            jax.ShapeDtypeStruct((pairs * tiles, 1, 2 * QTILE), F32),
            jax.ShapeDtypeStruct(grads.shape, BF16),
        ],
        scratch_shapes=[
            pltpu.VMEM((tiles, span, QTILE), F32),
            pltpu.VMEM(right, BF16),
            pltpu.SemaphoreType.DMA,
            pltpu.SemaphoreType.DMA((Ring.COPIES,)),
            pltpu.SemaphoreType.DMA((Ring.COPIES,)),
            pltpu.SemaphoreType.DMA((8,)),
        ],
        input_output_aliases={5: 2},
        compiler_params=pltpu.CompilerParams(
            collective_id=7, has_side_effects=True, vmem_limit_bytes=56 << 20
        ),
        cost_estimate=pl.CostEstimate(
            flops=16 * rows * span * LANES * pairs,
            bytes_accessed=4 * rows * width + 2 * keys * kv.shape[1],
            transcendentals=2 * rows * span * pairs,
        ),
    )(q, kv, kv, low, grad, grads)


def attend_back_kernel(
    reach, wide, z_size, mlp_count,
    q_ref, do_ref, o_ref, k_ref, v_ref, lse_ref, low_ref, cos_ref, sin_ref, cos_all, sin_all,
    *refs,
):
    mlp_ins, refs = refs[:mlp_count], refs[mlp_count:]
    dq_ref, dkv_ref = refs[:2]
    mlp_outs, refs = refs[2 : 2 + mlp_count], refs[2 + mlp_count :]
    bias_ref, dk_acc, dv_acc, own_part, send_part, recv_part, kv_send, kv_recv = refs[:8]
    home = refs[8:]
    block, half, tile, pair = (pl.program_id(at) for at in range(4))
    steps = pl.num_programs(1) * pl.num_programs(2) * pl.num_programs(3)
    inner = (half * pl.num_programs(2) + tile) * pl.num_programs(3) + pair
    step = block * steps + inner
    blocks = own_part.shape[0]
    rows = own_part.shape[1]
    count = reach // rows
    place = lax.axis_index("tensor")

    def exchange(at, distance):
        return pltpu.make_async_remote_copy(
            src_ref=send_part.at[at, pl.ds((count - distance) * rows, rows)],
            dst_ref=recv_part.at[at, distance - 1],
            send_sem=kv_send.at[at, distance - 1], recv_sem=kv_recv.at[at, distance - 1],
            device_id={"tensor": (place + z_size - distance) % z_size}, device_id_type=MESH,
        )

    def each_exchange(at, condition, action):
        for distance in range(1, count + 1):
            pl.when(condition(distance))(
                functools.partial(action, exchange(at, distance), at, distance)
            )

    @pl.when(step == 0)
    def _():
        greet(along_peers(place, z_size) + [device for _, device in others(wide)[1]])
        for copy in send_home(wide, mlp_ins, mlp_outs, *home):
            copy.start()
        fill_bias(bias_ref, low_ref, reach)

    @pl.when(inner == 0)
    def _():
        dk_acc[...] = jnp.zeros_like(dk_acc)
        dv_acc[...] = jnp.zeros_like(dv_acc)

    keys = pl.ds(pl.multiple_of(tile * QTILE, QTILE), bias_ref.shape[1])
    queries = spread_pair(q_ref[...], half)
    grads = spread_pair(do_ref[...], half)
    product = (do_ref[...].astype(F32) * o_ref[...].astype(F32)).T
    row_dot = jnp.concatenate(
        [
            jnp.sum(product[:64], axis=0, keepdims=True),
            jnp.sum(product[64:], axis=0, keepdims=True),
        ],
        axis=1,
    )
    bias = bias_ref[tile]
    key, value = k_ref[keys, :], v_ref[keys, :]
    score = dot_nt(key, queries) + jnp.concatenate([bias, bias], axis=1)
    weight = jnp.exp2(score * (SCALE * LOG2E) - lse_ref[0])
    dv_acc[keys, :] += dot_nn(weight.astype(BF16), grads)
    dscore = (weight * (dot_nt(value, grads) - row_dot)).astype(BF16)
    dk_acc[keys, :] += dot_nn(dscore, queries)
    dq = gather_pair(dot_tn(key, dscore), half) * SCALE
    dq_ref[...] = (dq * cos_ref[...] - swap_halves(dq) * sin_ref[...]).astype(BF16)

    @pl.when(inner == steps - 1)
    def _():
        send_part[block, :, :LANES] = (dk_acc[:reach] * SCALE).astype(BF16)
        send_part[block, :, LANES:] = dv_acc[:reach].astype(BF16)
        own_part[block, :, :LANES] = dk_acc[reach:] * SCALE
        own_part[block, :, LANES:] = dv_acc[reach:]
        each_exchange(block, lambda distance: place >= distance, lambda copy, *_: copy.start())

    @pl.when(step == blocks * steps - 1)
    def _():
        def collect(copy, at, distance):
            copy.wait_recv()
            own_part[at] += recv_part[at, distance - 1].astype(F32)

        for at in range(blocks):
            each_exchange(at, lambda distance: place + distance < z_size, collect)
            dkey = own_part[at, :, :LANES]
            dkey = dkey * cos_all[...] - swap_halves(dkey) * sin_all[...]
            dkv_ref[:, 2 * at * LANES : (2 * at + 1) * LANES] = dkey.astype(BF16)
            dkv_ref[:, (2 * at + 1) * LANES : (2 * at + 2) * LANES] = own_part[
                at, :, LANES:
            ].astype(BF16)
        for at in range(blocks):
            each_exchange(
                at, lambda distance: place >= distance, lambda copy, *_: copy.wait_send()
            )
        for copy in send_home(wide, mlp_ins, mlp_outs, *home):
            copy.wait()


def attend_back(q, do, att, kv, lse, low, cosine, sine, mlp, dp_size, z_size):
    rows, width = q.shape
    keys = kv.shape[0]
    reach = keys - rows
    tiles = rows // QTILE
    pairs = width // LANES
    heads = kv.shape[1] // LANES
    per_head = pairs // heads
    span = reach + QTILE
    blocks = heads // 2

    def pair_at(g, h, t, p):
        return (t, (2 * g + h) * per_head + p)

    def whole(shape):
        return pl.BlockSpec(shape, lambda g, h, t, p: (0, 0), pipeline_mode=pl.Buffered(1))

    table = pl.BlockSpec((QTILE, LANES), lambda g, h, t, p: (t, 0))
    return pl.pallas_call(
        functools.partial(
            attend_back_kernel, reach, 2 * math.isqrt(dp_size // GROUP), z_size, len(mlp)
        ),
        grid=(blocks, 2, tiles, per_head),
        in_specs=[
            pl.BlockSpec((QTILE, LANES), pair_at),
            pl.BlockSpec((QTILE, LANES), pair_at),
            pl.BlockSpec((QTILE, LANES), pair_at),
            pl.BlockSpec((keys, LANES), lambda g, h, t, p: (0, 2 * g)),
            pl.BlockSpec((keys, LANES), lambda g, h, t, p: (0, 2 * g + 1)),
            pl.BlockSpec(
                (1, 1, 2 * QTILE),
                lambda g, h, t, p: (((2 * g + h) * tiles + t) * per_head + p, 0, 0),
            ),
            whole((1, rows)),
            table,
            table,
            whole((rows, LANES)),
            whole((rows, LANES)),
        ]
        + [pl.BlockSpec(memory_space=pl.ANY)] * len(mlp),
        out_specs=[
            pl.BlockSpec((QTILE, LANES), pair_at),
            pl.BlockSpec((rows, kv.shape[1]), lambda g, h, t, p: (0, 0)),
        ]
        + [pl.BlockSpec(memory_space=pl.ANY)] * len(mlp),
        out_shape=[
            jax.ShapeDtypeStruct((rows, width), BF16),
            jax.ShapeDtypeStruct((rows, kv.shape[1]), BF16),
        ]
        + home_shapes(mlp),
        scratch_shapes=[
            pltpu.VMEM((tiles, span, QTILE), F32),
            pltpu.VMEM((keys, LANES), F32),
            pltpu.VMEM((keys, LANES), F32),
            pltpu.VMEM((blocks, rows, 2 * LANES), F32),
            pltpu.VMEM((blocks, reach, 2 * LANES), BF16),
            pltpu.VMEM((blocks, reach // rows, rows, 2 * LANES), BF16),
            pltpu.SemaphoreType.DMA((blocks, reach // rows)),
            pltpu.SemaphoreType.DMA((blocks, reach // rows)),
        ]
        + home_scratch(mlp),
        compiler_params=pltpu.CompilerParams(
            collective_id=5, has_side_effects=True, vmem_limit_bytes=60 << 20
        ),
        cost_estimate=pl.CostEstimate(
            flops=40 * rows * span * LANES * pairs,
            bytes_accessed=8 * rows * width + 4 * keys * kv.shape[1],
            transcendentals=2 * rows * span * pairs,
        ),
    )(q, do, att, kv, kv, lse, low, cosine, sine, cosine, sine, *mlp)


MESH = pl.DeviceIdType.MESH


def neighbours(wide):
    dp = lax.axis_index("dp")
    core, col, row = dp % 2, (dp // 2) % 2, (dp // (2 * wide)) % 2
    sibling = dp + 1 - 2 * core
    beside = dp + 2 - 4 * col
    above = dp + 2 * wide - 4 * wide * row
    return (row, col, core), (sibling, beside, above)


def meet(peers):
    barrier = pltpu.get_barrier_semaphore()
    for peer in peers:
        pl.semaphore_signal(barrier, inc=1, device_id={"dp": peer}, device_id_type=MESH)
    pl.semaphore_wait(barrier, len(peers))


def others(wide):
    (row, col, core), _ = neighbours(wide)
    base = lax.axis_index("dp") - (2 * wide * row + 2 * col + core)
    found = []
    for flip in range(1, GROUP):
        y, x, c = (row + flip // 4) % 2, (col + flip // 2) % 2, (core + flip) % 2
        found.append((4 * y + 2 * x + c, {"dp": base + 2 * wide * y + 2 * x + c}))
    return 4 * row + 2 * col + core, found


def along_peers(place, z_size):
    return [{"tensor": (place + step) % z_size} for step in range(1, z_size)]


def greet(peers):
    barrier = pltpu.get_barrier_semaphore()
    for peer in peers:
        pl.semaphore_signal(barrier, inc=1, device_id=peer, device_id_type=MESH)
    pl.semaphore_wait(barrier, len(peers))


def send_home(wide, ins, outs, own_sem, send_sem, recv_sem):
    mine, found = others(wide)
    copies = []
    for at, (src, dst) in enumerate(zip(ins, outs)):
        part, cols = dst.shape[0], src.shape[1]
        here = pl.ds(pl.multiple_of(mine * cols, LANES), cols)
        for index, (other, device) in enumerate(found):
            copies.append(
                pltpu.make_async_remote_copy(
                    src_ref=src.at[pl.ds(pl.multiple_of(other * part, part), part)],
                    dst_ref=dst.at[:, here],
                    send_sem=send_sem.at[at, index], recv_sem=recv_sem.at[at, index],
                    device_id=device, device_id_type=MESH,
                )
            )
        own = src.at[pl.ds(pl.multiple_of(mine * part, part), part)]
        copies.append(pltpu.make_async_copy(own, dst.at[:, here], own_sem.at[at]))
    return copies


def home_shapes(arrays):
    return [jax.ShapeDtypeStruct((a.shape[0] // GROUP, GROUP * a.shape[1]), BF16) for a in arrays]


def home_scratch(arrays):
    count = len(arrays)
    return [
        pltpu.SemaphoreType.DMA((count,)),
        pltpu.SemaphoreType.DMA((count, GROUP - 1)),
        pltpu.SemaphoreType.DMA((count, GROUP - 1)),
    ]


SIB, XN, YN = 0, 1, 2


def spread_kernel(wide, z_size, mlp_count, *refs):
    attn_count = (len(refs) - 5) // 2 - mlp_count
    count = mlp_count + attn_count
    ins, outs = refs[:count], refs[count : 2 * count]
    own_sem, send_sem, recv_sem, z_send, z_recv = refs[2 * count :]
    place = lax.axis_index("tensor")
    mine, found = others(wide)
    greet(along_peers(place, z_size) + [device for _, device in found])

    local, copies = [], []
    for at in range(mlp_count):
        src, dst = ins[at], outs[at]
        rows, cols = src.shape[0], dst.shape[1]
        here = pl.ds(pl.multiple_of(mine * rows, rows), rows)
        for index, (other, device) in enumerate(found):
            copies.append(
                pltpu.make_async_remote_copy(
                    src_ref=src.at[:, pl.ds(pl.multiple_of(other * cols, LANES), cols)],
                    dst_ref=dst.at[here],
                    send_sem=send_sem.at[at, index], recv_sem=recv_sem.at[at, index],
                    device_id=device, device_id_type=MESH,
                )
            )
        own = src.at[:, pl.ds(pl.multiple_of(mine * cols, LANES), cols)]
        local.append(pltpu.make_async_copy(own, dst.at[here], own_sem.at[at]))

    def block(at, origin):
        cols = ins[at].shape[1]
        return outs[at].at[:, pl.ds(pl.multiple_of(origin * cols, LANES), cols)]

    def hop(at, way, step, receive=False):
        sign = 1 - 2 * way
        origin = place - sign * (step if receive else step - 1)
        slot = 2 * (step - 1) + way
        src = block(at, origin) if receive or step > 1 else ins[at]
        return pltpu.make_async_remote_copy(
            src_ref=src, dst_ref=block(at, origin),
            send_sem=z_send.at[at - mlp_count, slot], recv_sem=z_recv.at[at - mlp_count, slot],
            device_id={"tensor": (place + z_size + sign) % z_size}, device_id_type=MESH,
        )

    def sends(way, step):
        if way == 0:
            return (place + 1 < z_size) & (place >= step - 1)
        return (place >= 1) & (place + step - 1 < z_size)

    def receives(way, step):
        return place >= step if way == 0 else place + step < z_size

    for at in range(mlp_count, count):
        local.append(pltpu.make_async_copy(ins[at], block(at, place), own_sem.at[at]))
        for way in range(2):
            pl.when(sends(way, 1))(lambda: hop(at, way, 1).start())
    for copy in copies + local:
        copy.start()
    for step in range(1, z_size):
        for at in range(mlp_count, count):
            for way in range(2):

                @pl.when(receives(way, step))
                def _():
                    hop(at, way, step, True).wait_recv()

                if step + 1 < z_size:
                    pl.when(sends(way, step + 1))(lambda: hop(at, way, step + 1).start())
    for step in range(1, z_size):
        for at in range(mlp_count, count):
            for way in range(2):
                pl.when(sends(way, step))(lambda: hop(at, way, step).wait_send())
    for copy in local + copies:
        copy.wait()


def spread_weights(mlp, attn, dp_size, z_size):
    count = len(mlp) + len(attn)
    spec = pl.BlockSpec(memory_space=pl.ANY)
    out = [jax.ShapeDtypeStruct((GROUP * w.shape[0], w.shape[1] // GROUP), BF16) for w in mlp]
    out += [jax.ShapeDtypeStruct((w.shape[0], z_size * w.shape[1]), BF16) for w in attn]
    return pl.pallas_call(
        functools.partial(spread_kernel, 2 * math.isqrt(dp_size // GROUP), z_size, len(mlp)),
        in_specs=[spec] * count,
        out_specs=[spec] * count,
        out_shape=out,
        scratch_shapes=[
            pltpu.SemaphoreType.DMA((count,)),
            pltpu.SemaphoreType.DMA((len(mlp), GROUP - 1)),
            pltpu.SemaphoreType.DMA((len(mlp), GROUP - 1)),
            pltpu.SemaphoreType.DMA((len(attn), 2 * (z_size - 1))),
            pltpu.SemaphoreType.DMA((len(attn), 2 * (z_size - 1))),
        ],
        compiler_params=pltpu.CompilerParams(collective_id=2, has_side_effects=True),
        cost_estimate=pl.CostEstimate(flops=LONG, bytes_accessed=0, transcendentals=0),
    )(*mlp, *attn)


class Ring:
    FLIP = {SIB: (0, 0, 1), XN: (0, 1, 0), YN: (1, 0, 0)}
    COPIES = 14

    def __init__(self, wide, ref, rows, send_sem, recv_sem):
        (self.row, self.col, self.core), self.peers = neighbours(wide)
        self.ref, self.rows, self.part = ref, rows, rows // 2
        self.send_sem, self.recv_sem = send_sem, recv_sem
        self.sends = {}
        for half in range(2):
            self.sends["own", XN, half] = (2 + half, 0, 0, 0, half)
            self.sends["own", YN, half] = (4 + half, 0, 0, 0, half)
            self.sends["own", SIB, half] = (0 + half, 0, 0, 0, half)
        for half in range(2):
            self.sends["x", SIB, half] = (6 + half, 0, 1, 0, half)
            self.sends["y", SIB, half] = (8 + half, 1, 0, 0, half)
            self.sends["d", SIB, half] = (10 + half, 1, 1, 0, half)
        self.sends["x", YN, 0] = (12, 0, 1, 0, 0)
        self.sends["y", XN, 1] = (13, 1, 0, 0, 1)

    def place(self, dy, dx, dc, half):
        p = 4 * ((self.row + dy) % 2) + 2 * ((self.col + dx) % 2) + (self.core + dc) % 2
        return pl.ds(pl.multiple_of(p * self.rows + half * self.part, self.part), self.part)

    def mine(self):
        p = 4 * self.row + 2 * self.col + self.core
        return pl.ds(pl.multiple_of(p * self.rows, self.rows), self.rows)

    def whole(self, dy, dx, dc):
        p = 4 * ((self.row + dy) % 2) + 2 * ((self.col + dx) % 2) + (self.core + dc) % 2
        return pl.ds(pl.multiple_of(p * self.rows, self.rows), self.rows)

    def copy(self, slot, dy, dx, dc, half, peer):
        where = self.place(dy, dx, dc, half)
        return pltpu.make_async_remote_copy(
            src_ref=self.ref.at[where], dst_ref=self.ref.at[where],
            send_sem=self.send_sem.at[slot], recv_sem=self.recv_sem.at[slot],
            device_id={"dp": self.peers[peer]}, device_id_type=MESH,
        )

    def start(self, name, peer, half):
        self.copy(*self.sends[name, peer, half], peer).start()

    def arrived(self, name, peer, half):
        slot, dy, dx, dc, half = self.sends[name, peer, half]
        fy, fx, fc = self.FLIP[peer]
        self.copy(slot, (dy + fy) % 2, (dx + fx) % 2, (dc + fc) % 2, half, peer).wait_recv()

    def start_own(self):
        for half in range(2):
            for peer in (XN, YN, SIB):
                self.start("own", peer, half)

    def first_halves(self):
        self.arrived("own", XN, 0)
        self.start("x", YN, 0)
        self.start("x", SIB, 0)
        self.arrived("own", YN, 0)
        self.start("y", SIB, 0)

    def second_halves(self):
        self.arrived("own", YN, 1)
        self.start("y", XN, 1)
        self.start("y", SIB, 1)
        self.arrived("own", XN, 1)
        self.start("x", SIB, 1)

    def far_halves(self):
        self.arrived("x", YN, 0)
        self.start("d", SIB, 0)
        self.arrived("y", XN, 1)
        self.start("d", SIB, 1)

    def from_sibling(self, name, *halves):
        for half in halves:
            self.arrived(name, SIB, half)

    def sent(self):
        for (name, peer, half), entry in self.sends.items():
            self.copy(*entry, peer).wait_send()


def project_kernel(
    wide, z_size, x_ref, cos_ref, sin_ref, wkv_ref, wq_ref, wo_ref, grad_ref,
    q_ref, kv_ref, wkv_out, wq_out, wo_out, grad_out,
    wkv_all, wq_all, wo_all, grad_all, keys, own_sem, send_sem, recv_sem, kv_send, kv_recv, out_sem,
):
    place = lax.axis_index("tensor")
    rows = x_ref.shape[0]
    count = keys.shape[0] // rows - 1
    left = pl.ds(0, grad_all.shape[1])
    parts = (
        (wkv_ref, wkv_all, wkv_out), (wq_ref, wq_all, wq_out), (wo_ref, wo_all, wo_out),
        (grad_ref.at[:, left], grad_all, grad_out.at[:, left]),
    )
    rings = [
        Ring(wide, full, part.shape[0], send_sem.at[at], recv_sem.at[at])
        for at, (part, full, _) in enumerate(parts)
    ]
    local = [
        pltpu.make_async_copy(part, full.at[ring.mine()], own_sem.at[at])
        for at, ((part, full, _), ring) in enumerate(zip(parts, rings))
    ]
    outward = [
        pltpu.make_async_copy(full, out, out_sem.at[at])
        for at, (_, full, out) in enumerate(parts)
    ]
    for copy in local:
        copy.start()
    keys[: count * rows, :] = jnp.zeros((count * rows, keys.shape[1]), BF16)
    greet([{"dp": peer} for peer in rings[0].peers] + along_peers(place, z_size))
    for copy in local:
        copy.wait()

    def rotated(value):
        return (value * cos_ref[...] + swap_halves(value) * sin_ref[...]).astype(BF16)

    def hop(step):
        return pltpu.make_async_remote_copy(
            src_ref=keys.at[pl.ds((count - step + 1) * rows, rows)],
            dst_ref=keys.at[pl.ds((count - step) * rows, rows)],
            send_sem=kv_send.at[step - 1], recv_sem=kv_recv.at[step - 1],
            device_id={"tensor": (place + 1) % z_size}, device_id_type=MESH,
        )

    def pass_keys(step):
        if step > 1:
            pl.when(place >= step - 1)(lambda: hop(step - 1).wait_recv())
        if step <= count:
            sends = (place + 1 < z_size) & (place >= step - 1)
            pl.when(sends)(lambda: hop(step).start())

    def finish(ring):
        ring.far_halves()
        for name in ("own", "x", "y", "d"):
            ring.from_sibling(name, 0, 1)

    rings[0].start_own()
    rings[0].first_halves()
    rings[0].second_halves()
    rings[1].start_own()
    finish(rings[0])
    outward[0].start()

    @pl.loop(0, wkv_all.shape[1] // (2 * LANES))
    def _(at):
        n = pl.ds(pl.multiple_of(at * 2 * LANES, LANES), 2 * LANES)
        value = dot_nn(x_ref[...], wkv_all[:, n])
        both = jnp.concatenate([rotated(value[:, :LANES]), value[:, LANES:].astype(BF16)], axis=1)
        keys[pl.ds(count * rows, rows), n] = both

    pass_keys(1)
    rings[1].first_halves()
    rings[1].second_halves()
    rings[2].start_own()
    finish(rings[1])
    outward[1].start()

    @pl.loop(0, wq_all.shape[1] // (2 * LANES))
    def _(at):
        n = pl.ds(pl.multiple_of(at * 2 * LANES, LANES), 2 * LANES)
        value = dot_nn(x_ref[...], wq_all[:, n])
        both = [rotated(value[:, :LANES]), rotated(value[:, LANES:])]
        q_ref[:, n] = jnp.concatenate(both, axis=1)

    rings[2].first_halves()
    rings[2].second_halves()
    rings[3].start_own()
    for step in range(2, count + 1):
        pass_keys(step)
    finish(rings[2])
    outward[2].start()
    rings[3].first_halves()
    rings[3].second_halves()
    finish(rings[3])
    outward[3].start()
    pass_keys(count + 1)
    keys_out = pltpu.make_async_copy(keys, kv_ref, out_sem.at[4])
    keys_out.start()
    for step in range(1, count + 1):
        sends = (place + 1 < z_size) & (place >= step - 1)
        pl.when(sends)(lambda: hop(step).wait_send())
    for ring in rings:
        ring.sent()
    for copy in outward + [keys_out]:
        copy.wait()


def project(x, cosine, sine, wkv, wq, wo, grad, reach, dp_size, z_size):
    rows, width = x.shape
    far = pl.BlockSpec(memory_space=pl.ANY)
    near = pl.BlockSpec(memory_space=pltpu.VMEM)
    weights = (wkv, wq, wo)
    whole = [(GROUP * w.shape[0], w.shape[1]) for w in weights]
    keys = (reach + rows, wkv.shape[1])
    grads = (GROUP * grad.shape[0], grad.shape[1])
    left = (grads[0], grads[1] * 3 // 8)
    return pl.pallas_call(
        functools.partial(project_kernel, 2 * math.isqrt(dp_size // GROUP), z_size),
        in_specs=[near] * 3 + [far] * 4,
        out_specs=[near] + [far] * 5,
        out_shape=[jax.ShapeDtypeStruct((rows, wq.shape[1]), BF16)]
        + [jax.ShapeDtypeStruct(shape, BF16) for shape in [keys] + whole + [grads]],
        scratch_shapes=[pltpu.VMEM(shape, BF16) for shape in whole + [left, keys]]
        + [
            pltpu.SemaphoreType.DMA((4,)),
            pltpu.SemaphoreType.DMA((4, Ring.COPIES)),
            pltpu.SemaphoreType.DMA((4, Ring.COPIES)),
            pltpu.SemaphoreType.DMA((reach // rows,)),
            pltpu.SemaphoreType.DMA((reach // rows,)),
            pltpu.SemaphoreType.DMA((5,)),
        ],
        compiler_params=pltpu.CompilerParams(
            collective_id=3, has_side_effects=True, vmem_limit_bytes=56 << 20
        ),
        cost_estimate=pl.CostEstimate(
            flops=2 * LONG, bytes_accessed=4 * width * sum(w.shape[1] for w in weights),
            transcendentals=0,
        ),
    )(x, cosine, sine, wkv, wq, wo, grad)


def gate_up_kernel(
    wide, own_ref, wg_ref, wu_ref, all_ref, gate_ref, up_ref, hid_ref, core_ref,
    full, stage, own_sem, send_sem, recv_sem, out_sem, all_sem,
):
    rows = own_ref.shape[0]
    cols = gate_ref.shape[1]
    ring = Ring(wide, full, rows, send_sem, recv_sem)
    local = pltpu.make_async_copy(own_ref, full.at[ring.mine()], own_sem)
    local.start()
    meet(ring.peers)
    local.wait()
    ring.start_own()

    def out_copies(slot, places):
        where, core, chip = places
        return [
            pltpu.make_async_copy(stage.at[slot, i], ref.at[where], out_sem.at[slot, i])
            for i, ref in enumerate((gate_ref, up_ref, hid_ref))
        ] + [
            pltpu.make_async_copy(stage.at[slot, 2], core_ref.at[core, chip], out_sem.at[slot, 3]),
            pltpu.make_async_copy(full.at[where], all_ref.at[where], all_sem.at[slot]),
        ]

    def step_place(step):
        phase, i = step // 4, step % 4
        high, low = phase // 2, phase % 2
        first, last = (1 - high) * (1 - low), high * low
        middle = high + low - 2 * last
        half = (first + last) * (i % 2) + high * (1 - low)
        dx = middle * (1 - i % 2) + last
        dy = middle * (i % 2) + last
        part = rows // 2
        chip_rows = pl.ds(pl.multiple_of((2 * dy + dx) * rows + half * part, part), part)
        return ring.place(dy, dx, i // 2, half), i // 2, chip_rows

    @pl.loop(0, 16)
    def _(step):
        pl.when(step == 2)(lambda: ring.from_sibling("own", 0, 1))
        pl.when(step == 4)(ring.first_halves)

        @pl.when(step == 6)
        def _():
            ring.from_sibling("x", 0)
            ring.from_sibling("y", 0)

        pl.when(step == 8)(ring.second_halves)

        @pl.when(step == 10)
        def _():
            ring.from_sibling("x", 1)
            ring.from_sibling("y", 1)

        pl.when(step == 12)(ring.far_halves)
        pl.when(step == 14)(lambda: ring.from_sibling("d", 0, 1))

        slot = step % 2
        places = step_place(step)

        @pl.when(step >= 2)
        def _():
            for copy in out_copies(slot, step_place(step - 2)):
                copy.wait()

        x = full[places[0], :]

        @pl.loop(0, cols // NTILE)
        def _(at):
            n = pl.ds(pl.multiple_of(at * NTILE, NTILE), NTILE)
            gate = dot_nn(x, wg_ref[:, n])
            up = dot_nn(x, wu_ref[:, n])
            stage[slot, 0, :, n] = gate.astype(BF16)
            stage[slot, 1, :, n] = up.astype(BF16)
            stage[slot, 2, :, n] = (gate * up / (1.0 + jnp.exp(-gate))).astype(BF16)

        for copy in out_copies(slot, places):
            copy.start()

    for step in (14, 15):
        for copy in out_copies(step % 2, step_place(step)):
            copy.wait()
    ring.sent()


def gate_up(hn, wg, wu, dp_size):
    rows, width = hn.shape
    cols = wg.shape[1]
    tokens = GROUP * rows
    far = pl.BlockSpec(memory_space=pl.ANY)
    near = pl.BlockSpec(memory_space=pltpu.VMEM)
    return pl.pallas_call(
        functools.partial(gate_up_kernel, 2 * math.isqrt(dp_size // GROUP)),
        in_specs=[far, near, near],
        out_specs=[far] * 5,
        out_shape=[jax.ShapeDtypeStruct((tokens, width), BF16)]
        + [jax.ShapeDtypeStruct((tokens, cols), BF16)] * 3
        + [jax.ShapeDtypeStruct((2, tokens // 2, cols), BF16)],
        scratch_shapes=[
            pltpu.VMEM((tokens, width), BF16),
            pltpu.VMEM((2, 3, rows // 2, cols), BF16),
            pltpu.SemaphoreType.DMA,
            pltpu.SemaphoreType.DMA((Ring.COPIES,)),
            pltpu.SemaphoreType.DMA((Ring.COPIES,)),
            pltpu.SemaphoreType.DMA((2, 4)),
            pltpu.SemaphoreType.DMA((2,)),
        ],
        compiler_params=pltpu.CompilerParams(
            collective_id=1, has_side_effects=True, vmem_limit_bytes=56 << 20
        ),
        cost_estimate=pl.CostEstimate(
            flops=SHORT, bytes_accessed=0, transcendentals=0
        ),
    )(hn, wg, wu)


FAR_CHUNK, X_CHUNK, Y_CHUNK, OWN_CHUNK = range(4)


class Reduce:
    COPIES = 10

    def __init__(self, wide, parts, cores, far, near, send_sem, recv_sem):
        self.at, self.peers = neighbours(wide)
        self.parts, self.cores, self.far, self.near = parts, cores, far, near
        self.send_sem, self.recv_sem = send_sem, recv_sem
        self.half = parts.shape[2] // 2

    @staticmethod
    def scratch(rows, cols):
        return [
            pltpu.VMEM((2, 4, rows, cols), BF16),
            pltpu.VMEM((4, rows, cols), BF16),
            pltpu.VMEM((2, rows // 2, cols), BF16),
            pltpu.VMEM((2, rows, cols), BF16),
            pltpu.SemaphoreType.DMA((Reduce.COPIES,)),
            pltpu.SemaphoreType.DMA((Reduce.COPIES,)),
        ]

    def chunk(self, step):
        slot, other = step // 2, 1 - step % 2
        row, col, core = self.at
        dy, dx = 1 - slot % 2, 1 - slot // 2
        place = 4 * ((row + dy) % 2) + 2 * ((col + dx) % 2) + (core + other) % 2
        return place, self.parts.at[other, slot]

    def copy(self, name):
        upper, lower = pl.ds(0, self.half), pl.ds(self.half, self.half)
        mine = self.parts.at[0]
        table = {
            "far0": (self.parts.at[1, FAR_CHUNK], self.cores.at[FAR_CHUNK], SIB),
            "x": (self.parts.at[1, X_CHUNK], self.cores.at[X_CHUNK], SIB),
            "y": (self.parts.at[1, Y_CHUNK], self.cores.at[Y_CHUNK], SIB),
            "own": (self.parts.at[1, OWN_CHUNK], self.cores.at[OWN_CHUNK], SIB),
            "far_x": (mine.at[FAR_CHUNK, lower], self.far.at[0], XN),
            "far_y": (mine.at[FAR_CHUNK, upper], self.far.at[1], YN),
            "x_upper": (mine.at[X_CHUNK, upper], self.near.at[0, upper], XN),
            "x_lower": (mine.at[X_CHUNK, lower], self.near.at[0, lower], XN),
            "y_upper": (mine.at[Y_CHUNK, upper], self.near.at[1, upper], YN),
            "y_lower": (mine.at[Y_CHUNK, lower], self.near.at[1, lower], YN),
        }
        src, dst, peer = table[name]
        at = list(table).index(name)
        return pltpu.make_async_remote_copy(
            src_ref=src, dst_ref=dst, send_sem=self.send_sem.at[at],
            recv_sem=self.recv_sem.at[at], device_id={"dp": self.peers[peer]},
            device_id_type=MESH,
        )

    def start(self, *names):
        for name in names:
            self.copy(name).start()

    def add(self, slot, start, other):
        count = other.shape[0] // STRIP

        @pl.loop(0, count)
        def _(at):
            here = pl.ds(pl.multiple_of(start + at * STRIP, STRIP), STRIP)
            there = pl.ds(pl.multiple_of(at * STRIP, STRIP), STRIP)
            value = self.parts[0, slot, here, :].astype(F32) + other[there, :].astype(F32)
            self.parts[0, slot, here, :] = value.astype(BF16)

    def merge_core(self, slot, name):
        self.copy(name).wait_recv()
        self.add(slot, 0, self.cores.at[slot])

    def after(self, step):
        names = ("far0", "x", "y", "own")
        for slot in range(4):
            pl.when(step == 2 * slot)(functools.partial(self.start, names[slot]))

        @pl.when(step == 1)
        def _():
            self.merge_core(FAR_CHUNK, "far0")
            self.start("far_x", "far_y")

        @pl.when(step == 3)
        def _():
            self.merge_core(X_CHUNK, "x")
            self.start("x_lower")

        @pl.when(step == 5)
        def _():
            self.merge_core(Y_CHUNK, "y")
            self.start("y_upper")

    def pass_on(self):
        self.copy("far_y").wait_recv()
        self.add(X_CHUNK, 0, self.far.at[1])
        self.start("x_upper")
        self.copy("far_x").wait_recv()
        self.add(Y_CHUNK, self.half, self.far.at[0])
        self.start("y_lower")

    def finish(self, store):
        for name in ("own", "x_upper", "x_lower", "y_upper", "y_lower"):
            self.copy(name).wait_recv()

        @pl.loop(0, 2 * self.half // STRIP)
        def _(at):
            here = pl.ds(pl.multiple_of(at * STRIP, STRIP), STRIP)
            value = self.parts[0, OWN_CHUNK, here, :].astype(F32)
            value += self.cores[OWN_CHUNK, here, :].astype(F32)
            value += self.near[0, here, :].astype(F32)
            value += self.near[1, here, :].astype(F32)
            store(here, value)

    def sent(self):
        for name in (
            "far0", "x", "y", "own", "far_x", "far_y", "x_upper", "x_lower", "y_upper", "y_lower",
        ):
            self.copy(name).wait_send()


def hidden_back_kernel(
    wide, dgate_ref, dup_ref, wg_ref, wu_ref, out_ref, loaded, load_sem, *scratch
):
    ring = Reduce(wide, *scratch)
    rows = out_ref.shape[0]

    def loads(step):
        chunk, _ = ring.chunk(step)
        here = pl.ds(pl.multiple_of(chunk * rows, rows), rows)
        return [
            pltpu.make_async_copy(
                ref.at[here], loaded.at[step % 2, at], load_sem.at[step % 2, at]
            )
            for at, ref in enumerate((dgate_ref, dup_ref))
        ]

    for copy in loads(0):
        copy.start()
    meet(ring.peers)

    @pl.loop(0, 8)
    def _(step):
        @pl.when(step < 7)
        def _():
            for copy in loads(step + 1):
                copy.start()

        for copy in loads(step):
            copy.wait()
        _, target = ring.chunk(step)
        dgate, dup = loaded[step % 2, 0], loaded[step % 2, 1]

        @pl.loop(0, out_ref.shape[1] // NTILE)
        def _(at):
            n = pl.ds(pl.multiple_of(at * NTILE, NTILE), NTILE)
            value = dot_nt(dgate, wg_ref[n, :]) + dot_nt(dup, wu_ref[n, :])
            target[:, n] = value.astype(BF16)

        ring.after(step)

    ring.pass_on()

    def store(here, value):
        out_ref[here, :] = value

    ring.finish(store)
    ring.sent()


def hidden_back(dgate, dup, wg, wu, dp_size):
    tokens, cols = dgate.shape
    width = wg.shape[0]
    rows = tokens // GROUP
    far = pl.BlockSpec(memory_space=pl.ANY)
    near = pl.BlockSpec(memory_space=pltpu.VMEM)
    return pl.pallas_call(
        functools.partial(hidden_back_kernel, 2 * math.isqrt(dp_size // GROUP)),
        in_specs=[far, far, near, near],
        out_specs=near,
        out_shape=jax.ShapeDtypeStruct((rows, width), F32),
        scratch_shapes=[
            pltpu.VMEM((2, 2, rows, cols), BF16),
            pltpu.SemaphoreType.DMA((2, 2)),
        ]
        + Reduce.scratch(rows, width),
        compiler_params=pltpu.CompilerParams(
            collective_id=6, has_side_effects=True, vmem_limit_bytes=60 << 20
        ),
        cost_estimate=pl.CostEstimate(
            flops=4 * tokens * width * cols,
            bytes_accessed=4 * tokens * cols + 4 * width * cols + 4 * rows * width,
            transcendentals=0,
        ),
    )(dgate, dup, wg, wu)


def tail_kernel(
    wide, z_size, mlp_count, x_ref, dq_ref, dkv_ref, wo_ref, scale_ref, gain_ref,
    raw_ref, dh_ref, wq_ref, wkv_ref, *refs
):
    mlp_ins, refs = refs[:mlp_count], refs[mlp_count:]
    wq_out, wkv_out, wo_out, gain_out, grad_out = refs[:5]
    mlp_outs, scratch = refs[5 : 5 + mlp_count], refs[5 + mlp_count :]
    own_scratch = scratch[:12]
    sums, zrecv, gain_z, gain_p, z_send, z_recv, g_send, g_recv = scratch[12:20]
    wo_recv, w_send, w_recv, m_own, m_send, m_recv = scratch[20:26]
    wq_all, wkv_all, raw, dh, dxn, gain_sum, load_sem = scratch[26:]
    rings = [Reduce(wide, *own_scratch[6 * at : 6 * at + 6]) for at in range(2)]
    place = lax.axis_index("tensor")
    mine, found = others(wide)
    along = along_peers(place, z_size)
    around = [device for _, device in found]

    tiles, tile_rows = raw.shape[0], raw.shape[1]
    loads = [
        pltpu.make_async_copy(wq_ref, wq_all, load_sem.at[0]),
        pltpu.make_async_copy(wkv_ref, wkv_all, load_sem.at[1]),
    ]
    for tile in range(tiles):
        here = pl.ds(tile * tile_rows, tile_rows)
        loads += [
            pltpu.make_async_copy(raw_ref.at[here], raw.at[tile], load_sem.at[2 + 2 * tile]),
            pltpu.make_async_copy(dh_ref.at[here], dh.at[tile], load_sem.at[3 + 2 * tile]),
        ]
    for copy in loads:
        copy.start()
    greet(along + around)

    mlp_copies = send_home(wide, mlp_ins, mlp_outs, m_own, m_send, m_recv)
    wo_part = wo_out.shape[1]
    wo_copies = [
        pltpu.make_async_remote_copy(
            src_ref=wo_ref.at[
                :,
                pl.ds(pl.multiple_of((place + at + 1) % z_size * wo_part, LANES), wo_part),
            ],
            dst_ref=wo_recv.at[at], send_sem=w_send.at[at], recv_sem=w_recv.at[at],
            device_id=peer, device_id_type=MESH,
        )
        for at, peer in enumerate(along)
    ]
    for copy in wo_copies:
        copy.start()

    rights = (dq_ref, dkv_ref)
    rows = sums.shape[0]
    outs = (wq_out, wkv_out)
    starts = [0, rights[0].shape[1]]
    z_copies = []

    def partial_sums(index):
        ring, right = rings[index], rights[index]

        @pl.loop(0, 8)
        def _(step):
            chunk, target = ring.chunk(step)
            x = x_ref[:, pl.ds(pl.multiple_of(chunk * rows, rows), rows)].T

            @pl.loop(0, right.shape[1] // NTILE)
            def _(at):
                n = pl.ds(pl.multiple_of(at * NTILE, NTILE), NTILE)
                target[:, n] = dot_nn(x, right[:, n]).astype(BF16)

            ring.after(step)

    gain_sum[...] = jnp.zeros_like(gain_sum)

    def input_rows(tile):
        part = pl.ds(tile * tile_rows, tile_rows)
        dq, dkv = dq_ref[part, :], dkv_ref[part, :]

        @pl.loop(0, dxn.shape[1] // NTILE)
        def _(at):
            n = pl.ds(pl.multiple_of(at * NTILE, NTILE), NTILE)
            dxn[:, n] = dot_nt(dq, wq_all[n, :]) + dot_nt(dkv, wkv_all[n, :])

        @pl.loop(0, tile_rows // STRIP)
        def _(at):
            here = pl.ds(pl.multiple_of(at * STRIP, STRIP), STRIP)
            there = pl.ds(pl.multiple_of(tile * tile_rows + at * STRIP, STRIP), STRIP)
            grad, value = dxn[here, :], raw[tile, here, :].astype(F32)
            scale = scale_ref[there, :]
            gained = grad * gain_ref[0:1, :]
            inner = jnp.mean(gained * value, axis=1, keepdims=True)
            gain_sum[...] += grad * value * scale
            total = scale * gained - value * (scale * scale * scale * inner)
            grad_out[there, :] = (dh[tile, here, :] + total).astype(BF16)

    def send_along(index):
        ring, start = rings[index], starts[index]
        cols = rights[index].shape[1]
        part = cols // z_size

        def store(here, value):
            sums[here, pl.ds(start, cols)] = value.astype(BF16)

        ring.finish(store)
        for at, peer in enumerate(along):
            other = (place + at + 1) % z_size
            copy = pltpu.make_async_remote_copy(
                src_ref=sums.at[:, pl.ds(pl.multiple_of(start + other * part, LANES), part)],
                dst_ref=zrecv.at[at, :, pl.ds(start // z_size, part)],
                send_sem=z_send.at[index, at], recv_sem=z_recv.at[index, at],
                device_id=peer, device_id_type=MESH,
            )
            z_copies.append(copy)
            copy.start()

    partial_sums(0)
    for copy in loads:
        copy.wait()
    input_rows(0)
    rings[0].pass_on()
    partial_sums(1)
    for tile in range(1, tiles):
        input_rows(tile)

    gain_z[place, 0:1] = jnp.sum(gain_sum[...], axis=0, keepdims=True)
    gain_z[place, 1:2] = gain_ref[1:2, :]
    gain_copies = [
        pltpu.make_async_remote_copy(
            src_ref=gain_z.at[place], dst_ref=gain_z.at[place], send_sem=g_send.at[at],
            recv_sem=g_recv.at[at], device_id=peer, device_id_type=MESH,
        )
        for at, peer in enumerate(along)
    ]
    for copy in gain_copies:
        copy.start()
    rings[1].pass_on()
    for copy in mlp_copies:
        copy.start()
    send_along(0)

    for copy in gain_copies:
        copy.wait_recv()
    total = gain_z[0]
    for at in range(1, z_size):
        total = total + gain_z[at]
    gain_p[mine] = total
    for at, peer in enumerate(around):
        copy = pltpu.make_async_remote_copy(
            src_ref=gain_p.at[mine], dst_ref=gain_p.at[mine],
            send_sem=g_send.at[z_size - 1 + at], recv_sem=g_recv.at[z_size - 1 + at],
            device_id=peer, device_id_type=MESH,
        )
        gain_copies.append(copy)
        copy.start()
    for copy in wo_copies:
        copy.wait()
    total = wo_ref[:, pl.ds(pl.multiple_of(place * wo_part, LANES), wo_part)].astype(F32)
    for at in range(z_size - 1):
        total += wo_recv[at].astype(F32)
    wo_out[...] = total
    send_along(1)

    for copy in gain_copies[z_size - 1 :]:
        copy.wait_recv()
    total = gain_p[0]
    for at in range(1, GROUP):
        total = total + gain_p[at]
    gain_out[...] = total
    for copy in z_copies:
        copy.wait_recv()
    for index in range(2):
        part = rights[index].shape[1] // z_size
        own = pl.ds(pl.multiple_of(starts[index] + place * part, LANES), part)
        value = sums[:, own].astype(F32)
        for at in range(z_size - 1):
            value += zrecv[at, :, pl.ds(starts[index] // z_size, part)].astype(F32)
        outs[index][...] = value
    for copy in z_copies + gain_copies:
        copy.wait_send()
    for ring in rings:
        ring.sent()
    for copy in mlp_copies:
        copy.wait()


def last_grads(x, dq, dkv, wo_sum, scale, gains, raw, dh, wq, wkv, mlp, dp_size, z_size):
    tokens, width = x.shape
    rows = width // GROUP
    tiles = tokens // QTILE
    near = pl.BlockSpec(memory_space=pltpu.VMEM)
    far = pl.BlockSpec(memory_space=pl.ANY)
    sizes = [dq.shape[1], dkv.shape[1]]
    scratch = []
    for cols in sizes:
        scratch += Reduce.scratch(rows, cols)
    total = sum(sizes)
    return pl.pallas_call(
        functools.partial(tail_kernel, 2 * math.isqrt(dp_size // GROUP), z_size, len(mlp)),
        in_specs=[near] * 6 + [far] * (4 + len(mlp)),
        out_specs=[near] * 5 + [far] * len(mlp),
        out_shape=[jax.ShapeDtypeStruct((rows, cols // z_size), F32) for cols in sizes]
        + [
            jax.ShapeDtypeStruct((rows, wo_sum.shape[1] // z_size), F32),
            jax.ShapeDtypeStruct(gains.shape, F32),
            jax.ShapeDtypeStruct((tokens, width), BF16),
        ]
        + home_shapes(mlp),
        scratch_shapes=scratch
        + [
            pltpu.VMEM((rows, total), BF16),
            pltpu.VMEM((z_size - 1, rows, total // z_size), BF16),
            pltpu.VMEM((z_size, *gains.shape), F32),
            pltpu.VMEM((GROUP, *gains.shape), F32),
            pltpu.SemaphoreType.DMA((2, z_size - 1)),
            pltpu.SemaphoreType.DMA((2, z_size - 1)),
            pltpu.SemaphoreType.DMA((z_size - 1 + GROUP - 1,)),
            pltpu.SemaphoreType.DMA((z_size - 1 + GROUP - 1,)),
            pltpu.VMEM((z_size - 1, rows, wo_sum.shape[1] // z_size), BF16),
            pltpu.SemaphoreType.DMA((z_size - 1,)),
            pltpu.SemaphoreType.DMA((z_size - 1,)),
        ]
        + home_scratch(mlp)
        + [
            pltpu.VMEM(wq.shape, BF16),
            pltpu.VMEM(wkv.shape, BF16),
            pltpu.VMEM((tiles, QTILE, width), BF16),
            pltpu.VMEM((tiles, QTILE, width), F32),
            pltpu.VMEM((QTILE, width), F32),
            pltpu.VMEM((STRIP, width), F32),
            pltpu.SemaphoreType.DMA((2 + 2 * tiles,)),
        ],
        compiler_params=pltpu.CompilerParams(
            collective_id=4, has_side_effects=True, vmem_limit_bytes=62 << 20
        ),
        cost_estimate=pl.CostEstimate(flops=SHORT, bytes_accessed=0, transcendentals=0),
    )(x, dq, dkv, wo_sum, scale, gains, raw, dh, wq, wkv, *mlp)


class Layout:
    def __init__(self, dp_size):
        self.blocks = dp_size // GROUP
        side = math.isqrt(self.blocks)
        self.rows, self.cols = side, self.blocks // side
        wide = 2 * self.cols

        def index(by, bx, y, x, core):
            return ((2 * by + y) * wide + 2 * bx + x) * 2 + core

        places = [(y, x, c) for y in range(2) for x in range(2) for c in range(2)]
        spots = [(by, bx) for by in range(self.rows) for bx in range(self.cols)]
        self.inner = [[index(*s, *p) for p in places] for s in spots]
        self.outer = [[index(*s, *p) for s in spots] for p in places]

    def groups(self):
        return None if self.blocks == 1 else self.inner

    def to_rows(self, array):
        if self.blocks == 1:
            return array
        rest = array.shape[1:]
        split = array.reshape(2, 2, 2, self.rows, self.cols, -1, *rest)
        order = (3, 0, 4, 1, 2, 5) + tuple(range(6, 6 + len(rest)))
        return split.transpose(order).reshape(array.shape)

    def from_rows(self, array):
        if self.blocks == 1:
            return array
        rest = array.shape[1:]
        split = array.reshape(self.rows, 2, self.cols, 2, 2, -1, *rest)
        order = (1, 3, 4, 0, 2, 5) + tuple(range(6, 6 + len(rest)))
        return split.transpose(order).reshape(array.shape)

    def from_cols(self, array):
        return array if self.blocks == 1 else self.from_rows(array.T).T

    def gather_outer(self, array):
        if self.blocks == 1:
            return array
        return lax.all_gather(array, "dp", axis_index_groups=self.outer, axis=0, tiled=True)

    def scatter_outer(self, array):
        if self.blocks == 1:
            return array
        return lax.psum_scatter(
            array, "dp", scatter_dimension=0, axis_index_groups=self.outer, tiled=True
        )

    def swap(self, array, flip):
        pairs = [
            (block[at], block[at ^ flip]) for block in self.inner for at in range(GROUP)
        ]
        return lax.ppermute(array, "dp", pairs)

    def sum_outer(self, array):
        if self.blocks == 1:
            return array
        return lax.psum(array, "dp", axis_index_groups=self.outer)

    def gather(self, array):
        return lax.all_gather(array, "dp", axis_index_groups=self.groups(), axis=0, tiled=True)

    def scatter(self, array):
        return lax.psum_scatter(
            array, "dp", scatter_dimension=0, axis_index_groups=self.groups(), tiled=True
        )


def rms_scale(values):
    return lax.rsqrt(jnp.mean(values * values, axis=-1, keepdims=True) + NORM_EPS)


def norm_back(values, scaling, gain, grad):
    gained = grad * gain
    gain_part = jnp.sum(grad * values * scaling, axis=0)
    inner = jnp.mean(gained * values, axis=-1, keepdims=True)
    return gain_part, scaling * gained - values * scaling * scaling * scaling * inner


def per_device(
    dp_size, z_size, activations, segment_ids, attn_gain, w_query, w_key, w_value, w_out,
    mlp_gain, w_gate, w_up, w_down, cotangent,
):
    layout = Layout(dp_size)
    rows, width = activations.shape[1:]
    x = activations[0].astype(F32)
    place = lax.axis_index("tensor")
    reach = -(-(MOST_DOC - 1) // rows) * rows

    def shift(array, step):
        pairs = [(at, at + step) for at in range(z_size) if 0 <= at + step < z_size]
        return lax.ppermute(array, "tensor", pairs)

    starts = document_starts(segment_ids[0])
    own_starts = lax.dynamic_slice_in_dim(starts, place * rows, rows)
    own_tokens = place * rows + jnp.arange(rows, dtype=jnp.int32)
    cosine, sine = rope_tables(own_tokens - own_starts)
    low = (own_starts - place * rows + reach)[None, :]

    shards = [
        layout.gather_outer(w)
        for w in (w_gate, w_up, w_down, jnp.concatenate([w_key, w_value], axis=1), w_query, w_out)
    ]
    spread = spread_weights(shards[:3], shards[3:], dp_size, z_size)
    def gather_z(array):
        return layout.to_rows(lax.all_gather(array, "tensor", axis=1, tiled=True))

    wg, wu = gather_z(spread[0]), gather_z(spread[1])

    def along_z(total):
        return lax.psum_scatter(
            layout.from_rows(total), "tensor", scatter_dimension=1, tiled=True
        )

    r1 = rms_scale(x)
    xn = (x * r1 * attn_gain).astype(BF16)
    q, kv_all, wkv, wq, wo, dy = project(
        layout.from_cols(xn), cosine, sine, *spread[3:], cotangent[0], reach, dp_size, z_size
    )
    wd = gather_z(spread[2])
    wkv, wq, wo = layout.to_rows(wkv), layout.to_rows(wq), layout.to_rows(wo)
    att, lse, dy = attend(q, kv_all, low, cotangent[0], dy, dp_size)
    h = x + dot_nt(att, wo)

    r2 = rms_scale(h)
    hn, gate, up, hidden, by_core = gate_up((h * r2 * mlp_gain).astype(BF16), wg, wu, dp_size)
    part = rows // 2
    away = dot_nt(by_core[1], wd).astype(BF16)
    dy, away = lax.optimization_barrier((dy, away))
    total_wd = dot_tn(dy, hidden).astype(BF16)
    part_wd = along_z(total_wd)
    from_core = layout.swap(away, 1)

    def out_rows(start, count, *more):
        some = slice(start * part, (start + count) * part)
        total = dot_nt(by_core[0, some], wd) + from_core[some].astype(F32)
        for other in more:
            total = total + other.astype(F32)
        return total.astype(BF16)

    far_y, far_x = out_rows(6, 1), out_rows(7, 1)
    dy, far_x, far_y = lax.optimization_barrier((dy, far_x, far_y))
    from_x, from_y = layout.swap(far_x, 2), layout.swap(far_y, 4)
    gate, up = gate.astype(F32), up.astype(F32)
    sigma = jax.nn.sigmoid(gate)
    dhid = dot_nn(dy, wd)
    dgate = (dhid * up * sigma * (1.0 + gate * (1.0 - sigma))).astype(BF16)
    dup = (dhid * gate * sigma).astype(BF16)
    dgate, dup, from_x, from_y = lax.optimization_barrier((dgate, dup, from_x, from_y))
    pieces = (out_rows(2, 1, from_y), out_rows(3, 1), out_rows(4, 1), out_rows(5, 1, from_x))
    dgate, dup, *pieces = lax.optimization_barrier((dgate, dup, *pieces))
    total_wg = dot_tn(hn, dgate).astype(BF16)
    dup, total_wg = lax.optimization_barrier((dup, total_wg))
    part_wg = along_z(total_wg)
    total_wu = dot_tn(hn, dup).astype(BF16)
    dup, total_wu = lax.optimization_barrier((dup, total_wu))
    part_wu = along_z(total_wu)
    dhn = hidden_back(dgate, dup, wg, wu, dp_size)
    dhn, part_wd, *pieces = lax.optimization_barrier((dhn, part_wd, *pieces))
    pieces = [layout.swap(piece, flip) for piece, flip in zip(pieces, (2, 2, 4, 4))]
    gain_two, dh_norm = norm_back(h, r2, mlp_gain, dhn)
    dh = cotangent[0].astype(F32) + dh_norm
    dhb = dh.astype(BF16)
    datt = dot_nn(dhb, wo).astype(BF16)
    total_wo = layout.from_rows(dot_tn(dhb, att).astype(BF16))
    datt, part_wg, total_wo = lax.optimization_barrier((datt, part_wg, total_wo))
    part_wo = layout.scatter(total_wo)
    dq, dkv, wd_grad, wg_grad = attend_back(
        q, datt, att, kv_all, lse, low, cosine, sine, (part_wd, part_wg), dp_size, z_size
    )
    dq, part_wu = lax.optimization_barrier((dq, part_wu))
    dq, part_wo = lax.optimization_barrier((dq, part_wo))
    wq_grad, wkv_grad, wo_grad, gains, input_grad, wu_grad = last_grads(
        layout.from_cols(xn), dq, dkv, part_wo, r1, jnp.stack([attn_gain, gain_two]),
        activations[0], dh, wq, wkv, (part_wu,), dp_size, z_size,
    )
    gains = layout.sum_outer(gains)
    gains, *pieces = lax.optimization_barrier((gains, *pieces))
    output = h + out_rows(0, 2).astype(F32)
    output = output + jnp.concatenate(pieces[:2]).astype(F32)
    output = output + jnp.concatenate(pieces[2:]).astype(F32)
    wo_grad, wq_grad, wkv_grad, wd_grad, wg_grad, wu_grad = (
        layout.scatter_outer(grad).astype(F32)
        for grad in (wo_grad, wq_grad, wkv_grad, wd_grad, wg_grad, wu_grad)
    )
    key_cols = w_key.shape[1]
    return (
        output.astype(BF16)[None],
        input_grad[None],
        gains[0],
        wq_grad,
        wkv_grad[:, :key_cols],
        wkv_grad[:, key_cols:],
        wo_grad,
        gains[1],
        wg_grad,
        wu_grad,
        wd_grad,
    )


def solution(mesh):
    split = P("dp", "tensor")
    tokens = P("dp", "tensor", None)
    in_specs = (
        tokens, P("dp", None), P(), split, split, split, split, P(), split, split, split, tokens,
    )
    out_specs = (tokens, tokens, P(), split, split, split, split, P(), split, split, split)
    return jax.shard_map(
        functools.partial(per_device, mesh.shape["dp"], mesh.shape["tensor"]),
        mesh=mesh, in_specs=in_specs, out_specs=out_specs, check_vma=False,
    )
```

```python
import functools
import math

import jax
import jax.numpy as jnp
from jax import lax
from jax.experimental import pallas as pl
from jax.experimental.pallas import tpu as pltpu
from jax.sharding import PartitionSpec as P

HEAD_DIM = 64
DOCS = 4
MOST_DOC = 1024
NORM_EPS = 1e-05
ROPE_THETA = 500000.0
GROUP = 8
LANES = 128
QTILE = 256
SCALE = HEAD_DIM ** (-0.5)
LOG2E = 1.4426950408889634
FAR = -1e30
NTILE = 512
STRIP = 16
LONG = 60_000_000_000
SHORT = 1_000_000

F32 = jnp.float32
BF16 = jnp.bfloat16


def dot_nn(left, right):
    return lax.dot_general(left, right, (((1,), (0,)), ((), ())), preferred_element_type=F32)


def dot_nt(left, right):
    return lax.dot_general(left, right, (((1,), (1,)), ((), ())), preferred_element_type=F32)


def dot_tn(left, right):
    return lax.dot_general(left, right, (((0,), (0,)), ((), ())), preferred_element_type=F32)


def document_starts(segments):
    doc_ids = jnp.arange(DOCS, dtype=jnp.int32)
    counts = jnp.sum((segments[:, None] == doc_ids).astype(jnp.int32), axis=0)
    before = (doc_ids < segments[:, None]).astype(jnp.int32)
    return jnp.sum(before * counts[None, :], axis=-1)


def rope_tables(positions):
    half = HEAD_DIM // 2
    frequency = jnp.exp(
        jnp.arange(half, dtype=F32) * (-2.0 * math.log(ROPE_THETA) / HEAD_DIM)
    )
    angles = positions.astype(F32)[:, None] * frequency
    cosine, sine = jnp.cos(angles), jnp.sin(angles)
    wide_cos = jnp.concatenate([cosine] * 4, axis=1)
    wide_sin = jnp.concatenate([-sine, sine, -sine, sine], axis=1)
    return wide_cos, wide_sin


def swap_halves(values):
    lane = lax.broadcasted_iota(jnp.int32, values.shape, 1)
    ahead = pltpu.roll(values, LANES - 32, 1)
    behind = pltpu.roll(values, 32, 1)
    return jnp.where((lane % 64) < 32, ahead, behind)


def fill_bias(bias_ref, low_ref, reach):
    span = bias_ref.shape[1]
    for tile in range(bias_ref.shape[0]):
        row = lax.broadcasted_iota(jnp.int32, (span, QTILE), 0)
        col = lax.broadcasted_iota(jnp.int32, (span, QTILE), 1)
        low = low_ref[0:1, tile * QTILE : (tile + 1) * QTILE]
        allowed = (row <= reach + col) & (row + tile * QTILE >= low)
        bias_ref[tile] = jnp.where(allowed, 0.0, FAR)


def spread_pair(pair, half):
    wide = pair.astype(F32)
    turned = pltpu.roll(wide, 64, 1)
    lane = lax.broadcasted_iota(jnp.int32, wide.shape, 1)
    mine = (lane // 64) == half
    even = half == 0
    first = jnp.where(mine, jnp.where(even, wide, turned), 0.0)
    second = jnp.where(mine, jnp.where(even, turned, wide), 0.0)
    return jnp.concatenate([first, second], axis=0).astype(BF16)


def gather_pair(transposed, half):
    count = transposed.shape[1] // 2
    mine = jnp.where(half == 0, transposed[:64], transposed[64:])
    return jnp.concatenate([mine[:, :count], mine[:, count:]], axis=0).T


def attend_kernel(
    reach, wide, q_ref, k_ref, v_ref, low_ref, own_ref, _, att_ref, lse_ref, all_ref,
    bias_ref, full, own_sem, send_sem, recv_sem, out_sem,
):
    head, tile, pair = pl.program_id(0), pl.program_id(1), pl.program_id(2)
    half = head % 2
    inner = pl.num_programs(1) * pl.num_programs(2)
    step = head * inner + tile * pl.num_programs(2) + pair
    ring = Ring(wide, full, own_ref.shape[0], send_sem, recv_sem)
    right = pl.ds(own_ref.shape[1] - full.shape[1], full.shape[1])

    def outward(slot, *flips):
        where = ring.whole(*flips)
        return pltpu.make_async_copy(full.at[where], all_ref.at[where, right], out_sem.at[slot])

    near = [(0, 0, 0), (0, 0, 1), (0, 1, 0), (1, 0, 0)]
    rest = [(0, 1, 1), (1, 0, 1), (1, 1, 0), (1, 1, 1)]

    @pl.when(step == 0)
    def _():
        local = pltpu.make_async_copy(own_ref.at[:, right], full.at[ring.mine()], own_sem)
        local.start()
        meet(ring.peers)
        local.wait()
        ring.start_own()
        fill_bias(bias_ref, low_ref, reach)

    pl.when(step == 2 * inner)(ring.first_halves)
    pl.when(step == 4 * inner)(ring.second_halves)

    keys = pl.ds(pl.multiple_of(tile * QTILE, QTILE), bias_ref.shape[1])
    queries = spread_pair(q_ref[...], half)
    bias = bias_ref[tile]
    score = dot_nt(k_ref[keys, :], queries)
    score = score + jnp.concatenate([bias, bias], axis=1)
    top = jnp.max(score, axis=0, keepdims=True) * (SCALE * LOG2E)
    weight = jnp.exp2(score * (SCALE * LOG2E) - top)
    total = jnp.sum(weight, axis=0, keepdims=True)
    result = dot_tn(v_ref[keys, :], weight.astype(BF16)) / total
    att_ref[...] = gather_pair(result, half).astype(BF16)
    lse_ref[0] = top + jnp.log2(total)

    @pl.when(step == pl.num_programs(0) * inner - 1)
    def _():
        ring.from_sibling("own", 0, 1)
        for slot, flips in enumerate(near):
            outward(slot, *flips).start()
        ring.far_halves()
        for name in ("x", "y", "d"):
            ring.from_sibling(name, 0, 1)
        for slot, flips in enumerate(rest):
            outward(4 + slot, *flips).start()
        for slot, flips in enumerate(near + rest):
            outward(slot, *flips).wait()
        ring.sent()


def attend(q, kv, low, grad, grads, dp_size):
    rows, width = q.shape
    keys = kv.shape[0]
    reach = keys - rows
    tiles = rows // QTILE
    pairs = width // LANES
    heads = kv.shape[1] // LANES
    per_head = pairs // heads
    span = reach + QTILE
    right = (grads.shape[0], grads.shape[1] * 5 // 8)
    far = pl.BlockSpec(memory_space=pl.ANY)
    return pl.pallas_call(
        functools.partial(attend_kernel, reach, 2 * math.isqrt(dp_size // GROUP)),
        grid=(heads, tiles, per_head),
        in_specs=[
            pl.BlockSpec((QTILE, LANES), lambda a, t, p: (t, a * per_head + p)),
            pl.BlockSpec((keys, LANES), lambda a, t, p: (0, 2 * (a // 2))),
            pl.BlockSpec((keys, LANES), lambda a, t, p: (0, 2 * (a // 2) + 1)),
            pl.BlockSpec((1, rows), lambda a, t, p: (0, 0)),
            far,
            far,
        ],
        out_specs=[
            pl.BlockSpec((QTILE, LANES), lambda a, t, p: (t, a * per_head + p)),
            pl.BlockSpec((1, 1, 2 * QTILE), lambda a, t, p: ((a * tiles + t) * per_head + p, 0, 0)),
            far,
        ],
        out_shape=[
            jax.ShapeDtypeStruct((rows, width), BF16),
            jax.ShapeDtypeStruct((pairs * tiles, 1, 2 * QTILE), F32),
            jax.ShapeDtypeStruct(grads.shape, BF16),
        ],
        scratch_shapes=[
            pltpu.VMEM((tiles, span, QTILE), F32),
            pltpu.VMEM(right, BF16),
            pltpu.SemaphoreType.DMA,
            pltpu.SemaphoreType.DMA((Ring.COPIES,)),
            pltpu.SemaphoreType.DMA((Ring.COPIES,)),
            pltpu.SemaphoreType.DMA((8,)),
        ],
        input_output_aliases={5: 2},
        compiler_params=pltpu.CompilerParams(
            collective_id=7, has_side_effects=True, vmem_limit_bytes=56 << 20
        ),
        cost_estimate=pl.CostEstimate(
            flops=16 * rows * span * LANES * pairs,
            bytes_accessed=4 * rows * width + 2 * keys * kv.shape[1],
            transcendentals=2 * rows * span * pairs,
        ),
    )(q, kv, kv, low, grad, grads)


def attend_back_kernel(
    reach, wide, z_size, mlp_count,
    q_ref, do_ref, o_ref, k_ref, v_ref, lse_ref, low_ref, cos_ref, sin_ref, cos_all, sin_all,
    *refs,
):
    mlp_ins, refs = refs[:mlp_count], refs[mlp_count:]
    dq_ref, dkv_ref = refs[:2]
    mlp_outs, refs = refs[2 : 2 + mlp_count], refs[2 + mlp_count :]
    bias_ref, dk_acc, dv_acc, own_part, send_part, recv_part, kv_send, kv_recv = refs[:8]
    home = refs[8:]
    block, half, tile, pair = (pl.program_id(at) for at in range(4))
    steps = pl.num_programs(1) * pl.num_programs(2) * pl.num_programs(3)
    inner = (half * pl.num_programs(2) + tile) * pl.num_programs(3) + pair
    step = block * steps + inner
    blocks = own_part.shape[0]
    rows = own_part.shape[1]
    count = reach // rows
    place = lax.axis_index("tensor")

    def exchange(at, distance):
        return pltpu.make_async_remote_copy(
            src_ref=send_part.at[at, pl.ds((count - distance) * rows, rows)],
            dst_ref=recv_part.at[at, distance - 1],
            send_sem=kv_send.at[at, distance - 1], recv_sem=kv_recv.at[at, distance - 1],
            device_id={"tensor": (place + z_size - distance) % z_size}, device_id_type=MESH,
        )

    def each_exchange(at, condition, action):
        for distance in range(1, count + 1):
            pl.when(condition(distance))(
                functools.partial(action, exchange(at, distance), at, distance)
            )

    @pl.when(step == 0)
    def _():
        greet(along_peers(place, z_size) + [device for _, device in others(wide)[1]])
        for copy in send_home(wide, mlp_ins, mlp_outs, *home):
            copy.start()
        fill_bias(bias_ref, low_ref, reach)

    @pl.when(inner == 0)
    def _():
        dk_acc[...] = jnp.zeros_like(dk_acc)
        dv_acc[...] = jnp.zeros_like(dv_acc)

    keys = pl.ds(pl.multiple_of(tile * QTILE, QTILE), bias_ref.shape[1])
    queries = spread_pair(q_ref[...], half)
    grads = spread_pair(do_ref[...], half)
    product = (do_ref[...].astype(F32) * o_ref[...].astype(F32)).T
    row_dot = jnp.concatenate(
        [
            jnp.sum(product[:64], axis=0, keepdims=True),
            jnp.sum(product[64:], axis=0, keepdims=True),
        ],
        axis=1,
    )
    bias = bias_ref[tile]
    key, value = k_ref[keys, :], v_ref[keys, :]
    score = dot_nt(key, queries) + jnp.concatenate([bias, bias], axis=1)
    weight = jnp.exp2(score * (SCALE * LOG2E) - lse_ref[0])
    dv_acc[keys, :] += dot_nn(weight.astype(BF16), grads)
    dscore = (weight * (dot_nt(value, grads) - row_dot)).astype(BF16)
    dk_acc[keys, :] += dot_nn(dscore, queries)
    dq = gather_pair(dot_tn(key, dscore), half) * SCALE
    dq_ref[...] = (dq * cos_ref[...] - swap_halves(dq) * sin_ref[...]).astype(BF16)

    @pl.when(inner == steps - 1)
    def _():
        send_part[block, :, :LANES] = (dk_acc[:reach] * SCALE).astype(BF16)
        send_part[block, :, LANES:] = dv_acc[:reach].astype(BF16)
        own_part[block, :, :LANES] = dk_acc[reach:] * SCALE
        own_part[block, :, LANES:] = dv_acc[reach:]
        each_exchange(block, lambda distance: place >= distance, lambda copy, *_: copy.start())

    @pl.when(step == blocks * steps - 1)
    def _():
        def collect(copy, at, distance):
            copy.wait_recv()
            own_part[at] += recv_part[at, distance - 1].astype(F32)

        for at in range(blocks):
            each_exchange(at, lambda distance: place + distance < z_size, collect)
            dkey = own_part[at, :, :LANES]
            dkey = dkey * cos_all[...] - swap_halves(dkey) * sin_all[...]
            dkv_ref[:, 2 * at * LANES : (2 * at + 1) * LANES] = dkey.astype(BF16)
            dkv_ref[:, (2 * at + 1) * LANES : (2 * at + 2) * LANES] = own_part[
                at, :, LANES:
            ].astype(BF16)
        for at in range(blocks):
            each_exchange(
                at, lambda distance: place >= distance, lambda copy, *_: copy.wait_send()
            )
        for copy in send_home(wide, mlp_ins, mlp_outs, *home):
            copy.wait()


def attend_back(q, do, att, kv, lse, low, cosine, sine, mlp, dp_size, z_size):
    rows, width = q.shape
    keys = kv.shape[0]
    reach = keys - rows
    tiles = rows // QTILE
    pairs = width // LANES
    heads = kv.shape[1] // LANES
    per_head = pairs // heads
    span = reach + QTILE
    blocks = heads // 2

    def pair_at(g, h, t, p):
        return (t, (2 * g + h) * per_head + p)

    def whole(shape):
        return pl.BlockSpec(shape, lambda g, h, t, p: (0, 0), pipeline_mode=pl.Buffered(1))

    table = pl.BlockSpec((QTILE, LANES), lambda g, h, t, p: (t, 0))
    return pl.pallas_call(
        functools.partial(
            attend_back_kernel, reach, 2 * math.isqrt(dp_size // GROUP), z_size, len(mlp)
        ),
        grid=(blocks, 2, tiles, per_head),
        in_specs=[
            pl.BlockSpec((QTILE, LANES), pair_at),
            pl.BlockSpec((QTILE, LANES), pair_at),
            pl.BlockSpec((QTILE, LANES), pair_at),
            pl.BlockSpec((keys, LANES), lambda g, h, t, p: (0, 2 * g)),
            pl.BlockSpec((keys, LANES), lambda g, h, t, p: (0, 2 * g + 1)),
            pl.BlockSpec(
                (1, 1, 2 * QTILE),
                lambda g, h, t, p: (((2 * g + h) * tiles + t) * per_head + p, 0, 0),
            ),
            whole((1, rows)),
            table,
            table,
            whole((rows, LANES)),
            whole((rows, LANES)),
        ]
        + [pl.BlockSpec(memory_space=pl.ANY)] * len(mlp),
        out_specs=[
            pl.BlockSpec((QTILE, LANES), pair_at),
            pl.BlockSpec((rows, kv.shape[1]), lambda g, h, t, p: (0, 0)),
        ]
        + [pl.BlockSpec(memory_space=pl.ANY)] * len(mlp),
        out_shape=[
            jax.ShapeDtypeStruct((rows, width), BF16),
            jax.ShapeDtypeStruct((rows, kv.shape[1]), BF16),
        ]
        + home_shapes(mlp),
        scratch_shapes=[
            pltpu.VMEM((tiles, span, QTILE), F32),
            pltpu.VMEM((keys, LANES), F32),
            pltpu.VMEM((keys, LANES), F32),
            pltpu.VMEM((blocks, rows, 2 * LANES), F32),
            pltpu.VMEM((blocks, reach, 2 * LANES), BF16),
            pltpu.VMEM((blocks, reach // rows, rows, 2 * LANES), BF16),
            pltpu.SemaphoreType.DMA((blocks, reach // rows)),
            pltpu.SemaphoreType.DMA((blocks, reach // rows)),
        ]
        + home_scratch(mlp),
        compiler_params=pltpu.CompilerParams(
            collective_id=5, has_side_effects=True, vmem_limit_bytes=60 << 20
        ),
        cost_estimate=pl.CostEstimate(
            flops=40 * rows * span * LANES * pairs,
            bytes_accessed=8 * rows * width + 4 * keys * kv.shape[1],
            transcendentals=2 * rows * span * pairs,
        ),
    )(q, do, att, kv, kv, lse, low, cosine, sine, cosine, sine, *mlp)


MESH = pl.DeviceIdType.MESH


def neighbours(wide):
    dp = lax.axis_index("dp")
    core, col, row = dp % 2, (dp // 2) % 2, (dp // (2 * wide)) % 2
    sibling = dp + 1 - 2 * core
    beside = dp + 2 - 4 * col
    above = dp + 2 * wide - 4 * wide * row
    return (row, col, core), (sibling, beside, above)


def meet(peers):
    barrier = pltpu.get_barrier_semaphore()
    for peer in peers:
        pl.semaphore_signal(barrier, inc=1, device_id={"dp": peer}, device_id_type=MESH)
    pl.semaphore_wait(barrier, len(peers))


def others(wide):
    (row, col, core), _ = neighbours(wide)
    base = lax.axis_index("dp") - (2 * wide * row + 2 * col + core)
    found = []
    for flip in range(1, GROUP):
        y, x, c = (row + flip // 4) % 2, (col + flip // 2) % 2, (core + flip) % 2
        found.append((4 * y + 2 * x + c, {"dp": base + 2 * wide * y + 2 * x + c}))
    return 4 * row + 2 * col + core, found


def along_peers(place, z_size):
    return [{"tensor": (place + step) % z_size} for step in range(1, z_size)]


def greet(peers):
    barrier = pltpu.get_barrier_semaphore()
    for peer in peers:
        pl.semaphore_signal(barrier, inc=1, device_id=peer, device_id_type=MESH)
    pl.semaphore_wait(barrier, len(peers))


def send_home(wide, ins, outs, own_sem, send_sem, recv_sem):
    mine, found = others(wide)
    copies = []
    for at, (src, dst) in enumerate(zip(ins, outs)):
        part, cols = dst.shape[0], src.shape[1]
        here = pl.ds(pl.multiple_of(mine * cols, LANES), cols)
        for index, (other, device) in enumerate(found):
            copies.append(
                pltpu.make_async_remote_copy(
                    src_ref=src.at[pl.ds(pl.multiple_of(other * part, part), part)],
                    dst_ref=dst.at[:, here],
                    send_sem=send_sem.at[at, index], recv_sem=recv_sem.at[at, index],
                    device_id=device, device_id_type=MESH,
                )
            )
        own = src.at[pl.ds(pl.multiple_of(mine * part, part), part)]
        copies.append(pltpu.make_async_copy(own, dst.at[:, here], own_sem.at[at]))
    return copies


def home_shapes(arrays):
    return [jax.ShapeDtypeStruct((a.shape[0] // GROUP, GROUP * a.shape[1]), BF16) for a in arrays]


def home_scratch(arrays):
    count = len(arrays)
    return [
        pltpu.SemaphoreType.DMA((count,)),
        pltpu.SemaphoreType.DMA((count, GROUP - 1)),
        pltpu.SemaphoreType.DMA((count, GROUP - 1)),
    ]


SIB, XN, YN = 0, 1, 2


def spread_kernel(wide, z_size, mlp_count, *refs):
    attn_count = (len(refs) - 7) // 2 - mlp_count
    count = mlp_count + attn_count
    ins, outs = refs[:count], refs[count : 2 * count]
    own_sem, send_sem, recv_sem, z_send, z_recv, ring_send, ring_recv = refs[2 * count :]
    first = mlp_count
    ring = Ring(wide, outs[first], ins[first].shape[0], ring_send, ring_recv)
    place = lax.axis_index("tensor")
    mine, found = others(wide)
    greet(along_peers(place, z_size) + [device for _, device in found])

    local, copies = [], []
    for at in range(mlp_count):
        src, dst = ins[at], outs[at]
        rows, cols = src.shape[0], dst.shape[1]
        here = pl.ds(pl.multiple_of(mine * rows, rows), rows)
        for index, (other, device) in enumerate(found):
            copies.append(
                pltpu.make_async_remote_copy(
                    src_ref=src.at[:, pl.ds(pl.multiple_of(other * cols, LANES), cols)],
                    dst_ref=dst.at[here],
                    send_sem=send_sem.at[at, index], recv_sem=recv_sem.at[at, index],
                    device_id=device, device_id_type=MESH,
                )
            )
        own = src.at[:, pl.ds(pl.multiple_of(mine * cols, LANES), cols)]
        local.append(pltpu.make_async_copy(own, dst.at[here], own_sem.at[at]))

    def block(at, origin):
        cols = ins[at].shape[1]
        part = pl.ds(pl.multiple_of(origin * cols, LANES), cols)
        return outs[at].at[ring.mine() if at == first else slice(None), part]

    def hop(at, way, step, receive=False):
        sign = 1 - 2 * way
        origin = place - sign * (step if receive else step - 1)
        slot = 2 * (step - 1) + way
        src = block(at, origin) if receive or step > 1 else ins[at]
        return pltpu.make_async_remote_copy(
            src_ref=src, dst_ref=block(at, origin),
            send_sem=z_send.at[at - mlp_count, slot], recv_sem=z_recv.at[at - mlp_count, slot],
            device_id={"tensor": (place + z_size + sign) % z_size}, device_id_type=MESH,
        )

    def sends(way, step):
        if way == 0:
            return (place + 1 < z_size) & (place >= step - 1)
        return (place >= 1) & (place + step - 1 < z_size)

    def receives(way, step):
        return place >= step if way == 0 else place + step < z_size

    for at in range(mlp_count, count):
        local.append(pltpu.make_async_copy(ins[at], block(at, place), own_sem.at[at]))
        for way in range(2):
            pl.when(sends(way, 1))(lambda: hop(at, way, 1).start())
    for copy in copies + local:
        copy.start()

    def advance(at, step):
        for way in range(2):
            pl.when(receives(way, step))(lambda: hop(at, way, step, True).wait_recv())
            if step + 1 < z_size:
                pl.when(sends(way, step + 1))(lambda: hop(at, way, step + 1).start())

    for step in range(1, z_size):
        advance(first, step)
    local.pop(first).wait()
    ring.start_own()
    stages = [ring.first_halves, ring.second_halves]
    for step in range(1, z_size):
        for at in range(first + 1, count):
            advance(at, step)
        if stages:
            stages.pop(0)()
    for stage in stages:
        stage()
    ring.far_halves()
    for name in ("own", "x", "y", "d"):
        ring.from_sibling(name, 0, 1)
    ring.sent()
    for step in range(1, z_size):
        for at in range(mlp_count, count):
            for way in range(2):
                pl.when(sends(way, step))(lambda: hop(at, way, step).wait_send())
    for copy in local + copies:
        copy.wait()


def spread_weights(mlp, attn, dp_size, z_size):
    count = len(mlp) + len(attn)
    spec = pl.BlockSpec(memory_space=pl.ANY)
    out = [jax.ShapeDtypeStruct((GROUP * w.shape[0], w.shape[1] // GROUP), BF16) for w in mlp]
    out += [
        jax.ShapeDtypeStruct(((1 if at else GROUP) * w.shape[0], z_size * w.shape[1]), BF16)
        for at, w in enumerate(attn)
    ]
    return pl.pallas_call(
        functools.partial(spread_kernel, 2 * math.isqrt(dp_size // GROUP), z_size, len(mlp)),
        in_specs=[spec] * count,
        out_specs=[spec] * count,
        out_shape=out,
        scratch_shapes=[
            pltpu.SemaphoreType.DMA((count,)),
            pltpu.SemaphoreType.DMA((len(mlp), GROUP - 1)),
            pltpu.SemaphoreType.DMA((len(mlp), GROUP - 1)),
            pltpu.SemaphoreType.DMA((len(attn), 2 * (z_size - 1))),
            pltpu.SemaphoreType.DMA((len(attn), 2 * (z_size - 1))),
            pltpu.SemaphoreType.DMA((Ring.COPIES,)),
            pltpu.SemaphoreType.DMA((Ring.COPIES,)),
        ],
        compiler_params=pltpu.CompilerParams(collective_id=2, has_side_effects=True),
        cost_estimate=pl.CostEstimate(flops=LONG, bytes_accessed=0, transcendentals=0),
    )(*mlp, *attn)


class Ring:
    FLIP = {SIB: (0, 0, 1), XN: (0, 1, 0), YN: (1, 0, 0)}
    COPIES = 14

    def __init__(self, wide, ref, rows, send_sem, recv_sem):
        (self.row, self.col, self.core), self.peers = neighbours(wide)
        self.ref, self.rows, self.part = ref, rows, rows // 2
        self.send_sem, self.recv_sem = send_sem, recv_sem
        self.sends = {}
        for half in range(2):
            self.sends["own", XN, half] = (2 + half, 0, 0, 0, half)
            self.sends["own", YN, half] = (4 + half, 0, 0, 0, half)
            self.sends["own", SIB, half] = (0 + half, 0, 0, 0, half)
        for half in range(2):
            self.sends["x", SIB, half] = (6 + half, 0, 1, 0, half)
            self.sends["y", SIB, half] = (8 + half, 1, 0, 0, half)
            self.sends["d", SIB, half] = (10 + half, 1, 1, 0, half)
        self.sends["x", YN, 0] = (12, 0, 1, 0, 0)
        self.sends["y", XN, 1] = (13, 1, 0, 0, 1)

    def place(self, dy, dx, dc, half):
        p = 4 * ((self.row + dy) % 2) + 2 * ((self.col + dx) % 2) + (self.core + dc) % 2
        return pl.ds(pl.multiple_of(p * self.rows + half * self.part, self.part), self.part)

    def mine(self):
        p = 4 * self.row + 2 * self.col + self.core
        return pl.ds(pl.multiple_of(p * self.rows, self.rows), self.rows)

    def whole(self, dy, dx, dc):
        p = 4 * ((self.row + dy) % 2) + 2 * ((self.col + dx) % 2) + (self.core + dc) % 2
        return pl.ds(pl.multiple_of(p * self.rows, self.rows), self.rows)

    def copy(self, slot, dy, dx, dc, half, peer):
        where = self.place(dy, dx, dc, half)
        return pltpu.make_async_remote_copy(
            src_ref=self.ref.at[where], dst_ref=self.ref.at[where],
            send_sem=self.send_sem.at[slot], recv_sem=self.recv_sem.at[slot],
            device_id={"dp": self.peers[peer]}, device_id_type=MESH,
        )

    def start(self, name, peer, half):
        self.copy(*self.sends[name, peer, half], peer).start()

    def arrived(self, name, peer, half):
        slot, dy, dx, dc, half = self.sends[name, peer, half]
        fy, fx, fc = self.FLIP[peer]
        self.copy(slot, (dy + fy) % 2, (dx + fx) % 2, (dc + fc) % 2, half, peer).wait_recv()

    def start_own(self):
        for half in range(2):
            for peer in (XN, YN, SIB):
                self.start("own", peer, half)

    def first_halves(self):
        self.arrived("own", XN, 0)
        self.start("x", YN, 0)
        self.start("x", SIB, 0)
        self.arrived("own", YN, 0)
        self.start("y", SIB, 0)

    def second_halves(self):
        self.arrived("own", YN, 1)
        self.start("y", XN, 1)
        self.start("y", SIB, 1)
        self.arrived("own", XN, 1)
        self.start("x", SIB, 1)

    def far_halves(self):
        self.arrived("x", YN, 0)
        self.start("d", SIB, 0)
        self.arrived("y", XN, 1)
        self.start("d", SIB, 1)

    def from_sibling(self, name, *halves):
        for half in halves:
            self.arrived(name, SIB, half)

    def sent(self):
        for (name, peer, half), entry in self.sends.items():
            self.copy(*entry, peer).wait_send()


def project_kernel(
    wide, z_size, x_ref, cos_ref, sin_ref, wkv_ref, wq_ref, wo_ref, grad_ref,
    q_ref, kv_ref, wq_out, wo_out, grad_out,
    wkv_all, wq_all, wo_all, grad_all, keys, own_sem, send_sem, recv_sem, kv_send, kv_recv, out_sem,
):
    place = lax.axis_index("tensor")
    rows = x_ref.shape[0]
    count = keys.shape[0] // rows - 1
    left = pl.ds(0, grad_all.shape[1])
    parts = (
        (wq_ref, wq_all, wq_out), (wo_ref, wo_all, wo_out),
        (grad_ref.at[:, left], grad_all, grad_out.at[:, left]),
    )
    rings = [
        Ring(wide, full, part.shape[0], send_sem.at[at], recv_sem.at[at])
        for at, (part, full, _) in enumerate(parts)
    ]
    local = [
        pltpu.make_async_copy(part, full.at[ring.mine()], own_sem.at[at])
        for at, ((part, full, _), ring) in enumerate(zip(parts, rings))
    ]
    outward = [
        pltpu.make_async_copy(full, out, out_sem.at[at])
        for at, (_, full, out) in enumerate(parts)
    ]
    load = pltpu.make_async_copy(wkv_ref, wkv_all, own_sem.at[len(parts)])
    for copy in local + [load]:
        copy.start()
    keys[: count * rows, :] = jnp.zeros((count * rows, keys.shape[1]), BF16)
    greet([{"dp": peer} for peer in rings[0].peers] + along_peers(place, z_size))
    for copy in local:
        copy.wait()

    def rotated(value):
        return (value * cos_ref[...] + swap_halves(value) * sin_ref[...]).astype(BF16)

    def hop(step):
        return pltpu.make_async_remote_copy(
            src_ref=keys.at[pl.ds((count - step + 1) * rows, rows)],
            dst_ref=keys.at[pl.ds((count - step) * rows, rows)],
            send_sem=kv_send.at[step - 1], recv_sem=kv_recv.at[step - 1],
            device_id={"tensor": (place + 1) % z_size}, device_id_type=MESH,
        )

    def pass_keys(step):
        if step > 1:
            pl.when(place >= step - 1)(lambda: hop(step - 1).wait_recv())
        if step <= count:
            sends = (place + 1 < z_size) & (place >= step - 1)
            pl.when(sends)(lambda: hop(step).start())

    def finish(ring):
        ring.far_halves()
        for name in ("own", "x", "y", "d"):
            ring.from_sibling(name, 0, 1)

    rings[0].start_own()
    load.wait()

    @pl.loop(0, wkv_all.shape[1] // (2 * LANES))
    def _(at):
        n = pl.ds(pl.multiple_of(at * 2 * LANES, LANES), 2 * LANES)
        value = dot_nn(x_ref[...], wkv_all[:, n])
        both = jnp.concatenate([rotated(value[:, :LANES]), value[:, LANES:].astype(BF16)], axis=1)
        keys[pl.ds(count * rows, rows), n] = both

    pass_keys(1)
    rings[0].first_halves()
    rings[0].second_halves()
    rings[1].start_own()
    finish(rings[0])
    outward[0].start()

    @pl.loop(0, wq_all.shape[1] // (2 * LANES))
    def _(at):
        n = pl.ds(pl.multiple_of(at * 2 * LANES, LANES), 2 * LANES)
        value = dot_nn(x_ref[...], wq_all[:, n])
        both = [rotated(value[:, :LANES]), rotated(value[:, LANES:])]
        q_ref[:, n] = jnp.concatenate(both, axis=1)

    for step in range(2, count + 1):
        pass_keys(step)
    rings[1].first_halves()
    rings[1].second_halves()
    rings[2].start_own()
    finish(rings[1])
    outward[1].start()
    rings[2].first_halves()
    rings[2].second_halves()
    finish(rings[2])
    outward[2].start()
    pass_keys(count + 1)
    keys_out = pltpu.make_async_copy(keys, kv_ref, out_sem.at[3])
    keys_out.start()
    for step in range(1, count + 1):
        sends = (place + 1 < z_size) & (place >= step - 1)
        pl.when(sends)(lambda: hop(step).wait_send())
    for ring in rings:
        ring.sent()
    for copy in outward + [keys_out]:
        copy.wait()


def project(x, cosine, sine, wkv, wq, wo, grad, reach, dp_size, z_size):
    rows, width = x.shape
    far = pl.BlockSpec(memory_space=pl.ANY)
    near = pl.BlockSpec(memory_space=pltpu.VMEM)
    whole = [(GROUP * w.shape[0], w.shape[1]) for w in (wq, wo)]
    keys = (reach + rows, wkv.shape[1])
    grads = (GROUP * grad.shape[0], grad.shape[1])
    left = (grads[0], grads[1] * 3 // 8)
    return pl.pallas_call(
        functools.partial(project_kernel, 2 * math.isqrt(dp_size // GROUP), z_size),
        in_specs=[near] * 3 + [far] * 4,
        out_specs=[near] + [far] * 4,
        out_shape=[jax.ShapeDtypeStruct((rows, wq.shape[1]), BF16)]
        + [jax.ShapeDtypeStruct(shape, BF16) for shape in [keys] + whole + [grads]],
        scratch_shapes=[pltpu.VMEM(shape, BF16) for shape in [wkv.shape] + whole + [left, keys]]
        + [
            pltpu.SemaphoreType.DMA((4,)),
            pltpu.SemaphoreType.DMA((3, Ring.COPIES)),
            pltpu.SemaphoreType.DMA((3, Ring.COPIES)),
            pltpu.SemaphoreType.DMA((reach // rows,)),
            pltpu.SemaphoreType.DMA((reach // rows,)),
            pltpu.SemaphoreType.DMA((4,)),
        ],
        compiler_params=pltpu.CompilerParams(
            collective_id=3, has_side_effects=True, vmem_limit_bytes=56 << 20
        ),
        cost_estimate=pl.CostEstimate(
            flops=2 * LONG, bytes_accessed=0, transcendentals=0
        ),
    )(x, cosine, sine, wkv, wq, wo, grad)


def gate_up_kernel(
    wide, own_ref, wg_ref, wu_ref, all_ref, gate_ref, up_ref, hid_ref, core_ref,
    full, stage, own_sem, send_sem, recv_sem, out_sem, all_sem,
):
    rows = own_ref.shape[0]
    cols = gate_ref.shape[1]
    ring = Ring(wide, full, rows, send_sem, recv_sem)
    local = pltpu.make_async_copy(own_ref, full.at[ring.mine()], own_sem)
    local.start()
    meet(ring.peers)
    local.wait()
    ring.start_own()

    def out_copies(slot, places):
        where, core, chip = places
        return [
            pltpu.make_async_copy(stage.at[slot, i], ref.at[where], out_sem.at[slot, i])
            for i, ref in enumerate((gate_ref, up_ref, hid_ref))
        ] + [
            pltpu.make_async_copy(stage.at[slot, 2], core_ref.at[core, chip], out_sem.at[slot, 3]),
            pltpu.make_async_copy(full.at[where], all_ref.at[where], all_sem.at[slot]),
        ]

    def step_place(step):
        phase, i = step // 4, step % 4
        high, low = phase // 2, phase % 2
        first, last = (1 - high) * (1 - low), high * low
        middle = high + low - 2 * last
        half = (first + last) * (i % 2) + high * (1 - low)
        dx = middle * (1 - i % 2) + last
        dy = middle * (i % 2) + last
        part = rows // 2
        chip_rows = pl.ds(pl.multiple_of((2 * dy + dx) * rows + half * part, part), part)
        return ring.place(dy, dx, i // 2, half), i // 2, chip_rows

    @pl.loop(0, 16)
    def _(step):
        pl.when(step == 2)(lambda: ring.from_sibling("own", 0, 1))
        pl.when(step == 4)(ring.first_halves)

        @pl.when(step == 6)
        def _():
            ring.from_sibling("x", 0)
            ring.from_sibling("y", 0)

        pl.when(step == 8)(ring.second_halves)

        @pl.when(step == 10)
        def _():
            ring.from_sibling("x", 1)
            ring.from_sibling("y", 1)

        pl.when(step == 12)(ring.far_halves)
        pl.when(step == 14)(lambda: ring.from_sibling("d", 0, 1))

        slot = step % 2
        places = step_place(step)

        @pl.when(step >= 2)
        def _():
            for copy in out_copies(slot, step_place(step - 2)):
                copy.wait()

        x = full[places[0], :]

        @pl.loop(0, cols // NTILE)
        def _(at):
            n = pl.ds(pl.multiple_of(at * NTILE, NTILE), NTILE)
            gate = dot_nn(x, wg_ref[:, n])
            up = dot_nn(x, wu_ref[:, n])
            stage[slot, 0, :, n] = gate.astype(BF16)
            stage[slot, 1, :, n] = up.astype(BF16)
            stage[slot, 2, :, n] = (gate * up / (1.0 + jnp.exp(-gate))).astype(BF16)

        for copy in out_copies(slot, places):
            copy.start()

    for step in (14, 15):
        for copy in out_copies(step % 2, step_place(step)):
            copy.wait()
    ring.sent()


def gate_up(hn, wg, wu, dp_size):
    rows, width = hn.shape
    cols = wg.shape[1]
    tokens = GROUP * rows
    far = pl.BlockSpec(memory_space=pl.ANY)
    near = pl.BlockSpec(memory_space=pltpu.VMEM)
    return pl.pallas_call(
        functools.partial(gate_up_kernel, 2 * math.isqrt(dp_size // GROUP)),
        in_specs=[far, near, near],
        out_specs=[far] * 5,
        out_shape=[jax.ShapeDtypeStruct((tokens, width), BF16)]
        + [jax.ShapeDtypeStruct((tokens, cols), BF16)] * 3
        + [jax.ShapeDtypeStruct((2, tokens // 2, cols), BF16)],
        scratch_shapes=[
            pltpu.VMEM((tokens, width), BF16),
            pltpu.VMEM((2, 3, rows // 2, cols), BF16),
            pltpu.SemaphoreType.DMA,
            pltpu.SemaphoreType.DMA((Ring.COPIES,)),
            pltpu.SemaphoreType.DMA((Ring.COPIES,)),
            pltpu.SemaphoreType.DMA((2, 4)),
            pltpu.SemaphoreType.DMA((2,)),
        ],
        compiler_params=pltpu.CompilerParams(
            collective_id=1, has_side_effects=True, vmem_limit_bytes=56 << 20
        ),
        cost_estimate=pl.CostEstimate(
            flops=SHORT, bytes_accessed=0, transcendentals=0
        ),
    )(hn, wg, wu)


FAR_CHUNK, X_CHUNK, Y_CHUNK, OWN_CHUNK = range(4)


class Reduce:
    COPIES = 10

    def __init__(self, wide, parts, cores, far, near, send_sem, recv_sem):
        self.at, self.peers = neighbours(wide)
        self.parts, self.cores, self.far, self.near = parts, cores, far, near
        self.send_sem, self.recv_sem = send_sem, recv_sem
        self.half = parts.shape[2] // 2

    @staticmethod
    def scratch(rows, cols):
        return [
            pltpu.VMEM((2, 4, rows, cols), BF16),
            pltpu.VMEM((4, rows, cols), BF16),
            pltpu.VMEM((2, rows // 2, cols), BF16),
            pltpu.VMEM((2, rows, cols), BF16),
            pltpu.SemaphoreType.DMA((Reduce.COPIES,)),
            pltpu.SemaphoreType.DMA((Reduce.COPIES,)),
        ]

    def chunk(self, step):
        slot, other = step // 2, 1 - step % 2
        row, col, core = self.at
        dy, dx = 1 - slot % 2, 1 - slot // 2
        place = 4 * ((row + dy) % 2) + 2 * ((col + dx) % 2) + (core + other) % 2
        return place, self.parts.at[other, slot]

    def copy(self, name):
        upper, lower = pl.ds(0, self.half), pl.ds(self.half, self.half)
        mine = self.parts.at[0]
        table = {
            "far0": (self.parts.at[1, FAR_CHUNK], self.cores.at[FAR_CHUNK], SIB),
            "x": (self.parts.at[1, X_CHUNK], self.cores.at[X_CHUNK], SIB),
            "y": (self.parts.at[1, Y_CHUNK], self.cores.at[Y_CHUNK], SIB),
            "own": (self.parts.at[1, OWN_CHUNK], self.cores.at[OWN_CHUNK], SIB),
            "far_x": (mine.at[FAR_CHUNK, lower], self.far.at[0], XN),
            "far_y": (mine.at[FAR_CHUNK, upper], self.far.at[1], YN),
            "x_upper": (mine.at[X_CHUNK, upper], self.near.at[0, upper], XN),
            "x_lower": (mine.at[X_CHUNK, lower], self.near.at[0, lower], XN),
            "y_upper": (mine.at[Y_CHUNK, upper], self.near.at[1, upper], YN),
            "y_lower": (mine.at[Y_CHUNK, lower], self.near.at[1, lower], YN),
        }
        src, dst, peer = table[name]
        at = list(table).index(name)
        return pltpu.make_async_remote_copy(
            src_ref=src, dst_ref=dst, send_sem=self.send_sem.at[at],
            recv_sem=self.recv_sem.at[at], device_id={"dp": self.peers[peer]},
            device_id_type=MESH,
        )

    def start(self, *names):
        for name in names:
            self.copy(name).start()

    def add(self, slot, start, other):
        count = other.shape[0] // STRIP

        @pl.loop(0, count)
        def _(at):
            here = pl.ds(pl.multiple_of(start + at * STRIP, STRIP), STRIP)
            there = pl.ds(pl.multiple_of(at * STRIP, STRIP), STRIP)
            value = self.parts[0, slot, here, :].astype(F32) + other[there, :].astype(F32)
            self.parts[0, slot, here, :] = value.astype(BF16)

    def merge_core(self, slot, name):
        self.copy(name).wait_recv()
        self.add(slot, 0, self.cores.at[slot])

    def after(self, step):
        names = ("far0", "x", "y", "own")
        for slot in range(4):
            pl.when(step == 2 * slot)(functools.partial(self.start, names[slot]))

        @pl.when(step == 1)
        def _():
            self.merge_core(FAR_CHUNK, "far0")
            self.start("far_x", "far_y")

        @pl.when(step == 3)
        def _():
            self.merge_core(X_CHUNK, "x")
            self.start("x_lower")

        @pl.when(step == 5)
        def _():
            self.merge_core(Y_CHUNK, "y")
            self.start("y_upper")

    def pass_on(self):
        self.copy("far_y").wait_recv()
        self.add(X_CHUNK, 0, self.far.at[1])
        self.start("x_upper")
        self.copy("far_x").wait_recv()
        self.add(Y_CHUNK, self.half, self.far.at[0])
        self.start("y_lower")

    def finish(self, store):
        for name in ("own", "x_upper", "x_lower", "y_upper", "y_lower"):
            self.copy(name).wait_recv()

        @pl.loop(0, 2 * self.half // STRIP)
        def _(at):
            here = pl.ds(pl.multiple_of(at * STRIP, STRIP), STRIP)
            value = self.parts[0, OWN_CHUNK, here, :].astype(F32)
            value += self.cores[OWN_CHUNK, here, :].astype(F32)
            value += self.near[0, here, :].astype(F32)
            value += self.near[1, here, :].astype(F32)
            store(here, value)

    def sent(self):
        for name in (
            "far0", "x", "y", "own", "far_x", "far_y", "x_upper", "x_lower", "y_upper", "y_lower",
        ):
            self.copy(name).wait_send()


def hidden_back_kernel(
    wide, dgate_ref, dup_ref, wg_ref, wu_ref, out_ref, loaded, load_sem, *scratch
):
    ring = Reduce(wide, *scratch)
    rows = out_ref.shape[0]

    def loads(step):
        chunk, _ = ring.chunk(step)
        here = pl.ds(pl.multiple_of(chunk * rows, rows), rows)
        return [
            pltpu.make_async_copy(
                ref.at[here], loaded.at[step % 2, at], load_sem.at[step % 2, at]
            )
            for at, ref in enumerate((dgate_ref, dup_ref))
        ]

    for copy in loads(0):
        copy.start()
    meet(ring.peers)

    @pl.loop(0, 8)
    def _(step):
        @pl.when(step < 7)
        def _():
            for copy in loads(step + 1):
                copy.start()

        for copy in loads(step):
            copy.wait()
        _, target = ring.chunk(step)
        dgate, dup = loaded[step % 2, 0], loaded[step % 2, 1]

        @pl.loop(0, out_ref.shape[1] // NTILE)
        def _(at):
            n = pl.ds(pl.multiple_of(at * NTILE, NTILE), NTILE)
            value = dot_nt(dgate, wg_ref[n, :]) + dot_nt(dup, wu_ref[n, :])
            target[:, n] = value.astype(BF16)

        ring.after(step)

    ring.pass_on()

    def store(here, value):
        out_ref[here, :] = value

    ring.finish(store)
    ring.sent()


def hidden_back(dgate, dup, wg, wu, dp_size):
    tokens, cols = dgate.shape
    width = wg.shape[0]
    rows = tokens // GROUP
    far = pl.BlockSpec(memory_space=pl.ANY)
    near = pl.BlockSpec(memory_space=pltpu.VMEM)
    return pl.pallas_call(
        functools.partial(hidden_back_kernel, 2 * math.isqrt(dp_size // GROUP)),
        in_specs=[far, far, near, near],
        out_specs=near,
        out_shape=jax.ShapeDtypeStruct((rows, width), F32),
        scratch_shapes=[
            pltpu.VMEM((2, 2, rows, cols), BF16),
            pltpu.SemaphoreType.DMA((2, 2)),
        ]
        + Reduce.scratch(rows, width),
        compiler_params=pltpu.CompilerParams(
            collective_id=6, has_side_effects=True, vmem_limit_bytes=60 << 20
        ),
        cost_estimate=pl.CostEstimate(
            flops=4 * tokens * width * cols,
            bytes_accessed=4 * tokens * cols + 4 * width * cols + 4 * rows * width,
            transcendentals=0,
        ),
    )(dgate, dup, wg, wu)


def tail_kernel(
    wide, z_size, mlp_count, x_ref, dq_ref, dkv_ref, wo_ref, scale_ref, gain_ref,
    raw_ref, dh_ref, wq_ref, wkv_ref, *refs
):
    mlp_ins, refs = refs[:mlp_count], refs[mlp_count:]
    wq_out, wkv_out, wo_out, gain_out, grad_out = refs[:5]
    mlp_outs, scratch = refs[5 : 5 + mlp_count], refs[5 + mlp_count :]
    own_scratch = scratch[:12]
    sums, zrecv, gain_z, gain_p, z_send, z_recv, g_send, g_recv = scratch[12:20]
    wo_recv, w_send, w_recv, m_own, m_send, m_recv = scratch[20:26]
    wq_all, wkv_all, raw, dh, dxn, gain_sum, load_sem = scratch[26:]
    rings = [Reduce(wide, *own_scratch[6 * at : 6 * at + 6]) for at in range(2)]
    place = lax.axis_index("tensor")
    mine, found = others(wide)
    along = along_peers(place, z_size)
    around = [device for _, device in found]

    tiles, tile_rows = raw.shape[0], raw.shape[1]
    loads = [
        pltpu.make_async_copy(wq_ref, wq_all, load_sem.at[0]),
        pltpu.make_async_copy(wkv_ref, wkv_all, load_sem.at[1]),
    ]
    for tile in range(tiles):
        here = pl.ds(tile * tile_rows, tile_rows)
        loads += [
            pltpu.make_async_copy(raw_ref.at[here], raw.at[tile], load_sem.at[2 + 2 * tile]),
            pltpu.make_async_copy(dh_ref.at[here], dh.at[tile], load_sem.at[3 + 2 * tile]),
        ]
    for copy in loads:
        copy.start()
    greet(along + around)

    mlp_copies = send_home(wide, mlp_ins, mlp_outs, m_own, m_send, m_recv)
    wo_part = wo_out.shape[1]
    wo_copies = [
        pltpu.make_async_remote_copy(
            src_ref=wo_ref.at[
                :,
                pl.ds(pl.multiple_of((place + at + 1) % z_size * wo_part, LANES), wo_part),
            ],
            dst_ref=wo_recv.at[at], send_sem=w_send.at[at], recv_sem=w_recv.at[at],
            device_id=peer, device_id_type=MESH,
        )
        for at, peer in enumerate(along)
    ]
    for copy in wo_copies:
        copy.start()

    rights = (dq_ref, dkv_ref)
    rows = sums.shape[0]
    outs = (wq_out, wkv_out)
    starts = [0, rights[0].shape[1]]
    z_copies = []

    def partial_sums(index):
        ring, right = rings[index], rights[index]

        @pl.loop(0, 8)
        def _(step):
            chunk, target = ring.chunk(step)
            x = x_ref[:, pl.ds(pl.multiple_of(chunk * rows, rows), rows)].T

            @pl.loop(0, right.shape[1] // NTILE)
            def _(at):
                n = pl.ds(pl.multiple_of(at * NTILE, NTILE), NTILE)
                target[:, n] = dot_nn(x, right[:, n]).astype(BF16)

            ring.after(step)

    gain_sum[...] = jnp.zeros_like(gain_sum)

    def input_rows(tile):
        part = pl.ds(tile * tile_rows, tile_rows)
        dq, dkv = dq_ref[part, :], dkv_ref[part, :]

        @pl.loop(0, dxn.shape[1] // NTILE)
        def _(at):
            n = pl.ds(pl.multiple_of(at * NTILE, NTILE), NTILE)
            dxn[:, n] = dot_nt(dq, wq_all[n, :]) + dot_nt(dkv, wkv_all[n, :])

        @pl.loop(0, tile_rows // STRIP)
        def _(at):
            here = pl.ds(pl.multiple_of(at * STRIP, STRIP), STRIP)
            there = pl.ds(pl.multiple_of(tile * tile_rows + at * STRIP, STRIP), STRIP)
            grad, value = dxn[here, :], raw[tile, here, :].astype(F32)
            scale = scale_ref[there, :]
            gained = grad * gain_ref[0:1, :]
            inner = jnp.mean(gained * value, axis=1, keepdims=True)
            gain_sum[...] += grad * value * scale
            total = scale * gained - value * (scale * scale * scale * inner)
            grad_out[there, :] = (dh[tile, here, :] + total).astype(BF16)

    def send_along(index):
        ring, start = rings[index], starts[index]
        cols = rights[index].shape[1]
        part = cols // z_size

        def store(here, value):
            sums[here, pl.ds(start, cols)] = value.astype(BF16)

        ring.finish(store)
        for at, peer in enumerate(along):
            other = (place + at + 1) % z_size
            copy = pltpu.make_async_remote_copy(
                src_ref=sums.at[:, pl.ds(pl.multiple_of(start + other * part, LANES), part)],
                dst_ref=zrecv.at[at, :, pl.ds(start // z_size, part)],
                send_sem=z_send.at[index, at], recv_sem=z_recv.at[index, at],
                device_id=peer, device_id_type=MESH,
            )
            z_copies.append(copy)
            copy.start()

    partial_sums(0)
    for copy in loads:
        copy.wait()
    input_rows(0)
    rings[0].pass_on()
    partial_sums(1)
    for tile in range(1, tiles):
        input_rows(tile)

    gain_z[place, 0:1] = jnp.sum(gain_sum[...], axis=0, keepdims=True)
    gain_z[place, 1:2] = gain_ref[1:2, :]
    gain_copies = [
        pltpu.make_async_remote_copy(
            src_ref=gain_z.at[place], dst_ref=gain_z.at[place], send_sem=g_send.at[at],
            recv_sem=g_recv.at[at], device_id=peer, device_id_type=MESH,
        )
        for at, peer in enumerate(along)
    ]
    for copy in gain_copies:
        copy.start()
    rings[1].pass_on()
    for copy in mlp_copies:
        copy.start()
    send_along(0)

    for copy in gain_copies:
        copy.wait_recv()
    total = gain_z[0]
    for at in range(1, z_size):
        total = total + gain_z[at]
    gain_p[mine] = total
    for at, peer in enumerate(around):
        copy = pltpu.make_async_remote_copy(
            src_ref=gain_p.at[mine], dst_ref=gain_p.at[mine],
            send_sem=g_send.at[z_size - 1 + at], recv_sem=g_recv.at[z_size - 1 + at],
            device_id=peer, device_id_type=MESH,
        )
        gain_copies.append(copy)
        copy.start()
    for copy in wo_copies:
        copy.wait()
    total = wo_ref[:, pl.ds(pl.multiple_of(place * wo_part, LANES), wo_part)].astype(F32)
    for at in range(z_size - 1):
        total += wo_recv[at].astype(F32)
    wo_out[...] = total
    send_along(1)

    for copy in gain_copies[z_size - 1 :]:
        copy.wait_recv()
    total = gain_p[0]
    for at in range(1, GROUP):
        total = total + gain_p[at]
    gain_out[...] = total
    for copy in z_copies:
        copy.wait_recv()
    for index in range(2):
        part = rights[index].shape[1] // z_size
        own = pl.ds(pl.multiple_of(starts[index] + place * part, LANES), part)
        value = sums[:, own].astype(F32)
        for at in range(z_size - 1):
            value += zrecv[at, :, pl.ds(starts[index] // z_size, part)].astype(F32)
        outs[index][...] = value
    for copy in z_copies + gain_copies:
        copy.wait_send()
    for ring in rings:
        ring.sent()
    for copy in mlp_copies:
        copy.wait()


def last_grads(x, dq, dkv, wo_sum, scale, gains, raw, dh, wq, wkv, mlp, dp_size, z_size):
    tokens, width = x.shape
    rows = width // GROUP
    tiles = tokens // QTILE
    near = pl.BlockSpec(memory_space=pltpu.VMEM)
    far = pl.BlockSpec(memory_space=pl.ANY)
    sizes = [dq.shape[1], dkv.shape[1]]
    scratch = []
    for cols in sizes:
        scratch += Reduce.scratch(rows, cols)
    total = sum(sizes)
    return pl.pallas_call(
        functools.partial(tail_kernel, 2 * math.isqrt(dp_size // GROUP), z_size, len(mlp)),
        in_specs=[near] * 6 + [far] * (4 + len(mlp)),
        out_specs=[near] * 5 + [far] * len(mlp),
        out_shape=[jax.ShapeDtypeStruct((rows, cols // z_size), F32) for cols in sizes]
        + [
            jax.ShapeDtypeStruct((rows, wo_sum.shape[1] // z_size), F32),
            jax.ShapeDtypeStruct(gains.shape, F32),
            jax.ShapeDtypeStruct((tokens, width), BF16),
        ]
        + home_shapes(mlp),
        scratch_shapes=scratch
        + [
            pltpu.VMEM((rows, total), BF16),
            pltpu.VMEM((z_size - 1, rows, total // z_size), BF16),
            pltpu.VMEM((z_size, *gains.shape), F32),
            pltpu.VMEM((GROUP, *gains.shape), F32),
            pltpu.SemaphoreType.DMA((2, z_size - 1)),
            pltpu.SemaphoreType.DMA((2, z_size - 1)),
            pltpu.SemaphoreType.DMA((z_size - 1 + GROUP - 1,)),
            pltpu.SemaphoreType.DMA((z_size - 1 + GROUP - 1,)),
            pltpu.VMEM((z_size - 1, rows, wo_sum.shape[1] // z_size), BF16),
            pltpu.SemaphoreType.DMA((z_size - 1,)),
            pltpu.SemaphoreType.DMA((z_size - 1,)),
        ]
        + home_scratch(mlp)
        + [
            pltpu.VMEM(wq.shape, BF16),
            pltpu.VMEM(wkv.shape, BF16),
            pltpu.VMEM((tiles, QTILE, width), BF16),
            pltpu.VMEM((tiles, QTILE, width), F32),
            pltpu.VMEM((QTILE, width), F32),
            pltpu.VMEM((STRIP, width), F32),
            pltpu.SemaphoreType.DMA((2 + 2 * tiles,)),
        ],
        compiler_params=pltpu.CompilerParams(
            collective_id=4, has_side_effects=True, vmem_limit_bytes=62 << 20
        ),
        cost_estimate=pl.CostEstimate(flops=SHORT, bytes_accessed=0, transcendentals=0),
    )(x, dq, dkv, wo_sum, scale, gains, raw, dh, wq, wkv, *mlp)


class Layout:
    def __init__(self, dp_size):
        self.blocks = dp_size // GROUP
        side = math.isqrt(self.blocks)
        self.rows, self.cols = side, self.blocks // side
        wide = 2 * self.cols

        def index(by, bx, y, x, core):
            return ((2 * by + y) * wide + 2 * bx + x) * 2 + core

        places = [(y, x, c) for y in range(2) for x in range(2) for c in range(2)]
        spots = [(by, bx) for by in range(self.rows) for bx in range(self.cols)]
        self.inner = [[index(*s, *p) for p in places] for s in spots]
        self.outer = [[index(*s, *p) for s in spots] for p in places]

    def groups(self):
        return None if self.blocks == 1 else self.inner

    def to_rows(self, array):
        if self.blocks == 1:
            return array
        rest = array.shape[1:]
        split = array.reshape(2, 2, 2, self.rows, self.cols, -1, *rest)
        order = (3, 0, 4, 1, 2, 5) + tuple(range(6, 6 + len(rest)))
        return split.transpose(order).reshape(array.shape)

    def from_rows(self, array):
        if self.blocks == 1:
            return array
        rest = array.shape[1:]
        split = array.reshape(self.rows, 2, self.cols, 2, 2, -1, *rest)
        order = (1, 3, 4, 0, 2, 5) + tuple(range(6, 6 + len(rest)))
        return split.transpose(order).reshape(array.shape)

    def from_cols(self, array):
        return array if self.blocks == 1 else self.from_rows(array.T).T

    def gather_outer(self, array):
        if self.blocks == 1:
            return array
        return lax.all_gather(array, "dp", axis_index_groups=self.outer, axis=0, tiled=True)

    def scatter_outer(self, array):
        if self.blocks == 1:
            return array
        return lax.psum_scatter(
            array, "dp", scatter_dimension=0, axis_index_groups=self.outer, tiled=True
        )

    def swap(self, array, flip):
        pairs = [
            (block[at], block[at ^ flip]) for block in self.inner for at in range(GROUP)
        ]
        return lax.ppermute(array, "dp", pairs)

    def sum_outer(self, array):
        if self.blocks == 1:
            return array
        return lax.psum(array, "dp", axis_index_groups=self.outer)

    def gather(self, array):
        return lax.all_gather(array, "dp", axis_index_groups=self.groups(), axis=0, tiled=True)

    def scatter(self, array):
        return lax.psum_scatter(
            array, "dp", scatter_dimension=0, axis_index_groups=self.groups(), tiled=True
        )


def rms_scale(values):
    return lax.rsqrt(jnp.mean(values * values, axis=-1, keepdims=True) + NORM_EPS)


def norm_back(values, scaling, gain, grad):
    gained = grad * gain
    gain_part = jnp.sum(grad * values * scaling, axis=0)
    inner = jnp.mean(gained * values, axis=-1, keepdims=True)
    return gain_part, scaling * gained - values * scaling * scaling * scaling * inner


def per_device(
    dp_size, z_size, activations, segment_ids, attn_gain, w_query, w_key, w_value, w_out,
    mlp_gain, w_gate, w_up, w_down, cotangent,
):
    layout = Layout(dp_size)
    rows, width = activations.shape[1:]
    x = activations[0].astype(F32)
    place = lax.axis_index("tensor")
    reach = -(-(MOST_DOC - 1) // rows) * rows

    def shift(array, step):
        pairs = [(at, at + step) for at in range(z_size) if 0 <= at + step < z_size]
        return lax.ppermute(array, "tensor", pairs)

    starts = document_starts(segment_ids[0])
    own_starts = lax.dynamic_slice_in_dim(starts, place * rows, rows)
    own_tokens = place * rows + jnp.arange(rows, dtype=jnp.int32)
    cosine, sine = rope_tables(own_tokens - own_starts)
    low = (own_starts - place * rows + reach)[None, :]

    shards = [
        layout.gather_outer(w)
        for w in (w_gate, w_up, w_down, jnp.concatenate([w_key, w_value], axis=1), w_query, w_out)
    ]
    spread = spread_weights(shards[:3], shards[3:], dp_size, z_size)
    def gather_z(array):
        return layout.to_rows(lax.all_gather(array, "tensor", axis=1, tiled=True))

    wg, wu = gather_z(spread[0]), gather_z(spread[1])

    def along_z(total):
        return lax.psum_scatter(
            layout.from_rows(total), "tensor", scatter_dimension=1, tiled=True
        )

    r1 = rms_scale(x)
    xn = (x * r1 * attn_gain).astype(BF16)
    q, kv_all, wq, wo, dy = project(
        layout.from_cols(xn), cosine, sine, *spread[3:], cotangent[0], reach, dp_size, z_size
    )
    wd = gather_z(spread[2])
    wkv, wq, wo = (layout.to_rows(w) for w in (spread[3], wq, wo))
    att, lse, dy = attend(q, kv_all, low, cotangent[0], dy, dp_size)
    h = x + dot_nt(att, wo)

    r2 = rms_scale(h)
    hn, gate, up, hidden, by_core = gate_up((h * r2 * mlp_gain).astype(BF16), wg, wu, dp_size)
    part = rows // 2
    away = dot_nt(by_core[1], wd).astype(BF16)
    dy, away = lax.optimization_barrier((dy, away))
    total_wd = dot_tn(dy, hidden).astype(BF16)
    part_wd = along_z(total_wd)
    from_core = layout.swap(away, 1)

    def out_rows(start, count, *more):
        some = slice(start * part, (start + count) * part)
        total = dot_nt(by_core[0, some], wd) + from_core[some].astype(F32)
        for other in more:
            total = total + other.astype(F32)
        return total.astype(BF16)

    far_y, far_x, x_lower, y_upper = (out_rows(at, 1) for at in (6, 7, 3, 4))
    dy, far_x, far_y, x_lower, y_upper = lax.optimization_barrier(
        (dy, far_x, far_y, x_lower, y_upper)
    )
    from_x, from_y = layout.swap(far_x, 2), layout.swap(far_y, 4)
    x_lower, y_upper = layout.swap(x_lower, 2), layout.swap(y_upper, 4)
    gate, up = gate.astype(F32), up.astype(F32)
    sigma = jax.nn.sigmoid(gate)
    dhid = dot_nn(dy, wd)
    dgate = (dhid * up * sigma * (1.0 + gate * (1.0 - sigma))).astype(BF16)
    dup = (dhid * gate * sigma).astype(BF16)
    dgate, dup, from_x, from_y, x_lower, y_upper = lax.optimization_barrier(
        (dgate, dup, from_x, from_y, x_lower, y_upper)
    )
    x_upper, y_lower = out_rows(2, 1, from_y), out_rows(5, 1, from_x)
    dgate, dup, x_upper, y_lower = lax.optimization_barrier((dgate, dup, x_upper, y_lower))
    x_upper, y_lower = layout.swap(x_upper, 2), layout.swap(y_lower, 4)
    total_wg = dot_tn(hn, dgate).astype(BF16)
    dup, total_wg = lax.optimization_barrier((dup, total_wg))
    part_wg = along_z(total_wg)
    total_wu = dot_tn(hn, dup).astype(BF16)
    dup, total_wu = lax.optimization_barrier((dup, total_wu))
    part_wu = along_z(total_wu)
    dup, x_upper, y_lower = lax.optimization_barrier((dup, x_upper, y_lower))
    dhn = hidden_back(dgate, dup, wg, wu, dp_size)
    dhn, part_wd = lax.optimization_barrier((dhn, part_wd))
    gain_two, dh_norm = norm_back(h, r2, mlp_gain, dhn)
    dh = cotangent[0].astype(F32) + dh_norm
    dhb = dh.astype(BF16)
    datt = dot_nn(dhb, wo).astype(BF16)
    total_wo = layout.from_rows(dot_tn(dhb, att).astype(BF16))
    datt, part_wg, total_wo = lax.optimization_barrier((datt, part_wg, total_wo))
    part_wo = layout.scatter(total_wo)
    dq, dkv, wd_grad, wg_grad = attend_back(
        q, datt, att, kv_all, lse, low, cosine, sine, (part_wd, part_wg), dp_size, z_size
    )
    dq, part_wu = lax.optimization_barrier((dq, part_wu))
    dq, part_wo = lax.optimization_barrier((dq, part_wo))
    wq_grad, wkv_grad, wo_grad, gains, input_grad, wu_grad = last_grads(
        layout.from_cols(xn), dq, dkv, part_wo, r1, jnp.stack([attn_gain, gain_two]),
        activations[0], dh, wq, wkv, (part_wu,), dp_size, z_size,
    )
    gains = layout.sum_outer(gains)
    output = h + out_rows(0, 2).astype(F32)
    output = output + jnp.concatenate([x_upper, x_lower]).astype(F32)
    output = output + jnp.concatenate([y_upper, y_lower]).astype(F32)
    wo_grad, wq_grad, wkv_grad, wd_grad, wg_grad, wu_grad = (
        layout.scatter_outer(grad).astype(F32)
        for grad in (wo_grad, wq_grad, wkv_grad, wd_grad, wg_grad, wu_grad)
    )
    key_cols = w_key.shape[1]
    return (
        output.astype(BF16)[None],
        input_grad[None],
        gains[0],
        wq_grad,
        wkv_grad[:, :key_cols],
        wkv_grad[:, key_cols:],
        wo_grad,
        gains[1],
        wg_grad,
        wu_grad,
        wd_grad,
    )


def solution(mesh):
    split = P("dp", "tensor")
    tokens = P("dp", "tensor", None)
    in_specs = (
        tokens, P("dp", None), P(), split, split, split, split, P(), split, split, split, tokens,
    )
    out_specs = (tokens, tokens, P(), split, split, split, split, P(), split, split, split)
    return jax.shard_map(
        functools.partial(per_device, mesh.shape["dp"], mesh.shape["tensor"]),
        mesh=mesh, in_specs=in_specs, out_specs=out_specs, check_vma=False,
    )
```

```python
import functools
import math

import jax
import jax.numpy as jnp
from jax import lax
from jax.experimental import pallas as pl
from jax.experimental.pallas import tpu as pltpu
from jax.sharding import PartitionSpec as P

HEAD_DIM = 64
DOCS = 4
MOST_DOC = 1024
NORM_EPS = 1e-05
ROPE_THETA = 500000.0
GROUP = 8
LANES = 128
QTILE = 256
SCALE = HEAD_DIM ** (-0.5)
LOG2E = 1.4426950408889634
FAR = -1e30
NTILE = 512
STRIP = 16
LONG = 60_000_000_000
SHORT = 1_000_000

F32 = jnp.float32
BF16 = jnp.bfloat16


def dot_nn(left, right):
    return lax.dot_general(left, right, (((1,), (0,)), ((), ())), preferred_element_type=F32)


def dot_nt(left, right):
    return lax.dot_general(left, right, (((1,), (1,)), ((), ())), preferred_element_type=F32)


def dot_tn(left, right):
    return lax.dot_general(left, right, (((0,), (0,)), ((), ())), preferred_element_type=F32)


def document_starts(segments):
    doc_ids = jnp.arange(DOCS, dtype=jnp.int32)
    counts = jnp.sum((segments[:, None] == doc_ids).astype(jnp.int32), axis=0)
    before = (doc_ids < segments[:, None]).astype(jnp.int32)
    return jnp.sum(before * counts[None, :], axis=-1)


def rope_tables(positions):
    half = HEAD_DIM // 2
    frequency = jnp.exp(
        jnp.arange(half, dtype=F32) * (-2.0 * math.log(ROPE_THETA) / HEAD_DIM)
    )
    angles = positions.astype(F32)[:, None] * frequency
    cosine, sine = jnp.cos(angles), jnp.sin(angles)
    wide_cos = jnp.concatenate([cosine] * 4, axis=1)
    wide_sin = jnp.concatenate([-sine, sine, -sine, sine], axis=1)
    return wide_cos, wide_sin


def swap_halves(values):
    lane = lax.broadcasted_iota(jnp.int32, values.shape, 1)
    ahead = pltpu.roll(values, LANES - 32, 1)
    behind = pltpu.roll(values, 32, 1)
    return jnp.where((lane % 64) < 32, ahead, behind)


def fill_bias(bias_ref, low_ref, reach):
    span = bias_ref.shape[1]
    for tile in range(bias_ref.shape[0]):
        row = lax.broadcasted_iota(jnp.int32, (span, QTILE), 0)
        col = lax.broadcasted_iota(jnp.int32, (span, QTILE), 1)
        low = low_ref[0:1, tile * QTILE : (tile + 1) * QTILE]
        allowed = (row <= reach + col) & (row + tile * QTILE >= low)
        bias_ref[tile] = jnp.where(allowed, 0.0, FAR)


def spread_pair(pair, half):
    wide = pair.astype(F32)
    turned = pltpu.roll(wide, 64, 1)
    lane = lax.broadcasted_iota(jnp.int32, wide.shape, 1)
    mine = (lane // 64) == half
    even = half == 0
    first = jnp.where(mine, jnp.where(even, wide, turned), 0.0)
    second = jnp.where(mine, jnp.where(even, turned, wide), 0.0)
    return jnp.concatenate([first, second], axis=0).astype(BF16)


def gather_pair(transposed, half):
    count = transposed.shape[1] // 2
    mine = jnp.where(half == 0, transposed[:64], transposed[64:])
    return jnp.concatenate([mine[:, :count], mine[:, count:]], axis=0).T


def attend_kernel(
    reach, wide, q_ref, k_ref, v_ref, low_ref, own_ref, _, att_ref, lse_ref, all_ref,
    bias_ref, full, own_sem, send_sem, recv_sem, out_sem,
):
    head, tile, pair = pl.program_id(0), pl.program_id(1), pl.program_id(2)
    half = head % 2
    inner = pl.num_programs(1) * pl.num_programs(2)
    step = head * inner + tile * pl.num_programs(2) + pair
    ring = Ring(wide, full, own_ref.shape[0], send_sem, recv_sem)
    right = pl.ds(own_ref.shape[1] - full.shape[1], full.shape[1])

    def outward(slot, *flips):
        where = ring.whole(*flips)
        return pltpu.make_async_copy(full.at[where], all_ref.at[where, right], out_sem.at[slot])

    near = [(0, 0, 0), (0, 0, 1), (0, 1, 0), (1, 0, 0)]
    rest = [(0, 1, 1), (1, 0, 1), (1, 1, 0), (1, 1, 1)]

    @pl.when(step == 0)
    def _():
        local = pltpu.make_async_copy(own_ref.at[:, right], full.at[ring.mine()], own_sem)
        local.start()
        meet(ring.peers)
        local.wait()
        ring.start_own()
        fill_bias(bias_ref, low_ref, reach)

    pl.when(step == 2 * inner)(ring.first_halves)
    pl.when(step == 4 * inner)(ring.second_halves)

    keys = pl.ds(pl.multiple_of(tile * QTILE, QTILE), bias_ref.shape[1])
    queries = spread_pair(q_ref[...], half)
    bias = bias_ref[tile]
    score = dot_nt(k_ref[keys, :], queries)
    score = score + jnp.concatenate([bias, bias], axis=1)
    top = jnp.max(score, axis=0, keepdims=True) * (SCALE * LOG2E)
    weight = jnp.exp2(score * (SCALE * LOG2E) - top)
    total = jnp.sum(weight, axis=0, keepdims=True)
    result = dot_tn(v_ref[keys, :], weight.astype(BF16)) / total
    att_ref[...] = gather_pair(result, half).astype(BF16)
    lse_ref[0] = top + jnp.log2(total)

    @pl.when(step == pl.num_programs(0) * inner - 1)
    def _():
        ring.from_sibling("own", 0, 1)
        for slot, flips in enumerate(near):
            outward(slot, *flips).start()
        ring.far_halves()
        for name in ("x", "y", "d"):
            ring.from_sibling(name, 0, 1)
        for slot, flips in enumerate(rest):
            outward(4 + slot, *flips).start()
        for slot, flips in enumerate(near + rest):
            outward(slot, *flips).wait()
        ring.sent()


def attend(q, kv, low, grad, grads, dp_size):
    rows, width = q.shape
    keys = kv.shape[0]
    reach = keys - rows
    tiles = rows // QTILE
    pairs = width // LANES
    heads = kv.shape[1] // LANES
    per_head = pairs // heads
    span = reach + QTILE
    right = (grads.shape[0], grads.shape[1] * 5 // 8)
    far = pl.BlockSpec(memory_space=pl.ANY)
    return pl.pallas_call(
        functools.partial(attend_kernel, reach, 2 * math.isqrt(dp_size // GROUP)),
        grid=(heads, tiles, per_head),
        in_specs=[
            pl.BlockSpec((QTILE, LANES), lambda a, t, p: (t, a * per_head + p)),
            pl.BlockSpec((keys, LANES), lambda a, t, p: (0, 2 * (a // 2))),
            pl.BlockSpec((keys, LANES), lambda a, t, p: (0, 2 * (a // 2) + 1)),
            pl.BlockSpec((1, rows), lambda a, t, p: (0, 0)),
            far,
            far,
        ],
        out_specs=[
            pl.BlockSpec((QTILE, LANES), lambda a, t, p: (t, a * per_head + p)),
            pl.BlockSpec((1, 1, 2 * QTILE), lambda a, t, p: ((a * tiles + t) * per_head + p, 0, 0)),
            far,
        ],
        out_shape=[
            jax.ShapeDtypeStruct((rows, width), BF16),
            jax.ShapeDtypeStruct((pairs * tiles, 1, 2 * QTILE), F32),
            jax.ShapeDtypeStruct(grads.shape, BF16),
        ],
        scratch_shapes=[
            pltpu.VMEM((tiles, span, QTILE), F32),
            pltpu.VMEM(right, BF16),
            pltpu.SemaphoreType.DMA,
            pltpu.SemaphoreType.DMA((Ring.COPIES,)),
            pltpu.SemaphoreType.DMA((Ring.COPIES,)),
            pltpu.SemaphoreType.DMA((8,)),
        ],
        input_output_aliases={5: 2},
        compiler_params=pltpu.CompilerParams(
            collective_id=7, has_side_effects=True, vmem_limit_bytes=56 << 20
        ),
        cost_estimate=pl.CostEstimate(
            flops=16 * rows * span * LANES * pairs,
            bytes_accessed=4 * rows * width + 2 * keys * kv.shape[1],
            transcendentals=2 * rows * span * pairs,
        ),
    )(q, kv, kv, low, grad, grads)


def attend_back_kernel(
    reach, wide, z_size, mlp_count,
    q_ref, do_ref, o_ref, k_ref, v_ref, lse_ref, low_ref, cos_ref, sin_ref, cos_all, sin_all,
    *refs,
):
    mlp_ins, refs = refs[:mlp_count], refs[mlp_count:]
    dq_ref, dkv_ref = refs[:2]
    mlp_outs, refs = refs[2 : 2 + mlp_count], refs[2 + mlp_count :]
    bias_ref, dk_acc, dv_acc, own_part, send_part, recv_part, kv_send, kv_recv = refs[:8]
    home = refs[8:]
    block, half, tile, pair = (pl.program_id(at) for at in range(4))
    steps = pl.num_programs(1) * pl.num_programs(2) * pl.num_programs(3)
    inner = (half * pl.num_programs(2) + tile) * pl.num_programs(3) + pair
    step = block * steps + inner
    blocks = own_part.shape[0]
    rows = own_part.shape[1]
    count = reach // rows
    place = lax.axis_index("tensor")

    def exchange(at, distance):
        return pltpu.make_async_remote_copy(
            src_ref=send_part.at[at, pl.ds((count - distance) * rows, rows)],
            dst_ref=recv_part.at[at, distance - 1],
            send_sem=kv_send.at[at, distance - 1], recv_sem=kv_recv.at[at, distance - 1],
            device_id={"tensor": (place + z_size - distance) % z_size}, device_id_type=MESH,
        )

    def each_exchange(at, condition, action):
        for distance in range(1, count + 1):
            pl.when(condition(distance))(
                functools.partial(action, exchange(at, distance), at, distance)
            )

    @pl.when(step == 0)
    def _():
        greet(along_peers(place, z_size) + [device for _, device in others(wide)[1]])
        for copy in send_home(wide, mlp_ins, mlp_outs, *home):
            copy.start()
        fill_bias(bias_ref, low_ref, reach)

    @pl.when(inner == 0)
    def _():
        dk_acc[...] = jnp.zeros_like(dk_acc)
        dv_acc[...] = jnp.zeros_like(dv_acc)

    keys = pl.ds(pl.multiple_of(tile * QTILE, QTILE), bias_ref.shape[1])
    queries = spread_pair(q_ref[...], half)
    grads = spread_pair(do_ref[...], half)
    product = (do_ref[...].astype(F32) * o_ref[...].astype(F32)).T
    row_dot = jnp.concatenate(
        [
            jnp.sum(product[:64], axis=0, keepdims=True),
            jnp.sum(product[64:], axis=0, keepdims=True),
        ],
        axis=1,
    )
    bias = bias_ref[tile]
    key, value = k_ref[keys, :], v_ref[keys, :]
    score = dot_nt(key, queries) + jnp.concatenate([bias, bias], axis=1)
    weight = jnp.exp2(score * (SCALE * LOG2E) - lse_ref[0])
    dv_acc[keys, :] += dot_nn(weight.astype(BF16), grads)
    dscore = (weight * (dot_nt(value, grads) - row_dot)).astype(BF16)
    dk_acc[keys, :] += dot_nn(dscore, queries)
    dq = gather_pair(dot_tn(key, dscore), half) * SCALE
    dq_ref[...] = (dq * cos_ref[...] - swap_halves(dq) * sin_ref[...]).astype(BF16)

    @pl.when(inner == steps - 1)
    def _():
        send_part[block, :, :LANES] = (dk_acc[:reach] * SCALE).astype(BF16)
        send_part[block, :, LANES:] = dv_acc[:reach].astype(BF16)
        own_part[block, :, :LANES] = dk_acc[reach:] * SCALE
        own_part[block, :, LANES:] = dv_acc[reach:]
        each_exchange(block, lambda distance: place >= distance, lambda copy, *_: copy.start())

    @pl.when(step == blocks * steps - 1)
    def _():
        def collect(copy, at, distance):
            copy.wait_recv()
            own_part[at] += recv_part[at, distance - 1].astype(F32)

        for at in range(blocks):
            each_exchange(at, lambda distance: place + distance < z_size, collect)
            dkey = own_part[at, :, :LANES]
            dkey = dkey * cos_all[...] - swap_halves(dkey) * sin_all[...]
            dkv_ref[:, 2 * at * LANES : (2 * at + 1) * LANES] = dkey.astype(BF16)
            dkv_ref[:, (2 * at + 1) * LANES : (2 * at + 2) * LANES] = own_part[
                at, :, LANES:
            ].astype(BF16)
        for at in range(blocks):
            each_exchange(
                at, lambda distance: place >= distance, lambda copy, *_: copy.wait_send()
            )
        for copy in send_home(wide, mlp_ins, mlp_outs, *home):
            copy.wait()


def attend_back(q, do, att, kv, lse, low, cosine, sine, mlp, dp_size, z_size):
    rows, width = q.shape
    keys = kv.shape[0]
    reach = keys - rows
    tiles = rows // QTILE
    pairs = width // LANES
    heads = kv.shape[1] // LANES
    per_head = pairs // heads
    span = reach + QTILE
    blocks = heads // 2

    def pair_at(g, h, t, p):
        return (t, (2 * g + h) * per_head + p)

    def whole(shape):
        return pl.BlockSpec(shape, lambda g, h, t, p: (0, 0), pipeline_mode=pl.Buffered(1))

    table = pl.BlockSpec((QTILE, LANES), lambda g, h, t, p: (t, 0))
    return pl.pallas_call(
        functools.partial(
            attend_back_kernel, reach, 2 * math.isqrt(dp_size // GROUP), z_size, len(mlp)
        ),
        grid=(blocks, 2, tiles, per_head),
        in_specs=[
            pl.BlockSpec((QTILE, LANES), pair_at),
            pl.BlockSpec((QTILE, LANES), pair_at),
            pl.BlockSpec((QTILE, LANES), pair_at),
            pl.BlockSpec((keys, LANES), lambda g, h, t, p: (0, 2 * g)),
            pl.BlockSpec((keys, LANES), lambda g, h, t, p: (0, 2 * g + 1)),
            pl.BlockSpec(
                (1, 1, 2 * QTILE),
                lambda g, h, t, p: (((2 * g + h) * tiles + t) * per_head + p, 0, 0),
            ),
            whole((1, rows)),
            table,
            table,
            whole((rows, LANES)),
            whole((rows, LANES)),
        ]
        + [pl.BlockSpec(memory_space=pl.ANY)] * len(mlp),
        out_specs=[
            pl.BlockSpec((QTILE, LANES), pair_at),
            pl.BlockSpec((rows, kv.shape[1]), lambda g, h, t, p: (0, 0)),
        ]
        + [pl.BlockSpec(memory_space=pl.ANY)] * len(mlp),
        out_shape=[
            jax.ShapeDtypeStruct((rows, width), BF16),
            jax.ShapeDtypeStruct((rows, kv.shape[1]), BF16),
        ]
        + home_shapes(mlp),
        scratch_shapes=[
            pltpu.VMEM((tiles, span, QTILE), F32),
            pltpu.VMEM((keys, LANES), F32),
            pltpu.VMEM((keys, LANES), F32),
            pltpu.VMEM((blocks, rows, 2 * LANES), F32),
            pltpu.VMEM((blocks, reach, 2 * LANES), BF16),
            pltpu.VMEM((blocks, reach // rows, rows, 2 * LANES), BF16),
            pltpu.SemaphoreType.DMA((blocks, reach // rows)),
            pltpu.SemaphoreType.DMA((blocks, reach // rows)),
        ]
        + home_scratch(mlp),
        compiler_params=pltpu.CompilerParams(
            collective_id=5, has_side_effects=True, vmem_limit_bytes=60 << 20
        ),
        cost_estimate=pl.CostEstimate(
            flops=40 * rows * span * LANES * pairs,
            bytes_accessed=8 * rows * width + 4 * keys * kv.shape[1],
            transcendentals=2 * rows * span * pairs,
        ),
    )(q, do, att, kv, kv, lse, low, cosine, sine, cosine, sine, *mlp)


MESH = pl.DeviceIdType.MESH


def neighbours(wide):
    dp = lax.axis_index("dp")
    core, col, row = dp % 2, (dp // 2) % 2, (dp // (2 * wide)) % 2
    sibling = dp + 1 - 2 * core
    beside = dp + 2 - 4 * col
    above = dp + 2 * wide - 4 * wide * row
    return (row, col, core), (sibling, beside, above)


def meet(peers):
    barrier = pltpu.get_barrier_semaphore()
    for peer in peers:
        pl.semaphore_signal(barrier, inc=1, device_id={"dp": peer}, device_id_type=MESH)
    pl.semaphore_wait(barrier, len(peers))


def others(wide):
    (row, col, core), _ = neighbours(wide)
    base = lax.axis_index("dp") - (2 * wide * row + 2 * col + core)
    found = []
    for flip in range(1, GROUP):
        y, x, c = (row + flip // 4) % 2, (col + flip // 2) % 2, (core + flip) % 2
        found.append((4 * y + 2 * x + c, {"dp": base + 2 * wide * y + 2 * x + c}))
    return 4 * row + 2 * col + core, found


def along_peers(place, z_size):
    return [{"tensor": (place + step) % z_size} for step in range(1, z_size)]


def greet(peers):
    barrier = pltpu.get_barrier_semaphore()
    for peer in peers:
        pl.semaphore_signal(barrier, inc=1, device_id=peer, device_id_type=MESH)
    pl.semaphore_wait(barrier, len(peers))


def send_home(wide, ins, outs, own_sem, send_sem, recv_sem):
    mine, found = others(wide)
    copies = []
    for at, (src, dst) in enumerate(zip(ins, outs)):
        part, cols = dst.shape[0], src.shape[1]
        here = pl.ds(pl.multiple_of(mine * cols, LANES), cols)
        for index, (other, device) in enumerate(found):
            copies.append(
                pltpu.make_async_remote_copy(
                    src_ref=src.at[pl.ds(pl.multiple_of(other * part, part), part)],
                    dst_ref=dst.at[:, here],
                    send_sem=send_sem.at[at, index], recv_sem=recv_sem.at[at, index],
                    device_id=device, device_id_type=MESH,
                )
            )
        own = src.at[pl.ds(pl.multiple_of(mine * part, part), part)]
        copies.append(pltpu.make_async_copy(own, dst.at[:, here], own_sem.at[at]))
    return copies


def home_shapes(arrays):
    return [jax.ShapeDtypeStruct((a.shape[0] // GROUP, GROUP * a.shape[1]), BF16) for a in arrays]


def home_scratch(arrays):
    count = len(arrays)
    return [
        pltpu.SemaphoreType.DMA((count,)),
        pltpu.SemaphoreType.DMA((count, GROUP - 1)),
        pltpu.SemaphoreType.DMA((count, GROUP - 1)),
    ]


SIB, XN, YN = 0, 1, 2


def spread_kernel(wide, z_size, mlp_count, *refs):
    attn_count = (len(refs) - 7) // 2 - mlp_count
    count = mlp_count + attn_count
    ins, outs = refs[:count], refs[count : 2 * count]
    own_sem, send_sem, recv_sem, z_send, z_recv, ring_send, ring_recv = refs[2 * count :]
    first = mlp_count
    ring = Ring(wide, outs[first], ins[first].shape[0], ring_send, ring_recv)
    place = lax.axis_index("tensor")
    mine, found = others(wide)
    greet(along_peers(place, z_size) + [device for _, device in found])

    local, copies = [], []
    for at in range(mlp_count):
        src, dst = ins[at], outs[at]
        rows, cols = src.shape[0], dst.shape[1]
        here = pl.ds(pl.multiple_of(mine * rows, rows), rows)
        for index, (other, device) in enumerate(found):
            copies.append(
                pltpu.make_async_remote_copy(
                    src_ref=src.at[:, pl.ds(pl.multiple_of(other * cols, LANES), cols)],
                    dst_ref=dst.at[here],
                    send_sem=send_sem.at[at, index], recv_sem=recv_sem.at[at, index],
                    device_id=device, device_id_type=MESH,
                )
            )
        own = src.at[:, pl.ds(pl.multiple_of(mine * cols, LANES), cols)]
        local.append(pltpu.make_async_copy(own, dst.at[here], own_sem.at[at]))

    def block(at, origin):
        cols = ins[at].shape[1]
        part = pl.ds(pl.multiple_of(origin * cols, LANES), cols)
        return outs[at].at[ring.mine() if at == first else slice(None), part]

    def hop(at, way, step, receive=False):
        sign = 1 - 2 * way
        origin = place - sign * (step if receive else step - 1)
        slot = 2 * (step - 1) + way
        src = block(at, origin) if receive or step > 1 else ins[at]
        return pltpu.make_async_remote_copy(
            src_ref=src, dst_ref=block(at, origin),
            send_sem=z_send.at[at - mlp_count, slot], recv_sem=z_recv.at[at - mlp_count, slot],
            device_id={"tensor": (place + z_size + sign) % z_size}, device_id_type=MESH,
        )

    def sends(way, step):
        if way == 0:
            return (place + 1 < z_size) & (place >= step - 1)
        return (place >= 1) & (place + step - 1 < z_size)

    def receives(way, step):
        return place >= step if way == 0 else place + step < z_size

    for at in range(mlp_count, count):
        local.append(pltpu.make_async_copy(ins[at], block(at, place), own_sem.at[at]))
        for way in range(2):
            pl.when(sends(way, 1))(lambda: hop(at, way, 1).start())
    for copy in copies + local:
        copy.start()

    def advance(at, step):
        for way in range(2):
            pl.when(receives(way, step))(lambda: hop(at, way, step, True).wait_recv())
            if step + 1 < z_size:
                pl.when(sends(way, step + 1))(lambda: hop(at, way, step + 1).start())

    for step in range(1, z_size):
        advance(first, step)
    local.pop(first).wait()
    ring.start_own()
    stages = [ring.first_halves, ring.second_halves]
    for step in range(1, z_size):
        for at in range(first + 1, count):
            advance(at, step)
        if stages:
            stages.pop(0)()
    for stage in stages:
        stage()
    ring.far_halves()
    for name in ("own", "x", "y", "d"):
        ring.from_sibling(name, 0, 1)
    ring.sent()
    for step in range(1, z_size):
        for at in range(mlp_count, count):
            for way in range(2):
                pl.when(sends(way, step))(lambda: hop(at, way, step).wait_send())
    for copy in local + copies:
        copy.wait()


def spread_weights(mlp, attn, dp_size, z_size):
    count = len(mlp) + len(attn)
    spec = pl.BlockSpec(memory_space=pl.ANY)
    out = [jax.ShapeDtypeStruct((GROUP * w.shape[0], w.shape[1] // GROUP), BF16) for w in mlp]
    out += [
        jax.ShapeDtypeStruct(((1 if at else GROUP) * w.shape[0], z_size * w.shape[1]), BF16)
        for at, w in enumerate(attn)
    ]
    return pl.pallas_call(
        functools.partial(spread_kernel, 2 * math.isqrt(dp_size // GROUP), z_size, len(mlp)),
        in_specs=[spec] * count,
        out_specs=[spec] * count,
        out_shape=out,
        scratch_shapes=[
            pltpu.SemaphoreType.DMA((count,)),
            pltpu.SemaphoreType.DMA((len(mlp), GROUP - 1)),
            pltpu.SemaphoreType.DMA((len(mlp), GROUP - 1)),
            pltpu.SemaphoreType.DMA((len(attn), 2 * (z_size - 1))),
            pltpu.SemaphoreType.DMA((len(attn), 2 * (z_size - 1))),
            pltpu.SemaphoreType.DMA((Ring.COPIES,)),
            pltpu.SemaphoreType.DMA((Ring.COPIES,)),
        ],
        compiler_params=pltpu.CompilerParams(collective_id=2, has_side_effects=True),
        cost_estimate=pl.CostEstimate(flops=LONG, bytes_accessed=0, transcendentals=0),
    )(*mlp, *attn)


class Ring:
    FLIP = {SIB: (0, 0, 1), XN: (0, 1, 0), YN: (1, 0, 0)}
    COPIES = 14

    def __init__(self, wide, ref, rows, send_sem, recv_sem):
        (self.row, self.col, self.core), self.peers = neighbours(wide)
        self.ref, self.rows, self.part = ref, rows, rows // 2
        self.send_sem, self.recv_sem = send_sem, recv_sem
        self.sends = {}
        for half in range(2):
            self.sends["own", XN, half] = (2 + half, 0, 0, 0, half)
            self.sends["own", YN, half] = (4 + half, 0, 0, 0, half)
            self.sends["own", SIB, half] = (0 + half, 0, 0, 0, half)
        for half in range(2):
            self.sends["x", SIB, half] = (6 + half, 0, 1, 0, half)
            self.sends["y", SIB, half] = (8 + half, 1, 0, 0, half)
            self.sends["d", SIB, half] = (10 + half, 1, 1, 0, half)
        self.sends["x", YN, 0] = (12, 0, 1, 0, 0)
        self.sends["y", XN, 1] = (13, 1, 0, 0, 1)

    def place(self, dy, dx, dc, half):
        p = 4 * ((self.row + dy) % 2) + 2 * ((self.col + dx) % 2) + (self.core + dc) % 2
        return pl.ds(pl.multiple_of(p * self.rows + half * self.part, self.part), self.part)

    def mine(self):
        p = 4 * self.row + 2 * self.col + self.core
        return pl.ds(pl.multiple_of(p * self.rows, self.rows), self.rows)

    def whole(self, dy, dx, dc):
        p = 4 * ((self.row + dy) % 2) + 2 * ((self.col + dx) % 2) + (self.core + dc) % 2
        return pl.ds(pl.multiple_of(p * self.rows, self.rows), self.rows)

    def copy(self, slot, dy, dx, dc, half, peer):
        where = self.place(dy, dx, dc, half)
        return pltpu.make_async_remote_copy(
            src_ref=self.ref.at[where], dst_ref=self.ref.at[where],
            send_sem=self.send_sem.at[slot], recv_sem=self.recv_sem.at[slot],
            device_id={"dp": self.peers[peer]}, device_id_type=MESH,
        )

    def start(self, name, peer, half):
        self.copy(*self.sends[name, peer, half], peer).start()

    def arrived(self, name, peer, half):
        slot, dy, dx, dc, half = self.sends[name, peer, half]
        fy, fx, fc = self.FLIP[peer]
        self.copy(slot, (dy + fy) % 2, (dx + fx) % 2, (dc + fc) % 2, half, peer).wait_recv()

    def start_own(self):
        for half in range(2):
            for peer in (XN, YN, SIB):
                self.start("own", peer, half)

    def first_halves(self):
        self.arrived("own", XN, 0)
        self.start("x", YN, 0)
        self.start("x", SIB, 0)
        self.arrived("own", YN, 0)
        self.start("y", SIB, 0)

    def second_halves(self):
        self.arrived("own", YN, 1)
        self.start("y", XN, 1)
        self.start("y", SIB, 1)
        self.arrived("own", XN, 1)
        self.start("x", SIB, 1)

    def far_halves(self):
        self.arrived("x", YN, 0)
        self.start("d", SIB, 0)
        self.arrived("y", XN, 1)
        self.start("d", SIB, 1)

    def from_sibling(self, name, *halves):
        for half in halves:
            self.arrived(name, SIB, half)

    def sent(self):
        for (name, peer, half), entry in self.sends.items():
            self.copy(*entry, peer).wait_send()


def project_kernel(
    wide, z_size, x_ref, cos_ref, sin_ref, wkv_ref, wq_ref, wo_ref, grad_ref,
    q_ref, kv_ref, wq_out, wo_out, grad_out,
    wkv_all, wq_all, wo_all, grad_all, keys, own_sem, send_sem, recv_sem, kv_send, kv_recv, out_sem,
):
    place = lax.axis_index("tensor")
    rows = x_ref.shape[0]
    count = keys.shape[0] // rows - 1
    left = pl.ds(0, grad_all.shape[1])
    parts = (
        (wq_ref, wq_all, wq_out), (wo_ref, wo_all, wo_out),
        (grad_ref.at[:, left], grad_all, grad_out.at[:, left]),
    )
    rings = [
        Ring(wide, full, part.shape[0], send_sem.at[at], recv_sem.at[at])
        for at, (part, full, _) in enumerate(parts)
    ]
    local = [
        pltpu.make_async_copy(part, full.at[ring.mine()], own_sem.at[at])
        for at, ((part, full, _), ring) in enumerate(zip(parts, rings))
    ]
    outward = [
        pltpu.make_async_copy(full, out, out_sem.at[at])
        for at, (_, full, out) in enumerate(parts)
    ]
    load = pltpu.make_async_copy(wkv_ref, wkv_all, own_sem.at[len(parts)])
    for copy in local + [load]:
        copy.start()
    keys[: count * rows, :] = jnp.zeros((count * rows, keys.shape[1]), BF16)
    greet([{"dp": peer} for peer in rings[0].peers] + along_peers(place, z_size))
    for copy in local:
        copy.wait()

    def rotated(value):
        return (value * cos_ref[...] + swap_halves(value) * sin_ref[...]).astype(BF16)

    def hop(step):
        return pltpu.make_async_remote_copy(
            src_ref=keys.at[pl.ds((count - step + 1) * rows, rows)],
            dst_ref=keys.at[pl.ds((count - step) * rows, rows)],
            send_sem=kv_send.at[step - 1], recv_sem=kv_recv.at[step - 1],
            device_id={"tensor": (place + 1) % z_size}, device_id_type=MESH,
        )

    def pass_keys(step):
        if step > 1:
            pl.when(place >= step - 1)(lambda: hop(step - 1).wait_recv())
        if step <= count:
            sends = (place + 1 < z_size) & (place >= step - 1)
            pl.when(sends)(lambda: hop(step).start())

    def finish(ring):
        ring.far_halves()
        for name in ("own", "x", "y", "d"):
            ring.from_sibling(name, 0, 1)

    rings[0].start_own()
    load.wait()

    @pl.loop(0, wkv_all.shape[1] // (2 * LANES))
    def _(at):
        n = pl.ds(pl.multiple_of(at * 2 * LANES, LANES), 2 * LANES)
        value = dot_nn(x_ref[...], wkv_all[:, n])
        both = jnp.concatenate([rotated(value[:, :LANES]), value[:, LANES:].astype(BF16)], axis=1)
        keys[pl.ds(count * rows, rows), n] = both

    pass_keys(1)
    rings[0].first_halves()
    rings[0].second_halves()
    rings[1].start_own()
    finish(rings[0])
    outward[0].start()

    @pl.loop(0, wq_all.shape[1] // (2 * LANES))
    def _(at):
        n = pl.ds(pl.multiple_of(at * 2 * LANES, LANES), 2 * LANES)
        value = dot_nn(x_ref[...], wq_all[:, n])
        both = [rotated(value[:, :LANES]), rotated(value[:, LANES:])]
        q_ref[:, n] = jnp.concatenate(both, axis=1)

    for step in range(2, count + 1):
        pass_keys(step)
    rings[1].first_halves()
    rings[1].second_halves()
    rings[2].start_own()
    finish(rings[1])
    outward[1].start()
    rings[2].first_halves()
    rings[2].second_halves()
    finish(rings[2])
    outward[2].start()
    pass_keys(count + 1)
    keys_out = pltpu.make_async_copy(keys, kv_ref, out_sem.at[3])
    keys_out.start()
    for step in range(1, count + 1):
        sends = (place + 1 < z_size) & (place >= step - 1)
        pl.when(sends)(lambda: hop(step).wait_send())
    for ring in rings:
        ring.sent()
    for copy in outward + [keys_out]:
        copy.wait()


def project(x, cosine, sine, wkv, wq, wo, grad, reach, dp_size, z_size):
    rows, width = x.shape
    far = pl.BlockSpec(memory_space=pl.ANY)
    near = pl.BlockSpec(memory_space=pltpu.VMEM)
    whole = [(GROUP * w.shape[0], w.shape[1]) for w in (wq, wo)]
    keys = (reach + rows, wkv.shape[1])
    grads = (GROUP * grad.shape[0], grad.shape[1])
    left = (grads[0], grads[1] * 3 // 8)
    return pl.pallas_call(
        functools.partial(project_kernel, 2 * math.isqrt(dp_size // GROUP), z_size),
        in_specs=[near] * 3 + [far] * 4,
        out_specs=[near] + [far] * 4,
        out_shape=[jax.ShapeDtypeStruct((rows, wq.shape[1]), BF16)]
        + [jax.ShapeDtypeStruct(shape, BF16) for shape in [keys] + whole + [grads]],
        scratch_shapes=[pltpu.VMEM(shape, BF16) for shape in [wkv.shape] + whole + [left, keys]]
        + [
            pltpu.SemaphoreType.DMA((4,)),
            pltpu.SemaphoreType.DMA((3, Ring.COPIES)),
            pltpu.SemaphoreType.DMA((3, Ring.COPIES)),
            pltpu.SemaphoreType.DMA((reach // rows,)),
            pltpu.SemaphoreType.DMA((reach // rows,)),
            pltpu.SemaphoreType.DMA((4,)),
        ],
        compiler_params=pltpu.CompilerParams(
            collective_id=3, has_side_effects=True, vmem_limit_bytes=56 << 20
        ),
        cost_estimate=pl.CostEstimate(
            flops=2 * LONG, bytes_accessed=0, transcendentals=0
        ),
    )(x, cosine, sine, wkv, wq, wo, grad)


def gate_up_kernel(
    wide, own_ref, wg_ref, wu_ref, all_ref, gate_ref, up_ref, hid_ref, core_ref,
    full, stage, wg_all, wu_all, own_sem, load_sem, send_sem, recv_sem, out_sem, all_sem,
):
    rows = own_ref.shape[0]
    cols = gate_ref.shape[1]
    ring = Ring(wide, full, rows, send_sem, recv_sem)
    local = pltpu.make_async_copy(own_ref, full.at[ring.mine()], own_sem)
    local.start()
    loads = [
        pltpu.make_async_copy(wg_ref, wg_all, load_sem.at[0]),
        pltpu.make_async_copy(wu_ref, wu_all, load_sem.at[1]),
    ]
    for copy in loads:
        copy.start()
    meet(ring.peers)
    local.wait()
    ring.start_own()
    for copy in loads:
        copy.wait()

    def out_copies(slot, places):
        where, core, chip = places
        return [
            pltpu.make_async_copy(stage.at[slot, i], ref.at[where], out_sem.at[slot, i])
            for i, ref in enumerate((gate_ref, up_ref, hid_ref))
        ] + [
            pltpu.make_async_copy(stage.at[slot, 2], core_ref.at[core, chip], out_sem.at[slot, 3]),
            pltpu.make_async_copy(full.at[where], all_ref.at[where], all_sem.at[slot]),
        ]

    def step_place(step):
        phase, i = step // 4, step % 4
        high, low = phase // 2, phase % 2
        first, last = (1 - high) * (1 - low), high * low
        middle = high + low - 2 * last
        half = (first + last) * (i % 2) + high * (1 - low)
        dx = middle * (1 - i % 2) + last
        dy = middle * (i % 2) + last
        part = rows // 2
        chip_rows = pl.ds(pl.multiple_of((2 * dy + dx) * rows + half * part, part), part)
        return ring.place(dy, dx, i // 2, half), i // 2, chip_rows

    @pl.loop(0, 16)
    def _(step):
        pl.when(step == 2)(lambda: ring.from_sibling("own", 0, 1))
        pl.when(step == 4)(ring.first_halves)

        @pl.when(step == 6)
        def _():
            ring.from_sibling("x", 0)
            ring.from_sibling("y", 0)

        pl.when(step == 8)(ring.second_halves)

        @pl.when(step == 10)
        def _():
            ring.from_sibling("x", 1)
            ring.from_sibling("y", 1)

        pl.when(step == 12)(ring.far_halves)
        pl.when(step == 14)(lambda: ring.from_sibling("d", 0, 1))

        slot = step % 2
        places = step_place(step)

        @pl.when(step >= 2)
        def _():
            for copy in out_copies(slot, step_place(step - 2)):
                copy.wait()

        x = full[places[0], :]

        @pl.loop(0, cols // NTILE)
        def _(at):
            n = pl.ds(pl.multiple_of(at * NTILE, NTILE), NTILE)
            gate = dot_nn(x, wg_all[:, n])
            up = dot_nn(x, wu_all[:, n])
            stage[slot, 0, :, n] = gate.astype(BF16)
            stage[slot, 1, :, n] = up.astype(BF16)
            stage[slot, 2, :, n] = (gate * up / (1.0 + jnp.exp(-gate))).astype(BF16)

        for copy in out_copies(slot, places):
            copy.start()

    for step in (14, 15):
        for copy in out_copies(step % 2, step_place(step)):
            copy.wait()
    ring.sent()


def gate_up(hn, wg, wu, dp_size):
    rows, width = hn.shape
    cols = wg.shape[1]
    tokens = GROUP * rows
    far = pl.BlockSpec(memory_space=pl.ANY)
    return pl.pallas_call(
        functools.partial(gate_up_kernel, 2 * math.isqrt(dp_size // GROUP)),
        in_specs=[far] * 3,
        out_specs=[far] * 5,
        out_shape=[jax.ShapeDtypeStruct((tokens, width), BF16)]
        + [jax.ShapeDtypeStruct((tokens, cols), BF16)] * 3
        + [jax.ShapeDtypeStruct((2, tokens // 2, cols), BF16)],
        scratch_shapes=[
            pltpu.VMEM((tokens, width), BF16),
            pltpu.VMEM((2, 3, rows // 2, cols), BF16),
            pltpu.VMEM(wg.shape, BF16),
            pltpu.VMEM(wu.shape, BF16),
            pltpu.SemaphoreType.DMA,
            pltpu.SemaphoreType.DMA((2,)),
            pltpu.SemaphoreType.DMA((Ring.COPIES,)),
            pltpu.SemaphoreType.DMA((Ring.COPIES,)),
            pltpu.SemaphoreType.DMA((2, 4)),
            pltpu.SemaphoreType.DMA((2,)),
        ],
        compiler_params=pltpu.CompilerParams(
            collective_id=1, has_side_effects=True, vmem_limit_bytes=56 << 20
        ),
        cost_estimate=pl.CostEstimate(
            flops=SHORT, bytes_accessed=0, transcendentals=0
        ),
    )(hn, wg, wu)


FAR_CHUNK, X_CHUNK, Y_CHUNK, OWN_CHUNK = range(4)


class Reduce:
    COPIES = 10

    def __init__(self, wide, parts, cores, far, near, send_sem, recv_sem):
        self.at, self.peers = neighbours(wide)
        self.parts, self.cores, self.far, self.near = parts, cores, far, near
        self.send_sem, self.recv_sem = send_sem, recv_sem
        self.half = parts.shape[2] // 2

    @staticmethod
    def scratch(rows, cols):
        return [
            pltpu.VMEM((2, 4, rows, cols), BF16),
            pltpu.VMEM((4, rows, cols), BF16),
            pltpu.VMEM((2, rows // 2, cols), BF16),
            pltpu.VMEM((2, rows, cols), BF16),
            pltpu.SemaphoreType.DMA((Reduce.COPIES,)),
            pltpu.SemaphoreType.DMA((Reduce.COPIES,)),
        ]

    def chunk(self, step):
        slot, other = step // 2, 1 - step % 2
        row, col, core = self.at
        dy, dx = 1 - slot % 2, 1 - slot // 2
        place = 4 * ((row + dy) % 2) + 2 * ((col + dx) % 2) + (core + other) % 2
        return place, self.parts.at[other, slot]

    def copy(self, name):
        upper, lower = pl.ds(0, self.half), pl.ds(self.half, self.half)
        mine = self.parts.at[0]
        table = {
            "far0": (self.parts.at[1, FAR_CHUNK], self.cores.at[FAR_CHUNK], SIB),
            "x": (self.parts.at[1, X_CHUNK], self.cores.at[X_CHUNK], SIB),
            "y": (self.parts.at[1, Y_CHUNK], self.cores.at[Y_CHUNK], SIB),
            "own": (self.parts.at[1, OWN_CHUNK], self.cores.at[OWN_CHUNK], SIB),
            "far_x": (mine.at[FAR_CHUNK, lower], self.far.at[0], XN),
            "far_y": (mine.at[FAR_CHUNK, upper], self.far.at[1], YN),
            "x_upper": (mine.at[X_CHUNK, upper], self.near.at[0, upper], XN),
            "x_lower": (mine.at[X_CHUNK, lower], self.near.at[0, lower], XN),
            "y_upper": (mine.at[Y_CHUNK, upper], self.near.at[1, upper], YN),
            "y_lower": (mine.at[Y_CHUNK, lower], self.near.at[1, lower], YN),
        }
        src, dst, peer = table[name]
        at = list(table).index(name)
        return pltpu.make_async_remote_copy(
            src_ref=src, dst_ref=dst, send_sem=self.send_sem.at[at],
            recv_sem=self.recv_sem.at[at], device_id={"dp": self.peers[peer]},
            device_id_type=MESH,
        )

    def start(self, *names):
        for name in names:
            self.copy(name).start()

    def add(self, slot, start, other):
        count = other.shape[0] // STRIP

        @pl.loop(0, count)
        def _(at):
            here = pl.ds(pl.multiple_of(start + at * STRIP, STRIP), STRIP)
            there = pl.ds(pl.multiple_of(at * STRIP, STRIP), STRIP)
            value = self.parts[0, slot, here, :].astype(F32) + other[there, :].astype(F32)
            self.parts[0, slot, here, :] = value.astype(BF16)

    def merge_core(self, slot, name):
        self.copy(name).wait_recv()
        self.add(slot, 0, self.cores.at[slot])

    def after(self, step):
        names = ("far0", "x", "y", "own")
        for slot in range(4):
            pl.when(step == 2 * slot)(functools.partial(self.start, names[slot]))

        @pl.when(step == 1)
        def _():
            self.merge_core(FAR_CHUNK, "far0")
            self.start("far_x", "far_y")

        @pl.when(step == 3)
        def _():
            self.merge_core(X_CHUNK, "x")
            self.start("x_lower")

        @pl.when(step == 5)
        def _():
            self.merge_core(Y_CHUNK, "y")
            self.start("y_upper")

    def pass_on(self):
        self.copy("far_y").wait_recv()
        self.add(X_CHUNK, 0, self.far.at[1])
        self.start("x_upper")
        self.copy("far_x").wait_recv()
        self.add(Y_CHUNK, self.half, self.far.at[0])
        self.start("y_lower")

    def finish(self, store):
        for name in ("own", "x_upper", "x_lower", "y_upper", "y_lower"):
            self.copy(name).wait_recv()

        @pl.loop(0, 2 * self.half // STRIP)
        def _(at):
            here = pl.ds(pl.multiple_of(at * STRIP, STRIP), STRIP)
            value = self.parts[0, OWN_CHUNK, here, :].astype(F32)
            value += self.cores[OWN_CHUNK, here, :].astype(F32)
            value += self.near[0, here, :].astype(F32)
            value += self.near[1, here, :].astype(F32)
            store(here, value)

    def sent(self):
        for name in (
            "far0", "x", "y", "own", "far_x", "far_y", "x_upper", "x_lower", "y_upper", "y_lower",
        ):
            self.copy(name).wait_send()


def hidden_back_kernel(
    wide, gain_ref, h_ref, grad_ref, dgate_ref, dup_ref, wg_ref, wu_ref,
    dh_ref, low_ref, gain_out,
    loaded, wg_all, wu_all, h_all, grad_all, load_sem, own_sem, *scratch,
):
    ring = Reduce(wide, *scratch)
    rows = dh_ref.shape[0]

    def loads(step):
        chunk, _ = ring.chunk(step)
        here = pl.ds(pl.multiple_of(chunk * rows, rows), rows)
        return [
            pltpu.make_async_copy(
                ref.at[here], loaded.at[step % 2, at], load_sem.at[step % 2, at]
            )
            for at, ref in enumerate((dgate_ref, dup_ref))
        ]

    pairs = ((wg_ref, wg_all), (wu_ref, wu_all), (h_ref, h_all), (grad_ref, grad_all))
    whole = [
        pltpu.make_async_copy(src, dst, own_sem.at[at]) for at, (src, dst) in enumerate(pairs)
    ]
    for copy in loads(0) + whole:
        copy.start()
    meet(ring.peers)
    for copy in whole[:2]:
        copy.wait()

    @pl.loop(0, 8)
    def _(step):
        @pl.when(step < 7)
        def _():
            for copy in loads(step + 1):
                copy.start()

        for copy in loads(step):
            copy.wait()
        _, target = ring.chunk(step)
        dgate, dup = loaded[step % 2, 0], loaded[step % 2, 1]

        @pl.loop(0, dh_ref.shape[1] // NTILE)
        def _(at):
            n = pl.ds(pl.multiple_of(at * NTILE, NTILE), NTILE)
            value = dot_nt(dgate, wg_all[n, :]) + dot_nt(dup, wu_all[n, :])
            target[:, n] = value.astype(BF16)

        ring.after(step)

    ring.pass_on()
    for copy in whole[2:]:
        copy.wait()
    gain_out[...] = jnp.zeros_like(gain_out)

    def store(here, value):
        h = h_all[here, :]
        scale = rms_scale(h)
        gained = value * gain_ref[...]
        inner = jnp.mean(gained * h, axis=1, keepdims=True)
        gain_out[...] += value * h * scale
        total = grad_all[here, :].astype(F32) + scale * gained
        total -= h * (scale * scale * scale * inner)
        dh_ref[here, :] = total
        low_ref[here, :] = total.astype(BF16)

    ring.finish(store)
    ring.sent()


def hidden_back(gain, h, grad, dgate, dup, wg, wu, dp_size):
    tokens, cols = dgate.shape
    rows, width = h.shape
    far = pl.BlockSpec(memory_space=pl.ANY)
    near = pl.BlockSpec(memory_space=pltpu.VMEM)
    return pl.pallas_call(
        functools.partial(hidden_back_kernel, 2 * math.isqrt(dp_size // GROUP)),
        in_specs=[near] + [far] * 6,
        out_specs=[near] * 3,
        out_shape=[
            jax.ShapeDtypeStruct((rows, width), F32),
            jax.ShapeDtypeStruct((rows, width), BF16),
            jax.ShapeDtypeStruct((STRIP, width), F32),
        ],
        scratch_shapes=[
            pltpu.VMEM((2, 2, rows, cols), BF16),
            pltpu.VMEM(wg.shape, BF16),
            pltpu.VMEM(wu.shape, BF16),
            pltpu.VMEM(h.shape, F32),
            pltpu.VMEM(grad.shape, BF16),
            pltpu.SemaphoreType.DMA((2, 2)),
            pltpu.SemaphoreType.DMA((4,)),
        ]
        + Reduce.scratch(rows, width),
        compiler_params=pltpu.CompilerParams(
            collective_id=6, has_side_effects=True, vmem_limit_bytes=62 << 20
        ),
        cost_estimate=pl.CostEstimate(
            flops=2 * LONG, bytes_accessed=4 * rows * width, transcendentals=0
        ),
    )(gain, h, grad, dgate, dup, wg, wu)


def tail_kernel(
    wide, z_size, x_ref, dq_ref, dkv_ref, wo_ref, gain_ref,
    raw_ref, dh_ref, wq_ref, wkv_ref, *refs
):
    wq_out, wkv_out, wo_out, gain_out, grad_out = refs[:5]
    scratch = refs[5:]
    own_scratch = scratch[:12]
    sums, zrecv, gain_z, gain_p, z_send, z_recv, g_send, g_recv = scratch[12:20]
    wo_recv, w_send, w_recv = scratch[20:23]
    wq_all, wkv_all, raw, dh, dxn, gain_sum, load_sem = scratch[23:]
    rings = [Reduce(wide, *own_scratch[6 * at : 6 * at + 6]) for at in range(2)]
    place = lax.axis_index("tensor")
    mine, found = others(wide)
    along = along_peers(place, z_size)
    around = [device for _, device in found]

    tiles, tile_rows = raw.shape[0], raw.shape[1]
    loads = [
        pltpu.make_async_copy(wq_ref, wq_all, load_sem.at[0]),
        pltpu.make_async_copy(wkv_ref, wkv_all, load_sem.at[1]),
    ]
    for tile in range(tiles):
        here = pl.ds(tile * tile_rows, tile_rows)
        loads += [
            pltpu.make_async_copy(raw_ref.at[here], raw.at[tile], load_sem.at[2 + 2 * tile]),
            pltpu.make_async_copy(dh_ref.at[here], dh.at[tile], load_sem.at[3 + 2 * tile]),
        ]
    for copy in loads:
        copy.start()
    greet(along + around)

    wo_part = wo_out.shape[1]
    wo_copies = [
        pltpu.make_async_remote_copy(
            src_ref=wo_ref.at[
                :,
                pl.ds(pl.multiple_of((place + at + 1) % z_size * wo_part, LANES), wo_part),
            ],
            dst_ref=wo_recv.at[at], send_sem=w_send.at[at], recv_sem=w_recv.at[at],
            device_id=peer, device_id_type=MESH,
        )
        for at, peer in enumerate(along)
    ]
    for copy in wo_copies:
        copy.start()

    rights = (dq_ref, dkv_ref)
    rows = sums.shape[0]
    outs = (wq_out, wkv_out)
    starts = [0, rights[0].shape[1]]
    z_copies = []

    def partial_sums(index):
        ring, right = rings[index], rights[index]

        @pl.loop(0, 8)
        def _(step):
            chunk, target = ring.chunk(step)
            x = x_ref[:, pl.ds(pl.multiple_of(chunk * rows, rows), rows)].T

            @pl.loop(0, right.shape[1] // NTILE)
            def _(at):
                n = pl.ds(pl.multiple_of(at * NTILE, NTILE), NTILE)
                target[:, n] = dot_nn(x, right[:, n]).astype(BF16)

            ring.after(step)

    gain_sum[...] = jnp.zeros_like(gain_sum)

    def input_rows(tile):
        part = pl.ds(tile * tile_rows, tile_rows)
        dq, dkv = dq_ref[part, :], dkv_ref[part, :]

        @pl.loop(0, dxn.shape[1] // NTILE)
        def _(at):
            n = pl.ds(pl.multiple_of(at * NTILE, NTILE), NTILE)
            dxn[:, n] = dot_nt(dq, wq_all[n, :]) + dot_nt(dkv, wkv_all[n, :])

        @pl.loop(0, tile_rows // STRIP)
        def _(at):
            here = pl.ds(pl.multiple_of(at * STRIP, STRIP), STRIP)
            there = pl.ds(pl.multiple_of(tile * tile_rows + at * STRIP, STRIP), STRIP)
            grad, value = dxn[here, :], raw[tile, here, :].astype(F32)
            scale = rms_scale(value)
            gained = grad * gain_ref[0:1, :]
            inner = jnp.mean(gained * value, axis=1, keepdims=True)
            gain_sum[...] += grad * value * scale
            total = scale * gained - value * (scale * scale * scale * inner)
            grad_out[there, :] = (dh[tile, here, :] + total).astype(BF16)

    def send_along(index):
        ring, start = rings[index], starts[index]
        cols = rights[index].shape[1]
        part = cols // z_size

        def store(here, value):
            sums[here, pl.ds(start, cols)] = value.astype(BF16)

        ring.finish(store)
        for at, peer in enumerate(along):
            other = (place + at + 1) % z_size
            copy = pltpu.make_async_remote_copy(
                src_ref=sums.at[:, pl.ds(pl.multiple_of(start + other * part, LANES), part)],
                dst_ref=zrecv.at[at, :, pl.ds(start // z_size, part)],
                send_sem=z_send.at[index, at], recv_sem=z_recv.at[index, at],
                device_id=peer, device_id_type=MESH,
            )
            z_copies.append(copy)
            copy.start()

    partial_sums(0)
    for copy in loads:
        copy.wait()
    input_rows(0)
    rings[0].pass_on()
    partial_sums(1)
    for tile in range(1, tiles):
        input_rows(tile)

    gain_z[place, 0:1] = jnp.sum(gain_sum[...], axis=0, keepdims=True)
    gain_z[place, 1:2] = gain_ref[1:2, :]
    gain_copies = [
        pltpu.make_async_remote_copy(
            src_ref=gain_z.at[place], dst_ref=gain_z.at[place], send_sem=g_send.at[at],
            recv_sem=g_recv.at[at], device_id=peer, device_id_type=MESH,
        )
        for at, peer in enumerate(along)
    ]
    for copy in gain_copies:
        copy.start()
    rings[1].pass_on()
    send_along(0)

    for copy in gain_copies:
        copy.wait_recv()
    total = gain_z[0]
    for at in range(1, z_size):
        total = total + gain_z[at]
    gain_p[mine] = total
    for at, peer in enumerate(around):
        copy = pltpu.make_async_remote_copy(
            src_ref=gain_p.at[mine], dst_ref=gain_p.at[mine],
            send_sem=g_send.at[z_size - 1 + at], recv_sem=g_recv.at[z_size - 1 + at],
            device_id=peer, device_id_type=MESH,
        )
        gain_copies.append(copy)
        copy.start()
    for copy in wo_copies:
        copy.wait()
    total = wo_ref[:, pl.ds(pl.multiple_of(place * wo_part, LANES), wo_part)].astype(F32)
    for at in range(z_size - 1):
        total += wo_recv[at].astype(F32)
    wo_out[...] = total
    send_along(1)

    for copy in gain_copies[z_size - 1 :]:
        copy.wait_recv()
    total = gain_p[0]
    for at in range(1, GROUP):
        total = total + gain_p[at]
    gain_out[...] = total
    for copy in z_copies:
        copy.wait_recv()
    for index in range(2):
        part = rights[index].shape[1] // z_size
        own = pl.ds(pl.multiple_of(starts[index] + place * part, LANES), part)
        value = sums[:, own].astype(F32)
        for at in range(z_size - 1):
            value += zrecv[at, :, pl.ds(starts[index] // z_size, part)].astype(F32)
        outs[index][...] = value
    for copy in z_copies + gain_copies:
        copy.wait_send()
    for ring in rings:
        ring.sent()


def last_grads(x, dq, dkv, wo_sum, gains, raw, dh, wq, wkv, dp_size, z_size):
    tokens, width = x.shape
    rows = width // GROUP
    tiles = tokens // QTILE
    near = pl.BlockSpec(memory_space=pltpu.VMEM)
    far = pl.BlockSpec(memory_space=pl.ANY)
    sizes = [dq.shape[1], dkv.shape[1]]
    scratch = []
    for cols in sizes:
        scratch += Reduce.scratch(rows, cols)
    total = sum(sizes)
    return pl.pallas_call(
        functools.partial(tail_kernel, 2 * math.isqrt(dp_size // GROUP), z_size),
        in_specs=[near] * 5 + [far] * 4,
        out_specs=[near] * 5,
        out_shape=[jax.ShapeDtypeStruct((rows, cols // z_size), F32) for cols in sizes]
        + [
            jax.ShapeDtypeStruct((rows, wo_sum.shape[1] // z_size), F32),
            jax.ShapeDtypeStruct(gains.shape, F32),
            jax.ShapeDtypeStruct((tokens, width), BF16),
        ],
        scratch_shapes=scratch
        + [
            pltpu.VMEM((rows, total), BF16),
            pltpu.VMEM((z_size - 1, rows, total // z_size), BF16),
            pltpu.VMEM((z_size, *gains.shape), F32),
            pltpu.VMEM((GROUP, *gains.shape), F32),
            pltpu.SemaphoreType.DMA((2, z_size - 1)),
            pltpu.SemaphoreType.DMA((2, z_size - 1)),
            pltpu.SemaphoreType.DMA((z_size - 1 + GROUP - 1,)),
            pltpu.SemaphoreType.DMA((z_size - 1 + GROUP - 1,)),
            pltpu.VMEM((z_size - 1, rows, wo_sum.shape[1] // z_size), BF16),
            pltpu.SemaphoreType.DMA((z_size - 1,)),
            pltpu.SemaphoreType.DMA((z_size - 1,)),
            pltpu.VMEM(wq.shape, BF16),
            pltpu.VMEM(wkv.shape, BF16),
            pltpu.VMEM((tiles, QTILE, width), BF16),
            pltpu.VMEM((tiles, QTILE, width), F32),
            pltpu.VMEM((QTILE, width), F32),
            pltpu.VMEM((STRIP, width), F32),
            pltpu.SemaphoreType.DMA((2 + 2 * tiles,)),
        ],
        compiler_params=pltpu.CompilerParams(
            collective_id=4, has_side_effects=True, vmem_limit_bytes=62 << 20
        ),
        cost_estimate=pl.CostEstimate(flops=SHORT, bytes_accessed=0, transcendentals=0),
    )(x, dq, dkv, wo_sum, gains, raw, dh, wq, wkv)


class Layout:
    def __init__(self, dp_size):
        self.blocks = dp_size // GROUP
        side = math.isqrt(self.blocks)
        self.rows, self.cols = side, self.blocks // side
        wide = 2 * self.cols

        def index(by, bx, y, x, core):
            return ((2 * by + y) * wide + 2 * bx + x) * 2 + core

        places = [(y, x, c) for y in range(2) for x in range(2) for c in range(2)]
        spots = [(by, bx) for by in range(self.rows) for bx in range(self.cols)]
        self.inner = [[index(*s, *p) for p in places] for s in spots]
        self.outer = [[index(*s, *p) for s in spots] for p in places]

    def groups(self):
        return None if self.blocks == 1 else self.inner

    def to_rows(self, array):
        if self.blocks == 1:
            return array
        rest = array.shape[1:]
        split = array.reshape(2, 2, 2, self.rows, self.cols, -1, *rest)
        order = (3, 0, 4, 1, 2, 5) + tuple(range(6, 6 + len(rest)))
        return split.transpose(order).reshape(array.shape)

    def from_rows(self, array):
        if self.blocks == 1:
            return array
        rest = array.shape[1:]
        split = array.reshape(self.rows, 2, self.cols, 2, 2, -1, *rest)
        order = (1, 3, 4, 0, 2, 5) + tuple(range(6, 6 + len(rest)))
        return split.transpose(order).reshape(array.shape)

    def from_cols(self, array):
        return array if self.blocks == 1 else self.from_rows(array.T).T

    def gather_outer(self, array):
        if self.blocks == 1:
            return array
        return lax.all_gather(array, "dp", axis_index_groups=self.outer, axis=0, tiled=True)

    def scatter_outer(self, array):
        if self.blocks == 1:
            return array
        return lax.psum_scatter(
            array, "dp", scatter_dimension=0, axis_index_groups=self.outer, tiled=True
        )

    def swap(self, array, flip):
        pairs = [
            (block[at], block[at ^ flip]) for block in self.inner for at in range(GROUP)
        ]
        return lax.ppermute(array, "dp", pairs)

    def sum_outer(self, array):
        if self.blocks == 1:
            return array
        return lax.psum(array, "dp", axis_index_groups=self.outer)

    def gather(self, array):
        return lax.all_gather(array, "dp", axis_index_groups=self.groups(), axis=0, tiled=True)

    def scatter(self, array):
        return lax.psum_scatter(
            array, "dp", scatter_dimension=0, axis_index_groups=self.groups(), tiled=True
        )


def rms_scale(values):
    return lax.rsqrt(jnp.mean(values * values, axis=-1, keepdims=True) + NORM_EPS)


def per_device(
    dp_size, z_size, activations, segment_ids, attn_gain, w_query, w_key, w_value, w_out,
    mlp_gain, w_gate, w_up, w_down, cotangent,
):
    layout = Layout(dp_size)
    rows, width = activations.shape[1:]
    x = activations[0].astype(F32)
    place = lax.axis_index("tensor")
    reach = -(-(MOST_DOC - 1) // rows) * rows

    def shift(array, step):
        pairs = [(at, at + step) for at in range(z_size) if 0 <= at + step < z_size]
        return lax.ppermute(array, "tensor", pairs)

    starts = document_starts(segment_ids[0])
    own_starts = lax.dynamic_slice_in_dim(starts, place * rows, rows)
    own_tokens = place * rows + jnp.arange(rows, dtype=jnp.int32)
    cosine, sine = rope_tables(own_tokens - own_starts)
    low = (own_starts - place * rows + reach)[None, :]

    shards = [
        layout.gather_outer(w)
        for w in (w_gate, w_up, w_down, jnp.concatenate([w_key, w_value], axis=1), w_query, w_out)
    ]
    spread = spread_weights(shards[:3], shards[3:], dp_size, z_size)
    def gather_z(array):
        return layout.to_rows(lax.all_gather(array, "tensor", axis=1, tiled=True))

    wg, wu = gather_z(spread[0]), gather_z(spread[1])

    def along_z(total):
        return lax.psum_scatter(
            layout.from_rows(total), "tensor", scatter_dimension=1, tiled=True
        )

    r1 = rms_scale(x)
    xn = (x * r1 * attn_gain).astype(BF16)
    q, kv_all, wq, wo, dy = project(
        layout.from_cols(xn), cosine, sine, *spread[3:], cotangent[0], reach, dp_size, z_size
    )
    wd = gather_z(spread[2])
    wkv, wq, wo = (layout.to_rows(w) for w in (spread[3], wq, wo))
    att, lse, dy = attend(q, kv_all, low, cotangent[0], dy, dp_size)
    h = x + dot_nt(att, wo)

    r2 = rms_scale(h)
    hn, gate, up, hidden, by_core = gate_up((h * r2 * mlp_gain).astype(BF16), wg, wu, dp_size)
    part = rows // 2
    away = dot_nt(by_core[1], wd).astype(BF16)
    dy, away = lax.optimization_barrier((dy, away))
    total_wd = dot_tn(dy, hidden).astype(BF16)
    part_wd = along_z(total_wd)
    from_core = layout.swap(away, 1)

    def out_rows(start, count, *more):
        some = slice(start * part, (start + count) * part)
        total = dot_nt(by_core[0, some], wd) + from_core[some].astype(F32)
        for other in more:
            total = total + other.astype(F32)
        return total.astype(BF16)

    far_y, far_x, x_lower, y_upper = (out_rows(at, 1) for at in (6, 7, 3, 4))
    dy, far_x, far_y, x_lower, y_upper = lax.optimization_barrier(
        (dy, far_x, far_y, x_lower, y_upper)
    )
    from_x, from_y = layout.swap(far_x, 2), layout.swap(far_y, 4)
    x_lower, y_upper = layout.swap(x_lower, 2), layout.swap(y_upper, 4)
    gate, up = gate.astype(F32), up.astype(F32)
    sigma = jax.nn.sigmoid(gate)
    dhid = dot_nn(dy, wd)
    dgate = (dhid * up * sigma * (1.0 + gate * (1.0 - sigma))).astype(BF16)
    dup = (dhid * gate * sigma).astype(BF16)
    dgate, dup, from_x, from_y = lax.optimization_barrier((dgate, dup, from_x, from_y))
    x_upper, y_lower = out_rows(2, 1, from_y), out_rows(5, 1, from_x)
    dgate, dup, x_upper, y_lower = lax.optimization_barrier((dgate, dup, x_upper, y_lower))
    x_upper, y_lower = layout.swap(x_upper, 2), layout.swap(y_lower, 4)
    total_wg = dot_tn(hn, dgate).astype(BF16)
    part_wg = along_z(total_wg)
    dup, total_wg, x_lower, y_upper = lax.optimization_barrier((dup, total_wg, x_lower, y_upper))
    total_wu = dot_tn(hn, dup).astype(BF16)
    dup, total_wu = lax.optimization_barrier((dup, total_wu))
    part_wu = along_z(total_wu)
    dup, x_upper, y_lower = lax.optimization_barrier((dup, x_upper, y_lower))
    dh, dhb, gain_two = hidden_back(
        mlp_gain[None], h, cotangent[0], dgate, dup, wg, wu, dp_size
    )
    gain_two = jnp.sum(gain_two, axis=0)
    dhb, part_wd = lax.optimization_barrier((dhb, part_wd))
    datt = dot_nn(dhb, wo).astype(BF16)
    total_wo = layout.from_rows(dot_tn(dhb, att).astype(BF16))
    datt, part_wg, total_wo = lax.optimization_barrier((datt, part_wg, total_wo))
    datt, part_wu = lax.optimization_barrier((datt, part_wu))
    part_wo = layout.scatter(total_wo)
    dq, dkv, wd_grad, wg_grad, wu_grad = attend_back(
        q, datt, att, kv_all, lse, low, cosine, sine, (part_wd, part_wg, part_wu), dp_size, z_size
    )
    dq, part_wo = lax.optimization_barrier((dq, part_wo))
    wq_grad, wkv_grad, wo_grad, gains, input_grad = last_grads(
        layout.from_cols(xn), dq, dkv, part_wo, jnp.stack([attn_gain, gain_two]),
        activations[0], dh, wq, wkv, dp_size, z_size,
    )
    gains = layout.sum_outer(gains)
    output = h + out_rows(0, 2).astype(F32)
    output = output + jnp.concatenate([x_upper, x_lower]).astype(F32)
    output = output + jnp.concatenate([y_upper, y_lower]).astype(F32)
    wo_grad, wq_grad, wkv_grad, wd_grad, wg_grad, wu_grad = (
        layout.scatter_outer(grad).astype(F32)
        for grad in (wo_grad, wq_grad, wkv_grad, wd_grad, wg_grad, wu_grad)
    )
    key_cols = w_key.shape[1]
    return (
        output.astype(BF16)[None],
        input_grad[None],
        gains[0],
        wq_grad,
        wkv_grad[:, :key_cols],
        wkv_grad[:, key_cols:],
        wo_grad,
        gains[1],
        wg_grad,
        wu_grad,
        wd_grad,
    )


def solution(mesh):
    split = P("dp", "tensor")
    tokens = P("dp", "tensor", None)
    in_specs = (
        tokens, P("dp", None), P(), split, split, split, split, P(), split, split, split, tokens,
    )
    out_specs = (tokens, tokens, P(), split, split, split, split, P(), split, split, split)
    return jax.shard_map(
        functools.partial(per_device, mesh.shape["dp"], mesh.shape["tensor"]),
        mesh=mesh, in_specs=in_specs, out_specs=out_specs, check_vma=False,
    )
```

```python
import functools
import math

import jax
import jax.numpy as jnp
from jax import lax
from jax.experimental import pallas as pl
from jax.experimental.pallas import tpu as pltpu
from jax.sharding import PartitionSpec as P

HEAD_DIM = 64
DOCS = 4
MOST_DOC = 1024
NORM_EPS = 1e-05
ROPE_THETA = 500000.0
GROUP = 8
LANES = 128
QTILE = 256
SCALE = HEAD_DIM ** (-0.5)
LOG2E = 1.4426950408889634
FAR = -1e30
NTILE = 512
STRIP = 16
LONG = 60_000_000_000
SHORT = 1_000_000

F32 = jnp.float32
BF16 = jnp.bfloat16


def dot_nn(left, right):
    return lax.dot_general(left, right, (((1,), (0,)), ((), ())), preferred_element_type=F32)


def dot_nt(left, right):
    return lax.dot_general(left, right, (((1,), (1,)), ((), ())), preferred_element_type=F32)


def dot_tn(left, right):
    return lax.dot_general(left, right, (((0,), (0,)), ((), ())), preferred_element_type=F32)


def document_starts(segments):
    doc_ids = jnp.arange(DOCS, dtype=jnp.int32)
    counts = jnp.sum((segments[:, None] == doc_ids).astype(jnp.int32), axis=0)
    before = (doc_ids < segments[:, None]).astype(jnp.int32)
    return jnp.sum(before * counts[None, :], axis=-1)


def rope_tables(positions):
    half = HEAD_DIM // 2
    frequency = jnp.exp(
        jnp.arange(half, dtype=F32) * (-2.0 * math.log(ROPE_THETA) / HEAD_DIM)
    )
    angles = positions.astype(F32)[:, None] * frequency
    cosine, sine = jnp.cos(angles), jnp.sin(angles)
    wide_cos = jnp.concatenate([cosine] * 4, axis=1)
    wide_sin = jnp.concatenate([-sine, sine, -sine, sine], axis=1)
    return wide_cos, wide_sin


def swap_halves(values):
    lane = lax.broadcasted_iota(jnp.int32, values.shape, 1)
    ahead = pltpu.roll(values, LANES - 32, 1)
    behind = pltpu.roll(values, 32, 1)
    return jnp.where((lane % 64) < 32, ahead, behind)


def fill_bias(bias_ref, low_ref, reach):
    span = bias_ref.shape[1]
    for tile in range(bias_ref.shape[0]):
        row = lax.broadcasted_iota(jnp.int32, (span, QTILE), 0)
        col = lax.broadcasted_iota(jnp.int32, (span, QTILE), 1)
        low = low_ref[0:1, tile * QTILE : (tile + 1) * QTILE]
        allowed = (row <= reach + col) & (row + tile * QTILE >= low)
        bias_ref[tile] = jnp.where(allowed, 0.0, FAR)


def spread_pair(pair, half):
    wide = pair.astype(F32)
    turned = pltpu.roll(wide, 64, 1)
    lane = lax.broadcasted_iota(jnp.int32, wide.shape, 1)
    mine = (lane // 64) == half
    even = half == 0
    first = jnp.where(mine, jnp.where(even, wide, turned), 0.0)
    second = jnp.where(mine, jnp.where(even, turned, wide), 0.0)
    return jnp.concatenate([first, second], axis=0).astype(BF16)


def gather_pair(transposed, half):
    count = transposed.shape[1] // 2
    mine = jnp.where(half == 0, transposed[:64], transposed[64:])
    return jnp.concatenate([mine[:, :count], mine[:, count:]], axis=0).T


def attend_kernel(
    reach, wide, q_ref, k_ref, v_ref, low_ref, own_ref, _, att_ref, lse_ref, all_ref,
    bias_ref, full, own_sem, send_sem, recv_sem, out_sem,
):
    head, tile, pair = pl.program_id(0), pl.program_id(1), pl.program_id(2)
    half = head % 2
    inner = pl.num_programs(1) * pl.num_programs(2)
    step = head * inner + tile * pl.num_programs(2) + pair
    ring = Ring(wide, full, own_ref.shape[0], send_sem, recv_sem)
    right = pl.ds(own_ref.shape[1] - full.shape[1], full.shape[1])

    def outward(slot, *flips):
        where = ring.whole(*flips)
        return pltpu.make_async_copy(full.at[where], all_ref.at[where, right], out_sem.at[slot])

    near = [(0, 0, 0), (0, 0, 1), (0, 1, 0), (1, 0, 0)]
    rest = [(0, 1, 1), (1, 0, 1), (1, 1, 0), (1, 1, 1)]

    @pl.when(step == 0)
    def _():
        local = pltpu.make_async_copy(own_ref.at[:, right], full.at[ring.mine()], own_sem)
        local.start()
        meet(ring.peers)
        local.wait()
        ring.start_own()
        fill_bias(bias_ref, low_ref, reach)

    pl.when(step == 2 * inner)(ring.first_halves)
    pl.when(step == 4 * inner)(ring.second_halves)

    keys = pl.ds(pl.multiple_of(tile * QTILE, QTILE), bias_ref.shape[1])
    queries = spread_pair(q_ref[...], half)
    bias = bias_ref[tile]
    score = dot_nt(k_ref[keys, :], queries)
    score = score + jnp.concatenate([bias, bias], axis=1)
    top = jnp.max(score, axis=0, keepdims=True) * (SCALE * LOG2E)
    weight = jnp.exp2(score * (SCALE * LOG2E) - top)
    total = jnp.sum(weight, axis=0, keepdims=True)
    result = dot_tn(v_ref[keys, :], weight.astype(BF16)) / total
    att_ref[...] = gather_pair(result, half).astype(BF16)
    lse_ref[0] = top + jnp.log2(total)

    @pl.when(step == pl.num_programs(0) * inner - 1)
    def _():
        ring.from_sibling("own", 0, 1)
        for slot, flips in enumerate(near):
            outward(slot, *flips).start()
        ring.far_halves()
        for name in ("x", "y", "d"):
            ring.from_sibling(name, 0, 1)
        for slot, flips in enumerate(rest):
            outward(4 + slot, *flips).start()
        for slot, flips in enumerate(near + rest):
            outward(slot, *flips).wait()
        ring.sent()


def attend(q, kv, low, grad, grads, dp_size):
    rows, width = q.shape
    keys = kv.shape[0]
    reach = keys - rows
    tiles = rows // QTILE
    pairs = width // LANES
    heads = kv.shape[1] // LANES
    per_head = pairs // heads
    span = reach + QTILE
    right = (grads.shape[0], grads.shape[1] * 5 // 8)
    far = pl.BlockSpec(memory_space=pl.ANY)
    return pl.pallas_call(
        functools.partial(attend_kernel, reach, 2 * math.isqrt(dp_size // GROUP)),
        grid=(heads, tiles, per_head),
        in_specs=[
            pl.BlockSpec((QTILE, LANES), lambda a, t, p: (t, a * per_head + p)),
            pl.BlockSpec((keys, LANES), lambda a, t, p: (0, 2 * (a // 2))),
            pl.BlockSpec((keys, LANES), lambda a, t, p: (0, 2 * (a // 2) + 1)),
            pl.BlockSpec((1, rows), lambda a, t, p: (0, 0)),
            far,
            far,
        ],
        out_specs=[
            pl.BlockSpec((QTILE, LANES), lambda a, t, p: (t, a * per_head + p)),
            pl.BlockSpec((1, 1, 2 * QTILE), lambda a, t, p: ((a * tiles + t) * per_head + p, 0, 0)),
            far,
        ],
        out_shape=[
            jax.ShapeDtypeStruct((rows, width), BF16),
            jax.ShapeDtypeStruct((pairs * tiles, 1, 2 * QTILE), F32),
            jax.ShapeDtypeStruct(grads.shape, BF16),
        ],
        scratch_shapes=[
            pltpu.VMEM((tiles, span, QTILE), F32),
            pltpu.VMEM(right, BF16),
            pltpu.SemaphoreType.DMA,
            pltpu.SemaphoreType.DMA((Ring.COPIES,)),
            pltpu.SemaphoreType.DMA((Ring.COPIES,)),
            pltpu.SemaphoreType.DMA((8,)),
        ],
        input_output_aliases={5: 2},
        compiler_params=pltpu.CompilerParams(
            collective_id=7, has_side_effects=True, vmem_limit_bytes=56 << 20
        ),
        cost_estimate=pl.CostEstimate(
            flops=16 * rows * span * LANES * pairs,
            bytes_accessed=4 * rows * width + 2 * keys * kv.shape[1],
            transcendentals=2 * rows * span * pairs,
        ),
    )(q, kv, kv, low, grad, grads)


def attend_back_kernel(
    reach, wide, z_size, mlp_count,
    q_ref, do_ref, o_ref, k_ref, v_ref, lse_ref, low_ref, cos_ref, sin_ref, cos_all, sin_all,
    *refs,
):
    mlp_ins, refs = refs[:mlp_count], refs[mlp_count:]
    dq_ref, dkv_ref = refs[:2]
    mlp_outs, refs = refs[2 : 2 + mlp_count], refs[2 + mlp_count :]
    bias_ref, dk_acc, dv_acc, own_part, send_part, recv_part, kv_send, kv_recv = refs[:8]
    home = refs[8:]
    block, half, tile, pair = (pl.program_id(at) for at in range(4))
    steps = pl.num_programs(1) * pl.num_programs(2) * pl.num_programs(3)
    inner = (half * pl.num_programs(2) + tile) * pl.num_programs(3) + pair
    step = block * steps + inner
    blocks = own_part.shape[0]
    rows = own_part.shape[1]
    count = reach // rows
    place = lax.axis_index("tensor")

    def exchange(at, distance):
        return pltpu.make_async_remote_copy(
            src_ref=send_part.at[at, pl.ds((count - distance) * rows, rows)],
            dst_ref=recv_part.at[at, distance - 1],
            send_sem=kv_send.at[at, distance - 1], recv_sem=kv_recv.at[at, distance - 1],
            device_id={"tensor": (place + z_size - distance) % z_size}, device_id_type=MESH,
        )

    def each_exchange(at, condition, action):
        for distance in range(1, count + 1):
            pl.when(condition(distance))(
                functools.partial(action, exchange(at, distance), at, distance)
            )

    @pl.when(step == 0)
    def _():
        greet(along_peers(place, z_size) + [device for _, device in others(wide)[1]])
        for copy in send_home(wide, mlp_ins, mlp_outs, *home):
            copy.start()
        fill_bias(bias_ref, low_ref, reach)

    @pl.when(inner == 0)
    def _():
        dk_acc[...] = jnp.zeros_like(dk_acc)
        dv_acc[...] = jnp.zeros_like(dv_acc)

    keys = pl.ds(pl.multiple_of(tile * QTILE, QTILE), bias_ref.shape[1])
    queries = spread_pair(q_ref[...], half)
    grads = spread_pair(do_ref[...], half)
    product = (do_ref[...].astype(F32) * o_ref[...].astype(F32)).T
    row_dot = jnp.concatenate(
        [
            jnp.sum(product[:64], axis=0, keepdims=True),
            jnp.sum(product[64:], axis=0, keepdims=True),
        ],
        axis=1,
    )
    bias = bias_ref[tile]
    key, value = k_ref[keys, :], v_ref[keys, :]
    score = dot_nt(key, queries) + jnp.concatenate([bias, bias], axis=1)
    weight = jnp.exp2(score * (SCALE * LOG2E) - lse_ref[0])
    dv_acc[keys, :] += dot_nn(weight.astype(BF16), grads)
    dscore = (weight * (dot_nt(value, grads) - row_dot)).astype(BF16)
    dk_acc[keys, :] += dot_nn(dscore, queries)
    dq = gather_pair(dot_tn(key, dscore), half) * SCALE
    dq_ref[...] = (dq * cos_ref[...] - swap_halves(dq) * sin_ref[...]).astype(BF16)

    @pl.when(inner == steps - 1)
    def _():
        send_part[block, :, :LANES] = (dk_acc[:reach] * SCALE).astype(BF16)
        send_part[block, :, LANES:] = dv_acc[:reach].astype(BF16)
        own_part[block, :, :LANES] = dk_acc[reach:] * SCALE
        own_part[block, :, LANES:] = dv_acc[reach:]
        each_exchange(block, lambda distance: place >= distance, lambda copy, *_: copy.start())

    @pl.when(step == blocks * steps - 1)
    def _():
        def collect(copy, at, distance):
            copy.wait_recv()
            own_part[at] += recv_part[at, distance - 1].astype(F32)

        for at in range(blocks):
            each_exchange(at, lambda distance: place + distance < z_size, collect)
            dkey = own_part[at, :, :LANES]
            dkey = dkey * cos_all[...] - swap_halves(dkey) * sin_all[...]
            dkv_ref[:, 2 * at * LANES : (2 * at + 1) * LANES] = dkey.astype(BF16)
            dkv_ref[:, (2 * at + 1) * LANES : (2 * at + 2) * LANES] = own_part[
                at, :, LANES:
            ].astype(BF16)
        for at in range(blocks):
            each_exchange(
                at, lambda distance: place >= distance, lambda copy, *_: copy.wait_send()
            )
        for copy in send_home(wide, mlp_ins, mlp_outs, *home):
            copy.wait()


def attend_back(q, do, att, kv, lse, low, cosine, sine, mlp, dp_size, z_size):
    rows, width = q.shape
    keys = kv.shape[0]
    reach = keys - rows
    tiles = rows // QTILE
    pairs = width // LANES
    heads = kv.shape[1] // LANES
    per_head = pairs // heads
    span = reach + QTILE
    blocks = heads // 2

    def pair_at(g, h, t, p):
        return (t, (2 * g + h) * per_head + p)

    def whole(shape):
        return pl.BlockSpec(shape, lambda g, h, t, p: (0, 0), pipeline_mode=pl.Buffered(1))

    table = pl.BlockSpec((QTILE, LANES), lambda g, h, t, p: (t, 0))
    return pl.pallas_call(
        functools.partial(
            attend_back_kernel, reach, 2 * math.isqrt(dp_size // GROUP), z_size, len(mlp)
        ),
        grid=(blocks, 2, tiles, per_head),
        in_specs=[
            pl.BlockSpec((QTILE, LANES), pair_at),
            pl.BlockSpec((QTILE, LANES), pair_at),
            pl.BlockSpec((QTILE, LANES), pair_at),
            pl.BlockSpec((keys, LANES), lambda g, h, t, p: (0, 2 * g)),
            pl.BlockSpec((keys, LANES), lambda g, h, t, p: (0, 2 * g + 1)),
            pl.BlockSpec(
                (1, 1, 2 * QTILE),
                lambda g, h, t, p: (((2 * g + h) * tiles + t) * per_head + p, 0, 0),
            ),
            whole((1, rows)),
            table,
            table,
            whole((rows, LANES)),
            whole((rows, LANES)),
        ]
        + [pl.BlockSpec(memory_space=pl.ANY)] * len(mlp),
        out_specs=[
            pl.BlockSpec((QTILE, LANES), pair_at),
            pl.BlockSpec((rows, kv.shape[1]), lambda g, h, t, p: (0, 0)),
        ]
        + [pl.BlockSpec(memory_space=pl.ANY)] * len(mlp),
        out_shape=[
            jax.ShapeDtypeStruct((rows, width), BF16),
            jax.ShapeDtypeStruct((rows, kv.shape[1]), BF16),
        ]
        + home_shapes(mlp),
        scratch_shapes=[
            pltpu.VMEM((tiles, span, QTILE), F32),
            pltpu.VMEM((keys, LANES), F32),
            pltpu.VMEM((keys, LANES), F32),
            pltpu.VMEM((blocks, rows, 2 * LANES), F32),
            pltpu.VMEM((blocks, reach, 2 * LANES), BF16),
            pltpu.VMEM((blocks, reach // rows, rows, 2 * LANES), BF16),
            pltpu.SemaphoreType.DMA((blocks, reach // rows)),
            pltpu.SemaphoreType.DMA((blocks, reach // rows)),
        ]
        + home_scratch(mlp),
        compiler_params=pltpu.CompilerParams(
            collective_id=5, has_side_effects=True, vmem_limit_bytes=60 << 20
        ),
        cost_estimate=pl.CostEstimate(
            flops=40 * rows * span * LANES * pairs,
            bytes_accessed=8 * rows * width + 4 * keys * kv.shape[1],
            transcendentals=2 * rows * span * pairs,
        ),
    )(q, do, att, kv, kv, lse, low, cosine, sine, cosine, sine, *mlp)


MESH = pl.DeviceIdType.MESH


def neighbours(wide):
    dp = lax.axis_index("dp")
    core, col, row = dp % 2, (dp // 2) % 2, (dp // (2 * wide)) % 2
    sibling = dp + 1 - 2 * core
    beside = dp + 2 - 4 * col
    above = dp + 2 * wide - 4 * wide * row
    return (row, col, core), (sibling, beside, above)


def meet(peers):
    barrier = pltpu.get_barrier_semaphore()
    for peer in peers:
        pl.semaphore_signal(barrier, inc=1, device_id={"dp": peer}, device_id_type=MESH)
    pl.semaphore_wait(barrier, len(peers))


def others(wide):
    (row, col, core), _ = neighbours(wide)
    base = lax.axis_index("dp") - (2 * wide * row + 2 * col + core)
    found = []
    for flip in range(1, GROUP):
        y, x, c = (row + flip // 4) % 2, (col + flip // 2) % 2, (core + flip) % 2
        found.append((4 * y + 2 * x + c, {"dp": base + 2 * wide * y + 2 * x + c}))
    return 4 * row + 2 * col + core, found


def along_peers(place, z_size):
    return [{"tensor": (place + step) % z_size} for step in range(1, z_size)]


def greet(peers):
    barrier = pltpu.get_barrier_semaphore()
    for peer in peers:
        pl.semaphore_signal(barrier, inc=1, device_id=peer, device_id_type=MESH)
    pl.semaphore_wait(barrier, len(peers))


def send_home(wide, ins, outs, own_sem, send_sem, recv_sem):
    mine, found = others(wide)
    copies = []
    for at, (src, dst) in enumerate(zip(ins, outs)):
        part, cols = dst.shape[0], src.shape[1]
        here = pl.ds(pl.multiple_of(mine * cols, LANES), cols)
        for index, (other, device) in enumerate(found):
            copies.append(
                pltpu.make_async_remote_copy(
                    src_ref=src.at[pl.ds(pl.multiple_of(other * part, part), part)],
                    dst_ref=dst.at[:, here],
                    send_sem=send_sem.at[at, index], recv_sem=recv_sem.at[at, index],
                    device_id=device, device_id_type=MESH,
                )
            )
        own = src.at[pl.ds(pl.multiple_of(mine * part, part), part)]
        copies.append(pltpu.make_async_copy(own, dst.at[:, here], own_sem.at[at]))
    return copies


def home_shapes(arrays):
    return [jax.ShapeDtypeStruct((a.shape[0] // GROUP, GROUP * a.shape[1]), BF16) for a in arrays]


def home_scratch(arrays):
    count = len(arrays)
    return [
        pltpu.SemaphoreType.DMA((count,)),
        pltpu.SemaphoreType.DMA((count, GROUP - 1)),
        pltpu.SemaphoreType.DMA((count, GROUP - 1)),
    ]


SIB, XN, YN = 0, 1, 2


def spread_kernel(wide, z_size, mlp_count, *refs):
    attn_count = (len(refs) - 7) // 2 - mlp_count
    count = mlp_count + attn_count
    ins, outs = refs[:count], refs[count : 2 * count]
    own_sem, send_sem, recv_sem, z_send, z_recv, ring_send, ring_recv = refs[2 * count :]
    first = mlp_count
    ring = Ring(wide, outs[first], ins[first].shape[0], ring_send, ring_recv)
    place = lax.axis_index("tensor")
    mine, found = others(wide)
    greet(along_peers(place, z_size) + [device for _, device in found])

    local, copies = [], []
    for at in range(mlp_count):
        src, dst = ins[at], outs[at]
        rows, cols = src.shape[0], dst.shape[1]
        here = pl.ds(pl.multiple_of(mine * rows, rows), rows)
        for index, (other, device) in enumerate(found):
            copies.append(
                pltpu.make_async_remote_copy(
                    src_ref=src.at[:, pl.ds(pl.multiple_of(other * cols, LANES), cols)],
                    dst_ref=dst.at[here],
                    send_sem=send_sem.at[at, index], recv_sem=recv_sem.at[at, index],
                    device_id=device, device_id_type=MESH,
                )
            )
        own = src.at[:, pl.ds(pl.multiple_of(mine * cols, LANES), cols)]
        local.append(pltpu.make_async_copy(own, dst.at[here], own_sem.at[at]))

    def block(at, origin):
        cols = ins[at].shape[1]
        part = pl.ds(pl.multiple_of(origin * cols, LANES), cols)
        return outs[at].at[ring.mine() if at == first else slice(None), part]

    def hop(at, way, step, receive=False):
        sign = 1 - 2 * way
        origin = place - sign * (step if receive else step - 1)
        slot = 2 * (step - 1) + way
        src = block(at, origin) if receive or step > 1 else ins[at]
        return pltpu.make_async_remote_copy(
            src_ref=src, dst_ref=block(at, origin),
            send_sem=z_send.at[at - mlp_count, slot], recv_sem=z_recv.at[at - mlp_count, slot],
            device_id={"tensor": (place + z_size + sign) % z_size}, device_id_type=MESH,
        )

    def sends(way, step):
        if way == 0:
            return (place + 1 < z_size) & (place >= step - 1)
        return (place >= 1) & (place + step - 1 < z_size)

    def receives(way, step):
        return place >= step if way == 0 else place + step < z_size

    for at in range(mlp_count, count):
        local.append(pltpu.make_async_copy(ins[at], block(at, place), own_sem.at[at]))
        for way in range(2):
            pl.when(sends(way, 1))(lambda: hop(at, way, 1).start())
    for copy in copies + local:
        copy.start()

    def advance(at, step):
        for way in range(2):
            pl.when(receives(way, step))(lambda: hop(at, way, step, True).wait_recv())
            if step + 1 < z_size:
                pl.when(sends(way, step + 1))(lambda: hop(at, way, step + 1).start())

    for step in range(1, z_size):
        advance(first, step)
    local.pop(first).wait()
    ring.start_own()
    stages = [ring.first_halves, ring.second_halves]
    for step in range(1, z_size):
        for at in range(first + 1, count):
            advance(at, step)
        if stages:
            stages.pop(0)()
    for stage in stages:
        stage()
    ring.far_halves()
    for name in ("own", "x", "y", "d"):
        ring.from_sibling(name, 0, 1)
    ring.sent()
    for step in range(1, z_size):
        for at in range(mlp_count, count):
            for way in range(2):
                pl.when(sends(way, step))(lambda: hop(at, way, step).wait_send())
    for copy in local + copies:
        copy.wait()


def spread_weights(mlp, attn, dp_size, z_size):
    count = len(mlp) + len(attn)
    spec = pl.BlockSpec(memory_space=pl.ANY)
    out = [jax.ShapeDtypeStruct((GROUP * w.shape[0], w.shape[1] // GROUP), BF16) for w in mlp]
    out += [
        jax.ShapeDtypeStruct(((1 if at else GROUP) * w.shape[0], z_size * w.shape[1]), BF16)
        for at, w in enumerate(attn)
    ]
    return pl.pallas_call(
        functools.partial(spread_kernel, 2 * math.isqrt(dp_size // GROUP), z_size, len(mlp)),
        in_specs=[spec] * count,
        out_specs=[spec] * count,
        out_shape=out,
        scratch_shapes=[
            pltpu.SemaphoreType.DMA((count,)),
            pltpu.SemaphoreType.DMA((len(mlp), GROUP - 1)),
            pltpu.SemaphoreType.DMA((len(mlp), GROUP - 1)),
            pltpu.SemaphoreType.DMA((len(attn), 2 * (z_size - 1))),
            pltpu.SemaphoreType.DMA((len(attn), 2 * (z_size - 1))),
            pltpu.SemaphoreType.DMA((Ring.COPIES,)),
            pltpu.SemaphoreType.DMA((Ring.COPIES,)),
        ],
        compiler_params=pltpu.CompilerParams(collective_id=2, has_side_effects=True),
        cost_estimate=pl.CostEstimate(flops=LONG, bytes_accessed=0, transcendentals=0),
    )(*mlp, *attn)


class Ring:
    FLIP = {SIB: (0, 0, 1), XN: (0, 1, 0), YN: (1, 0, 0)}
    COPIES = 14

    def __init__(self, wide, ref, rows, send_sem, recv_sem):
        (self.row, self.col, self.core), self.peers = neighbours(wide)
        self.ref, self.rows, self.part = ref, rows, rows // 2
        self.send_sem, self.recv_sem = send_sem, recv_sem
        self.sends = {}
        for half in range(2):
            self.sends["own", XN, half] = (2 + half, 0, 0, 0, half)
            self.sends["own", YN, half] = (4 + half, 0, 0, 0, half)
            self.sends["own", SIB, half] = (0 + half, 0, 0, 0, half)
        for half in range(2):
            self.sends["x", SIB, half] = (6 + half, 0, 1, 0, half)
            self.sends["y", SIB, half] = (8 + half, 1, 0, 0, half)
            self.sends["d", SIB, half] = (10 + half, 1, 1, 0, half)
        self.sends["x", YN, 0] = (12, 0, 1, 0, 0)
        self.sends["y", XN, 1] = (13, 1, 0, 0, 1)

    def place(self, dy, dx, dc, half):
        p = 4 * ((self.row + dy) % 2) + 2 * ((self.col + dx) % 2) + (self.core + dc) % 2
        return pl.ds(pl.multiple_of(p * self.rows + half * self.part, self.part), self.part)

    def mine(self):
        p = 4 * self.row + 2 * self.col + self.core
        return pl.ds(pl.multiple_of(p * self.rows, self.rows), self.rows)

    def whole(self, dy, dx, dc):
        p = 4 * ((self.row + dy) % 2) + 2 * ((self.col + dx) % 2) + (self.core + dc) % 2
        return pl.ds(pl.multiple_of(p * self.rows, self.rows), self.rows)

    def copy(self, slot, dy, dx, dc, half, peer):
        where = self.place(dy, dx, dc, half)
        return pltpu.make_async_remote_copy(
            src_ref=self.ref.at[where], dst_ref=self.ref.at[where],
            send_sem=self.send_sem.at[slot], recv_sem=self.recv_sem.at[slot],
            device_id={"dp": self.peers[peer]}, device_id_type=MESH,
        )

    def start(self, name, peer, half):
        self.copy(*self.sends[name, peer, half], peer).start()

    def arrived(self, name, peer, half):
        slot, dy, dx, dc, half = self.sends[name, peer, half]
        fy, fx, fc = self.FLIP[peer]
        self.copy(slot, (dy + fy) % 2, (dx + fx) % 2, (dc + fc) % 2, half, peer).wait_recv()

    def start_own(self):
        for half in range(2):
            for peer in (XN, YN, SIB):
                self.start("own", peer, half)

    def first_halves(self):
        self.arrived("own", XN, 0)
        self.start("x", YN, 0)
        self.start("x", SIB, 0)
        self.arrived("own", YN, 0)
        self.start("y", SIB, 0)

    def second_halves(self):
        self.arrived("own", YN, 1)
        self.start("y", XN, 1)
        self.start("y", SIB, 1)
        self.arrived("own", XN, 1)
        self.start("x", SIB, 1)

    def far_halves(self):
        self.arrived("x", YN, 0)
        self.start("d", SIB, 0)
        self.arrived("y", XN, 1)
        self.start("d", SIB, 1)

    def from_sibling(self, name, *halves):
        for half in halves:
            self.arrived(name, SIB, half)

    def sent(self):
        for (name, peer, half), entry in self.sends.items():
            self.copy(*entry, peer).wait_send()


def project_kernel(
    wide, z_size, x_ref, cos_ref, sin_ref, wkv_ref, wq_ref, wo_ref, grad_ref,
    q_ref, kv_ref, wq_out, wo_out, grad_out,
    wkv_all, wq_all, wo_all, grad_all, keys, own_sem, send_sem, recv_sem, kv_send, kv_recv, out_sem,
):
    place = lax.axis_index("tensor")
    rows = x_ref.shape[0]
    count = keys.shape[0] // rows - 1
    left = pl.ds(0, grad_all.shape[1])
    parts = (
        (wq_ref, wq_all, wq_out), (wo_ref, wo_all, wo_out),
        (grad_ref.at[:, left], grad_all, grad_out.at[:, left]),
    )
    rings = [
        Ring(wide, full, part.shape[0], send_sem.at[at], recv_sem.at[at])
        for at, (part, full, _) in enumerate(parts)
    ]
    local = [
        pltpu.make_async_copy(part, full.at[ring.mine()], own_sem.at[at])
        for at, ((part, full, _), ring) in enumerate(zip(parts, rings))
    ]
    outward = [
        pltpu.make_async_copy(full, out, out_sem.at[at])
        for at, (_, full, out) in enumerate(parts)
    ]
    load = pltpu.make_async_copy(wkv_ref, wkv_all, own_sem.at[len(parts)])
    for copy in local + [load]:
        copy.start()
    keys[: count * rows, :] = jnp.zeros((count * rows, keys.shape[1]), BF16)
    greet([{"dp": peer} for peer in rings[0].peers] + along_peers(place, z_size))
    for copy in local:
        copy.wait()

    def rotated(value):
        return (value * cos_ref[...] + swap_halves(value) * sin_ref[...]).astype(BF16)

    def hop(step):
        return pltpu.make_async_remote_copy(
            src_ref=keys.at[pl.ds((count - step + 1) * rows, rows)],
            dst_ref=keys.at[pl.ds((count - step) * rows, rows)],
            send_sem=kv_send.at[step - 1], recv_sem=kv_recv.at[step - 1],
            device_id={"tensor": (place + 1) % z_size}, device_id_type=MESH,
        )

    def pass_keys(step):
        if step > 1:
            pl.when(place >= step - 1)(lambda: hop(step - 1).wait_recv())
        if step <= count:
            sends = (place + 1 < z_size) & (place >= step - 1)
            pl.when(sends)(lambda: hop(step).start())

    def finish(ring):
        ring.far_halves()
        for name in ("own", "x", "y", "d"):
            ring.from_sibling(name, 0, 1)

    rings[0].start_own()
    load.wait()

    @pl.loop(0, wkv_all.shape[1] // (2 * LANES))
    def _(at):
        n = pl.ds(pl.multiple_of(at * 2 * LANES, LANES), 2 * LANES)
        value = dot_nn(x_ref[...], wkv_all[:, n])
        both = jnp.concatenate([rotated(value[:, :LANES]), value[:, LANES:].astype(BF16)], axis=1)
        keys[pl.ds(count * rows, rows), n] = both

    pass_keys(1)
    rings[0].first_halves()
    rings[0].second_halves()
    rings[1].start_own()
    finish(rings[0])
    outward[0].start()

    @pl.loop(0, wq_all.shape[1] // (2 * LANES))
    def _(at):
        n = pl.ds(pl.multiple_of(at * 2 * LANES, LANES), 2 * LANES)
        value = dot_nn(x_ref[...], wq_all[:, n])
        both = [rotated(value[:, :LANES]), rotated(value[:, LANES:])]
        q_ref[:, n] = jnp.concatenate(both, axis=1)

    for step in range(2, count + 1):
        pass_keys(step)
    rings[1].first_halves()
    rings[1].second_halves()
    rings[2].start_own()
    finish(rings[1])
    outward[1].start()
    rings[2].first_halves()
    rings[2].second_halves()
    finish(rings[2])
    outward[2].start()
    pass_keys(count + 1)
    keys_out = pltpu.make_async_copy(keys, kv_ref, out_sem.at[3])
    keys_out.start()
    for step in range(1, count + 1):
        sends = (place + 1 < z_size) & (place >= step - 1)
        pl.when(sends)(lambda: hop(step).wait_send())
    for ring in rings:
        ring.sent()
    for copy in outward + [keys_out]:
        copy.wait()


def project(x, cosine, sine, wkv, wq, wo, grad, reach, dp_size, z_size):
    rows, width = x.shape
    far = pl.BlockSpec(memory_space=pl.ANY)
    near = pl.BlockSpec(memory_space=pltpu.VMEM)
    whole = [(GROUP * w.shape[0], w.shape[1]) for w in (wq, wo)]
    keys = (reach + rows, wkv.shape[1])
    grads = (GROUP * grad.shape[0], grad.shape[1])
    left = (grads[0], grads[1] * 3 // 8)
    return pl.pallas_call(
        functools.partial(project_kernel, 2 * math.isqrt(dp_size // GROUP), z_size),
        in_specs=[near] * 3 + [far] * 4,
        out_specs=[near] + [far] * 4,
        out_shape=[jax.ShapeDtypeStruct((rows, wq.shape[1]), BF16)]
        + [jax.ShapeDtypeStruct(shape, BF16) for shape in [keys] + whole + [grads]],
        scratch_shapes=[pltpu.VMEM(shape, BF16) for shape in [wkv.shape] + whole + [left, keys]]
        + [
            pltpu.SemaphoreType.DMA((4,)),
            pltpu.SemaphoreType.DMA((3, Ring.COPIES)),
            pltpu.SemaphoreType.DMA((3, Ring.COPIES)),
            pltpu.SemaphoreType.DMA((reach // rows,)),
            pltpu.SemaphoreType.DMA((reach // rows,)),
            pltpu.SemaphoreType.DMA((4,)),
        ],
        compiler_params=pltpu.CompilerParams(
            collective_id=3, has_side_effects=True, vmem_limit_bytes=56 << 20
        ),
        cost_estimate=pl.CostEstimate(
            flops=2 * LONG, bytes_accessed=0, transcendentals=0
        ),
    )(x, cosine, sine, wkv, wq, wo, grad)


def gate_up_kernel(
    wide, own_ref, wg_ref, wu_ref, all_ref, gate_ref, up_ref, hid_ref, core_ref,
    full, stage, wg_all, wu_all, own_sem, load_sem, send_sem, recv_sem, out_sem, all_sem,
):
    rows = own_ref.shape[0]
    cols = gate_ref.shape[1]
    ring = Ring(wide, full, rows, send_sem, recv_sem)
    local = pltpu.make_async_copy(own_ref, full.at[ring.mine()], own_sem)
    local.start()
    loads = [
        pltpu.make_async_copy(wg_ref, wg_all, load_sem.at[0]),
        pltpu.make_async_copy(wu_ref, wu_all, load_sem.at[1]),
    ]
    for copy in loads:
        copy.start()
    meet(ring.peers)
    local.wait()
    ring.start_own()
    for copy in loads:
        copy.wait()

    def out_copies(slot, places):
        where, core, chip = places
        return [
            pltpu.make_async_copy(stage.at[slot, i], ref.at[where], out_sem.at[slot, i])
            for i, ref in enumerate((gate_ref, up_ref, hid_ref))
        ] + [
            pltpu.make_async_copy(stage.at[slot, 2], core_ref.at[core, chip], out_sem.at[slot, 3]),
            pltpu.make_async_copy(full.at[where], all_ref.at[where], all_sem.at[slot]),
        ]

    def step_place(step):
        phase, i = step // 4, step % 4
        high, low = phase // 2, phase % 2
        first, last = (1 - high) * (1 - low), high * low
        middle = high + low - 2 * last
        half = (first + last) * (i % 2) + high * (1 - low)
        dx = middle * (1 - i % 2) + last
        dy = middle * (i % 2) + last
        part = rows // 2
        chip_rows = pl.ds(pl.multiple_of((2 * dy + dx) * rows + half * part, part), part)
        return ring.place(dy, dx, i // 2, half), i // 2, chip_rows

    @pl.loop(0, 16)
    def _(step):
        pl.when(step == 2)(lambda: ring.from_sibling("own", 0, 1))
        pl.when(step == 4)(ring.first_halves)

        @pl.when(step == 6)
        def _():
            ring.from_sibling("x", 0)
            ring.from_sibling("y", 0)

        pl.when(step == 8)(ring.second_halves)

        @pl.when(step == 10)
        def _():
            ring.from_sibling("x", 1)
            ring.from_sibling("y", 1)

        pl.when(step == 12)(ring.far_halves)
        pl.when(step == 14)(lambda: ring.from_sibling("d", 0, 1))

        slot = step % 2
        places = step_place(step)

        @pl.when(step >= 2)
        def _():
            for copy in out_copies(slot, step_place(step - 2)):
                copy.wait()

        x = full[places[0], :]

        @pl.loop(0, cols // NTILE)
        def _(at):
            n = pl.ds(pl.multiple_of(at * NTILE, NTILE), NTILE)
            gate = dot_nn(x, wg_all[:, n])
            up = dot_nn(x, wu_all[:, n])
            stage[slot, 0, :, n] = gate.astype(BF16)
            stage[slot, 1, :, n] = up.astype(BF16)
            stage[slot, 2, :, n] = (gate * up / (1.0 + jnp.exp(-gate))).astype(BF16)

        for copy in out_copies(slot, places):
            copy.start()

    for step in (14, 15):
        for copy in out_copies(step % 2, step_place(step)):
            copy.wait()
    ring.sent()


def gate_up(hn, wg, wu, dp_size):
    rows, width = hn.shape
    cols = wg.shape[1]
    tokens = GROUP * rows
    far = pl.BlockSpec(memory_space=pl.ANY)
    return pl.pallas_call(
        functools.partial(gate_up_kernel, 2 * math.isqrt(dp_size // GROUP)),
        in_specs=[far] * 3,
        out_specs=[far] * 5,
        out_shape=[jax.ShapeDtypeStruct((tokens, width), BF16)]
        + [jax.ShapeDtypeStruct((tokens, cols), BF16)] * 3
        + [jax.ShapeDtypeStruct((2, tokens // 2, cols), BF16)],
        scratch_shapes=[
            pltpu.VMEM((tokens, width), BF16),
            pltpu.VMEM((2, 3, rows // 2, cols), BF16),
            pltpu.VMEM(wg.shape, BF16),
            pltpu.VMEM(wu.shape, BF16),
            pltpu.SemaphoreType.DMA,
            pltpu.SemaphoreType.DMA((2,)),
            pltpu.SemaphoreType.DMA((Ring.COPIES,)),
            pltpu.SemaphoreType.DMA((Ring.COPIES,)),
            pltpu.SemaphoreType.DMA((2, 4)),
            pltpu.SemaphoreType.DMA((2,)),
        ],
        compiler_params=pltpu.CompilerParams(
            collective_id=1, has_side_effects=True, vmem_limit_bytes=56 << 20
        ),
        cost_estimate=pl.CostEstimate(
            flops=SHORT, bytes_accessed=0, transcendentals=0
        ),
    )(hn, wg, wu)


FAR_CHUNK, X_CHUNK, Y_CHUNK, OWN_CHUNK = range(4)


class Reduce:
    COPIES = 10

    def __init__(self, wide, parts, cores, far, near, send_sem, recv_sem):
        self.at, self.peers = neighbours(wide)
        self.parts, self.cores, self.far, self.near = parts, cores, far, near
        self.send_sem, self.recv_sem = send_sem, recv_sem
        self.half = parts.shape[2] // 2

    @staticmethod
    def scratch(rows, cols):
        return [
            pltpu.VMEM((2, 4, rows, cols), BF16),
            pltpu.VMEM((4, rows, cols), BF16),
            pltpu.VMEM((2, rows // 2, cols), BF16),
            pltpu.VMEM((2, rows, cols), BF16),
            pltpu.SemaphoreType.DMA((Reduce.COPIES,)),
            pltpu.SemaphoreType.DMA((Reduce.COPIES,)),
        ]

    def chunk(self, step):
        slot, other = step // 2, 1 - step % 2
        row, col, core = self.at
        dy, dx = 1 - slot % 2, 1 - slot // 2
        place = 4 * ((row + dy) % 2) + 2 * ((col + dx) % 2) + (core + other) % 2
        return place, self.parts.at[other, slot]

    def copy(self, name):
        upper, lower = pl.ds(0, self.half), pl.ds(self.half, self.half)
        mine = self.parts.at[0]
        table = {
            "far0": (self.parts.at[1, FAR_CHUNK], self.cores.at[FAR_CHUNK], SIB),
            "x": (self.parts.at[1, X_CHUNK], self.cores.at[X_CHUNK], SIB),
            "y": (self.parts.at[1, Y_CHUNK], self.cores.at[Y_CHUNK], SIB),
            "own": (self.parts.at[1, OWN_CHUNK], self.cores.at[OWN_CHUNK], SIB),
            "far_x": (mine.at[FAR_CHUNK, lower], self.far.at[0], XN),
            "far_y": (mine.at[FAR_CHUNK, upper], self.far.at[1], YN),
            "x_upper": (mine.at[X_CHUNK, upper], self.near.at[0, upper], XN),
            "x_lower": (mine.at[X_CHUNK, lower], self.near.at[0, lower], XN),
            "y_upper": (mine.at[Y_CHUNK, upper], self.near.at[1, upper], YN),
            "y_lower": (mine.at[Y_CHUNK, lower], self.near.at[1, lower], YN),
        }
        src, dst, peer = table[name]
        at = list(table).index(name)
        return pltpu.make_async_remote_copy(
            src_ref=src, dst_ref=dst, send_sem=self.send_sem.at[at],
            recv_sem=self.recv_sem.at[at], device_id={"dp": self.peers[peer]},
            device_id_type=MESH,
        )

    def start(self, *names):
        for name in names:
            self.copy(name).start()

    def add(self, slot, start, other):
        count = other.shape[0] // STRIP

        @pl.loop(0, count)
        def _(at):
            here = pl.ds(pl.multiple_of(start + at * STRIP, STRIP), STRIP)
            there = pl.ds(pl.multiple_of(at * STRIP, STRIP), STRIP)
            value = self.parts[0, slot, here, :].astype(F32) + other[there, :].astype(F32)
            self.parts[0, slot, here, :] = value.astype(BF16)

    def merge_core(self, slot, name):
        self.copy(name).wait_recv()
        self.add(slot, 0, self.cores.at[slot])

    def after(self, step):
        names = ("far0", "x", "y", "own")
        for slot in range(4):
            pl.when(step == 2 * slot)(functools.partial(self.start, names[slot]))

        @pl.when(step == 1)
        def _():
            self.merge_core(FAR_CHUNK, "far0")
            self.start("far_x", "far_y")

        @pl.when(step == 3)
        def _():
            self.merge_core(X_CHUNK, "x")
            self.start("x_lower")

        @pl.when(step == 5)
        def _():
            self.merge_core(Y_CHUNK, "y")
            self.start("y_upper")

    def pass_on(self):
        self.copy("far_y").wait_recv()
        self.add(X_CHUNK, 0, self.far.at[1])
        self.start("x_upper")
        self.copy("far_x").wait_recv()
        self.add(Y_CHUNK, self.half, self.far.at[0])
        self.start("y_lower")

    def finish(self, store):
        for name in ("own", "x_upper", "x_lower", "y_upper", "y_lower"):
            self.copy(name).wait_recv()

        @pl.loop(0, 2 * self.half // STRIP)
        def _(at):
            here = pl.ds(pl.multiple_of(at * STRIP, STRIP), STRIP)
            value = self.parts[0, OWN_CHUNK, here, :].astype(F32)
            value += self.cores[OWN_CHUNK, here, :].astype(F32)
            value += self.near[0, here, :].astype(F32)
            value += self.near[1, here, :].astype(F32)
            store(here, value)

    def sent(self):
        for name in (
            "far0", "x", "y", "own", "far_x", "far_y", "x_upper", "x_lower", "y_upper", "y_lower",
        ):
            self.copy(name).wait_send()


def hidden_back_kernel(
    wide, gain_ref, h_ref, grad_ref, dgate_ref, dup_ref, wg_ref, wu_ref,
    dh_ref, low_ref, gain_out,
    loaded, wg_all, wu_all, h_all, grad_all, load_sem, own_sem, *scratch,
):
    ring = Reduce(wide, *scratch)
    rows = dh_ref.shape[0]

    def loads(step):
        chunk, _ = ring.chunk(step)
        here = pl.ds(pl.multiple_of(chunk * rows, rows), rows)
        return [
            pltpu.make_async_copy(
                ref.at[here], loaded.at[step % 2, at], load_sem.at[step % 2, at]
            )
            for at, ref in enumerate((dgate_ref, dup_ref))
        ]

    pairs = ((wg_ref, wg_all), (wu_ref, wu_all), (h_ref, h_all), (grad_ref, grad_all))
    whole = [
        pltpu.make_async_copy(src, dst, own_sem.at[at]) for at, (src, dst) in enumerate(pairs)
    ]
    for copy in loads(0) + whole:
        copy.start()
    meet(ring.peers)
    for copy in whole[:2]:
        copy.wait()

    @pl.loop(0, 8)
    def _(step):
        @pl.when(step < 7)
        def _():
            for copy in loads(step + 1):
                copy.start()

        for copy in loads(step):
            copy.wait()
        _, target = ring.chunk(step)
        dgate, dup = loaded[step % 2, 0], loaded[step % 2, 1]

        @pl.loop(0, dh_ref.shape[1] // NTILE)
        def _(at):
            n = pl.ds(pl.multiple_of(at * NTILE, NTILE), NTILE)
            value = dot_nt(dgate, wg_all[n, :]) + dot_nt(dup, wu_all[n, :])
            target[:, n] = value.astype(BF16)

        ring.after(step)

    ring.pass_on()
    for copy in whole[2:]:
        copy.wait()
    gain_out[...] = jnp.zeros_like(gain_out)

    def store(here, value):
        h = h_all[here, :]
        scale = rms_scale(h)
        gained = value * gain_ref[...]
        inner = jnp.mean(gained * h, axis=1, keepdims=True)
        gain_out[...] += value * h * scale
        total = grad_all[here, :].astype(F32) + scale * gained
        total -= h * (scale * scale * scale * inner)
        dh_ref[here, :] = total
        low_ref[here, :] = total.astype(BF16)

    ring.finish(store)
    ring.sent()


def hidden_back(gain, h, grad, dgate, dup, wg, wu, dp_size):
    tokens, cols = dgate.shape
    rows, width = h.shape
    far = pl.BlockSpec(memory_space=pl.ANY)
    near = pl.BlockSpec(memory_space=pltpu.VMEM)
    return pl.pallas_call(
        functools.partial(hidden_back_kernel, 2 * math.isqrt(dp_size // GROUP)),
        in_specs=[near] + [far] * 6,
        out_specs=[near] * 3,
        out_shape=[
            jax.ShapeDtypeStruct((rows, width), F32),
            jax.ShapeDtypeStruct((rows, width), BF16),
            jax.ShapeDtypeStruct((STRIP, width), F32),
        ],
        scratch_shapes=[
            pltpu.VMEM((2, 2, rows, cols), BF16),
            pltpu.VMEM(wg.shape, BF16),
            pltpu.VMEM(wu.shape, BF16),
            pltpu.VMEM(h.shape, F32),
            pltpu.VMEM(grad.shape, BF16),
            pltpu.SemaphoreType.DMA((2, 2)),
            pltpu.SemaphoreType.DMA((4,)),
        ]
        + Reduce.scratch(rows, width),
        compiler_params=pltpu.CompilerParams(
            collective_id=6, has_side_effects=True, vmem_limit_bytes=62 << 20
        ),
        cost_estimate=pl.CostEstimate(
            flops=2 * LONG, bytes_accessed=4 * rows * width, transcendentals=0
        ),
    )(gain, h, grad, dgate, dup, wg, wu)


def tail_kernel(
    wide, z_size, x_ref, dq_ref, dkv_ref, wo_ref, gain_ref,
    raw_ref, dh_ref, wq_ref, wkv_ref, *refs
):
    wq_out, wkv_out, wo_out, gain_out, grad_out = refs[:5]
    scratch = refs[5:]
    sub = wkv_out.shape[1]
    halves = wq_out.shape[1] // sub
    count = halves + 1
    rings = [Reduce(wide, *scratch[6 * at : 6 * at + 6]) for at in range(count)]
    sums, zrecv, gain_z, gain_p, z_send, z_recv, g_send, g_recv = scratch[6 * count : 6 * count + 8]
    wo_recv, w_send, w_recv = scratch[6 * count + 8 : 6 * count + 11]
    wq_all, wkv_all, raw, dh, dxn, gain_sum, load_sem = scratch[6 * count + 11 :]
    place = lax.axis_index("tensor")
    mine, found = others(wide)
    along = along_peers(place, z_size)
    around = [device for _, device in found]

    tiles, tile_rows = raw.shape[0], raw.shape[1]
    loads = [
        pltpu.make_async_copy(wq_ref, wq_all, load_sem.at[0]),
        pltpu.make_async_copy(wkv_ref, wkv_all, load_sem.at[1]),
    ]
    for tile in range(tiles):
        here = pl.ds(tile * tile_rows, tile_rows)
        loads += [
            pltpu.make_async_copy(raw_ref.at[here], raw.at[tile], load_sem.at[2 + 2 * tile]),
            pltpu.make_async_copy(dh_ref.at[here], dh.at[tile], load_sem.at[3 + 2 * tile]),
        ]
    for copy in loads:
        copy.start()
    greet(along + around)

    wo_part = wo_out.shape[1]
    wo_copies = [
        pltpu.make_async_remote_copy(
            src_ref=wo_ref.at[
                :,
                pl.ds(pl.multiple_of((place + at + 1) % z_size * wo_part, LANES), wo_part),
            ],
            dst_ref=wo_recv.at[at], send_sem=w_send.at[at], recv_sem=w_recv.at[at],
            device_id=peer, device_id_type=MESH,
        )
        for at, peer in enumerate(along)
    ]
    for copy in wo_copies:
        copy.start()

    pieces = [(dq_ref, wq_out, at * sub) for at in range(halves)] + [(dkv_ref, wkv_out, 0)]
    rows = sums.shape[1]
    z_copies = []

    def partial_sums(index):
        ring = rings[index]
        right, out, offset = pieces[index]

        @pl.loop(0, 8)
        def _(step):
            chunk, target = ring.chunk(step)
            x = x_ref[:, pl.ds(pl.multiple_of(chunk * rows, rows), rows)].T

            @pl.loop(0, z_size)
            def _(at):
                n = pl.ds(pl.multiple_of(at * sub, LANES), sub)
                source = pl.ds(pl.multiple_of(at * out.shape[1] + offset, LANES), sub)
                target[:, n] = dot_nn(x, right[:, source]).astype(BF16)

            ring.after(step)

    gain_sum[...] = jnp.zeros_like(gain_sum)

    def input_rows(tile):
        part = pl.ds(tile * tile_rows, tile_rows)
        dq, dkv = dq_ref[part, :], dkv_ref[part, :]

        @pl.loop(0, dxn.shape[1] // NTILE)
        def _(at):
            n = pl.ds(pl.multiple_of(at * NTILE, NTILE), NTILE)
            dxn[:, n] = dot_nt(dq, wq_all[n, :]) + dot_nt(dkv, wkv_all[n, :])

        @pl.loop(0, tile_rows // STRIP)
        def _(at):
            here = pl.ds(pl.multiple_of(at * STRIP, STRIP), STRIP)
            there = pl.ds(pl.multiple_of(tile * tile_rows + at * STRIP, STRIP), STRIP)
            grad, value = dxn[here, :], raw[tile, here, :].astype(F32)
            scale = rms_scale(value)
            gained = grad * gain_ref[0:1, :]
            inner = jnp.mean(gained * value, axis=1, keepdims=True)
            gain_sum[...] += grad * value * scale
            total = scale * gained - value * (scale * scale * scale * inner)
            grad_out[there, :] = (dh[tile, here, :] + total).astype(BF16)

    def send_along(index):
        def store(here, value):
            sums[index, here, :] = value.astype(BF16)

        rings[index].finish(store)
        for at, peer in enumerate(along):
            other = (place + at + 1) % z_size
            copy = pltpu.make_async_remote_copy(
                src_ref=sums.at[index, :, pl.ds(pl.multiple_of(other * sub, LANES), sub)],
                dst_ref=zrecv.at[index, at],
                send_sem=z_send.at[index, at], recv_sem=z_recv.at[index, at],
                device_id=peer, device_id_type=MESH,
            )
            z_copies.append(copy)
            copy.start()

    partial_sums(0)
    for copy in loads:
        copy.wait()
    input_rows(0)
    rings[0].pass_on()
    for index in range(1, count):
        partial_sums(index)
        if index < tiles:
            input_rows(index)
        if index + 1 < count:
            rings[index].pass_on()
            send_along(index - 1)
    for tile in range(count, tiles):
        input_rows(tile)

    gain_z[place, 0:1] = jnp.sum(gain_sum[...], axis=0, keepdims=True)
    gain_z[place, 1:2] = gain_ref[1:2, :]
    gain_copies = [
        pltpu.make_async_remote_copy(
            src_ref=gain_z.at[place], dst_ref=gain_z.at[place], send_sem=g_send.at[at],
            recv_sem=g_recv.at[at], device_id=peer, device_id_type=MESH,
        )
        for at, peer in enumerate(along)
    ]
    for copy in gain_copies:
        copy.start()
    rings[count - 1].pass_on()
    send_along(count - 2)

    for copy in gain_copies:
        copy.wait_recv()
    total = gain_z[0]
    for at in range(1, z_size):
        total = total + gain_z[at]
    gain_p[mine] = total
    for at, peer in enumerate(around):
        copy = pltpu.make_async_remote_copy(
            src_ref=gain_p.at[mine], dst_ref=gain_p.at[mine],
            send_sem=g_send.at[z_size - 1 + at], recv_sem=g_recv.at[z_size - 1 + at],
            device_id=peer, device_id_type=MESH,
        )
        gain_copies.append(copy)
        copy.start()
    for copy in wo_copies:
        copy.wait()
    total = wo_ref[:, pl.ds(pl.multiple_of(place * wo_part, LANES), wo_part)].astype(F32)
    for at in range(z_size - 1):
        total += wo_recv[at].astype(F32)
    wo_out[...] = total
    send_along(count - 1)

    for copy in gain_copies[z_size - 1 :]:
        copy.wait_recv()
    total = gain_p[0]
    for at in range(1, GROUP):
        total = total + gain_p[at]
    gain_out[...] = total
    for copy in z_copies:
        copy.wait_recv()
    for index, (_, out, offset) in enumerate(pieces):
        value = sums[index, :, pl.ds(pl.multiple_of(place * sub, LANES), sub)].astype(F32)
        for at in range(z_size - 1):
            value += zrecv[index, at].astype(F32)
        out[:, offset : offset + sub] = value
    for copy in z_copies + gain_copies:
        copy.wait_send()
    for ring in rings:
        ring.sent()


def last_grads(x, dq, dkv, wo_sum, gains, raw, dh, wq, wkv, dp_size, z_size):
    tokens, width = x.shape
    rows = width // GROUP
    tiles = tokens // QTILE
    near = pl.BlockSpec(memory_space=pltpu.VMEM)
    far = pl.BlockSpec(memory_space=pl.ANY)
    sizes = [dq.shape[1], dkv.shape[1]]
    cols = dkv.shape[1]
    count = sum(sizes) // cols
    scratch = []
    for _ in range(count):
        scratch += Reduce.scratch(rows, cols)
    return pl.pallas_call(
        functools.partial(tail_kernel, 2 * math.isqrt(dp_size // GROUP), z_size),
        in_specs=[near] * 5 + [far] * 4,
        out_specs=[near] * 5,
        out_shape=[jax.ShapeDtypeStruct((rows, size // z_size), F32) for size in sizes]
        + [
            jax.ShapeDtypeStruct((rows, wo_sum.shape[1] // z_size), F32),
            jax.ShapeDtypeStruct(gains.shape, F32),
            jax.ShapeDtypeStruct((tokens, width), BF16),
        ],
        scratch_shapes=scratch
        + [
            pltpu.VMEM((count, rows, cols), BF16),
            pltpu.VMEM((count, z_size - 1, rows, cols // z_size), BF16),
            pltpu.VMEM((z_size, *gains.shape), F32),
            pltpu.VMEM((GROUP, *gains.shape), F32),
            pltpu.SemaphoreType.DMA((count, z_size - 1)),
            pltpu.SemaphoreType.DMA((count, z_size - 1)),
            pltpu.SemaphoreType.DMA((z_size - 1 + GROUP - 1,)),
            pltpu.SemaphoreType.DMA((z_size - 1 + GROUP - 1,)),
            pltpu.VMEM((z_size - 1, rows, wo_sum.shape[1] // z_size), BF16),
            pltpu.SemaphoreType.DMA((z_size - 1,)),
            pltpu.SemaphoreType.DMA((z_size - 1,)),
            pltpu.VMEM(wq.shape, BF16),
            pltpu.VMEM(wkv.shape, BF16),
            pltpu.VMEM((tiles, QTILE, width), BF16),
            pltpu.VMEM((tiles, QTILE, width), F32),
            pltpu.VMEM((QTILE, width), F32),
            pltpu.VMEM((STRIP, width), F32),
            pltpu.SemaphoreType.DMA((2 + 2 * tiles,)),
        ],
        compiler_params=pltpu.CompilerParams(
            collective_id=4, has_side_effects=True, vmem_limit_bytes=62 << 20
        ),
        cost_estimate=pl.CostEstimate(flops=SHORT, bytes_accessed=0, transcendentals=0),
    )(x, dq, dkv, wo_sum, gains, raw, dh, wq, wkv)


class Layout:
    def __init__(self, dp_size):
        self.blocks = dp_size // GROUP
        side = math.isqrt(self.blocks)
        self.rows, self.cols = side, self.blocks // side
        wide = 2 * self.cols

        def index(by, bx, y, x, core):
            return ((2 * by + y) * wide + 2 * bx + x) * 2 + core

        places = [(y, x, c) for y in range(2) for x in range(2) for c in range(2)]
        spots = [(by, bx) for by in range(self.rows) for bx in range(self.cols)]
        self.inner = [[index(*s, *p) for p in places] for s in spots]
        self.outer = [[index(*s, *p) for s in spots] for p in places]

    def groups(self):
        return None if self.blocks == 1 else self.inner

    def to_rows(self, array):
        if self.blocks == 1:
            return array
        rest = array.shape[1:]
        split = array.reshape(2, 2, 2, self.rows, self.cols, -1, *rest)
        order = (3, 0, 4, 1, 2, 5) + tuple(range(6, 6 + len(rest)))
        return split.transpose(order).reshape(array.shape)

    def from_rows(self, array):
        if self.blocks == 1:
            return array
        rest = array.shape[1:]
        split = array.reshape(self.rows, 2, self.cols, 2, 2, -1, *rest)
        order = (1, 3, 4, 0, 2, 5) + tuple(range(6, 6 + len(rest)))
        return split.transpose(order).reshape(array.shape)

    def from_cols(self, array):
        return array if self.blocks == 1 else self.from_rows(array.T).T

    def gather_outer(self, array):
        if self.blocks == 1:
            return array
        return lax.all_gather(array, "dp", axis_index_groups=self.outer, axis=0, tiled=True)

    def scatter_outer(self, array):
        if self.blocks == 1:
            return array
        return lax.psum_scatter(
            array, "dp", scatter_dimension=0, axis_index_groups=self.outer, tiled=True
        )

    def swap(self, array, flip):
        pairs = [
            (block[at], block[at ^ flip]) for block in self.inner for at in range(GROUP)
        ]
        return lax.ppermute(array, "dp", pairs)

    def sum_outer(self, array):
        if self.blocks == 1:
            return array
        return lax.psum(array, "dp", axis_index_groups=self.outer)

    def gather(self, array):
        return lax.all_gather(array, "dp", axis_index_groups=self.groups(), axis=0, tiled=True)

    def scatter(self, array):
        return lax.psum_scatter(
            array, "dp", scatter_dimension=0, axis_index_groups=self.groups(), tiled=True
        )


def rms_scale(values):
    return lax.rsqrt(jnp.mean(values * values, axis=-1, keepdims=True) + NORM_EPS)


def per_device(
    dp_size, z_size, activations, segment_ids, attn_gain, w_query, w_key, w_value, w_out,
    mlp_gain, w_gate, w_up, w_down, cotangent,
):
    layout = Layout(dp_size)
    rows, width = activations.shape[1:]
    x = activations[0].astype(F32)
    place = lax.axis_index("tensor")
    reach = -(-(MOST_DOC - 1) // rows) * rows

    def shift(array, step):
        pairs = [(at, at + step) for at in range(z_size) if 0 <= at + step < z_size]
        return lax.ppermute(array, "tensor", pairs)

    starts = document_starts(segment_ids[0])
    own_starts = lax.dynamic_slice_in_dim(starts, place * rows, rows)
    own_tokens = place * rows + jnp.arange(rows, dtype=jnp.int32)
    cosine, sine = rope_tables(own_tokens - own_starts)
    low = (own_starts - place * rows + reach)[None, :]

    shards = [
        layout.gather_outer(w)
        for w in (w_gate, w_up, w_down, jnp.concatenate([w_key, w_value], axis=1), w_query, w_out)
    ]
    spread = spread_weights(shards[:3], shards[3:], dp_size, z_size)
    def gather_z(array):
        return layout.to_rows(lax.all_gather(array, "tensor", axis=1, tiled=True))

    wg, wu = gather_z(spread[0]), gather_z(spread[1])

    def along_z(total):
        return lax.psum_scatter(
            layout.from_rows(total), "tensor", scatter_dimension=1, tiled=True
        )

    r1 = rms_scale(x)
    xn = (x * r1 * attn_gain).astype(BF16)
    q, kv_all, wq, wo, dy = project(
        layout.from_cols(xn), cosine, sine, *spread[3:], cotangent[0], reach, dp_size, z_size
    )
    wd = gather_z(spread[2])
    wkv, wq, wo = (layout.to_rows(w) for w in (spread[3], wq, wo))
    att, lse, dy = attend(q, kv_all, low, cotangent[0], dy, dp_size)
    h = x + dot_nt(att, wo)

    r2 = rms_scale(h)
    hn, gate, up, hidden, by_core = gate_up((h * r2 * mlp_gain).astype(BF16), wg, wu, dp_size)
    part = rows // 2
    away = dot_nt(by_core[1], wd).astype(BF16)
    dy, away = lax.optimization_barrier((dy, away))
    total_wd = dot_tn(dy, hidden).astype(BF16)
    part_wd = along_z(total_wd)
    from_core = layout.swap(away, 1)

    def out_rows(start, count, *more):
        some = slice(start * part, (start + count) * part)
        total = dot_nt(by_core[0, some], wd) + from_core[some].astype(F32)
        for other in more:
            total = total + other.astype(F32)
        return total.astype(BF16)

    far_y, far_x, x_lower, y_upper = (out_rows(at, 1) for at in (6, 7, 3, 4))
    dy, far_x, far_y, x_lower, y_upper = lax.optimization_barrier(
        (dy, far_x, far_y, x_lower, y_upper)
    )
    from_x, from_y = layout.swap(far_x, 2), layout.swap(far_y, 4)
    x_lower, y_upper = layout.swap(x_lower, 2), layout.swap(y_upper, 4)
    gate, up = gate.astype(F32), up.astype(F32)
    sigma = jax.nn.sigmoid(gate)
    dhid = dot_nn(dy, wd)
    dgate = (dhid * up * sigma * (1.0 + gate * (1.0 - sigma))).astype(BF16)
    dup = (dhid * gate * sigma).astype(BF16)
    dgate, dup, from_x, from_y = lax.optimization_barrier((dgate, dup, from_x, from_y))
    x_upper, y_lower = out_rows(2, 1, from_y), out_rows(5, 1, from_x)
    dgate, dup, x_upper, y_lower = lax.optimization_barrier((dgate, dup, x_upper, y_lower))
    x_upper, y_lower = layout.swap(x_upper, 2), layout.swap(y_lower, 4)
    total_wg = dot_tn(hn, dgate).astype(BF16)
    dup, total_wg, x_lower, y_upper = lax.optimization_barrier((dup, total_wg, x_lower, y_upper))
    part_wg = along_z(total_wg)
    total_wu = dot_tn(hn, dup).astype(BF16)
    dup, total_wu = lax.optimization_barrier((dup, total_wu))
    part_wu = along_z(total_wu)
    dup, x_upper, y_lower = lax.optimization_barrier((dup, x_upper, y_lower))
    dh, dhb, gain_two = hidden_back(
        mlp_gain[None], h, cotangent[0], dgate, dup, wg, wu, dp_size
    )
    gain_two = jnp.sum(gain_two, axis=0)
    dhb, part_wd = lax.optimization_barrier((dhb, part_wd))
    datt = dot_nn(dhb, wo).astype(BF16)
    total_wo = layout.from_rows(dot_tn(dhb, att).astype(BF16))
    datt, part_wg, total_wo = lax.optimization_barrier((datt, part_wg, total_wo))
    datt, part_wu = lax.optimization_barrier((datt, part_wu))
    part_wo = layout.scatter(total_wo)
    dq, dkv, wd_grad, wg_grad, wu_grad = attend_back(
        q, datt, att, kv_all, lse, low, cosine, sine, (part_wd, part_wg, part_wu), dp_size, z_size
    )
    dq, part_wo = lax.optimization_barrier((dq, part_wo))
    wq_grad, wkv_grad, wo_grad, gains, input_grad = last_grads(
        layout.from_cols(xn), dq, dkv, part_wo, jnp.stack([attn_gain, gain_two]),
        activations[0], dh, wq, wkv, dp_size, z_size,
    )
    gains = layout.sum_outer(gains)
    output = h + out_rows(0, 2).astype(F32)
    output = output + jnp.concatenate([x_upper, x_lower]).astype(F32)
    output = output + jnp.concatenate([y_upper, y_lower]).astype(F32)
    wo_grad, wq_grad, wkv_grad, wd_grad, wg_grad, wu_grad = (
        layout.scatter_outer(grad).astype(F32)
        for grad in (wo_grad, wq_grad, wkv_grad, wd_grad, wg_grad, wu_grad)
    )
    key_cols = w_key.shape[1]
    return (
        output.astype(BF16)[None],
        input_grad[None],
        gains[0],
        wq_grad,
        wkv_grad[:, :key_cols],
        wkv_grad[:, key_cols:],
        wo_grad,
        gains[1],
        wg_grad,
        wu_grad,
        wd_grad,
    )


def solution(mesh):
    split = P("dp", "tensor")
    tokens = P("dp", "tensor", None)
    in_specs = (
        tokens, P("dp", None), P(), split, split, split, split, P(), split, split, split, tokens,
    )
    out_specs = (tokens, tokens, P(), split, split, split, split, P(), split, split, split)
    return jax.shard_map(
        functools.partial(per_device, mesh.shape["dp"], mesh.shape["tensor"]),
        mesh=mesh, in_specs=in_specs, out_specs=out_specs, check_vma=False,
    )
```

```python
import functools
import math

import jax
import jax.numpy as jnp
from jax import lax
from jax.experimental import pallas as pl
from jax.experimental.pallas import tpu as pltpu
from jax.sharding import PartitionSpec as P

HEAD_DIM = 64
DOCS = 4
MOST_DOC = 1024
NORM_EPS = 1e-05
ROPE_THETA = 500000.0
GROUP = 8
LANES = 128
QTILE = 256
SCALE = HEAD_DIM ** (-0.5)
LOG2E = 1.4426950408889634
FAR = -1e30
NTILE = 512
STRIP = 16
LONG = 60_000_000_000
SHORT = 1_000_000

F32 = jnp.float32
BF16 = jnp.bfloat16


def dot_nn(left, right):
    return lax.dot_general(left, right, (((1,), (0,)), ((), ())), preferred_element_type=F32)


def dot_nt(left, right):
    return lax.dot_general(left, right, (((1,), (1,)), ((), ())), preferred_element_type=F32)


def dot_tn(left, right):
    return lax.dot_general(left, right, (((0,), (0,)), ((), ())), preferred_element_type=F32)


def document_starts(segments):
    doc_ids = jnp.arange(DOCS, dtype=jnp.int32)
    counts = jnp.sum((segments[:, None] == doc_ids).astype(jnp.int32), axis=0)
    before = (doc_ids < segments[:, None]).astype(jnp.int32)
    return jnp.sum(before * counts[None, :], axis=-1)


def rope_tables(positions):
    half = HEAD_DIM // 2
    frequency = jnp.exp(
        jnp.arange(half, dtype=F32) * (-2.0 * math.log(ROPE_THETA) / HEAD_DIM)
    )
    angles = positions.astype(F32)[:, None] * frequency
    cosine, sine = jnp.cos(angles), jnp.sin(angles)
    wide_cos = jnp.concatenate([cosine] * 4, axis=1)
    wide_sin = jnp.concatenate([-sine, sine, -sine, sine], axis=1)
    return wide_cos, wide_sin


def swap_halves(values):
    lane = lax.broadcasted_iota(jnp.int32, values.shape, 1)
    ahead = pltpu.roll(values, LANES - 32, 1)
    behind = pltpu.roll(values, 32, 1)
    return jnp.where((lane % 64) < 32, ahead, behind)


def fill_bias(bias_ref, low_ref, reach):
    span = bias_ref.shape[1]
    for tile in range(bias_ref.shape[0]):
        row = lax.broadcasted_iota(jnp.int32, (span, QTILE), 0)
        col = lax.broadcasted_iota(jnp.int32, (span, QTILE), 1)
        low = low_ref[0:1, tile * QTILE : (tile + 1) * QTILE]
        allowed = (row <= reach + col) & (row + tile * QTILE >= low)
        bias_ref[tile] = jnp.where(allowed, 0.0, FAR)


def spread_pair(pair, half):
    wide = pair.astype(F32)
    turned = pltpu.roll(wide, 64, 1)
    lane = lax.broadcasted_iota(jnp.int32, wide.shape, 1)
    mine = (lane // 64) == half
    even = half == 0
    first = jnp.where(mine, jnp.where(even, wide, turned), 0.0)
    second = jnp.where(mine, jnp.where(even, turned, wide), 0.0)
    return jnp.concatenate([first, second], axis=0).astype(BF16)


def gather_pair(transposed, half):
    count = transposed.shape[1] // 2
    mine = jnp.where(half == 0, transposed[:64], transposed[64:])
    return jnp.concatenate([mine[:, :count], mine[:, count:]], axis=0).T


def attend_kernel(
    reach, wide, q_ref, k_ref, v_ref, low_ref, own_ref, _, att_ref, lse_ref, all_ref,
    bias_ref, full, own_sem, send_sem, recv_sem, out_sem,
):
    head, tile, pair = pl.program_id(0), pl.program_id(1), pl.program_id(2)
    half = head % 2
    inner = pl.num_programs(1) * pl.num_programs(2)
    step = head * inner + tile * pl.num_programs(2) + pair
    ring = Ring(wide, full, own_ref.shape[0], send_sem, recv_sem)
    right = pl.ds(own_ref.shape[1] - full.shape[1], full.shape[1])

    def outward(slot, *flips):
        where = ring.whole(*flips)
        return pltpu.make_async_copy(full.at[where], all_ref.at[where, right], out_sem.at[slot])

    near = [(0, 0, 0), (0, 0, 1), (0, 1, 0), (1, 0, 0)]
    rest = [(0, 1, 1), (1, 0, 1), (1, 1, 0), (1, 1, 1)]

    @pl.when(step == 0)
    def _():
        local = pltpu.make_async_copy(own_ref.at[:, right], full.at[ring.mine()], own_sem)
        local.start()
        meet(ring.peers)
        local.wait()
        ring.start_own()
        fill_bias(bias_ref, low_ref, reach)

    pl.when(step == 2 * inner)(ring.first_halves)
    pl.when(step == 4 * inner)(ring.second_halves)

    keys = pl.ds(pl.multiple_of(tile * QTILE, QTILE), bias_ref.shape[1])
    queries = spread_pair(q_ref[...], half)
    bias = bias_ref[tile]
    score = dot_nt(k_ref[keys, :], queries)
    score = score + jnp.concatenate([bias, bias], axis=1)
    top = jnp.max(score, axis=0, keepdims=True) * (SCALE * LOG2E)
    weight = jnp.exp2(score * (SCALE * LOG2E) - top)
    total = jnp.sum(weight, axis=0, keepdims=True)
    result = dot_tn(v_ref[keys, :], weight.astype(BF16)) / total
    att_ref[...] = gather_pair(result, half).astype(BF16)
    lse_ref[0] = top + jnp.log2(total)

    @pl.when(step == pl.num_programs(0) * inner - 1)
    def _():
        ring.from_sibling("own", 0, 1)
        for slot, flips in enumerate(near):
            outward(slot, *flips).start()
        ring.far_halves()
        for name in ("x", "y", "d"):
            ring.from_sibling(name, 0, 1)
        for slot, flips in enumerate(rest):
            outward(4 + slot, *flips).start()
        for slot, flips in enumerate(near + rest):
            outward(slot, *flips).wait()
        ring.sent()


def attend(q, kv, low, grad, grads, dp_size):
    rows, width = q.shape
    keys = kv.shape[0]
    reach = keys - rows
    tiles = rows // QTILE
    pairs = width // LANES
    heads = kv.shape[1] // LANES
    per_head = pairs // heads
    span = reach + QTILE
    right = (grads.shape[0], grads.shape[1] * 5 // 8)
    far = pl.BlockSpec(memory_space=pl.ANY)
    return pl.pallas_call(
        functools.partial(attend_kernel, reach, 2 * math.isqrt(dp_size // GROUP)),
        grid=(heads, tiles, per_head),
        in_specs=[
            pl.BlockSpec((QTILE, LANES), lambda a, t, p: (t, a * per_head + p)),
            pl.BlockSpec((keys, LANES), lambda a, t, p: (0, 2 * (a // 2))),
            pl.BlockSpec((keys, LANES), lambda a, t, p: (0, 2 * (a // 2) + 1)),
            pl.BlockSpec((1, rows), lambda a, t, p: (0, 0)),
            far,
            far,
        ],
        out_specs=[
            pl.BlockSpec((QTILE, LANES), lambda a, t, p: (t, a * per_head + p)),
            pl.BlockSpec((1, 1, 2 * QTILE), lambda a, t, p: ((a * tiles + t) * per_head + p, 0, 0)),
            far,
        ],
        out_shape=[
            jax.ShapeDtypeStruct((rows, width), BF16),
            jax.ShapeDtypeStruct((pairs * tiles, 1, 2 * QTILE), F32),
            jax.ShapeDtypeStruct(grads.shape, BF16),
        ],
        scratch_shapes=[
            pltpu.VMEM((tiles, span, QTILE), F32),
            pltpu.VMEM(right, BF16),
            pltpu.SemaphoreType.DMA,
            pltpu.SemaphoreType.DMA((Ring.COPIES,)),
            pltpu.SemaphoreType.DMA((Ring.COPIES,)),
            pltpu.SemaphoreType.DMA((8,)),
        ],
        input_output_aliases={5: 2},
        compiler_params=pltpu.CompilerParams(
            collective_id=7, has_side_effects=True, vmem_limit_bytes=56 << 20
        ),
        cost_estimate=pl.CostEstimate(
            flops=16 * rows * span * LANES * pairs,
            bytes_accessed=4 * rows * width + 2 * keys * kv.shape[1],
            transcendentals=2 * rows * span * pairs,
        ),
    )(q, kv, kv, low, grad, grads)


def attend_back_kernel(
    reach, wide, z_size, mlp_count,
    q_ref, do_ref, o_ref, k_ref, v_ref, lse_ref, low_ref, cos_ref, sin_ref, cos_all, sin_all,
    *refs,
):
    mlp_ins, refs = refs[:mlp_count], refs[mlp_count:]
    dq_ref, dkv_ref = refs[:2]
    mlp_outs, refs = refs[2 : 2 + mlp_count], refs[2 + mlp_count :]
    bias_ref, dk_acc, dv_acc, own_part, send_part, recv_part, kv_send, kv_recv = refs[:8]
    home = refs[8:]
    block, half, tile, pair = (pl.program_id(at) for at in range(4))
    steps = pl.num_programs(1) * pl.num_programs(2) * pl.num_programs(3)
    inner = (half * pl.num_programs(2) + tile) * pl.num_programs(3) + pair
    step = block * steps + inner
    blocks = own_part.shape[0]
    rows = own_part.shape[1]
    count = reach // rows
    place = lax.axis_index("tensor")

    def exchange(at, distance):
        return pltpu.make_async_remote_copy(
            src_ref=send_part.at[at, pl.ds((count - distance) * rows, rows)],
            dst_ref=recv_part.at[at, distance - 1],
            send_sem=kv_send.at[at, distance - 1], recv_sem=kv_recv.at[at, distance - 1],
            device_id={"tensor": (place + z_size - distance) % z_size}, device_id_type=MESH,
        )

    def each_exchange(at, condition, action):
        for distance in range(1, count + 1):
            pl.when(condition(distance))(
                functools.partial(action, exchange(at, distance), at, distance)
            )

    @pl.when(step == 0)
    def _():
        greet(along_peers(place, z_size) + [device for _, device in others(wide)[1]])
        for copy in send_home(wide, mlp_ins, mlp_outs, *home):
            copy.start()
        fill_bias(bias_ref, low_ref, reach)

    @pl.when(inner == 0)
    def _():
        dk_acc[...] = jnp.zeros_like(dk_acc)
        dv_acc[...] = jnp.zeros_like(dv_acc)

    keys = pl.ds(pl.multiple_of(tile * QTILE, QTILE), bias_ref.shape[1])
    queries = spread_pair(q_ref[...], half)
    grads = spread_pair(do_ref[...], half)
    product = (do_ref[...].astype(F32) * o_ref[...].astype(F32)).T
    row_dot = jnp.concatenate(
        [
            jnp.sum(product[:64], axis=0, keepdims=True),
            jnp.sum(product[64:], axis=0, keepdims=True),
        ],
        axis=1,
    )
    bias = bias_ref[tile]
    key, value = k_ref[keys, :], v_ref[keys, :]
    score = dot_nt(key, queries) + jnp.concatenate([bias, bias], axis=1)
    weight = jnp.exp2(score * (SCALE * LOG2E) - lse_ref[0])
    dv_acc[keys, :] += dot_nn(weight.astype(BF16), grads)
    dscore = (weight * (dot_nt(value, grads) - row_dot)).astype(BF16)
    dk_acc[keys, :] += dot_nn(dscore, queries)
    dq = gather_pair(dot_tn(key, dscore), half) * SCALE
    dq_ref[...] = (dq * cos_ref[...] - swap_halves(dq) * sin_ref[...]).astype(BF16)

    @pl.when(inner == steps - 1)
    def _():
        send_part[block, :, :LANES] = (dk_acc[:reach] * SCALE).astype(BF16)
        send_part[block, :, LANES:] = dv_acc[:reach].astype(BF16)
        own_part[block, :, :LANES] = dk_acc[reach:] * SCALE
        own_part[block, :, LANES:] = dv_acc[reach:]
        each_exchange(block, lambda distance: place >= distance, lambda copy, *_: copy.start())

    @pl.when(step == blocks * steps - 1)
    def _():
        def collect(copy, at, distance):
            copy.wait_recv()
            own_part[at] += recv_part[at, distance - 1].astype(F32)

        for at in range(blocks):
            each_exchange(at, lambda distance: place + distance < z_size, collect)
            dkey = own_part[at, :, :LANES]
            dkey = dkey * cos_all[...] - swap_halves(dkey) * sin_all[...]
            dkv_ref[:, 2 * at * LANES : (2 * at + 1) * LANES] = dkey.astype(BF16)
            dkv_ref[:, (2 * at + 1) * LANES : (2 * at + 2) * LANES] = own_part[
                at, :, LANES:
            ].astype(BF16)
        for at in range(blocks):
            each_exchange(
                at, lambda distance: place >= distance, lambda copy, *_: copy.wait_send()
            )
        for copy in send_home(wide, mlp_ins, mlp_outs, *home):
            copy.wait()


def attend_back(q, do, att, kv, lse, low, cosine, sine, mlp, dp_size, z_size):
    rows, width = q.shape
    keys = kv.shape[0]
    reach = keys - rows
    tiles = rows // QTILE
    pairs = width // LANES
    heads = kv.shape[1] // LANES
    per_head = pairs // heads
    span = reach + QTILE
    blocks = heads // 2

    def pair_at(g, h, t, p):
        return (t, (2 * g + h) * per_head + p)

    def whole(shape):
        return pl.BlockSpec(shape, lambda g, h, t, p: (0, 0), pipeline_mode=pl.Buffered(1))

    table = pl.BlockSpec((QTILE, LANES), lambda g, h, t, p: (t, 0))
    return pl.pallas_call(
        functools.partial(
            attend_back_kernel, reach, 2 * math.isqrt(dp_size // GROUP), z_size, len(mlp)
        ),
        grid=(blocks, 2, tiles, per_head),
        in_specs=[
            pl.BlockSpec((QTILE, LANES), pair_at),
            pl.BlockSpec((QTILE, LANES), pair_at),
            pl.BlockSpec((QTILE, LANES), pair_at),
            pl.BlockSpec((keys, LANES), lambda g, h, t, p: (0, 2 * g)),
            pl.BlockSpec((keys, LANES), lambda g, h, t, p: (0, 2 * g + 1)),
            pl.BlockSpec(
                (1, 1, 2 * QTILE),
                lambda g, h, t, p: (((2 * g + h) * tiles + t) * per_head + p, 0, 0),
            ),
            whole((1, rows)),
            table,
            table,
            whole((rows, LANES)),
            whole((rows, LANES)),
        ]
        + [pl.BlockSpec(memory_space=pl.ANY)] * len(mlp),
        out_specs=[
            pl.BlockSpec((QTILE, LANES), pair_at),
            pl.BlockSpec((rows, kv.shape[1]), lambda g, h, t, p: (0, 0)),
        ]
        + [pl.BlockSpec(memory_space=pl.ANY)] * len(mlp),
        out_shape=[
            jax.ShapeDtypeStruct((rows, width), BF16),
            jax.ShapeDtypeStruct((rows, kv.shape[1]), BF16),
        ]
        + home_shapes(mlp),
        scratch_shapes=[
            pltpu.VMEM((tiles, span, QTILE), F32),
            pltpu.VMEM((keys, LANES), F32),
            pltpu.VMEM((keys, LANES), F32),
            pltpu.VMEM((blocks, rows, 2 * LANES), F32),
            pltpu.VMEM((blocks, reach, 2 * LANES), BF16),
            pltpu.VMEM((blocks, reach // rows, rows, 2 * LANES), BF16),
            pltpu.SemaphoreType.DMA((blocks, reach // rows)),
            pltpu.SemaphoreType.DMA((blocks, reach // rows)),
        ]
        + home_scratch(mlp),
        compiler_params=pltpu.CompilerParams(
            collective_id=5, has_side_effects=True, vmem_limit_bytes=60 << 20
        ),
        cost_estimate=pl.CostEstimate(
            flops=40 * rows * span * LANES * pairs,
            bytes_accessed=8 * rows * width + 4 * keys * kv.shape[1],
            transcendentals=2 * rows * span * pairs,
        ),
    )(q, do, att, kv, kv, lse, low, cosine, sine, cosine, sine, *mlp)


MESH = pl.DeviceIdType.MESH


def neighbours(wide):
    dp = lax.axis_index("dp")
    core, col, row = dp % 2, (dp // 2) % 2, (dp // (2 * wide)) % 2
    sibling = dp + 1 - 2 * core
    beside = dp + 2 - 4 * col
    above = dp + 2 * wide - 4 * wide * row
    return (row, col, core), (sibling, beside, above)


def meet(peers):
    barrier = pltpu.get_barrier_semaphore()
    for peer in peers:
        pl.semaphore_signal(barrier, inc=1, device_id={"dp": peer}, device_id_type=MESH)
    pl.semaphore_wait(barrier, len(peers))


def others(wide):
    (row, col, core), _ = neighbours(wide)
    base = lax.axis_index("dp") - (2 * wide * row + 2 * col + core)
    found = []
    for flip in range(1, GROUP):
        y, x, c = (row + flip // 4) % 2, (col + flip // 2) % 2, (core + flip) % 2
        found.append((4 * y + 2 * x + c, {"dp": base + 2 * wide * y + 2 * x + c}))
    return 4 * row + 2 * col + core, found


def along_peers(place, z_size):
    return [{"tensor": (place + step) % z_size} for step in range(1, z_size)]


def greet(peers):
    barrier = pltpu.get_barrier_semaphore()
    for peer in peers:
        pl.semaphore_signal(barrier, inc=1, device_id=peer, device_id_type=MESH)
    pl.semaphore_wait(barrier, len(peers))


def send_home(wide, ins, outs, own_sem, send_sem, recv_sem):
    mine, found = others(wide)
    copies = []
    for at, (src, dst) in enumerate(zip(ins, outs)):
        part, cols = dst.shape[0], src.shape[1]
        here = pl.ds(pl.multiple_of(mine * cols, LANES), cols)
        for index, (other, device) in enumerate(found):
            copies.append(
                pltpu.make_async_remote_copy(
                    src_ref=src.at[pl.ds(pl.multiple_of(other * part, part), part)],
                    dst_ref=dst.at[:, here],
                    send_sem=send_sem.at[at, index], recv_sem=recv_sem.at[at, index],
                    device_id=device, device_id_type=MESH,
                )
            )
        own = src.at[pl.ds(pl.multiple_of(mine * part, part), part)]
        copies.append(pltpu.make_async_copy(own, dst.at[:, here], own_sem.at[at]))
    return copies


def home_shapes(arrays):
    return [jax.ShapeDtypeStruct((a.shape[0] // GROUP, GROUP * a.shape[1]), BF16) for a in arrays]


def home_scratch(arrays):
    count = len(arrays)
    return [
        pltpu.SemaphoreType.DMA((count,)),
        pltpu.SemaphoreType.DMA((count, GROUP - 1)),
        pltpu.SemaphoreType.DMA((count, GROUP - 1)),
    ]


SIB, XN, YN = 0, 1, 2


def spread_kernel(wide, z_size, mlp_count, x_ref, gain_ref, *refs):
    attn_count = (len(refs) - 8) // 2 - mlp_count
    count = mlp_count + attn_count
    ins, xn_ref, outs = refs[:count], refs[count], refs[count + 1 : 2 * count + 1]
    own_sem, send_sem, recv_sem, z_send, z_recv, ring_send, ring_recv = refs[2 * count + 1 :]
    first = mlp_count
    ring = Ring(wide, outs[first], ins[first].shape[0], ring_send, ring_recv)
    place = lax.axis_index("tensor")
    mine, found = others(wide)
    greet(along_peers(place, z_size) + [device for _, device in found])

    local, copies = [], []
    for at in range(mlp_count):
        src, dst = ins[at], outs[at]
        rows, cols = src.shape[0], dst.shape[1]
        here = pl.ds(pl.multiple_of(mine * rows, rows), rows)
        for index, (other, device) in enumerate(found):
            copies.append(
                pltpu.make_async_remote_copy(
                    src_ref=src.at[:, pl.ds(pl.multiple_of(other * cols, LANES), cols)],
                    dst_ref=dst.at[here],
                    send_sem=send_sem.at[at, index], recv_sem=recv_sem.at[at, index],
                    device_id=device, device_id_type=MESH,
                )
            )
        own = src.at[:, pl.ds(pl.multiple_of(mine * cols, LANES), cols)]
        local.append(pltpu.make_async_copy(own, dst.at[here], own_sem.at[at]))

    def block(at, origin):
        cols = ins[at].shape[1]
        part = pl.ds(pl.multiple_of(origin * cols, LANES), cols)
        return outs[at].at[ring.mine() if at == first else slice(None), part]

    def hop(at, way, step, receive=False):
        sign = 1 - 2 * way
        origin = place - sign * (step if receive else step - 1)
        slot = 2 * (step - 1) + way
        src = block(at, origin) if receive or step > 1 else ins[at]
        return pltpu.make_async_remote_copy(
            src_ref=src, dst_ref=block(at, origin),
            send_sem=z_send.at[at - mlp_count, slot], recv_sem=z_recv.at[at - mlp_count, slot],
            device_id={"tensor": (place + z_size + sign) % z_size}, device_id_type=MESH,
        )

    def sends(way, step):
        if way == 0:
            return (place + 1 < z_size) & (place >= step - 1)
        return (place >= 1) & (place + step - 1 < z_size)

    def receives(way, step):
        return place >= step if way == 0 else place + step < z_size

    for at in range(mlp_count, count):
        local.append(pltpu.make_async_copy(ins[at], block(at, place), own_sem.at[at]))
        for way in range(2):
            pl.when(sends(way, 1))(lambda: hop(at, way, 1).start())
    for copy in copies + local:
        copy.start()

    @pl.loop(0, x_ref.shape[0] // STRIP)
    def _(at):
        here = pl.ds(pl.multiple_of(at * STRIP, STRIP), STRIP)
        value = x_ref[here, :].astype(F32)
        xn_ref[here, :] = (value * rms_scale(value) * gain_ref[...]).astype(BF16)

    def advance(at, step):
        for way in range(2):
            pl.when(receives(way, step))(lambda: hop(at, way, step, True).wait_recv())
            if step + 1 < z_size:
                pl.when(sends(way, step + 1))(lambda: hop(at, way, step + 1).start())

    for step in range(1, z_size):
        advance(first, step)
    local.pop(first).wait()
    ring.start_own()
    stages = [ring.first_halves, ring.second_halves]
    for step in range(1, z_size):
        for at in range(first + 1, count):
            advance(at, step)
        if stages:
            stages.pop(0)()
    for stage in stages:
        stage()
    ring.far_halves()
    for name in ("own", "x", "y", "d"):
        ring.from_sibling(name, 0, 1)
    ring.sent()
    for step in range(1, z_size):
        for at in range(mlp_count, count):
            for way in range(2):
                pl.when(sends(way, step))(lambda: hop(at, way, step).wait_send())
    for copy in local + copies:
        copy.wait()


def spread_weights(x, gain, mlp, attn, dp_size, z_size):
    count = len(mlp) + len(attn)
    spec = pl.BlockSpec(memory_space=pl.ANY)
    near = pl.BlockSpec(memory_space=pltpu.VMEM)
    out = [jax.ShapeDtypeStruct(x.shape, BF16)]
    out += [jax.ShapeDtypeStruct((GROUP * w.shape[0], w.shape[1] // GROUP), BF16) for w in mlp]
    out += [
        jax.ShapeDtypeStruct(((1 if at else GROUP) * w.shape[0], z_size * w.shape[1]), BF16)
        for at, w in enumerate(attn)
    ]
    return pl.pallas_call(
        functools.partial(spread_kernel, 2 * math.isqrt(dp_size // GROUP), z_size, len(mlp)),
        in_specs=[near] * 2 + [spec] * count,
        out_specs=[near] + [spec] * count,
        out_shape=out,
        scratch_shapes=[
            pltpu.SemaphoreType.DMA((count,)),
            pltpu.SemaphoreType.DMA((len(mlp), GROUP - 1)),
            pltpu.SemaphoreType.DMA((len(mlp), GROUP - 1)),
            pltpu.SemaphoreType.DMA((len(attn), 2 * (z_size - 1))),
            pltpu.SemaphoreType.DMA((len(attn), 2 * (z_size - 1))),
            pltpu.SemaphoreType.DMA((Ring.COPIES,)),
            pltpu.SemaphoreType.DMA((Ring.COPIES,)),
        ],
        compiler_params=pltpu.CompilerParams(collective_id=2, has_side_effects=True),
        cost_estimate=pl.CostEstimate(flops=LONG, bytes_accessed=0, transcendentals=0),
    )(x, gain, *mlp, *attn)


class Ring:
    FLIP = {SIB: (0, 0, 1), XN: (0, 1, 0), YN: (1, 0, 0)}
    COPIES = 14

    def __init__(self, wide, ref, rows, send_sem, recv_sem):
        (self.row, self.col, self.core), self.peers = neighbours(wide)
        self.ref, self.rows, self.part = ref, rows, rows // 2
        self.send_sem, self.recv_sem = send_sem, recv_sem
        self.sends = {}
        for half in range(2):
            self.sends["own", XN, half] = (2 + half, 0, 0, 0, half)
            self.sends["own", YN, half] = (4 + half, 0, 0, 0, half)
            self.sends["own", SIB, half] = (0 + half, 0, 0, 0, half)
        for half in range(2):
            self.sends["x", SIB, half] = (6 + half, 0, 1, 0, half)
            self.sends["y", SIB, half] = (8 + half, 1, 0, 0, half)
            self.sends["d", SIB, half] = (10 + half, 1, 1, 0, half)
        self.sends["x", YN, 0] = (12, 0, 1, 0, 0)
        self.sends["y", XN, 1] = (13, 1, 0, 0, 1)

    def place(self, dy, dx, dc, half):
        p = 4 * ((self.row + dy) % 2) + 2 * ((self.col + dx) % 2) + (self.core + dc) % 2
        return pl.ds(pl.multiple_of(p * self.rows + half * self.part, self.part), self.part)

    def mine(self):
        p = 4 * self.row + 2 * self.col + self.core
        return pl.ds(pl.multiple_of(p * self.rows, self.rows), self.rows)

    def whole(self, dy, dx, dc):
        p = 4 * ((self.row + dy) % 2) + 2 * ((self.col + dx) % 2) + (self.core + dc) % 2
        return pl.ds(pl.multiple_of(p * self.rows, self.rows), self.rows)

    def copy(self, slot, dy, dx, dc, half, peer):
        where = self.place(dy, dx, dc, half)
        return pltpu.make_async_remote_copy(
            src_ref=self.ref.at[where], dst_ref=self.ref.at[where],
            send_sem=self.send_sem.at[slot], recv_sem=self.recv_sem.at[slot],
            device_id={"dp": self.peers[peer]}, device_id_type=MESH,
        )

    def start(self, name, peer, half):
        self.copy(*self.sends[name, peer, half], peer).start()

    def arrived(self, name, peer, half):
        slot, dy, dx, dc, half = self.sends[name, peer, half]
        fy, fx, fc = self.FLIP[peer]
        self.copy(slot, (dy + fy) % 2, (dx + fx) % 2, (dc + fc) % 2, half, peer).wait_recv()

    def start_own(self):
        for half in range(2):
            for peer in (XN, YN, SIB):
                self.start("own", peer, half)

    def first_halves(self):
        self.arrived("own", XN, 0)
        self.start("x", YN, 0)
        self.start("x", SIB, 0)
        self.arrived("own", YN, 0)
        self.start("y", SIB, 0)

    def second_halves(self):
        self.arrived("own", YN, 1)
        self.start("y", XN, 1)
        self.start("y", SIB, 1)
        self.arrived("own", XN, 1)
        self.start("x", SIB, 1)

    def far_halves(self):
        self.arrived("x", YN, 0)
        self.start("d", SIB, 0)
        self.arrived("y", XN, 1)
        self.start("d", SIB, 1)

    def from_sibling(self, name, *halves):
        for half in halves:
            self.arrived(name, SIB, half)

    def sent(self):
        for (name, peer, half), entry in self.sends.items():
            self.copy(*entry, peer).wait_send()


def project_kernel(
    wide, z_size, x_ref, cos_ref, sin_ref, wkv_ref, wq_ref, wo_ref, grad_ref,
    q_ref, kv_ref, wq_out, wo_out, grad_out,
    wkv_all, wq_all, wo_all, grad_all, keys, own_sem, send_sem, recv_sem, kv_send, kv_recv, out_sem,
):
    place = lax.axis_index("tensor")
    rows = x_ref.shape[0]
    count = keys.shape[0] // rows - 1
    left = pl.ds(0, grad_all.shape[1])
    parts = (
        (wq_ref, wq_all, wq_out), (wo_ref, wo_all, wo_out),
        (grad_ref.at[:, left], grad_all, grad_out.at[:, left]),
    )
    rings = [
        Ring(wide, full, part.shape[0], send_sem.at[at], recv_sem.at[at])
        for at, (part, full, _) in enumerate(parts)
    ]
    local = [
        pltpu.make_async_copy(part, full.at[ring.mine()], own_sem.at[at])
        for at, ((part, full, _), ring) in enumerate(zip(parts, rings))
    ]
    outward = [
        pltpu.make_async_copy(full, out, out_sem.at[at])
        for at, (_, full, out) in enumerate(parts)
    ]
    load = pltpu.make_async_copy(wkv_ref, wkv_all, own_sem.at[len(parts)])
    for copy in local + [load]:
        copy.start()
    keys[: count * rows, :] = jnp.zeros((count * rows, keys.shape[1]), BF16)
    greet([{"dp": peer} for peer in rings[0].peers] + along_peers(place, z_size))
    for copy in local:
        copy.wait()

    def rotated(value):
        return (value * cos_ref[...] + swap_halves(value) * sin_ref[...]).astype(BF16)

    def hop(step):
        return pltpu.make_async_remote_copy(
            src_ref=keys.at[pl.ds((count - step + 1) * rows, rows)],
            dst_ref=keys.at[pl.ds((count - step) * rows, rows)],
            send_sem=kv_send.at[step - 1], recv_sem=kv_recv.at[step - 1],
            device_id={"tensor": (place + 1) % z_size}, device_id_type=MESH,
        )

    def pass_keys(step):
        if step > 1:
            pl.when(place >= step - 1)(lambda: hop(step - 1).wait_recv())
        if step <= count:
            sends = (place + 1 < z_size) & (place >= step - 1)
            pl.when(sends)(lambda: hop(step).start())

    def finish(ring):
        ring.far_halves()
        for name in ("own", "x", "y", "d"):
            ring.from_sibling(name, 0, 1)

    rings[0].start_own()
    load.wait()

    @pl.loop(0, wkv_all.shape[1] // (2 * LANES))
    def _(at):
        n = pl.ds(pl.multiple_of(at * 2 * LANES, LANES), 2 * LANES)
        value = dot_nn(x_ref[...], wkv_all[:, n])
        both = jnp.concatenate([rotated(value[:, :LANES]), value[:, LANES:].astype(BF16)], axis=1)
        keys[pl.ds(count * rows, rows), n] = both

    pass_keys(1)
    rings[0].first_halves()
    rings[0].second_halves()
    rings[1].start_own()
    finish(rings[0])
    outward[0].start()

    @pl.loop(0, wq_all.shape[1] // (2 * LANES))
    def _(at):
        n = pl.ds(pl.multiple_of(at * 2 * LANES, LANES), 2 * LANES)
        value = dot_nn(x_ref[...], wq_all[:, n])
        both = [rotated(value[:, :LANES]), rotated(value[:, LANES:])]
        q_ref[:, n] = jnp.concatenate(both, axis=1)

    for step in range(2, count + 1):
        pass_keys(step)
    rings[1].first_halves()
    rings[1].second_halves()
    rings[2].start_own()
    finish(rings[1])
    outward[1].start()
    rings[2].first_halves()
    rings[2].second_halves()
    finish(rings[2])
    outward[2].start()
    pass_keys(count + 1)
    keys_out = pltpu.make_async_copy(keys, kv_ref, out_sem.at[3])
    keys_out.start()
    for step in range(1, count + 1):
        sends = (place + 1 < z_size) & (place >= step - 1)
        pl.when(sends)(lambda: hop(step).wait_send())
    for ring in rings:
        ring.sent()
    for copy in outward + [keys_out]:
        copy.wait()


def project(x, cosine, sine, wkv, wq, wo, grad, reach, dp_size, z_size):
    rows, width = x.shape
    far = pl.BlockSpec(memory_space=pl.ANY)
    near = pl.BlockSpec(memory_space=pltpu.VMEM)
    whole = [(GROUP * w.shape[0], w.shape[1]) for w in (wq, wo)]
    keys = (reach + rows, wkv.shape[1])
    grads = (GROUP * grad.shape[0], grad.shape[1])
    left = (grads[0], grads[1] * 3 // 8)
    return pl.pallas_call(
        functools.partial(project_kernel, 2 * math.isqrt(dp_size // GROUP), z_size),
        in_specs=[near] * 3 + [far] * 4,
        out_specs=[near] + [far] * 4,
        out_shape=[jax.ShapeDtypeStruct((rows, wq.shape[1]), BF16)]
        + [jax.ShapeDtypeStruct(shape, BF16) for shape in [keys] + whole + [grads]],
        scratch_shapes=[pltpu.VMEM(shape, BF16) for shape in [wkv.shape] + whole + [left, keys]]
        + [
            pltpu.SemaphoreType.DMA((4,)),
            pltpu.SemaphoreType.DMA((3, Ring.COPIES)),
            pltpu.SemaphoreType.DMA((3, Ring.COPIES)),
            pltpu.SemaphoreType.DMA((reach // rows,)),
            pltpu.SemaphoreType.DMA((reach // rows,)),
            pltpu.SemaphoreType.DMA((4,)),
        ],
        compiler_params=pltpu.CompilerParams(
            collective_id=3, has_side_effects=True, vmem_limit_bytes=56 << 20
        ),
        cost_estimate=pl.CostEstimate(
            flops=2 * LONG, bytes_accessed=0, transcendentals=0
        ),
    )(x, cosine, sine, wkv, wq, wo, grad)


def gate_up_kernel(
    wide, own_ref, wg_ref, wu_ref, all_ref, gate_ref, up_ref, hid_ref, core_ref,
    full, stage, wg_all, wu_all, own_sem, load_sem, send_sem, recv_sem, out_sem, all_sem,
):
    rows = own_ref.shape[0]
    cols = gate_ref.shape[1]
    ring = Ring(wide, full, rows, send_sem, recv_sem)
    local = pltpu.make_async_copy(own_ref, full.at[ring.mine()], own_sem)
    local.start()
    loads = [
        pltpu.make_async_copy(wg_ref, wg_all, load_sem.at[0]),
        pltpu.make_async_copy(wu_ref, wu_all, load_sem.at[1]),
    ]
    for copy in loads:
        copy.start()
    meet(ring.peers)
    local.wait()
    ring.start_own()
    for copy in loads:
        copy.wait()

    def out_copies(slot, places):
        where, core, chip = places
        return [
            pltpu.make_async_copy(stage.at[slot, i], ref.at[where], out_sem.at[slot, i])
            for i, ref in enumerate((gate_ref, up_ref, hid_ref))
        ] + [
            pltpu.make_async_copy(stage.at[slot, 2], core_ref.at[core, chip], out_sem.at[slot, 3]),
            pltpu.make_async_copy(full.at[where], all_ref.at[where], all_sem.at[slot]),
        ]

    def step_place(step):
        phase, i = step // 4, step % 4
        high, low = phase // 2, phase % 2
        first, last = (1 - high) * (1 - low), high * low
        middle = high + low - 2 * last
        half = (first + last) * (i % 2) + high * (1 - low)
        dx = middle * (1 - i % 2) + last
        dy = middle * (i % 2) + last
        part = rows // 2
        chip_rows = pl.ds(pl.multiple_of((2 * dy + dx) * rows + half * part, part), part)
        return ring.place(dy, dx, i // 2, half), i // 2, chip_rows

    @pl.loop(0, 16)
    def _(step):
        pl.when(step == 2)(lambda: ring.from_sibling("own", 0, 1))
        pl.when(step == 4)(ring.first_halves)

        @pl.when(step == 6)
        def _():
            ring.from_sibling("x", 0)
            ring.from_sibling("y", 0)

        pl.when(step == 8)(ring.second_halves)

        @pl.when(step == 10)
        def _():
            ring.from_sibling("x", 1)
            ring.from_sibling("y", 1)

        pl.when(step == 12)(ring.far_halves)
        pl.when(step == 14)(lambda: ring.from_sibling("d", 0, 1))

        slot = step % 2
        places = step_place(step)

        @pl.when(step >= 2)
        def _():
            for copy in out_copies(slot, step_place(step - 2)):
                copy.wait()

        x = full[places[0], :]

        @pl.loop(0, cols // NTILE)
        def _(at):
            n = pl.ds(pl.multiple_of(at * NTILE, NTILE), NTILE)
            gate = dot_nn(x, wg_all[:, n])
            up = dot_nn(x, wu_all[:, n])
            stage[slot, 0, :, n] = gate.astype(BF16)
            stage[slot, 1, :, n] = up.astype(BF16)
            stage[slot, 2, :, n] = (gate * up / (1.0 + jnp.exp(-gate))).astype(BF16)

        for copy in out_copies(slot, places):
            copy.start()

    for step in (14, 15):
        for copy in out_copies(step % 2, step_place(step)):
            copy.wait()
    ring.sent()


def gate_up(hn, wg, wu, dp_size):
    rows, width = hn.shape
    cols = wg.shape[1]
    tokens = GROUP * rows
    far = pl.BlockSpec(memory_space=pl.ANY)
    return pl.pallas_call(
        functools.partial(gate_up_kernel, 2 * math.isqrt(dp_size // GROUP)),
        in_specs=[far] * 3,
        out_specs=[far] * 5,
        out_shape=[jax.ShapeDtypeStruct((tokens, width), BF16)]
        + [jax.ShapeDtypeStruct((tokens, cols), BF16)] * 3
        + [jax.ShapeDtypeStruct((2, tokens // 2, cols), BF16)],
        scratch_shapes=[
            pltpu.VMEM((tokens, width), BF16),
            pltpu.VMEM((2, 3, rows // 2, cols), BF16),
            pltpu.VMEM(wg.shape, BF16),
            pltpu.VMEM(wu.shape, BF16),
            pltpu.SemaphoreType.DMA,
            pltpu.SemaphoreType.DMA((2,)),
            pltpu.SemaphoreType.DMA((Ring.COPIES,)),
            pltpu.SemaphoreType.DMA((Ring.COPIES,)),
            pltpu.SemaphoreType.DMA((2, 4)),
            pltpu.SemaphoreType.DMA((2,)),
        ],
        compiler_params=pltpu.CompilerParams(
            collective_id=1, has_side_effects=True, vmem_limit_bytes=56 << 20
        ),
        cost_estimate=pl.CostEstimate(
            flops=SHORT, bytes_accessed=0, transcendentals=0
        ),
    )(hn, wg, wu)


FAR_CHUNK, X_CHUNK, Y_CHUNK, OWN_CHUNK = range(4)


class Reduce:
    COPIES = 10

    def __init__(self, wide, parts, cores, far, near, send_sem, recv_sem):
        self.at, self.peers = neighbours(wide)
        self.parts, self.cores, self.far, self.near = parts, cores, far, near
        self.send_sem, self.recv_sem = send_sem, recv_sem
        self.half = parts.shape[2] // 2

    @staticmethod
    def scratch(rows, cols):
        return [
            pltpu.VMEM((2, 4, rows, cols), BF16),
            pltpu.VMEM((4, rows, cols), BF16),
            pltpu.VMEM((2, rows // 2, cols), BF16),
            pltpu.VMEM((2, rows, cols), BF16),
            pltpu.SemaphoreType.DMA((Reduce.COPIES,)),
            pltpu.SemaphoreType.DMA((Reduce.COPIES,)),
        ]

    def chunk(self, step):
        slot, other = step // 2, 1 - step % 2
        row, col, core = self.at
        dy, dx = 1 - slot % 2, 1 - slot // 2
        place = 4 * ((row + dy) % 2) + 2 * ((col + dx) % 2) + (core + other) % 2
        return place, self.parts.at[other, slot]

    def copy(self, name):
        upper, lower = pl.ds(0, self.half), pl.ds(self.half, self.half)
        mine = self.parts.at[0]
        table = {
            "far0": (self.parts.at[1, FAR_CHUNK], self.cores.at[FAR_CHUNK], SIB),
            "x": (self.parts.at[1, X_CHUNK], self.cores.at[X_CHUNK], SIB),
            "y": (self.parts.at[1, Y_CHUNK], self.cores.at[Y_CHUNK], SIB),
            "own": (self.parts.at[1, OWN_CHUNK], self.cores.at[OWN_CHUNK], SIB),
            "far_x": (mine.at[FAR_CHUNK, lower], self.far.at[0], XN),
            "far_y": (mine.at[FAR_CHUNK, upper], self.far.at[1], YN),
            "x_upper": (mine.at[X_CHUNK, upper], self.near.at[0, upper], XN),
            "x_lower": (mine.at[X_CHUNK, lower], self.near.at[0, lower], XN),
            "y_upper": (mine.at[Y_CHUNK, upper], self.near.at[1, upper], YN),
            "y_lower": (mine.at[Y_CHUNK, lower], self.near.at[1, lower], YN),
        }
        src, dst, peer = table[name]
        at = list(table).index(name)
        return pltpu.make_async_remote_copy(
            src_ref=src, dst_ref=dst, send_sem=self.send_sem.at[at],
            recv_sem=self.recv_sem.at[at], device_id={"dp": self.peers[peer]},
            device_id_type=MESH,
        )

    def start(self, *names):
        for name in names:
            self.copy(name).start()

    def add(self, slot, start, other):
        count = other.shape[0] // STRIP

        @pl.loop(0, count)
        def _(at):
            here = pl.ds(pl.multiple_of(start + at * STRIP, STRIP), STRIP)
            there = pl.ds(pl.multiple_of(at * STRIP, STRIP), STRIP)
            value = self.parts[0, slot, here, :].astype(F32) + other[there, :].astype(F32)
            self.parts[0, slot, here, :] = value.astype(BF16)

    def merge_core(self, slot, name):
        self.copy(name).wait_recv()
        self.add(slot, 0, self.cores.at[slot])

    def after(self, step):
        names = ("far0", "x", "y", "own")
        for slot in range(4):
            pl.when(step == 2 * slot)(functools.partial(self.start, names[slot]))

        @pl.when(step == 1)
        def _():
            self.merge_core(FAR_CHUNK, "far0")
            self.start("far_x", "far_y")

        @pl.when(step == 3)
        def _():
            self.merge_core(X_CHUNK, "x")
            self.start("x_lower")

        @pl.when(step == 5)
        def _():
            self.merge_core(Y_CHUNK, "y")
            self.start("y_upper")

    def pass_on(self):
        self.copy("far_y").wait_recv()
        self.add(X_CHUNK, 0, self.far.at[1])
        self.start("x_upper")
        self.copy("far_x").wait_recv()
        self.add(Y_CHUNK, self.half, self.far.at[0])
        self.start("y_lower")

    def finish(self, store):
        for name in ("own", "x_upper", "x_lower", "y_upper", "y_lower"):
            self.copy(name).wait_recv()

        @pl.loop(0, 2 * self.half // STRIP)
        def _(at):
            here = pl.ds(pl.multiple_of(at * STRIP, STRIP), STRIP)
            value = self.parts[0, OWN_CHUNK, here, :].astype(F32)
            value += self.cores[OWN_CHUNK, here, :].astype(F32)
            value += self.near[0, here, :].astype(F32)
            value += self.near[1, here, :].astype(F32)
            store(here, value)

    def sent(self):
        for name in (
            "far0", "x", "y", "own", "far_x", "far_y", "x_upper", "x_lower", "y_upper", "y_lower",
        ):
            self.copy(name).wait_send()


def hidden_back_kernel(
    wide, gain_ref, h_ref, grad_ref, dgate_ref, dup_ref, wg_ref, wu_ref,
    dh_ref, low_ref, gain_out,
    loaded, wg_all, wu_all, h_all, grad_all, load_sem, own_sem, *scratch,
):
    ring = Reduce(wide, *scratch)
    rows = dh_ref.shape[0]

    def loads(step):
        chunk, _ = ring.chunk(step)
        here = pl.ds(pl.multiple_of(chunk * rows, rows), rows)
        return [
            pltpu.make_async_copy(
                ref.at[here], loaded.at[step % 2, at], load_sem.at[step % 2, at]
            )
            for at, ref in enumerate((dgate_ref, dup_ref))
        ]

    pairs = ((wg_ref, wg_all), (wu_ref, wu_all), (h_ref, h_all), (grad_ref, grad_all))
    whole = [
        pltpu.make_async_copy(src, dst, own_sem.at[at]) for at, (src, dst) in enumerate(pairs)
    ]
    for copy in loads(0) + whole:
        copy.start()
    meet(ring.peers)
    for copy in whole[:2]:
        copy.wait()

    @pl.loop(0, 8)
    def _(step):
        @pl.when(step < 7)
        def _():
            for copy in loads(step + 1):
                copy.start()

        for copy in loads(step):
            copy.wait()
        _, target = ring.chunk(step)
        dgate, dup = loaded[step % 2, 0], loaded[step % 2, 1]

        @pl.loop(0, dh_ref.shape[1] // NTILE)
        def _(at):
            n = pl.ds(pl.multiple_of(at * NTILE, NTILE), NTILE)
            value = dot_nt(dgate, wg_all[n, :]) + dot_nt(dup, wu_all[n, :])
            target[:, n] = value.astype(BF16)

        ring.after(step)

    ring.pass_on()
    for copy in whole[2:]:
        copy.wait()
    gain_out[...] = jnp.zeros_like(gain_out)

    def store(here, value):
        h = h_all[here, :]
        scale = rms_scale(h)
        gained = value * gain_ref[...]
        inner = jnp.mean(gained * h, axis=1, keepdims=True)
        gain_out[...] += value * h * scale
        total = grad_all[here, :].astype(F32) + scale * gained
        total -= h * (scale * scale * scale * inner)
        dh_ref[here, :] = total
        low_ref[here, :] = total.astype(BF16)

    ring.finish(store)
    ring.sent()


def hidden_back(gain, h, grad, dgate, dup, wg, wu, dp_size):
    tokens, cols = dgate.shape
    rows, width = h.shape
    far = pl.BlockSpec(memory_space=pl.ANY)
    near = pl.BlockSpec(memory_space=pltpu.VMEM)
    return pl.pallas_call(
        functools.partial(hidden_back_kernel, 2 * math.isqrt(dp_size // GROUP)),
        in_specs=[near] + [far] * 6,
        out_specs=[near] * 3,
        out_shape=[
            jax.ShapeDtypeStruct((rows, width), F32),
            jax.ShapeDtypeStruct((rows, width), BF16),
            jax.ShapeDtypeStruct((STRIP, width), F32),
        ],
        scratch_shapes=[
            pltpu.VMEM((2, 2, rows, cols), BF16),
            pltpu.VMEM(wg.shape, BF16),
            pltpu.VMEM(wu.shape, BF16),
            pltpu.VMEM(h.shape, F32),
            pltpu.VMEM(grad.shape, BF16),
            pltpu.SemaphoreType.DMA((2, 2)),
            pltpu.SemaphoreType.DMA((4,)),
        ]
        + Reduce.scratch(rows, width),
        compiler_params=pltpu.CompilerParams(
            collective_id=6, has_side_effects=True, vmem_limit_bytes=62 << 20
        ),
        cost_estimate=pl.CostEstimate(
            flops=2 * LONG, bytes_accessed=4 * rows * width, transcendentals=0
        ),
    )(gain, h, grad, dgate, dup, wg, wu)


def tail_kernel(
    wide, z_size, mlp_count, x_ref, dq_ref, dkv_ref, wo_ref, gain_ref,
    raw_ref, dh_ref, wq_ref, wkv_ref, *refs
):
    mlp_ins, refs = refs[:mlp_count], refs[mlp_count:]
    wq_out, wkv_out, wo_out, gain_out, grad_out = refs[:5]
    mlp_outs, scratch = refs[5 : 5 + mlp_count], refs[5 + mlp_count :]
    sub = wkv_out.shape[1]
    halves = wq_out.shape[1] // sub
    count = halves + 1
    rings = [Reduce(wide, *scratch[6 * at : 6 * at + 6]) for at in range(count)]
    sums, zrecv, gain_z, gain_p, z_send, z_recv, g_send, g_recv = scratch[6 * count : 6 * count + 8]
    wo_recv, w_send, w_recv = scratch[6 * count + 8 : 6 * count + 11]
    wq_all, wkv_all, raw, dh, dxn, gain_sum, load_sem = scratch[6 * count + 11 : 6 * count + 18]
    mlp_copies = send_home(wide, mlp_ins, mlp_outs, *scratch[6 * count + 18 :])
    place = lax.axis_index("tensor")
    mine, found = others(wide)
    along = along_peers(place, z_size)
    around = [device for _, device in found]

    tiles, tile_rows = raw.shape[0], raw.shape[1]
    loads = [
        pltpu.make_async_copy(wq_ref, wq_all, load_sem.at[0]),
        pltpu.make_async_copy(wkv_ref, wkv_all, load_sem.at[1]),
    ]
    for tile in range(tiles):
        here = pl.ds(tile * tile_rows, tile_rows)
        loads += [
            pltpu.make_async_copy(raw_ref.at[here], raw.at[tile], load_sem.at[2 + 2 * tile]),
            pltpu.make_async_copy(dh_ref.at[here], dh.at[tile], load_sem.at[3 + 2 * tile]),
        ]
    for copy in loads:
        copy.start()
    greet(along + around)

    wo_part = wo_out.shape[1]
    wo_copies = [
        pltpu.make_async_remote_copy(
            src_ref=wo_ref.at[
                :,
                pl.ds(pl.multiple_of((place + at + 1) % z_size * wo_part, LANES), wo_part),
            ],
            dst_ref=wo_recv.at[at], send_sem=w_send.at[at], recv_sem=w_recv.at[at],
            device_id=peer, device_id_type=MESH,
        )
        for at, peer in enumerate(along)
    ]
    for copy in wo_copies:
        copy.start()

    pieces = [(dq_ref, wq_out, at * sub) for at in range(halves)] + [(dkv_ref, wkv_out, 0)]
    rows = sums.shape[1]
    z_copies = []

    def partial_sums(index):
        ring = rings[index]
        right, out, offset = pieces[index]

        @pl.loop(0, 8)
        def _(step):
            chunk, target = ring.chunk(step)
            x = x_ref[:, pl.ds(pl.multiple_of(chunk * rows, rows), rows)].T

            @pl.loop(0, z_size)
            def _(at):
                n = pl.ds(pl.multiple_of(at * sub, LANES), sub)
                source = pl.ds(pl.multiple_of(at * out.shape[1] + offset, LANES), sub)
                target[:, n] = dot_nn(x, right[:, source]).astype(BF16)

            ring.after(step)

    gain_sum[...] = jnp.zeros_like(gain_sum)

    def input_rows(tile):
        part = pl.ds(tile * tile_rows, tile_rows)
        dq, dkv = dq_ref[part, :], dkv_ref[part, :]

        @pl.loop(0, dxn.shape[1] // NTILE)
        def _(at):
            n = pl.ds(pl.multiple_of(at * NTILE, NTILE), NTILE)
            dxn[:, n] = dot_nt(dq, wq_all[n, :]) + dot_nt(dkv, wkv_all[n, :])

        @pl.loop(0, tile_rows // STRIP)
        def _(at):
            here = pl.ds(pl.multiple_of(at * STRIP, STRIP), STRIP)
            there = pl.ds(pl.multiple_of(tile * tile_rows + at * STRIP, STRIP), STRIP)
            grad, value = dxn[here, :], raw[tile, here, :].astype(F32)
            scale = rms_scale(value)
            gained = grad * gain_ref[0:1, :]
            inner = jnp.mean(gained * value, axis=1, keepdims=True)
            gain_sum[...] += grad * value * scale
            total = scale * gained - value * (scale * scale * scale * inner)
            grad_out[there, :] = (dh[tile, here, :] + total).astype(BF16)

    def send_along(index):
        def store(here, value):
            sums[index, here, :] = value.astype(BF16)

        rings[index].finish(store)
        for at, peer in enumerate(along):
            other = (place + at + 1) % z_size
            copy = pltpu.make_async_remote_copy(
                src_ref=sums.at[index, :, pl.ds(pl.multiple_of(other * sub, LANES), sub)],
                dst_ref=zrecv.at[index, at],
                send_sem=z_send.at[index, at], recv_sem=z_recv.at[index, at],
                device_id=peer, device_id_type=MESH,
            )
            z_copies.append(copy)
            copy.start()

    partial_sums(0)
    for copy in loads:
        copy.wait()
    input_rows(0)
    rings[0].pass_on()
    for index in range(1, count):
        partial_sums(index)
        if index < tiles:
            input_rows(index)
        if index + 1 < count:
            rings[index].pass_on()
            send_along(index - 1)
    for tile in range(count, tiles):
        input_rows(tile)

    gain_z[place, 0:1] = jnp.sum(gain_sum[...], axis=0, keepdims=True)
    gain_z[place, 1:2] = gain_ref[1:2, :]
    gain_copies = [
        pltpu.make_async_remote_copy(
            src_ref=gain_z.at[place], dst_ref=gain_z.at[place], send_sem=g_send.at[at],
            recv_sem=g_recv.at[at], device_id=peer, device_id_type=MESH,
        )
        for at, peer in enumerate(along)
    ]
    for copy in gain_copies:
        copy.start()
    rings[count - 1].pass_on()
    for copy in mlp_copies:
        copy.start()
    send_along(count - 2)

    for copy in gain_copies:
        copy.wait_recv()
    total = gain_z[0]
    for at in range(1, z_size):
        total = total + gain_z[at]
    gain_p[mine] = total
    for at, peer in enumerate(around):
        copy = pltpu.make_async_remote_copy(
            src_ref=gain_p.at[mine], dst_ref=gain_p.at[mine],
            send_sem=g_send.at[z_size - 1 + at], recv_sem=g_recv.at[z_size - 1 + at],
            device_id=peer, device_id_type=MESH,
        )
        gain_copies.append(copy)
        copy.start()
    for copy in wo_copies:
        copy.wait()
    total = wo_ref[:, pl.ds(pl.multiple_of(place * wo_part, LANES), wo_part)].astype(F32)
    for at in range(z_size - 1):
        total += wo_recv[at].astype(F32)
    wo_out[...] = total
    send_along(count - 1)

    for copy in gain_copies[z_size - 1 :]:
        copy.wait_recv()
    total = gain_p[0]
    for at in range(1, GROUP):
        total = total + gain_p[at]
    gain_out[...] = total
    for copy in z_copies:
        copy.wait_recv()
    for index, (_, out, offset) in enumerate(pieces):
        value = sums[index, :, pl.ds(pl.multiple_of(place * sub, LANES), sub)].astype(F32)
        for at in range(z_size - 1):
            value += zrecv[index, at].astype(F32)
        out[:, offset : offset + sub] = value
    for copy in z_copies + gain_copies:
        copy.wait_send()
    for ring in rings:
        ring.sent()
    for copy in mlp_copies:
        copy.wait()


def last_grads(x, dq, dkv, wo_sum, gains, raw, dh, wq, wkv, mlp, dp_size, z_size):
    tokens, width = x.shape
    rows = width // GROUP
    tiles = tokens // QTILE
    near = pl.BlockSpec(memory_space=pltpu.VMEM)
    far = pl.BlockSpec(memory_space=pl.ANY)
    sizes = [dq.shape[1], dkv.shape[1]]
    cols = dkv.shape[1]
    count = sum(sizes) // cols
    scratch = []
    for _ in range(count):
        scratch += Reduce.scratch(rows, cols)
    return pl.pallas_call(
        functools.partial(tail_kernel, 2 * math.isqrt(dp_size // GROUP), z_size, len(mlp)),
        in_specs=[near] * 5 + [far] * (4 + len(mlp)),
        out_specs=[near] * 5 + [far] * len(mlp),
        out_shape=[jax.ShapeDtypeStruct((rows, size // z_size), F32) for size in sizes]
        + [
            jax.ShapeDtypeStruct((rows, wo_sum.shape[1] // z_size), F32),
            jax.ShapeDtypeStruct(gains.shape, F32),
            jax.ShapeDtypeStruct((tokens, width), BF16),
        ]
        + home_shapes(mlp),
        scratch_shapes=scratch
        + [
            pltpu.VMEM((count, rows, cols), BF16),
            pltpu.VMEM((count, z_size - 1, rows, cols // z_size), BF16),
            pltpu.VMEM((z_size, *gains.shape), F32),
            pltpu.VMEM((GROUP, *gains.shape), F32),
            pltpu.SemaphoreType.DMA((count, z_size - 1)),
            pltpu.SemaphoreType.DMA((count, z_size - 1)),
            pltpu.SemaphoreType.DMA((z_size - 1 + GROUP - 1,)),
            pltpu.SemaphoreType.DMA((z_size - 1 + GROUP - 1,)),
            pltpu.VMEM((z_size - 1, rows, wo_sum.shape[1] // z_size), BF16),
            pltpu.SemaphoreType.DMA((z_size - 1,)),
            pltpu.SemaphoreType.DMA((z_size - 1,)),
            pltpu.VMEM(wq.shape, BF16),
            pltpu.VMEM(wkv.shape, BF16),
            pltpu.VMEM((tiles, QTILE, width), BF16),
            pltpu.VMEM((tiles, QTILE, width), F32),
            pltpu.VMEM((QTILE, width), F32),
            pltpu.VMEM((STRIP, width), F32),
            pltpu.SemaphoreType.DMA((2 + 2 * tiles,)),
        ]
        + home_scratch(mlp),
        compiler_params=pltpu.CompilerParams(
            collective_id=4, has_side_effects=True, vmem_limit_bytes=62 << 20
        ),
        cost_estimate=pl.CostEstimate(flops=SHORT, bytes_accessed=0, transcendentals=0),
    )(x, dq, dkv, wo_sum, gains, raw, dh, wq, wkv, *mlp)


class Layout:
    def __init__(self, dp_size):
        self.blocks = dp_size // GROUP
        side = math.isqrt(self.blocks)
        self.rows, self.cols = side, self.blocks // side
        wide = 2 * self.cols

        def index(by, bx, y, x, core):
            return ((2 * by + y) * wide + 2 * bx + x) * 2 + core

        places = [(y, x, c) for y in range(2) for x in range(2) for c in range(2)]
        spots = [(by, bx) for by in range(self.rows) for bx in range(self.cols)]
        self.inner = [[index(*s, *p) for p in places] for s in spots]
        self.outer = [[index(*s, *p) for s in spots] for p in places]

    def groups(self):
        return None if self.blocks == 1 else self.inner

    def to_rows(self, array):
        if self.blocks == 1:
            return array
        rest = array.shape[1:]
        split = array.reshape(2, 2, 2, self.rows, self.cols, -1, *rest)
        order = (3, 0, 4, 1, 2, 5) + tuple(range(6, 6 + len(rest)))
        return split.transpose(order).reshape(array.shape)

    def from_rows(self, array):
        if self.blocks == 1:
            return array
        rest = array.shape[1:]
        split = array.reshape(self.rows, 2, self.cols, 2, 2, -1, *rest)
        order = (1, 3, 4, 0, 2, 5) + tuple(range(6, 6 + len(rest)))
        return split.transpose(order).reshape(array.shape)

    def from_cols(self, array):
        return array if self.blocks == 1 else self.from_rows(array.T).T

    def gather_outer(self, array):
        if self.blocks == 1:
            return array
        return lax.all_gather(array, "dp", axis_index_groups=self.outer, axis=0, tiled=True)

    def scatter_outer(self, array):
        if self.blocks == 1:
            return array
        return lax.psum_scatter(
            array, "dp", scatter_dimension=0, axis_index_groups=self.outer, tiled=True
        )

    def swap(self, array, flip):
        pairs = [
            (block[at], block[at ^ flip]) for block in self.inner for at in range(GROUP)
        ]
        return lax.ppermute(array, "dp", pairs)

    def sum_outer(self, array):
        if self.blocks == 1:
            return array
        return lax.psum(array, "dp", axis_index_groups=self.outer)

    def gather(self, array):
        return lax.all_gather(array, "dp", axis_index_groups=self.groups(), axis=0, tiled=True)

    def scatter(self, array):
        return lax.psum_scatter(
            array, "dp", scatter_dimension=0, axis_index_groups=self.groups(), tiled=True
        )


def rms_scale(values):
    return lax.rsqrt(jnp.mean(values * values, axis=-1, keepdims=True) + NORM_EPS)


def per_device(
    dp_size, z_size, activations, segment_ids, attn_gain, w_query, w_key, w_value, w_out,
    mlp_gain, w_gate, w_up, w_down, cotangent,
):
    layout = Layout(dp_size)
    rows, width = activations.shape[1:]
    x = activations[0].astype(F32)
    place = lax.axis_index("tensor")
    reach = -(-(MOST_DOC - 1) // rows) * rows

    def shift(array, step):
        pairs = [(at, at + step) for at in range(z_size) if 0 <= at + step < z_size]
        return lax.ppermute(array, "tensor", pairs)

    starts = document_starts(segment_ids[0])
    own_starts = lax.dynamic_slice_in_dim(starts, place * rows, rows)
    own_tokens = place * rows + jnp.arange(rows, dtype=jnp.int32)
    cosine, sine = rope_tables(own_tokens - own_starts)
    low = (own_starts - place * rows + reach)[None, :]

    shards = [
        layout.gather_outer(w)
        for w in (w_gate, w_up, w_down, jnp.concatenate([w_key, w_value], axis=1), w_query, w_out)
    ]
    xn, *spread = spread_weights(
        activations[0], attn_gain[None], shards[:3], shards[3:], dp_size, z_size
    )
    def gather_z(array):
        return layout.to_rows(lax.all_gather(array, "tensor", axis=1, tiled=True))

    wg, wu = gather_z(spread[0]), gather_z(spread[1])

    def along_z(total):
        return lax.psum_scatter(
            layout.from_rows(total), "tensor", scatter_dimension=1, tiled=True
        )

    q, kv_all, wq, wo, dy = project(
        layout.from_cols(xn), cosine, sine, *spread[3:], cotangent[0], reach, dp_size, z_size
    )
    wd = gather_z(spread[2])
    wkv, wq, wo = (layout.to_rows(w) for w in (spread[3], wq, wo))
    att, lse, dy = attend(q, kv_all, low, cotangent[0], dy, dp_size)
    h = x + dot_nt(att, wo)

    r2 = rms_scale(h)
    hn, gate, up, hidden, by_core = gate_up((h * r2 * mlp_gain).astype(BF16), wg, wu, dp_size)
    part = rows // 2
    away = dot_nt(by_core[1], wd).astype(BF16)
    dy, away = lax.optimization_barrier((dy, away))
    total_wd = dot_tn(dy, hidden).astype(BF16)
    part_wd = along_z(total_wd)
    from_core = layout.swap(away, 1)

    def out_rows(start, count, *more):
        some = slice(start * part, (start + count) * part)
        total = dot_nt(by_core[0, some], wd) + from_core[some].astype(F32)
        for other in more:
            total = total + other.astype(F32)
        return total.astype(BF16)

    far_y, far_x, x_lower, y_upper = (out_rows(at, 1) for at in (6, 7, 3, 4))
    dy, far_x, far_y, x_lower, y_upper = lax.optimization_barrier(
        (dy, far_x, far_y, x_lower, y_upper)
    )
    from_x, from_y = layout.swap(far_x, 2), layout.swap(far_y, 4)
    x_lower, y_upper = layout.swap(x_lower, 2), layout.swap(y_upper, 4)
    gate, up = gate.astype(F32), up.astype(F32)
    sigma = jax.nn.sigmoid(gate)
    dhid = dot_nn(dy, wd)
    dgate = (dhid * up * sigma * (1.0 + gate * (1.0 - sigma))).astype(BF16)
    dup = (dhid * gate * sigma).astype(BF16)
    dgate, dup, from_x, from_y = lax.optimization_barrier((dgate, dup, from_x, from_y))
    x_upper, y_lower = out_rows(2, 1, from_y), out_rows(5, 1, from_x)
    dgate, dup, x_upper, y_lower = lax.optimization_barrier((dgate, dup, x_upper, y_lower))
    x_upper, y_lower = layout.swap(x_upper, 2), layout.swap(y_lower, 4)
    total_wg = dot_tn(hn, dgate).astype(BF16)
    dup, total_wg, x_lower, y_upper = lax.optimization_barrier((dup, total_wg, x_lower, y_upper))
    part_wg = along_z(total_wg)
    total_wu = dot_tn(hn, dup).astype(BF16)
    dup, total_wu = lax.optimization_barrier((dup, total_wu))
    part_wu = along_z(total_wu)
    dup, x_upper, y_lower = lax.optimization_barrier((dup, x_upper, y_lower))
    dh, dhb, gain_two = hidden_back(
        mlp_gain[None], h, cotangent[0], dgate, dup, wg, wu, dp_size
    )
    gain_two = jnp.sum(gain_two, axis=0)
    dhb, part_wd = lax.optimization_barrier((dhb, part_wd))
    datt = dot_nn(dhb, wo).astype(BF16)
    total_wo = layout.from_rows(dot_tn(dhb, att).astype(BF16))
    datt, part_wg, total_wo = lax.optimization_barrier((datt, part_wg, total_wo))
    part_wo = layout.scatter(total_wo)
    dq, dkv, wd_grad, wg_grad = attend_back(
        q, datt, att, kv_all, lse, low, cosine, sine, (part_wd, part_wg), dp_size, z_size
    )
    dq, part_wu = lax.optimization_barrier((dq, part_wu))
    dq, part_wo = lax.optimization_barrier((dq, part_wo))
    wq_grad, wkv_grad, wo_grad, gains, input_grad, wu_grad = last_grads(
        layout.from_cols(xn), dq, dkv, part_wo, jnp.stack([attn_gain, gain_two]),
        activations[0], dh, wq, wkv, (part_wu,), dp_size, z_size,
    )
    gains = layout.sum_outer(gains)
    output = h + out_rows(0, 2).astype(F32)
    output = output + jnp.concatenate([x_upper, x_lower]).astype(F32)
    output = output + jnp.concatenate([y_upper, y_lower]).astype(F32)
    wo_grad, wq_grad, wkv_grad, wd_grad, wg_grad, wu_grad = (
        layout.scatter_outer(grad).astype(F32)
        for grad in (wo_grad, wq_grad, wkv_grad, wd_grad, wg_grad, wu_grad)
    )
    key_cols = w_key.shape[1]
    return (
        output.astype(BF16)[None],
        input_grad[None],
        gains[0],
        wq_grad,
        wkv_grad[:, :key_cols],
        wkv_grad[:, key_cols:],
        wo_grad,
        gains[1],
        wg_grad,
        wu_grad,
        wd_grad,
    )


def solution(mesh):
    split = P("dp", "tensor")
    tokens = P("dp", "tensor", None)
    in_specs = (
        tokens, P("dp", None), P(), split, split, split, split, P(), split, split, split, tokens,
    )
    out_specs = (tokens, tokens, P(), split, split, split, split, P(), split, split, split)
    return jax.shard_map(
        functools.partial(per_device, mesh.shape["dp"], mesh.shape["tensor"]),
        mesh=mesh, in_specs=in_specs, out_specs=out_specs, check_vma=False,
    )
```

```python
import functools
import math

import jax
import jax.numpy as jnp
from jax import lax
from jax.experimental import pallas as pl
from jax.experimental.pallas import tpu as pltpu
from jax.sharding import PartitionSpec as P

HEAD_DIM = 64
DOCS = 4
MOST_DOC = 1024
NORM_EPS = 1e-05
ROPE_THETA = 500000.0
GROUP = 8
LANES = 128
QTILE = 256
SCALE = HEAD_DIM ** (-0.5)
LOG2E = 1.4426950408889634
FAR = -1e30
NTILE = 512
STRIP = 16
LONG = 60_000_000_000
SHORT = 1_000_000

F32 = jnp.float32
BF16 = jnp.bfloat16


def dot_nn(left, right):
    return lax.dot_general(left, right, (((1,), (0,)), ((), ())), preferred_element_type=F32)


def dot_nt(left, right):
    return lax.dot_general(left, right, (((1,), (1,)), ((), ())), preferred_element_type=F32)


def dot_tn(left, right):
    return lax.dot_general(left, right, (((0,), (0,)), ((), ())), preferred_element_type=F32)


def document_starts(segments):
    doc_ids = jnp.arange(DOCS, dtype=jnp.int32)
    counts = jnp.sum((segments[:, None] == doc_ids).astype(jnp.int32), axis=0)
    before = (doc_ids < segments[:, None]).astype(jnp.int32)
    return jnp.sum(before * counts[None, :], axis=-1)


def rope_tables(positions):
    half = HEAD_DIM // 2
    frequency = jnp.exp(
        jnp.arange(half, dtype=F32) * (-2.0 * math.log(ROPE_THETA) / HEAD_DIM)
    )
    angles = positions.astype(F32)[:, None] * frequency
    cosine, sine = jnp.cos(angles), jnp.sin(angles)
    wide_cos = jnp.concatenate([cosine] * 4, axis=1)
    wide_sin = jnp.concatenate([-sine, sine, -sine, sine], axis=1)
    return wide_cos, wide_sin


def swap_halves(values):
    lane = lax.broadcasted_iota(jnp.int32, values.shape, 1)
    ahead = pltpu.roll(values, LANES - 32, 1)
    behind = pltpu.roll(values, 32, 1)
    return jnp.where((lane % 64) < 32, ahead, behind)


def fill_bias(bias_ref, low_ref, reach):
    span = bias_ref.shape[1]
    for tile in range(bias_ref.shape[0]):
        row = lax.broadcasted_iota(jnp.int32, (span, QTILE), 0)
        col = lax.broadcasted_iota(jnp.int32, (span, QTILE), 1)
        low = low_ref[0:1, tile * QTILE : (tile + 1) * QTILE]
        allowed = (row <= reach + col) & (row + tile * QTILE >= low)
        bias_ref[tile] = jnp.where(allowed, 0.0, FAR)


def spread_pair(pair, half):
    wide = pair.astype(F32)
    turned = pltpu.roll(wide, 64, 1)
    lane = lax.broadcasted_iota(jnp.int32, wide.shape, 1)
    mine = (lane // 64) == half
    even = half == 0
    first = jnp.where(mine, jnp.where(even, wide, turned), 0.0)
    second = jnp.where(mine, jnp.where(even, turned, wide), 0.0)
    return jnp.concatenate([first, second], axis=0).astype(BF16)


def gather_pair(transposed, half):
    count = transposed.shape[1] // 2
    mine = jnp.where(half == 0, transposed[:64], transposed[64:])
    return jnp.concatenate([mine[:, :count], mine[:, count:]], axis=0).T


def attend_kernel(
    reach, wide, q_ref, k_ref, v_ref, low_ref, own_ref, _, att_ref, lse_ref, all_ref,
    bias_ref, full, own_sem, send_sem, recv_sem, out_sem,
):
    head, tile, pair = pl.program_id(0), pl.program_id(1), pl.program_id(2)
    half = head % 2
    inner = pl.num_programs(1) * pl.num_programs(2)
    step = head * inner + tile * pl.num_programs(2) + pair
    ring = Ring(wide, full, own_ref.shape[0], send_sem, recv_sem)
    right = pl.ds(own_ref.shape[1] - full.shape[1], full.shape[1])

    def outward(slot, *flips):
        where = ring.whole(*flips)
        return pltpu.make_async_copy(full.at[where], all_ref.at[where, right], out_sem.at[slot])

    near = [(0, 0, 0), (0, 0, 1), (0, 1, 0), (1, 0, 0)]
    rest = [(0, 1, 1), (1, 0, 1), (1, 1, 0), (1, 1, 1)]

    @pl.when(step == 0)
    def _():
        local = pltpu.make_async_copy(own_ref.at[:, right], full.at[ring.mine()], own_sem)
        local.start()
        meet(ring.peers)
        local.wait()
        ring.start_own()
        fill_bias(bias_ref, low_ref, reach)

    pl.when(step == 2 * inner)(ring.first_halves)
    pl.when(step == 4 * inner)(ring.second_halves)

    keys = pl.ds(pl.multiple_of(tile * QTILE, QTILE), bias_ref.shape[1])
    queries = spread_pair(q_ref[...], half)
    bias = bias_ref[tile]
    score = dot_nt(k_ref[keys, :], queries)
    score = score + jnp.concatenate([bias, bias], axis=1)
    top = jnp.max(score, axis=0, keepdims=True) * (SCALE * LOG2E)
    weight = jnp.exp2(score * (SCALE * LOG2E) - top)
    total = jnp.sum(weight, axis=0, keepdims=True)
    result = dot_tn(v_ref[keys, :], weight.astype(BF16)) / total
    att_ref[...] = gather_pair(result, half).astype(BF16)
    lse_ref[0] = top + jnp.log2(total)

    @pl.when(step == pl.num_programs(0) * inner - 1)
    def _():
        ring.from_sibling("own", 0, 1)
        for slot, flips in enumerate(near):
            outward(slot, *flips).start()
        ring.far_halves()
        for name in ("x", "y", "d"):
            ring.from_sibling(name, 0, 1)
        for slot, flips in enumerate(rest):
            outward(4 + slot, *flips).start()
        for slot, flips in enumerate(near + rest):
            outward(slot, *flips).wait()
        ring.sent()


def attend(q, kv, low, grad, grads, dp_size):
    rows, width = q.shape
    keys = kv.shape[0]
    reach = keys - rows
    tiles = rows // QTILE
    pairs = width // LANES
    heads = kv.shape[1] // LANES
    per_head = pairs // heads
    span = reach + QTILE
    right = (grads.shape[0], grads.shape[1] // 2)
    far = pl.BlockSpec(memory_space=pl.ANY)
    return pl.pallas_call(
        functools.partial(attend_kernel, reach, 2 * math.isqrt(dp_size // GROUP)),
        grid=(heads, tiles, per_head),
        in_specs=[
            pl.BlockSpec((QTILE, LANES), lambda a, t, p: (t, a * per_head + p)),
            pl.BlockSpec((keys, LANES), lambda a, t, p: (0, 2 * (a // 2))),
            pl.BlockSpec((keys, LANES), lambda a, t, p: (0, 2 * (a // 2) + 1)),
            pl.BlockSpec((1, rows), lambda a, t, p: (0, 0)),
            far,
            far,
        ],
        out_specs=[
            pl.BlockSpec((QTILE, LANES), lambda a, t, p: (t, a * per_head + p)),
            pl.BlockSpec((1, 1, 2 * QTILE), lambda a, t, p: ((a * tiles + t) * per_head + p, 0, 0)),
            far,
        ],
        out_shape=[
            jax.ShapeDtypeStruct((rows, width), BF16),
            jax.ShapeDtypeStruct((pairs * tiles, 1, 2 * QTILE), F32),
            jax.ShapeDtypeStruct(grads.shape, BF16),
        ],
        scratch_shapes=[
            pltpu.VMEM((tiles, span, QTILE), F32),
            pltpu.VMEM(right, BF16),
            pltpu.SemaphoreType.DMA,
            pltpu.SemaphoreType.DMA((Ring.COPIES,)),
            pltpu.SemaphoreType.DMA((Ring.COPIES,)),
            pltpu.SemaphoreType.DMA((8,)),
        ],
        input_output_aliases={5: 2},
        compiler_params=pltpu.CompilerParams(
            collective_id=7, has_side_effects=True, vmem_limit_bytes=56 << 20
        ),
        cost_estimate=pl.CostEstimate(
            flops=16 * rows * span * LANES * pairs,
            bytes_accessed=4 * rows * width + 2 * keys * kv.shape[1],
            transcendentals=2 * rows * span * pairs,
        ),
    )(q, kv, kv, low, grad, grads)


def attend_back_kernel(
    reach, wide, z_size, mlp_count,
    q_ref, do_ref, o_ref, k_ref, v_ref, lse_ref, low_ref, cos_ref, sin_ref, cos_all, sin_all,
    *refs,
):
    mlp_ins, refs = refs[:mlp_count], refs[mlp_count:]
    dq_ref, dkv_ref = refs[:2]
    mlp_outs, refs = refs[2 : 2 + mlp_count], refs[2 + mlp_count :]
    bias_ref, dk_acc, dv_acc, own_part, send_part, recv_part, kv_send, kv_recv = refs[:8]
    home = refs[8:]
    block, half, tile, pair = (pl.program_id(at) for at in range(4))
    steps = pl.num_programs(1) * pl.num_programs(2) * pl.num_programs(3)
    inner = (half * pl.num_programs(2) + tile) * pl.num_programs(3) + pair
    step = block * steps + inner
    blocks = own_part.shape[0]
    rows = own_part.shape[1]
    count = reach // rows
    place = lax.axis_index("tensor")

    def exchange(at, distance):
        return pltpu.make_async_remote_copy(
            src_ref=send_part.at[at, pl.ds((count - distance) * rows, rows)],
            dst_ref=recv_part.at[at, distance - 1],
            send_sem=kv_send.at[at, distance - 1], recv_sem=kv_recv.at[at, distance - 1],
            device_id={"tensor": (place + z_size - distance) % z_size}, device_id_type=MESH,
        )

    def each_exchange(at, condition, action):
        for distance in range(1, count + 1):
            pl.when(condition(distance))(
                functools.partial(action, exchange(at, distance), at, distance)
            )

    @pl.when(step == 0)
    def _():
        greet(along_peers(place, z_size) + [device for _, device in others(wide)[1]])
        for copy in send_home(wide, mlp_ins, mlp_outs, *home):
            copy.start()
        fill_bias(bias_ref, low_ref, reach)

    @pl.when(inner == 0)
    def _():
        dk_acc[...] = jnp.zeros_like(dk_acc)
        dv_acc[...] = jnp.zeros_like(dv_acc)

    keys = pl.ds(pl.multiple_of(tile * QTILE, QTILE), bias_ref.shape[1])
    queries = spread_pair(q_ref[...], half)
    grads = spread_pair(do_ref[...], half)
    product = (do_ref[...].astype(F32) * o_ref[...].astype(F32)).T
    row_dot = jnp.concatenate(
        [
            jnp.sum(product[:64], axis=0, keepdims=True),
            jnp.sum(product[64:], axis=0, keepdims=True),
        ],
        axis=1,
    )
    bias = bias_ref[tile]
    key, value = k_ref[keys, :], v_ref[keys, :]
    score = dot_nt(key, queries) + jnp.concatenate([bias, bias], axis=1)
    weight = jnp.exp2(score * (SCALE * LOG2E) - lse_ref[0])
    dv_acc[keys, :] += dot_nn(weight.astype(BF16), grads)
    dscore = (weight * (dot_nt(value, grads) - row_dot)).astype(BF16)
    dk_acc[keys, :] += dot_nn(dscore, queries)
    dq = gather_pair(dot_tn(key, dscore), half) * SCALE
    dq_ref[...] = (dq * cos_ref[...] - swap_halves(dq) * sin_ref[...]).astype(BF16)

    @pl.when(inner == steps - 1)
    def _():
        send_part[block, :, :LANES] = (dk_acc[:reach] * SCALE).astype(BF16)
        send_part[block, :, LANES:] = dv_acc[:reach].astype(BF16)
        own_part[block, :, :LANES] = dk_acc[reach:] * SCALE
        own_part[block, :, LANES:] = dv_acc[reach:]
        each_exchange(block, lambda distance: place >= distance, lambda copy, *_: copy.start())

    @pl.when(step == blocks * steps - 1)
    def _():
        def collect(copy, at, distance):
            copy.wait_recv()
            own_part[at] += recv_part[at, distance - 1].astype(F32)

        for at in range(blocks):
            each_exchange(at, lambda distance: place + distance < z_size, collect)
            dkey = own_part[at, :, :LANES]
            dkey = dkey * cos_all[...] - swap_halves(dkey) * sin_all[...]
            dkv_ref[:, 2 * at * LANES : (2 * at + 1) * LANES] = dkey.astype(BF16)
            dkv_ref[:, (2 * at + 1) * LANES : (2 * at + 2) * LANES] = own_part[
                at, :, LANES:
            ].astype(BF16)
        for at in range(blocks):
            each_exchange(
                at, lambda distance: place >= distance, lambda copy, *_: copy.wait_send()
            )
        for copy in send_home(wide, mlp_ins, mlp_outs, *home):
            copy.wait()


def attend_back(q, do, att, kv, lse, low, cosine, sine, mlp, dp_size, z_size):
    rows, width = q.shape
    keys = kv.shape[0]
    reach = keys - rows
    tiles = rows // QTILE
    pairs = width // LANES
    heads = kv.shape[1] // LANES
    per_head = pairs // heads
    span = reach + QTILE
    blocks = heads // 2

    def pair_at(g, h, t, p):
        return (t, (2 * g + h) * per_head + p)

    def whole(shape):
        return pl.BlockSpec(shape, lambda g, h, t, p: (0, 0), pipeline_mode=pl.Buffered(1))

    table = pl.BlockSpec((QTILE, LANES), lambda g, h, t, p: (t, 0))
    return pl.pallas_call(
        functools.partial(
            attend_back_kernel, reach, 2 * math.isqrt(dp_size // GROUP), z_size, len(mlp)
        ),
        grid=(blocks, 2, tiles, per_head),
        in_specs=[
            pl.BlockSpec((QTILE, LANES), pair_at),
            pl.BlockSpec((QTILE, LANES), pair_at),
            pl.BlockSpec((QTILE, LANES), pair_at),
            pl.BlockSpec((keys, LANES), lambda g, h, t, p: (0, 2 * g)),
            pl.BlockSpec((keys, LANES), lambda g, h, t, p: (0, 2 * g + 1)),
            pl.BlockSpec(
                (1, 1, 2 * QTILE),
                lambda g, h, t, p: (((2 * g + h) * tiles + t) * per_head + p, 0, 0),
            ),
            whole((1, rows)),
            table,
            table,
            whole((rows, LANES)),
            whole((rows, LANES)),
        ]
        + [pl.BlockSpec(memory_space=pl.ANY)] * len(mlp),
        out_specs=[
            pl.BlockSpec((QTILE, LANES), pair_at),
            pl.BlockSpec((rows, kv.shape[1]), lambda g, h, t, p: (0, 0)),
        ]
        + [pl.BlockSpec(memory_space=pl.ANY)] * len(mlp),
        out_shape=[
            jax.ShapeDtypeStruct((rows, width), BF16),
            jax.ShapeDtypeStruct((rows, kv.shape[1]), BF16),
        ]
        + home_shapes(mlp),
        scratch_shapes=[
            pltpu.VMEM((tiles, span, QTILE), F32),
            pltpu.VMEM((keys, LANES), F32),
            pltpu.VMEM((keys, LANES), F32),
            pltpu.VMEM((blocks, rows, 2 * LANES), F32),
            pltpu.VMEM((blocks, reach, 2 * LANES), BF16),
            pltpu.VMEM((blocks, reach // rows, rows, 2 * LANES), BF16),
            pltpu.SemaphoreType.DMA((blocks, reach // rows)),
            pltpu.SemaphoreType.DMA((blocks, reach // rows)),
        ]
        + home_scratch(mlp),
        compiler_params=pltpu.CompilerParams(
            collective_id=5, has_side_effects=True, vmem_limit_bytes=60 << 20
        ),
        cost_estimate=pl.CostEstimate(
            flops=40 * rows * span * LANES * pairs,
            bytes_accessed=8 * rows * width + 4 * keys * kv.shape[1],
            transcendentals=2 * rows * span * pairs,
        ),
    )(q, do, att, kv, kv, lse, low, cosine, sine, cosine, sine, *mlp)


MESH = pl.DeviceIdType.MESH


def neighbours(wide):
    dp = lax.axis_index("dp")
    core, col, row = dp % 2, (dp // 2) % 2, (dp // (2 * wide)) % 2
    sibling = dp + 1 - 2 * core
    beside = dp + 2 - 4 * col
    above = dp + 2 * wide - 4 * wide * row
    return (row, col, core), (sibling, beside, above)


def meet(peers):
    barrier = pltpu.get_barrier_semaphore()
    for peer in peers:
        pl.semaphore_signal(barrier, inc=1, device_id={"dp": peer}, device_id_type=MESH)
    pl.semaphore_wait(barrier, len(peers))


def others(wide):
    (row, col, core), _ = neighbours(wide)
    base = lax.axis_index("dp") - (2 * wide * row + 2 * col + core)
    found = []
    for flip in range(1, GROUP):
        y, x, c = (row + flip // 4) % 2, (col + flip // 2) % 2, (core + flip) % 2
        found.append((4 * y + 2 * x + c, {"dp": base + 2 * wide * y + 2 * x + c}))
    return 4 * row + 2 * col + core, found


def along_peers(place, z_size):
    return [{"tensor": (place + step) % z_size} for step in range(1, z_size)]


def greet(peers):
    barrier = pltpu.get_barrier_semaphore()
    for peer in peers:
        pl.semaphore_signal(barrier, inc=1, device_id=peer, device_id_type=MESH)
    pl.semaphore_wait(barrier, len(peers))


def send_home(wide, ins, outs, own_sem, send_sem, recv_sem):
    mine, found = others(wide)
    copies = []
    for at, (src, dst) in enumerate(zip(ins, outs)):
        part, cols = dst.shape[0], src.shape[1]
        here = pl.ds(pl.multiple_of(mine * cols, LANES), cols)
        for index, (other, device) in enumerate(found):
            copies.append(
                pltpu.make_async_remote_copy(
                    src_ref=src.at[pl.ds(pl.multiple_of(other * part, part), part)],
                    dst_ref=dst.at[:, here],
                    send_sem=send_sem.at[at, index], recv_sem=recv_sem.at[at, index],
                    device_id=device, device_id_type=MESH,
                )
            )
        own = src.at[pl.ds(pl.multiple_of(mine * part, part), part)]
        copies.append(pltpu.make_async_copy(own, dst.at[:, here], own_sem.at[at]))
    return copies


def home_shapes(arrays):
    return [jax.ShapeDtypeStruct((a.shape[0] // GROUP, GROUP * a.shape[1]), BF16) for a in arrays]


def home_scratch(arrays):
    count = len(arrays)
    return [
        pltpu.SemaphoreType.DMA((count,)),
        pltpu.SemaphoreType.DMA((count, GROUP - 1)),
        pltpu.SemaphoreType.DMA((count, GROUP - 1)),
    ]


SIB, XN, YN = 0, 1, 2


def spread_kernel(wide, z_size, mlp_count, x_ref, gain_ref, *refs):
    attn_count = (len(refs) - 10) // 2 - mlp_count
    count = mlp_count + attn_count
    ins, xn_ref, outs = refs[:count], refs[count], refs[count + 1 : 2 * count + 1]
    x_all, x_sem, own_sem, send_sem, recv_sem, z_send, z_recv, ring_send, ring_recv = refs[
        2 * count + 1 :
    ]
    first = mlp_count
    ring = Ring(wide, outs[first], ins[first].shape[0], ring_send, ring_recv)
    place = lax.axis_index("tensor")
    mine, found = others(wide)
    greet(along_peers(place, z_size) + [device for _, device in found])

    local, copies = [], []
    for at in range(mlp_count):
        src, dst = ins[at], outs[at]
        rows, cols = src.shape[0], dst.shape[1]
        here = pl.ds(pl.multiple_of(mine * rows, rows), rows)
        for index, (other, device) in enumerate(found):
            copies.append(
                pltpu.make_async_remote_copy(
                    src_ref=src.at[:, pl.ds(pl.multiple_of(other * cols, LANES), cols)],
                    dst_ref=dst.at[here],
                    send_sem=send_sem.at[at, index], recv_sem=recv_sem.at[at, index],
                    device_id=device, device_id_type=MESH,
                )
            )
        own = src.at[:, pl.ds(pl.multiple_of(mine * cols, LANES), cols)]
        local.append(pltpu.make_async_copy(own, dst.at[here], own_sem.at[at]))

    def block(at, origin):
        cols = ins[at].shape[1]
        part = pl.ds(pl.multiple_of(origin * cols, LANES), cols)
        return outs[at].at[ring.mine() if at == first else slice(None), part]

    def hop(at, way, step, receive=False):
        sign = 1 - 2 * way
        origin = place - sign * (step if receive else step - 1)
        slot = 2 * (step - 1) + way
        src = block(at, origin) if receive or step > 1 else ins[at]
        return pltpu.make_async_remote_copy(
            src_ref=src, dst_ref=block(at, origin),
            send_sem=z_send.at[at - mlp_count, slot], recv_sem=z_recv.at[at - mlp_count, slot],
            device_id={"tensor": (place + z_size + sign) % z_size}, device_id_type=MESH,
        )

    def sends(way, step):
        if way == 0:
            return (place + 1 < z_size) & (place >= step - 1)
        return (place >= 1) & (place + step - 1 < z_size)

    def receives(way, step):
        return place >= step if way == 0 else place + step < z_size

    for at in range(mlp_count, count):
        local.append(pltpu.make_async_copy(ins[at], block(at, place), own_sem.at[at]))
        for way in range(2):
            pl.when(sends(way, 1))(lambda: hop(at, way, 1).start())
    for copy in copies + local:
        copy.start()
    load = pltpu.make_async_copy(x_ref, x_all, x_sem)
    load.start()
    load.wait()

    @pl.loop(0, x_all.shape[0] // STRIP)
    def _(at):
        here = pl.ds(pl.multiple_of(at * STRIP, STRIP), STRIP)
        value = x_all[here, :].astype(F32)
        xn_ref[here, :] = (value * rms_scale(value) * gain_ref[...]).astype(BF16)

    def advance(at, step):
        for way in range(2):
            pl.when(receives(way, step))(lambda: hop(at, way, step, True).wait_recv())
            if step + 1 < z_size:
                pl.when(sends(way, step + 1))(lambda: hop(at, way, step + 1).start())

    for step in range(1, z_size):
        advance(first, step)
    local.pop(first).wait()
    ring.start_own()
    stages = [ring.first_halves, ring.second_halves]
    for step in range(1, z_size):
        for at in range(first + 1, count):
            advance(at, step)
        if stages:
            stages.pop(0)()
    for stage in stages:
        stage()
    ring.far_halves()
    for name in ("own", "x", "y", "d"):
        ring.from_sibling(name, 0, 1)
    ring.sent()
    for step in range(1, z_size):
        for at in range(mlp_count, count):
            for way in range(2):
                pl.when(sends(way, step))(lambda: hop(at, way, step).wait_send())
    for copy in local + copies:
        copy.wait()


def spread_weights(x, gain, mlp, attn, dp_size, z_size):
    count = len(mlp) + len(attn)
    spec = pl.BlockSpec(memory_space=pl.ANY)
    near = pl.BlockSpec(memory_space=pltpu.VMEM)
    out = [jax.ShapeDtypeStruct(x.shape, BF16)]
    out += [jax.ShapeDtypeStruct((GROUP * w.shape[0], w.shape[1] // GROUP), BF16) for w in mlp]
    out += [
        jax.ShapeDtypeStruct(((1 if at else GROUP) * w.shape[0], z_size * w.shape[1]), BF16)
        for at, w in enumerate(attn)
    ]
    return pl.pallas_call(
        functools.partial(spread_kernel, 2 * math.isqrt(dp_size // GROUP), z_size, len(mlp)),
        in_specs=[spec, near] + [spec] * count,
        out_specs=[near] + [spec] * count,
        out_shape=out,
        scratch_shapes=[
            pltpu.VMEM(x.shape, BF16),
            pltpu.SemaphoreType.DMA,
            pltpu.SemaphoreType.DMA((count,)),
            pltpu.SemaphoreType.DMA((len(mlp), GROUP - 1)),
            pltpu.SemaphoreType.DMA((len(mlp), GROUP - 1)),
            pltpu.SemaphoreType.DMA((len(attn), 2 * (z_size - 1))),
            pltpu.SemaphoreType.DMA((len(attn), 2 * (z_size - 1))),
            pltpu.SemaphoreType.DMA((Ring.COPIES,)),
            pltpu.SemaphoreType.DMA((Ring.COPIES,)),
        ],
        compiler_params=pltpu.CompilerParams(collective_id=2, has_side_effects=True),
        cost_estimate=pl.CostEstimate(flops=LONG, bytes_accessed=0, transcendentals=0),
    )(x, gain, *mlp, *attn)


class Ring:
    FLIP = {SIB: (0, 0, 1), XN: (0, 1, 0), YN: (1, 0, 0)}
    COPIES = 14

    def __init__(self, wide, ref, rows, send_sem, recv_sem):
        (self.row, self.col, self.core), self.peers = neighbours(wide)
        self.ref, self.rows, self.part = ref, rows, rows // 2
        self.send_sem, self.recv_sem = send_sem, recv_sem
        self.sends = {}
        for half in range(2):
            self.sends["own", XN, half] = (2 + half, 0, 0, 0, half)
            self.sends["own", YN, half] = (4 + half, 0, 0, 0, half)
            self.sends["own", SIB, half] = (0 + half, 0, 0, 0, half)
        for half in range(2):
            self.sends["x", SIB, half] = (6 + half, 0, 1, 0, half)
            self.sends["y", SIB, half] = (8 + half, 1, 0, 0, half)
            self.sends["d", SIB, half] = (10 + half, 1, 1, 0, half)
        self.sends["x", YN, 0] = (12, 0, 1, 0, 0)
        self.sends["y", XN, 1] = (13, 1, 0, 0, 1)

    def place(self, dy, dx, dc, half):
        p = 4 * ((self.row + dy) % 2) + 2 * ((self.col + dx) % 2) + (self.core + dc) % 2
        return pl.ds(pl.multiple_of(p * self.rows + half * self.part, self.part), self.part)

    def mine(self):
        p = 4 * self.row + 2 * self.col + self.core
        return pl.ds(pl.multiple_of(p * self.rows, self.rows), self.rows)

    def whole(self, dy, dx, dc):
        p = 4 * ((self.row + dy) % 2) + 2 * ((self.col + dx) % 2) + (self.core + dc) % 2
        return pl.ds(pl.multiple_of(p * self.rows, self.rows), self.rows)

    def copy(self, slot, dy, dx, dc, half, peer):
        where = self.place(dy, dx, dc, half)
        return pltpu.make_async_remote_copy(
            src_ref=self.ref.at[where], dst_ref=self.ref.at[where],
            send_sem=self.send_sem.at[slot], recv_sem=self.recv_sem.at[slot],
            device_id={"dp": self.peers[peer]}, device_id_type=MESH,
        )

    def start(self, name, peer, half):
        self.copy(*self.sends[name, peer, half], peer).start()

    def arrived(self, name, peer, half):
        slot, dy, dx, dc, half = self.sends[name, peer, half]
        fy, fx, fc = self.FLIP[peer]
        self.copy(slot, (dy + fy) % 2, (dx + fx) % 2, (dc + fc) % 2, half, peer).wait_recv()

    def start_own(self):
        for half in range(2):
            for peer in (XN, YN, SIB):
                self.start("own", peer, half)

    def first_halves(self):
        self.arrived("own", XN, 0)
        self.start("x", YN, 0)
        self.start("x", SIB, 0)
        self.arrived("own", YN, 0)
        self.start("y", SIB, 0)

    def second_halves(self):
        self.arrived("own", YN, 1)
        self.start("y", XN, 1)
        self.start("y", SIB, 1)
        self.arrived("own", XN, 1)
        self.start("x", SIB, 1)

    def far_halves(self):
        self.arrived("x", YN, 0)
        self.start("d", SIB, 0)
        self.arrived("y", XN, 1)
        self.start("d", SIB, 1)

    def from_sibling(self, name, *halves):
        for half in halves:
            self.arrived(name, SIB, half)

    def sent(self):
        for (name, peer, half), entry in self.sends.items():
            self.copy(*entry, peer).wait_send()


def project_kernel(
    wide, z_size, x_ref, cos_ref, sin_ref, wkv_ref, wq_ref, wo_ref, grad_ref,
    q_ref, kv_ref, wq_out, wo_out, grad_out,
    wkv_all, wq_all, wo_all, grad_all, keys, own_sem, send_sem, recv_sem, kv_send, kv_recv, out_sem,
):
    place = lax.axis_index("tensor")
    rows = x_ref.shape[0]
    count = keys.shape[0] // rows - 1
    left = pl.ds(0, grad_all.shape[1])
    parts = (
        (wq_ref, wq_all, wq_out), (wo_ref, wo_all, wo_out),
        (grad_ref.at[:, left], grad_all, grad_out.at[:, left]),
    )
    rings = [
        Ring(wide, full, part.shape[0], send_sem.at[at], recv_sem.at[at])
        for at, (part, full, _) in enumerate(parts)
    ]
    local = [
        pltpu.make_async_copy(part, full.at[ring.mine()], own_sem.at[at])
        for at, ((part, full, _), ring) in enumerate(zip(parts, rings))
    ]
    outward = [
        pltpu.make_async_copy(full, out, out_sem.at[at])
        for at, (_, full, out) in enumerate(parts)
    ]
    load = pltpu.make_async_copy(wkv_ref, wkv_all, own_sem.at[len(parts)])
    for copy in local + [load]:
        copy.start()
    keys[: count * rows, :] = jnp.zeros((count * rows, keys.shape[1]), BF16)
    greet([{"dp": peer} for peer in rings[0].peers] + along_peers(place, z_size))
    for copy in local:
        copy.wait()

    def rotated(value):
        return (value * cos_ref[...] + swap_halves(value) * sin_ref[...]).astype(BF16)

    def hop(step):
        return pltpu.make_async_remote_copy(
            src_ref=keys.at[pl.ds((count - step + 1) * rows, rows)],
            dst_ref=keys.at[pl.ds((count - step) * rows, rows)],
            send_sem=kv_send.at[step - 1], recv_sem=kv_recv.at[step - 1],
            device_id={"tensor": (place + 1) % z_size}, device_id_type=MESH,
        )

    def pass_keys(step):
        if step > 1:
            pl.when(place >= step - 1)(lambda: hop(step - 1).wait_recv())
        if step <= count:
            sends = (place + 1 < z_size) & (place >= step - 1)
            pl.when(sends)(lambda: hop(step).start())

    def finish(ring):
        ring.far_halves()
        for name in ("own", "x", "y", "d"):
            ring.from_sibling(name, 0, 1)

    rings[0].start_own()
    load.wait()

    @pl.loop(0, wkv_all.shape[1] // (2 * LANES))
    def _(at):
        n = pl.ds(pl.multiple_of(at * 2 * LANES, LANES), 2 * LANES)
        value = dot_nn(x_ref[...], wkv_all[:, n])
        both = jnp.concatenate([rotated(value[:, :LANES]), value[:, LANES:].astype(BF16)], axis=1)
        keys[pl.ds(count * rows, rows), n] = both

    pass_keys(1)
    rings[0].first_halves()
    rings[0].second_halves()
    rings[1].start_own()
    finish(rings[0])
    outward[0].start()

    @pl.loop(0, wq_all.shape[1] // (2 * LANES))
    def _(at):
        n = pl.ds(pl.multiple_of(at * 2 * LANES, LANES), 2 * LANES)
        value = dot_nn(x_ref[...], wq_all[:, n])
        both = [rotated(value[:, :LANES]), rotated(value[:, LANES:])]
        q_ref[:, n] = jnp.concatenate(both, axis=1)

    for step in range(2, count + 1):
        pass_keys(step)
    rings[1].first_halves()
    rings[1].second_halves()
    rings[2].start_own()
    finish(rings[1])
    outward[1].start()
    rings[2].first_halves()
    rings[2].second_halves()
    finish(rings[2])
    outward[2].start()
    pass_keys(count + 1)
    keys_out = pltpu.make_async_copy(keys, kv_ref, out_sem.at[3])
    keys_out.start()
    for step in range(1, count + 1):
        sends = (place + 1 < z_size) & (place >= step - 1)
        pl.when(sends)(lambda: hop(step).wait_send())
    for ring in rings:
        ring.sent()
    for copy in outward + [keys_out]:
        copy.wait()


def project(x, cosine, sine, wkv, wq, wo, grad, reach, dp_size, z_size):
    rows, width = x.shape
    far = pl.BlockSpec(memory_space=pl.ANY)
    near = pl.BlockSpec(memory_space=pltpu.VMEM)
    whole = [(GROUP * w.shape[0], w.shape[1]) for w in (wq, wo)]
    keys = (reach + rows, wkv.shape[1])
    grads = (GROUP * grad.shape[0], grad.shape[1])
    left = (grads[0], grads[1] // 2)
    return pl.pallas_call(
        functools.partial(project_kernel, 2 * math.isqrt(dp_size // GROUP), z_size),
        in_specs=[near] * 3 + [far] * 4,
        out_specs=[near] + [far] * 4,
        out_shape=[jax.ShapeDtypeStruct((rows, wq.shape[1]), BF16)]
        + [jax.ShapeDtypeStruct(shape, BF16) for shape in [keys] + whole + [grads]],
        scratch_shapes=[pltpu.VMEM(shape, BF16) for shape in [wkv.shape] + whole + [left, keys]]
        + [
            pltpu.SemaphoreType.DMA((4,)),
            pltpu.SemaphoreType.DMA((3, Ring.COPIES)),
            pltpu.SemaphoreType.DMA((3, Ring.COPIES)),
            pltpu.SemaphoreType.DMA((reach // rows,)),
            pltpu.SemaphoreType.DMA((reach // rows,)),
            pltpu.SemaphoreType.DMA((4,)),
        ],
        compiler_params=pltpu.CompilerParams(
            collective_id=3, has_side_effects=True, vmem_limit_bytes=56 << 20
        ),
        cost_estimate=pl.CostEstimate(
            flops=2 * LONG, bytes_accessed=0, transcendentals=0
        ),
    )(x, cosine, sine, wkv, wq, wo, grad)


def gate_up_kernel(
    wide, own_ref, wg_ref, wu_ref, all_ref, gate_ref, up_ref, hid_ref, core_ref,
    full, stage, wg_all, wu_all, own_sem, load_sem, send_sem, recv_sem, out_sem, all_sem,
):
    rows = own_ref.shape[0]
    cols = gate_ref.shape[1]
    ring = Ring(wide, full, rows, send_sem, recv_sem)
    local = pltpu.make_async_copy(own_ref, full.at[ring.mine()], own_sem)
    local.start()
    loads = [
        pltpu.make_async_copy(wg_ref, wg_all, load_sem.at[0]),
        pltpu.make_async_copy(wu_ref, wu_all, load_sem.at[1]),
    ]
    for copy in loads:
        copy.start()
    meet(ring.peers)
    local.wait()
    ring.start_own()
    for copy in loads:
        copy.wait()

    def out_copies(slot, places):
        where, core, chip = places
        return [
            pltpu.make_async_copy(stage.at[slot, i], ref.at[where], out_sem.at[slot, i])
            for i, ref in enumerate((gate_ref, up_ref, hid_ref))
        ] + [
            pltpu.make_async_copy(stage.at[slot, 2], core_ref.at[core, chip], out_sem.at[slot, 3]),
            pltpu.make_async_copy(full.at[where], all_ref.at[where], all_sem.at[slot]),
        ]

    def step_place(step):
        phase, i = step // 4, step % 4
        high, low = phase // 2, phase % 2
        first, last = (1 - high) * (1 - low), high * low
        middle = high + low - 2 * last
        half = (first + last) * (i % 2) + high * (1 - low)
        dx = middle * (1 - i % 2) + last
        dy = middle * (i % 2) + last
        part = rows // 2
        chip_rows = pl.ds(pl.multiple_of((2 * dy + dx) * rows + half * part, part), part)
        return ring.place(dy, dx, i // 2, half), i // 2, chip_rows

    @pl.loop(0, 16)
    def _(step):
        pl.when(step == 2)(lambda: ring.from_sibling("own", 0, 1))
        pl.when(step == 4)(ring.first_halves)

        @pl.when(step == 6)
        def _():
            ring.from_sibling("x", 0)
            ring.from_sibling("y", 0)

        pl.when(step == 8)(ring.second_halves)

        @pl.when(step == 10)
        def _():
            ring.from_sibling("x", 1)
            ring.from_sibling("y", 1)

        pl.when(step == 12)(ring.far_halves)
        pl.when(step == 14)(lambda: ring.from_sibling("d", 0, 1))

        slot = step % 2
        places = step_place(step)

        @pl.when(step >= 2)
        def _():
            for copy in out_copies(slot, step_place(step - 2)):
                copy.wait()

        x = full[places[0], :]

        @pl.loop(0, cols // NTILE)
        def _(at):
            n = pl.ds(pl.multiple_of(at * NTILE, NTILE), NTILE)
            gate = dot_nn(x, wg_all[:, n])
            up = dot_nn(x, wu_all[:, n])
            stage[slot, 0, :, n] = gate.astype(BF16)
            stage[slot, 1, :, n] = up.astype(BF16)
            stage[slot, 2, :, n] = (gate * up / (1.0 + jnp.exp(-gate))).astype(BF16)

        for copy in out_copies(slot, places):
            copy.start()

    for step in (14, 15):
        for copy in out_copies(step % 2, step_place(step)):
            copy.wait()
    ring.sent()


def gate_up(hn, wg, wu, dp_size):
    rows, width = hn.shape
    cols = wg.shape[1]
    tokens = GROUP * rows
    far = pl.BlockSpec(memory_space=pl.ANY)
    return pl.pallas_call(
        functools.partial(gate_up_kernel, 2 * math.isqrt(dp_size // GROUP)),
        in_specs=[far] * 3,
        out_specs=[far] * 5,
        out_shape=[jax.ShapeDtypeStruct((tokens, width), BF16)]
        + [jax.ShapeDtypeStruct((tokens, cols), BF16)] * 3
        + [jax.ShapeDtypeStruct((2, tokens // 2, cols), BF16)],
        scratch_shapes=[
            pltpu.VMEM((tokens, width), BF16),
            pltpu.VMEM((2, 3, rows // 2, cols), BF16),
            pltpu.VMEM(wg.shape, BF16),
            pltpu.VMEM(wu.shape, BF16),
            pltpu.SemaphoreType.DMA,
            pltpu.SemaphoreType.DMA((2,)),
            pltpu.SemaphoreType.DMA((Ring.COPIES,)),
            pltpu.SemaphoreType.DMA((Ring.COPIES,)),
            pltpu.SemaphoreType.DMA((2, 4)),
            pltpu.SemaphoreType.DMA((2,)),
        ],
        compiler_params=pltpu.CompilerParams(
            collective_id=1, has_side_effects=True, vmem_limit_bytes=56 << 20
        ),
        cost_estimate=pl.CostEstimate(
            flops=SHORT, bytes_accessed=0, transcendentals=0
        ),
    )(hn, wg, wu)


FAR_CHUNK, X_CHUNK, Y_CHUNK, OWN_CHUNK = range(4)


class Reduce:
    COPIES = 10

    def __init__(self, wide, parts, cores, far, near, send_sem, recv_sem):
        self.at, self.peers = neighbours(wide)
        self.parts, self.cores, self.far, self.near = parts, cores, far, near
        self.send_sem, self.recv_sem = send_sem, recv_sem
        self.half = parts.shape[2] // 2

    @staticmethod
    def scratch(rows, cols):
        return [
            pltpu.VMEM((2, 4, rows, cols), BF16),
            pltpu.VMEM((4, rows, cols), BF16),
            pltpu.VMEM((2, rows // 2, cols), BF16),
            pltpu.VMEM((2, rows, cols), BF16),
            pltpu.SemaphoreType.DMA((Reduce.COPIES,)),
            pltpu.SemaphoreType.DMA((Reduce.COPIES,)),
        ]

    def chunk(self, step):
        slot, other = step // 2, 1 - step % 2
        row, col, core = self.at
        dy, dx = 1 - slot % 2, 1 - slot // 2
        place = 4 * ((row + dy) % 2) + 2 * ((col + dx) % 2) + (core + other) % 2
        return place, self.parts.at[other, slot]

    def copy(self, name):
        upper, lower = pl.ds(0, self.half), pl.ds(self.half, self.half)
        mine = self.parts.at[0]
        table = {
            "far0": (self.parts.at[1, FAR_CHUNK], self.cores.at[FAR_CHUNK], SIB),
            "x": (self.parts.at[1, X_CHUNK], self.cores.at[X_CHUNK], SIB),
            "y": (self.parts.at[1, Y_CHUNK], self.cores.at[Y_CHUNK], SIB),
            "own": (self.parts.at[1, OWN_CHUNK], self.cores.at[OWN_CHUNK], SIB),
            "far_x": (mine.at[FAR_CHUNK, lower], self.far.at[0], XN),
            "far_y": (mine.at[FAR_CHUNK, upper], self.far.at[1], YN),
            "x_upper": (mine.at[X_CHUNK, upper], self.near.at[0, upper], XN),
            "x_lower": (mine.at[X_CHUNK, lower], self.near.at[0, lower], XN),
            "y_upper": (mine.at[Y_CHUNK, upper], self.near.at[1, upper], YN),
            "y_lower": (mine.at[Y_CHUNK, lower], self.near.at[1, lower], YN),
        }
        src, dst, peer = table[name]
        at = list(table).index(name)
        return pltpu.make_async_remote_copy(
            src_ref=src, dst_ref=dst, send_sem=self.send_sem.at[at],
            recv_sem=self.recv_sem.at[at], device_id={"dp": self.peers[peer]},
            device_id_type=MESH,
        )

    def start(self, *names):
        for name in names:
            self.copy(name).start()

    def add(self, slot, start, other):
        count = other.shape[0] // STRIP

        @pl.loop(0, count)
        def _(at):
            here = pl.ds(pl.multiple_of(start + at * STRIP, STRIP), STRIP)
            there = pl.ds(pl.multiple_of(at * STRIP, STRIP), STRIP)
            value = self.parts[0, slot, here, :].astype(F32) + other[there, :].astype(F32)
            self.parts[0, slot, here, :] = value.astype(BF16)

    def merge_core(self, slot, name):
        self.copy(name).wait_recv()
        self.add(slot, 0, self.cores.at[slot])

    def after(self, step):
        names = ("far0", "x", "y", "own")
        for slot in range(4):
            pl.when(step == 2 * slot)(functools.partial(self.start, names[slot]))

        @pl.when(step == 1)
        def _():
            self.merge_core(FAR_CHUNK, "far0")
            self.start("far_x", "far_y")

        @pl.when(step == 3)
        def _():
            self.merge_core(X_CHUNK, "x")
            self.start("x_lower")

        @pl.when(step == 5)
        def _():
            self.merge_core(Y_CHUNK, "y")
            self.start("y_upper")

    def pass_on(self):
        self.copy("far_y").wait_recv()
        self.add(X_CHUNK, 0, self.far.at[1])
        self.start("x_upper")
        self.copy("far_x").wait_recv()
        self.add(Y_CHUNK, self.half, self.far.at[0])
        self.start("y_lower")

    def finish(self, store):
        for name in ("own", "x_upper", "x_lower", "y_upper", "y_lower"):
            self.copy(name).wait_recv()

        @pl.loop(0, 2 * self.half // STRIP)
        def _(at):
            here = pl.ds(pl.multiple_of(at * STRIP, STRIP), STRIP)
            value = self.parts[0, OWN_CHUNK, here, :].astype(F32)
            value += self.cores[OWN_CHUNK, here, :].astype(F32)
            value += self.near[0, here, :].astype(F32)
            value += self.near[1, here, :].astype(F32)
            store(here, value)

    def sent(self):
        for name in (
            "far0", "x", "y", "own", "far_x", "far_y", "x_upper", "x_lower", "y_upper", "y_lower",
        ):
            self.copy(name).wait_send()


def hidden_back_kernel(
    wide, gain_ref, h_ref, grad_ref, dgate_ref, dup_ref, wg_ref, wu_ref,
    low_ref, gain_out,
    loaded, wg_all, wu_all, h_all, grad_all, load_sem, own_sem, *scratch,
):
    ring = Reduce(wide, *scratch)
    rows = low_ref.shape[0]

    def loads(step):
        chunk, _ = ring.chunk(step)
        here = pl.ds(pl.multiple_of(chunk * rows, rows), rows)
        return [
            pltpu.make_async_copy(
                ref.at[here], loaded.at[step % 2, at], load_sem.at[step % 2, at]
            )
            for at, ref in enumerate((dgate_ref, dup_ref))
        ]

    pairs = ((wg_ref, wg_all), (wu_ref, wu_all), (h_ref, h_all), (grad_ref, grad_all))
    whole = [
        pltpu.make_async_copy(src, dst, own_sem.at[at]) for at, (src, dst) in enumerate(pairs)
    ]
    for copy in loads(0) + whole:
        copy.start()
    meet(ring.peers)
    for copy in whole[:2]:
        copy.wait()

    @pl.loop(0, 8)
    def _(step):
        @pl.when(step < 7)
        def _():
            for copy in loads(step + 1):
                copy.start()

        for copy in loads(step):
            copy.wait()
        _, target = ring.chunk(step)
        dgate, dup = loaded[step % 2, 0], loaded[step % 2, 1]

        @pl.loop(0, low_ref.shape[1] // NTILE)
        def _(at):
            n = pl.ds(pl.multiple_of(at * NTILE, NTILE), NTILE)
            value = dot_nt(dgate, wg_all[n, :]) + dot_nt(dup, wu_all[n, :])
            target[:, n] = value.astype(BF16)

        ring.after(step)

    ring.pass_on()
    for copy in whole[2:]:
        copy.wait()
    gain_out[...] = jnp.zeros_like(gain_out)

    def store(here, value):
        h = h_all[here, :]
        scale = rms_scale(h)
        gained = value * gain_ref[...]
        inner = jnp.mean(gained * h, axis=1, keepdims=True)
        gain_out[...] += value * h * scale
        total = grad_all[here, :].astype(F32) + scale * gained
        total -= h * (scale * scale * scale * inner)
        low_ref[here, :] = total.astype(BF16)

    ring.finish(store)
    ring.sent()


def hidden_back(gain, h, grad, dgate, dup, wg, wu, dp_size):
    tokens, cols = dgate.shape
    rows, width = h.shape
    far = pl.BlockSpec(memory_space=pl.ANY)
    near = pl.BlockSpec(memory_space=pltpu.VMEM)
    return pl.pallas_call(
        functools.partial(hidden_back_kernel, 2 * math.isqrt(dp_size // GROUP)),
        in_specs=[near] + [far] * 6,
        out_specs=[near] * 2,
        out_shape=[
            jax.ShapeDtypeStruct((rows, width), BF16),
            jax.ShapeDtypeStruct((STRIP, width), F32),
        ],
        scratch_shapes=[
            pltpu.VMEM((2, 2, rows, cols), BF16),
            pltpu.VMEM(wg.shape, BF16),
            pltpu.VMEM(wu.shape, BF16),
            pltpu.VMEM(h.shape, F32),
            pltpu.VMEM(grad.shape, BF16),
            pltpu.SemaphoreType.DMA((2, 2)),
            pltpu.SemaphoreType.DMA((4,)),
        ]
        + Reduce.scratch(rows, width),
        compiler_params=pltpu.CompilerParams(
            collective_id=6, has_side_effects=True, vmem_limit_bytes=62 << 20
        ),
        cost_estimate=pl.CostEstimate(
            flops=2 * LONG, bytes_accessed=4 * rows * width, transcendentals=0
        ),
    )(gain, h, grad, dgate, dup, wg, wu)


def tail_kernel(
    wide, z_size, mlp_count, x_ref, dq_ref, dkv_ref, wo_ref, gain_ref,
    raw_ref, dh_ref, wq_ref, wkv_ref, *refs
):
    mlp_ins, refs = refs[:mlp_count], refs[mlp_count:]
    wq_out, wkv_out, wo_out, gain_out, grad_out = refs[:5]
    mlp_outs, scratch = refs[5 : 5 + mlp_count], refs[5 + mlp_count :]
    sub = wkv_out.shape[1]
    halves = wq_out.shape[1] // sub
    count = halves + 1
    rings = [Reduce(wide, *scratch[6 * at : 6 * at + 6]) for at in range(count)]
    sums, zrecv, gain_z, gain_p, z_send, z_recv, g_send, g_recv = scratch[6 * count : 6 * count + 8]
    wo_recv, w_send, w_recv = scratch[6 * count + 8 : 6 * count + 11]
    wq_all, wkv_all, raw, dh, dxn, gain_sum, load_sem = scratch[6 * count + 11 : 6 * count + 18]
    mlp_copies = send_home(wide, mlp_ins, mlp_outs, *scratch[6 * count + 18 :])
    place = lax.axis_index("tensor")
    mine, found = others(wide)
    along = along_peers(place, z_size)
    around = [device for _, device in found]

    tiles, tile_rows = raw.shape[0], raw.shape[1]
    loads = [
        pltpu.make_async_copy(wq_ref, wq_all, load_sem.at[0]),
        pltpu.make_async_copy(wkv_ref, wkv_all, load_sem.at[1]),
    ]
    for tile in range(tiles):
        here = pl.ds(tile * tile_rows, tile_rows)
        loads += [
            pltpu.make_async_copy(raw_ref.at[here], raw.at[tile], load_sem.at[2 + 2 * tile]),
            pltpu.make_async_copy(dh_ref.at[here], dh.at[tile], load_sem.at[3 + 2 * tile]),
        ]
    for copy in loads:
        copy.start()
    greet(along + around)

    wo_part = wo_out.shape[1]
    wo_copies = [
        pltpu.make_async_remote_copy(
            src_ref=wo_ref.at[
                :,
                pl.ds(pl.multiple_of((place + at + 1) % z_size * wo_part, LANES), wo_part),
            ],
            dst_ref=wo_recv.at[at], send_sem=w_send.at[at], recv_sem=w_recv.at[at],
            device_id=peer, device_id_type=MESH,
        )
        for at, peer in enumerate(along)
    ]
    for copy in wo_copies:
        copy.start()

    pieces = [(dq_ref, wq_out, at * sub) for at in range(halves)] + [(dkv_ref, wkv_out, 0)]
    rows = sums.shape[1]
    z_copies = []

    def partial_sums(index):
        ring = rings[index]
        right, out, offset = pieces[index]

        @pl.loop(0, 8)
        def _(step):
            chunk, target = ring.chunk(step)
            x = x_ref[:, pl.ds(pl.multiple_of(chunk * rows, rows), rows)].T

            @pl.loop(0, z_size)
            def _(at):
                n = pl.ds(pl.multiple_of(at * sub, LANES), sub)
                source = pl.ds(pl.multiple_of(at * out.shape[1] + offset, LANES), sub)
                target[:, n] = dot_nn(x, right[:, source]).astype(BF16)

            ring.after(step)

    gain_sum[...] = jnp.zeros_like(gain_sum)

    def input_rows(tile):
        part = pl.ds(tile * tile_rows, tile_rows)
        dq, dkv = dq_ref[part, :], dkv_ref[part, :]

        @pl.loop(0, dxn.shape[1] // NTILE)
        def _(at):
            n = pl.ds(pl.multiple_of(at * NTILE, NTILE), NTILE)
            dxn[:, n] = dot_nt(dq, wq_all[n, :]) + dot_nt(dkv, wkv_all[n, :])

        @pl.loop(0, tile_rows // STRIP)
        def _(at):
            here = pl.ds(pl.multiple_of(at * STRIP, STRIP), STRIP)
            there = pl.ds(pl.multiple_of(tile * tile_rows + at * STRIP, STRIP), STRIP)
            grad, value = dxn[here, :], raw[tile, here, :].astype(F32)
            scale = rms_scale(value)
            gained = grad * gain_ref[0:1, :]
            inner = jnp.mean(gained * value, axis=1, keepdims=True)
            gain_sum[...] += grad * value * scale
            total = scale * gained - value * (scale * scale * scale * inner)
            grad_out[there, :] = (dh[tile, here, :].astype(F32) + total).astype(BF16)

    def send_along(index):
        def store(here, value):
            sums[index, here, :] = value.astype(BF16)

        rings[index].finish(store)
        for at, peer in enumerate(along):
            other = (place + at + 1) % z_size
            copy = pltpu.make_async_remote_copy(
                src_ref=sums.at[index, :, pl.ds(pl.multiple_of(other * sub, LANES), sub)],
                dst_ref=zrecv.at[index, at],
                send_sem=z_send.at[index, at], recv_sem=z_recv.at[index, at],
                device_id=peer, device_id_type=MESH,
            )
            z_copies.append(copy)
            copy.start()

    partial_sums(0)
    for copy in loads:
        copy.wait()
    input_rows(0)
    rings[0].pass_on()
    for index in range(1, count):
        partial_sums(index)
        if index < tiles:
            input_rows(index)
        if index + 1 < count:
            rings[index].pass_on()
            send_along(index - 1)
    for tile in range(count, tiles):
        input_rows(tile)

    gain_z[place, 0:1] = jnp.sum(gain_sum[...], axis=0, keepdims=True)
    gain_z[place, 1:2] = gain_ref[1:2, :]
    gain_copies = [
        pltpu.make_async_remote_copy(
            src_ref=gain_z.at[place], dst_ref=gain_z.at[place], send_sem=g_send.at[at],
            recv_sem=g_recv.at[at], device_id=peer, device_id_type=MESH,
        )
        for at, peer in enumerate(along)
    ]
    for copy in gain_copies:
        copy.start()
    rings[count - 1].pass_on()
    for copy in mlp_copies:
        copy.start()
    send_along(count - 2)

    for copy in gain_copies:
        copy.wait_recv()
    total = gain_z[0]
    for at in range(1, z_size):
        total = total + gain_z[at]
    gain_p[mine] = total
    for at, peer in enumerate(around):
        copy = pltpu.make_async_remote_copy(
            src_ref=gain_p.at[mine], dst_ref=gain_p.at[mine],
            send_sem=g_send.at[z_size - 1 + at], recv_sem=g_recv.at[z_size - 1 + at],
            device_id=peer, device_id_type=MESH,
        )
        gain_copies.append(copy)
        copy.start()
    for copy in wo_copies:
        copy.wait()
    total = wo_ref[:, pl.ds(pl.multiple_of(place * wo_part, LANES), wo_part)].astype(F32)
    for at in range(z_size - 1):
        total += wo_recv[at].astype(F32)
    wo_out[...] = total
    send_along(count - 1)

    for copy in gain_copies[z_size - 1 :]:
        copy.wait_recv()
    total = gain_p[0]
    for at in range(1, GROUP):
        total = total + gain_p[at]
    gain_out[...] = total
    for copy in z_copies:
        copy.wait_recv()
    for index, (_, out, offset) in enumerate(pieces):
        value = sums[index, :, pl.ds(pl.multiple_of(place * sub, LANES), sub)].astype(F32)
        for at in range(z_size - 1):
            value += zrecv[index, at].astype(F32)
        out[:, offset : offset + sub] = value
    for copy in z_copies + gain_copies:
        copy.wait_send()
    for ring in rings:
        ring.sent()
    for copy in mlp_copies:
        copy.wait()


def last_grads(x, dq, dkv, wo_sum, gains, raw, dh, wq, wkv, mlp, dp_size, z_size):
    tokens, width = x.shape
    rows = width // GROUP
    tiles = tokens // QTILE
    near = pl.BlockSpec(memory_space=pltpu.VMEM)
    far = pl.BlockSpec(memory_space=pl.ANY)
    sizes = [dq.shape[1], dkv.shape[1]]
    cols = dkv.shape[1]
    count = sum(sizes) // cols
    scratch = []
    for _ in range(count):
        scratch += Reduce.scratch(rows, cols)
    return pl.pallas_call(
        functools.partial(tail_kernel, 2 * math.isqrt(dp_size // GROUP), z_size, len(mlp)),
        in_specs=[near] * 5 + [far] * (4 + len(mlp)),
        out_specs=[near] * 5 + [far] * len(mlp),
        out_shape=[jax.ShapeDtypeStruct((rows, size // z_size), F32) for size in sizes]
        + [
            jax.ShapeDtypeStruct((rows, wo_sum.shape[1] // z_size), F32),
            jax.ShapeDtypeStruct(gains.shape, F32),
            jax.ShapeDtypeStruct((tokens, width), BF16),
        ]
        + home_shapes(mlp),
        scratch_shapes=scratch
        + [
            pltpu.VMEM((count, rows, cols), BF16),
            pltpu.VMEM((count, z_size - 1, rows, cols // z_size), BF16),
            pltpu.VMEM((z_size, *gains.shape), F32),
            pltpu.VMEM((GROUP, *gains.shape), F32),
            pltpu.SemaphoreType.DMA((count, z_size - 1)),
            pltpu.SemaphoreType.DMA((count, z_size - 1)),
            pltpu.SemaphoreType.DMA((z_size - 1 + GROUP - 1,)),
            pltpu.SemaphoreType.DMA((z_size - 1 + GROUP - 1,)),
            pltpu.VMEM((z_size - 1, rows, wo_sum.shape[1] // z_size), BF16),
            pltpu.SemaphoreType.DMA((z_size - 1,)),
            pltpu.SemaphoreType.DMA((z_size - 1,)),
            pltpu.VMEM(wq.shape, BF16),
            pltpu.VMEM(wkv.shape, BF16),
            pltpu.VMEM((tiles, QTILE, width), BF16),
            pltpu.VMEM((tiles, QTILE, width), BF16),
            pltpu.VMEM((QTILE, width), F32),
            pltpu.VMEM((STRIP, width), F32),
            pltpu.SemaphoreType.DMA((2 + 2 * tiles,)),
        ]
        + home_scratch(mlp),
        compiler_params=pltpu.CompilerParams(
            collective_id=4, has_side_effects=True, vmem_limit_bytes=62 << 20
        ),
        cost_estimate=pl.CostEstimate(flops=SHORT, bytes_accessed=0, transcendentals=0),
    )(x, dq, dkv, wo_sum, gains, raw, dh, wq, wkv, *mlp)


class Layout:
    def __init__(self, dp_size):
        self.blocks = dp_size // GROUP
        side = math.isqrt(self.blocks)
        self.rows, self.cols = side, self.blocks // side
        wide = 2 * self.cols

        def index(by, bx, y, x, core):
            return ((2 * by + y) * wide + 2 * bx + x) * 2 + core

        places = [(y, x, c) for y in range(2) for x in range(2) for c in range(2)]
        spots = [(by, bx) for by in range(self.rows) for bx in range(self.cols)]
        self.inner = [[index(*s, *p) for p in places] for s in spots]
        self.outer = [[index(*s, *p) for s in spots] for p in places]

    def groups(self):
        return None if self.blocks == 1 else self.inner

    def to_rows(self, array):
        if self.blocks == 1:
            return array
        rest = array.shape[1:]
        split = array.reshape(2, 2, 2, self.rows, self.cols, -1, *rest)
        order = (3, 0, 4, 1, 2, 5) + tuple(range(6, 6 + len(rest)))
        return split.transpose(order).reshape(array.shape)

    def from_rows(self, array):
        if self.blocks == 1:
            return array
        rest = array.shape[1:]
        split = array.reshape(self.rows, 2, self.cols, 2, 2, -1, *rest)
        order = (1, 3, 4, 0, 2, 5) + tuple(range(6, 6 + len(rest)))
        return split.transpose(order).reshape(array.shape)

    def from_cols(self, array):
        return array if self.blocks == 1 else self.from_rows(array.T).T

    def gather_outer(self, array):
        if self.blocks == 1:
            return array
        return lax.all_gather(array, "dp", axis_index_groups=self.outer, axis=0, tiled=True)

    def scatter_outer(self, array):
        if self.blocks == 1:
            return array
        return lax.psum_scatter(
            array, "dp", scatter_dimension=0, axis_index_groups=self.outer, tiled=True
        )

    def swap(self, array, flip):
        pairs = [
            (block[at], block[at ^ flip]) for block in self.inner for at in range(GROUP)
        ]
        return lax.ppermute(array, "dp", pairs)

    def sum_outer(self, array):
        if self.blocks == 1:
            return array
        return lax.psum(array, "dp", axis_index_groups=self.outer)

    def gather(self, array):
        return lax.all_gather(array, "dp", axis_index_groups=self.groups(), axis=0, tiled=True)

    def scatter(self, array):
        return lax.psum_scatter(
            array, "dp", scatter_dimension=0, axis_index_groups=self.groups(), tiled=True
        )


def rms_scale(values):
    return lax.rsqrt(jnp.mean(values * values, axis=-1, keepdims=True) + NORM_EPS)


def per_device(
    dp_size, z_size, activations, segment_ids, attn_gain, w_query, w_key, w_value, w_out,
    mlp_gain, w_gate, w_up, w_down, cotangent,
):
    layout = Layout(dp_size)
    rows, width = activations.shape[1:]
    x = activations[0].astype(F32)
    place = lax.axis_index("tensor")
    reach = -(-(MOST_DOC - 1) // rows) * rows

    def shift(array, step):
        pairs = [(at, at + step) for at in range(z_size) if 0 <= at + step < z_size]
        return lax.ppermute(array, "tensor", pairs)

    starts = document_starts(segment_ids[0])
    own_starts = lax.dynamic_slice_in_dim(starts, place * rows, rows)
    own_tokens = place * rows + jnp.arange(rows, dtype=jnp.int32)
    cosine, sine = rope_tables(own_tokens - own_starts)
    low = (own_starts - place * rows + reach)[None, :]

    shards = [
        layout.gather_outer(w)
        for w in (w_gate, w_up, w_down, jnp.concatenate([w_key, w_value], axis=1), w_query, w_out)
    ]
    xn, *spread = spread_weights(
        activations[0], attn_gain[None], shards[:3], shards[3:], dp_size, z_size
    )
    def gather_z(array):
        return layout.to_rows(lax.all_gather(array, "tensor", axis=1, tiled=True))

    wg, wu = gather_z(spread[0]), gather_z(spread[1])

    def along_z(total):
        return lax.psum_scatter(
            layout.from_rows(total), "tensor", scatter_dimension=1, tiled=True
        )

    q, kv_all, wq, wo, dy = project(
        layout.from_cols(xn), cosine, sine, *spread[3:], cotangent[0], reach, dp_size, z_size
    )
    wd = gather_z(spread[2])
    wkv, wq, wo = (layout.to_rows(w) for w in (spread[3], wq, wo))
    att, lse, dy = attend(q, kv_all, low, cotangent[0], dy, dp_size)
    h = x + dot_nt(att, wo)

    r2 = rms_scale(h)
    hn, gate, up, hidden, by_core = gate_up((h * r2 * mlp_gain).astype(BF16), wg, wu, dp_size)
    part = rows // 2
    away = dot_nt(by_core[1], wd).astype(BF16)
    dy, away = lax.optimization_barrier((dy, away))
    total_wd = dot_tn(dy, hidden).astype(BF16)
    part_wd = along_z(total_wd)
    from_core = layout.swap(away, 1)

    near = (dot_nt(by_core[0], wd) + from_core.astype(F32)).astype(BF16)
    dy, near = lax.optimization_barrier((dy, near))

    def out_rows(start, count):
        return near[start * part : (start + count) * part]

    def joined(some, other):
        return (some.astype(F32) + other.astype(F32)).astype(BF16)

    far_y, far_x, x_lower, y_upper = (out_rows(at, 1) for at in (6, 7, 3, 4))
    dy, far_x, far_y, x_lower, y_upper = lax.optimization_barrier(
        (dy, far_x, far_y, x_lower, y_upper)
    )
    from_x, from_y = layout.swap(far_x, 2), layout.swap(far_y, 4)
    x_lower, y_upper = layout.swap(x_lower, 2), layout.swap(y_upper, 4)
    gate, up = gate.astype(F32), up.astype(F32)
    sigma = jax.nn.sigmoid(gate)
    dhid = dot_nn(dy, wd)
    dgate = (dhid * up * sigma * (1.0 + gate * (1.0 - sigma))).astype(BF16)
    dup = (dhid * gate * sigma).astype(BF16)
    dgate, dup, from_x, from_y = lax.optimization_barrier((dgate, dup, from_x, from_y))
    x_upper, y_lower = joined(out_rows(2, 1), from_y), joined(out_rows(5, 1), from_x)
    dgate, dup, x_upper, y_lower = lax.optimization_barrier((dgate, dup, x_upper, y_lower))
    x_upper, y_lower = layout.swap(x_upper, 2), layout.swap(y_lower, 4)
    total_wg = dot_tn(hn, dgate).astype(BF16)
    dup, total_wg, x_lower, y_upper = lax.optimization_barrier((dup, total_wg, x_lower, y_upper))
    part_wg = along_z(total_wg)
    total_wu = dot_tn(hn, dup).astype(BF16)
    dup, total_wu = lax.optimization_barrier((dup, total_wu))
    part_wu = along_z(total_wu)
    dup, x_upper, y_lower = lax.optimization_barrier((dup, x_upper, y_lower))
    dhb, gain_two = hidden_back(
        mlp_gain[None], h, cotangent[0], dgate, dup, wg, wu, dp_size
    )
    gain_two = jnp.sum(gain_two, axis=0)
    dhb, part_wd = lax.optimization_barrier((dhb, part_wd))
    datt = dot_nn(dhb, wo).astype(BF16)
    total_wo = layout.from_rows(dot_tn(dhb, att).astype(BF16))
    datt, part_wg, total_wo = lax.optimization_barrier((datt, part_wg, total_wo))
    part_wo = layout.scatter(total_wo)
    dq, dkv, wd_grad, wg_grad = attend_back(
        q, datt, att, kv_all, lse, low, cosine, sine, (part_wd, part_wg), dp_size, z_size
    )
    dq, part_wu = lax.optimization_barrier((dq, part_wu))
    dq, part_wo = lax.optimization_barrier((dq, part_wo))
    wq_grad, wkv_grad, wo_grad, gains, input_grad, wu_grad = last_grads(
        layout.from_cols(xn), dq, dkv, part_wo, jnp.stack([attn_gain, gain_two]),
        activations[0], dhb, wq, wkv, (part_wu,), dp_size, z_size,
    )
    gains = layout.sum_outer(gains)
    output = h + out_rows(0, 2).astype(F32)
    output = output + jnp.concatenate([x_upper, x_lower]).astype(F32)
    output = output + jnp.concatenate([y_upper, y_lower]).astype(F32)
    wo_grad, wq_grad, wkv_grad, wd_grad, wg_grad, wu_grad = (
        layout.scatter_outer(grad).astype(F32)
        for grad in (wo_grad, wq_grad, wkv_grad, wd_grad, wg_grad, wu_grad)
    )
    key_cols = w_key.shape[1]
    return (
        output.astype(BF16)[None],
        input_grad[None],
        gains[0],
        wq_grad,
        wkv_grad[:, :key_cols],
        wkv_grad[:, key_cols:],
        wo_grad,
        gains[1],
        wg_grad,
        wu_grad,
        wd_grad,
    )


def solution(mesh):
    split = P("dp", "tensor")
    tokens = P("dp", "tensor", None)
    in_specs = (
        tokens, P("dp", None), P(), split, split, split, split, P(), split, split, split, tokens,
    )
    out_specs = (tokens, tokens, P(), split, split, split, split, P(), split, split, split)
    return jax.shard_map(
        functools.partial(per_device, mesh.shape["dp"], mesh.shape["tensor"]),
        mesh=mesh, in_specs=in_specs, out_specs=out_specs, check_vma=False,
    )
```

```python
import functools
import math

import jax
import jax.numpy as jnp
from jax import lax
from jax.experimental import pallas as pl
from jax.experimental.pallas import tpu as pltpu
from jax.sharding import PartitionSpec as P

HEAD_DIM = 64
DOCS = 4
MOST_DOC = 1024
NORM_EPS = 1e-05
ROPE_THETA = 500000.0
GROUP = 8
LANES = 128
QTILE = 256
SCALE = HEAD_DIM ** (-0.5)
LOG2E = 1.4426950408889634
FAR = -1e30
NTILE = 512
STRIP = 16
LONG = 60_000_000_000
SHORT = 1_000_000

F32 = jnp.float32
BF16 = jnp.bfloat16


def dot_nn(left, right):
    return lax.dot_general(left, right, (((1,), (0,)), ((), ())), preferred_element_type=F32)


def dot_nt(left, right):
    return lax.dot_general(left, right, (((1,), (1,)), ((), ())), preferred_element_type=F32)


def dot_tn(left, right):
    return lax.dot_general(left, right, (((0,), (0,)), ((), ())), preferred_element_type=F32)


def document_starts(segments):
    doc_ids = jnp.arange(DOCS, dtype=jnp.int32)
    counts = jnp.sum((segments[:, None] == doc_ids).astype(jnp.int32), axis=0)
    before = (doc_ids < segments[:, None]).astype(jnp.int32)
    return jnp.sum(before * counts[None, :], axis=-1)


def rope_tables(positions):
    half = HEAD_DIM // 2
    frequency = jnp.exp(
        jnp.arange(half, dtype=F32) * (-2.0 * math.log(ROPE_THETA) / HEAD_DIM)
    )
    angles = positions.astype(F32)[:, None] * frequency
    cosine, sine = jnp.cos(angles), jnp.sin(angles)
    wide_cos = jnp.concatenate([cosine] * 4, axis=1)
    wide_sin = jnp.concatenate([-sine, sine, -sine, sine], axis=1)
    return wide_cos, wide_sin


def swap_halves(values):
    lane = lax.broadcasted_iota(jnp.int32, values.shape, 1)
    ahead = pltpu.roll(values, LANES - 32, 1)
    behind = pltpu.roll(values, 32, 1)
    return jnp.where((lane % 64) < 32, ahead, behind)


def fill_bias(bias_ref, low_ref, reach):
    span = bias_ref.shape[1]
    for tile in range(bias_ref.shape[0]):
        row = lax.broadcasted_iota(jnp.int32, (span, QTILE), 0)
        col = lax.broadcasted_iota(jnp.int32, (span, QTILE), 1)
        low = low_ref[0:1, tile * QTILE : (tile + 1) * QTILE]
        allowed = (row <= reach + col) & (row + tile * QTILE >= low)
        bias_ref[tile] = jnp.where(allowed, 0.0, FAR)


def spread_pair(pair, half):
    wide = pair.astype(F32)
    turned = pltpu.roll(wide, 64, 1)
    lane = lax.broadcasted_iota(jnp.int32, wide.shape, 1)
    mine = (lane // 64) == half
    even = half == 0
    first = jnp.where(mine, jnp.where(even, wide, turned), 0.0)
    second = jnp.where(mine, jnp.where(even, turned, wide), 0.0)
    return jnp.concatenate([first, second], axis=0).astype(BF16)


def gather_pair(transposed, half):
    count = transposed.shape[1] // 2
    mine = jnp.where(half == 0, transposed[:64], transposed[64:])
    return jnp.concatenate([mine[:, :count], mine[:, count:]], axis=0).T


def attend_kernel(
    reach, wide, q_ref, k_ref, v_ref, low_ref, own_ref, _, att_ref, lse_ref, all_ref,
    bias_ref, full, own_sem, send_sem, recv_sem, out_sem,
):
    head, tile, pair = pl.program_id(0), pl.program_id(1), pl.program_id(2)
    half = head % 2
    inner = pl.num_programs(1) * pl.num_programs(2)
    step = head * inner + tile * pl.num_programs(2) + pair
    ring = Ring(wide, full, own_ref.shape[0], send_sem, recv_sem)
    right = pl.ds(own_ref.shape[1] - full.shape[1], full.shape[1])

    def outward(slot, *flips):
        where = ring.whole(*flips)
        return pltpu.make_async_copy(full.at[where], all_ref.at[where, right], out_sem.at[slot])

    near = [(0, 0, 0), (0, 0, 1), (0, 1, 0), (1, 0, 0)]
    rest = [(0, 1, 1), (1, 0, 1), (1, 1, 0), (1, 1, 1)]

    @pl.when(step == 0)
    def _():
        local = pltpu.make_async_copy(own_ref.at[:, right], full.at[ring.mine()], own_sem)
        local.start()
        meet(ring.peers)
        local.wait()
        ring.start_own()
        fill_bias(bias_ref, low_ref, reach)

    pl.when(step == 2 * inner)(ring.first_halves)
    pl.when(step == 4 * inner)(ring.second_halves)

    keys = pl.ds(pl.multiple_of(tile * QTILE, QTILE), bias_ref.shape[1])
    queries = spread_pair(q_ref[...], half)
    bias = bias_ref[tile]
    score = dot_nt(k_ref[keys, :], queries)
    score = score + jnp.concatenate([bias, bias], axis=1)
    top = jnp.max(score, axis=0, keepdims=True) * (SCALE * LOG2E)
    weight = jnp.exp2(score * (SCALE * LOG2E) - top)
    total = jnp.sum(weight, axis=0, keepdims=True)
    result = dot_tn(v_ref[keys, :], weight.astype(BF16)) / total
    att_ref[...] = gather_pair(result, half).astype(BF16)
    lse_ref[0] = top + jnp.log2(total)

    @pl.when(step == pl.num_programs(0) * inner - 1)
    def _():
        ring.from_sibling("own", 0, 1)
        for slot, flips in enumerate(near):
            outward(slot, *flips).start()
        ring.far_halves()
        for name in ("x", "y", "d"):
            ring.from_sibling(name, 0, 1)
        for slot, flips in enumerate(rest):
            outward(4 + slot, *flips).start()
        for slot, flips in enumerate(near + rest):
            outward(slot, *flips).wait()
        ring.sent()


def attend(q, kv, low, grad, grads, dp_size):
    rows, width = q.shape
    keys = kv.shape[0]
    reach = keys - rows
    tiles = rows // QTILE
    pairs = width // LANES
    heads = kv.shape[1] // LANES
    per_head = pairs // heads
    span = reach + QTILE
    right = (grads.shape[0], grads.shape[1] // 2)
    far = pl.BlockSpec(memory_space=pl.ANY)
    return pl.pallas_call(
        functools.partial(attend_kernel, reach, 2 * math.isqrt(dp_size // GROUP)),
        grid=(heads, tiles, per_head),
        in_specs=[
            pl.BlockSpec((QTILE, LANES), lambda a, t, p: (t, a * per_head + p)),
            pl.BlockSpec((keys, LANES), lambda a, t, p: (0, 2 * (a // 2))),
            pl.BlockSpec((keys, LANES), lambda a, t, p: (0, 2 * (a // 2) + 1)),
            pl.BlockSpec((1, rows), lambda a, t, p: (0, 0)),
            far,
            far,
        ],
        out_specs=[
            pl.BlockSpec((QTILE, LANES), lambda a, t, p: (t, a * per_head + p)),
            pl.BlockSpec((1, 1, 2 * QTILE), lambda a, t, p: ((a * tiles + t) * per_head + p, 0, 0)),
            far,
        ],
        out_shape=[
            jax.ShapeDtypeStruct((rows, width), BF16),
            jax.ShapeDtypeStruct((pairs * tiles, 1, 2 * QTILE), F32),
            jax.ShapeDtypeStruct(grads.shape, BF16),
        ],
        scratch_shapes=[
            pltpu.VMEM((tiles, span, QTILE), F32),
            pltpu.VMEM(right, BF16),
            pltpu.SemaphoreType.DMA,
            pltpu.SemaphoreType.DMA((Ring.COPIES,)),
            pltpu.SemaphoreType.DMA((Ring.COPIES,)),
            pltpu.SemaphoreType.DMA((8,)),
        ],
        input_output_aliases={5: 2},
        compiler_params=pltpu.CompilerParams(
            collective_id=7, has_side_effects=True, vmem_limit_bytes=56 << 20
        ),
        cost_estimate=pl.CostEstimate(
            flops=16 * rows * span * LANES * pairs,
            bytes_accessed=4 * rows * width + 2 * keys * kv.shape[1],
            transcendentals=2 * rows * span * pairs,
        ),
    )(q, kv, kv, low, grad, grads)


def attend_back_kernel(
    reach, wide, z_size, mlp_count,
    q_ref, do_ref, o_ref, k_ref, v_ref, lse_ref, low_ref, cos_ref, sin_ref, cos_all, sin_all,
    *refs,
):
    mlp_ins, refs = refs[:mlp_count], refs[mlp_count:]
    dq_ref, dkv_ref = refs[:2]
    mlp_outs, refs = refs[2 : 2 + mlp_count], refs[2 + mlp_count :]
    bias_ref, dk_acc, dv_acc, own_part, send_part, recv_part, kv_send, kv_recv = refs[:8]
    home = refs[8:]
    block, half, tile, pair = (pl.program_id(at) for at in range(4))
    steps = pl.num_programs(1) * pl.num_programs(2) * pl.num_programs(3)
    inner = (half * pl.num_programs(2) + tile) * pl.num_programs(3) + pair
    step = block * steps + inner
    blocks = own_part.shape[0]
    rows = own_part.shape[1]
    count = reach // rows
    place = lax.axis_index("tensor")

    def exchange(at, distance):
        return pltpu.make_async_remote_copy(
            src_ref=send_part.at[at, pl.ds((count - distance) * rows, rows)],
            dst_ref=recv_part.at[at, distance - 1],
            send_sem=kv_send.at[at, distance - 1], recv_sem=kv_recv.at[at, distance - 1],
            device_id={"tensor": (place + z_size - distance) % z_size}, device_id_type=MESH,
        )

    def each_exchange(at, condition, action):
        for distance in range(1, count + 1):
            pl.when(condition(distance))(
                functools.partial(action, exchange(at, distance), at, distance)
            )

    @pl.when(step == 0)
    def _():
        greet(along_peers(place, z_size) + [device for _, device in others(wide)[1]])
        for copy in send_home(wide, mlp_ins, mlp_outs, *home):
            copy.start()
        fill_bias(bias_ref, low_ref, reach)

    @pl.when(inner == 0)
    def _():
        dk_acc[...] = jnp.zeros_like(dk_acc)
        dv_acc[...] = jnp.zeros_like(dv_acc)

    keys = pl.ds(pl.multiple_of(tile * QTILE, QTILE), bias_ref.shape[1])
    queries = spread_pair(q_ref[...], half)
    grads = spread_pair(do_ref[...], half)
    product = (do_ref[...].astype(F32) * o_ref[...].astype(F32)).T
    row_dot = jnp.concatenate(
        [
            jnp.sum(product[:64], axis=0, keepdims=True),
            jnp.sum(product[64:], axis=0, keepdims=True),
        ],
        axis=1,
    )
    bias = bias_ref[tile]
    key, value = k_ref[keys, :], v_ref[keys, :]
    score = dot_nt(key, queries) + jnp.concatenate([bias, bias], axis=1)
    weight = jnp.exp2(score * (SCALE * LOG2E) - lse_ref[0])
    dv_acc[keys, :] += dot_nn(weight.astype(BF16), grads)
    dscore = (weight * (dot_nt(value, grads) - row_dot)).astype(BF16)
    dk_acc[keys, :] += dot_nn(dscore, queries)
    dq = gather_pair(dot_tn(key, dscore), half) * SCALE
    dq_ref[...] = (dq * cos_ref[...] - swap_halves(dq) * sin_ref[...]).astype(BF16)

    @pl.when(inner == steps - 1)
    def _():
        send_part[block, :, :LANES] = (dk_acc[:reach] * SCALE).astype(BF16)
        send_part[block, :, LANES:] = dv_acc[:reach].astype(BF16)
        own_part[block, :, :LANES] = dk_acc[reach:] * SCALE
        own_part[block, :, LANES:] = dv_acc[reach:]
        each_exchange(block, lambda distance: place >= distance, lambda copy, *_: copy.start())

    @pl.when(step == blocks * steps - 1)
    def _():
        def collect(copy, at, distance):
            copy.wait_recv()
            own_part[at] += recv_part[at, distance - 1].astype(F32)

        for at in range(blocks):
            each_exchange(at, lambda distance: place + distance < z_size, collect)
            dkey = own_part[at, :, :LANES]
            dkey = dkey * cos_all[...] - swap_halves(dkey) * sin_all[...]
            dkv_ref[:, 2 * at * LANES : (2 * at + 1) * LANES] = dkey.astype(BF16)
            dkv_ref[:, (2 * at + 1) * LANES : (2 * at + 2) * LANES] = own_part[
                at, :, LANES:
            ].astype(BF16)
        for at in range(blocks):
            each_exchange(
                at, lambda distance: place >= distance, lambda copy, *_: copy.wait_send()
            )
        for copy in send_home(wide, mlp_ins, mlp_outs, *home):
            copy.wait()


def attend_back(q, do, att, kv, lse, low, cosine, sine, mlp, dp_size, z_size):
    rows, width = q.shape
    keys = kv.shape[0]
    reach = keys - rows
    tiles = rows // QTILE
    pairs = width // LANES
    heads = kv.shape[1] // LANES
    per_head = pairs // heads
    span = reach + QTILE
    blocks = heads // 2

    def pair_at(g, h, t, p):
        return (t, (2 * g + h) * per_head + p)

    def whole(shape):
        return pl.BlockSpec(shape, lambda g, h, t, p: (0, 0), pipeline_mode=pl.Buffered(1))

    table = pl.BlockSpec((QTILE, LANES), lambda g, h, t, p: (t, 0))
    return pl.pallas_call(
        functools.partial(
            attend_back_kernel, reach, 2 * math.isqrt(dp_size // GROUP), z_size, len(mlp)
        ),
        grid=(blocks, 2, tiles, per_head),
        in_specs=[
            pl.BlockSpec((QTILE, LANES), pair_at),
            pl.BlockSpec((QTILE, LANES), pair_at),
            pl.BlockSpec((QTILE, LANES), pair_at),
            pl.BlockSpec((keys, LANES), lambda g, h, t, p: (0, 2 * g)),
            pl.BlockSpec((keys, LANES), lambda g, h, t, p: (0, 2 * g + 1)),
            pl.BlockSpec(
                (1, 1, 2 * QTILE),
                lambda g, h, t, p: (((2 * g + h) * tiles + t) * per_head + p, 0, 0),
            ),
            whole((1, rows)),
            table,
            table,
            whole((rows, LANES)),
            whole((rows, LANES)),
        ]
        + [pl.BlockSpec(memory_space=pl.ANY)] * len(mlp),
        out_specs=[
            pl.BlockSpec((QTILE, LANES), pair_at),
            pl.BlockSpec((rows, kv.shape[1]), lambda g, h, t, p: (0, 0)),
        ]
        + [pl.BlockSpec(memory_space=pl.ANY)] * len(mlp),
        out_shape=[
            jax.ShapeDtypeStruct((rows, width), BF16),
            jax.ShapeDtypeStruct((rows, kv.shape[1]), BF16),
        ]
        + home_shapes(mlp),
        scratch_shapes=[
            pltpu.VMEM((tiles, span, QTILE), F32),
            pltpu.VMEM((keys, LANES), F32),
            pltpu.VMEM((keys, LANES), F32),
            pltpu.VMEM((blocks, rows, 2 * LANES), F32),
            pltpu.VMEM((blocks, reach, 2 * LANES), BF16),
            pltpu.VMEM((blocks, reach // rows, rows, 2 * LANES), BF16),
            pltpu.SemaphoreType.DMA((blocks, reach // rows)),
            pltpu.SemaphoreType.DMA((blocks, reach // rows)),
        ]
        + home_scratch(mlp),
        compiler_params=pltpu.CompilerParams(
            collective_id=5, has_side_effects=True, vmem_limit_bytes=60 << 20
        ),
        cost_estimate=pl.CostEstimate(
            flops=40 * rows * span * LANES * pairs,
            bytes_accessed=8 * rows * width + 4 * keys * kv.shape[1],
            transcendentals=2 * rows * span * pairs,
        ),
    )(q, do, att, kv, kv, lse, low, cosine, sine, cosine, sine, *mlp)


MESH = pl.DeviceIdType.MESH


def neighbours(wide):
    dp = lax.axis_index("dp")
    core, col, row = dp % 2, (dp // 2) % 2, (dp // (2 * wide)) % 2
    sibling = dp + 1 - 2 * core
    beside = dp + 2 - 4 * col
    above = dp + 2 * wide - 4 * wide * row
    return (row, col, core), (sibling, beside, above)


def meet(peers):
    barrier = pltpu.get_barrier_semaphore()
    for peer in peers:
        pl.semaphore_signal(barrier, inc=1, device_id={"dp": peer}, device_id_type=MESH)
    pl.semaphore_wait(barrier, len(peers))


def others(wide):
    (row, col, core), _ = neighbours(wide)
    base = lax.axis_index("dp") - (2 * wide * row + 2 * col + core)
    found = []
    for flip in range(1, GROUP):
        y, x, c = (row + flip // 4) % 2, (col + flip // 2) % 2, (core + flip) % 2
        found.append((4 * y + 2 * x + c, {"dp": base + 2 * wide * y + 2 * x + c}))
    return 4 * row + 2 * col + core, found


def along_peers(place, z_size):
    return [{"tensor": (place + step) % z_size} for step in range(1, z_size)]


def greet(peers):
    barrier = pltpu.get_barrier_semaphore()
    for peer in peers:
        pl.semaphore_signal(barrier, inc=1, device_id=peer, device_id_type=MESH)
    pl.semaphore_wait(barrier, len(peers))


def send_home(wide, ins, outs, own_sem, send_sem, recv_sem):
    mine, found = others(wide)
    copies = []
    for at, (src, dst) in enumerate(zip(ins, outs)):
        part, cols = dst.shape[0], src.shape[1]
        here = pl.ds(pl.multiple_of(mine * cols, LANES), cols)
        for index, (other, device) in enumerate(found):
            copies.append(
                pltpu.make_async_remote_copy(
                    src_ref=src.at[pl.ds(pl.multiple_of(other * part, part), part)],
                    dst_ref=dst.at[:, here],
                    send_sem=send_sem.at[at, index], recv_sem=recv_sem.at[at, index],
                    device_id=device, device_id_type=MESH,
                )
            )
        own = src.at[pl.ds(pl.multiple_of(mine * part, part), part)]
        copies.append(pltpu.make_async_copy(own, dst.at[:, here], own_sem.at[at]))
    return copies


def home_shapes(arrays):
    return [jax.ShapeDtypeStruct((a.shape[0] // GROUP, GROUP * a.shape[1]), BF16) for a in arrays]


def home_scratch(arrays):
    count = len(arrays)
    return [
        pltpu.SemaphoreType.DMA((count,)),
        pltpu.SemaphoreType.DMA((count, GROUP - 1)),
        pltpu.SemaphoreType.DMA((count, GROUP - 1)),
    ]


SIB, XN, YN = 0, 1, 2


def spread_kernel(wide, z_size, mlp_count, x_ref, gain_ref, *refs):
    attn_count = (len(refs) - 10) // 2 - mlp_count
    count = mlp_count + attn_count
    ins, xn_ref, outs = refs[:count], refs[count], refs[count + 1 : 2 * count + 1]
    x_all, x_sem, own_sem, send_sem, recv_sem, z_send, z_recv, ring_send, ring_recv = refs[
        2 * count + 1 :
    ]
    first = mlp_count
    ring = Ring(wide, outs[first], ins[first].shape[0], ring_send, ring_recv)
    place = lax.axis_index("tensor")
    mine, found = others(wide)
    greet(along_peers(place, z_size) + [device for _, device in found])

    local, copies = [], []
    for at in range(mlp_count):
        src, dst = ins[at], outs[at]
        rows, cols = src.shape[0], dst.shape[1]
        here = pl.ds(pl.multiple_of(mine * rows, rows), rows)
        for index, (other, device) in enumerate(found):
            copies.append(
                pltpu.make_async_remote_copy(
                    src_ref=src.at[:, pl.ds(pl.multiple_of(other * cols, LANES), cols)],
                    dst_ref=dst.at[here],
                    send_sem=send_sem.at[at, index], recv_sem=recv_sem.at[at, index],
                    device_id=device, device_id_type=MESH,
                )
            )
        own = src.at[:, pl.ds(pl.multiple_of(mine * cols, LANES), cols)]
        local.append(pltpu.make_async_copy(own, dst.at[here], own_sem.at[at]))

    def block(at, origin):
        cols = ins[at].shape[1]
        part = pl.ds(pl.multiple_of(origin * cols, LANES), cols)
        return outs[at].at[ring.mine() if at == first else slice(None), part]

    def hop(at, way, step, receive=False):
        sign = 1 - 2 * way
        origin = place - sign * (step if receive else step - 1)
        slot = 2 * (step - 1) + way
        src = block(at, origin) if receive or step > 1 else ins[at]
        return pltpu.make_async_remote_copy(
            src_ref=src, dst_ref=block(at, origin),
            send_sem=z_send.at[at - mlp_count, slot], recv_sem=z_recv.at[at - mlp_count, slot],
            device_id={"tensor": (place + z_size + sign) % z_size}, device_id_type=MESH,
        )

    def sends(way, step):
        if way == 0:
            return (place + 1 < z_size) & (place >= step - 1)
        return (place >= 1) & (place + step - 1 < z_size)

    def receives(way, step):
        return place >= step if way == 0 else place + step < z_size

    for at in range(mlp_count, count):
        local.append(pltpu.make_async_copy(ins[at], block(at, place), own_sem.at[at]))
        for way in range(2):
            pl.when(sends(way, 1))(lambda: hop(at, way, 1).start())
    for copy in copies + local:
        copy.start()
    load = pltpu.make_async_copy(x_ref, x_all, x_sem)
    load.start()
    load.wait()

    @pl.loop(0, x_all.shape[0] // STRIP)
    def _(at):
        here = pl.ds(pl.multiple_of(at * STRIP, STRIP), STRIP)
        value = x_all[here, :].astype(F32)
        xn_ref[here, :] = (value * rms_scale(value) * gain_ref[...]).astype(BF16)

    def advance(at, step):
        for way in range(2):
            pl.when(receives(way, step))(lambda: hop(at, way, step, True).wait_recv())
            if step + 1 < z_size:
                pl.when(sends(way, step + 1))(lambda: hop(at, way, step + 1).start())

    for step in range(1, z_size):
        advance(first, step)
    local.pop(first).wait()
    ring.start_own()
    stages = [ring.first_halves, ring.second_halves]
    for step in range(1, z_size):
        for at in range(first + 1, count):
            advance(at, step)
        if stages:
            stages.pop(0)()
    for stage in stages:
        stage()
    ring.far_halves()
    for name in ("own", "x", "y", "d"):
        ring.from_sibling(name, 0, 1)
    ring.sent()
    for step in range(1, z_size):
        for at in range(mlp_count, count):
            for way in range(2):
                pl.when(sends(way, step))(lambda: hop(at, way, step).wait_send())
    for copy in local + copies:
        copy.wait()


def spread_weights(x, gain, mlp, attn, dp_size, z_size):
    count = len(mlp) + len(attn)
    spec = pl.BlockSpec(memory_space=pl.ANY)
    near = pl.BlockSpec(memory_space=pltpu.VMEM)
    out = [jax.ShapeDtypeStruct(x.shape, BF16)]
    out += [jax.ShapeDtypeStruct((GROUP * w.shape[0], w.shape[1] // GROUP), BF16) for w in mlp]
    out += [
        jax.ShapeDtypeStruct(((1 if at else GROUP) * w.shape[0], z_size * w.shape[1]), BF16)
        for at, w in enumerate(attn)
    ]
    return pl.pallas_call(
        functools.partial(spread_kernel, 2 * math.isqrt(dp_size // GROUP), z_size, len(mlp)),
        in_specs=[spec, near] + [spec] * count,
        out_specs=[near] + [spec] * count,
        out_shape=out,
        scratch_shapes=[
            pltpu.VMEM(x.shape, BF16),
            pltpu.SemaphoreType.DMA,
            pltpu.SemaphoreType.DMA((count,)),
            pltpu.SemaphoreType.DMA((len(mlp), GROUP - 1)),
            pltpu.SemaphoreType.DMA((len(mlp), GROUP - 1)),
            pltpu.SemaphoreType.DMA((len(attn), 2 * (z_size - 1))),
            pltpu.SemaphoreType.DMA((len(attn), 2 * (z_size - 1))),
            pltpu.SemaphoreType.DMA((Ring.COPIES,)),
            pltpu.SemaphoreType.DMA((Ring.COPIES,)),
        ],
        compiler_params=pltpu.CompilerParams(collective_id=2, has_side_effects=True),
        cost_estimate=pl.CostEstimate(flops=LONG, bytes_accessed=0, transcendentals=0),
    )(x, gain, *mlp, *attn)


class Ring:
    FLIP = {SIB: (0, 0, 1), XN: (0, 1, 0), YN: (1, 0, 0)}
    COPIES = 14

    def __init__(self, wide, ref, rows, send_sem, recv_sem):
        (self.row, self.col, self.core), self.peers = neighbours(wide)
        self.ref, self.rows, self.part = ref, rows, rows // 2
        self.send_sem, self.recv_sem = send_sem, recv_sem
        self.sends = {}
        for half in range(2):
            self.sends["own", XN, half] = (2 + half, 0, 0, 0, half)
            self.sends["own", YN, half] = (4 + half, 0, 0, 0, half)
            self.sends["own", SIB, half] = (0 + half, 0, 0, 0, half)
        for half in range(2):
            self.sends["x", SIB, half] = (6 + half, 0, 1, 0, half)
            self.sends["y", SIB, half] = (8 + half, 1, 0, 0, half)
            self.sends["d", SIB, half] = (10 + half, 1, 1, 0, half)
        self.sends["x", YN, 0] = (12, 0, 1, 0, 0)
        self.sends["y", XN, 1] = (13, 1, 0, 0, 1)

    def place(self, dy, dx, dc, half):
        p = 4 * ((self.row + dy) % 2) + 2 * ((self.col + dx) % 2) + (self.core + dc) % 2
        return pl.ds(pl.multiple_of(p * self.rows + half * self.part, self.part), self.part)

    def mine(self):
        p = 4 * self.row + 2 * self.col + self.core
        return pl.ds(pl.multiple_of(p * self.rows, self.rows), self.rows)

    def whole(self, dy, dx, dc):
        p = 4 * ((self.row + dy) % 2) + 2 * ((self.col + dx) % 2) + (self.core + dc) % 2
        return pl.ds(pl.multiple_of(p * self.rows, self.rows), self.rows)

    def copy(self, slot, dy, dx, dc, half, peer):
        where = self.place(dy, dx, dc, half)
        return pltpu.make_async_remote_copy(
            src_ref=self.ref.at[where], dst_ref=self.ref.at[where],
            send_sem=self.send_sem.at[slot], recv_sem=self.recv_sem.at[slot],
            device_id={"dp": self.peers[peer]}, device_id_type=MESH,
        )

    def start(self, name, peer, half):
        self.copy(*self.sends[name, peer, half], peer).start()

    def arrived(self, name, peer, half):
        slot, dy, dx, dc, half = self.sends[name, peer, half]
        fy, fx, fc = self.FLIP[peer]
        self.copy(slot, (dy + fy) % 2, (dx + fx) % 2, (dc + fc) % 2, half, peer).wait_recv()

    def start_own(self):
        for half in range(2):
            for peer in (XN, YN, SIB):
                self.start("own", peer, half)

    def first_halves(self):
        self.arrived("own", XN, 0)
        self.start("x", YN, 0)
        self.start("x", SIB, 0)
        self.arrived("own", YN, 0)
        self.start("y", SIB, 0)

    def second_halves(self):
        self.arrived("own", YN, 1)
        self.start("y", XN, 1)
        self.start("y", SIB, 1)
        self.arrived("own", XN, 1)
        self.start("x", SIB, 1)

    def far_halves(self):
        self.arrived("x", YN, 0)
        self.start("d", SIB, 0)
        self.arrived("y", XN, 1)
        self.start("d", SIB, 1)

    def from_sibling(self, name, *halves):
        for half in halves:
            self.arrived(name, SIB, half)

    def sent(self):
        for (name, peer, half), entry in self.sends.items():
            self.copy(*entry, peer).wait_send()


def project_kernel(
    wide, z_size, x_ref, cos_ref, sin_ref, wkv_ref, wq_ref, wo_ref, grad_ref,
    q_ref, kv_ref, wq_out, wo_out, grad_out,
    wkv_all, wq_all, wo_all, grad_all, keys, own_sem, send_sem, recv_sem, kv_send, kv_recv, out_sem,
):
    place = lax.axis_index("tensor")
    rows = x_ref.shape[0]
    count = keys.shape[0] // rows - 1
    left = pl.ds(0, grad_all.shape[1])
    parts = (
        (wq_ref, wq_all, wq_out), (wo_ref, wo_all, wo_out),
        (grad_ref.at[:, left], grad_all, grad_out.at[:, left]),
    )
    rings = [
        Ring(wide, full, part.shape[0], send_sem.at[at], recv_sem.at[at])
        for at, (part, full, _) in enumerate(parts)
    ]
    local = [
        pltpu.make_async_copy(part, full.at[ring.mine()], own_sem.at[at])
        for at, ((part, full, _), ring) in enumerate(zip(parts, rings))
    ]
    outward = [
        pltpu.make_async_copy(full, out, out_sem.at[at])
        for at, (_, full, out) in enumerate(parts)
    ]
    load = pltpu.make_async_copy(wkv_ref, wkv_all, own_sem.at[len(parts)])
    for copy in local + [load]:
        copy.start()
    keys[: count * rows, :] = jnp.zeros((count * rows, keys.shape[1]), BF16)
    greet([{"dp": peer} for peer in rings[0].peers] + along_peers(place, z_size))
    for copy in local:
        copy.wait()

    def rotated(value):
        return (value * cos_ref[...] + swap_halves(value) * sin_ref[...]).astype(BF16)

    def hop(step):
        return pltpu.make_async_remote_copy(
            src_ref=keys.at[pl.ds((count - step + 1) * rows, rows)],
            dst_ref=keys.at[pl.ds((count - step) * rows, rows)],
            send_sem=kv_send.at[step - 1], recv_sem=kv_recv.at[step - 1],
            device_id={"tensor": (place + 1) % z_size}, device_id_type=MESH,
        )

    def pass_keys(step):
        if step > 1:
            pl.when(place >= step - 1)(lambda: hop(step - 1).wait_recv())
        if step <= count:
            sends = (place + 1 < z_size) & (place >= step - 1)
            pl.when(sends)(lambda: hop(step).start())

    def finish(ring):
        ring.far_halves()
        for name in ("own", "x", "y", "d"):
            ring.from_sibling(name, 0, 1)

    rings[0].start_own()
    load.wait()

    @pl.loop(0, wkv_all.shape[1] // (2 * LANES))
    def _(at):
        n = pl.ds(pl.multiple_of(at * 2 * LANES, LANES), 2 * LANES)
        value = dot_nn(x_ref[...], wkv_all[:, n])
        both = jnp.concatenate([rotated(value[:, :LANES]), value[:, LANES:].astype(BF16)], axis=1)
        keys[pl.ds(count * rows, rows), n] = both

    pass_keys(1)
    rings[0].first_halves()
    rings[0].second_halves()
    rings[1].start_own()
    finish(rings[0])
    outward[0].start()

    @pl.loop(0, wq_all.shape[1] // (2 * LANES))
    def _(at):
        n = pl.ds(pl.multiple_of(at * 2 * LANES, LANES), 2 * LANES)
        value = dot_nn(x_ref[...], wq_all[:, n])
        both = [rotated(value[:, :LANES]), rotated(value[:, LANES:])]
        q_ref[:, n] = jnp.concatenate(both, axis=1)

    for step in range(2, count + 1):
        pass_keys(step)
    rings[1].first_halves()
    rings[1].second_halves()
    rings[2].start_own()
    finish(rings[1])
    outward[1].start()
    rings[2].first_halves()
    rings[2].second_halves()
    finish(rings[2])
    outward[2].start()
    pass_keys(count + 1)
    keys_out = pltpu.make_async_copy(keys, kv_ref, out_sem.at[3])
    keys_out.start()
    for step in range(1, count + 1):
        sends = (place + 1 < z_size) & (place >= step - 1)
        pl.when(sends)(lambda: hop(step).wait_send())
    for ring in rings:
        ring.sent()
    for copy in outward + [keys_out]:
        copy.wait()


def project(x, cosine, sine, wkv, wq, wo, grad, reach, dp_size, z_size):
    rows, width = x.shape
    far = pl.BlockSpec(memory_space=pl.ANY)
    near = pl.BlockSpec(memory_space=pltpu.VMEM)
    whole = [(GROUP * w.shape[0], w.shape[1]) for w in (wq, wo)]
    keys = (reach + rows, wkv.shape[1])
    grads = (GROUP * grad.shape[0], grad.shape[1])
    left = (grads[0], grads[1] // 2)
    return pl.pallas_call(
        functools.partial(project_kernel, 2 * math.isqrt(dp_size // GROUP), z_size),
        in_specs=[near] * 3 + [far] * 4,
        out_specs=[near] + [far] * 4,
        out_shape=[jax.ShapeDtypeStruct((rows, wq.shape[1]), BF16)]
        + [jax.ShapeDtypeStruct(shape, BF16) for shape in [keys] + whole + [grads]],
        scratch_shapes=[pltpu.VMEM(shape, BF16) for shape in [wkv.shape] + whole + [left, keys]]
        + [
            pltpu.SemaphoreType.DMA((4,)),
            pltpu.SemaphoreType.DMA((3, Ring.COPIES)),
            pltpu.SemaphoreType.DMA((3, Ring.COPIES)),
            pltpu.SemaphoreType.DMA((reach // rows,)),
            pltpu.SemaphoreType.DMA((reach // rows,)),
            pltpu.SemaphoreType.DMA((4,)),
        ],
        compiler_params=pltpu.CompilerParams(
            collective_id=3, has_side_effects=True, vmem_limit_bytes=56 << 20
        ),
        cost_estimate=pl.CostEstimate(
            flops=2 * LONG, bytes_accessed=0, transcendentals=0
        ),
    )(x, cosine, sine, wkv, wq, wo, grad)


def gate_up_kernel(
    wide, own_ref, wg_ref, wu_ref, all_ref, gate_ref, up_ref, hid_ref, core_ref,
    full, stage, wg_all, wu_all, own_sem, load_sem, send_sem, recv_sem, out_sem, all_sem,
):
    rows = own_ref.shape[0]
    cols = gate_ref.shape[1]
    ring = Ring(wide, full, rows, send_sem, recv_sem)
    local = pltpu.make_async_copy(own_ref, full.at[ring.mine()], own_sem)
    local.start()
    loads = [
        pltpu.make_async_copy(wg_ref, wg_all, load_sem.at[0]),
        pltpu.make_async_copy(wu_ref, wu_all, load_sem.at[1]),
    ]
    for copy in loads:
        copy.start()
    meet(ring.peers)
    local.wait()
    ring.start_own()
    for copy in loads:
        copy.wait()

    def out_copies(slot, places):
        where, core, chip = places
        return [
            pltpu.make_async_copy(stage.at[slot, i], ref.at[where], out_sem.at[slot, i])
            for i, ref in enumerate((gate_ref, up_ref, hid_ref))
        ] + [
            pltpu.make_async_copy(stage.at[slot, 2], core_ref.at[core, chip], out_sem.at[slot, 3]),
            pltpu.make_async_copy(full.at[where], all_ref.at[where], all_sem.at[slot]),
        ]

    def step_place(step):
        phase, i = step // 4, step % 4
        high, low = phase // 2, phase % 2
        first, last = (1 - high) * (1 - low), high * low
        middle = high + low - 2 * last
        half = (first + last) * (i % 2) + high * (1 - low)
        dx = middle * (1 - i % 2) + last
        dy = middle * (i % 2) + last
        part = rows // 2
        chip_rows = pl.ds(pl.multiple_of((2 * dy + dx) * rows + half * part, part), part)
        return ring.place(dy, dx, i // 2, half), i // 2, chip_rows

    @pl.loop(0, 16)
    def _(step):
        pl.when(step == 2)(lambda: ring.from_sibling("own", 0, 1))
        pl.when(step == 4)(ring.first_halves)

        @pl.when(step == 6)
        def _():
            ring.from_sibling("x", 0)
            ring.from_sibling("y", 0)

        pl.when(step == 8)(ring.second_halves)

        @pl.when(step == 10)
        def _():
            ring.from_sibling("x", 1)
            ring.from_sibling("y", 1)

        pl.when(step == 12)(ring.far_halves)
        pl.when(step == 14)(lambda: ring.from_sibling("d", 0, 1))

        slot = step % 2
        places = step_place(step)

        @pl.when(step >= 2)
        def _():
            for copy in out_copies(slot, step_place(step - 2)):
                copy.wait()

        x = full[places[0], :]

        @pl.loop(0, cols // NTILE)
        def _(at):
            n = pl.ds(pl.multiple_of(at * NTILE, NTILE), NTILE)
            gate = dot_nn(x, wg_all[:, n])
            up = dot_nn(x, wu_all[:, n])
            stage[slot, 0, :, n] = gate.astype(BF16)
            stage[slot, 1, :, n] = up.astype(BF16)
            stage[slot, 2, :, n] = (gate * up / (1.0 + jnp.exp(-gate))).astype(BF16)

        for copy in out_copies(slot, places):
            copy.start()

    for step in (14, 15):
        for copy in out_copies(step % 2, step_place(step)):
            copy.wait()
    ring.sent()


def gate_up(hn, wg, wu, dp_size):
    rows, width = hn.shape
    cols = wg.shape[1]
    tokens = GROUP * rows
    far = pl.BlockSpec(memory_space=pl.ANY)
    return pl.pallas_call(
        functools.partial(gate_up_kernel, 2 * math.isqrt(dp_size // GROUP)),
        in_specs=[far] * 3,
        out_specs=[far] * 5,
        out_shape=[jax.ShapeDtypeStruct((tokens, width), BF16)]
        + [jax.ShapeDtypeStruct((tokens, cols), BF16)] * 3
        + [jax.ShapeDtypeStruct((2, tokens // 2, cols), BF16)],
        scratch_shapes=[
            pltpu.VMEM((tokens, width), BF16),
            pltpu.VMEM((2, 3, rows // 2, cols), BF16),
            pltpu.VMEM(wg.shape, BF16),
            pltpu.VMEM(wu.shape, BF16),
            pltpu.SemaphoreType.DMA,
            pltpu.SemaphoreType.DMA((2,)),
            pltpu.SemaphoreType.DMA((Ring.COPIES,)),
            pltpu.SemaphoreType.DMA((Ring.COPIES,)),
            pltpu.SemaphoreType.DMA((2, 4)),
            pltpu.SemaphoreType.DMA((2,)),
        ],
        compiler_params=pltpu.CompilerParams(
            collective_id=1, has_side_effects=True, vmem_limit_bytes=56 << 20
        ),
        cost_estimate=pl.CostEstimate(
            flops=SHORT, bytes_accessed=0, transcendentals=0
        ),
    )(hn, wg, wu)


FAR_CHUNK, X_CHUNK, Y_CHUNK, OWN_CHUNK = range(4)


class Reduce:
    COPIES = 10

    def __init__(self, wide, parts, cores, far, near, send_sem, recv_sem):
        self.at, self.peers = neighbours(wide)
        self.parts, self.cores, self.far, self.near = parts, cores, far, near
        self.send_sem, self.recv_sem = send_sem, recv_sem
        self.half = parts.shape[2] // 2

    @staticmethod
    def scratch(rows, cols):
        return [
            pltpu.VMEM((2, 4, rows, cols), BF16),
            pltpu.VMEM((4, rows, cols), BF16),
            pltpu.VMEM((2, rows // 2, cols), BF16),
            pltpu.VMEM((2, rows, cols), BF16),
            pltpu.SemaphoreType.DMA((Reduce.COPIES,)),
            pltpu.SemaphoreType.DMA((Reduce.COPIES,)),
        ]

    def chunk(self, step):
        slot, other = step // 2, 1 - step % 2
        row, col, core = self.at
        dy, dx = 1 - slot % 2, 1 - slot // 2
        place = 4 * ((row + dy) % 2) + 2 * ((col + dx) % 2) + (core + other) % 2
        return place, self.parts.at[other, slot]

    def copy(self, name):
        upper, lower = pl.ds(0, self.half), pl.ds(self.half, self.half)
        mine = self.parts.at[0]
        table = {
            "far0": (self.parts.at[1, FAR_CHUNK], self.cores.at[FAR_CHUNK], SIB),
            "x": (self.parts.at[1, X_CHUNK], self.cores.at[X_CHUNK], SIB),
            "y": (self.parts.at[1, Y_CHUNK], self.cores.at[Y_CHUNK], SIB),
            "own": (self.parts.at[1, OWN_CHUNK], self.cores.at[OWN_CHUNK], SIB),
            "far_x": (mine.at[FAR_CHUNK, lower], self.far.at[0], XN),
            "far_y": (mine.at[FAR_CHUNK, upper], self.far.at[1], YN),
            "x_upper": (mine.at[X_CHUNK, upper], self.near.at[0, upper], XN),
            "x_lower": (mine.at[X_CHUNK, lower], self.near.at[0, lower], XN),
            "y_upper": (mine.at[Y_CHUNK, upper], self.near.at[1, upper], YN),
            "y_lower": (mine.at[Y_CHUNK, lower], self.near.at[1, lower], YN),
        }
        src, dst, peer = table[name]
        at = list(table).index(name)
        return pltpu.make_async_remote_copy(
            src_ref=src, dst_ref=dst, send_sem=self.send_sem.at[at],
            recv_sem=self.recv_sem.at[at], device_id={"dp": self.peers[peer]},
            device_id_type=MESH,
        )

    def start(self, *names):
        for name in names:
            self.copy(name).start()

    def add(self, slot, start, other):
        count = other.shape[0] // STRIP

        @pl.loop(0, count)
        def _(at):
            here = pl.ds(pl.multiple_of(start + at * STRIP, STRIP), STRIP)
            there = pl.ds(pl.multiple_of(at * STRIP, STRIP), STRIP)
            value = self.parts[0, slot, here, :].astype(F32) + other[there, :].astype(F32)
            self.parts[0, slot, here, :] = value.astype(BF16)

    def merge_core(self, slot, name):
        self.copy(name).wait_recv()
        self.add(slot, 0, self.cores.at[slot])

    def after(self, step):
        names = ("far0", "x", "y", "own")
        for slot in range(4):
            pl.when(step == 2 * slot)(functools.partial(self.start, names[slot]))

        @pl.when(step == 1)
        def _():
            self.merge_core(FAR_CHUNK, "far0")
            self.start("far_x", "far_y")

        @pl.when(step == 3)
        def _():
            self.merge_core(X_CHUNK, "x")
            self.start("x_lower")

        @pl.when(step == 5)
        def _():
            self.merge_core(Y_CHUNK, "y")
            self.start("y_upper")

    def pass_on(self):
        self.copy("far_y").wait_recv()
        self.add(X_CHUNK, 0, self.far.at[1])
        self.start("x_upper")
        self.copy("far_x").wait_recv()
        self.add(Y_CHUNK, self.half, self.far.at[0])
        self.start("y_lower")

    def finish(self, store):
        for name in ("own", "x_upper", "x_lower", "y_upper", "y_lower"):
            self.copy(name).wait_recv()

        @pl.loop(0, 2 * self.half // STRIP)
        def _(at):
            here = pl.ds(pl.multiple_of(at * STRIP, STRIP), STRIP)
            value = self.parts[0, OWN_CHUNK, here, :].astype(F32)
            value += self.cores[OWN_CHUNK, here, :].astype(F32)
            value += self.near[0, here, :].astype(F32)
            value += self.near[1, here, :].astype(F32)
            store(here, value)

    def sent(self):
        for name in (
            "far0", "x", "y", "own", "far_x", "far_y", "x_upper", "x_lower", "y_upper", "y_lower",
        ):
            self.copy(name).wait_send()


def hidden_back_kernel(
    wide, gain_ref, h_ref, grad_ref, dgate_ref, dup_ref, wg_ref, wu_ref,
    low_ref, gain_out,
    loaded, wg_all, wu_all, h_all, grad_all, load_sem, own_sem, *scratch,
):
    ring = Reduce(wide, *scratch)
    rows = low_ref.shape[0]

    def loads(step):
        chunk, _ = ring.chunk(step)
        here = pl.ds(pl.multiple_of(chunk * rows, rows), rows)
        return [
            pltpu.make_async_copy(
                ref.at[here], loaded.at[step % 2, at], load_sem.at[step % 2, at]
            )
            for at, ref in enumerate((dgate_ref, dup_ref))
        ]

    pairs = ((wg_ref, wg_all), (wu_ref, wu_all), (h_ref, h_all), (grad_ref, grad_all))
    whole = [
        pltpu.make_async_copy(src, dst, own_sem.at[at]) for at, (src, dst) in enumerate(pairs)
    ]
    for copy in loads(0) + whole:
        copy.start()
    meet(ring.peers)
    for copy in whole[:2]:
        copy.wait()

    @pl.loop(0, 8)
    def _(step):
        @pl.when(step < 7)
        def _():
            for copy in loads(step + 1):
                copy.start()

        for copy in loads(step):
            copy.wait()
        _, target = ring.chunk(step)
        dgate, dup = loaded[step % 2, 0], loaded[step % 2, 1]

        @pl.loop(0, low_ref.shape[1] // NTILE)
        def _(at):
            n = pl.ds(pl.multiple_of(at * NTILE, NTILE), NTILE)
            value = dot_nt(dgate, wg_all[n, :]) + dot_nt(dup, wu_all[n, :])
            target[:, n] = value.astype(BF16)

        ring.after(step)

    ring.pass_on()
    for copy in whole[2:]:
        copy.wait()
    gain_out[...] = jnp.zeros_like(gain_out)

    def store(here, value):
        h = h_all[here, :]
        scale = rms_scale(h)
        gained = value * gain_ref[...]
        inner = jnp.mean(gained * h, axis=1, keepdims=True)
        gain_out[...] += value * h * scale
        total = grad_all[here, :].astype(F32) + scale * gained
        total -= h * (scale * scale * scale * inner)
        low_ref[here, :] = total.astype(BF16)

    ring.finish(store)
    ring.sent()


def hidden_back(gain, h, grad, dgate, dup, wg, wu, dp_size):
    tokens, cols = dgate.shape
    rows, width = h.shape
    far = pl.BlockSpec(memory_space=pl.ANY)
    near = pl.BlockSpec(memory_space=pltpu.VMEM)
    return pl.pallas_call(
        functools.partial(hidden_back_kernel, 2 * math.isqrt(dp_size // GROUP)),
        in_specs=[near] + [far] * 6,
        out_specs=[near] * 2,
        out_shape=[
            jax.ShapeDtypeStruct((rows, width), BF16),
            jax.ShapeDtypeStruct((STRIP, width), F32),
        ],
        scratch_shapes=[
            pltpu.VMEM((2, 2, rows, cols), BF16),
            pltpu.VMEM(wg.shape, BF16),
            pltpu.VMEM(wu.shape, BF16),
            pltpu.VMEM(h.shape, F32),
            pltpu.VMEM(grad.shape, BF16),
            pltpu.SemaphoreType.DMA((2, 2)),
            pltpu.SemaphoreType.DMA((4,)),
        ]
        + Reduce.scratch(rows, width),
        compiler_params=pltpu.CompilerParams(
            collective_id=6, has_side_effects=True, vmem_limit_bytes=62 << 20
        ),
        cost_estimate=pl.CostEstimate(
            flops=2 * LONG, bytes_accessed=4 * rows * width, transcendentals=0
        ),
    )(gain, h, grad, dgate, dup, wg, wu)


def tail_kernel(
    wide, z_size, mlp_count, x_ref, dq_ref, dkv_ref, wo_ref, gain_ref,
    raw_ref, dh_ref, wq_ref, wkv_ref, *refs
):
    mlp_ins, refs = refs[:mlp_count], refs[mlp_count:]
    wq_out, wkv_out, wo_out, gain_out, grad_out = refs[:5]
    mlp_outs, scratch = refs[5 : 5 + mlp_count], refs[5 + mlp_count :]
    sub = wkv_out.shape[1]
    halves = wq_out.shape[1] // sub
    count = halves + 1
    rings = [Reduce(wide, *scratch[6 * at : 6 * at + 6]) for at in range(count)]
    sums, zrecv, gain_z, gain_p, z_send, z_recv, g_send, g_recv = scratch[6 * count : 6 * count + 8]
    wo_recv, w_send, w_recv = scratch[6 * count + 8 : 6 * count + 11]
    wq_all, wkv_all, raw, dh, dxn, gain_sum, load_sem = scratch[6 * count + 11 : 6 * count + 18]
    mlp_copies = send_home(wide, mlp_ins, mlp_outs, *scratch[6 * count + 18 :])
    place = lax.axis_index("tensor")
    mine, found = others(wide)
    along = along_peers(place, z_size)
    around = [device for _, device in found]

    tiles, tile_rows = raw.shape[0], raw.shape[1]
    loads = [
        pltpu.make_async_copy(wq_ref, wq_all, load_sem.at[0]),
        pltpu.make_async_copy(wkv_ref, wkv_all, load_sem.at[1]),
    ]
    for tile in range(tiles):
        here = pl.ds(tile * tile_rows, tile_rows)
        loads += [
            pltpu.make_async_copy(raw_ref.at[here], raw.at[tile], load_sem.at[2 + 2 * tile]),
            pltpu.make_async_copy(dh_ref.at[here], dh.at[tile], load_sem.at[3 + 2 * tile]),
        ]
    for copy in loads:
        copy.start()
    greet(along + around)

    wo_part = wo_out.shape[1]
    wo_copies = [
        pltpu.make_async_remote_copy(
            src_ref=wo_ref.at[
                :,
                pl.ds(pl.multiple_of((place + at + 1) % z_size * wo_part, LANES), wo_part),
            ],
            dst_ref=wo_recv.at[at], send_sem=w_send.at[at], recv_sem=w_recv.at[at],
            device_id=peer, device_id_type=MESH,
        )
        for at, peer in enumerate(along)
    ]
    for copy in wo_copies:
        copy.start()

    pieces = [(dq_ref, wq_out, at * sub) for at in range(halves)] + [(dkv_ref, wkv_out, 0)]
    rows = sums.shape[1]
    z_copies = []

    def partial_sums(index):
        ring = rings[index]
        right, out, offset = pieces[index]

        @pl.loop(0, 8)
        def _(step):
            chunk, target = ring.chunk(step)
            x = x_ref[:, pl.ds(pl.multiple_of(chunk * rows, rows), rows)].T

            @pl.loop(0, z_size)
            def _(at):
                n = pl.ds(pl.multiple_of(at * sub, LANES), sub)
                source = pl.ds(pl.multiple_of(at * out.shape[1] + offset, LANES), sub)
                target[:, n] = dot_nn(x, right[:, source]).astype(BF16)

            ring.after(step)

    gain_sum[...] = jnp.zeros_like(gain_sum)

    def input_rows(tile):
        part = pl.ds(tile * tile_rows, tile_rows)
        dq, dkv = dq_ref[part, :], dkv_ref[part, :]

        @pl.loop(0, dxn.shape[1] // NTILE)
        def _(at):
            n = pl.ds(pl.multiple_of(at * NTILE, NTILE), NTILE)
            dxn[:, n] = dot_nt(dq, wq_all[n, :]) + dot_nt(dkv, wkv_all[n, :])

        @pl.loop(0, tile_rows // STRIP)
        def _(at):
            here = pl.ds(pl.multiple_of(at * STRIP, STRIP), STRIP)
            there = pl.ds(pl.multiple_of(tile * tile_rows + at * STRIP, STRIP), STRIP)
            grad, value = dxn[here, :], raw[tile, here, :].astype(F32)
            scale = rms_scale(value)
            gained = grad * gain_ref[0:1, :]
            inner = jnp.mean(gained * value, axis=1, keepdims=True)
            gain_sum[...] += grad * value * scale
            total = scale * gained - value * (scale * scale * scale * inner)
            grad_out[there, :] = (dh[tile, here, :].astype(F32) + total).astype(BF16)

    def send_along(index):
        def store(here, value):
            sums[index, here, :] = value.astype(BF16)

        rings[index].finish(store)
        for at, peer in enumerate(along):
            other = (place + at + 1) % z_size
            copy = pltpu.make_async_remote_copy(
                src_ref=sums.at[index, :, pl.ds(pl.multiple_of(other * sub, LANES), sub)],
                dst_ref=zrecv.at[index, at],
                send_sem=z_send.at[index, at], recv_sem=z_recv.at[index, at],
                device_id=peer, device_id_type=MESH,
            )
            z_copies.append(copy)
            copy.start()

    partial_sums(0)
    for copy in loads:
        copy.wait()
    input_rows(0)
    rings[0].pass_on()
    for index in range(1, count):
        partial_sums(index)
        if index < tiles:
            input_rows(index)
        if index + 1 < count:
            rings[index].pass_on()
            send_along(index - 1)
    for tile in range(count, tiles):
        input_rows(tile)

    gain_z[place, 0:1] = jnp.sum(gain_sum[...], axis=0, keepdims=True)
    gain_z[place, 1:2] = gain_ref[1:2, :]
    gain_copies = [
        pltpu.make_async_remote_copy(
            src_ref=gain_z.at[place], dst_ref=gain_z.at[place], send_sem=g_send.at[at],
            recv_sem=g_recv.at[at], device_id=peer, device_id_type=MESH,
        )
        for at, peer in enumerate(along)
    ]
    for copy in gain_copies:
        copy.start()
    rings[count - 1].pass_on()
    for copy in mlp_copies:
        copy.start()
    send_along(count - 2)

    for copy in gain_copies:
        copy.wait_recv()
    total = gain_z[0]
    for at in range(1, z_size):
        total = total + gain_z[at]
    gain_p[mine] = total
    for at, peer in enumerate(around):
        copy = pltpu.make_async_remote_copy(
            src_ref=gain_p.at[mine], dst_ref=gain_p.at[mine],
            send_sem=g_send.at[z_size - 1 + at], recv_sem=g_recv.at[z_size - 1 + at],
            device_id=peer, device_id_type=MESH,
        )
        gain_copies.append(copy)
        copy.start()
    for copy in wo_copies:
        copy.wait()
    total = wo_ref[:, pl.ds(pl.multiple_of(place * wo_part, LANES), wo_part)].astype(F32)
    for at in range(z_size - 1):
        total += wo_recv[at].astype(F32)
    wo_out[...] = total
    send_along(count - 1)

    for copy in gain_copies[z_size - 1 :]:
        copy.wait_recv()
    total = gain_p[0]
    for at in range(1, GROUP):
        total = total + gain_p[at]
    gain_out[...] = total
    for copy in z_copies:
        copy.wait_recv()
    for index, (_, out, offset) in enumerate(pieces):
        value = sums[index, :, pl.ds(pl.multiple_of(place * sub, LANES), sub)].astype(F32)
        for at in range(z_size - 1):
            value += zrecv[index, at].astype(F32)
        out[:, offset : offset + sub] = value
    for copy in z_copies + gain_copies:
        copy.wait_send()
    for ring in rings:
        ring.sent()
    for copy in mlp_copies:
        copy.wait()


def last_grads(x, dq, dkv, wo_sum, gains, raw, dh, wq, wkv, mlp, dp_size, z_size):
    tokens, width = x.shape
    rows = width // GROUP
    tiles = tokens // QTILE
    near = pl.BlockSpec(memory_space=pltpu.VMEM)
    far = pl.BlockSpec(memory_space=pl.ANY)
    sizes = [dq.shape[1], dkv.shape[1]]
    cols = dkv.shape[1]
    count = sum(sizes) // cols
    scratch = []
    for _ in range(count):
        scratch += Reduce.scratch(rows, cols)
    return pl.pallas_call(
        functools.partial(tail_kernel, 2 * math.isqrt(dp_size // GROUP), z_size, len(mlp)),
        in_specs=[near] * 5 + [far] * (4 + len(mlp)),
        out_specs=[near] * 5 + [far] * len(mlp),
        out_shape=[jax.ShapeDtypeStruct((rows, size // z_size), F32) for size in sizes]
        + [
            jax.ShapeDtypeStruct((rows, wo_sum.shape[1] // z_size), F32),
            jax.ShapeDtypeStruct(gains.shape, F32),
            jax.ShapeDtypeStruct((tokens, width), BF16),
        ]
        + home_shapes(mlp),
        scratch_shapes=scratch
        + [
            pltpu.VMEM((count, rows, cols), BF16),
            pltpu.VMEM((count, z_size - 1, rows, cols // z_size), BF16),
            pltpu.VMEM((z_size, *gains.shape), F32),
            pltpu.VMEM((GROUP, *gains.shape), F32),
            pltpu.SemaphoreType.DMA((count, z_size - 1)),
            pltpu.SemaphoreType.DMA((count, z_size - 1)),
            pltpu.SemaphoreType.DMA((z_size - 1 + GROUP - 1,)),
            pltpu.SemaphoreType.DMA((z_size - 1 + GROUP - 1,)),
            pltpu.VMEM((z_size - 1, rows, wo_sum.shape[1] // z_size), BF16),
            pltpu.SemaphoreType.DMA((z_size - 1,)),
            pltpu.SemaphoreType.DMA((z_size - 1,)),
            pltpu.VMEM(wq.shape, BF16),
            pltpu.VMEM(wkv.shape, BF16),
            pltpu.VMEM((tiles, QTILE, width), BF16),
            pltpu.VMEM((tiles, QTILE, width), BF16),
            pltpu.VMEM((QTILE, width), F32),
            pltpu.VMEM((STRIP, width), F32),
            pltpu.SemaphoreType.DMA((2 + 2 * tiles,)),
        ]
        + home_scratch(mlp),
        compiler_params=pltpu.CompilerParams(
            collective_id=4, has_side_effects=True, vmem_limit_bytes=62 << 20
        ),
        cost_estimate=pl.CostEstimate(flops=SHORT, bytes_accessed=0, transcendentals=0),
    )(x, dq, dkv, wo_sum, gains, raw, dh, wq, wkv, *mlp)


def emit_kernel(*refs):
    ins, outs = refs[:7], refs[7:]
    for src, dst in zip(ins[:6], outs[:6]):
        dst[...] = src[...].astype(dst.dtype)
    outs[6][...] = ins[6][:, :LANES]
    outs[7][...] = ins[6][:, LANES:]


def emit(mlp, grad, wq, wo, wkv):
    ins = (*mlp, grad, wq, wo, wkv)
    apart = (wkv.shape[0], LANES)
    outs = [(m.shape, F32) for m in mlp] + [(grad.shape, BF16), (wq.shape, F32), (wo.shape, F32)]
    outs += [(apart, F32)] * 2
    steps = 4

    def spec(shape):
        return pl.BlockSpec((shape[0] // steps, shape[1]), lambda at: (at, 0))

    return pl.pallas_call(
        emit_kernel,
        grid=(steps,),
        in_specs=[spec(array.shape) for array in ins],
        out_specs=[spec(shape) for shape, _ in outs],
        out_shape=[jax.ShapeDtypeStruct(*out) for out in outs],
    )(*ins)


class Layout:
    def __init__(self, dp_size):
        self.blocks = dp_size // GROUP
        side = math.isqrt(self.blocks)
        self.rows, self.cols = side, self.blocks // side
        wide = 2 * self.cols

        def index(by, bx, y, x, core):
            return ((2 * by + y) * wide + 2 * bx + x) * 2 + core

        places = [(y, x, c) for y in range(2) for x in range(2) for c in range(2)]
        spots = [(by, bx) for by in range(self.rows) for bx in range(self.cols)]
        self.inner = [[index(*s, *p) for p in places] for s in spots]
        self.outer = [[index(*s, *p) for s in spots] for p in places]

    def groups(self):
        return None if self.blocks == 1 else self.inner

    def to_rows(self, array):
        if self.blocks == 1:
            return array
        rest = array.shape[1:]
        split = array.reshape(2, 2, 2, self.rows, self.cols, -1, *rest)
        order = (3, 0, 4, 1, 2, 5) + tuple(range(6, 6 + len(rest)))
        return split.transpose(order).reshape(array.shape)

    def from_rows(self, array):
        if self.blocks == 1:
            return array
        rest = array.shape[1:]
        split = array.reshape(self.rows, 2, self.cols, 2, 2, -1, *rest)
        order = (1, 3, 4, 0, 2, 5) + tuple(range(6, 6 + len(rest)))
        return split.transpose(order).reshape(array.shape)

    def from_cols(self, array):
        return array if self.blocks == 1 else self.from_rows(array.T).T

    def gather_outer(self, array):
        if self.blocks == 1:
            return array
        return lax.all_gather(array, "dp", axis_index_groups=self.outer, axis=0, tiled=True)

    def scatter_outer(self, array):
        if self.blocks == 1:
            return array
        return lax.psum_scatter(
            array, "dp", scatter_dimension=0, axis_index_groups=self.outer, tiled=True
        )

    def swap(self, array, flip):
        pairs = [
            (block[at], block[at ^ flip]) for block in self.inner for at in range(GROUP)
        ]
        return lax.ppermute(array, "dp", pairs)

    def sum_outer(self, array):
        if self.blocks == 1:
            return array
        return lax.psum(array, "dp", axis_index_groups=self.outer)

    def gather(self, array):
        return lax.all_gather(array, "dp", axis_index_groups=self.groups(), axis=0, tiled=True)

    def scatter(self, array):
        return lax.psum_scatter(
            array, "dp", scatter_dimension=0, axis_index_groups=self.groups(), tiled=True
        )


def rms_scale(values):
    return lax.rsqrt(jnp.mean(values * values, axis=-1, keepdims=True) + NORM_EPS)


def per_device(
    dp_size, z_size, activations, segment_ids, attn_gain, w_query, w_key, w_value, w_out,
    mlp_gain, w_gate, w_up, w_down, cotangent,
):
    layout = Layout(dp_size)
    rows, width = activations.shape[1:]
    x = activations[0].astype(F32)
    place = lax.axis_index("tensor")
    reach = -(-(MOST_DOC - 1) // rows) * rows

    def shift(array, step):
        pairs = [(at, at + step) for at in range(z_size) if 0 <= at + step < z_size]
        return lax.ppermute(array, "tensor", pairs)

    starts = document_starts(segment_ids[0])
    own_starts = lax.dynamic_slice_in_dim(starts, place * rows, rows)
    own_tokens = place * rows + jnp.arange(rows, dtype=jnp.int32)
    cosine, sine = rope_tables(own_tokens - own_starts)
    low = (own_starts - place * rows + reach)[None, :]

    shards = [
        layout.gather_outer(w)
        for w in (w_gate, w_up, w_down, jnp.concatenate([w_key, w_value], axis=1), w_query, w_out)
    ]
    xn, *spread = spread_weights(
        activations[0], attn_gain[None], shards[:3], shards[3:], dp_size, z_size
    )
    def gather_z(array):
        return layout.to_rows(lax.all_gather(array, "tensor", axis=1, tiled=True))

    wg, wu = gather_z(spread[0]), gather_z(spread[1])

    def along_z(total):
        return lax.psum_scatter(
            layout.from_rows(total), "tensor", scatter_dimension=1, tiled=True
        )

    q, kv_all, wq, wo, dy = project(
        layout.from_cols(xn), cosine, sine, *spread[3:], cotangent[0], reach, dp_size, z_size
    )
    wd = gather_z(spread[2])
    wkv, wq, wo = (layout.to_rows(w) for w in (spread[3], wq, wo))
    att, lse, dy = attend(q, kv_all, low, cotangent[0], dy, dp_size)
    h = x + dot_nt(att, wo)

    r2 = rms_scale(h)
    hn, gate, up, hidden, by_core = gate_up((h * r2 * mlp_gain).astype(BF16), wg, wu, dp_size)
    part = rows // 2
    away = dot_nt(by_core[1], wd).astype(BF16)
    dy, away = lax.optimization_barrier((dy, away))
    total_wd = dot_tn(dy, hidden).astype(BF16)
    part_wd = along_z(total_wd)
    from_core = layout.swap(away, 1)

    near = (dot_nt(by_core[0], wd) + from_core.astype(F32)).astype(BF16)
    dy, near = lax.optimization_barrier((dy, near))

    def out_rows(start, count):
        return near[start * part : (start + count) * part]

    def joined(some, other):
        return (some.astype(F32) + other.astype(F32)).astype(BF16)

    far_y, far_x, x_lower, y_upper = (out_rows(at, 1) for at in (6, 7, 3, 4))
    dy, far_x, far_y, x_lower, y_upper = lax.optimization_barrier(
        (dy, far_x, far_y, x_lower, y_upper)
    )
    from_x, from_y = layout.swap(far_x, 2), layout.swap(far_y, 4)
    x_lower, y_upper = layout.swap(x_lower, 2), layout.swap(y_upper, 4)
    gate, up = gate.astype(F32), up.astype(F32)
    sigma = jax.nn.sigmoid(gate)
    dhid = dot_nn(dy, wd)
    dgate = (dhid * up * sigma * (1.0 + gate * (1.0 - sigma))).astype(BF16)
    dup = (dhid * gate * sigma).astype(BF16)
    dgate, dup, from_x, from_y = lax.optimization_barrier((dgate, dup, from_x, from_y))
    x_upper, y_lower = joined(out_rows(2, 1), from_y), joined(out_rows(5, 1), from_x)
    dgate, dup, x_upper, y_lower = lax.optimization_barrier((dgate, dup, x_upper, y_lower))
    x_upper, y_lower = layout.swap(x_upper, 2), layout.swap(y_lower, 4)
    total_wg = dot_tn(hn, dgate).astype(BF16)
    dup, total_wg, x_lower, y_upper = lax.optimization_barrier((dup, total_wg, x_lower, y_upper))
    part_wg = along_z(total_wg)
    total_wu = dot_tn(hn, dup).astype(BF16)
    dup, total_wu = lax.optimization_barrier((dup, total_wu))
    part_wu = along_z(total_wu)
    dup, x_upper, y_lower = lax.optimization_barrier((dup, x_upper, y_lower))
    dhb, gain_two = hidden_back(
        mlp_gain[None], h, cotangent[0], dgate, dup, wg, wu, dp_size
    )
    gain_two = jnp.sum(gain_two, axis=0)
    dhb, part_wd = lax.optimization_barrier((dhb, part_wd))
    datt = dot_nn(dhb, wo).astype(BF16)
    total_wo = layout.from_rows(dot_tn(dhb, att).astype(BF16))
    datt, part_wg, total_wo = lax.optimization_barrier((datt, part_wg, total_wo))
    part_wo = layout.scatter(total_wo)
    dq, dkv, wd_grad, wg_grad = attend_back(
        q, datt, att, kv_all, lse, low, cosine, sine, (part_wd, part_wg), dp_size, z_size
    )
    dq, part_wu = lax.optimization_barrier((dq, part_wu))
    dq, part_wo = lax.optimization_barrier((dq, part_wo))
    wq_grad, wkv_grad, wo_grad, gains, input_grad, wu_grad = last_grads(
        layout.from_cols(xn), dq, dkv, part_wo, jnp.stack([attn_gain, gain_two]),
        activations[0], dhb, wq, wkv, (part_wu,), dp_size, z_size,
    )
    gains = layout.sum_outer(gains)
    output = h + out_rows(0, 2).astype(F32)
    output = output + jnp.concatenate([x_upper, x_lower]).astype(F32)
    output = output + jnp.concatenate([y_upper, y_lower]).astype(F32)
    wo_grad, wq_grad, wkv_grad, wd_grad, wg_grad, wu_grad = (
        layout.scatter_outer(grad)
        for grad in (wo_grad, wq_grad, wkv_grad, wd_grad, wg_grad, wu_grad)
    )
    wd_grad, wg_grad, wu_grad, input_grad, wq_grad, wo_grad, wk_grad, wv_grad = emit(
        (wd_grad, wg_grad, wu_grad), input_grad, wq_grad, wo_grad, wkv_grad
    )
    return (
        output.astype(BF16)[None],
        input_grad[None],
        gains[0],
        wq_grad,
        wk_grad,
        wv_grad,
        wo_grad,
        gains[1],
        wg_grad,
        wu_grad,
        wd_grad,
    )


def solution(mesh):
    split = P("dp", "tensor")
    tokens = P("dp", "tensor", None)
    in_specs = (
        tokens, P("dp", None), P(), split, split, split, split, P(), split, split, split, tokens,
    )
    out_specs = (tokens, tokens, P(), split, split, split, split, P(), split, split, split)
    return jax.shard_map(
        functools.partial(per_device, mesh.shape["dp"], mesh.shape["tensor"]),
        mesh=mesh, in_specs=in_specs, out_specs=out_specs, check_vma=False,
    )
```

```python
import functools
import math

import jax
import jax.numpy as jnp
from jax import lax
from jax.experimental import pallas as pl
from jax.experimental.pallas import tpu as pltpu
from jax.sharding import PartitionSpec as P

HEAD_DIM = 64
DOCS = 4
MOST_DOC = 1024
NORM_EPS = 1e-05
ROPE_THETA = 500000.0
GROUP = 8
LANES = 128
QTILE = 256
SCALE = HEAD_DIM ** (-0.5)
LOG2E = 1.4426950408889634
FAR = -1e30
NTILE = 512
STRIP = 32
LONG = 60_000_000_000
SHORT = 1_000_000

F32 = jnp.float32
BF16 = jnp.bfloat16


def dot_nn(left, right):
    return lax.dot_general(left, right, (((1,), (0,)), ((), ())), preferred_element_type=F32)


def dot_nt(left, right):
    return lax.dot_general(left, right, (((1,), (1,)), ((), ())), preferred_element_type=F32)


def dot_tn(left, right):
    return lax.dot_general(left, right, (((0,), (0,)), ((), ())), preferred_element_type=F32)


def document_starts(segments):
    doc_ids = jnp.arange(DOCS, dtype=jnp.int32)
    counts = jnp.sum((segments[:, None] == doc_ids).astype(jnp.int32), axis=0)
    before = (doc_ids < segments[:, None]).astype(jnp.int32)
    return jnp.sum(before * counts[None, :], axis=-1)


def rope_tables(positions):
    half = HEAD_DIM // 2
    frequency = jnp.exp(
        jnp.arange(half, dtype=F32) * (-2.0 * math.log(ROPE_THETA) / HEAD_DIM)
    )
    angles = positions.astype(F32)[:, None] * frequency
    cosine, sine = jnp.cos(angles), jnp.sin(angles)
    wide_cos = jnp.concatenate([cosine] * 4, axis=1)
    wide_sin = jnp.concatenate([-sine, sine, -sine, sine], axis=1)
    return wide_cos, wide_sin


def swap_halves(values):
    lane = lax.broadcasted_iota(jnp.int32, values.shape, 1)
    ahead = pltpu.roll(values, LANES - 32, 1)
    behind = pltpu.roll(values, 32, 1)
    return jnp.where((lane % 64) < 32, ahead, behind)


def fill_bias(bias_ref, low_ref, reach):
    span = bias_ref.shape[1]
    for tile in range(bias_ref.shape[0]):
        row = lax.broadcasted_iota(jnp.int32, (span, QTILE), 0)
        col = lax.broadcasted_iota(jnp.int32, (span, QTILE), 1)
        low = low_ref[0:1, tile * QTILE : (tile + 1) * QTILE]
        allowed = (row <= reach + col) & (row + tile * QTILE >= low)
        bias_ref[tile] = jnp.where(allowed, 0.0, FAR)


def spread_pair(pair, half):
    wide = pair.astype(F32)
    turned = pltpu.roll(wide, 64, 1)
    lane = lax.broadcasted_iota(jnp.int32, wide.shape, 1)
    mine = (lane // 64) == half
    even = half == 0
    first = jnp.where(mine, jnp.where(even, wide, turned), 0.0)
    second = jnp.where(mine, jnp.where(even, turned, wide), 0.0)
    return jnp.concatenate([first, second], axis=0).astype(BF16)


def gather_pair(transposed, half):
    count = transposed.shape[1] // 2
    mine = jnp.where(half == 0, transposed[:64], transposed[64:])
    return jnp.concatenate([mine[:, :count], mine[:, count:]], axis=0).T


def attend_kernel(
    reach, wide, q_ref, k_ref, v_ref, low_ref, own_ref, _, att_ref, lse_ref, all_ref,
    bias_ref, full, own_sem, send_sem, recv_sem, out_sem,
):
    head, tile, pair = pl.program_id(0), pl.program_id(1), pl.program_id(2)
    half = head % 2
    inner = pl.num_programs(1) * pl.num_programs(2)
    step = head * inner + tile * pl.num_programs(2) + pair
    ring = Ring(wide, full, own_ref.shape[0], send_sem, recv_sem)
    right = pl.ds(own_ref.shape[1] - full.shape[1], full.shape[1])

    def outward(slot, *flips):
        where = ring.whole(*flips)
        return pltpu.make_async_copy(full.at[where], all_ref.at[where, right], out_sem.at[slot])

    near = [(0, 0, 0), (0, 0, 1), (0, 1, 0), (1, 0, 0)]
    rest = [(0, 1, 1), (1, 0, 1), (1, 1, 0), (1, 1, 1)]

    @pl.when(step == 0)
    def _():
        local = pltpu.make_async_copy(own_ref.at[:, right], full.at[ring.mine()], own_sem)
        local.start()
        meet(ring.peers)
        local.wait()
        ring.start_own()
        fill_bias(bias_ref, low_ref, reach)

    pl.when(step == 2 * inner)(ring.first_halves)
    pl.when(step == 4 * inner)(ring.second_halves)

    keys = pl.ds(pl.multiple_of(tile * QTILE, QTILE), bias_ref.shape[1])
    queries = spread_pair(q_ref[...], half)
    bias = bias_ref[tile]
    score = dot_nt(k_ref[keys, :], queries)
    score = score + jnp.concatenate([bias, bias], axis=1)
    top = jnp.max(score, axis=0, keepdims=True) * (SCALE * LOG2E)
    weight = jnp.exp2(score * (SCALE * LOG2E) - top)
    total = jnp.sum(weight, axis=0, keepdims=True)
    result = dot_tn(v_ref[keys, :], weight.astype(BF16)) / total
    att_ref[...] = gather_pair(result, half).astype(BF16)
    lse_ref[0] = top + jnp.log2(total)

    @pl.when(step == pl.num_programs(0) * inner - 1)
    def _():
        ring.from_sibling("own", 0, 1)
        for slot, flips in enumerate(near):
            outward(slot, *flips).start()
        ring.far_halves()
        for name in ("x", "y", "d"):
            ring.from_sibling(name, 0, 1)
        for slot, flips in enumerate(rest):
            outward(4 + slot, *flips).start()
        for slot, flips in enumerate(near + rest):
            outward(slot, *flips).wait()
        ring.sent()


def attend(q, kv, low, grad, grads, dp_size):
    rows, width = q.shape
    keys = kv.shape[0]
    reach = keys - rows
    tiles = rows // QTILE
    pairs = width // LANES
    heads = kv.shape[1] // LANES
    per_head = pairs // heads
    span = reach + QTILE
    right = (grads.shape[0], grads.shape[1] // 2)
    far = pl.BlockSpec(memory_space=pl.ANY)
    return pl.pallas_call(
        functools.partial(attend_kernel, reach, 2 * math.isqrt(dp_size // GROUP)),
        grid=(heads, tiles, per_head),
        in_specs=[
            pl.BlockSpec((QTILE, LANES), lambda a, t, p: (t, a * per_head + p)),
            pl.BlockSpec((keys, LANES), lambda a, t, p: (0, 2 * (a // 2))),
            pl.BlockSpec((keys, LANES), lambda a, t, p: (0, 2 * (a // 2) + 1)),
            pl.BlockSpec((1, rows), lambda a, t, p: (0, 0)),
            far,
            far,
        ],
        out_specs=[
            pl.BlockSpec((QTILE, LANES), lambda a, t, p: (t, a * per_head + p)),
            pl.BlockSpec((1, 1, 2 * QTILE), lambda a, t, p: ((a * tiles + t) * per_head + p, 0, 0)),
            far,
        ],
        out_shape=[
            jax.ShapeDtypeStruct((rows, width), BF16),
            jax.ShapeDtypeStruct((pairs * tiles, 1, 2 * QTILE), F32),
            jax.ShapeDtypeStruct(grads.shape, BF16),
        ],
        scratch_shapes=[
            pltpu.VMEM((tiles, span, QTILE), F32),
            pltpu.VMEM(right, BF16),
            pltpu.SemaphoreType.DMA,
            pltpu.SemaphoreType.DMA((Ring.COPIES,)),
            pltpu.SemaphoreType.DMA((Ring.COPIES,)),
            pltpu.SemaphoreType.DMA((8,)),
        ],
        input_output_aliases={5: 2},
        compiler_params=pltpu.CompilerParams(
            collective_id=7, has_side_effects=True, vmem_limit_bytes=56 << 20
        ),
        cost_estimate=pl.CostEstimate(
            flops=16 * rows * span * LANES * pairs,
            bytes_accessed=4 * rows * width + 2 * keys * kv.shape[1],
            transcendentals=2 * rows * span * pairs,
        ),
    )(q, kv, kv, low, grad, grads)


def attend_back_kernel(
    reach, wide, z_size, mlp_count,
    q_ref, do_ref, o_ref, k_ref, v_ref, lse_ref, low_ref, cos_ref, sin_ref, cos_all, sin_all,
    *refs,
):
    mlp_ins, refs = refs[:mlp_count], refs[mlp_count:]
    dq_ref, dkv_ref = refs[:2]
    mlp_outs, refs = refs[2 : 2 + mlp_count], refs[2 + mlp_count :]
    bias_ref, dk_acc, dv_acc, own_part, send_part, recv_part, kv_send, kv_recv = refs[:8]
    home = refs[8:]
    block, half, tile, pair = (pl.program_id(at) for at in range(4))
    steps = pl.num_programs(1) * pl.num_programs(2) * pl.num_programs(3)
    inner = (half * pl.num_programs(2) + tile) * pl.num_programs(3) + pair
    step = block * steps + inner
    blocks = own_part.shape[0]
    rows = own_part.shape[1]
    count = reach // rows
    place = lax.axis_index("tensor")

    def exchange(at, distance):
        return pltpu.make_async_remote_copy(
            src_ref=send_part.at[at, pl.ds((count - distance) * rows, rows)],
            dst_ref=recv_part.at[at, distance - 1],
            send_sem=kv_send.at[at, distance - 1], recv_sem=kv_recv.at[at, distance - 1],
            device_id={"tensor": (place + z_size - distance) % z_size}, device_id_type=MESH,
        )

    def each_exchange(at, condition, action):
        for distance in range(1, count + 1):
            pl.when(condition(distance))(
                functools.partial(action, exchange(at, distance), at, distance)
            )

    @pl.when(step == 0)
    def _():
        greet(along_peers(place, z_size) + [device for _, device in others(wide)[1]])
        for copy in send_home(wide, mlp_ins, mlp_outs, *home):
            copy.start()
        fill_bias(bias_ref, low_ref, reach)

    @pl.when(inner == 0)
    def _():
        dk_acc[...] = jnp.zeros_like(dk_acc)
        dv_acc[...] = jnp.zeros_like(dv_acc)

    keys = pl.ds(pl.multiple_of(tile * QTILE, QTILE), bias_ref.shape[1])
    queries = spread_pair(q_ref[...], half)
    grads = spread_pair(do_ref[...], half)
    product = (do_ref[...].astype(F32) * o_ref[...].astype(F32)).T
    row_dot = jnp.concatenate(
        [
            jnp.sum(product[:64], axis=0, keepdims=True),
            jnp.sum(product[64:], axis=0, keepdims=True),
        ],
        axis=1,
    )
    bias = bias_ref[tile]
    key, value = k_ref[keys, :], v_ref[keys, :]
    score = dot_nt(key, queries) + jnp.concatenate([bias, bias], axis=1)
    weight = jnp.exp2(score * (SCALE * LOG2E) - lse_ref[0])
    dv_acc[keys, :] += dot_nn(weight.astype(BF16), grads)
    dscore = (weight * (dot_nt(value, grads) - row_dot)).astype(BF16)
    dk_acc[keys, :] += dot_nn(dscore, queries)
    dq = gather_pair(dot_tn(key, dscore), half) * SCALE
    dq_ref[...] = (dq * cos_ref[...] - swap_halves(dq) * sin_ref[...]).astype(BF16)

    @pl.when(inner == steps - 1)
    def _():
        send_part[block, :, :LANES] = (dk_acc[:reach] * SCALE).astype(BF16)
        send_part[block, :, LANES:] = dv_acc[:reach].astype(BF16)
        own_part[block, :, :LANES] = dk_acc[reach:] * SCALE
        own_part[block, :, LANES:] = dv_acc[reach:]
        each_exchange(block, lambda distance: place >= distance, lambda copy, *_: copy.start())

    @pl.when(step == blocks * steps - 1)
    def _():
        def collect(copy, at, distance):
            copy.wait_recv()
            own_part[at] += recv_part[at, distance - 1].astype(F32)

        for at in range(blocks):
            each_exchange(at, lambda distance: place + distance < z_size, collect)
            dkey = own_part[at, :, :LANES]
            dkey = dkey * cos_all[...] - swap_halves(dkey) * sin_all[...]
            dkv_ref[:, 2 * at * LANES : (2 * at + 1) * LANES] = dkey.astype(BF16)
            dkv_ref[:, (2 * at + 1) * LANES : (2 * at + 2) * LANES] = own_part[
                at, :, LANES:
            ].astype(BF16)
        for at in range(blocks):
            each_exchange(
                at, lambda distance: place >= distance, lambda copy, *_: copy.wait_send()
            )
        for copy in send_home(wide, mlp_ins, mlp_outs, *home):
            copy.wait()


def attend_back(q, do, att, kv, lse, low, cosine, sine, mlp, dp_size, z_size):
    rows, width = q.shape
    keys = kv.shape[0]
    reach = keys - rows
    tiles = rows // QTILE
    pairs = width // LANES
    heads = kv.shape[1] // LANES
    per_head = pairs // heads
    span = reach + QTILE
    blocks = heads // 2

    def pair_at(g, h, t, p):
        return (t, (2 * g + h) * per_head + p)

    def whole(shape):
        return pl.BlockSpec(shape, lambda g, h, t, p: (0, 0), pipeline_mode=pl.Buffered(1))

    table = pl.BlockSpec((QTILE, LANES), lambda g, h, t, p: (t, 0))
    return pl.pallas_call(
        functools.partial(
            attend_back_kernel, reach, 2 * math.isqrt(dp_size // GROUP), z_size, len(mlp)
        ),
        grid=(blocks, 2, tiles, per_head),
        in_specs=[
            pl.BlockSpec((QTILE, LANES), pair_at),
            pl.BlockSpec((QTILE, LANES), pair_at),
            pl.BlockSpec((QTILE, LANES), pair_at),
            pl.BlockSpec((keys, LANES), lambda g, h, t, p: (0, 2 * g)),
            pl.BlockSpec((keys, LANES), lambda g, h, t, p: (0, 2 * g + 1)),
            pl.BlockSpec(
                (1, 1, 2 * QTILE),
                lambda g, h, t, p: (((2 * g + h) * tiles + t) * per_head + p, 0, 0),
            ),
            whole((1, rows)),
            table,
            table,
            whole((rows, LANES)),
            whole((rows, LANES)),
        ]
        + [pl.BlockSpec(memory_space=pl.ANY)] * len(mlp),
        out_specs=[
            pl.BlockSpec((QTILE, LANES), pair_at),
            pl.BlockSpec((rows, kv.shape[1]), lambda g, h, t, p: (0, 0)),
        ]
        + [pl.BlockSpec(memory_space=pl.ANY)] * len(mlp),
        out_shape=[
            jax.ShapeDtypeStruct((rows, width), BF16),
            jax.ShapeDtypeStruct((rows, kv.shape[1]), BF16),
        ]
        + home_shapes(mlp),
        scratch_shapes=[
            pltpu.VMEM((tiles, span, QTILE), F32),
            pltpu.VMEM((keys, LANES), F32),
            pltpu.VMEM((keys, LANES), F32),
            pltpu.VMEM((blocks, rows, 2 * LANES), F32),
            pltpu.VMEM((blocks, reach, 2 * LANES), BF16),
            pltpu.VMEM((blocks, reach // rows, rows, 2 * LANES), BF16),
            pltpu.SemaphoreType.DMA((blocks, reach // rows)),
            pltpu.SemaphoreType.DMA((blocks, reach // rows)),
        ]
        + home_scratch(mlp),
        compiler_params=pltpu.CompilerParams(
            collective_id=5, has_side_effects=True, vmem_limit_bytes=60 << 20
        ),
        cost_estimate=pl.CostEstimate(
            flops=40 * rows * span * LANES * pairs,
            bytes_accessed=8 * rows * width + 4 * keys * kv.shape[1],
            transcendentals=2 * rows * span * pairs,
        ),
    )(q, do, att, kv, kv, lse, low, cosine, sine, cosine, sine, *mlp)


MESH = pl.DeviceIdType.MESH


def neighbours(wide):
    dp = lax.axis_index("dp")
    core, col, row = dp % 2, (dp // 2) % 2, (dp // (2 * wide)) % 2
    sibling = dp + 1 - 2 * core
    beside = dp + 2 - 4 * col
    above = dp + 2 * wide - 4 * wide * row
    return (row, col, core), (sibling, beside, above)


def meet(peers):
    barrier = pltpu.get_barrier_semaphore()
    for peer in peers:
        pl.semaphore_signal(barrier, inc=1, device_id={"dp": peer}, device_id_type=MESH)
    pl.semaphore_wait(barrier, len(peers))


def others(wide):
    (row, col, core), _ = neighbours(wide)
    base = lax.axis_index("dp") - (2 * wide * row + 2 * col + core)
    found = []
    for flip in range(1, GROUP):
        y, x, c = (row + flip // 4) % 2, (col + flip // 2) % 2, (core + flip) % 2
        found.append((4 * y + 2 * x + c, {"dp": base + 2 * wide * y + 2 * x + c}))
    return 4 * row + 2 * col + core, found


def along_peers(place, z_size):
    return [{"tensor": (place + step) % z_size} for step in range(1, z_size)]


def greet(peers):
    barrier = pltpu.get_barrier_semaphore()
    for peer in peers:
        pl.semaphore_signal(barrier, inc=1, device_id=peer, device_id_type=MESH)
    pl.semaphore_wait(barrier, len(peers))


def send_home(wide, ins, outs, own_sem, send_sem, recv_sem):
    mine, found = others(wide)
    copies = []
    for at, (src, dst) in enumerate(zip(ins, outs)):
        part, cols = dst.shape[0], src.shape[1]
        here = pl.ds(pl.multiple_of(mine * cols, LANES), cols)
        for index, (other, device) in enumerate(found):
            copies.append(
                pltpu.make_async_remote_copy(
                    src_ref=src.at[pl.ds(pl.multiple_of(other * part, part), part)],
                    dst_ref=dst.at[:, here],
                    send_sem=send_sem.at[at, index], recv_sem=recv_sem.at[at, index],
                    device_id=device, device_id_type=MESH,
                )
            )
        own = src.at[pl.ds(pl.multiple_of(mine * part, part), part)]
        copies.append(pltpu.make_async_copy(own, dst.at[:, here], own_sem.at[at]))
    return copies


def home_shapes(arrays):
    return [jax.ShapeDtypeStruct((a.shape[0] // GROUP, GROUP * a.shape[1]), BF16) for a in arrays]


def home_scratch(arrays):
    count = len(arrays)
    return [
        pltpu.SemaphoreType.DMA((count,)),
        pltpu.SemaphoreType.DMA((count, GROUP - 1)),
        pltpu.SemaphoreType.DMA((count, GROUP - 1)),
    ]


SIB, XN, YN = 0, 1, 2


def spread_kernel(wide, z_size, mlp_count, x_ref, gain_ref, *refs):
    attn_count = (len(refs) - 10) // 2 - mlp_count
    count = mlp_count + attn_count
    ins, xn_ref, outs = refs[:count], refs[count], refs[count + 1 : 2 * count + 1]
    x_all, x_sem, own_sem, send_sem, recv_sem, z_send, z_recv, ring_send, ring_recv = refs[
        2 * count + 1 :
    ]
    first = mlp_count
    ring = Ring(wide, outs[first], ins[first].shape[0], ring_send, ring_recv)
    place = lax.axis_index("tensor")
    mine, found = others(wide)
    greet(along_peers(place, z_size) + [device for _, device in found])

    local, copies = [], []
    for at in range(mlp_count):
        src, dst = ins[at], outs[at]
        rows, cols = src.shape[0], dst.shape[1]
        here = pl.ds(pl.multiple_of(mine * rows, rows), rows)
        for index, (other, device) in enumerate(found):
            copies.append(
                pltpu.make_async_remote_copy(
                    src_ref=src.at[:, pl.ds(pl.multiple_of(other * cols, LANES), cols)],
                    dst_ref=dst.at[here],
                    send_sem=send_sem.at[at, index], recv_sem=recv_sem.at[at, index],
                    device_id=device, device_id_type=MESH,
                )
            )
        own = src.at[:, pl.ds(pl.multiple_of(mine * cols, LANES), cols)]
        local.append(pltpu.make_async_copy(own, dst.at[here], own_sem.at[at]))

    def block(at, origin):
        cols = ins[at].shape[1]
        part = pl.ds(pl.multiple_of(origin * cols, LANES), cols)
        return outs[at].at[ring.mine() if at == first else slice(None), part]

    def hop(at, way, step, receive=False):
        sign = 1 - 2 * way
        origin = place - sign * (step if receive else step - 1)
        slot = 2 * (step - 1) + way
        src = block(at, origin) if receive or step > 1 else ins[at]
        return pltpu.make_async_remote_copy(
            src_ref=src, dst_ref=block(at, origin),
            send_sem=z_send.at[at - mlp_count, slot], recv_sem=z_recv.at[at - mlp_count, slot],
            device_id={"tensor": (place + z_size + sign) % z_size}, device_id_type=MESH,
        )

    def sends(way, step):
        if way == 0:
            return (place + 1 < z_size) & (place >= step - 1)
        return (place >= 1) & (place + step - 1 < z_size)

    def receives(way, step):
        return place >= step if way == 0 else place + step < z_size

    for at in range(mlp_count, count):
        local.append(pltpu.make_async_copy(ins[at], block(at, place), own_sem.at[at]))
        for way in range(2):
            pl.when(sends(way, 1))(lambda: hop(at, way, 1).start())
    for copy in copies + local:
        copy.start()
    load = pltpu.make_async_copy(x_ref, x_all, x_sem)
    load.start()
    load.wait()

    @pl.loop(0, x_all.shape[0] // STRIP)
    def _(at):
        here = pl.ds(pl.multiple_of(at * STRIP, STRIP), STRIP)
        value = x_all[here, :].astype(F32)
        xn_ref[here, :] = (value * rms_scale(value) * gain_ref[...]).astype(BF16)

    def advance(at, step):
        for way in range(2):
            pl.when(receives(way, step))(lambda: hop(at, way, step, True).wait_recv())
            if step + 1 < z_size:
                pl.when(sends(way, step + 1))(lambda: hop(at, way, step + 1).start())

    for step in range(1, z_size):
        advance(first, step)
    local.pop(first).wait()
    ring.start_own()
    stages = [ring.first_halves, ring.second_halves]
    for step in range(1, z_size):
        for at in range(first + 1, count):
            advance(at, step)
        if stages:
            stages.pop(0)()
    for stage in stages:
        stage()
    ring.far_halves()
    for name in ("own", "x", "y", "d"):
        ring.from_sibling(name, 0, 1)
    ring.sent()
    for step in range(1, z_size):
        for at in range(mlp_count, count):
            for way in range(2):
                pl.when(sends(way, step))(lambda: hop(at, way, step).wait_send())
    for copy in local + copies:
        copy.wait()


def spread_weights(x, gain, mlp, attn, dp_size, z_size):
    count = len(mlp) + len(attn)
    spec = pl.BlockSpec(memory_space=pl.ANY)
    near = pl.BlockSpec(memory_space=pltpu.VMEM)
    out = [jax.ShapeDtypeStruct(x.shape, BF16)]
    out += [jax.ShapeDtypeStruct((GROUP * w.shape[0], w.shape[1] // GROUP), BF16) for w in mlp]
    out += [
        jax.ShapeDtypeStruct(((1 if at else GROUP) * w.shape[0], z_size * w.shape[1]), BF16)
        for at, w in enumerate(attn)
    ]
    return pl.pallas_call(
        functools.partial(spread_kernel, 2 * math.isqrt(dp_size // GROUP), z_size, len(mlp)),
        in_specs=[spec, near] + [spec] * count,
        out_specs=[near] + [spec] * count,
        out_shape=out,
        scratch_shapes=[
            pltpu.VMEM(x.shape, BF16),
            pltpu.SemaphoreType.DMA,
            pltpu.SemaphoreType.DMA((count,)),
            pltpu.SemaphoreType.DMA((len(mlp), GROUP - 1)),
            pltpu.SemaphoreType.DMA((len(mlp), GROUP - 1)),
            pltpu.SemaphoreType.DMA((len(attn), 2 * (z_size - 1))),
            pltpu.SemaphoreType.DMA((len(attn), 2 * (z_size - 1))),
            pltpu.SemaphoreType.DMA((Ring.COPIES,)),
            pltpu.SemaphoreType.DMA((Ring.COPIES,)),
        ],
        compiler_params=pltpu.CompilerParams(collective_id=2, has_side_effects=True),
        cost_estimate=pl.CostEstimate(flops=LONG, bytes_accessed=0, transcendentals=0),
    )(x, gain, *mlp, *attn)


class Ring:
    FLIP = {SIB: (0, 0, 1), XN: (0, 1, 0), YN: (1, 0, 0)}
    COPIES = 14

    def __init__(self, wide, ref, rows, send_sem, recv_sem):
        (self.row, self.col, self.core), self.peers = neighbours(wide)
        self.ref, self.rows, self.part = ref, rows, rows // 2
        self.send_sem, self.recv_sem = send_sem, recv_sem
        self.sends = {}
        for half in range(2):
            self.sends["own", XN, half] = (2 + half, 0, 0, 0, half)
            self.sends["own", YN, half] = (4 + half, 0, 0, 0, half)
            self.sends["own", SIB, half] = (0 + half, 0, 0, 0, half)
        for half in range(2):
            self.sends["x", SIB, half] = (6 + half, 0, 1, 0, half)
            self.sends["y", SIB, half] = (8 + half, 1, 0, 0, half)
            self.sends["d", SIB, half] = (10 + half, 1, 1, 0, half)
        self.sends["x", YN, 0] = (12, 0, 1, 0, 0)
        self.sends["y", XN, 1] = (13, 1, 0, 0, 1)

    def place(self, dy, dx, dc, half):
        p = 4 * ((self.row + dy) % 2) + 2 * ((self.col + dx) % 2) + (self.core + dc) % 2
        return pl.ds(pl.multiple_of(p * self.rows + half * self.part, self.part), self.part)

    def mine(self):
        p = 4 * self.row + 2 * self.col + self.core
        return pl.ds(pl.multiple_of(p * self.rows, self.rows), self.rows)

    def whole(self, dy, dx, dc):
        p = 4 * ((self.row + dy) % 2) + 2 * ((self.col + dx) % 2) + (self.core + dc) % 2
        return pl.ds(pl.multiple_of(p * self.rows, self.rows), self.rows)

    def copy(self, slot, dy, dx, dc, half, peer):
        where = self.place(dy, dx, dc, half)
        return pltpu.make_async_remote_copy(
            src_ref=self.ref.at[where], dst_ref=self.ref.at[where],
            send_sem=self.send_sem.at[slot], recv_sem=self.recv_sem.at[slot],
            device_id={"dp": self.peers[peer]}, device_id_type=MESH,
        )

    def start(self, name, peer, half):
        self.copy(*self.sends[name, peer, half], peer).start()

    def arrived(self, name, peer, half):
        slot, dy, dx, dc, half = self.sends[name, peer, half]
        fy, fx, fc = self.FLIP[peer]
        self.copy(slot, (dy + fy) % 2, (dx + fx) % 2, (dc + fc) % 2, half, peer).wait_recv()

    def start_own(self):
        for half in range(2):
            for peer in (XN, YN, SIB):
                self.start("own", peer, half)

    def first_halves(self):
        self.arrived("own", XN, 0)
        self.start("x", YN, 0)
        self.start("x", SIB, 0)
        self.arrived("own", YN, 0)
        self.start("y", SIB, 0)

    def second_halves(self):
        self.arrived("own", YN, 1)
        self.start("y", XN, 1)
        self.start("y", SIB, 1)
        self.arrived("own", XN, 1)
        self.start("x", SIB, 1)

    def far_halves(self):
        self.arrived("x", YN, 0)
        self.start("d", SIB, 0)
        self.arrived("y", XN, 1)
        self.start("d", SIB, 1)

    def from_sibling(self, name, *halves):
        for half in halves:
            self.arrived(name, SIB, half)

    def sent(self):
        for (name, peer, half), entry in self.sends.items():
            self.copy(*entry, peer).wait_send()


def project_kernel(
    wide, z_size, x_ref, cos_ref, sin_ref, wkv_ref, wq_ref, wo_ref, grad_ref,
    q_ref, kv_ref, wq_out, wo_out, grad_out,
    wkv_all, wq_all, wo_all, grad_all, keys, own_sem, send_sem, recv_sem, kv_send, kv_recv, out_sem,
):
    place = lax.axis_index("tensor")
    rows = x_ref.shape[0]
    count = keys.shape[0] // rows - 1
    left = pl.ds(0, grad_all.shape[1])
    parts = (
        (wq_ref, wq_all, wq_out), (wo_ref, wo_all, wo_out),
        (grad_ref.at[:, left], grad_all, grad_out.at[:, left]),
    )
    rings = [
        Ring(wide, full, part.shape[0], send_sem.at[at], recv_sem.at[at])
        for at, (part, full, _) in enumerate(parts)
    ]
    local = [
        pltpu.make_async_copy(part, full.at[ring.mine()], own_sem.at[at])
        for at, ((part, full, _), ring) in enumerate(zip(parts, rings))
    ]
    outward = [
        pltpu.make_async_copy(full, out, out_sem.at[at])
        for at, (_, full, out) in enumerate(parts)
    ]
    load = pltpu.make_async_copy(wkv_ref, wkv_all, own_sem.at[len(parts)])
    for copy in local + [load]:
        copy.start()
    keys[: count * rows, :] = jnp.zeros((count * rows, keys.shape[1]), BF16)
    greet([{"dp": peer} for peer in rings[0].peers] + along_peers(place, z_size))
    for copy in local:
        copy.wait()

    def rotated(value):
        return (value * cos_ref[...] + swap_halves(value) * sin_ref[...]).astype(BF16)

    def hop(step):
        return pltpu.make_async_remote_copy(
            src_ref=keys.at[pl.ds((count - step + 1) * rows, rows)],
            dst_ref=keys.at[pl.ds((count - step) * rows, rows)],
            send_sem=kv_send.at[step - 1], recv_sem=kv_recv.at[step - 1],
            device_id={"tensor": (place + 1) % z_size}, device_id_type=MESH,
        )

    def pass_keys(step):
        if step > 1:
            pl.when(place >= step - 1)(lambda: hop(step - 1).wait_recv())
        if step <= count:
            sends = (place + 1 < z_size) & (place >= step - 1)
            pl.when(sends)(lambda: hop(step).start())

    def finish(ring):
        ring.far_halves()
        for name in ("own", "x", "y", "d"):
            ring.from_sibling(name, 0, 1)

    rings[0].start_own()
    load.wait()

    @pl.loop(0, wkv_all.shape[1] // (2 * LANES))
    def _(at):
        n = pl.ds(pl.multiple_of(at * 2 * LANES, LANES), 2 * LANES)
        value = dot_nn(x_ref[...], wkv_all[:, n])
        both = jnp.concatenate([rotated(value[:, :LANES]), value[:, LANES:].astype(BF16)], axis=1)
        keys[pl.ds(count * rows, rows), n] = both

    pass_keys(1)
    rings[0].first_halves()
    rings[0].second_halves()
    rings[1].start_own()
    finish(rings[0])
    outward[0].start()

    @pl.loop(0, wq_all.shape[1] // (2 * LANES))
    def _(at):
        n = pl.ds(pl.multiple_of(at * 2 * LANES, LANES), 2 * LANES)
        value = dot_nn(x_ref[...], wq_all[:, n])
        both = [rotated(value[:, :LANES]), rotated(value[:, LANES:])]
        q_ref[:, n] = jnp.concatenate(both, axis=1)

    for step in range(2, count + 1):
        pass_keys(step)
    rings[1].first_halves()
    rings[1].second_halves()
    rings[2].start_own()
    finish(rings[1])
    outward[1].start()
    rings[2].first_halves()
    rings[2].second_halves()
    finish(rings[2])
    outward[2].start()
    pass_keys(count + 1)
    keys_out = pltpu.make_async_copy(keys, kv_ref, out_sem.at[3])
    keys_out.start()
    for step in range(1, count + 1):
        sends = (place + 1 < z_size) & (place >= step - 1)
        pl.when(sends)(lambda: hop(step).wait_send())
    for ring in rings:
        ring.sent()
    for copy in outward + [keys_out]:
        copy.wait()


def project(x, cosine, sine, wkv, wq, wo, grad, reach, dp_size, z_size):
    rows, width = x.shape
    far = pl.BlockSpec(memory_space=pl.ANY)
    near = pl.BlockSpec(memory_space=pltpu.VMEM)
    whole = [(GROUP * w.shape[0], w.shape[1]) for w in (wq, wo)]
    keys = (reach + rows, wkv.shape[1])
    grads = (GROUP * grad.shape[0], grad.shape[1])
    left = (grads[0], grads[1] // 2)
    return pl.pallas_call(
        functools.partial(project_kernel, 2 * math.isqrt(dp_size // GROUP), z_size),
        in_specs=[near] * 3 + [far] * 4,
        out_specs=[near] + [far] * 4,
        out_shape=[jax.ShapeDtypeStruct((rows, wq.shape[1]), BF16)]
        + [jax.ShapeDtypeStruct(shape, BF16) for shape in [keys] + whole + [grads]],
        scratch_shapes=[pltpu.VMEM(shape, BF16) for shape in [wkv.shape] + whole + [left, keys]]
        + [
            pltpu.SemaphoreType.DMA((4,)),
            pltpu.SemaphoreType.DMA((3, Ring.COPIES)),
            pltpu.SemaphoreType.DMA((3, Ring.COPIES)),
            pltpu.SemaphoreType.DMA((reach // rows,)),
            pltpu.SemaphoreType.DMA((reach // rows,)),
            pltpu.SemaphoreType.DMA((4,)),
        ],
        compiler_params=pltpu.CompilerParams(
            collective_id=3, has_side_effects=True, vmem_limit_bytes=56 << 20
        ),
        cost_estimate=pl.CostEstimate(
            flops=2 * LONG, bytes_accessed=0, transcendentals=0
        ),
    )(x, cosine, sine, wkv, wq, wo, grad)


def gate_up_kernel(
    wide, own_ref, wg_ref, wu_ref, all_ref, gate_ref, up_ref, hid_ref, core_ref,
    full, stage, wg_all, wu_all, own_sem, load_sem, send_sem, recv_sem, out_sem, all_sem,
):
    rows = own_ref.shape[0]
    cols = gate_ref.shape[1]
    ring = Ring(wide, full, rows, send_sem, recv_sem)
    local = pltpu.make_async_copy(own_ref, full.at[ring.mine()], own_sem)
    local.start()
    loads = [
        pltpu.make_async_copy(wg_ref, wg_all, load_sem.at[0]),
        pltpu.make_async_copy(wu_ref, wu_all, load_sem.at[1]),
    ]
    for copy in loads:
        copy.start()
    meet(ring.peers)
    local.wait()
    ring.start_own()
    for copy in loads:
        copy.wait()

    def out_copies(slot, places):
        where, core, chip = places
        return [
            pltpu.make_async_copy(stage.at[slot, i], ref.at[where], out_sem.at[slot, i])
            for i, ref in enumerate((gate_ref, up_ref, hid_ref))
        ] + [
            pltpu.make_async_copy(stage.at[slot, 2], core_ref.at[core, chip], out_sem.at[slot, 3]),
            pltpu.make_async_copy(full.at[where], all_ref.at[where], all_sem.at[slot]),
        ]

    def step_place(step):
        phase, i = step // 4, step % 4
        high, low = phase // 2, phase % 2
        first, last = (1 - high) * (1 - low), high * low
        middle = high + low - 2 * last
        half = (first + last) * (i % 2) + high * (1 - low)
        dx = middle * (1 - i % 2) + last
        dy = middle * (i % 2) + last
        part = rows // 2
        chip_rows = pl.ds(pl.multiple_of((2 * dy + dx) * rows + half * part, part), part)
        return ring.place(dy, dx, i // 2, half), i // 2, chip_rows

    @pl.loop(0, 16)
    def _(step):
        pl.when(step == 2)(lambda: ring.from_sibling("own", 0, 1))
        pl.when(step == 4)(ring.first_halves)

        @pl.when(step == 6)
        def _():
            ring.from_sibling("x", 0)
            ring.from_sibling("y", 0)

        pl.when(step == 8)(ring.second_halves)

        @pl.when(step == 10)
        def _():
            ring.from_sibling("x", 1)
            ring.from_sibling("y", 1)

        pl.when(step == 12)(ring.far_halves)
        pl.when(step == 14)(lambda: ring.from_sibling("d", 0, 1))

        slot = step % 2
        places = step_place(step)

        @pl.when(step >= 2)
        def _():
            for copy in out_copies(slot, step_place(step - 2)):
                copy.wait()

        x = full[places[0], :]

        @pl.loop(0, cols // NTILE)
        def _(at):
            n = pl.ds(pl.multiple_of(at * NTILE, NTILE), NTILE)
            gate = dot_nn(x, wg_all[:, n])
            up = dot_nn(x, wu_all[:, n])
            stage[slot, 0, :, n] = gate.astype(BF16)
            stage[slot, 1, :, n] = up.astype(BF16)
            stage[slot, 2, :, n] = (gate * up / (1.0 + jnp.exp(-gate))).astype(BF16)

        for copy in out_copies(slot, places):
            copy.start()

    for step in (14, 15):
        for copy in out_copies(step % 2, step_place(step)):
            copy.wait()
    ring.sent()


def gate_up(hn, wg, wu, dp_size):
    rows, width = hn.shape
    cols = wg.shape[1]
    tokens = GROUP * rows
    far = pl.BlockSpec(memory_space=pl.ANY)
    return pl.pallas_call(
        functools.partial(gate_up_kernel, 2 * math.isqrt(dp_size // GROUP)),
        in_specs=[far] * 3,
        out_specs=[far] * 5,
        out_shape=[jax.ShapeDtypeStruct((tokens, width), BF16)]
        + [jax.ShapeDtypeStruct((tokens, cols), BF16)] * 3
        + [jax.ShapeDtypeStruct((2, tokens // 2, cols), BF16)],
        scratch_shapes=[
            pltpu.VMEM((tokens, width), BF16),
            pltpu.VMEM((2, 3, rows // 2, cols), BF16),
            pltpu.VMEM(wg.shape, BF16),
            pltpu.VMEM(wu.shape, BF16),
            pltpu.SemaphoreType.DMA,
            pltpu.SemaphoreType.DMA((2,)),
            pltpu.SemaphoreType.DMA((Ring.COPIES,)),
            pltpu.SemaphoreType.DMA((Ring.COPIES,)),
            pltpu.SemaphoreType.DMA((2, 4)),
            pltpu.SemaphoreType.DMA((2,)),
        ],
        compiler_params=pltpu.CompilerParams(
            collective_id=1, has_side_effects=True, vmem_limit_bytes=56 << 20
        ),
        cost_estimate=pl.CostEstimate(
            flops=SHORT, bytes_accessed=0, transcendentals=0
        ),
    )(hn, wg, wu)


FAR_CHUNK, X_CHUNK, Y_CHUNK, OWN_CHUNK = range(4)


class Reduce:
    COPIES = 10

    def __init__(self, wide, parts, cores, far, near, send_sem, recv_sem):
        self.at, self.peers = neighbours(wide)
        self.parts, self.cores, self.far, self.near = parts, cores, far, near
        self.send_sem, self.recv_sem = send_sem, recv_sem
        self.half = parts.shape[2] // 2

    @staticmethod
    def scratch(rows, cols):
        return [
            pltpu.VMEM((2, 4, rows, cols), BF16),
            pltpu.VMEM((4, rows, cols), BF16),
            pltpu.VMEM((2, rows // 2, cols), BF16),
            pltpu.VMEM((2, rows, cols), BF16),
            pltpu.SemaphoreType.DMA((Reduce.COPIES,)),
            pltpu.SemaphoreType.DMA((Reduce.COPIES,)),
        ]

    def chunk(self, step):
        slot, other = step // 2, 1 - step % 2
        row, col, core = self.at
        dy, dx = 1 - slot % 2, 1 - slot // 2
        place = 4 * ((row + dy) % 2) + 2 * ((col + dx) % 2) + (core + other) % 2
        return place, self.parts.at[other, slot]

    def copy(self, name):
        upper, lower = pl.ds(0, self.half), pl.ds(self.half, self.half)
        mine = self.parts.at[0]
        table = {
            "far0": (self.parts.at[1, FAR_CHUNK], self.cores.at[FAR_CHUNK], SIB),
            "x": (self.parts.at[1, X_CHUNK], self.cores.at[X_CHUNK], SIB),
            "y": (self.parts.at[1, Y_CHUNK], self.cores.at[Y_CHUNK], SIB),
            "own": (self.parts.at[1, OWN_CHUNK], self.cores.at[OWN_CHUNK], SIB),
            "far_x": (mine.at[FAR_CHUNK, lower], self.far.at[0], XN),
            "far_y": (mine.at[FAR_CHUNK, upper], self.far.at[1], YN),
            "x_upper": (mine.at[X_CHUNK, upper], self.near.at[0, upper], XN),
            "x_lower": (mine.at[X_CHUNK, lower], self.near.at[0, lower], XN),
            "y_upper": (mine.at[Y_CHUNK, upper], self.near.at[1, upper], YN),
            "y_lower": (mine.at[Y_CHUNK, lower], self.near.at[1, lower], YN),
        }
        src, dst, peer = table[name]
        at = list(table).index(name)
        return pltpu.make_async_remote_copy(
            src_ref=src, dst_ref=dst, send_sem=self.send_sem.at[at],
            recv_sem=self.recv_sem.at[at], device_id={"dp": self.peers[peer]},
            device_id_type=MESH,
        )

    def start(self, *names):
        for name in names:
            self.copy(name).start()

    def add(self, slot, start, other):
        count = other.shape[0] // STRIP

        @pl.loop(0, count)
        def _(at):
            here = pl.ds(pl.multiple_of(start + at * STRIP, STRIP), STRIP)
            there = pl.ds(pl.multiple_of(at * STRIP, STRIP), STRIP)
            value = self.parts[0, slot, here, :].astype(F32) + other[there, :].astype(F32)
            self.parts[0, slot, here, :] = value.astype(BF16)

    def merge_core(self, slot, name):
        self.copy(name).wait_recv()
        self.add(slot, 0, self.cores.at[slot])

    def after(self, step):
        names = ("far0", "x", "y", "own")
        for slot in range(4):
            pl.when(step == 2 * slot)(functools.partial(self.start, names[slot]))

        @pl.when(step == 1)
        def _():
            self.merge_core(FAR_CHUNK, "far0")
            self.start("far_x", "far_y")

        @pl.when(step == 3)
        def _():
            self.merge_core(X_CHUNK, "x")
            self.start("x_lower")

        @pl.when(step == 5)
        def _():
            self.merge_core(Y_CHUNK, "y")
            self.start("y_upper")

    def pass_on(self):
        self.copy("far_y").wait_recv()
        self.add(X_CHUNK, 0, self.far.at[1])
        self.start("x_upper")
        self.copy("far_x").wait_recv()
        self.add(Y_CHUNK, self.half, self.far.at[0])
        self.start("y_lower")

    def finish(self, store):
        for name in ("own", "x_upper", "x_lower", "y_upper", "y_lower"):
            self.copy(name).wait_recv()

        @pl.loop(0, 2 * self.half // STRIP)
        def _(at):
            here = pl.ds(pl.multiple_of(at * STRIP, STRIP), STRIP)
            value = self.parts[0, OWN_CHUNK, here, :].astype(F32)
            value += self.cores[OWN_CHUNK, here, :].astype(F32)
            value += self.near[0, here, :].astype(F32)
            value += self.near[1, here, :].astype(F32)
            store(here, value)

    def sent(self):
        for name in (
            "far0", "x", "y", "own", "far_x", "far_y", "x_upper", "x_lower", "y_upper", "y_lower",
        ):
            self.copy(name).wait_send()


def hidden_back_kernel(
    wide, gain_ref, h_ref, grad_ref, dgate_ref, dup_ref, wg_ref, wu_ref,
    low_ref, gain_out,
    loaded, wg_all, wu_all, h_all, grad_all, load_sem, own_sem, *scratch,
):
    ring = Reduce(wide, *scratch)
    rows = low_ref.shape[0]

    def loads(step):
        chunk, _ = ring.chunk(step)
        here = pl.ds(pl.multiple_of(chunk * rows, rows), rows)
        return [
            pltpu.make_async_copy(
                ref.at[here], loaded.at[step % 2, at], load_sem.at[step % 2, at]
            )
            for at, ref in enumerate((dgate_ref, dup_ref))
        ]

    pairs = ((wg_ref, wg_all), (wu_ref, wu_all), (h_ref, h_all), (grad_ref, grad_all))
    whole = [
        pltpu.make_async_copy(src, dst, own_sem.at[at]) for at, (src, dst) in enumerate(pairs)
    ]
    for copy in loads(0) + whole:
        copy.start()
    meet(ring.peers)
    for copy in whole[:2]:
        copy.wait()

    @pl.loop(0, 8)
    def _(step):
        @pl.when(step < 7)
        def _():
            for copy in loads(step + 1):
                copy.start()

        for copy in loads(step):
            copy.wait()
        _, target = ring.chunk(step)
        dgate, dup = loaded[step % 2, 0], loaded[step % 2, 1]

        @pl.loop(0, low_ref.shape[1] // NTILE)
        def _(at):
            n = pl.ds(pl.multiple_of(at * NTILE, NTILE), NTILE)
            value = dot_nt(dgate, wg_all[n, :]) + dot_nt(dup, wu_all[n, :])
            target[:, n] = value.astype(BF16)

        ring.after(step)

    ring.pass_on()
    for copy in whole[2:]:
        copy.wait()
    gain_out[...] = jnp.zeros_like(gain_out)

    def store(here, value):
        h = h_all[here, :]
        scale = rms_scale(h)
        gained = value * gain_ref[...]
        inner = jnp.mean(gained * h, axis=1, keepdims=True)
        gain_out[...] += value * h * scale
        total = grad_all[here, :].astype(F32) + scale * gained
        total -= h * (scale * scale * scale * inner)
        low_ref[here, :] = total.astype(BF16)

    ring.finish(store)
    ring.sent()


def hidden_back(gain, h, grad, dgate, dup, wg, wu, dp_size):
    tokens, cols = dgate.shape
    rows, width = h.shape
    far = pl.BlockSpec(memory_space=pl.ANY)
    near = pl.BlockSpec(memory_space=pltpu.VMEM)
    return pl.pallas_call(
        functools.partial(hidden_back_kernel, 2 * math.isqrt(dp_size // GROUP)),
        in_specs=[near] + [far] * 6,
        out_specs=[near] * 2,
        out_shape=[
            jax.ShapeDtypeStruct((rows, width), BF16),
            jax.ShapeDtypeStruct((STRIP, width), F32),
        ],
        scratch_shapes=[
            pltpu.VMEM((2, 2, rows, cols), BF16),
            pltpu.VMEM(wg.shape, BF16),
            pltpu.VMEM(wu.shape, BF16),
            pltpu.VMEM(h.shape, F32),
            pltpu.VMEM(grad.shape, BF16),
            pltpu.SemaphoreType.DMA((2, 2)),
            pltpu.SemaphoreType.DMA((4,)),
        ]
        + Reduce.scratch(rows, width),
        compiler_params=pltpu.CompilerParams(
            collective_id=6, has_side_effects=True, vmem_limit_bytes=62 << 20
        ),
        cost_estimate=pl.CostEstimate(
            flops=2 * LONG, bytes_accessed=4 * rows * width, transcendentals=0
        ),
    )(gain, h, grad, dgate, dup, wg, wu)


def tail_kernel(
    wide, z_size, mlp_count, x_ref, dq_ref, dkv_ref, wo_ref, gain_ref,
    raw_ref, dh_ref, wq_ref, wkv_ref, *refs
):
    mlp_ins, refs = refs[:mlp_count], refs[mlp_count:]
    wq_out, wkv_out, wo_out, gain_out, grad_out = refs[:5]
    mlp_outs, scratch = refs[5 : 5 + mlp_count], refs[5 + mlp_count :]
    sub = wkv_out.shape[1]
    halves = wq_out.shape[1] // sub
    count = halves + 1
    rings = [Reduce(wide, *scratch[6 * at : 6 * at + 6]) for at in range(count)]
    sums, zrecv, gain_z, gain_p, z_send, z_recv, g_send, g_recv = scratch[6 * count : 6 * count + 8]
    wo_recv, w_send, w_recv = scratch[6 * count + 8 : 6 * count + 11]
    wq_all, wkv_all, raw, dh, dxn, gain_sum, load_sem = scratch[6 * count + 11 : 6 * count + 18]
    mlp_copies = send_home(wide, mlp_ins, mlp_outs, *scratch[6 * count + 18 :])
    place = lax.axis_index("tensor")
    mine, found = others(wide)
    along = along_peers(place, z_size)
    around = [device for _, device in found]

    tiles, tile_rows = raw.shape[0], raw.shape[1]
    loads = [
        pltpu.make_async_copy(wq_ref, wq_all, load_sem.at[0]),
        pltpu.make_async_copy(wkv_ref, wkv_all, load_sem.at[1]),
    ]
    for tile in range(tiles):
        here = pl.ds(tile * tile_rows, tile_rows)
        loads += [
            pltpu.make_async_copy(raw_ref.at[here], raw.at[tile], load_sem.at[2 + 2 * tile]),
            pltpu.make_async_copy(dh_ref.at[here], dh.at[tile], load_sem.at[3 + 2 * tile]),
        ]
    for copy in loads:
        copy.start()
    greet(along + around)

    wo_part = wo_out.shape[1]
    wo_copies = [
        pltpu.make_async_remote_copy(
            src_ref=wo_ref.at[
                :,
                pl.ds(pl.multiple_of((place + at + 1) % z_size * wo_part, LANES), wo_part),
            ],
            dst_ref=wo_recv.at[at], send_sem=w_send.at[at], recv_sem=w_recv.at[at],
            device_id=peer, device_id_type=MESH,
        )
        for at, peer in enumerate(along)
    ]
    for copy in wo_copies:
        copy.start()

    pieces = [(dq_ref, wq_out, at * sub) for at in range(halves)] + [(dkv_ref, wkv_out, 0)]
    rows = sums.shape[1]
    z_copies = []

    def partial_sums(index):
        ring = rings[index]
        right, out, offset = pieces[index]

        @pl.loop(0, 8)
        def _(step):
            chunk, target = ring.chunk(step)
            x = x_ref[:, pl.ds(pl.multiple_of(chunk * rows, rows), rows)].T

            @pl.loop(0, z_size)
            def _(at):
                n = pl.ds(pl.multiple_of(at * sub, LANES), sub)
                source = pl.ds(pl.multiple_of(at * out.shape[1] + offset, LANES), sub)
                target[:, n] = dot_nn(x, right[:, source]).astype(BF16)

            ring.after(step)

    gain_sum[...] = jnp.zeros_like(gain_sum)

    def input_rows(tile):
        part = pl.ds(tile * tile_rows, tile_rows)
        dq, dkv = dq_ref[part, :], dkv_ref[part, :]

        @pl.loop(0, dxn.shape[1] // NTILE)
        def _(at):
            n = pl.ds(pl.multiple_of(at * NTILE, NTILE), NTILE)
            dxn[:, n] = dot_nt(dq, wq_all[n, :]) + dot_nt(dkv, wkv_all[n, :])

        @pl.loop(0, tile_rows // STRIP)
        def _(at):
            here = pl.ds(pl.multiple_of(at * STRIP, STRIP), STRIP)
            there = pl.ds(pl.multiple_of(tile * tile_rows + at * STRIP, STRIP), STRIP)
            grad, value = dxn[here, :], raw[tile, here, :].astype(F32)
            scale = rms_scale(value)
            gained = grad * gain_ref[0:1, :]
            inner = jnp.mean(gained * value, axis=1, keepdims=True)
            gain_sum[...] += grad * value * scale
            total = scale * gained - value * (scale * scale * scale * inner)
            grad_out[there, :] = (dh[tile, here, :].astype(F32) + total).astype(BF16)

    def send_along(index):
        def store(here, value):
            sums[index, here, :] = value.astype(BF16)

        rings[index].finish(store)
        for at, peer in enumerate(along):
            other = (place + at + 1) % z_size
            copy = pltpu.make_async_remote_copy(
                src_ref=sums.at[index, :, pl.ds(pl.multiple_of(other * sub, LANES), sub)],
                dst_ref=zrecv.at[index, at],
                send_sem=z_send.at[index, at], recv_sem=z_recv.at[index, at],
                device_id=peer, device_id_type=MESH,
            )
            z_copies.append(copy)
            copy.start()

    partial_sums(0)
    for copy in loads:
        copy.wait()
    input_rows(0)
    rings[0].pass_on()
    for index in range(1, count):
        partial_sums(index)
        if index < tiles:
            input_rows(index)
        if index + 1 < count:
            rings[index].pass_on()
            send_along(index - 1)
    for tile in range(count, tiles):
        input_rows(tile)

    gain_z[place, 0:1] = jnp.sum(gain_sum[...], axis=0, keepdims=True)
    gain_z[place, 1:2] = gain_ref[1:2, :]
    gain_copies = [
        pltpu.make_async_remote_copy(
            src_ref=gain_z.at[place], dst_ref=gain_z.at[place], send_sem=g_send.at[at],
            recv_sem=g_recv.at[at], device_id=peer, device_id_type=MESH,
        )
        for at, peer in enumerate(along)
    ]
    for copy in gain_copies:
        copy.start()
    rings[count - 1].pass_on()
    for copy in mlp_copies:
        copy.start()
    send_along(count - 2)

    for copy in gain_copies:
        copy.wait_recv()
    total = gain_z[0]
    for at in range(1, z_size):
        total = total + gain_z[at]
    gain_p[mine] = total
    for at, peer in enumerate(around):
        copy = pltpu.make_async_remote_copy(
            src_ref=gain_p.at[mine], dst_ref=gain_p.at[mine],
            send_sem=g_send.at[z_size - 1 + at], recv_sem=g_recv.at[z_size - 1 + at],
            device_id=peer, device_id_type=MESH,
        )
        gain_copies.append(copy)
        copy.start()
    for copy in wo_copies:
        copy.wait()
    total = wo_ref[:, pl.ds(pl.multiple_of(place * wo_part, LANES), wo_part)].astype(F32)
    for at in range(z_size - 1):
        total += wo_recv[at].astype(F32)
    wo_out[...] = total
    send_along(count - 1)

    for copy in gain_copies[z_size - 1 :]:
        copy.wait_recv()
    total = gain_p[0]
    for at in range(1, GROUP):
        total = total + gain_p[at]
    gain_out[...] = total
    for copy in z_copies:
        copy.wait_recv()
    for index, (_, out, offset) in enumerate(pieces):
        value = sums[index, :, pl.ds(pl.multiple_of(place * sub, LANES), sub)].astype(F32)
        for at in range(z_size - 1):
            value += zrecv[index, at].astype(F32)
        out[:, offset : offset + sub] = value
    for copy in z_copies + gain_copies:
        copy.wait_send()
    for ring in rings:
        ring.sent()
    for copy in mlp_copies:
        copy.wait()


def last_grads(x, dq, dkv, wo_sum, gains, raw, dh, wq, wkv, mlp, dp_size, z_size):
    tokens, width = x.shape
    rows = width // GROUP
    tiles = tokens // QTILE
    near = pl.BlockSpec(memory_space=pltpu.VMEM)
    far = pl.BlockSpec(memory_space=pl.ANY)
    sizes = [dq.shape[1], dkv.shape[1]]
    cols = dkv.shape[1]
    count = sum(sizes) // cols
    scratch = []
    for _ in range(count):
        scratch += Reduce.scratch(rows, cols)
    return pl.pallas_call(
        functools.partial(tail_kernel, 2 * math.isqrt(dp_size // GROUP), z_size, len(mlp)),
        in_specs=[near] * 5 + [far] * (4 + len(mlp)),
        out_specs=[near] * 5 + [far] * len(mlp),
        out_shape=[jax.ShapeDtypeStruct((rows, size // z_size), F32) for size in sizes]
        + [
            jax.ShapeDtypeStruct((rows, wo_sum.shape[1] // z_size), F32),
            jax.ShapeDtypeStruct(gains.shape, F32),
            jax.ShapeDtypeStruct((tokens, width), BF16),
        ]
        + home_shapes(mlp),
        scratch_shapes=scratch
        + [
            pltpu.VMEM((count, rows, cols), BF16),
            pltpu.VMEM((count, z_size - 1, rows, cols // z_size), BF16),
            pltpu.VMEM((z_size, *gains.shape), F32),
            pltpu.VMEM((GROUP, *gains.shape), F32),
            pltpu.SemaphoreType.DMA((count, z_size - 1)),
            pltpu.SemaphoreType.DMA((count, z_size - 1)),
            pltpu.SemaphoreType.DMA((z_size - 1 + GROUP - 1,)),
            pltpu.SemaphoreType.DMA((z_size - 1 + GROUP - 1,)),
            pltpu.VMEM((z_size - 1, rows, wo_sum.shape[1] // z_size), BF16),
            pltpu.SemaphoreType.DMA((z_size - 1,)),
            pltpu.SemaphoreType.DMA((z_size - 1,)),
            pltpu.VMEM(wq.shape, BF16),
            pltpu.VMEM(wkv.shape, BF16),
            pltpu.VMEM((tiles, QTILE, width), BF16),
            pltpu.VMEM((tiles, QTILE, width), BF16),
            pltpu.VMEM((QTILE, width), F32),
            pltpu.VMEM((STRIP, width), F32),
            pltpu.SemaphoreType.DMA((2 + 2 * tiles,)),
        ]
        + home_scratch(mlp),
        compiler_params=pltpu.CompilerParams(
            collective_id=4, has_side_effects=True, vmem_limit_bytes=62 << 20
        ),
        cost_estimate=pl.CostEstimate(flops=SHORT, bytes_accessed=0, transcendentals=0),
    )(x, dq, dkv, wo_sum, gains, raw, dh, wq, wkv, *mlp)


def emit_kernel(*refs):
    ins, outs = refs[:7], refs[7:]
    for src, dst in zip(ins[:6], outs[:6]):
        dst[...] = src[...].astype(dst.dtype)
    outs[6][...] = ins[6][:, :LANES]
    outs[7][...] = ins[6][:, LANES:]


def emit(mlp, grad, wq, wo, wkv):
    ins = (*mlp, grad, wq, wo, wkv)
    apart = (wkv.shape[0], LANES)
    outs = [(m.shape, F32) for m in mlp] + [(grad.shape, BF16), (wq.shape, F32), (wo.shape, F32)]
    outs += [(apart, F32)] * 2
    steps = 4

    def spec(shape):
        return pl.BlockSpec((shape[0] // steps, shape[1]), lambda at: (at, 0))

    return pl.pallas_call(
        emit_kernel,
        grid=(steps,),
        in_specs=[spec(array.shape) for array in ins],
        out_specs=[spec(shape) for shape, _ in outs],
        out_shape=[jax.ShapeDtypeStruct(*out) for out in outs],
    )(*ins)


class Layout:
    def __init__(self, dp_size):
        self.blocks = dp_size // GROUP
        side = math.isqrt(self.blocks)
        self.rows, self.cols = side, self.blocks // side
        wide = 2 * self.cols

        def index(by, bx, y, x, core):
            return ((2 * by + y) * wide + 2 * bx + x) * 2 + core

        places = [(y, x, c) for y in range(2) for x in range(2) for c in range(2)]
        spots = [(by, bx) for by in range(self.rows) for bx in range(self.cols)]
        self.inner = [[index(*s, *p) for p in places] for s in spots]
        self.outer = [[index(*s, *p) for s in spots] for p in places]

    def groups(self):
        return None if self.blocks == 1 else self.inner

    def to_rows(self, array):
        if self.blocks == 1:
            return array
        rest = array.shape[1:]
        split = array.reshape(2, 2, 2, self.rows, self.cols, -1, *rest)
        order = (3, 0, 4, 1, 2, 5) + tuple(range(6, 6 + len(rest)))
        return split.transpose(order).reshape(array.shape)

    def from_rows(self, array):
        if self.blocks == 1:
            return array
        rest = array.shape[1:]
        split = array.reshape(self.rows, 2, self.cols, 2, 2, -1, *rest)
        order = (1, 3, 4, 0, 2, 5) + tuple(range(6, 6 + len(rest)))
        return split.transpose(order).reshape(array.shape)

    def from_cols(self, array):
        return array if self.blocks == 1 else self.from_rows(array.T).T

    def gather_outer(self, array):
        if self.blocks == 1:
            return array
        return lax.all_gather(array, "dp", axis_index_groups=self.outer, axis=0, tiled=True)

    def scatter_outer(self, array):
        if self.blocks == 1:
            return array
        return lax.psum_scatter(
            array, "dp", scatter_dimension=0, axis_index_groups=self.outer, tiled=True
        )

    def swap(self, array, flip):
        pairs = [
            (block[at], block[at ^ flip]) for block in self.inner for at in range(GROUP)
        ]
        return lax.ppermute(array, "dp", pairs)

    def sum_outer(self, array):
        if self.blocks == 1:
            return array
        return lax.psum(array, "dp", axis_index_groups=self.outer)

    def gather(self, array):
        return lax.all_gather(array, "dp", axis_index_groups=self.groups(), axis=0, tiled=True)

    def scatter(self, array):
        return lax.psum_scatter(
            array, "dp", scatter_dimension=0, axis_index_groups=self.groups(), tiled=True
        )


def rms_scale(values):
    return lax.rsqrt(jnp.mean(values * values, axis=-1, keepdims=True) + NORM_EPS)


def per_device(
    dp_size, z_size, activations, segment_ids, attn_gain, w_query, w_key, w_value, w_out,
    mlp_gain, w_gate, w_up, w_down, cotangent,
):
    layout = Layout(dp_size)
    rows, width = activations.shape[1:]
    x = activations[0].astype(F32)
    place = lax.axis_index("tensor")
    reach = -(-(MOST_DOC - 1) // rows) * rows

    def shift(array, step):
        pairs = [(at, at + step) for at in range(z_size) if 0 <= at + step < z_size]
        return lax.ppermute(array, "tensor", pairs)

    starts = document_starts(segment_ids[0])
    own_starts = lax.dynamic_slice_in_dim(starts, place * rows, rows)
    own_tokens = place * rows + jnp.arange(rows, dtype=jnp.int32)
    cosine, sine = rope_tables(own_tokens - own_starts)
    low = (own_starts - place * rows + reach)[None, :]

    shards = [
        layout.gather_outer(w)
        for w in (w_gate, w_up, w_down, jnp.concatenate([w_key, w_value], axis=1), w_query, w_out)
    ]
    xn, *spread = spread_weights(
        activations[0], attn_gain[None], shards[:3], shards[3:], dp_size, z_size
    )
    def gather_z(array):
        return layout.to_rows(lax.all_gather(array, "tensor", axis=1, tiled=True))

    wg, wu = gather_z(spread[0]), gather_z(spread[1])

    def along_z(total):
        return lax.psum_scatter(
            layout.from_rows(total), "tensor", scatter_dimension=1, tiled=True
        )

    q, kv_all, wq, wo, dy = project(
        layout.from_cols(xn), cosine, sine, *spread[3:], cotangent[0], reach, dp_size, z_size
    )
    wd = gather_z(spread[2])
    wkv, wq, wo = (layout.to_rows(w) for w in (spread[3], wq, wo))
    att, lse, dy = attend(q, kv_all, low, cotangent[0], dy, dp_size)
    h = x + dot_nt(att, wo)

    r2 = rms_scale(h)
    hn, gate, up, hidden, by_core = gate_up((h * r2 * mlp_gain).astype(BF16), wg, wu, dp_size)
    part = rows // 2
    away = dot_nt(by_core[1], wd).astype(BF16)
    dy, away = lax.optimization_barrier((dy, away))
    total_wd = dot_tn(dy, hidden).astype(BF16)
    part_wd = along_z(total_wd)
    from_core = layout.swap(away, 1)

    near = (dot_nt(by_core[0], wd) + from_core.astype(F32)).astype(BF16)
    dy, near = lax.optimization_barrier((dy, near))

    def out_rows(start, count):
        return near[start * part : (start + count) * part]

    def joined(some, other):
        return (some.astype(F32) + other.astype(F32)).astype(BF16)

    far_y, far_x, x_lower, y_upper = (out_rows(at, 1) for at in (6, 7, 3, 4))
    dy, far_x, far_y, x_lower, y_upper = lax.optimization_barrier(
        (dy, far_x, far_y, x_lower, y_upper)
    )
    from_x, from_y = layout.swap(far_x, 2), layout.swap(far_y, 4)
    x_lower, y_upper = layout.swap(x_lower, 2), layout.swap(y_upper, 4)
    gate, up = gate.astype(F32), up.astype(F32)
    sigma = jax.nn.sigmoid(gate)
    dhid = dot_nn(dy, wd)
    dgate = (dhid * up * sigma * (1.0 + gate * (1.0 - sigma))).astype(BF16)
    dup = (dhid * gate * sigma).astype(BF16)
    dgate, dup, from_x, from_y = lax.optimization_barrier((dgate, dup, from_x, from_y))
    x_upper, y_lower = joined(out_rows(2, 1), from_y), joined(out_rows(5, 1), from_x)
    dgate, dup, x_upper, y_lower = lax.optimization_barrier((dgate, dup, x_upper, y_lower))
    x_upper, y_lower = layout.swap(x_upper, 2), layout.swap(y_lower, 4)
    total_wg = dot_tn(hn, dgate).astype(BF16)
    dup, total_wg, x_lower, y_upper = lax.optimization_barrier((dup, total_wg, x_lower, y_upper))
    part_wg = along_z(total_wg)
    total_wu = dot_tn(hn, dup).astype(BF16)
    dup, total_wu = lax.optimization_barrier((dup, total_wu))
    part_wu = along_z(total_wu)
    dup, x_upper, y_lower = lax.optimization_barrier((dup, x_upper, y_lower))
    dhb, gain_two = hidden_back(
        mlp_gain[None], h, cotangent[0], dgate, dup, wg, wu, dp_size
    )
    gain_two = jnp.sum(gain_two, axis=0)
    dhb, part_wd = lax.optimization_barrier((dhb, part_wd))
    datt = dot_nn(dhb, wo).astype(BF16)
    total_wo = layout.from_rows(dot_tn(dhb, att).astype(BF16))
    datt, part_wg, total_wo = lax.optimization_barrier((datt, part_wg, total_wo))
    part_wo = layout.scatter(total_wo)
    dq, dkv, wd_grad, wg_grad = attend_back(
        q, datt, att, kv_all, lse, low, cosine, sine, (part_wd, part_wg), dp_size, z_size
    )
    dq, part_wu = lax.optimization_barrier((dq, part_wu))
    dq, part_wo = lax.optimization_barrier((dq, part_wo))
    wq_grad, wkv_grad, wo_grad, gains, input_grad, wu_grad = last_grads(
        layout.from_cols(xn), dq, dkv, part_wo, jnp.stack([attn_gain, gain_two]),
        activations[0], dhb, wq, wkv, (part_wu,), dp_size, z_size,
    )
    gains = layout.sum_outer(gains)
    output = h + out_rows(0, 2).astype(F32)
    output = output + jnp.concatenate([x_upper, x_lower]).astype(F32)
    output = output + jnp.concatenate([y_upper, y_lower]).astype(F32)
    wo_grad, wq_grad, wkv_grad, wd_grad, wg_grad, wu_grad = (
        layout.scatter_outer(grad)
        for grad in (wo_grad, wq_grad, wkv_grad, wd_grad, wg_grad, wu_grad)
    )
    wd_grad, wg_grad, wu_grad, input_grad, wq_grad, wo_grad, wk_grad, wv_grad = emit(
        (wd_grad, wg_grad, wu_grad), input_grad, wq_grad, wo_grad, wkv_grad
    )
    return (
        output.astype(BF16)[None],
        input_grad[None],
        gains[0],
        wq_grad,
        wk_grad,
        wv_grad,
        wo_grad,
        gains[1],
        wg_grad,
        wu_grad,
        wd_grad,
    )


def solution(mesh):
    split = P("dp", "tensor")
    tokens = P("dp", "tensor", None)
    in_specs = (
        tokens, P("dp", None), P(), split, split, split, split, P(), split, split, split, tokens,
    )
    out_specs = (tokens, tokens, P(), split, split, split, split, P(), split, split, split)
    return jax.shard_map(
        functools.partial(per_device, mesh.shape["dp"], mesh.shape["tensor"]),
        mesh=mesh, in_specs=in_specs, out_specs=out_specs, check_vma=False,
    )
```
